32 devices in a mesh: items: 4 (over y, x), rows: 8 (over z, core).
Axes of the slice: x: 2, y: 2, z: 4, core: 2. Of those that a mesh axis runs over, the one named last changes fastest.
Arguments:
- image: bfloat16 [4, 64, 64, 512], P('items', 'rows'), may hold values from -18 to 18
- embed: bfloat16 [4, 2048], P('items'), may hold values from -6 to 6
- text: bfloat16 [4, 128, 2048], P('items', 'rows'), may hold values from -6 to 6
- extent: int32 [4, 2], P('items'), may hold values from 32 to 64, as said below
- first_norm_gain1: float32 [512], replicated, may hold values from 0.1 to 1.9
- conv1_w: bfloat16 [3, 3, 512, 512], replicated, may hold values from -0.09375 to 0.09375
- embed_w: bfloat16 [2048, 1024], replicated, may hold values from -0.125 to 0.125
- second_norm_gain2: float32 [512], replicated, may hold values from 0.1 to 1.9
- conv2_w: bfloat16 [3, 3, 512, 512], replicated, may hold values from -0.09375 to 0.09375
- attention_norm_gain: float32 [512], replicated, may hold values from 0.1 to 1.9
- qkv_w: bfloat16 [512, 1536], replicated, may hold values from -0.25 to 0.25
- text_w: bfloat16 [2048, 1024], replicated, may hold values from -0.125 to 0.125
- proj_w: bfloat16 [512, 512], replicated, may hold values from -6 to 6
- cotangent: bfloat16 [4, 64, 64, 512], P('items', 'rows'), may hold values from -6 to 6
Outputs:
- output: bfloat16 [4, 64, 64, 512], P('items', 'rows')
- image_grad: float32 [4, 64, 64, 512], P('items', 'rows')
- embed_grad: float32 [4, 2048], P('items')
- text_grad: float32 [4, 128, 2048], P('items', 'rows')
- norm1_gain_grad: float32 [512], P('rows')
- conv1_w_grad: float32 [3, 3, 512, 512], P(None, None, None, 'rows')
- embed_w_grad: float32 [2048, 1024], P('rows')
- norm2_gain_grad: float32 [512], P('rows')
- conv2_w_grad: float32 [3, 3, 512, 512], P(None, None, None, 'rows')
- attn_gain_grad: float32 [512], P('rows')
- qkv_w_grad: float32 [512, 1536], P(None, 'rows')
- text_w_grad: float32 [2048, 1024], P('rows')
- proj_w_grad: float32 [512, 512], P(None, 'rows')
The draws below stay inside these ranges and needn't reach their ends.
Inputs may be any that keep to these rules, and one draw needn't show every extreme that they name: `extent`: each image's valid rows and columns are 64 and 64 minus the same multiple 0, 1 or 2 of a quarter of them; in every draw some image fills its frame and some other image keeps half of its rows and half of its columns.
All inputs are finite; a program needn't handle non-finite values.
Results may differ from the reference program's by a relative error of at most 0.018.
Values may be sent and summed in bfloat16 or wider, within the bound.
A program may use at most 192 MiB of HBM per device.

```python
import jax
import jax.numpy as jnp
from jax import lax

C = 512
GROUPS = 32
HEADS = 8
EMB = 2048
TW = 2048
TEXT = 128
FRAME_H = 64
FRAME_W = 64
ITEMS = 4


def draw_image(key, part):
    rising = 3.0 ** (jnp.arange(FRAME_H, dtype=jnp.float32) / (FRAME_H - 1))
    shape = (ITEMS, FRAME_H, FRAME_W, C)
    base = jnp.clip(jax.random.normal(key, shape, jnp.float32), -6.0, 6.0)
    return (base * rising[None, :, None, None]).astype(jnp.bfloat16)


def draw_extent(key, part):
    level_key = jax.random.fold_in(key, 11)
    order_key = jax.random.fold_in(key, 23)
    pick = jax.random.randint(level_key, (ITEMS,), 0, 22)
    level = (pick >= 12).astype(jnp.int32) + (pick >= 20).astype(jnp.int32)
    order = jax.random.permutation(order_key, ITEMS).astype(jnp.int32)
    position = jnp.arange(ITEMS, dtype=jnp.int32)
    level = jnp.where(position == order[0], 0, level)
    level = jnp.where(position == order[1], 2, level)
    rows_valid = FRAME_H - level * (FRAME_H // 4)
    cols_valid = FRAME_W - level * (FRAME_W // 4)
    return jnp.stack([rows_valid, cols_valid], axis=1).astype(jnp.int32)


def block_scale(own_key, shape, shards, least, top_value):
    loudness = 1.0
    for dim, shards_of in shards:
        heights = jax.random.uniform(jax.random.fold_in(jax.random.fold_in(own_key, 6), dim), (shards_of,), jnp.float32, least / len(shards), top_value / len(shards))
        loudness = loudness * jnp.repeat(jnp.exp(heights), shape[dim] // shards_of).reshape((-1,) + (1,) * (len(shape) - 1 - dim))
    return loudness


def normal_values(rng, shape, deviation, bound, pieces=(), held_as=jnp.bfloat16):
    gain = block_scale(rng, shape, pieces, -0.22, 0.18) if pieces else 1.0
    values = jax.random.normal(rng, shape, jnp.float32) * deviation * gain
    return jnp.minimum(jnp.maximum(values, -bound), bound).astype(held_as)


def setup_inputs(seed: int = 0) -> dict:
    streams_of = jax.random.split(jax.random.key(seed), 15)
    image = draw_image(jax.random.fold_in(streams_of[14], 71), 0)
    embed = normal_values(streams_of[1], (ITEMS, EMB), 1.0, 6.0, ((0, 4),))
    text = normal_values(streams_of[2], (ITEMS, TEXT, TW), 1.0, 6.0, ((0, 4), (1, 8)))
    extent = draw_extent(jax.random.fold_in(streams_of[14], 71), 0)
    first_norm_gain1 = jnp.clip(1.0 + 0.18 * jax.random.normal(streams_of[4], (C,), jnp.float32), 0.1, 1.9)
    conv1_w = normal_values(streams_of[5], (3, 3, C, C), (9 * C) ** -0.5, 0.09375)
    embed_w = normal_values(streams_of[6], (EMB, 2 * C), EMB ** -0.5, 0.125)
    second_norm_gain2 = jnp.clip(1.0 + 0.18 * jax.random.normal(streams_of[7], (C,), jnp.float32), 0.1, 1.9)
    conv2_w = normal_values(streams_of[8], (3, 3, C, C), (9 * C) ** -0.5, 0.09375)
    attention_norm_gain = jnp.clip(1.0 + 0.18 * jax.random.normal(streams_of[9], (C,), jnp.float32), 0.1, 1.9)
    qkv_w = normal_values(streams_of[10], (C, 3 * C), C ** -0.5, 0.25)
    text_w = normal_values(streams_of[11], (TW, 2 * C), TW ** -0.5, 0.125)
    proj_w = normal_values(streams_of[12], (C, C), (max(C // 512, 1)) ** -0.5, 6.0)
    cotangent = normal_values(streams_of[13], (ITEMS, FRAME_H, FRAME_W, C), 1.0, 6.0, ((0, 4), (1, 8)))
    return dict(image=image, embed=embed, text=text, extent=extent, first_norm_gain1=first_norm_gain1, conv1_w=conv1_w, embed_w=embed_w, second_norm_gain2=second_norm_gain2, conv2_w=conv2_w, attention_norm_gain=attention_norm_gain, qkv_w=qkv_w, text_w=text_w, proj_w=proj_w, cotangent=cotangent)


@jax.custom_vjp
def low(v):
    return lax.optimization_barrier(v.astype(jnp.bfloat16)).astype(jnp.float32)

@jax.custom_vjp
def low_back(v):
    return v

def low_keep(v):
    return (low(v), None)

def low_pass(kept, grad):
    return (grad,)

def back_keep(v):
    return (v, None)

def back_low(kept, grad):
    return (low(grad),)
low.defvjp(low_keep, low_pass)
low_back.defvjp(back_keep, back_low)
eps = 1e-05
negative = -1e+30
highest = lax.Precision.HIGHEST

def group_norm(values, inside, norm_gain):
    shaped = values.reshape(values.shape[:3] + (GROUPS, values.shape[3] // GROUPS))
    group_counts = lax.optimization_barrier(jnp.sum(inside, axis=(1, 2))) * (values.shape[3] // GROUPS)
    average = lax.optimization_barrier(jnp.sum(shaped, axis=(1, 2, 4))) / group_counts[:, None]
    squares = lax.optimization_barrier(jnp.sum(shaped * shaped, axis=(1, 2, 4))) / group_counts[:, None]
    inverse_deviation = lax.rsqrt(squares - average * average + eps)
    normal = (shaped - average[:, None, None, :, None]) * inverse_deviation[:, None, None, :, None]
    return normal.reshape(values.shape) * inside[..., None] * norm_gain

def convolve(field, kernel):
    return lax.conv_general_dilated(field, kernel, (1, 1), ((1, 1), (1, 1)), dimension_numbers=('NHWC', 'HWIO', 'NHWC'), precision=highest)

def attend_item(packed):
    queries, keys, values, key_ok = packed
    tokens = queries.shape[0]
    block = min(512, tokens)
    factor = queries.shape[2] ** (-0.5)

    def one_block(query_block):
        scores = low_back(jnp.einsum('qhd,khd->hqk', query_block, keys, precision=highest) * factor)
        scores = jnp.where(key_ok[None, None, :], scores, negative)
        weights_soft = low(jax.nn.softmax(scores, axis=-1))
        return low(low_back(jnp.einsum('hqk,khd->qhd', weights_soft, values, precision=highest)))
    blocks = queries.reshape(tokens // block, block, queries.shape[1], queries.shape[2])
    return lax.map(jax.checkpoint(one_block), blocks).reshape(queries.shape)

def forward(image, embed, text, first_norm_gain1, conv1_w, embed_w, second_norm_gain2, conv2_w, attention_norm_gain, qkv_w, text_w, proj_w, inside, key_ok):
    images, frame_rows, frame_cols, channels = image.shape
    image_window = inside[..., None]
    start_index = image * image_window
    hidden = low(jax.nn.silu(group_norm(start_index, inside, first_norm_gain1)) * image_window)
    first_output = low_back(convolve(hidden, conv1_w)) * image_window
    shifts = low_back(jnp.dot(low(jax.nn.silu(embed)), embed_w, precision=highest))
    scale = shifts[:, None, None, :channels]
    shift = shifts[:, None, None, channels:]
    moved = group_norm(first_output, inside, second_norm_gain2) * (1.0 + scale) + shift
    second = low(jax.nn.silu(moved) * image_window)
    middle_output = start_index + low_back(convolve(second, conv2_w)) * image_window
    attention_input = low(group_norm(middle_output, inside, attention_norm_gain))
    head_dim = channels // HEADS
    tokens = frame_rows * frame_cols
    qkv_all = low(low_back(jnp.einsum('irwc,ck->irwk', attention_input, qkv_w, precision=highest)))
    qkv_all = qkv_all.reshape(images, tokens, HEADS, 3, head_dim)
    text_kv = low(low_back(jnp.einsum('itc,ck->itk', text, text_w, precision=highest)))
    text_kv = text_kv.reshape(images, text.shape[1], HEADS, 2, head_dim)
    keys = jnp.concatenate([text_kv[:, :, :, 0], qkv_all[:, :, :, 1]], axis=1)
    values = jnp.concatenate([text_kv[:, :, :, 1], qkv_all[:, :, :, 2]], axis=1)
    attended = lax.map(attend_item, (qkv_all[:, :, :, 0], keys, values, key_ok))
    projected = low_back(jnp.einsum('iqc,ck->iqk', attended.reshape(images, tokens, channels), proj_w, precision=highest))
    return middle_output + projected.reshape(image.shape) * image_window

def reference(image, embed, text, extent, first_norm_gain1, conv1_w, embed_w, second_norm_gain2, conv2_w, attention_norm_gain, qkv_w, text_w, proj_w, cotangent):
    rowpos = jnp.arange(FRAME_H, dtype=jnp.int32)
    colpos = jnp.arange(FRAME_W, dtype=jnp.int32)
    valid = (rowpos[None, :, None] < extent[:, 0, None, None]) & (colpos[None, None, :] < extent[:, 1, None, None])
    inside = valid.astype(jnp.float32)
    key_ok = jnp.concatenate([jnp.ones((ITEMS, TEXT), dtype=jnp.bool_), valid.reshape(ITEMS, FRAME_H * FRAME_W)], axis=1)
    members = (image, embed, text, first_norm_gain1, conv1_w, embed_w, second_norm_gain2, conv2_w, attention_norm_gain, qkv_w, text_w, proj_w)
    floats = tuple((member.astype(jnp.float32) for member in members))

    def wrapped(*arrays):
        return forward(*arrays, inside, key_ok)
    result, pullback = jax.vjp(wrapped, *floats)
    grads = pullback(cotangent.astype(jnp.float32))
    return (result.astype(jnp.bfloat16), grads[0], grads[1], grads[2], grads[3], grads[4], grads[5], grads[6], grads[7], grads[8], grads[9], grads[10], grads[11])
```

```python
import functools

import jax
import jax.numpy as jnp
from jax import lax
from jax.experimental import pallas as pl
from jax.experimental.pallas import tpu as pltpu
from jax.sharding import PartitionSpec as P

GROUPS = 32
HEADS = 8
F32, BF16 = jnp.float32, jnp.bfloat16
NEG = -1e30


def dot(a, b, ca, cb):
    return lax.dot_general(a, b, (((ca,), (cb,)), ((), ())), preferred_element_type=F32)

def attention_kernel(width, step, bq, ext_ref, qkv_ref, text_ref, go_ref, out_ref, dqkv_ref, dtext_ref,
                     kn, vn, kt, vt, s0, s1, e0, e1, dkt, dvt):
    scores, raised = (s0, s1), (e0, e1)
    chunks, _, span = qkv_ref.shape
    tlen = text_ref.shape[0]
    d = go_ref.shape[1]
    pix = chunks * span
    keys = pix + tlen
    steps = keys // step
    rows_ok, cols_ok = ext_ref[0, 0], ext_ref[0, 1]
    def stage(c, carry):
        base = pl.multiple_of(c * span, span)
        pos = base + lax.broadcasted_iota(jnp.int32, (16, span), 1)
        row = lax.broadcasted_iota(jnp.int32, (16, span), 0)
        ok = (pos // width < rows_ok) & (pos % width < cols_ok)
        extra = jnp.where((row == 0) & jnp.logical_not(ok), NEG, 0.0)
        k = qkv_ref[c, d:2 * d, :]
        v = qkv_ref[c, 2 * d:, :]
        kt[:, pl.ds(base, span)] = k
        vt[:, pl.ds(base, span)] = v
        rest = jnp.zeros((128 - d - 16, span), F32)
        ka = jnp.concatenate([k.astype(F32), extra, rest], axis=0)
        va = jnp.concatenate([v.astype(F32), jnp.where(row < 3, 1.0, 0.0), rest], axis=0)
        kn[pl.ds(base, span), :] = ka.T.astype(BF16)
        vn[pl.ds(base, span), :] = va.T.astype(BF16)
        return carry
    lax.fori_loop(0, chunks, stage, 0)
    tk = text_ref[:, :d].astype(F32)
    tv = text_ref[:, d:].astype(F32)
    kt[:, pix:] = tk.T.astype(BF16)
    vt[:, pix:] = tv.T.astype(BF16)
    lanes = lax.broadcasted_iota(jnp.int32, (tlen, 128 - d), 1)
    kn[pix:, :] = jnp.concatenate([tk, jnp.zeros((tlen, 128 - d), F32)], axis=1).astype(BF16)
    vn[pix:, :] = jnp.concatenate([tv, jnp.where(lanes < 3, 1.0, 0.0)], axis=1).astype(BF16)
    dkt[...] = jnp.zeros_like(dkt)
    dvt[...] = jnp.zeros_like(dvt)

    low_peak = jnp.full((8, bq), -3e38, F32)

    def q_aug(c, half):
        q = qkv_ref[c, :d, half * bq:(half + 1) * bq].astype(F32) * (d ** -0.5)
        r = lax.broadcasted_iota(jnp.int32, (128 - d, bq), 0)
        return jnp.concatenate([q, jnp.where(r == 0, 1.0, 0.0)], axis=0).astype(BF16)

    def run(score, exp, back):
        def body(j, carry):
            pk, total, acc, dq = carry
            at = pl.ds(pl.multiple_of(j * step, step), step)
            if score:
                slot, qa = score
                s = dot(kn[at, :], qa, 1, 0)
                scores[slot][at, :] = s
                pk = jnp.maximum(pk, jnp.max(s.reshape(step // 8, 8, bq), axis=0))
            if exp:
                slot, peak = exp
                e = jnp.exp(scores[slot][at, :] - peak)
                total = total + jnp.sum(e.reshape(step // 8, 8, bq), axis=0)
                low = e.astype(BF16)
                raised[slot][at, :] = low
                acc = acc + dot(vt[:, at], low, 1, 0)
            if back:
                slot, goa, gs, q = back
                dp = dot(vn[at, :], goa, 1, 0)
                e = raised[slot][at, :]
                ds = (e.astype(F32) * dp).astype(BF16)
                dvt[:, at] += dot(gs, e, 1, 1)
                dkt[:, at] += dot(q, ds, 1, 1)
                dq = dq + dot(kt[:, at], ds, 1, 0)
            return pk, total, acc, dq
        init = (low_peak, jnp.zeros((8, bq), F32), jnp.zeros((d, bq), F32), jnp.zeros((d, bq), F32))
        return lax.fori_loop(0, steps, body, init)

    def finish_exp(c, half, total, acc):
        inv = 1.0 / jnp.sum(total, axis=0, keepdims=True)
        o = acc * inv
        cols = slice(half * bq, (half + 1) * bq)
        out_ref[c, :, cols] = o.astype(BF16)
        go = go_ref[c, :, cols].astype(F32)
        nd = -jnp.sum(go * o, axis=0, keepdims=True) * inv
        gs = go * inv
        hi = nd.astype(BF16).astype(F32)
        mid = (nd - hi).astype(BF16).astype(F32)
        lo = nd - hi - mid
        r = lax.broadcasted_iota(jnp.int32, (16, bq), 0)
        extra = jnp.where(r == 0, hi, jnp.where(r == 1, mid, jnp.where(r == 2, lo, 0.0)))
        goa = jnp.concatenate([gs, extra, jnp.zeros((128 - d - 16, bq), F32)], axis=0).astype(BF16)
        return goa

    def put_dq(c, half, dq):
        dqkv_ref[c, :d, half * bq:(half + 1) * bq] = (dq * (d ** -0.5)).astype(BF16)

    def top(pk):
        return jnp.max(pk, axis=0, keepdims=True)

    def q_of(c, half):
        return qkv_ref[c, :d, half * bq:(half + 1) * bq]

    pk, _, _, _ = run((0, q_aug(0, 0)), None, None)
    pk, total, acc, _ = run((1, q_aug(0, 1)), (0, top(pk)), None)
    goa = finish_exp(0, 0, total, acc)

    def two(h, carry):
        pk, goa = carry
        pk2, total, acc, dq = run((0, q_aug(h + 1, 0)), (1, top(pk)), (0, goa, goa[:d], q_of(h, 0)))
        put_dq(h, 0, dq)
        goa = finish_exp(h, 1, total, acc)
        pk3, total, acc, dq = run((1, q_aug(h + 1, 1)), (0, top(pk2)), (1, goa, goa[:d], q_of(h, 1)))
        put_dq(h, 1, dq)
        return pk3, finish_exp(h + 1, 0, total, acc)
    pk, goa = lax.fori_loop(0, chunks - 1, two, (pk, goa))
    last = chunks - 1
    _, total, acc, dq = run(None, (1, top(pk)), (0, goa, goa[:d], q_of(last, 0)))
    put_dq(last, 0, dq)
    goa = finish_exp(last, 1, total, acc)
    _, _, _, dq = run(None, None, (1, goa, goa[:d], q_of(last, 1)))
    put_dq(last, 1, dq)

    def finish(c, carry):
        at = pl.ds(pl.multiple_of(c * span, span), span)
        dqkv_ref[c, d:2 * d, :] = (dkt[:, at] * (d ** -0.5)).astype(BF16)
        dqkv_ref[c, 2 * d:, :] = dvt[:, at].astype(BF16)
        return carry
    lax.fori_loop(0, chunks, finish, 0)
    dtext_ref[:d, :] = (dkt[:, pix:] * (d ** -0.5)).astype(BF16)
    dtext_ref[d:, :] = dvt[:, pix:].astype(BF16)

def attention(ext, qkv, text, go, width):
    chunks, wide, span = qkv.shape
    d = wide // 3
    tlen = text.shape[0]
    keys = chunks * span + tlen
    bq = span // 2
    lanes = keys // 128
    step = 128 * max(n for n in range(1, 12) if lanes % n == 0)
    vm = pl.BlockSpec(memory_space=pltpu.VMEM)
    flops = 2 * 6 * chunks * span * keys * d
    return pl.pallas_call(
        functools.partial(attention_kernel, width, step, bq),
        out_shape=(
            jax.ShapeDtypeStruct(go.shape, BF16),
            jax.ShapeDtypeStruct(qkv.shape, BF16),
            jax.ShapeDtypeStruct((2 * d, tlen), BF16),
        ),
        in_specs=[pl.BlockSpec(memory_space=pltpu.SMEM), vm, vm, vm],
        out_specs=(vm, vm, vm),
        scratch_shapes=[
            pltpu.VMEM((keys, 128), BF16),
            pltpu.VMEM((keys, 128), BF16),
            pltpu.VMEM((d, keys), BF16),
            pltpu.VMEM((d, keys), BF16),
            pltpu.VMEM((keys, bq), F32),
            pltpu.VMEM((keys, bq), F32),
            pltpu.VMEM((keys, bq), BF16),
            pltpu.VMEM((keys, bq), BF16),
            pltpu.VMEM((d, keys), F32),
            pltpu.VMEM((d, keys), F32),
        ],
        compiler_params=pltpu.CompilerParams(vmem_limit_bytes=56 << 20),
        cost_estimate=pl.CostEstimate(
            flops=4 * flops, bytes_accessed=16 * chunks * span * d, transcendentals=chunks * span * keys
        ),
    )(ext, qkv, text, go)


eps = 1e-05


def padded_2(shard, sides, width):
    for axis, dim in sides:
        count, length = (lax.axis_size(axis), shard.shape[dim])
        up = [(i, (i + 1) % count) for i in range(count - 1)]
        down = [(j, i) for i, j in up]
        last = lax.slice_in_dim(shard, length - width, length, axis=dim)
        first = lax.slice_in_dim(shard, 0, width, axis=dim)
        before = lax.ppermute(last, axis, up)
        after = lax.ppermute(first, axis, down)
        shard = jnp.concatenate([before, shard, after], axis=dim)
    return shard


def framed(values):
    padded = padded_2(values, (("rows", 1),), 1)
    return jnp.pad(padded, ((0, 0), (0, 0), (1, 1), (0, 0)))


def conv_apply(padded, kernel, layout):
    return lax.conv_general_dilated(
        padded,
        kernel,
        (1, 1),
        ((0, 0), (0, 0)),
        dimension_numbers=("NHWC", layout, "NHWC"),
        preferred_element_type=jnp.float32,
    )


def kernel_grad(padded, grad_out):
    rows_dev, width = (grad_out.shape[1], grad_out.shape[2])
    taps = []
    for tap_row in range(3):
        for tap_col in range(3):
            shifted = padded[:, tap_row : tap_row + rows_dev, tap_col : tap_col + width]
            taps.append(
                jnp.einsum(
                    "irwk,irwc->kc", grad_out, shifted, preferred_element_type=jnp.float32
                ).astype(BF16)
            )
    return jnp.stack(taps, axis=1)


def silu_slope(values):
    sigmoid = jax.nn.sigmoid(values)
    return sigmoid * (1.0 + values * (1.0 - sigmoid))


def grouped_input(values):
    return values.reshape(values.shape[:3] + (GROUPS, values.shape[3] // GROUPS))


def group_norm_forward(values, group_counts, image_window):
    shaped = grouped_input(values)
    sums, squares = lax.psum(
        (jnp.sum(shaped, axis=(1, 2, 4)), jnp.sum(shaped * shaped, axis=(1, 2, 4))), "rows"
    )
    average = sums / group_counts[:, None]
    inverse_deviation = lax.rsqrt(squares / group_counts[:, None] - average * average + eps)
    normal = (shaped - average[:, None, None, :, None]) * inverse_deviation[:, None, None, :, None]
    return (normal.reshape(values.shape) * image_window, inverse_deviation)


def apply_group_norm(
    normalized_gradient,
    normalized_input,
    inverse_deviation,
    gradient_total_sum,
    cross_product_sum,
    group_counts,
    image_window,
):
    shaped_grad = grouped_input(normalized_gradient)
    reshaped_input = grouped_input(normalized_input)
    mean_grad = (gradient_total_sum / group_counts[:, None])[:, None, None, :, None]
    mean_cross = (cross_product_sum / group_counts[:, None])[:, None, None, :, None]
    result = (shaped_grad - mean_grad - reshaped_input * mean_cross) * inverse_deviation[
        :, None, None, :, None
    ]
    return result.reshape(normalized_gradient.shape) * image_window


def group_norm_backward(
    norm_gradient, normalized_input, inverse_deviation, norm_gain, group_counts, image_window
):
    normalized_gradient = norm_gradient * norm_gain
    shaped_grad = grouped_input(normalized_gradient)
    reshaped_input = grouped_input(normalized_input)
    gradient_total_sum, cross_product_sum = lax.psum(
        (
            jnp.sum(shaped_grad, axis=(1, 2, 4)),
            jnp.sum(shaped_grad * reshaped_input, axis=(1, 2, 4)),
        ),
        "rows",
    )
    correction_term = apply_group_norm(
        normalized_gradient,
        normalized_input,
        inverse_deviation,
        gradient_total_sum,
        cross_product_sum,
        group_counts,
        image_window,
    )
    return (correction_term, jnp.sum(norm_gradient * normalized_input, axis=(0, 1, 2)))


def shards(
    image,
    embed,
    text,
    extent,
    first_norm_gain1,
    conv1_w,
    embed_w,
    second_norm_gain2,
    conv2_w,
    attention_norm_gain,
    qkv_w,
    text_w,
    proj_w,
    cotangent,
):
    images, rows_dev, width, channels = image.shape
    parts = lax.axis_size("rows")
    pairs = images * HEADS // parts
    head_dim = channels // HEADS
    first_row = lax.axis_index("rows") * rows_dev
    rowpos = first_row + jnp.arange(rows_dev, dtype=jnp.int32)
    colpos = jnp.arange(width, dtype=jnp.int32)
    inside = (
        (rowpos[None, :, None] < extent[:, 0, None, None])
        & (colpos[None, None, :] < extent[:, 1, None, None])
    ).astype(jnp.float32)
    image_window = inside[..., None]
    group_counts = (extent[:, 0] * extent[:, 1]).astype(jnp.float32) * (channels // GROUPS)
    start_index = image.astype(jnp.float32) * image_window
    first_normalized_input, first_inverse_deviation = group_norm_forward(
        start_index, group_counts, image_window
    )
    first_preactivation = first_normalized_input * first_norm_gain1
    hidden = (jax.nn.silu(first_preactivation) * image_window).astype(jnp.bfloat16)
    hidden_pad = framed(hidden)
    first_output = conv_apply(hidden_pad, conv1_w, "HWIO") * image_window
    embed_float = embed.astype(jnp.float32)
    embed_low = jax.nn.silu(embed_float).astype(jnp.bfloat16)
    shifts = jnp.dot(embed_low, embed_w, preferred_element_type=jnp.float32)
    scale = shifts[:, None, None, :channels]
    shift = shifts[:, None, None, channels:]
    second_normalized_input, second_inverse_deviation = group_norm_forward(
        first_output, group_counts, image_window
    )
    normalized_output = second_normalized_input * second_norm_gain2
    moved = normalized_output * (1.0 + scale) + shift
    second = (jax.nn.silu(moved) * image_window).astype(jnp.bfloat16)
    second_pad = framed(second)
    middle_output = start_index + conv_apply(second_pad, conv2_w, "HWIO") * image_window
    attention_normalized_input, attention_inverse_deviation = group_norm_forward(
        middle_output, group_counts, image_window
    )
    attention_input = (attention_normalized_input * attention_norm_gain).astype(jnp.bfloat16)
    qkv_shaped = qkv_w.reshape(channels, HEADS, 3 * head_dim)
    text_shaped = text_w.reshape(text_w.shape[0], HEADS, 2 * head_dim)
    proj_shaped = proj_w.reshape(HEADS, head_dim, channels)
    pixels = rows_dev * width
    group = max(1, 512 // pixels)
    span = group * pixels
    chunks = parts // group

    def to_pairs(values):
        wide = values.shape[1]
        moved = lax.all_to_all(values, "rows", split_axis=0, concat_axis=0, tiled=True)
        moved = moved.reshape(chunks, group, pairs, wide, pixels)
        return jnp.transpose(moved, (2, 0, 3, 1, 4)).reshape(pairs, chunks, wide, span)

    def from_pairs(values):
        wide = values.shape[2]
        moved = values.reshape(pairs, chunks, wide, group, pixels)
        moved = jnp.transpose(moved, (1, 3, 0, 2, 4)).reshape(parts * pairs, wide, pixels)
        return lax.all_to_all(moved, "rows", split_axis=0, concat_axis=0, tiled=True)

    attn_flat = attention_input.reshape(images, pixels, channels)
    qkv_pix = jnp.einsum(
        "ipc,chk->ihkp", attn_flat, qkv_shaped, preferred_element_type=jnp.float32
    ).astype(BF16)
    text_pix = jnp.einsum(
        "itc,chk->ihtk", text, text_shaped, preferred_element_type=jnp.float32
    ).astype(BF16)
    grad_out = cotangent.astype(jnp.float32)
    grad_proj = (grad_out * image_window).astype(BF16).reshape(images, pixels, channels)
    grad_heads = jnp.einsum(
        "ipc,hdc->ihdp", grad_proj, proj_shaped, preferred_element_type=jnp.float32
    ).astype(BF16)
    grad_pair = to_pairs(grad_heads.reshape(images * HEADS, head_dim, pixels))
    text_pair = lax.all_to_all(
        text_pix.reshape(images * HEADS, text.shape[1], 2 * head_dim),
        "rows",
        split_axis=0,
        concat_axis=0,
        tiled=True,
    )
    text_pair = jnp.moveaxis(
        text_pair.reshape(parts, pairs, text.shape[1], 2 * head_dim), 1, 0
    ).reshape(pairs, parts * text.shape[1], 2 * head_dim)
    text_share = text.shape[2] // parts
    text_cols = lax.all_to_all(text, "rows", split_axis=2, concat_axis=1, tiled=True)
    text_cols = lax.all_gather(text_cols, "items", axis=0, tiled=True)
    qkv_pair = to_pairs(qkv_pix.reshape(images * HEADS, 3 * head_dim, pixels))
    pair_index = lax.axis_index("rows") * pairs + jnp.arange(pairs, dtype=jnp.int32)
    pick = ((pair_index // HEADS)[:, None] == jnp.arange(images, dtype=jnp.int32)[None, :]).astype(
        jnp.int32
    )
    pair_extent = jnp.sum(pick[:, :, None] * extent[None, :, :], axis=1)
    results = [
        attention(pair_extent[p : p + 1], qkv_pair[p], text_pair[p], grad_pair[p], width)
        for p in range(pairs)
    ]
    attended, qkv_grad_pair, text_grad_pair = (jnp.stack(parts_of) for parts_of in zip(*results))
    qkv_back = from_pairs(qkv_grad_pair).reshape(images, HEADS, 3 * head_dim, pixels)
    heads_out = from_pairs(attended).reshape(images, HEADS, head_dim, pixels)
    text_back = lax.all_gather(text_grad_pair, "rows", axis=0, tiled=True)
    text_back = text_back.reshape(images, HEADS, 2 * head_dim, parts * text.shape[1])
    text_all = lax.all_gather(text_back, "items", axis=0, tiled=True)
    own_text = lax.dynamic_slice_in_dim(
        text_back, lax.axis_index("rows") * text.shape[1], text.shape[1], 3
    )
    projected = jnp.einsum(
        "ihdp,hdc->ipc", heads_out, proj_shaped, preferred_element_type=jnp.float32
    ).reshape(image.shape)
    output = (middle_output + projected * image_window).astype(BF16)
    proj_grad = jnp.einsum(
        "ipc,ihdp->chd", grad_proj, heads_out, preferred_element_type=jnp.float32
    ).reshape(channels, channels)
    attention_gradient = jnp.einsum(
        "ihkp,chk->ipc", qkv_back, qkv_shaped, preferred_element_type=jnp.float32
    ).reshape(image.shape)
    qkv_grad = jnp.einsum(
        "ihkp,ipc->hkc", qkv_back, attn_flat, preferred_element_type=jnp.float32
    ).reshape(3 * channels, channels)
    text_grad = jnp.einsum(
        "ihkt,chk->itc", own_text, text_shaped, preferred_element_type=jnp.float32
    )
    text_w_grad = jnp.einsum(
        "gtc,ghkt->chk", text_cols, text_all, preferred_element_type=jnp.float32
    ).reshape(text_share, 2 * channels)
    attn_term, attn_gain_grad = group_norm_backward(
        attention_gradient * image_window,
        attention_normalized_input,
        attention_inverse_deviation,
        attention_norm_gain,
        group_counts,
        image_window,
    )
    grad_middle = grad_out + attn_term
    grad_conv2 = (grad_middle * image_window).astype(jnp.bfloat16)
    conv2_grad = kernel_grad(second_pad, grad_conv2)
    grad_second = conv_apply(framed(grad_conv2), conv2_w[::-1, ::-1], "HWOI") * image_window
    grad_moved = grad_second * silu_slope(moved)
    normalized_output_gradient = grad_moved * (1.0 + scale)
    second_normalized_gradient = normalized_output_gradient * second_norm_gain2
    shaped_grad = grouped_input(second_normalized_gradient)
    reshaped_input = grouped_input(second_normalized_input)
    gradient_total_sum, cross_product_sum, scale_sum, shift_sum = lax.psum(
        (
            jnp.sum(shaped_grad, axis=(1, 2, 4)),
            jnp.sum(shaped_grad * reshaped_input, axis=(1, 2, 4)),
            jnp.sum(grad_moved * normalized_output, axis=(1, 2)),
            jnp.sum(grad_moved, axis=(1, 2)),
        ),
        "rows",
    )
    first_output_gradient = apply_group_norm(
        second_normalized_gradient,
        second_normalized_input,
        second_inverse_deviation,
        gradient_total_sum,
        cross_product_sum,
        group_counts,
        image_window,
    )
    second_norm_gradient2 = jnp.sum(
        normalized_output_gradient * second_normalized_input, axis=(0, 1, 2)
    )
    grad_shifts = jnp.concatenate([scale_sum, shift_sum], axis=1).astype(jnp.bfloat16)
    embed_grad = jnp.einsum(
        "ik,ck->ic", grad_shifts, embed_w, preferred_element_type=jnp.float32
    ) * silu_slope(embed_float)
    embed_share = embed_w.shape[0] // parts
    embed_rows = lax.dynamic_slice_in_dim(
        embed_low, lax.axis_index("rows") * embed_share, embed_share, 1
    )
    embed_w_grad = jnp.einsum(
        "ic,ik->ck",
        lax.all_gather(embed_rows, "items", axis=0, tiled=True),
        lax.all_gather(grad_shifts, "items", axis=0, tiled=True),
        preferred_element_type=jnp.float32,
    )
    grad_conv1 = first_output_gradient.astype(jnp.bfloat16)
    conv1_grad = kernel_grad(hidden_pad, grad_conv1)
    grad_hidden = conv_apply(framed(grad_conv1), conv1_w[::-1, ::-1], "HWOI") * image_window
    preactivation_gradient = grad_hidden * silu_slope(first_preactivation)
    start_term, norm1_grad = group_norm_backward(
        preactivation_gradient,
        first_normalized_input,
        first_inverse_deviation,
        first_norm_gain1,
        group_counts,
        image_window,
    )
    image_grad = (grad_middle + start_term) * image_window
    gains = lax.psum(jnp.stack([norm1_grad, second_norm_gradient2, attn_gain_grad]), ("items", "rows"))
    share = channels // parts
    gains = lax.dynamic_slice_in_dim(gains, lax.axis_index("rows") * share, share, 1)

    def total(values):
        return lax.psum(
            lax.psum_scatter(values.astype(BF16), "rows", scatter_dimension=0, tiled=True), "items"
        ).astype(F32)

    def kernel_total(values):
        return jnp.transpose(total(values), (1, 2, 0)).reshape(3, 3, channels, share)

    summed = (
        gains[0],
        kernel_total(conv1_grad),
        embed_w_grad,
        gains[1],
        kernel_total(conv2_grad),
        gains[2],
        total(qkv_grad).T,
        text_w_grad,
        total(proj_grad).T,
    )
    return (
        output,
        image_grad,
        embed_grad,
        text_grad,
        summed[0],
        summed[1],
        summed[2],
        summed[3],
        summed[4],
        summed[5],
        summed[6],
        summed[7],
        summed[8],
    )


def solution(mesh):
    in_specs = (
        P("items", "rows", None, None),
        P("items", None),
        P("items", "rows", None),
        P("items", None),
        P(),
        P(),
        P(),
        P(),
        P(),
        P(),
        P(),
        P(),
        P(),
        P("items", "rows", None, None),
    )
    out_specs = (
        P("items", "rows", None, None),
        P("items", "rows", None, None),
        P("items", None),
        P("items", "rows", None),
        P("rows"),
        P(None, None, None, "rows"),
        P("rows", None),
        P("rows"),
        P(None, None, None, "rows"),
        P("rows"),
        P(None, "rows"),
        P("rows", None),
        P(None, "rows"),
    )
    return jax.shard_map(shards, mesh=mesh, in_specs=in_specs, out_specs=out_specs, check_vma=False)
```

```python
import functools

import jax
import jax.numpy as jnp
from jax import lax
from jax.experimental import pallas as pl
from jax.experimental.pallas import tpu as pltpu
from jax.sharding import PartitionSpec as P

GROUPS = 32
HEADS = 8
F32, BF16 = jnp.float32, jnp.bfloat16
NEG = -1e30


def dot(a, b, ca, cb):
    return lax.dot_general(a, b, (((ca,), (cb,)), ((), ())), preferred_element_type=F32)

def attention_kernel(width, step, bq, ext_ref, qkv_ref, text_ref, go_ref, out_ref, dqkv_ref, dtext_ref,
                     kn, vn, kt, vt, s0, s1, e0, e1, dkt, dvt):
    scores, raised = (s0, s1), (e0, e1)
    chunks, _, span = qkv_ref.shape
    tlen = text_ref.shape[0]
    d = go_ref.shape[1]
    pix = chunks * span
    keys = pix + tlen
    steps = keys // step
    rows_ok, cols_ok = ext_ref[0, 0], ext_ref[0, 1]
    def stage(c, carry):
        base = pl.multiple_of(c * span, span)
        pos = base + lax.broadcasted_iota(jnp.int32, (16, span), 1)
        row = lax.broadcasted_iota(jnp.int32, (16, span), 0)
        ok = (pos // width < rows_ok) & (pos % width < cols_ok)
        extra = jnp.where((row == 0) & jnp.logical_not(ok), NEG, 0.0)
        k = qkv_ref[c, d:2 * d, :]
        v = qkv_ref[c, 2 * d:, :]
        kt[:, pl.ds(base, span)] = k
        vt[:, pl.ds(base, span)] = v
        rest = jnp.zeros((128 - d - 16, span), F32)
        ka = jnp.concatenate([k.astype(F32), extra, rest], axis=0)
        va = jnp.concatenate([v.astype(F32), jnp.where(row < 3, 1.0, 0.0), rest], axis=0)
        kn[pl.ds(base, span), :] = ka.T.astype(BF16)
        vn[pl.ds(base, span), :] = va.T.astype(BF16)
        return carry
    lax.fori_loop(0, chunks, stage, 0)
    tk = text_ref[:, :d].astype(F32)
    tv = text_ref[:, d:].astype(F32)
    kt[:, pix:] = tk.T.astype(BF16)
    vt[:, pix:] = tv.T.astype(BF16)
    lanes = lax.broadcasted_iota(jnp.int32, (tlen, 128 - d), 1)
    kn[pix:, :] = jnp.concatenate([tk, jnp.zeros((tlen, 128 - d), F32)], axis=1).astype(BF16)
    vn[pix:, :] = jnp.concatenate([tv, jnp.where(lanes < 3, 1.0, 0.0)], axis=1).astype(BF16)
    dkt[...] = jnp.zeros_like(dkt)
    dvt[...] = jnp.zeros_like(dvt)

    low_peak = jnp.full((8, bq), -3e38, F32)

    def q_aug(c, half):
        q = qkv_ref[c, :d, half * bq:(half + 1) * bq].astype(F32) * (d ** -0.5)
        r = lax.broadcasted_iota(jnp.int32, (128 - d, bq), 0)
        return jnp.concatenate([q, jnp.where(r == 0, 1.0, 0.0)], axis=0).astype(BF16)

    def run(score, exp, back):
        def body(j, carry):
            pk, total, acc, dq = carry
            at = pl.ds(pl.multiple_of(j * step, step), step)
            if score:
                slot, qa = score
                s = dot(kn[at, :], qa, 1, 0)
                scores[slot][at, :] = s
                pk = jnp.maximum(pk, jnp.max(s.reshape(step // 8, 8, bq), axis=0))
            if exp:
                slot, peak = exp
                e = jnp.exp(scores[slot][at, :] - peak)
                total = total + jnp.sum(e.reshape(step // 8, 8, bq), axis=0)
                low = e.astype(BF16)
                raised[slot][at, :] = low
                acc = acc + dot(vt[:, at], low, 1, 0)
            if back:
                slot, goa, gs, q = back
                dp = dot(vn[at, :], goa, 1, 0)
                e = raised[slot][at, :]
                ds = (e.astype(F32) * dp).astype(BF16)
                dvt[:, at] += dot(gs, e, 1, 1)
                dkt[:, at] += dot(q, ds, 1, 1)
                dq = dq + dot(kt[:, at], ds, 1, 0)
            return pk, total, acc, dq
        init = (low_peak, jnp.zeros((8, bq), F32), jnp.zeros((d, bq), F32), jnp.zeros((d, bq), F32))
        return lax.fori_loop(0, steps, body, init)

    def finish_exp(c, half, total, acc):
        inv = 1.0 / jnp.sum(total, axis=0, keepdims=True)
        o = acc * inv
        cols = slice(half * bq, (half + 1) * bq)
        out_ref[c, :, cols] = o.astype(BF16)
        go = go_ref[c, :, cols].astype(F32)
        nd = -jnp.sum(go * o, axis=0, keepdims=True) * inv
        gs = go * inv
        hi = nd.astype(BF16).astype(F32)
        mid = (nd - hi).astype(BF16).astype(F32)
        lo = nd - hi - mid
        r = lax.broadcasted_iota(jnp.int32, (16, bq), 0)
        extra = jnp.where(r == 0, hi, jnp.where(r == 1, mid, jnp.where(r == 2, lo, 0.0)))
        goa = jnp.concatenate([gs, extra, jnp.zeros((128 - d - 16, bq), F32)], axis=0).astype(BF16)
        return goa

    def put_dq(c, half, dq):
        dqkv_ref[c, :d, half * bq:(half + 1) * bq] = (dq * (d ** -0.5)).astype(BF16)

    def top(pk):
        return jnp.max(pk, axis=0, keepdims=True)

    def q_of(c, half):
        return qkv_ref[c, :d, half * bq:(half + 1) * bq]

    pk, _, _, _ = run((0, q_aug(0, 0)), None, None)
    pk, total, acc, _ = run((1, q_aug(0, 1)), (0, top(pk)), None)
    goa = finish_exp(0, 0, total, acc)

    def two(h, carry):
        pk, goa = carry
        pk2, total, acc, dq = run((0, q_aug(h + 1, 0)), (1, top(pk)), (0, goa, goa[:d], q_of(h, 0)))
        put_dq(h, 0, dq)
        goa = finish_exp(h, 1, total, acc)
        pk3, total, acc, dq = run((1, q_aug(h + 1, 1)), (0, top(pk2)), (1, goa, goa[:d], q_of(h, 1)))
        put_dq(h, 1, dq)
        return pk3, finish_exp(h + 1, 0, total, acc)
    pk, goa = lax.fori_loop(0, chunks - 1, two, (pk, goa))
    last = chunks - 1
    _, total, acc, dq = run(None, (1, top(pk)), (0, goa, goa[:d], q_of(last, 0)))
    put_dq(last, 0, dq)
    goa = finish_exp(last, 1, total, acc)
    _, _, _, dq = run(None, None, (1, goa, goa[:d], q_of(last, 1)))
    put_dq(last, 1, dq)

    def finish(c, carry):
        at = pl.ds(pl.multiple_of(c * span, span), span)
        dqkv_ref[c, d:2 * d, :] = (dkt[:, at] * (d ** -0.5)).astype(BF16)
        dqkv_ref[c, 2 * d:, :] = dvt[:, at].astype(BF16)
        return carry
    lax.fori_loop(0, chunks, finish, 0)
    dtext_ref[:d, :] = (dkt[:, pix:] * (d ** -0.5)).astype(BF16)
    dtext_ref[d:, :] = dvt[:, pix:].astype(BF16)

def attention(ext, qkv, text, go, width):
    chunks, wide, span = qkv.shape
    d = wide // 3
    tlen = text.shape[0]
    keys = chunks * span + tlen
    bq = span // 2
    lanes = keys // 128
    step = 128 * max(n for n in range(1, 12) if lanes % n == 0)
    vm = pl.BlockSpec(memory_space=pltpu.VMEM)
    flops = 2 * 6 * chunks * span * keys * d
    return pl.pallas_call(
        functools.partial(attention_kernel, width, step, bq),
        out_shape=(
            jax.ShapeDtypeStruct(go.shape, BF16),
            jax.ShapeDtypeStruct(qkv.shape, BF16),
            jax.ShapeDtypeStruct((2 * d, tlen), BF16),
        ),
        in_specs=[pl.BlockSpec(memory_space=pltpu.SMEM), vm, vm, vm],
        out_specs=(vm, vm, vm),
        scratch_shapes=[
            pltpu.VMEM((keys, 128), BF16),
            pltpu.VMEM((keys, 128), BF16),
            pltpu.VMEM((d, keys), BF16),
            pltpu.VMEM((d, keys), BF16),
            pltpu.VMEM((keys, bq), F32),
            pltpu.VMEM((keys, bq), F32),
            pltpu.VMEM((keys, bq), BF16),
            pltpu.VMEM((keys, bq), BF16),
            pltpu.VMEM((d, keys), F32),
            pltpu.VMEM((d, keys), F32),
        ],
        compiler_params=pltpu.CompilerParams(vmem_limit_bytes=56 << 20),
        cost_estimate=pl.CostEstimate(
            flops=4 * flops, bytes_accessed=16 * chunks * span * d, transcendentals=chunks * span * keys
        ),
    )(ext, qkv, text, go)


MESH = pl.DeviceIdType.MESH
EPS = 1e-05
WHOLE = pl.BlockSpec(memory_space=pltpu.VMEM)
SCALARS = pl.BlockSpec(memory_space=pltpu.SMEM)
ANYWHERE = pl.BlockSpec(memory_space=pl.ANY)


def exchange_kernel(n, count, *refs):
    stats_ref, rows = refs[0], refs[1 : 1 + count]
    total_ref = refs[1 + count]
    outs = refs[2 + count : 2 + 3 * count]
    slots = refs[2 + 3 * count]
    lands = refs[3 + 3 * count : 3 + 5 * count]
    send, recv, row_send, row_recv = refs[3 + 5 * count :]
    me = lax.axis_index("rows")
    barrier = pltpu.get_barrier_semaphore()

    def greet(k, carry):
        pl.semaphore_signal(
            barrier, inc=1, device_id={"rows": lax.rem(me + k, n)}, device_id_type=MESH
        )
        return carry

    lax.fori_loop(1, n, greet, 0)
    slots[me] = stats_ref[...]
    pl.semaphore_wait(barrier, n - 1)

    def share(k):
        return pltpu.make_async_remote_copy(
            src_ref=stats_ref,
            dst_ref=slots.at[me],
            send_sem=send.at[k],
            recv_sem=recv.at[k],
            device_id={"rows": lax.rem(me + k, n)},
            device_id_type=MESH,
        )

    def start(k, carry):
        share(k).start()
        return carry

    lax.fori_loop(1, n, start, 0)

    def row_copy(j, side):
        last = rows[j].shape[1] - 1
        at = last if side == 0 else 0
        return pltpu.make_async_remote_copy(
            src_ref=rows[j].at[:, at : at + 1],
            dst_ref=lands[2 * j + side],
            send_sem=row_send.at[2 * j + side],
            recv_sem=row_recv.at[2 * j + side],
            device_id={"rows": me + 1 if side == 0 else me - 1},
            device_id_type=MESH,
        )

    for j in range(count):

        @pl.when(me < n - 1)
        def _():
            row_copy(j, 0).start()

        @pl.when(me > 0)
        def _():
            row_copy(j, 1).start()

    def finish(k, carry):
        share(k).wait()
        return carry

    lax.fori_loop(1, n, finish, 0)
    total_ref[...] = lax.fori_loop(1, n, lambda k, s: s + slots[k], slots[0])
    for j in range(count):

        @pl.when(me > 0)
        def _():
            row_copy(j, 0).wait_recv()
            outs[2 * j][...] = lands[2 * j][...]

        @pl.when(me == 0)
        def _():
            outs[2 * j][...] = jnp.zeros_like(outs[2 * j])

        @pl.when(me < n - 1)
        def _():
            row_copy(j, 1).wait_recv()
            outs[2 * j + 1][...] = lands[2 * j + 1][...]
            row_copy(j, 0).wait_send()

        @pl.when(me == n - 1)
        def _():
            outs[2 * j + 1][...] = jnp.zeros_like(outs[2 * j + 1])

        @pl.when(me > 0)
        def _():
            row_copy(j, 1).wait_send()


def exchange(stats, rows, identity):
    n = lax.axis_size("rows")
    edge = []
    for array in rows:
        edge += [jax.ShapeDtypeStruct(array.shape[:1] + (1,) + array.shape[2:], array.dtype)] * 2
    count = len(rows)
    return pl.pallas_call(
        functools.partial(exchange_kernel, n, count),
        out_shape=(jax.ShapeDtypeStruct(stats.shape, F32), *edge),
        in_specs=[WHOLE] + [ANYWHERE] * count,
        out_specs=(WHOLE,) * (1 + 2 * count),
        scratch_shapes=[
            pltpu.VMEM((n,) + stats.shape, F32),
            *[pltpu.VMEM(e.shape, e.dtype) for e in edge],
            pltpu.SemaphoreType.DMA((n,)),
            pltpu.SemaphoreType.DMA((n,)),
            pltpu.SemaphoreType.DMA((max(1, 2 * count),)),
            pltpu.SemaphoreType.DMA((max(1, 2 * count),)),
        ],
        compiler_params=pltpu.CompilerParams(collective_id=identity, has_side_effects=True),
        name=f"exchange{identity}",
    )(stats, *rows)


def group_sums(rows):
    channels = rows.shape[1]
    size = channels // GROUPS
    one = lax.broadcasted_iota(jnp.int32, (channels, channels), 0) // size
    two = lax.broadcasted_iota(jnp.int32, (channels, channels), 1) // size
    same = jnp.where(one == two, 1.0, 0.0).astype(BF16)
    high = rows.astype(BF16)
    rest = rows - high.astype(F32)
    mid = rest.astype(BF16)
    tail = (rest - mid.astype(F32)).astype(BF16)
    return dot(high, same, 1, 0) + dot(mid, same, 1, 0) + dot(tail, same, 1, 0)


def image_count(info, i, channels):
    return (info[i, 0] * info[i, 1]).astype(F32) * (channels // GROUPS)


def norm_of(stats, count):
    sums = group_sums(stats)
    average = sums[0:1] / count
    square = sums[1:2] / count
    return average, lax.rsqrt(square - average * average + EPS)


def means_of(stats, weight, count):
    sums = group_sums(stats * weight)
    return sums[0:1] / count, sums[1:2] / count


def window(info, i, row, shape):
    ok = (row >= 0) & (row < info[i, 0])
    limit = jnp.where(ok, info[i, 1], 0)
    return jnp.where(lax.broadcasted_iota(jnp.int32, shape, 0) < limit, 1.0, 0.0)


def padded_row(center, above, below, i, r):
    if r == 0:
        return above[i, 0]
    if r == center.shape[1] + 1:
        return below[i, 0]
    return center[i, r - 1]


def put_shifted(out, i, r, value):
    width, channels = value.shape
    column = lax.broadcasted_iota(jnp.int32, value.shape, 0)
    left = jnp.where(column == 0, 0.0, pltpu.roll(value, 1, 0))
    right = jnp.where(column == width - 1, 0.0, pltpu.roll(value, width - 1, 0))
    out[i, r, :, :channels] = left.astype(BF16)
    out[i, r, :, channels : 2 * channels] = value.astype(BF16)
    out[i, r, :, 2 * channels :] = right.astype(BF16)


def sigmoid(v):
    return 1.0 / (1.0 + jnp.exp(-v))


def silu_slope(v):
    s = sigmoid(v)
    return s * (1.0 + v * (1.0 - s))


def put_stats(stats_ref, i, first, second):
    channels = first.shape[1]
    one = jnp.sum(first, axis=0, keepdims=True)
    two = jnp.sum(second, axis=0, keepdims=True)
    row = lax.broadcasted_iota(jnp.int32, (8, channels), 0)
    stats_ref[i] = jnp.where(row == 0, one, jnp.where(row == 1, two, 0.0))


def tap_rows(shifted, tap, images, rows_dev, width):
    block = shifted[:, pl.ds(tap, rows_dev)]
    return block.reshape(images * rows_dev * width, shifted.shape[3])


def conv1_kernel(info, image, above, below, stats, gain, weight, first, out_stats, shifted, acc):
    images, rows_dev, width, channels = image.shape
    tap = pl.program_id(0)
    base = info[0, 2]

    @pl.when(tap == 0)
    def _():
        for i in range(images):
            average, inverse = norm_of(stats[i], image_count(info, i, channels))
            for r in range(rows_dev + 2):
                inside = window(info, i, base + r - 1, (width, channels))
                start = padded_row(image, above, below, i, r).astype(F32) * inside
                value = (start - average) * inverse * inside * gain[...]
                put_shifted(shifted, i, r, value * sigmoid(value) * inside)

    part = dot(tap_rows(shifted, tap, images, rows_dev, width), weight[0], 1, 0)

    @pl.when(tap == 0)
    def _():
        acc[...] = part

    @pl.when(tap > 0)
    def _():
        acc[...] += part

    @pl.when(tap == 2)
    def _():
        for i in range(images):
            one = two = jnp.zeros((width, channels), F32)
            for r in range(rows_dev):
                inside = window(info, i, base + r, (width, channels))
                at = (i * rows_dev + r) * width
                value = acc[at : at + width] * inside
                first[i, r] = value
                one = one + value
                two = two + value * value
            put_stats(out_stats, i, one, two)


def moved_of(value, inside, average, inverse, gain, scale, shift):
    normal = (value - average) * inverse * inside
    return normal, normal * gain * (1.0 + scale) + shift


def conv2_kernel(
    info, first, above, below, stats, gain, shifts, image, weight, middle, out_stats, shifted, acc
):
    images, rows_dev, width, channels = first.shape
    tap = pl.program_id(0)
    base = info[0, 2]

    @pl.when(tap == 0)
    def _():
        for i in range(images):
            average, inverse = norm_of(stats[i], image_count(info, i, channels))
            scale, shift = shifts[i : i + 1, :channels], shifts[i : i + 1, channels:]
            for r in range(rows_dev + 2):
                inside = window(info, i, base + r - 1, (width, channels))
                value = padded_row(first, above, below, i, r)
                _, moved = moved_of(value, inside, average, inverse, gain[...], scale, shift)
                put_shifted(shifted, i, r, moved * sigmoid(moved) * inside)

    part = dot(tap_rows(shifted, tap, images, rows_dev, width), weight[0], 1, 0)

    @pl.when(tap == 0)
    def _():
        acc[...] = part

    @pl.when(tap > 0)
    def _():
        acc[...] += part

    @pl.when(tap == 2)
    def _():
        for i in range(images):
            one = two = jnp.zeros((width, channels), F32)
            for r in range(rows_dev):
                inside = window(info, i, base + r, (width, channels))
                at = (i * rows_dev + r) * width
                value = (image[i, r].astype(F32) + acc[at : at + width]) * inside
                middle[i, r] = value
                one = one + value
                two = two + value * value
            put_stats(out_stats, i, one, two)


def dgrad(shifted, tap, weight, images, rows_dev, width):
    channels = weight.shape[2]
    lhs = tap_rows(shifted, tap, images, rows_dev, width)
    part = None
    for b in range(3):
        term = dot(
            lhs[:, b * channels : (b + 1) * channels],
            weight[0, (2 - b) * channels : (3 - b) * channels, :],
            1,
            1,
        )
        part = term if part is None else part + term
    return part


def back2_kernel(
    info, grad, grad_above, grad_below, middle, mid_above, mid_below, cot, cot_above, cot_below,
    mid_stats, grad_stats, attn_gain, first, first_stats, gain, shifts, weight,
    grad_middle, moved_grad, out_stats, shifted, acc,
):
    images, rows_dev, width, channels = first.shape
    tap = pl.program_id(0)
    base = info[0, 2]

    @pl.when(tap == 0)
    def _():
        for i in range(images):
            count = image_count(info, i, channels)
            average, inverse = norm_of(mid_stats[i], count)
            mean, cross = means_of(grad_stats[i], attn_gain[...], count)
            for r in range(rows_dev + 2):
                inside = window(info, i, base + r - 1, (width, channels))
                normal = (padded_row(middle, mid_above, mid_below, i, r) - average) * inverse
                dx = padded_row(grad, grad_above, grad_below, i, r) * attn_gain[...]
                term = (dx - mean - normal * cross) * inverse * inside
                total = padded_row(cot, cot_above, cot_below, i, r).astype(F32) + term
                if 0 < r <= rows_dev:
                    grad_middle[i, r - 1] = total
                put_shifted(shifted, i, r, total * inside)

    part = dgrad(shifted, tap, weight, images, rows_dev, width)

    @pl.when(tap == 0)
    def _():
        acc[...] = part

    @pl.when(tap > 0)
    def _():
        acc[...] += part

    @pl.when(tap == 2)
    def _():
        for i in range(images):
            average, inverse = norm_of(first_stats[i], image_count(info, i, channels))
            scale, shift = shifts[i : i + 1, :channels], shifts[i : i + 1, channels:]
            one = two = jnp.zeros((width, channels), F32)
            for r in range(rows_dev):
                inside = window(info, i, base + r, (width, channels))
                at = (i * rows_dev + r) * width
                normal, moved = moved_of(
                    first[i, r], inside, average, inverse, gain[...], scale, shift
                )
                value = acc[at : at + width] * inside * silu_slope(moved)
                moved_grad[i, r] = value
                one = one + value
                two = two + value * normal
            put_stats(out_stats, i, one, two)


def back1_kernel(
    info, grad, grad_above, grad_below, first, first_above, first_below, first_stats, grad_stats,
    gain, shifts, image, image_stats, first_gain, weight,
    pre_grad, out_stats, shifted, acc,
):
    images, rows_dev, width, channels = first.shape
    tap = pl.program_id(0)
    base = info[0, 2]

    @pl.when(tap == 0)
    def _():
        for i in range(images):
            count = image_count(info, i, channels)
            average, inverse = norm_of(first_stats[i], count)
            factor = gain[...] * (1.0 + shifts[i : i + 1, :channels])
            mean, cross = means_of(grad_stats[i], factor, count)
            for r in range(rows_dev + 2):
                inside = window(info, i, base + r - 1, (width, channels))
                normal = (padded_row(first, first_above, first_below, i, r) - average) * inverse
                dx = padded_row(grad, grad_above, grad_below, i, r) * factor
                put_shifted(shifted, i, r, (dx - mean - normal * cross) * inverse * inside)

    part = dgrad(shifted, tap, weight, images, rows_dev, width)

    @pl.when(tap == 0)
    def _():
        acc[...] = part

    @pl.when(tap > 0)
    def _():
        acc[...] += part

    @pl.when(tap == 2)
    def _():
        for i in range(images):
            average, inverse = norm_of(image_stats[i], image_count(info, i, channels))
            one = two = jnp.zeros((width, channels), F32)
            for r in range(rows_dev):
                inside = window(info, i, base + r, (width, channels))
                at = (i * rows_dev + r) * width
                normal = (image[i, r].astype(F32) - average) * inverse * inside
                slope = silu_slope(normal * first_gain[...])
                value = acc[at : at + width] * inside * slope
                pre_grad[i, r] = value
                one = one + value
                two = two + value * normal
            put_stats(out_stats, i, one, two)


def conv_call(kernel, info, inputs, weight, outs, flipped):
    images, rows_dev, width, channels = outs[0].shape

    def whole(shape):
        return pl.BlockSpec(shape, lambda tap: (0,) * len(shape))

    def tap_of(tap):
        return ((2 - tap) if flipped else tap, 0, 0)

    weight = weight.reshape(3, 3 * channels, channels)
    flops = 2 * 9 * images * rows_dev * width * channels * channels
    moved = sum(a.size * a.dtype.itemsize for a in (*inputs, weight, *outs))
    return pl.pallas_call(
        kernel,
        grid=(3,),
        out_shape=tuple(outs),
        in_specs=[SCALARS]
        + [whole(a.shape) for a in inputs]
        + [pl.BlockSpec((1, 3 * channels, channels), tap_of)],
        out_specs=tuple(whole(o.shape) for o in outs),
        scratch_shapes=[pltpu.VMEM((images * rows_dev * width, channels), F32)],
        compiler_params=pltpu.CompilerParams(vmem_limit_bytes=48 << 20),
        cost_estimate=pl.CostEstimate(flops=flops, bytes_accessed=moved, transcendentals=0),
        name=kernel.__name__,
    )(info, *inputs, weight)


def weight_grad_kernel(grads, shifted, out, turned):
    images, padded, width, wide = shifted.shape
    rows_dev, channels = padded - 2, wide // 3
    pixels = images * rows_dev * width
    tap = pl.program_id(0)

    @pl.when(tap == 0)
    def _():
        center = grads[:, 1 : rows_dev + 1, :, channels : 2 * channels]
        turned[...] = center.reshape(pixels, channels).astype(F32).T.astype(BF16)

    column = pl.multiple_of((tap % 3) * channels, channels)
    rhs = shifted[:, pl.ds(tap // 3, rows_dev), :, pl.ds(column, channels)]
    out[...] = dot(turned[...], rhs.reshape(pixels, channels), 1, 0).astype(BF16)


def weight_grad(grads, shifted):
    images, padded, width, wide = shifted.shape
    channels = wide // 3
    pixels = images * (padded - 2) * width

    def whole(shape):
        return pl.BlockSpec(shape, lambda tap: (0,) * len(shape))

    return pl.pallas_call(
        weight_grad_kernel,
        grid=(9,),
        out_shape=jax.ShapeDtypeStruct((channels, 9 * channels), BF16),
        in_specs=[whole(grads.shape), whole(shifted.shape)],
        out_specs=pl.BlockSpec((channels, channels), lambda tap: (0, tap)),
        scratch_shapes=[pltpu.VMEM((channels, pixels), BF16)],
        compiler_params=pltpu.CompilerParams(vmem_limit_bytes=32 << 20),
        cost_estimate=pl.CostEstimate(
            flops=18 * pixels * channels * channels, bytes_accessed=18 * channels * channels, transcendentals=0
        ),
        name="weight_grad",
    )(grads, shifted)


def project_kernel(info, middle, stats, gain, weight, attn, qkv):
    images, rows_dev, width, channels = middle.shape
    pixels = rows_dev * width
    heads, wide = HEADS, weight.shape[0] // HEADS
    base = info[0, 2]
    for i in range(images):
        average, inverse = norm_of(stats[i], image_count(info, i, channels))
        for r in range(rows_dev):
            inside = window(info, i, base + r, (width, channels))
            value = (middle[i, r] - average) * inverse * inside * gain[...]
            attn[i, r * width : (r + 1) * width] = value.astype(BF16)
        for h in range(heads):
            block = dot(weight[h * wide : (h + 1) * wide], attn[i], 1, 1)
            qkv[i * heads + h] = block.astype(BF16)


def project(info, middle, stats, gain, weight):
    images, rows_dev, width, channels = middle.shape
    pixels = rows_dev * width
    return pl.pallas_call(
        project_kernel,
        out_shape=(
            jax.ShapeDtypeStruct((images, pixels, channels), BF16),
            jax.ShapeDtypeStruct((images * HEADS, weight.shape[0] // HEADS, pixels), BF16),
        ),
        in_specs=[SCALARS, WHOLE, WHOLE, WHOLE, WHOLE],
        out_specs=(WHOLE, WHOLE),
        compiler_params=pltpu.CompilerParams(vmem_limit_bytes=32 << 20),
        name="project",
    )(info, middle, stats, gain, weight)


def unproject_kernel(info, middle, stats, grads, weight, out, out_stats):
    images, rows_dev, width, channels = middle.shape
    wide, pixels = grads.shape[1], grads.shape[2]
    base = info[0, 2]
    for i in range(images):
        average, inverse = norm_of(stats[i], image_count(info, i, channels))
        acc = None
        for h in range(HEADS):
            turned = grads[i * HEADS + h].astype(F32).T.astype(BF16)
            term = dot(turned, weight[h * wide : (h + 1) * wide], 1, 0)
            acc = term if acc is None else acc + term
        one = two = jnp.zeros((width, channels), F32)
        for r in range(rows_dev):
            inside = window(info, i, base + r, (width, channels))
            value = acc[r * width : (r + 1) * width] * inside
            out[i, r] = value
            one = one + value
            two = two + value * ((middle[i, r] - average) * inverse)
        put_stats(out_stats, i, one, two)


def unproject(info, middle, stats, grads, weight):
    images, rows_dev, width, channels = middle.shape
    return pl.pallas_call(
        unproject_kernel,
        out_shape=(
            jax.ShapeDtypeStruct(middle.shape, F32),
            jax.ShapeDtypeStruct(stats.shape, F32),
        ),
        in_specs=[SCALARS, WHOLE, WHOLE, WHOLE, WHOLE],
        out_specs=(WHOLE, WHOLE),
        compiler_params=pltpu.CompilerParams(vmem_limit_bytes=32 << 20),
        name="unproject",
    )(info, middle, stats, grads, weight)


def finish_kernel(info, pre_grad, grad_stats, image, stats, gain, grad_middle, out):
    images, rows_dev, width, channels = image.shape
    base = info[0, 2]
    for i in range(images):
        count = image_count(info, i, channels)
        average, inverse = norm_of(stats[i], count)
        mean, cross = means_of(grad_stats[i], gain[...], count)
        for r in range(rows_dev):
            inside = window(info, i, base + r, (width, channels))
            normal = (image[i, r].astype(F32) - average) * inverse
            term = (pre_grad[i, r] * gain[...] - mean - normal * cross) * inverse
            out[i, r] = (grad_middle[i, r] + term) * inside


def finish(info, pre_grad, grad_stats, image, stats, gain, grad_middle):
    return pl.pallas_call(
        finish_kernel,
        out_shape=jax.ShapeDtypeStruct(image.shape, F32),
        in_specs=[SCALARS] + [WHOLE] * 6,
        out_specs=WHOLE,
        compiler_params=pltpu.CompilerParams(vmem_limit_bytes=32 << 20),
        name="finish",
    )(info, pre_grad, grad_stats, image, stats, gain, grad_middle)


def shards(
    image, embed, text, extent, first_norm_gain1, conv1_w, embed_w, second_norm_gain2, conv2_w,
    attention_norm_gain, qkv_w, text_w, proj_w, cotangent,
):
    images, rows_dev, width, channels = image.shape
    parts = lax.axis_size("rows")
    me = lax.axis_index("rows")
    pairs = images * HEADS // parts
    head_dim = channels // HEADS
    pixels = rows_dev * width
    group = max(1, 512 // pixels)
    span = group * pixels
    chunks = parts // group
    tokens = text.shape[1]
    first_row = jnp.full((images, 1), me * rows_dev, jnp.int32)
    info = jnp.concatenate([extent, first_row], axis=1)
    gain1 = first_norm_gain1.reshape(1, channels)
    gain2 = second_norm_gain2.reshape(1, channels)
    gain3 = attention_norm_gain.reshape(1, channels)
    rowpos = me * rows_dev + jnp.arange(rows_dev, dtype=jnp.int32)
    colpos = jnp.arange(width, dtype=jnp.int32)
    inside = (rowpos[None, :, None] < extent[:, 0, None, None]) & (
        colpos[None, None, :] < extent[:, 1, None, None]
    )
    image_window = inside.astype(F32)[..., None]

    gathered_text = lax.all_gather(text, "rows", axis=1, tiled=True)
    embed_float = embed.astype(F32)
    embed_low = jax.nn.silu(embed_float).astype(BF16)
    shifts = jnp.dot(embed_low, embed_w, preferred_element_type=F32)
    qkv_turned = qkv_w.T
    proj_shaped = proj_w.reshape(HEADS, head_dim, channels)

    start = image.astype(F32) * image_window
    zeros = jnp.zeros((images, 6, channels), F32)
    stats0 = jnp.concatenate(
        [
            jnp.sum(start, axis=(1, 2))[:, None],
            jnp.sum(start * start, axis=(1, 2))[:, None],
            zeros,
        ],
        axis=1,
    )
    stats1, image_above, image_below, cot_above, cot_below = exchange(
        stats0, (image, cotangent), 0
    )
    full = jax.ShapeDtypeStruct(image.shape, F32)
    sums = jax.ShapeDtypeStruct((images, 8, channels), F32)
    padded = jax.ShapeDtypeStruct((images, rows_dev + 2, width, 3 * channels), BF16)
    first, stats, hidden3 = conv_call(
        conv1_kernel,
        info,
        (image, image_above, image_below, stats1, gain1),
        conv1_w,
        (full, sums, padded),
        False,
    )
    stats2, first_above, first_below = exchange(stats, (first,), 1)
    middle, stats, second3 = conv_call(
        conv2_kernel,
        info,
        (first, first_above, first_below, stats2, gain2, shifts, image),
        conv2_w,
        (full, sums, padded),
        False,
    )
    stats3, mid_above, mid_below = exchange(stats, (middle,), 2)
    attn_flat, qkv_pix = project(info, middle, stats3, gain3, qkv_turned)

    def to_pairs(values):
        wide = values.shape[1]
        moved = lax.all_to_all(values, "rows", split_axis=0, concat_axis=0, tiled=True)
        moved = moved.reshape(chunks, group, pairs, wide, pixels)
        return jnp.transpose(moved, (2, 0, 3, 1, 4)).reshape(pairs, chunks, wide, span)

    def from_pairs(values):
        wide = values.shape[2]
        moved = values.reshape(pairs, chunks, wide, group, pixels)
        moved = jnp.transpose(moved, (1, 3, 0, 2, 4)).reshape(parts * pairs, wide, pixels)
        return lax.all_to_all(moved, "rows", split_axis=0, concat_axis=0, tiled=True)

    qkv_pair = to_pairs(qkv_pix)
    grad_proj = (cotangent.astype(F32) * image_window).astype(BF16).reshape(images, pixels, channels)
    grad_heads = jnp.einsum(
        "ipc,hdc->ihdp", grad_proj, proj_shaped, preferred_element_type=F32
    ).astype(BF16)
    grad_pair = to_pairs(grad_heads.reshape(images * HEADS, head_dim, pixels))
    pair_results = []
    for p in range(pairs):
        pair = me * pairs + p
        item, head = pair // HEADS, pair % HEADS
        weight = lax.dynamic_slice_in_dim(text_w, head * 2 * head_dim, 2 * head_dim, 1)
        own = lax.dynamic_index_in_dim(gathered_text, item, 0, False)
        text_pair = jnp.dot(own, weight, preferred_element_type=F32).astype(BF16)
        pair_extent = lax.dynamic_slice_in_dim(extent, item, 1, 0)
        pair_results.append(attention(pair_extent, qkv_pair[p], text_pair, grad_pair[p], width))
    attended, qkv_grad_pair, text_grad_pair = (jnp.stack(r) for r in zip(*pair_results))
    qkv_back = from_pairs(qkv_grad_pair)
    heads_out = from_pairs(attended).reshape(images, HEADS, head_dim, pixels)
    text_back = lax.all_gather(text_grad_pair, "rows", axis=0, tiled=True)
    text_back = text_back.reshape(images, HEADS, 2 * head_dim, parts * tokens)

    attn_grad, stats = unproject(info, middle, stats3, qkv_back, qkv_turned)
    stats4, grad_above, grad_below = exchange(stats, (attn_grad,), 3)
    grad_middle, moved_grad, stats, conv2_grad3 = conv_call(
        back2_kernel,
        info,
        (attn_grad, grad_above, grad_below, middle, mid_above, mid_below, cotangent, cot_above,
         cot_below, stats3, stats4, gain3, first, stats2, gain2, shifts),
        conv2_w,
        (full, full, sums, padded),
        True,
    )
    conv2_grad = weight_grad(conv2_grad3, second3)
    stats5, moved_above, moved_below = exchange(stats, (moved_grad,), 4)
    pre_grad, stats, conv1_grad3 = conv_call(
        back1_kernel,
        info,
        (moved_grad, moved_above, moved_below, first, first_above, first_below, stats2, stats5,
         gain2, shifts, image, stats1, gain1),
        conv1_w,
        (full, sums, padded),
        True,
    )
    conv1_grad = weight_grad(conv1_grad3, hidden3)
    (stats6,) = exchange(stats, (), 5)
    image_grad = finish(info, pre_grad, stats6, image, stats1, gain1, grad_middle)

    projected = jnp.einsum(
        "ihdp,hdc->ipc", heads_out, proj_shaped, preferred_element_type=F32
    ).reshape(image.shape)
    output = (middle + projected * image_window).astype(BF16)
    proj_grad = jnp.einsum(
        "ipc,ihdp->chd", grad_proj, heads_out, preferred_element_type=F32
    ).reshape(channels, channels)
    qkv_grad = jnp.einsum(
        "ihkp,ipc->hkc",
        qkv_back.reshape(images, HEADS, 3 * head_dim, pixels),
        attn_flat,
        preferred_element_type=F32,
    ).reshape(3 * channels, channels)
    own_text = lax.dynamic_slice_in_dim(text_back, me * tokens, tokens, 3)
    text_shaped = text_w.reshape(text_w.shape[0], HEADS, 2 * head_dim)
    text_grad = jnp.einsum("ihkt,chk->itc", own_text, text_shaped, preferred_element_type=F32)
    text_share = text.shape[2] // parts
    text_cols = lax.dynamic_slice_in_dim(gathered_text, me * text_share, text_share, 2)
    text_cols = lax.all_gather(text_cols, "items", axis=0, tiled=True)
    text_all = lax.all_gather(text_back, "items", axis=0, tiled=True)
    text_w_grad = jnp.einsum(
        "gtc,ghkt->chk", text_cols, text_all, preferred_element_type=F32
    ).reshape(text_share, 2 * channels)

    scale_sum = stats5[:, 1] * gain2
    grad_shifts = jnp.concatenate([scale_sum, stats5[:, 0]], axis=1).astype(BF16)
    embed_grad = jnp.einsum(
        "ik,ck->ic", grad_shifts, embed_w, preferred_element_type=F32
    ) * silu_slope(embed_float)
    embed_share = embed_w.shape[0] // parts
    embed_rows = lax.dynamic_slice_in_dim(embed_low, me * embed_share, embed_share, 1)
    embed_w_grad = jnp.einsum(
        "ic,ik->ck",
        lax.all_gather(embed_rows, "items", axis=0, tiled=True),
        lax.all_gather(grad_shifts, "items", axis=0, tiled=True),
        preferred_element_type=F32,
    )
    share = channels // parts
    gains = jnp.stack(
        [
            jnp.sum(stats6[:, 1], axis=0),
            jnp.sum(stats5[:, 1] * (1.0 + shifts[:, :channels]), axis=0),
            jnp.sum(stats4[:, 1], axis=0),
        ]
    )
    gains = lax.dynamic_slice_in_dim(gains, me * share, share, 1)
    gains = lax.psum(gains, "items")

    def total(values):
        return lax.psum(
            lax.psum_scatter(values.astype(BF16), "rows", scatter_dimension=0, tiled=True), "items"
        ).astype(F32)

    def kernel_total(values):
        return total(values).T.reshape(3, 3, channels, share)

    return (
        output,
        image_grad,
        embed_grad,
        text_grad,
        gains[0],
        kernel_total(conv1_grad),
        embed_w_grad,
        gains[1],
        kernel_total(conv2_grad),
        gains[2],
        total(qkv_grad).T,
        text_w_grad,
        total(proj_grad).T,
    )


def solution(mesh):
    in_specs = (
        P("items", "rows", None, None),
        P("items", None),
        P("items", "rows", None),
        P("items", None),
        P(),
        P(),
        P(),
        P(),
        P(),
        P(),
        P(),
        P(),
        P(),
        P("items", "rows", None, None),
    )
    out_specs = (
        P("items", "rows", None, None),
        P("items", "rows", None, None),
        P("items", None),
        P("items", "rows", None),
        P("rows"),
        P(None, None, None, "rows"),
        P("rows", None),
        P("rows"),
        P(None, None, None, "rows"),
        P("rows"),
        P(None, "rows"),
        P("rows", None),
        P(None, "rows"),
    )
    return jax.shard_map(shards, mesh=mesh, in_specs=in_specs, out_specs=out_specs, check_vma=False)
```

```python
import functools

import jax
import jax.numpy as jnp
from jax import lax
from jax.experimental import pallas as pl
from jax.experimental.pallas import tpu as pltpu
from jax.sharding import PartitionSpec as P

GROUPS = 32
HEADS = 8
F32, BF16 = jnp.float32, jnp.bfloat16
NEG = -1e30


def dot(a, b, ca, cb):
    return lax.dot_general(a, b, (((ca,), (cb,)), ((), ())), preferred_element_type=F32)

def attention_kernel(width, step, bq, ext_ref, qkv_ref, text_ref, go_ref, out_ref, dqkv_ref, dtext_ref,
                     kn, vn, kt, vt, s0, s1, e0, e1, dkt, dvt):
    scores, raised = (s0, s1), (e0, e1)
    chunks, _, span = qkv_ref.shape
    tlen = text_ref.shape[0]
    d = go_ref.shape[1]
    pix = chunks * span
    keys = pix + tlen
    steps = keys // step
    rows_ok, cols_ok = ext_ref[0, 0], ext_ref[0, 1]
    def stage(c, carry):
        base = pl.multiple_of(c * span, span)
        pos = base + lax.broadcasted_iota(jnp.int32, (16, span), 1)
        row = lax.broadcasted_iota(jnp.int32, (16, span), 0)
        ok = (pos // width < rows_ok) & (pos % width < cols_ok)
        extra = jnp.where((row == 0) & jnp.logical_not(ok), NEG, 0.0)
        k = qkv_ref[c, d:2 * d, :]
        v = qkv_ref[c, 2 * d:, :]
        kt[:, pl.ds(base, span)] = k
        vt[:, pl.ds(base, span)] = v
        rest = jnp.zeros((128 - d - 16, span), F32)
        ka = jnp.concatenate([k.astype(F32), extra, rest], axis=0)
        va = jnp.concatenate([v.astype(F32), jnp.where(row < 3, 1.0, 0.0), rest], axis=0)
        kn[pl.ds(base, span), :] = ka.T.astype(BF16)
        vn[pl.ds(base, span), :] = va.T.astype(BF16)
        return carry
    lax.fori_loop(0, chunks, stage, 0)
    tk = text_ref[:, :d].astype(F32)
    tv = text_ref[:, d:].astype(F32)
    kt[:, pix:] = tk.T.astype(BF16)
    vt[:, pix:] = tv.T.astype(BF16)
    lanes = lax.broadcasted_iota(jnp.int32, (tlen, 128 - d), 1)
    kn[pix:, :] = jnp.concatenate([tk, jnp.zeros((tlen, 128 - d), F32)], axis=1).astype(BF16)
    vn[pix:, :] = jnp.concatenate([tv, jnp.where(lanes < 3, 1.0, 0.0)], axis=1).astype(BF16)
    dkt[...] = jnp.zeros_like(dkt)
    dvt[...] = jnp.zeros_like(dvt)

    low_peak = jnp.full((8, bq), -3e38, F32)

    def q_aug(c, half):
        q = qkv_ref[c, :d, half * bq:(half + 1) * bq].astype(F32) * (d ** -0.5)
        r = lax.broadcasted_iota(jnp.int32, (128 - d, bq), 0)
        return jnp.concatenate([q, jnp.where(r == 0, 1.0, 0.0)], axis=0).astype(BF16)

    def run(score, exp, back):
        def body(j, carry):
            pk, total, acc, dq = carry
            at = pl.ds(pl.multiple_of(j * step, step), step)
            if score:
                slot, qa = score
                s = dot(kn[at, :], qa, 1, 0)
                scores[slot][at, :] = s
                pk = jnp.maximum(pk, jnp.max(s.reshape(step // 8, 8, bq), axis=0))
            if exp:
                slot, peak = exp
                e = jnp.exp(scores[slot][at, :] - peak)
                total = total + jnp.sum(e.reshape(step // 8, 8, bq), axis=0)
                low = e.astype(BF16)
                raised[slot][at, :] = low
                acc = acc + dot(vt[:, at], low, 1, 0)
            if back:
                slot, goa, gs, q = back
                dp = dot(vn[at, :], goa, 1, 0)
                e = raised[slot][at, :]
                ds = (e.astype(F32) * dp).astype(BF16)
                dvt[:, at] += dot(gs, e, 1, 1)
                dkt[:, at] += dot(q, ds, 1, 1)
                dq = dq + dot(kt[:, at], ds, 1, 0)
            return pk, total, acc, dq
        init = (low_peak, jnp.zeros((8, bq), F32), jnp.zeros((d, bq), F32), jnp.zeros((d, bq), F32))
        return lax.fori_loop(0, steps, body, init)

    def finish_exp(c, half, total, acc):
        inv = 1.0 / jnp.sum(total, axis=0, keepdims=True)
        o = acc * inv
        cols = slice(half * bq, (half + 1) * bq)
        out_ref[c, :, cols] = o.astype(BF16)
        go = go_ref[c, :, cols].astype(F32)
        nd = -jnp.sum(go * o, axis=0, keepdims=True) * inv
        gs = go * inv
        hi = nd.astype(BF16).astype(F32)
        mid = (nd - hi).astype(BF16).astype(F32)
        lo = nd - hi - mid
        r = lax.broadcasted_iota(jnp.int32, (16, bq), 0)
        extra = jnp.where(r == 0, hi, jnp.where(r == 1, mid, jnp.where(r == 2, lo, 0.0)))
        goa = jnp.concatenate([gs, extra, jnp.zeros((128 - d - 16, bq), F32)], axis=0).astype(BF16)
        return goa

    def put_dq(c, half, dq):
        dqkv_ref[c, :d, half * bq:(half + 1) * bq] = (dq * (d ** -0.5)).astype(BF16)

    def top(pk):
        return jnp.max(pk, axis=0, keepdims=True)

    def q_of(c, half):
        return qkv_ref[c, :d, half * bq:(half + 1) * bq]

    pk, _, _, _ = run((0, q_aug(0, 0)), None, None)
    pk, total, acc, _ = run((1, q_aug(0, 1)), (0, top(pk)), None)
    goa = finish_exp(0, 0, total, acc)

    def two(h, carry):
        pk, goa = carry
        pk2, total, acc, dq = run((0, q_aug(h + 1, 0)), (1, top(pk)), (0, goa, goa[:d], q_of(h, 0)))
        put_dq(h, 0, dq)
        goa = finish_exp(h, 1, total, acc)
        pk3, total, acc, dq = run((1, q_aug(h + 1, 1)), (0, top(pk2)), (1, goa, goa[:d], q_of(h, 1)))
        put_dq(h, 1, dq)
        return pk3, finish_exp(h + 1, 0, total, acc)
    pk, goa = lax.fori_loop(0, chunks - 1, two, (pk, goa))
    last = chunks - 1
    _, total, acc, dq = run(None, (1, top(pk)), (0, goa, goa[:d], q_of(last, 0)))
    put_dq(last, 0, dq)
    goa = finish_exp(last, 1, total, acc)
    _, _, _, dq = run(None, None, (1, goa, goa[:d], q_of(last, 1)))
    put_dq(last, 1, dq)

    def finish(c, carry):
        at = pl.ds(pl.multiple_of(c * span, span), span)
        dqkv_ref[c, d:2 * d, :] = (dkt[:, at] * (d ** -0.5)).astype(BF16)
        dqkv_ref[c, 2 * d:, :] = dvt[:, at].astype(BF16)
        return carry
    lax.fori_loop(0, chunks, finish, 0)
    dtext_ref[:d, :] = (dkt[:, pix:] * (d ** -0.5)).astype(BF16)
    dtext_ref[d:, :] = dvt[:, pix:].astype(BF16)

def attention(ext, qkv, text, go, width):
    chunks, wide, span = qkv.shape
    d = wide // 3
    tlen = text.shape[0]
    keys = chunks * span + tlen
    bq = span // 2
    lanes = keys // 128
    step = 128 * max(n for n in range(1, 12) if lanes % n == 0)
    vm = pl.BlockSpec(memory_space=pltpu.VMEM)
    flops = 2 * 6 * chunks * span * keys * d
    return pl.pallas_call(
        functools.partial(attention_kernel, width, step, bq),
        out_shape=(
            jax.ShapeDtypeStruct(go.shape, BF16),
            jax.ShapeDtypeStruct(qkv.shape, BF16),
            jax.ShapeDtypeStruct((2 * d, tlen), BF16),
        ),
        in_specs=[pl.BlockSpec(memory_space=pltpu.SMEM), vm, vm, vm],
        out_specs=(vm, vm, vm),
        scratch_shapes=[
            pltpu.VMEM((keys, 128), BF16),
            pltpu.VMEM((keys, 128), BF16),
            pltpu.VMEM((d, keys), BF16),
            pltpu.VMEM((d, keys), BF16),
            pltpu.VMEM((keys, bq), F32),
            pltpu.VMEM((keys, bq), F32),
            pltpu.VMEM((keys, bq), BF16),
            pltpu.VMEM((keys, bq), BF16),
            pltpu.VMEM((d, keys), F32),
            pltpu.VMEM((d, keys), F32),
        ],
        compiler_params=pltpu.CompilerParams(vmem_limit_bytes=56 << 20),
        cost_estimate=pl.CostEstimate(
            flops=4 * flops, bytes_accessed=16 * chunks * span * d, transcendentals=chunks * span * keys
        ),
    )(ext, qkv, text, go)


MESH = pl.DeviceIdType.MESH
EPS = 1e-05
WHOLE = pl.BlockSpec(memory_space=pltpu.VMEM)
SCALARS = pl.BlockSpec(memory_space=pltpu.SMEM)
ANYWHERE = pl.BlockSpec(memory_space=pl.ANY)


def exchange_kernel(n, count, gathers, *refs):
    inputs, refs = refs[: 1 + count + gathers], refs[1 + count + gathers :]
    outputs, refs = refs[: 1 + 2 * count + gathers], refs[1 + 2 * count + gathers :]
    stats_ref, rows, given = inputs[0], inputs[1 : 1 + count], inputs[1 + count :]
    total_ref, outs, gathered = outputs[0], outputs[1 : 1 + 2 * count], outputs[1 + 2 * count :]
    slots, lands = refs[0], refs[1 : 1 + 2 * count]
    send, recv, row_send, row_recv, own = refs[1 + 2 * count :]
    me = lax.axis_index("rows")
    barrier = pltpu.get_barrier_semaphore()

    def greet(k, carry):
        pl.semaphore_signal(
            barrier, inc=1, device_id={"rows": lax.rem(me + k, n)}, device_id_type=MESH
        )
        return carry

    lax.fori_loop(1, n, greet, 0)
    slots[me] = stats_ref[...]
    pl.semaphore_wait(barrier, n - 1)
    shared = [(stats_ref, slots)] + list(zip(given, gathered))

    def share(j, k):
        return pltpu.make_async_remote_copy(
            src_ref=shared[j][0],
            dst_ref=shared[j][1].at[me],
            send_sem=send.at[j, k],
            recv_sem=recv.at[j, k],
            device_id={"rows": lax.rem(me + k, n)},
            device_id_type=MESH,
        )

    def start(k, carry):
        share(0, k).start()
        return carry

    lax.fori_loop(1, n, start, 0)

    def row_copy(j, side):
        last = rows[j].shape[1] - 1
        at = last if side == 0 else 0
        return pltpu.make_async_remote_copy(
            src_ref=rows[j].at[:, at : at + 1],
            dst_ref=lands[2 * j + side],
            send_sem=row_send.at[2 * j + side],
            recv_sem=row_recv.at[2 * j + side],
            device_id={"rows": me + 1 if side == 0 else me - 1},
            device_id_type=MESH,
        )

    for j in range(count):

        @pl.when(me < n - 1)
        def _():
            row_copy(j, 0).start()

        @pl.when(me > 0)
        def _():
            row_copy(j, 1).start()

    for j in range(gathers):

        def start_given(k, carry):
            share(1 + j, k).start()
            return carry

        lax.fori_loop(1, n, start_given, 0)
        pltpu.make_async_copy(given[j], gathered[j].at[me], own.at[j]).start()

    def finish(k, carry):
        share(0, k).wait()
        return carry

    lax.fori_loop(1, n, finish, 0)
    total_ref[...] = lax.fori_loop(1, n, lambda k, s: s + slots[k], slots[0])
    for j in range(count):

        @pl.when(me > 0)
        def _():
            row_copy(j, 0).wait_recv()
            outs[2 * j][...] = lands[2 * j][...]

        @pl.when(me == 0)
        def _():
            outs[2 * j][...] = jnp.zeros_like(outs[2 * j])

        @pl.when(me < n - 1)
        def _():
            row_copy(j, 1).wait_recv()
            outs[2 * j + 1][...] = lands[2 * j + 1][...]
            row_copy(j, 0).wait_send()

        @pl.when(me == n - 1)
        def _():
            outs[2 * j + 1][...] = jnp.zeros_like(outs[2 * j + 1])

        @pl.when(me > 0)
        def _():
            row_copy(j, 1).wait_send()

    for j in range(gathers):

        def finish_given(k, carry):
            share(1 + j, k).wait()
            return carry

        lax.fori_loop(1, n, finish_given, 0)
        pltpu.make_async_copy(given[j], gathered[j].at[me], own.at[j]).wait()


def exchange(stats, rows, identity, given=()):
    n = lax.axis_size("rows")
    edge = []
    for array in rows:
        edge += [jax.ShapeDtypeStruct(array.shape[:1] + (1,) + array.shape[2:], array.dtype)] * 2
    whole = [jax.ShapeDtypeStruct((n,) + array.shape, array.dtype) for array in given]
    count, gathers = len(rows), len(given)
    nbytes = 4 * stats.size * n + sum(2 * e.size * e.dtype.itemsize for e in (*edge, *whole))
    return pl.pallas_call(
        functools.partial(exchange_kernel, n, count, gathers),
        out_shape=(jax.ShapeDtypeStruct(stats.shape, F32), *edge, *whole),
        in_specs=[WHOLE] + [ANYWHERE] * (count + gathers),
        out_specs=(WHOLE,) * (1 + 2 * count) + (ANYWHERE,) * gathers,
        scratch_shapes=[
            pltpu.VMEM((n,) + stats.shape, F32),
            *[pltpu.VMEM(e.shape, e.dtype) for e in edge],
            pltpu.SemaphoreType.DMA((1 + gathers, n)),
            pltpu.SemaphoreType.DMA((1 + gathers, n)),
            pltpu.SemaphoreType.DMA((max(1, 2 * count),)),
            pltpu.SemaphoreType.DMA((max(1, 2 * count),)),
            pltpu.SemaphoreType.DMA((max(1, gathers),)),
        ],
        compiler_params=pltpu.CompilerParams(collective_id=identity, has_side_effects=True),
        cost_estimate=pl.CostEstimate(
            flops=6_000_000_000, bytes_accessed=nbytes, transcendentals=0
        ),
        name=f"exchange{identity}",
    )(stats, *rows, *given)


def group_sums(rows):
    channels = rows.shape[1]
    size = channels // GROUPS
    one = lax.broadcasted_iota(jnp.int32, (channels, channels), 0) // size
    two = lax.broadcasted_iota(jnp.int32, (channels, channels), 1) // size
    same = jnp.where(one == two, 1.0, 0.0).astype(BF16)
    high = rows.astype(BF16)
    rest = rows - high.astype(F32)
    mid = rest.astype(BF16)
    tail = (rest - mid.astype(F32)).astype(BF16)
    return dot(high, same, 1, 0) + dot(mid, same, 1, 0) + dot(tail, same, 1, 0)


def image_count(info, i, channels):
    return (info[i, 0] * info[i, 1]).astype(F32) * (channels // GROUPS)


def norm_of(stats, count):
    sums = group_sums(stats)
    average = sums[0:1] / count
    square = sums[1:2] / count
    return average, lax.rsqrt(square - average * average + EPS)


def means_of(stats, weight, count):
    sums = group_sums(stats * weight)
    return sums[0:1] / count, sums[1:2] / count


def window(info, i, row, shape):
    ok = (row >= 0) & (row < info[i, 0])
    limit = jnp.where(ok, info[i, 1], 0)
    return jnp.where(lax.broadcasted_iota(jnp.int32, shape, 0) < limit, 1.0, 0.0)


def padded_row(center, above, below, i, r):
    if r == 0:
        return above[i, 0]
    if r == center.shape[1] + 1:
        return below[i, 0]
    return center[i, r - 1]


def put_shifted(out, i, r, value, plain=None):
    width, channels = value.shape
    column = lax.broadcasted_iota(jnp.int32, value.shape, 0)
    left = jnp.where(column == 0, 0.0, pltpu.roll(value, 1, 0))
    right = jnp.where(column == width - 1, 0.0, pltpu.roll(value, width - 1, 0))
    out[i, r, :, :channels] = left.astype(BF16)
    low = value.astype(BF16)
    out[i, r, :, channels : 2 * channels] = low
    if plain is not None:
        plain[i, r] = low
    out[i, r, :, 2 * channels :] = right.astype(BF16)


def sigmoid(v):
    return 1.0 / (1.0 + jnp.exp(-v))


def silu_slope(v):
    s = sigmoid(v)
    return s * (1.0 + v * (1.0 - s))


def put_stats(stats_ref, i, first, second):
    channels = first.shape[1]
    one = jnp.sum(first, axis=0, keepdims=True)
    two = jnp.sum(second, axis=0, keepdims=True)
    row = lax.broadcasted_iota(jnp.int32, (8, channels), 0)
    stats_ref[i] = jnp.where(row == 0, one, jnp.where(row == 1, two, 0.0))


def tap_rows(shifted, tap, images, rows_dev, width):
    block = shifted[:, pl.ds(tap, rows_dev)]
    return block.reshape(images * rows_dev * width, shifted.shape[3])


def conv1_kernel(info, image, above, below, stats, gain, weight, first, out_stats, hidden, acc, shifted):
    images, rows_dev, width, channels = image.shape
    tap = pl.program_id(0)
    base = info[0, 2]

    @pl.when(tap == 0)
    def _():
        for i in range(images):
            average, inverse = norm_of(stats[i], image_count(info, i, channels))
            for r in range(rows_dev + 2):
                inside = window(info, i, base + r - 1, (width, channels))
                start = padded_row(image, above, below, i, r).astype(F32) * inside
                value = (start - average) * inverse * inside * gain[...]
                put_shifted(shifted, i, r, value * sigmoid(value) * inside, hidden)

    part = dot(tap_rows(shifted, tap, images, rows_dev, width), weight[0], 1, 0)

    @pl.when(tap == 0)
    def _():
        acc[...] = part

    @pl.when(tap > 0)
    def _():
        acc[...] += part

    @pl.when(tap == 2)
    def _():
        for i in range(images):
            one = two = jnp.zeros((width, channels), F32)
            for r in range(rows_dev):
                inside = window(info, i, base + r, (width, channels))
                at = (i * rows_dev + r) * width
                value = acc[at : at + width] * inside
                first[i, r] = value
                one = one + value
                two = two + value * value
            put_stats(out_stats, i, one, two)


def moved_of(value, inside, average, inverse, gain, scale, shift):
    normal = (value - average) * inverse * inside
    return normal, normal * gain * (1.0 + scale) + shift


def conv2_kernel(
    info, first, above, below, stats, gain, shifts, image, weight, middle, out_stats, second, acc,
    shifted,
):
    images, rows_dev, width, channels = first.shape
    tap = pl.program_id(0)
    base = info[0, 2]

    @pl.when(tap == 0)
    def _():
        for i in range(images):
            average, inverse = norm_of(stats[i], image_count(info, i, channels))
            scale, shift = shifts[i : i + 1, :channels], shifts[i : i + 1, channels:]
            for r in range(rows_dev + 2):
                inside = window(info, i, base + r - 1, (width, channels))
                value = padded_row(first, above, below, i, r)
                _, moved = moved_of(value, inside, average, inverse, gain[...], scale, shift)
                put_shifted(shifted, i, r, moved * sigmoid(moved) * inside, second)

    part = dot(tap_rows(shifted, tap, images, rows_dev, width), weight[0], 1, 0)

    @pl.when(tap == 0)
    def _():
        acc[...] = part

    @pl.when(tap > 0)
    def _():
        acc[...] += part

    @pl.when(tap == 2)
    def _():
        for i in range(images):
            one = two = jnp.zeros((width, channels), F32)
            for r in range(rows_dev):
                inside = window(info, i, base + r, (width, channels))
                at = (i * rows_dev + r) * width
                value = (image[i, r].astype(F32) + acc[at : at + width]) * inside
                middle[i, r] = value
                one = one + value
                two = two + value * value
            put_stats(out_stats, i, one, two)


def dgrad(shifted, tap, weight, images, rows_dev, width):
    channels = weight.shape[2]
    lhs = tap_rows(shifted, tap, images, rows_dev, width)
    part = None
    for b in range(3):
        term = dot(
            lhs[:, b * channels : (b + 1) * channels],
            weight[0, (2 - b) * channels : (3 - b) * channels, :],
            1,
            1,
        )
        part = term if part is None else part + term
    return part


def back2_kernel(
    info, grad, grad_above, grad_below, middle, mid_above, mid_below, cot, cot_above, cot_below,
    mid_stats, grad_stats, attn_gain, first, first_stats, gain, shifts, weight,
    grad_middle, moved_grad, out_stats, plain, acc, shifted,
):
    images, rows_dev, width, channels = first.shape
    tap = pl.program_id(0)
    base = info[0, 2]

    @pl.when(tap == 0)
    def _():
        for i in range(images):
            count = image_count(info, i, channels)
            average, inverse = norm_of(mid_stats[i], count)
            mean, cross = means_of(grad_stats[i], attn_gain[...], count)
            for r in range(rows_dev + 2):
                inside = window(info, i, base + r - 1, (width, channels))
                normal = (padded_row(middle, mid_above, mid_below, i, r) - average) * inverse
                dx = padded_row(grad, grad_above, grad_below, i, r) * attn_gain[...]
                term = (dx - mean - normal * cross) * inverse * inside
                total = padded_row(cot, cot_above, cot_below, i, r).astype(F32) + term
                if 0 < r <= rows_dev:
                    grad_middle[i, r - 1] = total
                put_shifted(shifted, i, r, total * inside, plain)

    part = dgrad(shifted, tap, weight, images, rows_dev, width)

    @pl.when(tap == 0)
    def _():
        acc[...] = part

    @pl.when(tap > 0)
    def _():
        acc[...] += part

    @pl.when(tap == 2)
    def _():
        for i in range(images):
            average, inverse = norm_of(first_stats[i], image_count(info, i, channels))
            scale, shift = shifts[i : i + 1, :channels], shifts[i : i + 1, channels:]
            one = two = jnp.zeros((width, channels), F32)
            for r in range(rows_dev):
                inside = window(info, i, base + r, (width, channels))
                at = (i * rows_dev + r) * width
                normal, moved = moved_of(
                    first[i, r], inside, average, inverse, gain[...], scale, shift
                )
                value = acc[at : at + width] * inside * silu_slope(moved)
                moved_grad[i, r] = value
                one = one + value
                two = two + value * normal
            put_stats(out_stats, i, one, two)


def back1_kernel(
    info, grad, grad_above, grad_below, first, first_above, first_below, first_stats, grad_stats,
    gain, shifts, image, image_stats, first_gain, weight,
    pre_grad, out_stats, plain, acc, shifted,
):
    images, rows_dev, width, channels = first.shape
    tap = pl.program_id(0)
    base = info[0, 2]

    @pl.when(tap == 0)
    def _():
        for i in range(images):
            count = image_count(info, i, channels)
            average, inverse = norm_of(first_stats[i], count)
            factor = gain[...] * (1.0 + shifts[i : i + 1, :channels])
            mean, cross = means_of(grad_stats[i], factor, count)
            for r in range(rows_dev + 2):
                inside = window(info, i, base + r - 1, (width, channels))
                normal = (padded_row(first, first_above, first_below, i, r) - average) * inverse
                dx = padded_row(grad, grad_above, grad_below, i, r) * factor
                put_shifted(shifted, i, r, (dx - mean - normal * cross) * inverse * inside, plain)

    part = dgrad(shifted, tap, weight, images, rows_dev, width)

    @pl.when(tap == 0)
    def _():
        acc[...] = part

    @pl.when(tap > 0)
    def _():
        acc[...] += part

    @pl.when(tap == 2)
    def _():
        for i in range(images):
            average, inverse = norm_of(image_stats[i], image_count(info, i, channels))
            one = two = jnp.zeros((width, channels), F32)
            for r in range(rows_dev):
                inside = window(info, i, base + r, (width, channels))
                at = (i * rows_dev + r) * width
                normal = (image[i, r].astype(F32) - average) * inverse * inside
                slope = silu_slope(normal * first_gain[...])
                value = acc[at : at + width] * inside * slope
                pre_grad[i, r] = value
                one = one + value
                two = two + value * normal
            put_stats(out_stats, i, one, two)


def conv_call(kernel, info, inputs, weight, outs, flipped):
    images, rows_dev, width, channels = outs[0].shape

    def whole(shape):
        return pl.BlockSpec(shape, lambda tap: (0,) * len(shape))

    def tap_of(tap):
        return ((2 - tap) if flipped else tap, 0, 0)

    weight = weight.reshape(3, 3 * channels, channels)
    flops = 2 * 9 * images * rows_dev * width * channels * channels
    moved = sum(a.size * a.dtype.itemsize for a in (*inputs, weight, *outs))
    return pl.pallas_call(
        kernel,
        grid=(3,),
        out_shape=tuple(outs),
        in_specs=[SCALARS]
        + [whole(a.shape) for a in inputs]
        + [pl.BlockSpec((1, 3 * channels, channels), tap_of)],
        out_specs=tuple(whole(o.shape) for o in outs),
        scratch_shapes=[
            pltpu.VMEM((images * rows_dev * width, channels), F32),
            pltpu.VMEM((images, rows_dev + 2, width, 3 * channels), BF16),
        ],
        compiler_params=pltpu.CompilerParams(vmem_limit_bytes=48 << 20),
        cost_estimate=pl.CostEstimate(flops=flops, bytes_accessed=moved, transcendentals=0),
        name=kernel.__name__,
    )(info, *inputs, weight)


def weight_grad_kernel(grads, hidden, out, turned, shifted):
    images, padded, width, channels = hidden.shape
    rows_dev = padded - 2
    pixels = images * rows_dev * width
    tap = pl.program_id(0)

    @pl.when(tap == 0)
    def _():
        center = grads[:, 1 : rows_dev + 1]
        turned[...] = center.reshape(pixels, channels).astype(F32).T.astype(BF16)
        for i in range(images):
            for r in range(padded):
                put_shifted(shifted, i, r, hidden[i, r].astype(F32))

    column = pl.multiple_of((tap % 3) * channels, channels)
    rhs = shifted[:, pl.ds(tap // 3, rows_dev), :, pl.ds(column, channels)]
    out[...] = dot(turned[...], rhs.reshape(pixels, channels), 1, 0).astype(BF16)


def weight_grad(grads, hidden):
    images, padded, width, channels = hidden.shape
    pixels = images * (padded - 2) * width

    def whole(shape):
        return pl.BlockSpec(shape, lambda tap: (0,) * len(shape))

    return pl.pallas_call(
        weight_grad_kernel,
        grid=(9,),
        out_shape=jax.ShapeDtypeStruct((channels, 9 * channels), BF16),
        in_specs=[whole(grads.shape), whole(hidden.shape)],
        out_specs=pl.BlockSpec((channels, channels), lambda tap: (0, tap)),
        scratch_shapes=[
            pltpu.VMEM((channels, pixels), BF16),
            pltpu.VMEM(hidden.shape[:3] + (3 * channels,), BF16),
        ],
        compiler_params=pltpu.CompilerParams(vmem_limit_bytes=32 << 20),
        cost_estimate=pl.CostEstimate(
            flops=18 * pixels * channels * channels,
            bytes_accessed=18 * channels * channels,
            transcendentals=0,
        ),
        name="weight_grad",
    )(grads, hidden)


def reduce_kernel(items, chips, has_extra, *refs):
    if has_extra:
        grads, hidden, extra, vector, out, extra_out, vectors, *refs = refs
    else:
        grads, hidden, out, *refs = refs
    (turned, quarter, shifted, part, from_core, chip_sum, from_chip, final, g_send, g_recv, c_send, c_recv,
     z_send, z_recv, f_send, f_recv, *refs) = refs
    _, padded, width, channels = grads.shape
    rows_dev = padded - 2
    pixels = rows_dev * width
    share = channels // (2 * chips)
    slice_rows = share // items
    item, row = lax.axis_index("items"), lax.axis_index("rows")
    chip, core = row // 2, lax.rem(row, 2)
    barrier = pltpu.get_barrier_semaphore()
    peers = [{"items": lax.rem(item + k, items), "rows": row} for k in range(1, items)]
    others = [
        {"items": item, "rows": lax.rem(chip + k, chips) * 2 + core} for k in range(1, chips)
    ]
    sibling = {"items": item, "rows": row + 1 - 2 * core}
    for device in (sibling, *peers, *others):
        pl.semaphore_signal(barrier, inc=1, device_id=device, device_id_type=MESH)

    for r in range(rows_dev):
        block = grads[0, 1 + r].astype(F32).T.astype(BF16)
        for z in range(chips):
            for c in range(2):
                for q in range(items):
                    at = (z * 2 + c) * share + q * slice_rows
                    to = (c * chips + z) * slice_rows
                    turned[q, to : to + slice_rows, r * width : (r + 1) * width] = block[
                        at : at + slice_rows
                    ]
    pl.semaphore_wait(barrier, items + chips - 1)

    def copy(src, dst, send, recv, device):
        return pltpu.make_async_remote_copy(
            src_ref=src,
            dst_ref=dst,
            send_sem=send,
            recv_sem=recv,
            device_id=device,
            device_id_type=MESH,
        )

    started = []

    def go(*args):
        c = copy(*args)
        c.start()
        started.append(c)
        return c

    g_copies = [
        go(
            turned.at[lax.rem(item + k, items)],
            quarter.at[item],
            g_send.at[k],
            g_recv.at[k],
            peers[k - 1],
        )
        for k in range(1, items)
    ]
    if has_extra:
        land, summed, v_land, e_send, e_recv, h_send, h_recv, v_send, v_recv = refs
        e_copies = [
            go(
                extra.at[lax.rem(item + k, items)],
                land.at[item],
                e_send.at[k],
                e_recv.at[k],
                peers[k - 1],
            )
            for k in range(1, items)
        ]
        v_copies = [
            go(vector, v_land.at[item], v_send.at[k], v_recv.at[k], peers[k - 1])
            for k in range(1, items)
        ]
        land[item] = extra[item]
        v_land[item] = vector[...]
    quarter[item] = turned[item]
    for g in range(items):

        def shift(r, carry):
            put_shifted(shifted, g, r, hidden[g, r].astype(F32))
            return carry

        lax.fori_loop(0, padded, shift, 0)
    for c in g_copies:
        c.wait_recv()
    if has_extra:
        for c in e_copies:
            c.wait_recv()
        total = land[0].astype(F32)
        for g in range(1, items):
            total = total + land[g].astype(F32)
        summed[item] = total.astype(BF16)
        h_copies = [
            go(summed.at[item], summed.at[item], h_send.at[k], h_recv.at[k], peers[k - 1])
            for k in range(1, items)
        ]

    half = chips * slice_rows
    core_copies, chip_copies, final_copies = [], [], []

    def compute(a):
        for b in range(3):
            acc = None
            for g in range(items):
                rhs = shifted[g, a : a + rows_dev, :, b * channels : (b + 1) * channels]
                term = dot(quarter[g], rhs.reshape(pixels, channels), 1, 0)
                acc = term if acc is None else acc + term
            part[a, 0, b] = acc[:half].astype(BF16)
            part[a, 1, b] = acc[half:].astype(BF16)
        core_copies.append(
            go(part.at[a, 1 - core], from_core.at[a], c_send.at[a], c_recv.at[a], sibling)
        )

    def over_chips(a):
        core_copies[a].wait_recv()
        for b in range(3):
            both = part[a, core, b].astype(F32) + from_core[a, b].astype(F32)
            for z in range(chips):
                chip_sum[a, z, b] = both[z * slice_rows : (z + 1) * slice_rows].astype(BF16)
        chip_copies.append(
            [
                go(
                    chip_sum.at[a, lax.rem(chip + k, chips)],
                    from_chip.at[a, k],
                    z_send.at[a, k],
                    z_recv.at[a, k],
                    others[k - 1],
                )
                for k in range(1, chips)
            ]
        )

    def over_items(a):
        for c in chip_copies[a]:
            c.wait_recv()
        total = chip_sum[a, chip].astype(F32)
        for k in range(1, chips):
            total = total + from_chip[a, k].astype(F32)
        final[a, item] = total.astype(BF16)
        final_copies.append(
            [
                go(
                    final.at[a, item],
                    final.at[a, item],
                    f_send.at[a, k],
                    f_recv.at[a, k],
                    peers[k - 1],
                )
                for k in range(1, items)
            ]
        )

    def put(a):
        for c in final_copies[a]:
            c.wait_recv()
        for b in range(3):
            rows = jnp.concatenate([final[a, q, b].astype(F32) for q in range(items)], axis=0)
            at = (a * 3 + b) * channels
            out[at : at + channels] = rows.T

    compute(0)
    compute(1)
    over_chips(0)
    compute(2)
    over_chips(1)
    over_chips(2)
    over_items(0)
    over_items(1)
    over_items(2)
    if has_extra:
        for c in h_copies:
            c.wait_recv()
        for q in range(items):
            rows = summed.shape[1]
            extra_out[q * rows : (q + 1) * rows] = summed[q].astype(F32)
        for c in v_copies:
            c.wait_recv()
        vectors[...] = v_land[...]
    put(0)
    put(1)
    put(2)
    for c in started:
        c.wait_send()


def reduce_weight(grads, hidden, identity, extra=None, vector=None):
    items, chips = lax.axis_size("items"), lax.axis_size("rows") // 2
    _, padded, width, channels = grads.shape
    pixels = (padded - 2) * width
    share = channels // (2 * chips)
    rows = share // items
    inputs = [grads, hidden]
    outs = [jax.ShapeDtypeStruct((9 * channels, share), F32)]
    sem = pltpu.SemaphoreType.DMA
    scratch = [
        pltpu.VMEM((items, channels // items, pixels), BF16),
        pltpu.VMEM((items, channels // items, pixels), BF16),
        pltpu.VMEM((items, padded, width, 3 * channels), BF16),
        pltpu.VMEM((3, 2, 3, chips * rows, channels), BF16),
        pltpu.VMEM((3, 3, chips * rows, channels), BF16),
        pltpu.VMEM((3, chips, 3, rows, channels), BF16),
        pltpu.VMEM((3, chips, 3, rows, channels), BF16),
        pltpu.VMEM((3, items, 3, rows, channels), BF16),
        sem((items,)),
        sem((items,)),
        sem((3,)),
        sem((3,)),
        sem((3, chips)),
        sem((3, chips)),
        sem((3, items)),
        sem((3, items)),
    ]
    if extra is not None:
        inputs += [extra.reshape(items, extra.shape[0] // items, extra.shape[1]), vector]
        outs += [
            jax.ShapeDtypeStruct(extra.shape, F32),
            jax.ShapeDtypeStruct((items,) + vector.shape, F32),
        ]
        scratch += [
            pltpu.VMEM(inputs[2].shape, BF16),
            pltpu.VMEM(inputs[2].shape, BF16),
            pltpu.VMEM((items,) + vector.shape, F32),
        ] + [sem((items,))] * 6
    return pl.pallas_call(
        functools.partial(reduce_kernel, items, chips, extra is not None),
        out_shape=tuple(outs),
        in_specs=[WHOLE] * len(inputs),
        out_specs=(WHOLE,) * len(outs),
        scratch_shapes=scratch,
        compiler_params=pltpu.CompilerParams(
            collective_id=identity, has_side_effects=True, vmem_limit_bytes=48 << 20
        ),
        cost_estimate=pl.CostEstimate(
            flops=20_000_000_000, bytes_accessed=40 * channels * channels, transcendentals=0
        ),
        name=f"reduce{identity}",
    )(*inputs)


def project_kernel(info, middle, stats, gain, weight, attn, qkv):
    images, rows_dev, width, channels = middle.shape
    pixels = rows_dev * width
    heads, wide = HEADS, weight.shape[0] // HEADS
    base = info[0, 2]
    for i in range(images):
        average, inverse = norm_of(stats[i], image_count(info, i, channels))
        for r in range(rows_dev):
            inside = window(info, i, base + r, (width, channels))
            value = (middle[i, r] - average) * inverse * inside * gain[...]
            attn[i, r * width : (r + 1) * width] = value.astype(BF16)
        for h in range(heads):
            block = dot(weight[h * wide : (h + 1) * wide], attn[i], 1, 1)
            qkv[i * heads + h] = block.astype(BF16)


def project(info, middle, stats, gain, weight):
    images, rows_dev, width, channels = middle.shape
    pixels = rows_dev * width
    return pl.pallas_call(
        project_kernel,
        out_shape=(
            jax.ShapeDtypeStruct((images, pixels, channels), BF16),
            jax.ShapeDtypeStruct((images * HEADS, weight.shape[0] // HEADS, pixels), BF16),
        ),
        in_specs=[SCALARS, WHOLE, WHOLE, WHOLE, WHOLE],
        out_specs=(WHOLE, WHOLE),
        compiler_params=pltpu.CompilerParams(vmem_limit_bytes=32 << 20),
        name="project",
    )(info, middle, stats, gain, weight)


def unproject_kernel(info, middle, stats, grads, weight, out, out_stats):
    images, rows_dev, width, channels = middle.shape
    wide, pixels = grads.shape[1], grads.shape[2]
    base = info[0, 2]
    for i in range(images):
        average, inverse = norm_of(stats[i], image_count(info, i, channels))
        acc = None
        for h in range(HEADS):
            turned = grads[i * HEADS + h].astype(F32).T.astype(BF16)
            term = dot(turned, weight[h * wide : (h + 1) * wide], 1, 0)
            acc = term if acc is None else acc + term
        one = two = jnp.zeros((width, channels), F32)
        for r in range(rows_dev):
            inside = window(info, i, base + r, (width, channels))
            value = acc[r * width : (r + 1) * width] * inside
            out[i, r] = value
            one = one + value
            two = two + value * ((middle[i, r] - average) * inverse)
        put_stats(out_stats, i, one, two)


def unproject(info, middle, stats, grads, weight):
    images, rows_dev, width, channels = middle.shape
    return pl.pallas_call(
        unproject_kernel,
        out_shape=(
            jax.ShapeDtypeStruct(middle.shape, F32),
            jax.ShapeDtypeStruct(stats.shape, F32),
        ),
        in_specs=[SCALARS, WHOLE, WHOLE, WHOLE, WHOLE],
        out_specs=(WHOLE, WHOLE),
        compiler_params=pltpu.CompilerParams(vmem_limit_bytes=32 << 20),
        name="unproject",
    )(info, middle, stats, grads, weight)


def finish_kernel(info, pre_grad, grad_stats, image, stats, gain, grad_middle, out):
    images, rows_dev, width, channels = image.shape
    base = info[0, 2]
    for i in range(images):
        count = image_count(info, i, channels)
        average, inverse = norm_of(stats[i], count)
        mean, cross = means_of(grad_stats[i], gain[...], count)
        for r in range(rows_dev):
            inside = window(info, i, base + r, (width, channels))
            normal = (image[i, r].astype(F32) - average) * inverse
            term = (pre_grad[i, r] * gain[...] - mean - normal * cross) * inverse
            out[i, r] = (grad_middle[i, r] + term) * inside


def finish(info, pre_grad, grad_stats, image, stats, gain, grad_middle):
    return pl.pallas_call(
        finish_kernel,
        out_shape=jax.ShapeDtypeStruct(image.shape, F32),
        in_specs=[SCALARS] + [WHOLE] * 6,
        out_specs=WHOLE,
        compiler_params=pltpu.CompilerParams(vmem_limit_bytes=32 << 20),
        name="finish",
    )(info, pre_grad, grad_stats, image, stats, gain, grad_middle)


def shards(
    image, embed, text, extent, first_norm_gain1, conv1_w, embed_w, second_norm_gain2, conv2_w,
    attention_norm_gain, qkv_w, text_w, proj_w, cotangent,
):
    images, rows_dev, width, channels = image.shape
    parts = lax.axis_size("rows")
    me = lax.axis_index("rows")
    pairs = images * HEADS // parts
    head_dim = channels // HEADS
    pixels = rows_dev * width
    group = max(1, 512 // pixels)
    span = group * pixels
    chunks = parts // group
    tokens = text.shape[1]
    first_row = jnp.full((images, 1), me * rows_dev, jnp.int32)
    info = jnp.concatenate([extent, first_row], axis=1)
    gain1 = first_norm_gain1.reshape(1, channels)
    gain2 = second_norm_gain2.reshape(1, channels)
    gain3 = attention_norm_gain.reshape(1, channels)
    rowpos = me * rows_dev + jnp.arange(rows_dev, dtype=jnp.int32)
    colpos = jnp.arange(width, dtype=jnp.int32)
    inside = (rowpos[None, :, None] < extent[:, 0, None, None]) & (
        colpos[None, None, :] < extent[:, 1, None, None]
    )
    image_window = inside.astype(F32)[..., None]

    embed_float = embed.astype(F32)
    embed_low = jax.nn.silu(embed_float).astype(BF16)
    shifts = jnp.dot(embed_low, embed_w, preferred_element_type=F32)
    qkv_turned = qkv_w.T
    proj_shaped = proj_w.reshape(HEADS, head_dim, channels)

    start = image.astype(F32) * image_window
    zeros = jnp.zeros((images, 6, channels), F32)
    stats0 = jnp.concatenate(
        [
            jnp.sum(start, axis=(1, 2))[:, None],
            jnp.sum(start * start, axis=(1, 2))[:, None],
            zeros,
        ],
        axis=1,
    )
    stats1, image_above, image_below, cot_above, cot_below = exchange(
        stats0, (image, cotangent), 0
    )
    full = jax.ShapeDtypeStruct(image.shape, F32)
    sums = jax.ShapeDtypeStruct((images, 8, channels), F32)
    padded = jax.ShapeDtypeStruct((images, rows_dev + 2, width, channels), BF16)
    items = lax.axis_size("items")
    own_reduce = images == 1 and parts % 2 == 0 and channels % (16 * items * parts) == 0
    first, stats, hidden = conv_call(
        conv1_kernel,
        info,
        (image, image_above, image_below, stats1, gain1),
        conv1_w,
        (full, sums, padded),
        False,
    )
    stats2, first_above, first_below, all_text = exchange(stats, (first,), 1, (text,))
    gathered_text = jnp.moveaxis(all_text, 0, 1).reshape(images, parts * tokens, text.shape[2])
    text_share = text.shape[2] // parts
    text_cols = lax.dynamic_slice_in_dim(gathered_text, me * text_share, text_share, 2)
    text_cols = lax.all_gather(text_cols, "items", axis=0, tiled=True)
    if own_reduce:
        hidden_all = lax.all_gather(hidden, "items", axis=0, tiled=True)
    middle, stats, second = conv_call(
        conv2_kernel,
        info,
        (first, first_above, first_below, stats2, gain2, shifts, image),
        conv2_w,
        (full, sums, padded),
        False,
    )
    stats3, mid_above, mid_below = exchange(stats, (middle,), 2)
    if own_reduce:
        second_all = lax.all_gather(second, "items", axis=0, tiled=True)
    attn_flat, qkv_pix = project(info, middle, stats3, gain3, qkv_turned)

    def to_pairs(values):
        wide = values.shape[1]
        moved = lax.all_to_all(values, "rows", split_axis=0, concat_axis=0, tiled=True)
        moved = moved.reshape(chunks, group, pairs, wide, pixels)
        return jnp.transpose(moved, (2, 0, 3, 1, 4)).reshape(pairs, chunks, wide, span)

    def from_pairs(values):
        wide = values.shape[2]
        moved = values.reshape(pairs, chunks, wide, group, pixels)
        moved = jnp.transpose(moved, (1, 3, 0, 2, 4)).reshape(parts * pairs, wide, pixels)
        return lax.all_to_all(moved, "rows", split_axis=0, concat_axis=0, tiled=True)

    qkv_pair = to_pairs(qkv_pix)
    grad_proj = (cotangent.astype(F32) * image_window).astype(BF16).reshape(images, pixels, channels)
    grad_heads = jnp.einsum(
        "ipc,hdc->ihdp", grad_proj, proj_shaped, preferred_element_type=F32
    ).astype(BF16)
    grad_pair = to_pairs(grad_heads.reshape(images * HEADS, head_dim, pixels))
    pair_results = []
    for p in range(pairs):
        pair = me * pairs + p
        item, head = pair // HEADS, pair % HEADS
        weight = lax.dynamic_slice_in_dim(text_w, head * 2 * head_dim, 2 * head_dim, 1)
        own = lax.dynamic_index_in_dim(gathered_text, item, 0, False)
        text_pair = jnp.dot(own, weight, preferred_element_type=F32).astype(BF16)
        pair_extent = lax.dynamic_slice_in_dim(extent, item, 1, 0)
        pair_results.append(attention(pair_extent, qkv_pair[p], text_pair, grad_pair[p], width))
    attended, qkv_grad_pair, text_grad_pair = (jnp.stack(r) for r in zip(*pair_results))
    qkv_back = from_pairs(qkv_grad_pair)
    heads_out = from_pairs(attended).reshape(images, HEADS, head_dim, pixels)

    attn_grad, stats = unproject(info, middle, stats3, qkv_back, qkv_turned)
    stats4, grad_above, grad_below, text_back = exchange(stats, (attn_grad,), 3, (text_grad_pair,))
    text_back = text_back.reshape(images, HEADS, 2 * head_dim, parts * tokens)
    text_all = lax.all_gather(text_back, "items", axis=0, tiled=True)
    proj_grad = jnp.einsum("ipc,ihdp->chd", grad_proj, heads_out, preferred_element_type=F32)
    qkv_grad = jnp.einsum(
        "ihwdp,ipc->hdwc",
        qkv_back.reshape(images, HEADS, 3, head_dim, pixels),
        attn_flat,
        preferred_element_type=F32,
    )
    if own_reduce:
        side = jnp.concatenate(
            [
                qkv_grad.astype(BF16).reshape(channels, 3 * channels),
                proj_grad.astype(BF16).reshape(channels, channels),
            ],
            axis=1,
        )
        side = lax.psum_scatter(side, "rows", scatter_dimension=0, tiled=True)
    grad_middle, moved_grad, stats, conv2_grad = conv_call(
        back2_kernel,
        info,
        (attn_grad, grad_above, grad_below, middle, mid_above, mid_below, cotangent, cot_above,
         cot_below, stats3, stats4, gain3, first, stats2, gain2, shifts),
        conv2_w,
        (full, full, sums, padded),
        True,
    )
    stats5, moved_above, moved_below = exchange(stats, (moved_grad,), 4)
    pre_grad, stats, conv1_grad = conv_call(
        back1_kernel,
        info,
        (moved_grad, moved_above, moved_below, first, first_above, first_below, stats2, stats5,
         gain2, shifts, image, stats1, gain1),
        conv1_w,
        (full, sums, padded),
        True,
    )
    (stats6,) = exchange(stats, (), 5)
    image_grad = finish(info, pre_grad, stats6, image, stats1, gain1, grad_middle)

    projected = jnp.einsum(
        "ihdp,hdc->ipc", heads_out, proj_shaped, preferred_element_type=F32
    ).reshape(image.shape)
    output = (middle + projected * image_window).astype(BF16)
    own_text = lax.dynamic_slice_in_dim(text_back, me * tokens, tokens, 3)
    text_shaped = text_w.reshape(text_w.shape[0], HEADS, 2 * head_dim)
    text_grad = jnp.einsum("ihkt,chk->itc", own_text, text_shaped, preferred_element_type=F32)
    text_w_grad = jnp.einsum(
        "gtc,ghkt->chk", text_cols, text_all, preferred_element_type=F32
    ).reshape(text_share, 2 * channels)
    scale_sum = stats5[:, 1] * gain2
    grad_shifts = jnp.concatenate([scale_sum, stats5[:, 0]], axis=1).astype(BF16)
    embed_grad = jnp.einsum(
        "ik,ck->ic", grad_shifts, embed_w, preferred_element_type=F32
    ) * silu_slope(embed_float)
    embed_share = embed_w.shape[0] // parts
    gains = jnp.stack(
        [
            jnp.sum(stats6[:, 1], axis=0),
            jnp.sum(stats5[:, 1] * (1.0 + shifts[:, :channels]), axis=0),
            jnp.sum(stats4[:, 1], axis=0),
        ]
    )
    share = channels // parts
    if own_reduce:
        vector = jnp.concatenate(
            [
                gains,
                grad_shifts.astype(F32).reshape(2, channels),
                embed_low.astype(F32).reshape(-1, channels),
            ],
            axis=0,
        )
        filled = vector.shape[0]
        vector = jnp.pad(vector, ((0, -filled % 8), (0, 0)))
        (conv2_total,) = reduce_weight(conv2_grad, second_all, 6)
        conv1_total, side, vectors = reduce_weight(conv1_grad, hidden_all, 7, side, vector)
        conv1_total = conv1_total.reshape(3, 3, channels, share)
        conv2_total = conv2_total.reshape(3, 3, channels, share)
        qkv_total = side[:, : 3 * channels].reshape(head_dim, 3, channels)
        qkv_total = jnp.transpose(qkv_total, (2, 1, 0)).reshape(channels, 3 * share)
        proj_total = side[:, 3 * channels :].T
        gains = jnp.sum(vectors[:, :3], axis=0)
        all_shifts = vectors[:, 3:5].reshape(items, 2 * channels).astype(BF16)
        all_embed = vectors[:, 5:filled].reshape(items, embed.shape[1]).astype(BF16)
        embed_rows = lax.dynamic_slice_in_dim(all_embed, me * embed_share, embed_share, 1)
    else:

        def total(values):
            return lax.psum(
                lax.psum_scatter(values.astype(BF16), "rows", scatter_dimension=0, tiled=True),
                "items",
            ).astype(F32)

        def kernel_total(values):
            return total(values).T.reshape(3, 3, channels, share)

        conv1_total = kernel_total(weight_grad(conv1_grad, hidden))
        conv2_total = kernel_total(weight_grad(conv2_grad, second))
        by_head = jnp.swapaxes(qkv_grad, 1, 2).reshape(3 * channels, channels)
        qkv_total = total(by_head).T
        proj_total = total(proj_grad.reshape(channels, channels)).T
        gains = lax.psum(gains, "items")
        all_shifts = lax.all_gather(grad_shifts, "items", axis=0, tiled=True)
        embed_rows = lax.dynamic_slice_in_dim(embed_low, me * embed_share, embed_share, 1)
        embed_rows = lax.all_gather(embed_rows, "items", axis=0, tiled=True)
    embed_w_grad = jnp.einsum("ic,ik->ck", embed_rows, all_shifts, preferred_element_type=F32)
    gains = lax.dynamic_slice_in_dim(gains, me * share, share, 1)
    return (
        output,
        image_grad,
        embed_grad,
        text_grad,
        gains[0],
        conv1_total,
        embed_w_grad,
        gains[1],
        conv2_total,
        gains[2],
        qkv_total,
        text_w_grad,
        proj_total,
    )


def solution(mesh):
    in_specs = (
        P("items", "rows", None, None),
        P("items", None),
        P("items", "rows", None),
        P("items", None),
        P(),
        P(),
        P(),
        P(),
        P(),
        P(),
        P(),
        P(),
        P(),
        P("items", "rows", None, None),
    )
    out_specs = (
        P("items", "rows", None, None),
        P("items", "rows", None, None),
        P("items", None),
        P("items", "rows", None),
        P("rows"),
        P(None, None, None, "rows"),
        P("rows", None),
        P("rows"),
        P(None, None, None, "rows"),
        P("rows"),
        P(None, "rows"),
        P("rows", None),
        P(None, "rows"),
    )
    return jax.shard_map(shards, mesh=mesh, in_specs=in_specs, out_specs=out_specs, check_vma=False)
```

```python
import functools

import jax
import jax.numpy as jnp
from jax import lax
from jax.experimental import pallas as pl
from jax.experimental.pallas import tpu as pltpu
from jax.sharding import PartitionSpec as P

GROUPS = 32
HEADS = 8
F32, BF16 = jnp.float32, jnp.bfloat16
NEG = -1e30


def dot(a, b, ca, cb):
    return lax.dot_general(a, b, (((ca,), (cb,)), ((), ())), preferred_element_type=F32)

def attention_kernel(width, step, bq, ext_ref, qkv_ref, text_ref, go_ref, out_ref, dqkv_ref, dtext_ref,
                     kn, vn, kt, vt, s0, s1, e0, e1, dkt, dvt):
    scores, raised = (s0, s1), (e0, e1)
    chunks, _, span = qkv_ref.shape
    tlen = text_ref.shape[0]
    d = go_ref.shape[1]
    pix = chunks * span
    keys = pix + tlen
    steps = keys // step
    rows_ok, cols_ok = ext_ref[0, 0], ext_ref[0, 1]
    def stage(c, carry):
        base = pl.multiple_of(c * span, span)
        pos = base + lax.broadcasted_iota(jnp.int32, (16, span), 1)
        row = lax.broadcasted_iota(jnp.int32, (16, span), 0)
        ok = (pos // width < rows_ok) & (pos % width < cols_ok)
        extra = jnp.where((row == 0) & jnp.logical_not(ok), NEG, 0.0)
        k = qkv_ref[c, d:2 * d, :]
        v = qkv_ref[c, 2 * d:, :]
        kt[:, pl.ds(base, span)] = k
        vt[:, pl.ds(base, span)] = v
        rest = jnp.zeros((128 - d - 16, span), F32)
        ka = jnp.concatenate([k.astype(F32), extra, rest], axis=0)
        va = jnp.concatenate([v.astype(F32), jnp.where(row < 3, 1.0, 0.0), rest], axis=0)
        kn[pl.ds(base, span), :] = ka.T.astype(BF16)
        vn[pl.ds(base, span), :] = va.T.astype(BF16)
        return carry
    lax.fori_loop(0, chunks, stage, 0)
    tk = text_ref[:, :d].astype(F32)
    tv = text_ref[:, d:].astype(F32)
    kt[:, pix:] = tk.T.astype(BF16)
    vt[:, pix:] = tv.T.astype(BF16)
    lanes = lax.broadcasted_iota(jnp.int32, (tlen, 128 - d), 1)
    kn[pix:, :] = jnp.concatenate([tk, jnp.zeros((tlen, 128 - d), F32)], axis=1).astype(BF16)
    vn[pix:, :] = jnp.concatenate([tv, jnp.where(lanes < 3, 1.0, 0.0)], axis=1).astype(BF16)
    dkt[...] = jnp.zeros_like(dkt)
    dvt[...] = jnp.zeros_like(dvt)

    low_peak = jnp.full((8, bq), -3e38, F32)

    def q_aug(c, half):
        q = qkv_ref[c, :d, half * bq:(half + 1) * bq].astype(F32) * (d ** -0.5)
        r = lax.broadcasted_iota(jnp.int32, (128 - d, bq), 0)
        return jnp.concatenate([q, jnp.where(r == 0, 1.0, 0.0)], axis=0).astype(BF16)

    def run(score, exp, back):
        def body(j, carry):
            pk, total, acc, dq = carry
            at = pl.ds(pl.multiple_of(j * step, step), step)
            if score:
                slot, qa = score
                s = dot(kn[at, :], qa, 1, 0)
                scores[slot][at, :] = s
                pk = jnp.maximum(pk, jnp.max(s.reshape(step // 8, 8, bq), axis=0))
            if exp:
                slot, peak = exp
                e = jnp.exp(scores[slot][at, :] - peak)
                total = total + jnp.sum(e.reshape(step // 8, 8, bq), axis=0)
                low = e.astype(BF16)
                raised[slot][at, :] = low
                acc = acc + dot(vt[:, at], low, 1, 0)
            if back:
                slot, goa, gs, q = back
                dp = dot(vn[at, :], goa, 1, 0)
                e = raised[slot][at, :]
                ds = (e.astype(F32) * dp).astype(BF16)
                dvt[:, at] += dot(gs, e, 1, 1)
                dkt[:, at] += dot(q, ds, 1, 1)
                dq = dq + dot(kt[:, at], ds, 1, 0)
            return pk, total, acc, dq
        init = (low_peak, jnp.zeros((8, bq), F32), jnp.zeros((d, bq), F32), jnp.zeros((d, bq), F32))
        return lax.fori_loop(0, steps, body, init)

    def finish_exp(c, half, total, acc):
        inv = 1.0 / jnp.sum(total, axis=0, keepdims=True)
        o = acc * inv
        cols = slice(half * bq, (half + 1) * bq)
        out_ref[c, :, cols] = o.astype(BF16)
        go = go_ref[c, :, cols].astype(F32)
        nd = -jnp.sum(go * o, axis=0, keepdims=True) * inv
        gs = go * inv
        hi = nd.astype(BF16).astype(F32)
        mid = (nd - hi).astype(BF16).astype(F32)
        lo = nd - hi - mid
        r = lax.broadcasted_iota(jnp.int32, (16, bq), 0)
        extra = jnp.where(r == 0, hi, jnp.where(r == 1, mid, jnp.where(r == 2, lo, 0.0)))
        goa = jnp.concatenate([gs, extra, jnp.zeros((128 - d - 16, bq), F32)], axis=0).astype(BF16)
        return goa

    def put_dq(c, half, dq):
        dqkv_ref[c, :d, half * bq:(half + 1) * bq] = (dq * (d ** -0.5)).astype(BF16)

    def top(pk):
        return jnp.max(pk, axis=0, keepdims=True)

    def q_of(c, half):
        return qkv_ref[c, :d, half * bq:(half + 1) * bq]

    pk, _, _, _ = run((0, q_aug(0, 0)), None, None)
    pk, total, acc, _ = run((1, q_aug(0, 1)), (0, top(pk)), None)
    goa = finish_exp(0, 0, total, acc)

    def two(h, carry):
        pk, goa = carry
        pk2, total, acc, dq = run((0, q_aug(h + 1, 0)), (1, top(pk)), (0, goa, goa[:d], q_of(h, 0)))
        put_dq(h, 0, dq)
        goa = finish_exp(h, 1, total, acc)
        pk3, total, acc, dq = run((1, q_aug(h + 1, 1)), (0, top(pk2)), (1, goa, goa[:d], q_of(h, 1)))
        put_dq(h, 1, dq)
        return pk3, finish_exp(h + 1, 0, total, acc)
    pk, goa = lax.fori_loop(0, chunks - 1, two, (pk, goa))
    last = chunks - 1
    _, total, acc, dq = run(None, (1, top(pk)), (0, goa, goa[:d], q_of(last, 0)))
    put_dq(last, 0, dq)
    goa = finish_exp(last, 1, total, acc)
    _, _, _, dq = run(None, None, (1, goa, goa[:d], q_of(last, 1)))
    put_dq(last, 1, dq)

    def finish(c, carry):
        at = pl.ds(pl.multiple_of(c * span, span), span)
        dqkv_ref[c, d:2 * d, :] = (dkt[:, at] * (d ** -0.5)).astype(BF16)
        dqkv_ref[c, 2 * d:, :] = dvt[:, at].astype(BF16)
        return carry
    lax.fori_loop(0, chunks, finish, 0)
    dtext_ref[:d, :] = (dkt[:, pix:] * (d ** -0.5)).astype(BF16)
    dtext_ref[d:, :] = dvt[:, pix:].astype(BF16)

def attention(ext, qkv, text, go, width):
    chunks, wide, span = qkv.shape
    d = wide // 3
    tlen = text.shape[0]
    keys = chunks * span + tlen
    bq = span // 2
    lanes = keys // 128
    step = 128 * max(n for n in range(1, 12) if lanes % n == 0)
    vm = pl.BlockSpec(memory_space=pltpu.VMEM)
    flops = 2 * 6 * chunks * span * keys * d
    return pl.pallas_call(
        functools.partial(attention_kernel, width, step, bq),
        out_shape=(
            jax.ShapeDtypeStruct(go.shape, BF16),
            jax.ShapeDtypeStruct(qkv.shape, BF16),
            jax.ShapeDtypeStruct((2 * d, tlen), BF16),
        ),
        in_specs=[pl.BlockSpec(memory_space=pltpu.SMEM), vm, vm, vm],
        out_specs=(vm, vm, vm),
        scratch_shapes=[
            pltpu.VMEM((keys, 128), BF16),
            pltpu.VMEM((keys, 128), BF16),
            pltpu.VMEM((d, keys), BF16),
            pltpu.VMEM((d, keys), BF16),
            pltpu.VMEM((keys, bq), F32),
            pltpu.VMEM((keys, bq), F32),
            pltpu.VMEM((keys, bq), BF16),
            pltpu.VMEM((keys, bq), BF16),
            pltpu.VMEM((d, keys), F32),
            pltpu.VMEM((d, keys), F32),
        ],
        compiler_params=pltpu.CompilerParams(vmem_limit_bytes=56 << 20),
        cost_estimate=pl.CostEstimate(
            flops=4 * flops, bytes_accessed=16 * chunks * span * d, transcendentals=chunks * span * keys
        ),
    )(ext, qkv, text, go)


MESH = pl.DeviceIdType.MESH
EPS = 1e-05
WHOLE = pl.BlockSpec(memory_space=pltpu.VMEM)
SCALARS = pl.BlockSpec(memory_space=pltpu.SMEM)
ANYWHERE = pl.BlockSpec(memory_space=pl.ANY)


def exchange_kernel(n, count, gathers, *refs):
    inputs, refs = refs[: 1 + count + gathers], refs[1 + count + gathers :]
    outputs, refs = refs[: 1 + 2 * count + gathers], refs[1 + 2 * count + gathers :]
    stats_ref, rows, given = inputs[0], inputs[1 : 1 + count], inputs[1 + count :]
    total_ref, outs, gathered = outputs[0], outputs[1 : 1 + 2 * count], outputs[1 + 2 * count :]
    slots, lands = refs[0], refs[1 : 1 + 2 * count]
    send, recv, row_send, row_recv, own = refs[1 + 2 * count :]
    me = lax.axis_index("rows")
    barrier = pltpu.get_barrier_semaphore()

    def greet(k, carry):
        pl.semaphore_signal(
            barrier, inc=1, device_id={"rows": lax.rem(me + k, n)}, device_id_type=MESH
        )
        return carry

    lax.fori_loop(1, n, greet, 0)
    slots[me] = stats_ref[...]
    pl.semaphore_wait(barrier, n - 1)
    shared = [(stats_ref, slots)] + list(zip(given, gathered))

    def share(j, k):
        return pltpu.make_async_remote_copy(
            src_ref=shared[j][0],
            dst_ref=shared[j][1].at[me],
            send_sem=send.at[j, k],
            recv_sem=recv.at[j, k],
            device_id={"rows": lax.rem(me + k, n)},
            device_id_type=MESH,
        )

    def start(k, carry):
        share(0, k).start()
        return carry

    lax.fori_loop(1, n, start, 0)

    def row_copy(j, side):
        last = rows[j].shape[1] - 1
        at = last if side == 0 else 0
        return pltpu.make_async_remote_copy(
            src_ref=rows[j].at[:, at : at + 1],
            dst_ref=lands[2 * j + side],
            send_sem=row_send.at[2 * j + side],
            recv_sem=row_recv.at[2 * j + side],
            device_id={"rows": me + 1 if side == 0 else me - 1},
            device_id_type=MESH,
        )

    for j in range(count):

        @pl.when(me < n - 1)
        def _():
            row_copy(j, 0).start()

        @pl.when(me > 0)
        def _():
            row_copy(j, 1).start()

    for j in range(gathers):

        def start_given(k, carry):
            share(1 + j, k).start()
            return carry

        lax.fori_loop(1, n, start_given, 0)
        pltpu.make_async_copy(given[j], gathered[j].at[me], own.at[j]).start()

    def finish(k, carry):
        share(0, k).wait()
        return carry

    lax.fori_loop(1, n, finish, 0)
    total_ref[...] = lax.fori_loop(1, n, lambda k, s: s + slots[k], slots[0])
    for j in range(count):

        @pl.when(me > 0)
        def _():
            row_copy(j, 0).wait_recv()
            outs[2 * j][...] = lands[2 * j][...]

        @pl.when(me == 0)
        def _():
            outs[2 * j][...] = jnp.zeros_like(outs[2 * j])

        @pl.when(me < n - 1)
        def _():
            row_copy(j, 1).wait_recv()
            outs[2 * j + 1][...] = lands[2 * j + 1][...]
            row_copy(j, 0).wait_send()

        @pl.when(me == n - 1)
        def _():
            outs[2 * j + 1][...] = jnp.zeros_like(outs[2 * j + 1])

        @pl.when(me > 0)
        def _():
            row_copy(j, 1).wait_send()

    for j in range(gathers):

        def finish_given(k, carry):
            share(1 + j, k).wait()
            return carry

        lax.fori_loop(1, n, finish_given, 0)
        pltpu.make_async_copy(given[j], gathered[j].at[me], own.at[j]).wait()


def exchange(stats, rows, identity, given=()):
    n = lax.axis_size("rows")
    edge = []
    for array in rows:
        edge += [jax.ShapeDtypeStruct(array.shape[:1] + (1,) + array.shape[2:], array.dtype)] * 2
    whole = [jax.ShapeDtypeStruct((n,) + array.shape, array.dtype) for array in given]
    count, gathers = len(rows), len(given)
    nbytes = 4 * stats.size * n + sum(2 * e.size * e.dtype.itemsize for e in (*edge, *whole))
    return pl.pallas_call(
        functools.partial(exchange_kernel, n, count, gathers),
        out_shape=(jax.ShapeDtypeStruct(stats.shape, F32), *edge, *whole),
        in_specs=[WHOLE] + [ANYWHERE] * (count + gathers),
        out_specs=(WHOLE,) * (1 + 2 * count) + (ANYWHERE,) * gathers,
        scratch_shapes=[
            pltpu.VMEM((n,) + stats.shape, F32),
            *[pltpu.VMEM(e.shape, e.dtype) for e in edge],
            pltpu.SemaphoreType.DMA((1 + gathers, n)),
            pltpu.SemaphoreType.DMA((1 + gathers, n)),
            pltpu.SemaphoreType.DMA((max(1, 2 * count),)),
            pltpu.SemaphoreType.DMA((max(1, 2 * count),)),
            pltpu.SemaphoreType.DMA((max(1, gathers),)),
        ],
        compiler_params=pltpu.CompilerParams(collective_id=identity, has_side_effects=True),
        cost_estimate=pl.CostEstimate(
            flops=6_000_000_000, bytes_accessed=nbytes, transcendentals=0
        ),
        name=f"exchange{identity}",
    )(stats, *rows, *given)


def group_sums(rows):
    channels = rows.shape[1]
    size = channels // GROUPS
    one = lax.broadcasted_iota(jnp.int32, (channels, channels), 0) // size
    two = lax.broadcasted_iota(jnp.int32, (channels, channels), 1) // size
    same = jnp.where(one == two, 1.0, 0.0).astype(BF16)
    high = rows.astype(BF16)
    rest = rows - high.astype(F32)
    mid = rest.astype(BF16)
    tail = (rest - mid.astype(F32)).astype(BF16)
    return dot(high, same, 1, 0) + dot(mid, same, 1, 0) + dot(tail, same, 1, 0)


def image_count(info, i, channels):
    return (info[i, 0] * info[i, 1]).astype(F32) * (channels // GROUPS)


def norm_of(stats, count):
    sums = group_sums(stats)
    average = sums[0:1] / count
    square = sums[1:2] / count
    return average, lax.rsqrt(square - average * average + EPS)


def means_of(stats, weight, count):
    sums = group_sums(stats * weight)
    return sums[0:1] / count, sums[1:2] / count


def window(info, i, row, shape):
    ok = (row >= 0) & (row < info[i, 0])
    limit = jnp.where(ok, info[i, 1], 0)
    return jnp.where(lax.broadcasted_iota(jnp.int32, shape, 0) < limit, 1.0, 0.0)


def padded_row(center, above, below, i, r):
    if r == 0:
        return above[i, 0]
    if r == center.shape[1] + 1:
        return below[i, 0]
    return center[i, r - 1]


def put_shifted(out, i, r, value, plain=None):
    width, channels = value.shape
    column = lax.broadcasted_iota(jnp.int32, value.shape, 0)
    left = jnp.where(column == 0, 0.0, pltpu.roll(value, 1, 0))
    right = jnp.where(column == width - 1, 0.0, pltpu.roll(value, width - 1, 0))
    out[i, r, :, :channels] = left.astype(BF16)
    low = value.astype(BF16)
    out[i, r, :, channels : 2 * channels] = low
    if plain is not None:
        plain[i, r] = low
    out[i, r, :, 2 * channels :] = right.astype(BF16)


def sigmoid(v):
    return 1.0 / (1.0 + jnp.exp(-v))


def silu_slope(v):
    s = sigmoid(v)
    return s * (1.0 + v * (1.0 - s))


def put_stats(stats_ref, i, first, second):
    channels = first.shape[1]
    one = jnp.sum(first, axis=0, keepdims=True)
    two = jnp.sum(second, axis=0, keepdims=True)
    row = lax.broadcasted_iota(jnp.int32, (8, channels), 0)
    stats_ref[i] = jnp.where(row == 0, one, jnp.where(row == 1, two, 0.0))


def tap_rows(shifted, tap, images, rows_dev, width):
    block = shifted[:, pl.ds(tap, rows_dev)]
    return block.reshape(images * rows_dev * width, shifted.shape[3])


def conv1_kernel(info, image, above, below, stats, gain, weight, first, out_stats, hidden, acc, shifted):
    images, rows_dev, width, channels = image.shape
    tap = pl.program_id(0)
    base = info[0, 2]

    @pl.when(tap == 0)
    def _():
        for i in range(images):
            average, inverse = norm_of(stats[i], image_count(info, i, channels))
            for r in range(rows_dev + 2):
                inside = window(info, i, base + r - 1, (width, channels))
                start = padded_row(image, above, below, i, r).astype(F32) * inside
                value = (start - average) * inverse * inside * gain[...]
                put_shifted(shifted, i, r, value * sigmoid(value) * inside, hidden)

    part = dot(tap_rows(shifted, tap, images, rows_dev, width), weight[0], 1, 0)

    @pl.when(tap == 0)
    def _():
        acc[...] = part

    @pl.when(tap > 0)
    def _():
        acc[...] += part

    @pl.when(tap == 2)
    def _():
        for i in range(images):
            one = two = jnp.zeros((width, channels), F32)
            for r in range(rows_dev):
                inside = window(info, i, base + r, (width, channels))
                at = (i * rows_dev + r) * width
                value = acc[at : at + width] * inside
                first[i, r] = value
                one = one + value
                two = two + value * value
            put_stats(out_stats, i, one, two)


def moved_of(value, inside, average, inverse, gain, scale, shift):
    normal = (value - average) * inverse * inside
    return normal, normal * gain * (1.0 + scale) + shift


def conv2_kernel(
    info, first, above, below, stats, gain, shifts, image, weight, middle, out_stats, second, acc,
    shifted,
):
    images, rows_dev, width, channels = first.shape
    tap = pl.program_id(0)
    base = info[0, 2]

    @pl.when(tap == 0)
    def _():
        for i in range(images):
            average, inverse = norm_of(stats[i], image_count(info, i, channels))
            scale, shift = shifts[i : i + 1, :channels], shifts[i : i + 1, channels:]
            for r in range(rows_dev + 2):
                inside = window(info, i, base + r - 1, (width, channels))
                value = padded_row(first, above, below, i, r)
                _, moved = moved_of(value, inside, average, inverse, gain[...], scale, shift)
                put_shifted(shifted, i, r, moved * sigmoid(moved) * inside, second)

    part = dot(tap_rows(shifted, tap, images, rows_dev, width), weight[0], 1, 0)

    @pl.when(tap == 0)
    def _():
        acc[...] = part

    @pl.when(tap > 0)
    def _():
        acc[...] += part

    @pl.when(tap == 2)
    def _():
        for i in range(images):
            one = two = jnp.zeros((width, channels), F32)
            for r in range(rows_dev):
                inside = window(info, i, base + r, (width, channels))
                at = (i * rows_dev + r) * width
                value = (image[i, r].astype(F32) + acc[at : at + width]) * inside
                middle[i, r] = value
                one = one + value
                two = two + value * value
            put_stats(out_stats, i, one, two)


def dgrad(shifted, tap, weight, images, rows_dev, width):
    channels = weight.shape[2]
    lhs = tap_rows(shifted, tap, images, rows_dev, width)
    part = None
    for b in range(3):
        term = dot(
            lhs[:, b * channels : (b + 1) * channels],
            weight[0, (2 - b) * channels : (3 - b) * channels, :],
            1,
            1,
        )
        part = term if part is None else part + term
    return part


def back2_kernel(
    info, grad, grad_above, grad_below, middle, mid_above, mid_below, cot, cot_above, cot_below,
    mid_stats, grad_stats, attn_gain, first, first_stats, gain, shifts, weight,
    grad_middle, moved_grad, out_stats, plain, acc, shifted,
):
    images, rows_dev, width, channels = first.shape
    tap = pl.program_id(0)
    base = info[0, 2]

    @pl.when(tap == 0)
    def _():
        for i in range(images):
            count = image_count(info, i, channels)
            average, inverse = norm_of(mid_stats[i], count)
            mean, cross = means_of(grad_stats[i], attn_gain[...], count)
            for r in range(rows_dev + 2):
                inside = window(info, i, base + r - 1, (width, channels))
                normal = (padded_row(middle, mid_above, mid_below, i, r) - average) * inverse
                dx = padded_row(grad, grad_above, grad_below, i, r) * attn_gain[...]
                term = (dx - mean - normal * cross) * inverse * inside
                total = padded_row(cot, cot_above, cot_below, i, r).astype(F32) + term
                if 0 < r <= rows_dev:
                    grad_middle[i, r - 1] = total
                put_shifted(shifted, i, r, total * inside, plain)

    part = dgrad(shifted, tap, weight, images, rows_dev, width)

    @pl.when(tap == 0)
    def _():
        acc[...] = part

    @pl.when(tap > 0)
    def _():
        acc[...] += part

    @pl.when(tap == 2)
    def _():
        for i in range(images):
            average, inverse = norm_of(first_stats[i], image_count(info, i, channels))
            scale, shift = shifts[i : i + 1, :channels], shifts[i : i + 1, channels:]
            one = two = jnp.zeros((width, channels), F32)
            for r in range(rows_dev):
                inside = window(info, i, base + r, (width, channels))
                at = (i * rows_dev + r) * width
                normal, moved = moved_of(
                    first[i, r], inside, average, inverse, gain[...], scale, shift
                )
                value = acc[at : at + width] * inside * silu_slope(moved)
                moved_grad[i, r] = value
                one = one + value
                two = two + value * normal
            put_stats(out_stats, i, one, two)


def back1_kernel(
    info, grad, grad_above, grad_below, first, first_above, first_below, first_stats, grad_stats,
    gain, shifts, image, image_stats, first_gain, weight,
    pre_grad, out_stats, plain, acc, shifted,
):
    images, rows_dev, width, channels = first.shape
    tap = pl.program_id(0)
    base = info[0, 2]

    @pl.when(tap == 0)
    def _():
        for i in range(images):
            count = image_count(info, i, channels)
            average, inverse = norm_of(first_stats[i], count)
            factor = gain[...] * (1.0 + shifts[i : i + 1, :channels])
            mean, cross = means_of(grad_stats[i], factor, count)
            for r in range(rows_dev + 2):
                inside = window(info, i, base + r - 1, (width, channels))
                normal = (padded_row(first, first_above, first_below, i, r) - average) * inverse
                dx = padded_row(grad, grad_above, grad_below, i, r) * factor
                put_shifted(shifted, i, r, (dx - mean - normal * cross) * inverse * inside, plain)

    part = dgrad(shifted, tap, weight, images, rows_dev, width)

    @pl.when(tap == 0)
    def _():
        acc[...] = part

    @pl.when(tap > 0)
    def _():
        acc[...] += part

    @pl.when(tap == 2)
    def _():
        for i in range(images):
            average, inverse = norm_of(image_stats[i], image_count(info, i, channels))
            one = two = jnp.zeros((width, channels), F32)
            for r in range(rows_dev):
                inside = window(info, i, base + r, (width, channels))
                at = (i * rows_dev + r) * width
                normal = (image[i, r].astype(F32) - average) * inverse * inside
                slope = silu_slope(normal * first_gain[...])
                value = acc[at : at + width] * inside * slope
                pre_grad[i, r] = value
                one = one + value
                two = two + value * normal
            put_stats(out_stats, i, one, two)


def conv_call(kernel, info, inputs, weight, outs, flipped):
    images, rows_dev, width, channels = outs[0].shape

    def whole(shape):
        return pl.BlockSpec(shape, lambda tap: (0,) * len(shape))

    def tap_of(tap):
        return ((2 - tap) if flipped else tap, 0, 0)

    weight = weight.reshape(3, 3 * channels, channels)
    flops = 2 * 9 * images * rows_dev * width * channels * channels
    moved = sum(a.size * a.dtype.itemsize for a in (*inputs, weight, *outs))
    return pl.pallas_call(
        kernel,
        grid=(3,),
        out_shape=tuple(outs),
        in_specs=[SCALARS]
        + [whole(a.shape) for a in inputs]
        + [pl.BlockSpec((1, 3 * channels, channels), tap_of)],
        out_specs=tuple(whole(o.shape) for o in outs),
        scratch_shapes=[
            pltpu.VMEM((images * rows_dev * width, channels), F32),
            pltpu.VMEM((images, rows_dev + 2, width, 3 * channels), BF16),
        ],
        compiler_params=pltpu.CompilerParams(vmem_limit_bytes=48 << 20),
        cost_estimate=pl.CostEstimate(flops=flops, bytes_accessed=moved, transcendentals=0),
        name=kernel.__name__,
    )(info, *inputs, weight)


def weight_grad_kernel(grads, hidden, out, turned, shifted):
    images, padded, width, channels = hidden.shape
    rows_dev = padded - 2
    pixels = images * rows_dev * width
    tap = pl.program_id(0)

    @pl.when(tap == 0)
    def _():
        center = grads[:, 1 : rows_dev + 1]
        turned[...] = center.reshape(pixels, channels).astype(F32).T.astype(BF16)
        for i in range(images):
            for r in range(padded):
                put_shifted(shifted, i, r, hidden[i, r].astype(F32))

    column = pl.multiple_of((tap % 3) * channels, channels)
    rhs = shifted[:, pl.ds(tap // 3, rows_dev), :, pl.ds(column, channels)]
    out[...] = dot(turned[...], rhs.reshape(pixels, channels), 1, 0).astype(BF16)


def weight_grad(grads, hidden):
    images, padded, width, channels = hidden.shape
    pixels = images * (padded - 2) * width

    def whole(shape):
        return pl.BlockSpec(shape, lambda tap: (0,) * len(shape))

    return pl.pallas_call(
        weight_grad_kernel,
        grid=(9,),
        out_shape=jax.ShapeDtypeStruct((channels, 9 * channels), BF16),
        in_specs=[whole(grads.shape), whole(hidden.shape)],
        out_specs=pl.BlockSpec((channels, channels), lambda tap: (0, tap)),
        scratch_shapes=[
            pltpu.VMEM((channels, pixels), BF16),
            pltpu.VMEM(hidden.shape[:3] + (3 * channels,), BF16),
        ],
        compiler_params=pltpu.CompilerParams(vmem_limit_bytes=32 << 20),
        cost_estimate=pl.CostEstimate(
            flops=18 * pixels * channels * channels,
            bytes_accessed=18 * channels * channels,
            transcendentals=0,
        ),
        name="weight_grad",
    )(grads, hidden)


def reduce_kernel(items, chips, has_extra, *refs):
    if has_extra:
        grads, hidden, extra, vector, out, extra_out, vectors, *refs = refs
    else:
        grads, hidden, out, *refs = refs
    (turned, quarter, shifted, part, from_core, chip_sum, from_chip, final, g_send, g_recv, c_send, c_recv,
     z_send, z_recv, f_send, f_recv, *refs) = refs
    _, padded, width, channels = grads.shape
    rows_dev = padded - 2
    pixels = rows_dev * width
    share = channels // (2 * chips)
    slice_rows = share // items
    item, row = lax.axis_index("items"), lax.axis_index("rows")
    chip, core = row // 2, lax.rem(row, 2)
    barrier = pltpu.get_barrier_semaphore()
    peers = [{"items": lax.rem(item + k, items), "rows": row} for k in range(1, items)]
    others = [
        {"items": item, "rows": lax.rem(chip + k, chips) * 2 + core} for k in range(1, chips)
    ]
    sibling = {"items": item, "rows": row + 1 - 2 * core}
    for device in (sibling, *peers, *others):
        pl.semaphore_signal(barrier, inc=1, device_id=device, device_id_type=MESH)

    for r in range(rows_dev):
        block = grads[0, 1 + r].astype(F32).T.astype(BF16)
        for z in range(chips):
            for c in range(2):
                for q in range(items):
                    at = (z * 2 + c) * share + q * slice_rows
                    to = (c * chips + z) * slice_rows
                    turned[q, to : to + slice_rows, r * width : (r + 1) * width] = block[
                        at : at + slice_rows
                    ]
    pl.semaphore_wait(barrier, items + chips - 1)

    def copy(src, dst, send, recv, device):
        return pltpu.make_async_remote_copy(
            src_ref=src,
            dst_ref=dst,
            send_sem=send,
            recv_sem=recv,
            device_id=device,
            device_id_type=MESH,
        )

    started = []

    def go(*args):
        c = copy(*args)
        c.start()
        started.append(c)
        return c

    g_copies = [
        go(
            turned.at[lax.rem(item + k, items)],
            quarter.at[item],
            g_send.at[k],
            g_recv.at[k],
            peers[k - 1],
        )
        for k in range(1, items)
    ]
    if has_extra:
        land, summed, v_land, e_send, e_recv, h_send, h_recv, v_send, v_recv = refs
        e_copies = [
            go(
                extra.at[lax.rem(item + k, items)],
                land.at[item],
                e_send.at[k],
                e_recv.at[k],
                peers[k - 1],
            )
            for k in range(1, items)
        ]
        v_copies = [
            go(vector, v_land.at[item], v_send.at[k], v_recv.at[k], peers[k - 1])
            for k in range(1, items)
        ]
        land[item] = extra[item]
        v_land[item] = vector[...]
    quarter[item] = turned[item]
    for g in range(items):

        def shift(r, carry):
            put_shifted(shifted, g, r, hidden[g, r].astype(F32))
            return carry

        lax.fori_loop(0, padded, shift, 0)
    for c in g_copies:
        c.wait_recv()
    if has_extra:
        for c in e_copies:
            c.wait_recv()
        total = land[0].astype(F32)
        for g in range(1, items):
            total = total + land[g].astype(F32)
        summed[item] = total.astype(BF16)
        h_copies = [
            go(summed.at[item], summed.at[item], h_send.at[k], h_recv.at[k], peers[k - 1])
            for k in range(1, items)
        ]

    half = chips * slice_rows
    core_copies, chip_copies, final_copies = [], [], []

    def compute(a):
        for b in range(3):
            acc = None
            for g in range(items):
                rhs = shifted[g, a : a + rows_dev, :, b * channels : (b + 1) * channels]
                term = dot(quarter[g], rhs.reshape(pixels, channels), 1, 0)
                acc = term if acc is None else acc + term
            part[a, 0, b] = acc[:half].astype(BF16)
            part[a, 1, b] = acc[half:].astype(BF16)
        core_copies.append(
            go(part.at[a, 1 - core], from_core.at[a], c_send.at[a], c_recv.at[a], sibling)
        )

    def over_chips(a):
        core_copies[a].wait_recv()
        for b in range(3):
            both = part[a, core, b].astype(F32) + from_core[a, b].astype(F32)
            for z in range(chips):
                chip_sum[a, z, b] = both[z * slice_rows : (z + 1) * slice_rows].astype(BF16)
        chip_copies.append(
            [
                go(
                    chip_sum.at[a, lax.rem(chip + k, chips)],
                    from_chip.at[a, k],
                    z_send.at[a, k],
                    z_recv.at[a, k],
                    others[k - 1],
                )
                for k in range(1, chips)
            ]
        )

    def over_items(a):
        for c in chip_copies[a]:
            c.wait_recv()
        total = chip_sum[a, chip].astype(F32)
        for k in range(1, chips):
            total = total + from_chip[a, k].astype(F32)
        final[a, item] = total.astype(BF16)
        final_copies.append(
            [
                go(
                    final.at[a, item],
                    final.at[a, item],
                    f_send.at[a, k],
                    f_recv.at[a, k],
                    peers[k - 1],
                )
                for k in range(1, items)
            ]
        )

    def put(a):
        for c in final_copies[a]:
            c.wait_recv()
        for b in range(3):
            rows = jnp.concatenate([final[a, q, b].astype(F32) for q in range(items)], axis=0)
            at = (a * 3 + b) * channels
            out[at : at + channels] = rows.T

    compute(0)
    compute(1)
    over_chips(0)
    compute(2)
    over_chips(1)
    over_chips(2)
    over_items(0)
    over_items(1)
    over_items(2)
    if has_extra:
        for c in h_copies:
            c.wait_recv()
        for q in range(items):
            rows = summed.shape[1]
            extra_out[q * rows : (q + 1) * rows] = summed[q].astype(F32)
        for c in v_copies:
            c.wait_recv()
        vectors[...] = v_land[...]
    put(0)
    put(1)
    put(2)
    for c in started:
        c.wait_send()


def reduce_weight(grads, hidden, identity, extra=None, vector=None):
    items, chips = lax.axis_size("items"), lax.axis_size("rows") // 2
    _, padded, width, channels = grads.shape
    pixels = (padded - 2) * width
    share = channels // (2 * chips)
    rows = share // items
    inputs = [grads, hidden]
    outs = [jax.ShapeDtypeStruct((9 * channels, share), F32)]
    sem = pltpu.SemaphoreType.DMA
    scratch = [
        pltpu.VMEM((items, channels // items, pixels), BF16),
        pltpu.VMEM((items, channels // items, pixels), BF16),
        pltpu.VMEM((items, padded, width, 3 * channels), BF16),
        pltpu.VMEM((3, 2, 3, chips * rows, channels), BF16),
        pltpu.VMEM((3, 3, chips * rows, channels), BF16),
        pltpu.VMEM((3, chips, 3, rows, channels), BF16),
        pltpu.VMEM((3, chips, 3, rows, channels), BF16),
        pltpu.VMEM((3, items, 3, rows, channels), BF16),
        sem((items,)),
        sem((items,)),
        sem((3,)),
        sem((3,)),
        sem((3, chips)),
        sem((3, chips)),
        sem((3, items)),
        sem((3, items)),
    ]
    if extra is not None:
        inputs += [extra.reshape(items, extra.shape[0] // items, extra.shape[1]), vector]
        outs += [
            jax.ShapeDtypeStruct(extra.shape, F32),
            jax.ShapeDtypeStruct((items,) + vector.shape, F32),
        ]
        scratch += [
            pltpu.VMEM(inputs[2].shape, BF16),
            pltpu.VMEM(inputs[2].shape, BF16),
            pltpu.VMEM((items,) + vector.shape, F32),
        ] + [sem((items,))] * 6
    return pl.pallas_call(
        functools.partial(reduce_kernel, items, chips, extra is not None),
        out_shape=tuple(outs),
        in_specs=[WHOLE] * len(inputs),
        out_specs=(WHOLE,) * len(outs),
        scratch_shapes=scratch,
        compiler_params=pltpu.CompilerParams(
            collective_id=identity, has_side_effects=True, vmem_limit_bytes=48 << 20
        ),
        cost_estimate=pl.CostEstimate(
            flops=20_000_000_000, bytes_accessed=40 * channels * channels, transcendentals=0
        ),
        name=f"reduce{identity}",
    )(*inputs)


def project_kernel(info, middle, stats, gain, weight, attn, qkv):
    images, rows_dev, width, channels = middle.shape
    pixels = rows_dev * width
    heads, wide = HEADS, weight.shape[0] // HEADS
    base = info[0, 2]
    for i in range(images):
        average, inverse = norm_of(stats[i], image_count(info, i, channels))
        for r in range(rows_dev):
            inside = window(info, i, base + r, (width, channels))
            value = (middle[i, r] - average) * inverse * inside * gain[...]
            attn[i, r * width : (r + 1) * width] = value.astype(BF16)
        for h in range(heads):
            block = dot(weight[h * wide : (h + 1) * wide], attn[i], 1, 1)
            qkv[i * heads + h] = block.astype(BF16)


def project(info, middle, stats, gain, weight):
    images, rows_dev, width, channels = middle.shape
    pixels = rows_dev * width
    return pl.pallas_call(
        project_kernel,
        out_shape=(
            jax.ShapeDtypeStruct((images, pixels, channels), BF16),
            jax.ShapeDtypeStruct((images * HEADS, weight.shape[0] // HEADS, pixels), BF16),
        ),
        in_specs=[SCALARS, WHOLE, WHOLE, WHOLE, WHOLE],
        out_specs=(WHOLE, WHOLE),
        compiler_params=pltpu.CompilerParams(vmem_limit_bytes=32 << 20),
        name="project",
    )(info, middle, stats, gain, weight)


def unproject_kernel(info, middle, stats, grads, weight, out, out_stats):
    images, rows_dev, width, channels = middle.shape
    wide, pixels = grads.shape[1], grads.shape[2]
    base = info[0, 2]
    for i in range(images):
        average, inverse = norm_of(stats[i], image_count(info, i, channels))
        acc = None
        for h in range(HEADS):
            turned = grads[i * HEADS + h].astype(F32).T.astype(BF16)
            term = dot(turned, weight[h * wide : (h + 1) * wide], 1, 0)
            acc = term if acc is None else acc + term
        one = two = jnp.zeros((width, channels), F32)
        for r in range(rows_dev):
            inside = window(info, i, base + r, (width, channels))
            value = acc[r * width : (r + 1) * width] * inside
            out[i, r] = value
            one = one + value
            two = two + value * ((middle[i, r] - average) * inverse)
        put_stats(out_stats, i, one, two)


def unproject(info, middle, stats, grads, weight):
    images, rows_dev, width, channels = middle.shape
    return pl.pallas_call(
        unproject_kernel,
        out_shape=(
            jax.ShapeDtypeStruct(middle.shape, F32),
            jax.ShapeDtypeStruct(stats.shape, F32),
        ),
        in_specs=[SCALARS, WHOLE, WHOLE, WHOLE, WHOLE],
        out_specs=(WHOLE, WHOLE),
        compiler_params=pltpu.CompilerParams(vmem_limit_bytes=32 << 20),
        name="unproject",
    )(info, middle, stats, grads, weight)


def finish_kernel(info, pre_grad, grad_stats, image, stats, gain, grad_middle, out):
    images, rows_dev, width, channels = image.shape
    base = info[0, 2]
    for i in range(images):
        count = image_count(info, i, channels)
        average, inverse = norm_of(stats[i], count)
        mean, cross = means_of(grad_stats[i], gain[...], count)
        for r in range(rows_dev):
            inside = window(info, i, base + r, (width, channels))
            normal = (image[i, r].astype(F32) - average) * inverse
            term = (pre_grad[i, r] * gain[...] - mean - normal * cross) * inverse
            out[i, r] = (grad_middle[i, r] + term) * inside


def finish(info, pre_grad, grad_stats, image, stats, gain, grad_middle):
    return pl.pallas_call(
        finish_kernel,
        out_shape=jax.ShapeDtypeStruct(image.shape, F32),
        in_specs=[SCALARS] + [WHOLE] * 6,
        out_specs=WHOLE,
        compiler_params=pltpu.CompilerParams(vmem_limit_bytes=32 << 20),
        name="finish",
    )(info, pre_grad, grad_stats, image, stats, gain, grad_middle)


DMA = pltpu.SemaphoreType.DMA


def remote(src, dst, send, recv, device):
    return pltpu.make_async_remote_copy(
        src_ref=src,
        dst_ref=dst,
        send_sem=send,
        recv_sem=recv,
        device_id=device,
        device_id_type=MESH,
    )


class Grid:
    def __init__(self, items, n):
        self.items, self.n = items, n
        self.item, self.me = lax.axis_index("items"), lax.axis_index("rows")

    def row(self, k):
        return {"items": self.item, "rows": lax.rem(self.me + k, self.n)}

    def peer(self, k):
        return {"items": lax.rem(self.item + k, self.items), "rows": self.me}

    def greet(self):
        barrier = pltpu.get_barrier_semaphore()

        def rows(k, carry):
            pl.semaphore_signal(barrier, inc=1, device_id=self.row(k), device_id_type=MESH)
            return carry

        def items(k, carry):
            pl.semaphore_signal(barrier, inc=1, device_id=self.peer(k), device_id_type=MESH)
            return carry

        lax.fori_loop(1, self.n, rows, 0)
        lax.fori_loop(1, self.items, items, 0)

    def met(self):
        pl.semaphore_wait(pltpu.get_barrier_semaphore(), self.n + self.items - 2)

    def loop(self, count, body):
        def step(k, carry):
            body(k)
            return carry

        lax.fori_loop(1, count, step, 0)


class Sums:
    def __init__(self, grid, own, slots, send, recv):
        self.grid, self.own, self.slots, self.send, self.recv = grid, own, slots, send, recv

    def copy(self, k):
        return remote(
            self.own, self.slots.at[self.grid.me], self.send.at[k], self.recv.at[k], self.grid.row(k)
        )

    def start(self):
        self.grid.loop(self.grid.n, lambda k: self.copy(k).start())
        self.slots[self.grid.me] = self.own[...]

    def result(self):
        self.grid.loop(self.grid.n, lambda k: self.copy(k).wait())
        slots = self.slots
        return lax.fori_loop(1, self.grid.n, lambda k, s: s + slots[k], slots[0])


class Edges:
    def __init__(self, grid, field, send, recv):
        self.grid, self.field, self.send, self.recv = grid, field, send, recv

    def copy(self, side):
        last = self.field.shape[0] - 1
        at, to = (last - 1, 0) if side == 0 else (1, last)
        grid = self.grid
        return remote(
            self.field.at[at : at + 1],
            self.field.at[to : to + 1],
            self.send.at[side],
            self.recv.at[side],
            {"items": grid.item, "rows": grid.me + 1 if side == 0 else grid.me - 1},
        )

    def both(self, down, up):
        @pl.when(self.grid.me < self.grid.n - 1)
        def _():
            down()

        @pl.when(self.grid.me > 0)
        def _():
            up()

    def clear(self):
        last = self.field.shape[0] - 1

        @pl.when(self.grid.me == 0)
        def _():
            self.field[0] = jnp.zeros(self.field.shape[1:], self.field.dtype)

        @pl.when(self.grid.me == self.grid.n - 1)
        def _():
            self.field[last] = jnp.zeros(self.field.shape[1:], self.field.dtype)

    def start(self):
        self.both(lambda: self.copy(0).start(), lambda: self.copy(1).start())

    def wait(self):
        self.both(lambda: self.copy(1).wait_recv(), lambda: self.copy(0).wait_recv())
        self.both(lambda: self.copy(0).wait_send(), lambda: self.copy(1).wait_send())


def shift_into(out, r, value):
    width, channels = value.shape
    column = lax.broadcasted_iota(jnp.int32, value.shape, 0)
    left = jnp.where(column == 0, 0.0, pltpu.roll(value, 1, 0))
    right = jnp.where(column == width - 1, 0.0, pltpu.roll(value, width - 1, 0))
    out[r, :, :channels] = left.astype(BF16)
    out[r, :, channels : 2 * channels] = value.astype(BF16)
    out[r, :, 2 * channels :] = right.astype(BF16)


def row_stats(rows, width, channels, row):
    def step(r, carry):
        one, two = row(r)
        return carry[0] + one, carry[1] + two

    zero = jnp.zeros((width, channels), F32)
    one, two = lax.fori_loop(0, rows, step, (zero, zero))
    one = jnp.sum(one, axis=0, keepdims=True)
    two = jnp.sum(two, axis=0, keepdims=True)
    at = lax.broadcasted_iota(jnp.int32, (8, channels), 0)
    return jnp.where(at == 0, one, jnp.where(at == 1, two, 0.0))


def each_row(rows, body):
    def step(r, carry):
        body(r)
        return carry

    lax.fori_loop(0, rows, step, 0)


def conv_taps(shifted, weight, acc, rows_dev):
    pixels, wide = acc.shape[0], shifted.shape[2]
    acc[...] = jnp.zeros_like(acc)

    def step(tap, carry):
        acc[...] += dot(shifted[pl.ds(tap, rows_dev)].reshape(pixels, wide), weight[tap], 1, 0)
        return carry

    lax.fori_loop(0, 3, step, 0)


def forward_kernel(items, n, *refs):
    (info, image, cot, text, embed, gain1, gain2, gain3, w1_in, w2_in, embed_in, text_in, qkv_in, proj_in,
     first_out, mid_out, cot_out, hidden_all, second_all, attn_out, turned_out, qkv_pair, go_pair, text_pair,
     text_cols, stats_out, shifts_out,
     image_v, cot_v, text_v, w1, w2, embed_w, text_w, qkv_w, proj_w, first_v, mid_v, hidden, second, attn,
     turned, qkv, go, text_kv, cols, shifted, acc, own, slots,
     load, sum_send, sum_recv, edge_send, edge_recv, row_send, row_recv, item_send, item_recv) = refs
    grid = Grid(items, n)
    item, me = grid.item, grid.me
    rows_dev, width, channels = image.shape
    pixels = rows_dev * width
    heads, head_dim, wide = HEADS, channels // HEADS, 3 * channels // HEADS
    base = me * rows_dev
    count = (info[0, 0] * info[0, 1]).astype(F32) * (channels // GROUPS)

    def inside(row):
        return window(info, 0, row, (width, channels))

    loads = []

    def fetch(src, dst):
        c = pltpu.make_async_copy(src, dst, load.at[len(loads)])
        c.start()
        loads.append(c)
        return c

    center = slice(1, rows_dev + 1)
    got_image = fetch(image, image_v.at[center])
    got_cot = fetch(cot, cot_v.at[center])
    got_proj = fetch(proj_in, proj_w)
    got_text = fetch(text, text_v)
    got_text_w = fetch(text_in, text_w)
    got_w1 = fetch(w1_in, w1)
    got_embed_w = fetch(embed_in, embed_w)
    got_w2 = fetch(w2_in, w2)
    got_qkv_w = fetch(qkv_in, qkv_w)
    edges = [
        Edges(grid, field, edge_send.at[j], edge_recv.at[j])
        for j, field in enumerate((image_v, cot_v, first_v, mid_v))
    ]
    sums = [Sums(grid, own.at[j], slots.at[j], sum_send.at[j], sum_recv.at[j]) for j in range(3)]
    grid.greet()
    for e in edges:
        e.clear()
    got_image.wait()

    def start_row(r):
        return image_v[1 + r].astype(F32) * inside(base + r)

    def start_stats(r):
        v = start_row(r)
        return v, v * v

    own[0] = row_stats(rows_dev, width, channels, start_stats)
    grid.met()
    sums[0].start()
    edges[0].start()
    got_cot.wait()
    edges[1].start()

    got_text.wait()
    got_text_w.wait()
    text_all = dot(text_v[...], text_w[...], 1, 0).astype(BF16)
    share = text_v.shape[1] // n
    for h in range(heads):
        text_kv[h] = text_all[:, h * 2 * head_dim : (h + 1) * 2 * head_dim]
    for r in range(n):
        cols[r] = text_v[:, r * share : (r + 1) * share]

    def scatter(j, src, dst):
        def copy(k):
            to = lax.rem(me + k, n)
            return remote(src.at[to], dst.at[me], row_send.at[j, k], row_recv.at[j, k], grid.row(k))

        return copy

    kv_copy = scatter(0, text_kv, text_pair)
    col_copy = scatter(1, cols, text_cols.at[item])
    grid.loop(n, lambda k: kv_copy(k).start())
    grid.loop(n, lambda k: col_copy(k).start())
    own_kv = fetch(text_kv.at[me], text_pair.at[me])
    own_col = fetch(cols.at[me], text_cols.at[item, me])

    got_proj.wait()

    def to_grad(r):
        attn[pl.ds(r * width, width)] = (cot_v[1 + r].astype(F32) * inside(base + r)).astype(BF16)

    each_row(rows_dev, to_grad)
    for h in range(heads):
        go[h] = dot(proj_w[h * head_dim : (h + 1) * head_dim], attn[...], 1, 1).astype(BF16)
    go_copy = scatter(2, go, go_pair)
    own_go = fetch(go.at[me], go_pair.at[me])

    stats = sums[0].result()
    stats_out[0] = stats
    average, inverse = norm_of(stats, count)
    edges[0].wait()
    grid.loop(n, lambda k: go_copy(k).start())

    def to_hidden(r):
        ok = inside(base + r - 1)
        value = (image_v[r].astype(F32) * ok - average) * inverse * ok * gain1[...]
        value = value * sigmoid(value) * ok
        shift_into(shifted, r, value)
        hidden[r] = value.astype(BF16)

    each_row(rows_dev + 2, to_hidden)

    def spread(j, src, dst):
        def copy(k):
            return remote(src, dst.at[item], item_send.at[j, k], item_recv.at[j, k], grid.peer(k))

        return copy

    hidden_copy = spread(0, hidden, hidden_all)
    grid.loop(items, lambda k: hidden_copy(k).start())
    own_hidden = fetch(hidden, hidden_all.at[item])
    got_w1.wait()
    conv_taps(shifted, w1, acc, rows_dev)

    def first_row(r):
        value = acc[pl.ds(r * width, width)] * inside(base + r)
        first_v[1 + r] = value
        return value, value * value

    own[1] = row_stats(rows_dev, width, channels, first_row)
    sums[1].start()
    edges[2].start()

    e = embed[...].astype(F32)
    low = (e * sigmoid(e)).astype(BF16)
    got_embed_w.wait()
    shifts_out[...] = dot(low, embed_w[...], 1, 0)
    scale, shift = shifts_out[:, :channels], shifts_out[:, channels:]

    stats = sums[1].result()
    stats_out[1] = stats
    average, inverse = norm_of(stats, count)
    edges[2].wait()
    own_first = fetch(first_v, first_out)

    def to_second(r):
        ok = inside(base + r - 1)
        _, moved = moved_of(first_v[r], ok, average, inverse, gain2[...], scale, shift)
        value = moved * sigmoid(moved) * ok
        shift_into(shifted, r, value)
        second[r] = value.astype(BF16)

    each_row(rows_dev + 2, to_second)
    second_copy = spread(1, second, second_all)
    grid.loop(items, lambda k: second_copy(k).start())
    own_second = fetch(second, second_all.at[item])
    got_w2.wait()
    conv_taps(shifted, w2, acc, rows_dev)

    def middle_row(r):
        value = (image_v[1 + r].astype(F32) + acc[pl.ds(r * width, width)]) * inside(base + r)
        mid_v[1 + r] = value
        return value, value * value

    own[2] = row_stats(rows_dev, width, channels, middle_row)
    sums[2].start()
    edges[3].start()
    own_go.wait()
    edges[1].wait()
    own_cot = fetch(cot_v, cot_out)
    got_qkv_w.wait()
    for j in range(3):
        block = qkv_w[:, j * channels : (j + 1) * channels].astype(F32).T
        turned[j * channels : (j + 1) * channels] = block.astype(BF16)
    own_turned = fetch(turned, turned_out)

    stats = sums[2].result()
    stats_out[2] = stats
    average, inverse = norm_of(stats, count)

    def to_attn(r):
        value = (mid_v[1 + r] - average) * inverse * inside(base + r) * gain3[...]
        attn[pl.ds(r * width, width)] = value.astype(BF16)

    each_row(rows_dev, to_attn)
    own_attn = fetch(attn, attn_out)
    qkv_copy = scatter(3, qkv, qkv_pair)

    def head(k, carry):
        to = lax.rem(me + k, n)
        rows = pl.ds(pl.multiple_of(to * wide, wide), wide)
        qkv[to] = dot(turned[rows], attn[...], 1, 1).astype(BF16)
        return carry

    def send_head(k, carry):
        head(k, carry)
        qkv_copy(k).start()
        return carry

    lax.fori_loop(1, n, send_head, 0)
    head(0, 0)
    own_qkv = fetch(qkv.at[me], qkv_pair.at[me])
    edges[3].wait()
    own_mid = fetch(mid_v, mid_out)

    grid.loop(n, lambda k: kv_copy(k).wait())
    grid.loop(n, lambda k: col_copy(k).wait())
    own_col.wait()
    cols_copy = spread(2, text_cols.at[item], text_cols)
    grid.loop(items, lambda k: cols_copy(k).start())
    grid.loop(n, lambda k: go_copy(k).wait())
    grid.loop(n, lambda k: qkv_copy(k).wait())
    grid.loop(items, lambda k: hidden_copy(k).wait())
    grid.loop(items, lambda k: second_copy(k).wait())
    grid.loop(items, lambda k: cols_copy(k).wait())
    for c in (own_kv, own_hidden, own_first, own_second, own_cot, own_turned, own_attn, own_qkv, own_mid):
        c.wait()


def forward_call(info, image, cot, text, embed, gains, weights, identity):
    items, n = lax.axis_size("items"), lax.axis_size("rows")
    rows_dev, width, channels = image.shape
    pixels = rows_dev * width
    padded = (rows_dev + 2, width, channels)
    tokens, text_width = text.shape
    head_dim = channels // HEADS
    w1, w2, embed_w, text_w, qkv_w, proj_w = weights
    sds = jax.ShapeDtypeStruct
    outs = (
        sds(padded, F32),
        sds(padded, F32),
        sds(padded, BF16),
        sds((items,) + padded, BF16),
        sds((items,) + padded, BF16),
        sds((pixels, channels), BF16),
        sds((3 * channels, channels), BF16),
        sds((n, 3 * head_dim, pixels), BF16),
        sds((n, head_dim, pixels), BF16),
        sds((n, tokens, 2 * head_dim), BF16),
        sds((items, n, tokens, text_width // n), BF16),
        sds((3, 8, channels), F32),
        sds((1, 2 * channels), F32),
    )
    v = pltpu.VMEM
    scratch = [
        v(padded, BF16),
        v(padded, BF16),
        v(text.shape, BF16),
        v(w1.shape, BF16),
        v(w2.shape, BF16),
        v(embed_w.shape, BF16),
        v(text_w.shape, BF16),
        v(qkv_w.shape, BF16),
        v(proj_w.shape, BF16),
        v(padded, F32),
        v(padded, F32),
        v(padded, BF16),
        v(padded, BF16),
        v((pixels, channels), BF16),
        v((3 * channels, channels), BF16),
        v((n, 3 * head_dim, pixels), BF16),
        v((n, head_dim, pixels), BF16),
        v((n, tokens, 2 * head_dim), BF16),
        v((n, tokens, text_width // n), BF16),
        v((rows_dev + 2, width, 3 * channels), BF16),
        v((pixels, channels), F32),
        v((3, 8, channels), F32),
        v((3, n, 8, channels), F32),
        DMA((24,)),
        DMA((3, n)),
        DMA((3, n)),
        DMA((4, 2)),
        DMA((4, 2)),
        DMA((4, n)),
        DMA((4, n)),
        DMA((3, items)),
        DMA((3, items)),
    ]
    return pl.pallas_call(
        functools.partial(forward_kernel, items, n),
        out_shape=outs,
        in_specs=[SCALARS] + [ANYWHERE] * 3 + [WHOLE] * 4 + [ANYWHERE] * 6,
        out_specs=(ANYWHERE,) * 11 + (WHOLE,) * 2,
        scratch_shapes=scratch,
        compiler_params=pltpu.CompilerParams(
            collective_id=identity, has_side_effects=True, vmem_limit_bytes=56 << 20
        ),
        cost_estimate=pl.CostEstimate(
            flops=40 * pixels * channels * channels, bytes_accessed=60 << 20, transcendentals=0
        ),
        name="forward",
    )(info, image, cot, text, embed, *gains, *weights)


def own_shards(
    info, image, embed, text, gain1, conv1_w, embed_w, gain2, conv2_w, gain3, qkv_w, text_w, proj_w,
    cotangent, image_window,
):
    _, rows_dev, width, channels = image.shape
    items, parts = lax.axis_size("items"), lax.axis_size("rows")
    me = lax.axis_index("rows")
    head_dim = channels // HEADS
    pixels = rows_dev * width
    tokens = text.shape[1]
    share = channels // parts
    embed_float = embed.astype(F32)
    embed_low = jax.nn.silu(embed_float).astype(BF16)
    (first, middle, cot, hidden_all, second_all, attn_flat, qkv_turned, qkv_pair, go_pair, text_pair, text_cols,
     stats, shifts) = forward_call(
        info,
        image[0],
        cotangent[0],
        text[0],
        embed,
        (gain1, gain2, gain3),
        (
            conv1_w.reshape(3, 3 * channels, channels),
            conv2_w.reshape(3, 3 * channels, channels),
            embed_w,
            text_w,
            qkv_w,
            proj_w,
        ),
        0,
    )
    stats1, stats2, stats3 = stats[0:1], stats[1:2], stats[2:3]
    attended, qkv_grad_pair, text_grad_pair = attention(
        info[:, :2], qkv_pair, text_pair.reshape(parts * tokens, 2 * head_dim), go_pair, width
    )

    def swap(values):
        return lax.all_to_all(values, "rows", split_axis=0, concat_axis=0, tiled=True)

    qkv_back = swap(qkv_grad_pair)
    heads_out = swap(attended)
    mid = middle[None, 1 : rows_dev + 1]
    attn_grad, sums = unproject(info, mid, stats3, qkv_back, qkv_turned)
    stats4, grad_above, grad_below, text_back = exchange(sums, (attn_grad,), 3, (text_grad_pair,))
    text_all = lax.all_gather(text_back[None], "items", axis=0, tiled=True)
    proj_shaped = proj_w.reshape(HEADS, head_dim, channels)
    grad_proj = (cotangent.astype(F32) * image_window).astype(BF16).reshape(pixels, channels)
    proj_grad = jnp.einsum("pc,hdp->chd", grad_proj, heads_out, preferred_element_type=F32)
    qkv_grad = jnp.einsum(
        "hwdp,pc->hdwc",
        qkv_back.reshape(HEADS, 3, head_dim, pixels),
        attn_flat,
        preferred_element_type=F32,
    )
    side = jnp.concatenate(
        [
            qkv_grad.astype(BF16).reshape(channels, 3 * channels),
            proj_grad.astype(BF16).reshape(channels, channels),
        ],
        axis=1,
    )
    side = lax.psum_scatter(side, "rows", scatter_dimension=0, tiled=True)
    full = jax.ShapeDtypeStruct(image.shape, F32)
    summed = jax.ShapeDtypeStruct((1, 8, channels), F32)
    padded = jax.ShapeDtypeStruct((1, rows_dev + 2, width, channels), BF16)
    own_first = first[None, 1 : rows_dev + 1]
    last = rows_dev + 1
    grad_middle, moved_grad, sums, conv2_grad = conv_call(
        back2_kernel,
        info,
        (attn_grad, grad_above, grad_below, mid, middle[None, :1], middle[None, last:], cotangent,
         cot[None, :1], cot[None, last:], stats3, stats4, gain3, own_first, stats2, gain2, shifts),
        conv2_w,
        (full, full, summed, padded),
        True,
    )
    stats5, moved_above, moved_below = exchange(sums, (moved_grad,), 4)
    pre_grad, sums, conv1_grad = conv_call(
        back1_kernel,
        info,
        (moved_grad, moved_above, moved_below, own_first, first[None, :1], first[None, last:], stats2,
         stats5, gain2, shifts, image, stats1, gain1),
        conv1_w,
        (full, summed, padded),
        True,
    )
    (stats6,) = exchange(sums, (), 5)
    image_grad = finish(info, pre_grad, stats6, image, stats1, gain1, grad_middle)
    projected = jnp.einsum("hdp,hdc->pc", heads_out, proj_shaped, preferred_element_type=F32)
    output = (mid + projected.reshape(image.shape) * image_window).astype(BF16)
    grad_shifts = jnp.concatenate([stats5[:, 1] * gain2, stats5[:, 0]], axis=1).astype(BF16)
    gains = jnp.concatenate(
        [stats6[:, 1], stats5[:, 1] * (1.0 + shifts[:, :channels]), stats4[:, 1]], axis=0
    )
    vector = jnp.concatenate(
        [
            gains,
            grad_shifts.astype(F32).reshape(2, channels),
            embed_low.astype(F32).reshape(-1, channels),
        ],
        axis=0,
    )
    filled = vector.shape[0]
    vector = jnp.pad(vector, ((0, -filled % 8), (0, 0)))
    (conv2_total,) = reduce_weight(conv2_grad, second_all, 6)
    conv1_total, side, vectors = reduce_weight(conv1_grad, hidden_all, 7, side, vector)
    own_text = lax.dynamic_slice_in_dim(text_all, lax.axis_index("items"), 1, 0)
    own_text = lax.dynamic_slice_in_dim(own_text[0], me * tokens, tokens, 2)
    text_shaped = text_w.reshape(text_w.shape[0], HEADS, 2 * head_dim)
    text_grad = jnp.einsum("hkt,chk->tc", own_text, text_shaped, preferred_element_type=F32)
    text_w_grad = jnp.einsum(
        "gtc,ghkt->chk",
        text_cols.reshape(items, parts * tokens, text.shape[2] // parts),
        text_all,
        preferred_element_type=F32,
    )
    embed_grad = jnp.einsum(
        "ik,ck->ic", grad_shifts, embed_w, preferred_element_type=F32
    ) * silu_slope(embed_float)
    all_shifts = vectors[:, 3:5].reshape(items, 2 * channels).astype(BF16)
    all_embed = vectors[:, 5:filled].reshape(items, embed.shape[1]).astype(BF16)
    embed_share = embed_w.shape[0] // parts
    embed_rows = lax.dynamic_slice_in_dim(all_embed, me * embed_share, embed_share, 1)
    embed_w_grad = jnp.einsum("ic,ik->ck", embed_rows, all_shifts, preferred_element_type=F32)
    gains = jnp.sum(vectors[:, :3], axis=0)
    gains = lax.dynamic_slice_in_dim(gains, me * share, share, 1)
    qkv_total = side[:, : 3 * channels].reshape(head_dim, 3, channels)
    qkv_total = jnp.transpose(qkv_total, (2, 1, 0)).reshape(channels, 3 * share)
    return (
        output,
        image_grad,
        embed_grad,
        text_grad[None],
        gains[0],
        conv1_total.reshape(3, 3, channels, share),
        embed_w_grad,
        gains[1],
        conv2_total.reshape(3, 3, channels, share),
        gains[2],
        qkv_total,
        text_w_grad.reshape(-1, 2 * channels),
        side[:, 3 * channels :].T,
    )


def shards(
    image, embed, text, extent, first_norm_gain1, conv1_w, embed_w, second_norm_gain2, conv2_w,
    attention_norm_gain, qkv_w, text_w, proj_w, cotangent,
):
    images, rows_dev, width, channels = image.shape
    parts = lax.axis_size("rows")
    me = lax.axis_index("rows")
    pairs = images * HEADS // parts
    head_dim = channels // HEADS
    pixels = rows_dev * width
    group = max(1, 512 // pixels)
    span = group * pixels
    chunks = parts // group
    tokens = text.shape[1]
    first_row = jnp.full((images, 1), me * rows_dev, jnp.int32)
    info = jnp.concatenate([extent, first_row], axis=1)
    gain1 = first_norm_gain1.reshape(1, channels)
    gain2 = second_norm_gain2.reshape(1, channels)
    gain3 = attention_norm_gain.reshape(1, channels)
    rowpos = me * rows_dev + jnp.arange(rows_dev, dtype=jnp.int32)
    colpos = jnp.arange(width, dtype=jnp.int32)
    inside = (rowpos[None, :, None] < extent[:, 0, None, None]) & (
        colpos[None, None, :] < extent[:, 1, None, None]
    )
    image_window = inside.astype(F32)[..., None]

    items = lax.axis_size("items")
    own_path = (
        images == 1
        and parts == HEADS
        and channels % (16 * items * parts) == 0
        and pixels % 512 == 0
        and tokens % 16 == 0
        and text.shape[2] % (128 * parts) == 0
    )
    if own_path:
        return own_shards(
            info, image, embed, text, gain1, conv1_w, embed_w, gain2, conv2_w, gain3, qkv_w, text_w,
            proj_w, cotangent, image_window,
        )

    embed_float = embed.astype(F32)
    embed_low = jax.nn.silu(embed_float).astype(BF16)
    shifts = jnp.dot(embed_low, embed_w, preferred_element_type=F32)
    qkv_turned = qkv_w.T
    proj_shaped = proj_w.reshape(HEADS, head_dim, channels)

    start = image.astype(F32) * image_window
    zeros = jnp.zeros((images, 6, channels), F32)
    stats0 = jnp.concatenate(
        [
            jnp.sum(start, axis=(1, 2))[:, None],
            jnp.sum(start * start, axis=(1, 2))[:, None],
            zeros,
        ],
        axis=1,
    )
    stats1, image_above, image_below, cot_above, cot_below = exchange(
        stats0, (image, cotangent), 0
    )
    full = jax.ShapeDtypeStruct(image.shape, F32)
    sums = jax.ShapeDtypeStruct((images, 8, channels), F32)
    padded = jax.ShapeDtypeStruct((images, rows_dev + 2, width, channels), BF16)
    first, stats, hidden = conv_call(
        conv1_kernel,
        info,
        (image, image_above, image_below, stats1, gain1),
        conv1_w,
        (full, sums, padded),
        False,
    )
    stats2, first_above, first_below, all_text = exchange(stats, (first,), 1, (text,))
    gathered_text = jnp.moveaxis(all_text, 0, 1).reshape(images, parts * tokens, text.shape[2])
    text_share = text.shape[2] // parts
    text_cols = lax.dynamic_slice_in_dim(gathered_text, me * text_share, text_share, 2)
    text_cols = lax.all_gather(text_cols, "items", axis=0, tiled=True)
    middle, stats, second = conv_call(
        conv2_kernel,
        info,
        (first, first_above, first_below, stats2, gain2, shifts, image),
        conv2_w,
        (full, sums, padded),
        False,
    )
    stats3, mid_above, mid_below = exchange(stats, (middle,), 2)
    attn_flat, qkv_pix = project(info, middle, stats3, gain3, qkv_turned)

    def to_pairs(values):
        wide = values.shape[1]
        moved = lax.all_to_all(values, "rows", split_axis=0, concat_axis=0, tiled=True)
        moved = moved.reshape(chunks, group, pairs, wide, pixels)
        return jnp.transpose(moved, (2, 0, 3, 1, 4)).reshape(pairs, chunks, wide, span)

    def from_pairs(values):
        wide = values.shape[2]
        moved = values.reshape(pairs, chunks, wide, group, pixels)
        moved = jnp.transpose(moved, (1, 3, 0, 2, 4)).reshape(parts * pairs, wide, pixels)
        return lax.all_to_all(moved, "rows", split_axis=0, concat_axis=0, tiled=True)

    qkv_pair = to_pairs(qkv_pix)
    grad_proj = (cotangent.astype(F32) * image_window).astype(BF16).reshape(images, pixels, channels)
    grad_heads = jnp.einsum(
        "ipc,hdc->ihdp", grad_proj, proj_shaped, preferred_element_type=F32
    ).astype(BF16)
    grad_pair = to_pairs(grad_heads.reshape(images * HEADS, head_dim, pixels))
    pair_results = []
    for p in range(pairs):
        pair = me * pairs + p
        item, head = pair // HEADS, pair % HEADS
        weight = lax.dynamic_slice_in_dim(text_w, head * 2 * head_dim, 2 * head_dim, 1)
        own = lax.dynamic_index_in_dim(gathered_text, item, 0, False)
        text_pair = jnp.dot(own, weight, preferred_element_type=F32).astype(BF16)
        pair_extent = lax.dynamic_slice_in_dim(extent, item, 1, 0)
        pair_results.append(attention(pair_extent, qkv_pair[p], text_pair, grad_pair[p], width))
    attended, qkv_grad_pair, text_grad_pair = (jnp.stack(r) for r in zip(*pair_results))
    qkv_back = from_pairs(qkv_grad_pair)
    heads_out = from_pairs(attended).reshape(images, HEADS, head_dim, pixels)

    attn_grad, stats = unproject(info, middle, stats3, qkv_back, qkv_turned)
    stats4, grad_above, grad_below, text_back = exchange(stats, (attn_grad,), 3, (text_grad_pair,))
    text_back = text_back.reshape(images, HEADS, 2 * head_dim, parts * tokens)
    text_all = lax.all_gather(text_back, "items", axis=0, tiled=True)
    proj_grad = jnp.einsum("ipc,ihdp->chd", grad_proj, heads_out, preferred_element_type=F32)
    qkv_grad = jnp.einsum(
        "ihwdp,ipc->hdwc",
        qkv_back.reshape(images, HEADS, 3, head_dim, pixels),
        attn_flat,
        preferred_element_type=F32,
    )
    grad_middle, moved_grad, stats, conv2_grad = conv_call(
        back2_kernel,
        info,
        (attn_grad, grad_above, grad_below, middle, mid_above, mid_below, cotangent, cot_above,
         cot_below, stats3, stats4, gain3, first, stats2, gain2, shifts),
        conv2_w,
        (full, full, sums, padded),
        True,
    )
    stats5, moved_above, moved_below = exchange(stats, (moved_grad,), 4)
    pre_grad, stats, conv1_grad = conv_call(
        back1_kernel,
        info,
        (moved_grad, moved_above, moved_below, first, first_above, first_below, stats2, stats5,
         gain2, shifts, image, stats1, gain1),
        conv1_w,
        (full, sums, padded),
        True,
    )
    (stats6,) = exchange(stats, (), 5)
    image_grad = finish(info, pre_grad, stats6, image, stats1, gain1, grad_middle)

    projected = jnp.einsum(
        "ihdp,hdc->ipc", heads_out, proj_shaped, preferred_element_type=F32
    ).reshape(image.shape)
    output = (middle + projected * image_window).astype(BF16)
    own_text = lax.dynamic_slice_in_dim(text_back, me * tokens, tokens, 3)
    text_shaped = text_w.reshape(text_w.shape[0], HEADS, 2 * head_dim)
    text_grad = jnp.einsum("ihkt,chk->itc", own_text, text_shaped, preferred_element_type=F32)
    text_w_grad = jnp.einsum(
        "gtc,ghkt->chk", text_cols, text_all, preferred_element_type=F32
    ).reshape(text_share, 2 * channels)
    scale_sum = stats5[:, 1] * gain2
    grad_shifts = jnp.concatenate([scale_sum, stats5[:, 0]], axis=1).astype(BF16)
    embed_grad = jnp.einsum(
        "ik,ck->ic", grad_shifts, embed_w, preferred_element_type=F32
    ) * silu_slope(embed_float)
    embed_share = embed_w.shape[0] // parts
    gains = jnp.stack(
        [
            jnp.sum(stats6[:, 1], axis=0),
            jnp.sum(stats5[:, 1] * (1.0 + shifts[:, :channels]), axis=0),
            jnp.sum(stats4[:, 1], axis=0),
        ]
    )
    share = channels // parts
    def total(values):
        return lax.psum(
            lax.psum_scatter(values.astype(BF16), "rows", scatter_dimension=0, tiled=True),
            "items",
        ).astype(F32)

    def kernel_total(values):
        return total(values).T.reshape(3, 3, channels, share)

    conv1_total = kernel_total(weight_grad(conv1_grad, hidden))
    conv2_total = kernel_total(weight_grad(conv2_grad, second))
    by_head = jnp.swapaxes(qkv_grad, 1, 2).reshape(3 * channels, channels)
    qkv_total = total(by_head).T
    proj_total = total(proj_grad.reshape(channels, channels)).T
    gains = lax.psum(gains, "items")
    all_shifts = lax.all_gather(grad_shifts, "items", axis=0, tiled=True)
    embed_rows = lax.dynamic_slice_in_dim(embed_low, me * embed_share, embed_share, 1)
    embed_rows = lax.all_gather(embed_rows, "items", axis=0, tiled=True)
    embed_w_grad = jnp.einsum("ic,ik->ck", embed_rows, all_shifts, preferred_element_type=F32)
    gains = lax.dynamic_slice_in_dim(gains, me * share, share, 1)
    return (
        output,
        image_grad,
        embed_grad,
        text_grad,
        gains[0],
        conv1_total,
        embed_w_grad,
        gains[1],
        conv2_total,
        gains[2],
        qkv_total,
        text_w_grad,
        proj_total,
    )


def solution(mesh):
    in_specs = (
        P("items", "rows", None, None),
        P("items", None),
        P("items", "rows", None),
        P("items", None),
        P(),
        P(),
        P(),
        P(),
        P(),
        P(),
        P(),
        P(),
        P(),
        P("items", "rows", None, None),
    )
    out_specs = (
        P("items", "rows", None, None),
        P("items", "rows", None, None),
        P("items", None),
        P("items", "rows", None),
        P("rows"),
        P(None, None, None, "rows"),
        P("rows", None),
        P("rows"),
        P(None, None, None, "rows"),
        P("rows"),
        P(None, "rows"),
        P("rows", None),
        P(None, "rows"),
    )
    return jax.shard_map(shards, mesh=mesh, in_specs=in_specs, out_specs=out_specs, check_vma=False)
```

```python
import functools

import jax
import jax.numpy as jnp
from jax import lax
from jax.experimental import pallas as pl
from jax.experimental.pallas import tpu as pltpu
from jax.sharding import PartitionSpec as P

GROUPS = 32
HEADS = 8
F32, BF16 = jnp.float32, jnp.bfloat16
NEG = -1e30


def dot(a, b, ca, cb):
    return lax.dot_general(a, b, (((ca,), (cb,)), ((), ())), preferred_element_type=F32)

def attention_kernel(width, step, bq, ext_ref, qkv_ref, text_ref, go_ref, out_ref, dqkv_ref, dtext_ref,
                     kn, vn, kt, vt, s0, s1, e0, e1, dkt, dvt):
    scores, raised = (s0, s1), (e0, e1)
    chunks, _, span = qkv_ref.shape
    tlen = text_ref.shape[0]
    d = go_ref.shape[1]
    pix = chunks * span
    keys = pix + tlen
    steps = keys // step
    rows_ok, cols_ok = ext_ref[0, 0], ext_ref[0, 1]
    def stage(c, carry):
        base = pl.multiple_of(c * span, span)
        pos = base + lax.broadcasted_iota(jnp.int32, (16, span), 1)
        row = lax.broadcasted_iota(jnp.int32, (16, span), 0)
        ok = (pos // width < rows_ok) & (pos % width < cols_ok)
        extra = jnp.where((row == 0) & jnp.logical_not(ok), NEG, 0.0)
        k = qkv_ref[c, d:2 * d, :]
        v = qkv_ref[c, 2 * d:, :]
        kt[:, pl.ds(base, span)] = k
        vt[:, pl.ds(base, span)] = v
        rest = jnp.zeros((128 - d - 16, span), F32)
        ka = jnp.concatenate([k.astype(F32), extra, rest], axis=0)
        va = jnp.concatenate([v.astype(F32), jnp.where(row < 3, 1.0, 0.0), rest], axis=0)
        kn[pl.ds(base, span), :] = ka.T.astype(BF16)
        vn[pl.ds(base, span), :] = va.T.astype(BF16)
        return carry
    lax.fori_loop(0, chunks, stage, 0)
    tk = text_ref[:, :d].astype(F32)
    tv = text_ref[:, d:].astype(F32)
    kt[:, pix:] = tk.T.astype(BF16)
    vt[:, pix:] = tv.T.astype(BF16)
    lanes = lax.broadcasted_iota(jnp.int32, (tlen, 128 - d), 1)
    kn[pix:, :] = jnp.concatenate([tk, jnp.zeros((tlen, 128 - d), F32)], axis=1).astype(BF16)
    vn[pix:, :] = jnp.concatenate([tv, jnp.where(lanes < 3, 1.0, 0.0)], axis=1).astype(BF16)
    dkt[...] = jnp.zeros_like(dkt)
    dvt[...] = jnp.zeros_like(dvt)

    low_peak = jnp.full((8, bq), -3e38, F32)

    def q_aug(c, half):
        q = qkv_ref[c, :d, half * bq:(half + 1) * bq].astype(F32) * (d ** -0.5)
        r = lax.broadcasted_iota(jnp.int32, (128 - d, bq), 0)
        return jnp.concatenate([q, jnp.where(r == 0, 1.0, 0.0)], axis=0).astype(BF16)

    def run(score, exp, back):
        def body(j, carry):
            pk, total, acc, dq = carry
            at = pl.ds(pl.multiple_of(j * step, step), step)
            if score:
                slot, qa = score
                s = dot(kn[at, :], qa, 1, 0)
                scores[slot][at, :] = s
                pk = jnp.maximum(pk, jnp.max(s.reshape(step // 8, 8, bq), axis=0))
            if exp:
                slot, peak = exp
                e = jnp.exp(scores[slot][at, :] - peak)
                total = total + jnp.sum(e.reshape(step // 8, 8, bq), axis=0)
                low = e.astype(BF16)
                raised[slot][at, :] = low
                acc = acc + dot(vt[:, at], low, 1, 0)
            if back:
                slot, goa, gs, q = back
                dp = dot(vn[at, :], goa, 1, 0)
                e = raised[slot][at, :]
                ds = (e.astype(F32) * dp).astype(BF16)
                dvt[:, at] += dot(gs, e, 1, 1)
                dkt[:, at] += dot(q, ds, 1, 1)
                dq = dq + dot(kt[:, at], ds, 1, 0)
            return pk, total, acc, dq
        init = (low_peak, jnp.zeros((8, bq), F32), jnp.zeros((d, bq), F32), jnp.zeros((d, bq), F32))
        return lax.fori_loop(0, steps, body, init)

    def finish_exp(c, half, total, acc):
        inv = 1.0 / jnp.sum(total, axis=0, keepdims=True)
        o = acc * inv
        cols = slice(half * bq, (half + 1) * bq)
        out_ref[c, :, cols] = o.astype(BF16)
        go = go_ref[c, :, cols].astype(F32)
        nd = -jnp.sum(go * o, axis=0, keepdims=True) * inv
        gs = go * inv
        hi = nd.astype(BF16).astype(F32)
        mid = (nd - hi).astype(BF16).astype(F32)
        lo = nd - hi - mid
        r = lax.broadcasted_iota(jnp.int32, (16, bq), 0)
        extra = jnp.where(r == 0, hi, jnp.where(r == 1, mid, jnp.where(r == 2, lo, 0.0)))
        goa = jnp.concatenate([gs, extra, jnp.zeros((128 - d - 16, bq), F32)], axis=0).astype(BF16)
        return goa

    def put_dq(c, half, dq):
        dqkv_ref[c, :d, half * bq:(half + 1) * bq] = (dq * (d ** -0.5)).astype(BF16)

    def top(pk):
        return jnp.max(pk, axis=0, keepdims=True)

    def q_of(c, half):
        return qkv_ref[c, :d, half * bq:(half + 1) * bq]

    pk, _, _, _ = run((0, q_aug(0, 0)), None, None)
    pk, total, acc, _ = run((1, q_aug(0, 1)), (0, top(pk)), None)
    goa = finish_exp(0, 0, total, acc)

    def two(h, carry):
        pk, goa = carry
        pk2, total, acc, dq = run((0, q_aug(h + 1, 0)), (1, top(pk)), (0, goa, goa[:d], q_of(h, 0)))
        put_dq(h, 0, dq)
        goa = finish_exp(h, 1, total, acc)
        pk3, total, acc, dq = run((1, q_aug(h + 1, 1)), (0, top(pk2)), (1, goa, goa[:d], q_of(h, 1)))
        put_dq(h, 1, dq)
        return pk3, finish_exp(h + 1, 0, total, acc)
    pk, goa = lax.fori_loop(0, chunks - 1, two, (pk, goa))
    last = chunks - 1
    _, total, acc, dq = run(None, (1, top(pk)), (0, goa, goa[:d], q_of(last, 0)))
    put_dq(last, 0, dq)
    goa = finish_exp(last, 1, total, acc)
    _, _, _, dq = run(None, None, (1, goa, goa[:d], q_of(last, 1)))
    put_dq(last, 1, dq)

    def finish(c, carry):
        at = pl.ds(pl.multiple_of(c * span, span), span)
        dqkv_ref[c, d:2 * d, :] = (dkt[:, at] * (d ** -0.5)).astype(BF16)
        dqkv_ref[c, 2 * d:, :] = dvt[:, at].astype(BF16)
        return carry
    lax.fori_loop(0, chunks, finish, 0)
    dtext_ref[:, :d] = (dkt[:, pix:] * (d ** -0.5)).T.astype(BF16)
    dtext_ref[:, d:] = dvt[:, pix:].T.astype(BF16)

def attention(ext, qkv, text, go, width):
    chunks, wide, span = qkv.shape
    d = wide // 3
    tlen = text.shape[0]
    keys = chunks * span + tlen
    bq = span // 2
    lanes = keys // 128
    step = 128 * max(n for n in range(1, 12) if lanes % n == 0)
    vm = pl.BlockSpec(memory_space=pltpu.VMEM)
    flops = 2 * 6 * chunks * span * keys * d
    return pl.pallas_call(
        functools.partial(attention_kernel, width, step, bq),
        out_shape=(
            jax.ShapeDtypeStruct(go.shape, BF16),
            jax.ShapeDtypeStruct(qkv.shape, BF16),
            jax.ShapeDtypeStruct((tlen, 2 * d), BF16),
        ),
        in_specs=[pl.BlockSpec(memory_space=pltpu.SMEM), vm, vm, vm],
        out_specs=(vm, vm, vm),
        scratch_shapes=[
            pltpu.VMEM((keys, 128), BF16),
            pltpu.VMEM((keys, 128), BF16),
            pltpu.VMEM((d, keys), BF16),
            pltpu.VMEM((d, keys), BF16),
            pltpu.VMEM((keys, bq), F32),
            pltpu.VMEM((keys, bq), F32),
            pltpu.VMEM((keys, bq), BF16),
            pltpu.VMEM((keys, bq), BF16),
            pltpu.VMEM((d, keys), F32),
            pltpu.VMEM((d, keys), F32),
        ],
        compiler_params=pltpu.CompilerParams(vmem_limit_bytes=56 << 20),
        cost_estimate=pl.CostEstimate(
            flops=4 * flops, bytes_accessed=16 * chunks * span * d, transcendentals=chunks * span * keys
        ),
    )(ext, qkv, text, go)


MESH = pl.DeviceIdType.MESH
EPS = 1e-05
WHOLE = pl.BlockSpec(memory_space=pltpu.VMEM)
SCALARS = pl.BlockSpec(memory_space=pltpu.SMEM)
ANYWHERE = pl.BlockSpec(memory_space=pl.ANY)


def exchange_kernel(n, count, gathers, *refs):
    inputs, refs = refs[: 1 + count + gathers], refs[1 + count + gathers :]
    outputs, refs = refs[: 1 + 2 * count + gathers], refs[1 + 2 * count + gathers :]
    stats_ref, rows, given = inputs[0], inputs[1 : 1 + count], inputs[1 + count :]
    total_ref, outs, gathered = outputs[0], outputs[1 : 1 + 2 * count], outputs[1 + 2 * count :]
    slots, lands = refs[0], refs[1 : 1 + 2 * count]
    send, recv, row_send, row_recv, own = refs[1 + 2 * count :]
    me = lax.axis_index("rows")
    barrier = pltpu.get_barrier_semaphore()

    def greet(k, carry):
        pl.semaphore_signal(
            barrier, inc=1, device_id={"rows": lax.rem(me + k, n)}, device_id_type=MESH
        )
        return carry

    lax.fori_loop(1, n, greet, 0)
    slots[me] = stats_ref[...]
    pl.semaphore_wait(barrier, n - 1)
    shared = [(stats_ref, slots)] + list(zip(given, gathered))

    def share(j, k):
        return pltpu.make_async_remote_copy(
            src_ref=shared[j][0],
            dst_ref=shared[j][1].at[me],
            send_sem=send.at[j, k],
            recv_sem=recv.at[j, k],
            device_id={"rows": lax.rem(me + k, n)},
            device_id_type=MESH,
        )

    def start(k, carry):
        share(0, k).start()
        return carry

    lax.fori_loop(1, n, start, 0)

    def row_copy(j, side):
        last = rows[j].shape[1] - 1
        at = last if side == 0 else 0
        return pltpu.make_async_remote_copy(
            src_ref=rows[j].at[:, at : at + 1],
            dst_ref=lands[2 * j + side],
            send_sem=row_send.at[2 * j + side],
            recv_sem=row_recv.at[2 * j + side],
            device_id={"rows": me + 1 if side == 0 else me - 1},
            device_id_type=MESH,
        )

    for j in range(count):

        @pl.when(me < n - 1)
        def _():
            row_copy(j, 0).start()

        @pl.when(me > 0)
        def _():
            row_copy(j, 1).start()

    for j in range(gathers):

        def start_given(k, carry):
            share(1 + j, k).start()
            return carry

        lax.fori_loop(1, n, start_given, 0)
        pltpu.make_async_copy(given[j], gathered[j].at[me], own.at[j]).start()

    def finish(k, carry):
        share(0, k).wait()
        return carry

    lax.fori_loop(1, n, finish, 0)
    total_ref[...] = lax.fori_loop(1, n, lambda k, s: s + slots[k], slots[0])
    for j in range(count):

        @pl.when(me > 0)
        def _():
            row_copy(j, 0).wait_recv()
            outs[2 * j][...] = lands[2 * j][...]

        @pl.when(me == 0)
        def _():
            outs[2 * j][...] = jnp.zeros_like(outs[2 * j])

        @pl.when(me < n - 1)
        def _():
            row_copy(j, 1).wait_recv()
            outs[2 * j + 1][...] = lands[2 * j + 1][...]
            row_copy(j, 0).wait_send()

        @pl.when(me == n - 1)
        def _():
            outs[2 * j + 1][...] = jnp.zeros_like(outs[2 * j + 1])

        @pl.when(me > 0)
        def _():
            row_copy(j, 1).wait_send()

    for j in range(gathers):

        def finish_given(k, carry):
            share(1 + j, k).wait()
            return carry

        lax.fori_loop(1, n, finish_given, 0)
        pltpu.make_async_copy(given[j], gathered[j].at[me], own.at[j]).wait()


def exchange(stats, rows, identity, given=()):
    n = lax.axis_size("rows")
    edge = []
    for array in rows:
        edge += [jax.ShapeDtypeStruct(array.shape[:1] + (1,) + array.shape[2:], array.dtype)] * 2
    whole = [jax.ShapeDtypeStruct((n,) + array.shape, array.dtype) for array in given]
    count, gathers = len(rows), len(given)
    nbytes = 4 * stats.size * n + sum(2 * e.size * e.dtype.itemsize for e in (*edge, *whole))
    return pl.pallas_call(
        functools.partial(exchange_kernel, n, count, gathers),
        out_shape=(jax.ShapeDtypeStruct(stats.shape, F32), *edge, *whole),
        in_specs=[WHOLE] + [ANYWHERE] * (count + gathers),
        out_specs=(WHOLE,) * (1 + 2 * count) + (ANYWHERE,) * gathers,
        scratch_shapes=[
            pltpu.VMEM((n,) + stats.shape, F32),
            *[pltpu.VMEM(e.shape, e.dtype) for e in edge],
            pltpu.SemaphoreType.DMA((1 + gathers, n)),
            pltpu.SemaphoreType.DMA((1 + gathers, n)),
            pltpu.SemaphoreType.DMA((max(1, 2 * count),)),
            pltpu.SemaphoreType.DMA((max(1, 2 * count),)),
            pltpu.SemaphoreType.DMA((max(1, gathers),)),
        ],
        compiler_params=pltpu.CompilerParams(collective_id=identity, has_side_effects=True),
        cost_estimate=pl.CostEstimate(
            flops=6_000_000_000, bytes_accessed=nbytes, transcendentals=0
        ),
        name=f"exchange{identity}",
    )(stats, *rows, *given)


def group_sums(rows):
    channels = rows.shape[1]
    size = channels // GROUPS
    one = lax.broadcasted_iota(jnp.int32, (channels, channels), 0) // size
    two = lax.broadcasted_iota(jnp.int32, (channels, channels), 1) // size
    same = jnp.where(one == two, 1.0, 0.0).astype(BF16)
    high = rows.astype(BF16)
    rest = rows - high.astype(F32)
    mid = rest.astype(BF16)
    tail = (rest - mid.astype(F32)).astype(BF16)
    return dot(high, same, 1, 0) + dot(mid, same, 1, 0) + dot(tail, same, 1, 0)


def image_count(info, i, channels):
    return (info[i, 0] * info[i, 1]).astype(F32) * (channels // GROUPS)


def norm_of(stats, count):
    sums = group_sums(stats)
    average = sums[0:1] / count
    square = sums[1:2] / count
    return average, lax.rsqrt(square - average * average + EPS)


def means_of(stats, weight, count):
    sums = group_sums(stats * weight)
    return sums[0:1] / count, sums[1:2] / count


def window(info, i, row, shape):
    ok = (row >= 0) & (row < info[i, 0])
    limit = jnp.where(ok, info[i, 1], 0)
    return jnp.where(lax.broadcasted_iota(jnp.int32, shape, 0) < limit, 1.0, 0.0)


def padded_row(center, above, below, i, r):
    if r == 0:
        return above[i, 0]
    if r == center.shape[1] + 1:
        return below[i, 0]
    return center[i, r - 1]


def put_shifted(out, i, r, value, plain=None):
    width, channels = value.shape
    column = lax.broadcasted_iota(jnp.int32, value.shape, 0)
    left = jnp.where(column == 0, 0.0, pltpu.roll(value, 1, 0))
    right = jnp.where(column == width - 1, 0.0, pltpu.roll(value, width - 1, 0))
    out[i, r, :, :channels] = left.astype(BF16)
    low = value.astype(BF16)
    out[i, r, :, channels : 2 * channels] = low
    if plain is not None:
        plain[i, r] = low
    out[i, r, :, 2 * channels :] = right.astype(BF16)


def sigmoid(v):
    return 1.0 / (1.0 + jnp.exp(-v))


def silu_slope(v):
    s = sigmoid(v)
    return s * (1.0 + v * (1.0 - s))


def put_stats(stats_ref, i, first, second):
    channels = first.shape[1]
    one = jnp.sum(first, axis=0, keepdims=True)
    two = jnp.sum(second, axis=0, keepdims=True)
    row = lax.broadcasted_iota(jnp.int32, (8, channels), 0)
    stats_ref[i] = jnp.where(row == 0, one, jnp.where(row == 1, two, 0.0))


def tap_rows(shifted, tap, images, rows_dev, width):
    block = shifted[:, pl.ds(tap, rows_dev)]
    return block.reshape(images * rows_dev * width, shifted.shape[3])


def conv1_kernel(info, image, above, below, stats, gain, weight, first, out_stats, hidden, acc, shifted):
    images, rows_dev, width, channels = image.shape
    tap = pl.program_id(0)
    base = info[0, 2]

    @pl.when(tap == 0)
    def _():
        for i in range(images):
            average, inverse = norm_of(stats[i], image_count(info, i, channels))
            for r in range(rows_dev + 2):
                inside = window(info, i, base + r - 1, (width, channels))
                start = padded_row(image, above, below, i, r).astype(F32) * inside
                value = (start - average) * inverse * inside * gain[...]
                put_shifted(shifted, i, r, value * sigmoid(value) * inside, hidden)

    part = dot(tap_rows(shifted, tap, images, rows_dev, width), weight[0], 1, 0)

    @pl.when(tap == 0)
    def _():
        acc[...] = part

    @pl.when(tap > 0)
    def _():
        acc[...] += part

    @pl.when(tap == 2)
    def _():
        for i in range(images):
            one = two = jnp.zeros((width, channels), F32)
            for r in range(rows_dev):
                inside = window(info, i, base + r, (width, channels))
                at = (i * rows_dev + r) * width
                value = acc[at : at + width] * inside
                first[i, r] = value
                one = one + value
                two = two + value * value
            put_stats(out_stats, i, one, two)


def moved_of(value, inside, average, inverse, gain, scale, shift):
    normal = (value - average) * inverse * inside
    return normal, normal * gain * (1.0 + scale) + shift


def conv2_kernel(
    info, first, above, below, stats, gain, shifts, image, weight, middle, out_stats, second, acc,
    shifted,
):
    images, rows_dev, width, channels = first.shape
    tap = pl.program_id(0)
    base = info[0, 2]

    @pl.when(tap == 0)
    def _():
        for i in range(images):
            average, inverse = norm_of(stats[i], image_count(info, i, channels))
            scale, shift = shifts[i : i + 1, :channels], shifts[i : i + 1, channels:]
            for r in range(rows_dev + 2):
                inside = window(info, i, base + r - 1, (width, channels))
                value = padded_row(first, above, below, i, r)
                _, moved = moved_of(value, inside, average, inverse, gain[...], scale, shift)
                put_shifted(shifted, i, r, moved * sigmoid(moved) * inside, second)

    part = dot(tap_rows(shifted, tap, images, rows_dev, width), weight[0], 1, 0)

    @pl.when(tap == 0)
    def _():
        acc[...] = part

    @pl.when(tap > 0)
    def _():
        acc[...] += part

    @pl.when(tap == 2)
    def _():
        for i in range(images):
            one = two = jnp.zeros((width, channels), F32)
            for r in range(rows_dev):
                inside = window(info, i, base + r, (width, channels))
                at = (i * rows_dev + r) * width
                value = (image[i, r].astype(F32) + acc[at : at + width]) * inside
                middle[i, r] = value
                one = one + value
                two = two + value * value
            put_stats(out_stats, i, one, two)


def dgrad(shifted, tap, weight, images, rows_dev, width):
    channels = weight.shape[2]
    lhs = tap_rows(shifted, tap, images, rows_dev, width)
    part = None
    for b in range(3):
        term = dot(
            lhs[:, b * channels : (b + 1) * channels],
            weight[0, (2 - b) * channels : (3 - b) * channels, :],
            1,
            1,
        )
        part = term if part is None else part + term
    return part


def back2_kernel(
    info, grad, grad_above, grad_below, middle, mid_above, mid_below, cot, cot_above, cot_below,
    mid_stats, grad_stats, attn_gain, first, first_stats, gain, shifts, weight,
    grad_middle, moved_grad, out_stats, plain, acc, shifted,
):
    images, rows_dev, width, channels = first.shape
    tap = pl.program_id(0)
    base = info[0, 2]

    @pl.when(tap == 0)
    def _():
        for i in range(images):
            count = image_count(info, i, channels)
            average, inverse = norm_of(mid_stats[i], count)
            mean, cross = means_of(grad_stats[i], attn_gain[...], count)
            for r in range(rows_dev + 2):
                inside = window(info, i, base + r - 1, (width, channels))
                normal = (padded_row(middle, mid_above, mid_below, i, r) - average) * inverse
                dx = padded_row(grad, grad_above, grad_below, i, r) * attn_gain[...]
                term = (dx - mean - normal * cross) * inverse * inside
                total = padded_row(cot, cot_above, cot_below, i, r).astype(F32) + term
                if 0 < r <= rows_dev:
                    grad_middle[i, r - 1] = total
                put_shifted(shifted, i, r, total * inside, plain)

    part = dgrad(shifted, tap, weight, images, rows_dev, width)

    @pl.when(tap == 0)
    def _():
        acc[...] = part

    @pl.when(tap > 0)
    def _():
        acc[...] += part

    @pl.when(tap == 2)
    def _():
        for i in range(images):
            average, inverse = norm_of(first_stats[i], image_count(info, i, channels))
            scale, shift = shifts[i : i + 1, :channels], shifts[i : i + 1, channels:]
            one = two = jnp.zeros((width, channels), F32)
            for r in range(rows_dev):
                inside = window(info, i, base + r, (width, channels))
                at = (i * rows_dev + r) * width
                normal, moved = moved_of(
                    first[i, r], inside, average, inverse, gain[...], scale, shift
                )
                value = acc[at : at + width] * inside * silu_slope(moved)
                moved_grad[i, r] = value
                one = one + value
                two = two + value * normal
            put_stats(out_stats, i, one, two)


def back1_kernel(
    info, grad, grad_above, grad_below, first, first_above, first_below, first_stats, grad_stats,
    gain, shifts, image, image_stats, first_gain, weight,
    pre_grad, out_stats, plain, acc, shifted,
):
    images, rows_dev, width, channels = first.shape
    tap = pl.program_id(0)
    base = info[0, 2]

    @pl.when(tap == 0)
    def _():
        for i in range(images):
            count = image_count(info, i, channels)
            average, inverse = norm_of(first_stats[i], count)
            factor = gain[...] * (1.0 + shifts[i : i + 1, :channels])
            mean, cross = means_of(grad_stats[i], factor, count)
            for r in range(rows_dev + 2):
                inside = window(info, i, base + r - 1, (width, channels))
                normal = (padded_row(first, first_above, first_below, i, r) - average) * inverse
                dx = padded_row(grad, grad_above, grad_below, i, r) * factor
                put_shifted(shifted, i, r, (dx - mean - normal * cross) * inverse * inside, plain)

    part = dgrad(shifted, tap, weight, images, rows_dev, width)

    @pl.when(tap == 0)
    def _():
        acc[...] = part

    @pl.when(tap > 0)
    def _():
        acc[...] += part

    @pl.when(tap == 2)
    def _():
        for i in range(images):
            average, inverse = norm_of(image_stats[i], image_count(info, i, channels))
            one = two = jnp.zeros((width, channels), F32)
            for r in range(rows_dev):
                inside = window(info, i, base + r, (width, channels))
                at = (i * rows_dev + r) * width
                normal = (image[i, r].astype(F32) - average) * inverse * inside
                slope = silu_slope(normal * first_gain[...])
                value = acc[at : at + width] * inside * slope
                pre_grad[i, r] = value
                one = one + value
                two = two + value * normal
            put_stats(out_stats, i, one, two)


def conv_call(kernel, info, inputs, weight, outs, flipped):
    images, rows_dev, width, channels = outs[0].shape

    def whole(shape):
        return pl.BlockSpec(shape, lambda tap: (0,) * len(shape))

    def tap_of(tap):
        return ((2 - tap) if flipped else tap, 0, 0)

    weight = weight.reshape(3, 3 * channels, channels)
    flops = 2 * 9 * images * rows_dev * width * channels * channels
    moved = sum(a.size * a.dtype.itemsize for a in (*inputs, weight, *outs))
    return pl.pallas_call(
        kernel,
        grid=(3,),
        out_shape=tuple(outs),
        in_specs=[SCALARS]
        + [whole(a.shape) for a in inputs]
        + [pl.BlockSpec((1, 3 * channels, channels), tap_of)],
        out_specs=tuple(whole(o.shape) for o in outs),
        scratch_shapes=[
            pltpu.VMEM((images * rows_dev * width, channels), F32),
            pltpu.VMEM((images, rows_dev + 2, width, 3 * channels), BF16),
        ],
        compiler_params=pltpu.CompilerParams(vmem_limit_bytes=48 << 20),
        cost_estimate=pl.CostEstimate(flops=flops, bytes_accessed=moved, transcendentals=0),
        name=kernel.__name__,
    )(info, *inputs, weight)


def weight_grad_kernel(grads, hidden, out, turned, shifted):
    images, padded, width, channels = hidden.shape
    rows_dev = padded - 2
    pixels = images * rows_dev * width
    tap = pl.program_id(0)

    @pl.when(tap == 0)
    def _():
        center = grads[:, 1 : rows_dev + 1]
        turned[...] = center.reshape(pixels, channels).astype(F32).T.astype(BF16)
        for i in range(images):
            for r in range(padded):
                put_shifted(shifted, i, r, hidden[i, r].astype(F32))

    column = pl.multiple_of((tap % 3) * channels, channels)
    rhs = shifted[:, pl.ds(tap // 3, rows_dev), :, pl.ds(column, channels)]
    out[...] = dot(turned[...], rhs.reshape(pixels, channels), 1, 0).astype(BF16)


def weight_grad(grads, hidden):
    images, padded, width, channels = hidden.shape
    pixels = images * (padded - 2) * width

    def whole(shape):
        return pl.BlockSpec(shape, lambda tap: (0,) * len(shape))

    return pl.pallas_call(
        weight_grad_kernel,
        grid=(9,),
        out_shape=jax.ShapeDtypeStruct((channels, 9 * channels), BF16),
        in_specs=[whole(grads.shape), whole(hidden.shape)],
        out_specs=pl.BlockSpec((channels, channels), lambda tap: (0, tap)),
        scratch_shapes=[
            pltpu.VMEM((channels, pixels), BF16),
            pltpu.VMEM(hidden.shape[:3] + (3 * channels,), BF16),
        ],
        compiler_params=pltpu.CompilerParams(vmem_limit_bytes=32 << 20),
        cost_estimate=pl.CostEstimate(
            flops=18 * pixels * channels * channels,
            bytes_accessed=18 * channels * channels,
            transcendentals=0,
        ),
        name="weight_grad",
    )(grads, hidden)


def project_kernel(info, middle, stats, gain, weight, attn, qkv):
    images, rows_dev, width, channels = middle.shape
    pixels = rows_dev * width
    heads, wide = HEADS, weight.shape[0] // HEADS
    base = info[0, 2]
    for i in range(images):
        average, inverse = norm_of(stats[i], image_count(info, i, channels))
        for r in range(rows_dev):
            inside = window(info, i, base + r, (width, channels))
            value = (middle[i, r] - average) * inverse * inside * gain[...]
            attn[i, r * width : (r + 1) * width] = value.astype(BF16)
        for h in range(heads):
            block = dot(weight[h * wide : (h + 1) * wide], attn[i], 1, 1)
            qkv[i * heads + h] = block.astype(BF16)


def project(info, middle, stats, gain, weight):
    images, rows_dev, width, channels = middle.shape
    pixels = rows_dev * width
    return pl.pallas_call(
        project_kernel,
        out_shape=(
            jax.ShapeDtypeStruct((images, pixels, channels), BF16),
            jax.ShapeDtypeStruct((images * HEADS, weight.shape[0] // HEADS, pixels), BF16),
        ),
        in_specs=[SCALARS, WHOLE, WHOLE, WHOLE, WHOLE],
        out_specs=(WHOLE, WHOLE),
        compiler_params=pltpu.CompilerParams(vmem_limit_bytes=32 << 20),
        name="project",
    )(info, middle, stats, gain, weight)


def unproject_kernel(info, middle, stats, grads, weight, out, out_stats):
    images, rows_dev, width, channels = middle.shape
    wide, pixels = grads.shape[1], grads.shape[2]
    base = info[0, 2]
    for i in range(images):
        average, inverse = norm_of(stats[i], image_count(info, i, channels))
        acc = None
        for h in range(HEADS):
            turned = grads[i * HEADS + h].astype(F32).T.astype(BF16)
            term = dot(turned, weight[h * wide : (h + 1) * wide], 1, 0)
            acc = term if acc is None else acc + term
        one = two = jnp.zeros((width, channels), F32)
        for r in range(rows_dev):
            inside = window(info, i, base + r, (width, channels))
            value = acc[r * width : (r + 1) * width] * inside
            out[i, r] = value
            one = one + value
            two = two + value * ((middle[i, r] - average) * inverse)
        put_stats(out_stats, i, one, two)


def unproject(info, middle, stats, grads, weight):
    images, rows_dev, width, channels = middle.shape
    return pl.pallas_call(
        unproject_kernel,
        out_shape=(
            jax.ShapeDtypeStruct(middle.shape, F32),
            jax.ShapeDtypeStruct(stats.shape, F32),
        ),
        in_specs=[SCALARS, WHOLE, WHOLE, WHOLE, WHOLE],
        out_specs=(WHOLE, WHOLE),
        compiler_params=pltpu.CompilerParams(vmem_limit_bytes=32 << 20),
        name="unproject",
    )(info, middle, stats, grads, weight)


def finish_kernel(info, pre_grad, grad_stats, image, stats, gain, grad_middle, out):
    images, rows_dev, width, channels = image.shape
    base = info[0, 2]
    for i in range(images):
        count = image_count(info, i, channels)
        average, inverse = norm_of(stats[i], count)
        mean, cross = means_of(grad_stats[i], gain[...], count)
        for r in range(rows_dev):
            inside = window(info, i, base + r, (width, channels))
            normal = (image[i, r].astype(F32) - average) * inverse
            term = (pre_grad[i, r] * gain[...] - mean - normal * cross) * inverse
            out[i, r] = (grad_middle[i, r] + term) * inside


def finish(info, pre_grad, grad_stats, image, stats, gain, grad_middle):
    return pl.pallas_call(
        finish_kernel,
        out_shape=jax.ShapeDtypeStruct(image.shape, F32),
        in_specs=[SCALARS] + [WHOLE] * 6,
        out_specs=WHOLE,
        compiler_params=pltpu.CompilerParams(vmem_limit_bytes=32 << 20),
        name="finish",
    )(info, pre_grad, grad_stats, image, stats, gain, grad_middle)


DMA = pltpu.SemaphoreType.DMA


def remote(src, dst, send, recv, device):
    return pltpu.make_async_remote_copy(
        src_ref=src,
        dst_ref=dst,
        send_sem=send,
        recv_sem=recv,
        device_id=device,
        device_id_type=MESH,
    )


class Grid:
    def __init__(self, items, n):
        self.items, self.n = items, n
        self.item, self.me = lax.axis_index("items"), lax.axis_index("rows")

    def row(self, k):
        return {"items": self.item, "rows": lax.rem(self.me + k, self.n)}

    def peer(self, k):
        return {"items": lax.rem(self.item + k, self.items), "rows": self.me}

    def greet(self):
        barrier = pltpu.get_barrier_semaphore()

        def rows(k, carry):
            pl.semaphore_signal(barrier, inc=1, device_id=self.row(k), device_id_type=MESH)
            return carry

        def items(k, carry):
            pl.semaphore_signal(barrier, inc=1, device_id=self.peer(k), device_id_type=MESH)
            return carry

        lax.fori_loop(1, self.n, rows, 0)
        lax.fori_loop(1, self.items, items, 0)

    def met(self):
        pl.semaphore_wait(pltpu.get_barrier_semaphore(), self.n + self.items - 2)

    def loop(self, count, body):
        def step(k, carry):
            body(k)
            return carry

        lax.fori_loop(1, count, step, 0)


class Sums:
    def __init__(self, grid, own, slots, send, recv):
        self.grid, self.own, self.slots, self.send, self.recv = grid, own, slots, send, recv

    def copy(self, k):
        return remote(
            self.own, self.slots.at[self.grid.me], self.send.at[k], self.recv.at[k], self.grid.row(k)
        )

    def start(self):
        self.grid.loop(self.grid.n, lambda k: self.copy(k).start())
        self.slots[self.grid.me] = self.own[...]

    def result(self):
        self.grid.loop(self.grid.n, lambda k: self.copy(k).wait())
        slots = self.slots
        return lax.fori_loop(1, self.grid.n, lambda k, s: s + slots[k], slots[0])


class Edges:
    def __init__(self, grid, field, send, recv):
        self.grid, self.field, self.send, self.recv = grid, field, send, recv

    def copy(self, side):
        last = self.field.shape[0] - 1
        at, to = (last - 1, 0) if side == 0 else (1, last)
        grid = self.grid
        return remote(
            self.field.at[at : at + 1],
            self.field.at[to : to + 1],
            self.send.at[side],
            self.recv.at[side],
            {"items": grid.item, "rows": grid.me + 1 if side == 0 else grid.me - 1},
        )

    def both(self, down, up):
        @pl.when(self.grid.me < self.grid.n - 1)
        def _():
            down()

        @pl.when(self.grid.me > 0)
        def _():
            up()

    def clear(self):
        last = self.field.shape[0] - 1

        @pl.when(self.grid.me == 0)
        def _():
            self.field[0] = jnp.zeros(self.field.shape[1:], self.field.dtype)

        @pl.when(self.grid.me == self.grid.n - 1)
        def _():
            self.field[last] = jnp.zeros(self.field.shape[1:], self.field.dtype)

    def start(self):
        self.both(lambda: self.copy(0).start(), lambda: self.copy(1).start())

    def wait(self):
        self.both(lambda: self.copy(1).wait_recv(), lambda: self.copy(0).wait_recv())
        self.both(lambda: self.copy(0).wait_send(), lambda: self.copy(1).wait_send())


def shift_into(out, r, value):
    width, channels = value.shape
    column = lax.broadcasted_iota(jnp.int32, value.shape, 0)
    left = jnp.where(column == 0, 0.0, pltpu.roll(value, 1, 0))
    right = jnp.where(column == width - 1, 0.0, pltpu.roll(value, width - 1, 0))
    out[r, :, :channels] = left.astype(BF16)
    out[r, :, channels : 2 * channels] = value.astype(BF16)
    out[r, :, 2 * channels :] = right.astype(BF16)


def row_stats(rows, width, channels, row):
    def step(r, carry):
        one, two = row(r)
        return carry[0] + one, carry[1] + two

    zero = jnp.zeros((width, channels), F32)
    one, two = lax.fori_loop(0, rows, step, (zero, zero))
    one = jnp.sum(one, axis=0, keepdims=True)
    two = jnp.sum(two, axis=0, keepdims=True)
    at = lax.broadcasted_iota(jnp.int32, (8, channels), 0)
    return jnp.where(at == 0, one, jnp.where(at == 1, two, 0.0))


def each_row(rows, body):
    def step(r, carry):
        body(r)
        return carry

    lax.fori_loop(0, rows, step, 0)


def conv_taps(shifted, weight, acc, rows_dev):
    pixels, wide = acc.shape[0], shifted.shape[2]
    acc[...] = jnp.zeros_like(acc)

    def step(tap, carry):
        acc[...] += dot(shifted[pl.ds(tap, rows_dev)].reshape(pixels, wide), weight[tap], 1, 0)
        return carry

    lax.fori_loop(0, 3, step, 0)


def forward_kernel(items, n, *refs):
    (info, image, cot, text, embed, gain1, gain2, gain3, w1_in, w2_in, embed_in, text_in, qkv_in, proj_in,
     first_out, mid_out, cot_out, hidden_all, second_all, attn_out, turned_out, qkv_pair, go_pair, text_pair,
     text_cols, stats_out, shifts_out,
     image_v, cot_v, text_v, w1, w2, embed_w, text_w, qkv_w, proj_w, first_v, mid_v, hidden, second, attn,
     turned, qkv, go, text_kv, cols, shifted, acc, own, slots,
     load, sum_send, sum_recv, edge_send, edge_recv, row_send, row_recv, item_send, item_recv) = refs
    grid = Grid(items, n)
    item, me = grid.item, grid.me
    rows_dev, width, channels = image.shape
    pixels = rows_dev * width
    heads, head_dim, wide = HEADS, channels // HEADS, 3 * channels // HEADS
    base = me * rows_dev
    count = (info[0, 0] * info[0, 1]).astype(F32) * (channels // GROUPS)

    def inside(row):
        return window(info, 0, row, (width, channels))

    loads = []

    def fetch(src, dst):
        c = pltpu.make_async_copy(src, dst, load.at[len(loads)])
        c.start()
        loads.append(c)
        return c

    center = slice(1, rows_dev + 1)
    got_image = fetch(image, image_v.at[center])
    got_cot = fetch(cot, cot_v.at[center])
    got_proj = fetch(proj_in, proj_w)
    got_text = fetch(text, text_v)
    got_text_w = fetch(text_in, text_w)
    got_w1 = fetch(w1_in, w1)
    got_embed_w = fetch(embed_in, embed_w)
    got_w2 = fetch(w2_in, w2)
    got_qkv_w = fetch(qkv_in, qkv_w)
    edges = [
        Edges(grid, field, edge_send.at[j], edge_recv.at[j])
        for j, field in enumerate((image_v, cot_v, first_v, mid_v))
    ]
    sums = [Sums(grid, own.at[j], slots.at[j], sum_send.at[j], sum_recv.at[j]) for j in range(3)]
    grid.greet()
    for e in edges:
        e.clear()
    got_image.wait()

    def start_row(r):
        return image_v[1 + r].astype(F32) * inside(base + r)

    def start_stats(r):
        v = start_row(r)
        return v, v * v

    own[0] = row_stats(rows_dev, width, channels, start_stats)
    grid.met()
    sums[0].start()
    edges[0].start()
    got_cot.wait()
    edges[1].start()

    got_text.wait()
    got_text_w.wait()
    text_all = dot(text_v[...], text_w[...], 1, 0).astype(BF16)
    share = text_v.shape[1] // n
    for h in range(heads):
        text_kv[h] = text_all[:, h * 2 * head_dim : (h + 1) * 2 * head_dim]
    for r in range(n):
        cols[r] = text_v[:, r * share : (r + 1) * share]

    def scatter(j, src, dst):
        def copy(k):
            to = lax.rem(me + k, n)
            return remote(src.at[to], dst.at[me], row_send.at[j, k], row_recv.at[j, k], grid.row(k))

        return copy

    kv_copy = scatter(0, text_kv, text_pair)
    col_copy = scatter(1, cols, text_cols.at[item])
    grid.loop(n, lambda k: kv_copy(k).start())
    grid.loop(n, lambda k: col_copy(k).start())
    own_kv = fetch(text_kv.at[me], text_pair.at[me])
    own_col = fetch(cols.at[me], text_cols.at[item, me])

    got_proj.wait()

    def to_grad(r):
        attn[pl.ds(r * width, width)] = (cot_v[1 + r].astype(F32) * inside(base + r)).astype(BF16)

    each_row(rows_dev, to_grad)
    for h in range(heads):
        go[h] = dot(proj_w[h * head_dim : (h + 1) * head_dim], attn[...], 1, 1).astype(BF16)
    go_copy = scatter(2, go, go_pair)
    own_go = fetch(go.at[me], go_pair.at[me])

    stats = sums[0].result()
    stats_out[0] = stats
    average, inverse = norm_of(stats, count)
    edges[0].wait()
    grid.loop(n, lambda k: go_copy(k).start())

    def to_hidden(r):
        ok = inside(base + r - 1)
        value = (image_v[r].astype(F32) * ok - average) * inverse * ok * gain1[...]
        value = value * sigmoid(value) * ok
        shift_into(shifted, r, value)
        hidden[r] = value.astype(BF16)

    each_row(rows_dev + 2, to_hidden)

    def spread(j, src, dst):
        def copy(k):
            return remote(src, dst.at[item], item_send.at[j, k], item_recv.at[j, k], grid.peer(k))

        return copy

    hidden_copy = spread(0, hidden, hidden_all)
    grid.loop(items, lambda k: hidden_copy(k).start())
    own_hidden = fetch(hidden, hidden_all.at[item])
    got_w1.wait()
    conv_taps(shifted, w1, acc, rows_dev)

    def first_row(r):
        value = acc[pl.ds(r * width, width)] * inside(base + r)
        first_v[1 + r] = value
        return value, value * value

    own[1] = row_stats(rows_dev, width, channels, first_row)
    sums[1].start()
    edges[2].start()

    e = embed[...].astype(F32)
    low = (e * sigmoid(e)).astype(BF16)
    got_embed_w.wait()
    shifts_out[...] = dot(low, embed_w[...], 1, 0)
    scale, shift = shifts_out[:, :channels], shifts_out[:, channels:]

    stats = sums[1].result()
    stats_out[1] = stats
    average, inverse = norm_of(stats, count)
    edges[2].wait()
    own_first = fetch(first_v, first_out)

    def to_second(r):
        ok = inside(base + r - 1)
        _, moved = moved_of(first_v[r], ok, average, inverse, gain2[...], scale, shift)
        value = moved * sigmoid(moved) * ok
        shift_into(shifted, r, value)
        second[r] = value.astype(BF16)

    each_row(rows_dev + 2, to_second)
    second_copy = spread(1, second, second_all)
    grid.loop(items, lambda k: second_copy(k).start())
    own_second = fetch(second, second_all.at[item])
    got_w2.wait()
    conv_taps(shifted, w2, acc, rows_dev)

    def middle_row(r):
        value = (image_v[1 + r].astype(F32) + acc[pl.ds(r * width, width)]) * inside(base + r)
        mid_v[1 + r] = value
        return value, value * value

    own[2] = row_stats(rows_dev, width, channels, middle_row)
    sums[2].start()
    edges[3].start()
    own_go.wait()
    edges[1].wait()
    own_cot = fetch(cot_v, cot_out)
    got_qkv_w.wait()
    for j in range(3):
        block = qkv_w[:, j * channels : (j + 1) * channels].astype(F32).T
        turned[j * channels : (j + 1) * channels] = block.astype(BF16)
    own_turned = fetch(turned, turned_out)

    stats = sums[2].result()
    stats_out[2] = stats
    average, inverse = norm_of(stats, count)

    def to_attn(r):
        value = (mid_v[1 + r] - average) * inverse * inside(base + r) * gain3[...]
        attn[pl.ds(r * width, width)] = value.astype(BF16)

    each_row(rows_dev, to_attn)
    own_attn = fetch(attn, attn_out)
    qkv_copy = scatter(3, qkv, qkv_pair)

    def head(k, carry):
        to = lax.rem(me + k, n)
        rows = pl.ds(pl.multiple_of(to * wide, wide), wide)
        qkv[to] = dot(turned[rows], attn[...], 1, 1).astype(BF16)
        return carry

    def send_head(k, carry):
        head(k, carry)
        qkv_copy(k).start()
        return carry

    lax.fori_loop(1, n, send_head, 0)
    head(0, 0)
    own_qkv = fetch(qkv.at[me], qkv_pair.at[me])
    edges[3].wait()
    own_mid = fetch(mid_v, mid_out)

    grid.loop(n, lambda k: kv_copy(k).wait())
    grid.loop(n, lambda k: col_copy(k).wait())
    own_col.wait()
    cols_copy = spread(2, text_cols.at[item], text_cols)
    grid.loop(items, lambda k: cols_copy(k).start())
    grid.loop(n, lambda k: go_copy(k).wait())
    grid.loop(n, lambda k: qkv_copy(k).wait())
    grid.loop(items, lambda k: hidden_copy(k).wait())
    grid.loop(items, lambda k: second_copy(k).wait())
    grid.loop(items, lambda k: cols_copy(k).wait())
    for c in (own_kv, own_hidden, own_first, own_second, own_cot, own_turned, own_attn, own_qkv, own_mid):
        c.wait()


def forward_call(info, image, cot, text, embed, gains, weights, identity):
    items, n = lax.axis_size("items"), lax.axis_size("rows")
    rows_dev, width, channels = image.shape
    pixels = rows_dev * width
    padded = (rows_dev + 2, width, channels)
    tokens, text_width = text.shape
    head_dim = channels // HEADS
    w1, w2, embed_w, text_w, qkv_w, proj_w = weights
    sds = jax.ShapeDtypeStruct
    outs = (
        sds(padded, F32),
        sds(padded, F32),
        sds(padded, BF16),
        sds((items,) + padded, BF16),
        sds((items,) + padded, BF16),
        sds((pixels, channels), BF16),
        sds((3 * channels, channels), BF16),
        sds((n, 3 * head_dim, pixels), BF16),
        sds((n, head_dim, pixels), BF16),
        sds((n, tokens, 2 * head_dim), BF16),
        sds((items, n, tokens, text_width // n), BF16),
        sds((3, 8, channels), F32),
        sds((1, 2 * channels), F32),
    )
    v = pltpu.VMEM
    scratch = [
        v(padded, BF16),
        v(padded, BF16),
        v(text.shape, BF16),
        v(w1.shape, BF16),
        v(w2.shape, BF16),
        v(embed_w.shape, BF16),
        v(text_w.shape, BF16),
        v(qkv_w.shape, BF16),
        v(proj_w.shape, BF16),
        v(padded, F32),
        v(padded, F32),
        v(padded, BF16),
        v(padded, BF16),
        v((pixels, channels), BF16),
        v((3 * channels, channels), BF16),
        v((n, 3 * head_dim, pixels), BF16),
        v((n, head_dim, pixels), BF16),
        v((n, tokens, 2 * head_dim), BF16),
        v((n, tokens, text_width // n), BF16),
        v((rows_dev + 2, width, 3 * channels), BF16),
        v((pixels, channels), F32),
        v((3, 8, channels), F32),
        v((3, n, 8, channels), F32),
        DMA((24,)),
        DMA((3, n)),
        DMA((3, n)),
        DMA((4, 2)),
        DMA((4, 2)),
        DMA((4, n)),
        DMA((4, n)),
        DMA((3, items)),
        DMA((3, items)),
    ]
    return pl.pallas_call(
        functools.partial(forward_kernel, items, n),
        out_shape=outs,
        in_specs=[SCALARS] + [ANYWHERE] * 3 + [WHOLE] * 4 + [ANYWHERE] * 6,
        out_specs=(ANYWHERE,) * 11 + (WHOLE,) * 2,
        scratch_shapes=scratch,
        compiler_params=pltpu.CompilerParams(
            collective_id=identity, has_side_effects=True, vmem_limit_bytes=56 << 20
        ),
        cost_estimate=pl.CostEstimate(
            flops=40 * pixels * channels * channels, bytes_accessed=60 << 20, transcendentals=0
        ),
        name="forward",
    )(info, image, cot, text, embed, *gains, *weights)


class KernelSum:
    def __init__(self, grid, turned, quarter, part, from_core, chip_sum, from_chip, final, item_sems, core_sems,
                 chip_sems, final_sems):
        self.grid = grid
        self.turned, self.quarter, self.part, self.from_core = turned, quarter, part, from_core
        self.chip_sum, self.from_chip, self.final = chip_sum, from_chip, final
        self.item_sems, self.core_sems = item_sems, core_sems
        self.chip_sems, self.final_sems = chip_sems, final_sems
        self.chips = grid.n // 2
        self.chip, self.core = grid.me // 2, lax.rem(grid.me, 2)

    def grads_copy(self, k):
        grid = self.grid
        send, recv = self.item_sems
        to = lax.rem(grid.item + k, grid.items)
        return remote(
            self.turned.at[to], self.quarter.at[grid.item], send.at[k], recv.at[k], grid.peer(k)
        )

    def send_grads(self, shifted):
        grid, chips = self.grid, self.chips
        rows_dev, width, channels = shifted.shape[0] - 2, shifted.shape[1], shifted.shape[2] // 3
        center = shifted[1 : rows_dev + 1, :, channels : 2 * channels]
        block = center.reshape(rows_dev * width, channels).astype(F32).T.astype(BF16)
        share = channels // grid.n
        rows = share // grid.items
        for z in range(chips):
            for c in range(2):
                for q in range(grid.items):
                    at = (z * 2 + c) * share + q * rows
                    to = (c * chips + z) * rows
                    self.turned[q, to : to + rows] = block[at : at + rows]
        grid.loop(grid.items, lambda k: self.grads_copy(k).start())
        self.quarter[grid.item] = self.turned[grid.item]

    def wait_grads(self):
        self.grid.loop(self.grid.items, lambda k: self.grads_copy(k).wait())

    def core_copy(self, a):
        send, recv = self.core_sems
        grid = self.grid
        return remote(
            self.part.at[a, 1 - self.core],
            self.from_core.at[a],
            send.at[a],
            recv.at[a],
            {"items": grid.item, "rows": grid.me + 1 - 2 * self.core},
        )

    def compute(self, a, shifted):
        items, padded, width, wide = shifted.shape
        rows_dev, channels = padded - 2, wide // 3
        half = self.turned.shape[1] // 2
        for b in range(3):
            acc = None
            for g in range(items):
                rhs = shifted[g, a : a + rows_dev, :, b * channels : (b + 1) * channels]
                term = dot(self.quarter[g], rhs.reshape(rows_dev * width, channels), 1, 0)
                acc = term if acc is None else acc + term
            self.part[a, 0, b] = acc[:half].astype(BF16)
            self.part[a, 1, b] = acc[half:].astype(BF16)
        self.core_copy(a).start()

    def chip_copy(self, a, k):
        send, recv = self.chip_sems
        grid = self.grid
        to = lax.rem(self.chip + k, self.chips)
        return remote(
            self.chip_sum.at[a, to],
            self.from_chip.at[a, k],
            send.at[a, k],
            recv.at[a, k],
            {"items": grid.item, "rows": to * 2 + self.core},
        )

    def over_chips(self, a):
        self.core_copy(a).wait()
        rows = self.chip_sum.shape[3]
        for b in range(3):
            both = self.part[a, self.core, b].astype(F32) + self.from_core[a, b].astype(F32)
            for z in range(self.chips):
                self.chip_sum[a, z, b] = both[z * rows : (z + 1) * rows].astype(BF16)
        for k in range(1, self.chips):
            self.chip_copy(a, k).start()

    def final_copy(self, a, k):
        send, recv = self.final_sems
        mine = self.final.at[a, self.grid.item]
        return remote(mine, mine, send.at[a, k], recv.at[a, k], self.grid.peer(k))

    def over_items(self, a):
        for k in range(1, self.chips):
            self.chip_copy(a, k).wait()
        total = self.chip_sum[a, self.chip].astype(F32)
        for k in range(1, self.chips):
            total = total + self.from_chip[a, k].astype(F32)
        self.final[a, self.grid.item] = total.astype(BF16)
        for k in range(1, self.grid.items):
            self.final_copy(a, k).start()

    def put(self, a, out):
        for k in range(1, self.grid.items):
            self.final_copy(a, k).wait()
        channels = self.final.shape[4]
        for b in range(3):
            rows = [self.final[a, q, b].astype(F32) for q in range(self.grid.items)]
            at = (a * 3 + b) * channels
            out[at : at + channels] = jnp.concatenate(rows, axis=0).T


class SideSum:
    def __init__(self, grid, values, from_core, core_sum, from_item, item_sum, from_chip, final, core_sems,
                 item_sems, chip_sems, final_sems):
        self.grid = grid
        self.values, self.from_core, self.core_sum = values, from_core, core_sum
        self.from_item, self.item_sum, self.from_chip, self.final = (
            from_item,
            item_sum,
            from_chip,
            final,
        )
        self.core_sems, self.item_sems = core_sems, item_sems
        self.chip_sems, self.final_sems = chip_sems, final_sems
        self.chips = grid.n // 2
        self.chip, self.core = grid.me // 2, lax.rem(grid.me, 2)

    def core_copy(self):
        send, recv = self.core_sems
        grid = self.grid
        return remote(
            self.values.at[1 - self.core],
            self.from_core,
            send.at[0],
            recv.at[0],
            {"items": grid.item, "rows": grid.me + 1 - 2 * self.core},
        )

    def item_copy(self, k):
        send, recv = self.item_sems
        grid = self.grid
        to = lax.rem(grid.item + k, grid.items)
        return remote(
            self.core_sum.at[to], self.from_item.at[k], send.at[k], recv.at[k], grid.peer(k)
        )

    def over_items(self):
        self.core_copy().wait()
        for z in range(self.chips):
            both = self.values[self.core, z].astype(F32) + self.from_core[z].astype(F32)
            for q in range(self.grid.items):
                self.core_sum[q, z] = both[q].astype(BF16)
        for k in range(1, self.grid.items):
            self.item_copy(k).start()

    def chip_copy(self, k):
        send, recv = self.chip_sems
        grid = self.grid
        to = lax.rem(self.chip + k, self.chips)
        return remote(
            self.item_sum.at[to],
            self.from_chip.at[k],
            send.at[k],
            recv.at[k],
            {"items": grid.item, "rows": to * 2 + self.core},
        )

    def over_chips(self):
        for k in range(1, self.grid.items):
            self.item_copy(k).wait()
        total = self.core_sum[self.grid.item].astype(F32)
        for k in range(1, self.grid.items):
            total = total + self.from_item[k].astype(F32)
        self.item_sum[...] = total.astype(BF16)
        for k in range(1, self.chips):
            self.chip_copy(k).start()

    def final_copy(self, k):
        send, recv = self.final_sems
        mine = self.final.at[self.grid.item]
        return remote(mine, mine, send.at[k], recv.at[k], self.grid.peer(k))

    def spread(self):
        for k in range(1, self.chips):
            self.chip_copy(k).wait()
        total = self.item_sum[self.chip].astype(F32)
        for k in range(1, self.chips):
            total = total + self.from_chip[k].astype(F32)
        self.final[self.grid.item] = total.astype(BF16)
        for k in range(1, self.grid.items):
            self.final_copy(k).start()

    def put(self, qkv_out, proj_out):
        for k in range(1, self.grid.items):
            self.final_copy(k).wait()
        rows = jnp.concatenate(
            [self.final[q].astype(F32) for q in range(self.grid.items)], axis=0
        )
        share, channels = rows.shape[0], rows.shape[1] // 4
        for w in range(3):
            qkv_out[:, w * share : (w + 1) * share] = rows[:, w * channels : (w + 1) * channels].T
        proj_out[...] = rows[:, 3 * channels :].T


def conv_taps_back(shifted, weight, acc, rows_dev):
    pixels, channels = acc.shape
    acc[...] = jnp.zeros_like(acc)

    def step(tap, carry):
        lhs = shifted[pl.ds(tap, rows_dev)].reshape(pixels, 3 * channels)
        total = None
        for b in range(3):
            at = pl.multiple_of(((2 - tap) * 3 + 2 - b) * channels, channels)
            term = dot(
                lhs[:, b * channels : (b + 1) * channels], weight[pl.ds(at, channels)], 1, 1
            )
            total = term if total is None else total + term
        acc[...] += total
        return carry

    lax.fori_loop(0, 3, step, 0)


def backward_kernel(items, n, *refs):
    (info, embed, gain1, gain2, gain3, stats_in, shifts,
     o_pair, dqkv_pair, dtext, first, middle, cot, image, hidden_all, second_all, attn_in, turned_in, text_cols,
     proj_in, w1_in, w2_in, text_in, embed_in,
     output, image_grad, conv1_out, conv2_out, qkv_out, proj_out, vectors, text_grad, text_w_grad, embed_grad,
     weight, proj_w, qkv_turned, first_v, mid_v, cot_v, image_v, attn, cols, rows_v, dq, o, dt, own_dt,
     grad_v, grad_mid, moved_v, pre, acc, shifted, shifted_all, masked, out_v, image_out,
     turned, quarter, part, from_core, chip_sum, from_chip, final,
     side_v, side_core, side_sum, side_item, side_total, side_chip, side_final,
     vector, vector_land, own, slots,
     load, sum_send, sum_recv, edge_send, edge_recv, row_send, row_recv, dt_send, dt_recv, vec_send, vec_recv,
     k_item_send, k_item_recv, k_core_send, k_core_recv, k_chip_send, k_chip_recv, k_final_send, k_final_recv,
     s_core_send, s_core_recv, s_item_send, s_item_recv, s_chip_send, s_chip_recv, s_final_send,
     s_final_recv) = refs
    grid = Grid(items, n)
    item, me = grid.item, grid.me
    rows_dev, width, channels = image.shape
    pixels = rows_dev * width
    heads, head_dim, wide = HEADS, channels // HEADS, 3 * channels // HEADS
    share = channels // n
    base = me * rows_dev
    count = (info[0, 0] * info[0, 1]).astype(F32) * (channels // GROUPS)
    scale, shift = shifts[:, :channels], shifts[:, channels:]

    def inside(row):
        return window(info, 0, row, (width, channels))

    fetched = []

    def fetch(src, dst):
        c = pltpu.make_async_copy(src, dst, load.at[len(fetched)])
        c.start()
        fetched.append(c)
        return c

    def scatter(j, src, dst):
        def copy(k):
            to = lax.rem(me + k, n)
            return remote(src.at[to], dst.at[me], row_send.at[j, k], row_recv.at[j, k], grid.row(k))

        return copy

    own_dq = fetch(dqkv_pair.at[me], dq.at[me])
    got_turned = fetch(turned_in, qkv_turned)
    got_mid = fetch(middle, mid_v)
    got_cot = fetch(cot, cot_v)
    got_w2 = fetch(w2_in, weight)
    got_first = fetch(first, first_v)
    got_attn = fetch(attn_in, attn)
    own_o = fetch(o_pair.at[me], o.at[me])
    got_proj = fetch(proj_in, proj_w)
    own_text = fetch(dtext.at[me], own_dt.at[me])
    own_all = fetch(dtext, dt.at[item, me])
    got_second = fetch(second_all, rows_v)
    got_image = fetch(image, image_v)
    got_cols = fetch(text_cols, cols)
    grid.greet()
    edges = [
        Edges(grid, field, edge_send.at[j], edge_recv.at[j])
        for j, field in enumerate((grad_v, moved_v))
    ]
    for e in edges:
        e.clear()
    sums = [Sums(grid, own.at[j], slots.at[j], sum_send.at[j], sum_recv.at[j]) for j in range(3)]
    kernel_sums = [
        KernelSum(grid, turned.at[j], quarter.at[j], part.at[j], from_core.at[j], chip_sum.at[j], from_chip.at[j],
                  final.at[j], (k_item_send.at[j], k_item_recv.at[j]), (k_core_send.at[j], k_core_recv.at[j]),
                  (k_chip_send.at[j], k_chip_recv.at[j]), (k_final_send.at[j], k_final_recv.at[j]))
        for j in range(2)
    ]
    sum2, sum1 = kernel_sums
    side = SideSum(grid, side_v, side_core, side_sum, side_item, side_total, side_chip, side_final,
                   (s_core_send, s_core_recv), (s_item_send, s_item_recv), (s_chip_send, s_chip_recv),
                   (s_final_send, s_final_recv))
    dq_copy = scatter(0, dqkv_pair, dq)
    o_copy = scatter(1, o_pair, o)
    text_copy = scatter(2, dtext, own_dt)

    def gather_copy(k):
        return remote(
            dtext, dt.at[item, me], row_send.at[3, k], row_recv.at[3, k], grid.row(k)
        )

    grid.met()
    grid.loop(n, lambda k: dq_copy(k).start())
    grid.loop(n, lambda k: o_copy(k).start())
    grid.loop(n, lambda k: text_copy(k).start())
    grid.loop(n, lambda k: gather_copy(k).start())

    got_turned.wait()
    own_dq.wait()

    def unproject_head(h):
        rows = pl.ds(pl.multiple_of(h * wide, wide), wide)
        return dot(dq[h].astype(F32).T.astype(BF16), qkv_turned[rows], 1, 0)

    acc[...] = unproject_head(me)

    def next_head(k):
        dq_copy(k).wait()
        acc[...] += unproject_head(lax.rem(me + n - k, n))

    grid.loop(n, next_head)
    got_mid.wait()
    average, inverse = norm_of(stats_in[2], count)

    def grad_row(r):
        value = acc[pl.ds(r * width, width)] * inside(base + r)
        grad_v[1 + r] = value
        return value, value * ((mid_v[1 + r] - average) * inverse)

    own[0] = row_stats(rows_dev, width, channels, grad_row)
    sums[0].start()
    edges[0].start()

    got_attn.wait()

    def qkv_head(h):
        block = dot(dq[h], attn[...], 1, 0).astype(BF16)
        for w in range(3):
            rows = block[w * head_dim : (w + 1) * head_dim]
            side_v[lax.rem(h, 2), h // 2, :, :, w * channels : (w + 1) * channels] = rows.reshape(
                items, share // items, channels
            )

    each_row(heads, qkv_head)
    got_cot.wait()

    def mask_row(r):
        masked[pl.ds(r * width, width)] = (cot_v[1 + r].astype(F32) * inside(base + r)).astype(BF16)

    each_row(rows_dev, mask_row)

    stats4 = sums[0].result()
    mean, cross = means_of(stats4, gain3[...], count)
    edges[0].wait()

    def to_grad2(r):
        normal = (mid_v[r] - average) * inverse
        ok = inside(base + r - 1)
        term = (grad_v[r] * gain3[...] - mean - normal * cross) * inverse * ok
        total = cot_v[r].astype(F32) + term
        grad_mid[r] = total
        shift_into(shifted, r, total * ok)

    each_row(rows_dev + 2, to_grad2)
    sum2.send_grads(shifted)
    got_w2.wait()
    conv_taps_back(shifted, weight, acc, rows_dev)
    got_first.wait()
    average2, inverse2 = norm_of(stats_in[1], count)

    def moved_row(r):
        ok = inside(base + r)
        normal, moved = moved_of(first_v[1 + r], ok, average2, inverse2, gain2[...], scale, shift)
        value = acc[pl.ds(r * width, width)] * ok * silu_slope(moved)
        moved_v[1 + r] = value
        return value, value * normal

    own[1] = row_stats(rows_dev, width, channels, moved_row)
    sums[1].start()
    edges[1].start()
    got_w1 = fetch(w1_in, weight)
    got_second.wait()

    def shift_rows():
        for g in range(items):
            each_row(rows_dev + 2, lambda r: shift_into(shifted_all.at[g], r, rows_v[g, r].astype(F32)))

    shift_rows()
    got_hidden = fetch(hidden_all, rows_v)
    sum2.wait_grads()
    for a in range(3):
        sum2.compute(a, shifted_all)

    own_o.wait()
    grid.loop(n, lambda k: o_copy(k).wait())
    flat_o = o[...].reshape(channels, pixels)
    block = dot(masked[...].astype(F32).T.astype(BF16), flat_o, 1, 1).astype(BF16)
    for r in range(n):
        rows = block[r * share : (r + 1) * share]
        side_v[r % 2, r // 2, :, :, 3 * channels :] = rows.reshape(items, share // items, channels)
    side.core_copy().start()

    stats5 = sums[1].result()
    factor = gain2[...] * (1.0 + scale)
    mean, cross = means_of(stats5, factor, count)
    edges[1].wait()

    def to_grad1(r):
        normal = (first_v[r] - average2) * inverse2
        value = (moved_v[r] * factor - mean - normal * cross) * inverse2
        shift_into(shifted, r, value * inside(base + r - 1))

    each_row(rows_dev + 2, to_grad1)
    sum1.send_grads(shifted)
    for a in range(3):
        sum2.over_chips(a)
    got_w1.wait()
    conv_taps_back(shifted, weight, acc, rows_dev)
    got_image.wait()
    average1, inverse1 = norm_of(stats_in[0], count)

    def pre_row(r):
        ok = inside(base + r)
        normal = (image_v[r].astype(F32) - average1) * inverse1 * ok
        value = acc[pl.ds(r * width, width)] * ok * silu_slope(normal * gain1[...])
        pre[r] = value
        return value, value * normal

    own[2] = row_stats(rows_dev, width, channels, pre_row)
    sums[2].start()
    tall = text_in.shape[0]
    got_text_w = [
        fetch(text_in.at[:, j * channels : (j + 1) * channels], weight.at[j * tall : (j + 1) * tall])
        for j in range(2)
    ]
    side.over_items()
    got_hidden.wait()
    shift_rows()
    sum1.wait_grads()
    sum1.compute(0, shifted_all)
    sum1.compute(1, shifted_all)
    sum1.over_chips(0)
    sum1.compute(2, shifted_all)
    sum1.over_chips(1)
    sum1.over_chips(2)
    for a in range(3):
        sum2.over_items(a)
    side.over_chips()

    stats6 = sums[2].result()
    e = embed[...].astype(F32)
    low = (e * sigmoid(e)).astype(BF16).astype(F32)
    vector[...] = jnp.zeros_like(vector)
    vector[0:1] = stats6[1:2]
    vector[1:2] = stats5[1:2] * (1.0 + scale)
    vector[2:3] = stats4[1:2]
    vector[3:4] = (stats5[1:2] * gain2[...]).astype(BF16).astype(F32)
    vector[4:5] = stats5[0:1].astype(BF16).astype(F32)
    for j in range(embed.shape[1] // channels):
        vector[5 + j : 6 + j] = low[:, j * channels : (j + 1) * channels]

    def vector_copy(k):
        return remote(
            vector, vector_land.at[item], vec_send.at[k], vec_recv.at[k], grid.peer(k)
        )

    grid.loop(items, lambda k: vector_copy(k).start())
    vector_land[item] = vector[...]

    grid.loop(n, lambda k: gather_copy(k).wait())
    own_all.wait()

    def dt_copy(k):
        mine = dt.at[item]
        return remote(mine, mine, dt_send.at[k], dt_recv.at[k], grid.peer(k))

    grid.loop(items, lambda k: dt_copy(k).start())
    mean, cross = means_of(stats6, gain1[...], count)

    def finish_row(r):
        normal = (image_v[r].astype(F32) - average1) * inverse1
        term = (pre[r] * gain1[...] - mean - normal * cross) * inverse1
        image_out[r] = (grad_mid[1 + r] + term) * inside(base + r)

    each_row(rows_dev, finish_row)
    put_image = fetch(image_out, image_grad)
    side.spread()

    got_proj.wait()
    acc[...] = dot(flat_o.astype(F32).T.astype(BF16), proj_w[...], 1, 0)

    def output_row(r):
        value = mid_v[1 + r] + acc[pl.ds(r * width, width)] * inside(base + r)
        out_v[r] = value.astype(BF16)

    each_row(rows_dev, output_row)
    put_output = fetch(out_v, output)

    own_text.wait()
    grid.loop(n, lambda k: text_copy(k).wait())
    for c in got_text_w:
        c.wait()
    half = heads // 2
    total = None
    for j in range(2):
        lhs = jnp.concatenate([own_dt[j * half + h] for h in range(half)], axis=1)
        term = dot(lhs, weight[j * tall : (j + 1) * tall], 1, 1)
        total = term if total is None else total + term
    text_grad[...] = total
    got_embed_w = [
        fetch(embed_in.at[:, j * channels : (j + 1) * channels], weight.at[j * tall : (j + 1) * tall])
        for j in range(2)
    ]
    for a in range(3):
        sum1.over_items(a)
    for a in range(3):
        sum2.put(a, conv2_out)

    grid.loop(items, lambda k: dt_copy(k).wait())
    got_cols.wait()
    tokens = cols.shape[0] * cols.shape[1]
    flat_cols = cols[...].reshape(tokens, cols.shape[2]).astype(F32).T.astype(BF16)
    for h in range(heads):
        rhs = jnp.concatenate([dt[g, h].reshape(tokens // items, 2 * head_dim) for g in range(items)], axis=0)
        text_w_grad[:, h * 2 * head_dim : (h + 1) * 2 * head_dim] = dot(flat_cols, rhs, 1, 0)

    for c in got_embed_w:
        c.wait()
    total = None
    for j in range(2):
        lhs = vector[3 + j : 4 + j] if j else vector[3:4]
        lhs = jnp.broadcast_to(lhs, (8, channels)).astype(BF16)
        term = dot(lhs, weight[j * tall : (j + 1) * tall], 1, 1)
        total = term if total is None else total + term
    embed_grad[...] = total[0:1] * silu_slope(e)
    side.put(qkv_out, proj_out)
    for a in range(3):
        sum1.put(a, conv1_out)
    grid.loop(items, lambda k: vector_copy(k).wait())
    vectors[...] = vector_land[...]
    put_image.wait()
    put_output.wait()


def backward_call(info, embed, gains, stats, shifts, arrays, identity):
    items, n = lax.axis_size("items"), lax.axis_size("rows")
    o_pair, dqkv_pair, dtext = arrays[:3]
    image, text_cols, text_w = arrays[6], arrays[11], arrays[15]
    rows_dev, width, channels = image.shape
    pixels = rows_dev * width
    head_dim = channels // HEADS
    share = channels // n
    rows = share // items
    chips = n // 2
    padded = (rows_dev + 2, width, channels)
    tokens = dtext.shape[1]
    sds = jax.ShapeDtypeStruct
    outs = (
        sds(image.shape, BF16),
        sds(image.shape, F32),
        sds((9 * channels, share), F32),
        sds((9 * channels, share), F32),
        sds((channels, 3 * share), F32),
        sds((channels, share), F32),
        sds((items, 16, channels), F32),
        sds((tokens, text_w.shape[0]), F32),
        sds((text_w.shape[0] // n, 2 * channels), F32),
        sds(embed.shape, F32),
    )
    v = pltpu.VMEM
    scratch = [
        v((9 * channels, channels), BF16),
        v((channels, channels), BF16),
        v((3 * channels, channels), BF16),
        v(padded, F32),
        v(padded, F32),
        v(padded, BF16),
        v(image.shape, BF16),
        v((pixels, channels), BF16),
        v(text_cols.shape, BF16),
        v((items,) + padded, BF16),
        v(dqkv_pair.shape, BF16),
        v(o_pair.shape, BF16),
        v((items, n) + dtext.shape, BF16),
        v(dtext.shape, BF16),
        v(padded, F32),
        v(padded, F32),
        v(padded, F32),
        v(image.shape, F32),
        v((pixels, channels), F32),
        v((rows_dev + 2, width, 3 * channels), BF16),
        v((items, rows_dev + 2, width, 3 * channels), BF16),
        v((pixels, channels), BF16),
        v(image.shape, BF16),
        v(image.shape, F32),
        v((2, items, channels // items, pixels), BF16),
        v((2, items, channels // items, pixels), BF16),
        v((2, 3, 2, 3, chips * rows, channels), BF16),
        v((2, 3, 3, chips * rows, channels), BF16),
        v((2, 3, chips, 3, rows, channels), BF16),
        v((2, 3, chips, 3, rows, channels), BF16),
        v((2, 3, items, 3, rows, channels), BF16),
        v((2, chips, items, rows, 4 * channels), BF16),
        v((chips, items, rows, 4 * channels), BF16),
        v((items, chips, rows, 4 * channels), BF16),
        v((items, chips, rows, 4 * channels), BF16),
        v((chips, rows, 4 * channels), BF16),
        v((chips, rows, 4 * channels), BF16),
        v((items, rows, 4 * channels), BF16),
        v((16, channels), F32),
        v((items, 16, channels), F32),
        v((3, 8, channels), F32),
        v((3, n, 8, channels), F32),
        DMA((32,)),
        DMA((3, n)),
        DMA((3, n)),
        DMA((2, 2)),
        DMA((2, 2)),
        DMA((4, n)),
        DMA((4, n)),
        DMA((items,)),
        DMA((items,)),
        DMA((items,)),
        DMA((items,)),
        DMA((2, items)),
        DMA((2, items)),
        DMA((2, 3)),
        DMA((2, 3)),
        DMA((2, 3, chips)),
        DMA((2, 3, chips)),
        DMA((2, 3, items)),
        DMA((2, 3, items)),
        DMA((1,)),
        DMA((1,)),
        DMA((items,)),
        DMA((items,)),
        DMA((chips,)),
        DMA((chips,)),
        DMA((items,)),
        DMA((items,)),
    ]
    return pl.pallas_call(
        functools.partial(backward_kernel, items, n),
        out_shape=outs,
        in_specs=[SCALARS] + [WHOLE] * 6 + [ANYWHERE] * len(arrays),
        out_specs=(ANYWHERE,) * 2 + (WHOLE,) * 8,
        scratch_shapes=scratch,
        compiler_params=pltpu.CompilerParams(
            collective_id=identity, has_side_effects=True, vmem_limit_bytes=62 << 20
        ),
        cost_estimate=pl.CostEstimate(
            flops=80 * pixels * channels * channels, bytes_accessed=60 << 20, transcendentals=0
        ),
        name="backward",
    )(info, embed, *gains, stats, shifts, *arrays)


def own_shards(
    info, image, embed, text, gain1, conv1_w, embed_w, gain2, conv2_w, gain3, qkv_w, text_w, proj_w,
    cotangent,
):
    _, rows_dev, width, channels = image.shape
    items, parts = lax.axis_size("items"), lax.axis_size("rows")
    me = lax.axis_index("rows")
    head_dim = channels // HEADS
    tokens = text.shape[1]
    share = channels // parts
    (first, middle, cot, hidden_all, second_all, attn_flat, qkv_turned, qkv_pair, go_pair, text_pair, text_cols,
     stats, shifts) = forward_call(
        info,
        image[0],
        cotangent[0],
        text[0],
        embed,
        (gain1, gain2, gain3),
        (
            conv1_w.reshape(3, 3 * channels, channels),
            conv2_w.reshape(3, 3 * channels, channels),
            embed_w,
            text_w,
            qkv_w,
            proj_w,
        ),
        0,
    )
    stats1, stats2, stats3 = stats[0:1], stats[1:2], stats[2:3]
    attended, qkv_grad_pair, text_grad_pair = attention(
        info[:, :2], qkv_pair, text_pair.reshape(parts * tokens, 2 * head_dim), go_pair, width
    )

    text_w_rows = text_cols.shape[3]
    (output, image_grad, conv1_total, conv2_total, qkv_total, proj_total, vectors, text_grad, text_w_grad,
     embed_grad) = backward_call(
        info,
        embed,
        (gain1, gain2, gain3),
        stats,
        shifts,
        (
            attended,
            qkv_grad_pair,
            text_grad_pair.reshape(parts, tokens, 2 * head_dim),
            first,
            middle,
            cot,
            image[0],
            hidden_all,
            second_all,
            attn_flat,
            qkv_turned,
            text_cols.reshape(items * parts, tokens, text_w_rows),
            proj_w,
            conv1_w.reshape(9 * channels, channels),
            conv2_w.reshape(9 * channels, channels),
            text_w,
            embed_w,
        ),
        1,
    )
    embed_rows = embed.shape[1] // channels
    all_shifts = vectors[:, 3:5].reshape(items, 2 * channels).astype(BF16)
    all_embed = vectors[:, 5 : 5 + embed_rows].reshape(items, embed.shape[1]).astype(BF16)
    embed_share = embed_w.shape[0] // parts
    own_embed = lax.dynamic_slice_in_dim(all_embed, me * embed_share, embed_share, 1)
    embed_w_grad = jnp.einsum("ic,ik->ck", own_embed, all_shifts, preferred_element_type=F32)
    gains = jnp.sum(vectors[:, :3], axis=0)
    gains = lax.dynamic_slice_in_dim(gains, me * share, share, 1)
    return (
        output[None],
        image_grad[None],
        embed_grad,
        text_grad[None],
        gains[0],
        conv1_total.reshape(3, 3, channels, share),
        embed_w_grad,
        gains[1],
        conv2_total.reshape(3, 3, channels, share),
        gains[2],
        qkv_total,
        text_w_grad,
        proj_total,
    )


def shards(
    image, embed, text, extent, first_norm_gain1, conv1_w, embed_w, second_norm_gain2, conv2_w,
    attention_norm_gain, qkv_w, text_w, proj_w, cotangent,
):
    images, rows_dev, width, channels = image.shape
    parts = lax.axis_size("rows")
    me = lax.axis_index("rows")
    pairs = images * HEADS // parts
    head_dim = channels // HEADS
    pixels = rows_dev * width
    group = max(1, 512 // pixels)
    span = group * pixels
    chunks = parts // group
    tokens = text.shape[1]
    first_row = jnp.full((images, 1), me * rows_dev, jnp.int32)
    info = jnp.concatenate([extent, first_row], axis=1)
    gain1 = first_norm_gain1.reshape(1, channels)
    gain2 = second_norm_gain2.reshape(1, channels)
    gain3 = attention_norm_gain.reshape(1, channels)
    rowpos = me * rows_dev + jnp.arange(rows_dev, dtype=jnp.int32)
    colpos = jnp.arange(width, dtype=jnp.int32)
    inside = (rowpos[None, :, None] < extent[:, 0, None, None]) & (
        colpos[None, None, :] < extent[:, 1, None, None]
    )
    image_window = inside.astype(F32)[..., None]

    items = lax.axis_size("items")
    own_path = (
        images == 1
        and parts == HEADS
        and channels % (16 * items * parts) == 0
        and pixels % 512 == 0
        and tokens % 16 == 0
        and text.shape[2] % (128 * parts) == 0
        and text.shape[2] == embed.shape[1] <= 4 * channels
    )
    if own_path:
        return own_shards(
            info, image, embed, text, gain1, conv1_w, embed_w, gain2, conv2_w, gain3, qkv_w, text_w,
            proj_w, cotangent,
        )

    embed_float = embed.astype(F32)
    embed_low = jax.nn.silu(embed_float).astype(BF16)
    shifts = jnp.dot(embed_low, embed_w, preferred_element_type=F32)
    qkv_turned = qkv_w.T
    proj_shaped = proj_w.reshape(HEADS, head_dim, channels)

    start = image.astype(F32) * image_window
    zeros = jnp.zeros((images, 6, channels), F32)
    stats0 = jnp.concatenate(
        [
            jnp.sum(start, axis=(1, 2))[:, None],
            jnp.sum(start * start, axis=(1, 2))[:, None],
            zeros,
        ],
        axis=1,
    )
    stats1, image_above, image_below, cot_above, cot_below = exchange(
        stats0, (image, cotangent), 0
    )
    full = jax.ShapeDtypeStruct(image.shape, F32)
    sums = jax.ShapeDtypeStruct((images, 8, channels), F32)
    padded = jax.ShapeDtypeStruct((images, rows_dev + 2, width, channels), BF16)
    first, stats, hidden = conv_call(
        conv1_kernel,
        info,
        (image, image_above, image_below, stats1, gain1),
        conv1_w,
        (full, sums, padded),
        False,
    )
    stats2, first_above, first_below, all_text = exchange(stats, (first,), 1, (text,))
    gathered_text = jnp.moveaxis(all_text, 0, 1).reshape(images, parts * tokens, text.shape[2])
    text_share = text.shape[2] // parts
    text_cols = lax.dynamic_slice_in_dim(gathered_text, me * text_share, text_share, 2)
    text_cols = lax.all_gather(text_cols, "items", axis=0, tiled=True)
    middle, stats, second = conv_call(
        conv2_kernel,
        info,
        (first, first_above, first_below, stats2, gain2, shifts, image),
        conv2_w,
        (full, sums, padded),
        False,
    )
    stats3, mid_above, mid_below = exchange(stats, (middle,), 2)
    attn_flat, qkv_pix = project(info, middle, stats3, gain3, qkv_turned)

    def to_pairs(values):
        wide = values.shape[1]
        moved = lax.all_to_all(values, "rows", split_axis=0, concat_axis=0, tiled=True)
        moved = moved.reshape(chunks, group, pairs, wide, pixels)
        return jnp.transpose(moved, (2, 0, 3, 1, 4)).reshape(pairs, chunks, wide, span)

    def from_pairs(values):
        wide = values.shape[2]
        moved = values.reshape(pairs, chunks, wide, group, pixels)
        moved = jnp.transpose(moved, (1, 3, 0, 2, 4)).reshape(parts * pairs, wide, pixels)
        return lax.all_to_all(moved, "rows", split_axis=0, concat_axis=0, tiled=True)

    qkv_pair = to_pairs(qkv_pix)
    grad_proj = (cotangent.astype(F32) * image_window).astype(BF16).reshape(images, pixels, channels)
    grad_heads = jnp.einsum(
        "ipc,hdc->ihdp", grad_proj, proj_shaped, preferred_element_type=F32
    ).astype(BF16)
    grad_pair = to_pairs(grad_heads.reshape(images * HEADS, head_dim, pixels))
    pair_results = []
    for p in range(pairs):
        pair = me * pairs + p
        item, head = pair // HEADS, pair % HEADS
        weight = lax.dynamic_slice_in_dim(text_w, head * 2 * head_dim, 2 * head_dim, 1)
        own = lax.dynamic_index_in_dim(gathered_text, item, 0, False)
        text_pair = jnp.dot(own, weight, preferred_element_type=F32).astype(BF16)
        pair_extent = lax.dynamic_slice_in_dim(extent, item, 1, 0)
        pair_results.append(attention(pair_extent, qkv_pair[p], text_pair, grad_pair[p], width))
    attended, qkv_grad_pair, text_grad_pair = (jnp.stack(r) for r in zip(*pair_results))
    qkv_back = from_pairs(qkv_grad_pair)
    heads_out = from_pairs(attended).reshape(images, HEADS, head_dim, pixels)

    attn_grad, stats = unproject(info, middle, stats3, qkv_back, qkv_turned)
    stats4, grad_above, grad_below, text_back = exchange(stats, (attn_grad,), 3, (text_grad_pair,))
    text_back = text_back.reshape(images, HEADS, parts * tokens, 2 * head_dim)
    text_all = lax.all_gather(text_back, "items", axis=0, tiled=True)
    proj_grad = jnp.einsum("ipc,ihdp->chd", grad_proj, heads_out, preferred_element_type=F32)
    qkv_grad = jnp.einsum(
        "ihwdp,ipc->hdwc",
        qkv_back.reshape(images, HEADS, 3, head_dim, pixels),
        attn_flat,
        preferred_element_type=F32,
    )
    grad_middle, moved_grad, stats, conv2_grad = conv_call(
        back2_kernel,
        info,
        (attn_grad, grad_above, grad_below, middle, mid_above, mid_below, cotangent, cot_above,
         cot_below, stats3, stats4, gain3, first, stats2, gain2, shifts),
        conv2_w,
        (full, full, sums, padded),
        True,
    )
    stats5, moved_above, moved_below = exchange(stats, (moved_grad,), 4)
    pre_grad, stats, conv1_grad = conv_call(
        back1_kernel,
        info,
        (moved_grad, moved_above, moved_below, first, first_above, first_below, stats2, stats5,
         gain2, shifts, image, stats1, gain1),
        conv1_w,
        (full, sums, padded),
        True,
    )
    (stats6,) = exchange(stats, (), 5)
    image_grad = finish(info, pre_grad, stats6, image, stats1, gain1, grad_middle)

    projected = jnp.einsum(
        "ihdp,hdc->ipc", heads_out, proj_shaped, preferred_element_type=F32
    ).reshape(image.shape)
    output = (middle + projected * image_window).astype(BF16)
    own_text = lax.dynamic_slice_in_dim(text_back, me * tokens, tokens, 2)
    text_shaped = text_w.reshape(text_w.shape[0], HEADS, 2 * head_dim)
    text_grad = jnp.einsum("ihtk,chk->itc", own_text, text_shaped, preferred_element_type=F32)
    text_w_grad = jnp.einsum(
        "gtc,ghtk->chk", text_cols, text_all, preferred_element_type=F32
    ).reshape(text_share, 2 * channels)
    scale_sum = stats5[:, 1] * gain2
    grad_shifts = jnp.concatenate([scale_sum, stats5[:, 0]], axis=1).astype(BF16)
    embed_grad = jnp.einsum(
        "ik,ck->ic", grad_shifts, embed_w, preferred_element_type=F32
    ) * silu_slope(embed_float)
    embed_share = embed_w.shape[0] // parts
    gains = jnp.stack(
        [
            jnp.sum(stats6[:, 1], axis=0),
            jnp.sum(stats5[:, 1] * (1.0 + shifts[:, :channels]), axis=0),
            jnp.sum(stats4[:, 1], axis=0),
        ]
    )
    share = channels // parts
    def total(values):
        return lax.psum(
            lax.psum_scatter(values.astype(BF16), "rows", scatter_dimension=0, tiled=True),
            "items",
        ).astype(F32)

    def kernel_total(values):
        return total(values).T.reshape(3, 3, channels, share)

    conv1_total = kernel_total(weight_grad(conv1_grad, hidden))
    conv2_total = kernel_total(weight_grad(conv2_grad, second))
    by_head = jnp.swapaxes(qkv_grad, 1, 2).reshape(3 * channels, channels)
    qkv_total = total(by_head).T
    proj_total = total(proj_grad.reshape(channels, channels)).T
    gains = lax.psum(gains, "items")
    all_shifts = lax.all_gather(grad_shifts, "items", axis=0, tiled=True)
    embed_rows = lax.dynamic_slice_in_dim(embed_low, me * embed_share, embed_share, 1)
    embed_rows = lax.all_gather(embed_rows, "items", axis=0, tiled=True)
    embed_w_grad = jnp.einsum("ic,ik->ck", embed_rows, all_shifts, preferred_element_type=F32)
    gains = lax.dynamic_slice_in_dim(gains, me * share, share, 1)
    return (
        output,
        image_grad,
        embed_grad,
        text_grad,
        gains[0],
        conv1_total,
        embed_w_grad,
        gains[1],
        conv2_total,
        gains[2],
        qkv_total,
        text_w_grad,
        proj_total,
    )


def solution(mesh):
    in_specs = (
        P("items", "rows", None, None),
        P("items", None),
        P("items", "rows", None),
        P("items", None),
        P(),
        P(),
        P(),
        P(),
        P(),
        P(),
        P(),
        P(),
        P(),
        P("items", "rows", None, None),
    )
    out_specs = (
        P("items", "rows", None, None),
        P("items", "rows", None, None),
        P("items", None),
        P("items", "rows", None),
        P("rows"),
        P(None, None, None, "rows"),
        P("rows", None),
        P("rows"),
        P(None, None, None, "rows"),
        P("rows"),
        P(None, "rows"),
        P("rows", None),
        P(None, "rows"),
    )
    return jax.shard_map(shards, mesh=mesh, in_specs=in_specs, out_specs=out_specs, check_vma=False)
```

```python
import functools

import jax
import jax.numpy as jnp
from jax import lax
from jax.experimental import pallas as pl
from jax.experimental.pallas import tpu as pltpu
from jax.sharding import PartitionSpec as P

GROUPS = 32
HEADS = 8
F32, BF16 = jnp.float32, jnp.bfloat16
NEG = -1e30


def dot(a, b, ca, cb):
    return lax.dot_general(a, b, (((ca,), (cb,)), ((), ())), preferred_element_type=F32)

def nothing(*_):
    return None


class Attention:
    def __init__(self, chunks, span, d, tlen, step, bq, scratch):
        self.chunks, self.span, self.d, self.tlen, self.step, self.bq = chunks, span, d, tlen, step, bq
        self.kn, self.vn, self.kt, self.vt, s0, s1, e0, e1, self.dkt, self.dvt = scratch
        self.scores, self.raised = (s0, s1), (e0, e1)
        self.pix = chunks * span

    def stage_key(self, c, k, width, rows_ok, cols_ok):
        d, span = self.d, self.span
        base = pl.multiple_of(c * span, span)
        pos = base + lax.broadcasted_iota(jnp.int32, (16, span), 1)
        row = lax.broadcasted_iota(jnp.int32, (16, span), 0)
        ok = (pos // width < rows_ok) & (pos % width < cols_ok)
        extra = jnp.where((row == 0) & jnp.logical_not(ok), NEG, 0.0)
        rest = jnp.zeros((128 - d - 16, span), F32)
        self.kt[:, pl.ds(base, span)] = k
        ka = jnp.concatenate([k.astype(F32), extra, rest], axis=0)
        self.kn[pl.ds(base, span), :] = ka.T.astype(BF16)

    def stage_value(self, c, v):
        d, span = self.d, self.span
        base = pl.multiple_of(c * span, span)
        row = lax.broadcasted_iota(jnp.int32, (16, span), 0)
        rest = jnp.zeros((128 - d - 16, span), F32)
        self.vt[:, pl.ds(base, span)] = v
        va = jnp.concatenate([v.astype(F32), jnp.where(row < 3, 1.0, 0.0), rest], axis=0)
        self.vn[pl.ds(base, span), :] = va.T.astype(BF16)

    def stage_text(self, text):
        d, tlen, pix = self.d, self.tlen, self.pix
        tk = text[:, :d].astype(F32)
        tv = text[:, d:].astype(F32)
        self.kt[:, pix:] = tk.T.astype(BF16)
        self.vt[:, pix:] = tv.T.astype(BF16)
        lanes = lax.broadcasted_iota(jnp.int32, (tlen, 128 - d), 1)
        rest = jnp.zeros((tlen, 128 - d), F32)
        self.kn[pix:, :] = jnp.concatenate([tk, rest], axis=1).astype(BF16)
        ones = jnp.where(lanes < 3, 1.0, 0.0)
        self.vn[pix:, :] = jnp.concatenate([tv, ones], axis=1).astype(BF16)

    def query(self, q):
        d, bq = self.d, self.bq
        r = lax.broadcasted_iota(jnp.int32, (128 - d, bq), 0)
        rest = jnp.where(r == 0, 1.0, 0.0)
        return jnp.concatenate([q.astype(F32) * (d**-0.5), rest], axis=0).astype(BF16)

    def run(self, score, exp, back):
        d, bq, step = self.d, self.bq, self.step
        kn, vn, kt, vt, dkt, dvt = self.kn, self.vn, self.kt, self.vt, self.dkt, self.dvt
        scores, raised = self.scores, self.raised

        def body(j, carry):
            pk, total, acc, dq = carry
            at = pl.ds(pl.multiple_of(j * step, step), step)
            if score:
                slot, qa = score
                s = dot(kn[at, :], qa, 1, 0)
                scores[slot][at, :] = s
                pk = jnp.maximum(pk, jnp.max(s.reshape(step // 8, 8, bq), axis=0))
            if exp:
                slot, peak = exp
                e = jnp.exp(scores[slot][at, :] - peak)
                total = total + jnp.sum(e.reshape(step // 8, 8, bq), axis=0)
                low = e.astype(BF16)
                raised[slot][at, :] = low
                acc = acc + dot(vt[:, at], low, 1, 0)
            if back:
                slot, goa, q = back
                dp = dot(vn[at, :], goa, 1, 0)
                e = raised[slot][at, :]
                ds = (e.astype(F32) * dp).astype(BF16)
                dvt[:, at] += dot(goa[:d], e, 1, 1)
                dkt[:, at] += dot(q, ds, 1, 1)
                dq = dq + dot(kt[:, at], ds, 1, 0)
            return pk, total, acc, dq

        init = (
            jnp.full((8, bq), -3e38, F32),
            jnp.zeros((8, bq), F32),
            jnp.zeros((d, bq), F32),
            jnp.zeros((d, bq), F32),
        )
        return lax.fori_loop(0, (self.pix + self.tlen) // step, body, init)

    def attended(self, go, total, acc):
        d, bq = self.d, self.bq
        inv = 1.0 / jnp.sum(total, axis=0, keepdims=True)
        o = acc * inv
        go = go.astype(F32)
        nd = -jnp.sum(go * o, axis=0, keepdims=True) * inv
        hi = nd.astype(BF16).astype(F32)
        mid = (nd - hi).astype(BF16).astype(F32)
        lo = nd - hi - mid
        r = lax.broadcasted_iota(jnp.int32, (16, bq), 0)
        extra = jnp.where(r == 0, hi, jnp.where(r == 1, mid, jnp.where(r == 2, lo, 0.0)))
        rest = jnp.zeros((128 - d - 16, bq), F32)
        return o.astype(BF16), jnp.concatenate([go * inv, extra, rest], axis=0).astype(BF16)

    def attend(self, q_ref, go_ref, o_ref, dq_ref, order, scored=nothing, before=nothing, done=nothing):
        d, bq, chunks = self.d, self.bq, self.chunks
        self.dkt[...] = jnp.zeros_like(self.dkt)
        self.dvt[...] = jnp.zeros_like(self.dvt)

        def columns(half):
            return slice(half * bq, (half + 1) * bq)

        def q_of(h, half):
            return q_ref[order(h), :d, columns(half)]

        def finish_exp(h, half, total, acc):
            c = order(h)
            o, goa = self.attended(go_ref[c, :, columns(half)], total, acc)
            o_ref[c, :, columns(half)] = o
            return goa

        def put_dq(h, half, dq):
            dq_ref[order(h), :d, columns(half)] = (dq * (d**-0.5)).astype(BF16)

        def top(pk):
            return jnp.max(pk, axis=0, keepdims=True)

        run = self.run
        pk, _, _, _ = run((0, self.query(q_of(0, 0))), None, None)
        scored()
        pk, total, acc, _ = run((1, self.query(q_of(0, 1))), (0, top(pk)), None)
        goa = finish_exp(0, 0, total, acc)

        def two(h, carry):
            pk, goa = carry
            before(h + 1)
            qa = self.query(q_of(h + 1, 0))
            pk2, total, acc, dq = run((0, qa), (1, top(pk)), (0, goa, q_of(h, 0)))
            put_dq(h, 0, dq)
            goa = finish_exp(h, 1, total, acc)
            qa = self.query(q_of(h + 1, 1))
            pk3, total, acc, dq = run((1, qa), (0, top(pk2)), (1, goa, q_of(h, 1)))
            put_dq(h, 1, dq)
            done(h)
            return pk3, finish_exp(h + 1, 0, total, acc)

        pk, goa = lax.fori_loop(0, chunks - 1, two, (pk, goa))
        last = chunks - 1
        _, total, acc, dq = run(None, (1, top(pk)), (0, goa, q_of(last, 0)))
        put_dq(last, 0, dq)
        goa = finish_exp(last, 1, total, acc)
        _, _, _, dq = run(None, None, (1, goa, q_of(last, 1)))
        put_dq(last, 1, dq)
        done(last)

    def key_grad(self, at):
        return (self.dkt[:, at] * (self.d**-0.5)).astype(BF16)

    def value_grad(self, at):
        return self.dvt[:, at].astype(BF16)

    def text_grad(self, out):
        d, pix = self.d, self.pix
        out[:, :d] = (self.dkt[:, pix:] * (d**-0.5)).T.astype(BF16)
        out[:, d:] = self.dvt[:, pix:].T.astype(BF16)


def attention_scratch(chunks, span, d, tlen):
    keys = chunks * span + tlen
    bq = span // 2
    lanes = keys // 128
    step = 128 * max(n for n in range(1, 12) if lanes % n == 0)
    shapes = [((keys, 128), BF16)] * 2 + [((d, keys), BF16)] * 2
    shapes += [((keys, bq), F32)] * 2 + [((keys, bq), BF16)] * 2 + [((d, keys), F32)] * 2
    return step, bq, [pltpu.VMEM(*shape) for shape in shapes]


def attention_kernel(width, step, bq, ext_ref, qkv_ref, text_ref, go_ref, out_ref, dqkv_ref, dtext_ref, *scratch):
    chunks, _, span = qkv_ref.shape
    d = go_ref.shape[1]
    att = Attention(chunks, span, d, text_ref.shape[0], step, bq, scratch)

    def stage(c, carry):
        att.stage_key(c, qkv_ref[c, d : 2 * d, :], width, ext_ref[0, 0], ext_ref[0, 1])
        att.stage_value(c, qkv_ref[c, 2 * d :, :])
        return carry

    lax.fori_loop(0, chunks, stage, 0)
    att.stage_text(text_ref)
    att.attend(qkv_ref, go_ref, out_ref, dqkv_ref, lambda h: h)

    def finish(c, carry):
        at = pl.ds(pl.multiple_of(c * span, span), span)
        dqkv_ref[c, d : 2 * d, :] = att.key_grad(at)
        dqkv_ref[c, 2 * d :, :] = att.value_grad(at)
        return carry

    lax.fori_loop(0, chunks, finish, 0)
    att.text_grad(dtext_ref)


def attention(ext, qkv, text, go, width):
    chunks, wide, span = qkv.shape
    d = wide // 3
    tlen = text.shape[0]
    keys = chunks * span + tlen
    step, bq, scratch = attention_scratch(chunks, span, d, tlen)
    vm = pl.BlockSpec(memory_space=pltpu.VMEM)
    flops = 2 * 6 * chunks * span * keys * d
    return pl.pallas_call(
        functools.partial(attention_kernel, width, step, bq),
        out_shape=(
            jax.ShapeDtypeStruct(go.shape, BF16),
            jax.ShapeDtypeStruct(qkv.shape, BF16),
            jax.ShapeDtypeStruct((tlen, 2 * d), BF16),
        ),
        in_specs=[pl.BlockSpec(memory_space=pltpu.SMEM), vm, vm, vm],
        out_specs=(vm, vm, vm),
        scratch_shapes=scratch,
        compiler_params=pltpu.CompilerParams(vmem_limit_bytes=56 << 20),
        cost_estimate=pl.CostEstimate(
            flops=4 * flops, bytes_accessed=16 * chunks * span * d, transcendentals=chunks * span * keys
        ),
    )(ext, qkv, text, go)


MESH = pl.DeviceIdType.MESH
EPS = 1e-05
WHOLE = pl.BlockSpec(memory_space=pltpu.VMEM)
SCALARS = pl.BlockSpec(memory_space=pltpu.SMEM)
ANYWHERE = pl.BlockSpec(memory_space=pl.ANY)


def exchange_kernel(n, count, gathers, *refs):
    inputs, refs = refs[: 1 + count + gathers], refs[1 + count + gathers :]
    outputs, refs = refs[: 1 + 2 * count + gathers], refs[1 + 2 * count + gathers :]
    stats_ref, rows, given = inputs[0], inputs[1 : 1 + count], inputs[1 + count :]
    total_ref, outs, gathered = outputs[0], outputs[1 : 1 + 2 * count], outputs[1 + 2 * count :]
    slots, lands = refs[0], refs[1 : 1 + 2 * count]
    send, recv, row_send, row_recv, own = refs[1 + 2 * count :]
    me = lax.axis_index("rows")
    barrier = pltpu.get_barrier_semaphore()

    def greet(k, carry):
        pl.semaphore_signal(
            barrier, inc=1, device_id={"rows": lax.rem(me + k, n)}, device_id_type=MESH
        )
        return carry

    lax.fori_loop(1, n, greet, 0)
    slots[me] = stats_ref[...]
    pl.semaphore_wait(barrier, n - 1)
    shared = [(stats_ref, slots)] + list(zip(given, gathered))

    def share(j, k):
        return pltpu.make_async_remote_copy(
            src_ref=shared[j][0],
            dst_ref=shared[j][1].at[me],
            send_sem=send.at[j, k],
            recv_sem=recv.at[j, k],
            device_id={"rows": lax.rem(me + k, n)},
            device_id_type=MESH,
        )

    def start(k, carry):
        share(0, k).start()
        return carry

    lax.fori_loop(1, n, start, 0)

    def row_copy(j, side):
        last = rows[j].shape[1] - 1
        at = last if side == 0 else 0
        return pltpu.make_async_remote_copy(
            src_ref=rows[j].at[:, at : at + 1],
            dst_ref=lands[2 * j + side],
            send_sem=row_send.at[2 * j + side],
            recv_sem=row_recv.at[2 * j + side],
            device_id={"rows": me + 1 if side == 0 else me - 1},
            device_id_type=MESH,
        )

    for j in range(count):

        @pl.when(me < n - 1)
        def _():
            row_copy(j, 0).start()

        @pl.when(me > 0)
        def _():
            row_copy(j, 1).start()

    for j in range(gathers):

        def start_given(k, carry):
            share(1 + j, k).start()
            return carry

        lax.fori_loop(1, n, start_given, 0)
        pltpu.make_async_copy(given[j], gathered[j].at[me], own.at[j]).start()

    def finish(k, carry):
        share(0, k).wait()
        return carry

    lax.fori_loop(1, n, finish, 0)
    total_ref[...] = lax.fori_loop(1, n, lambda k, s: s + slots[k], slots[0])
    for j in range(count):

        @pl.when(me > 0)
        def _():
            row_copy(j, 0).wait_recv()
            outs[2 * j][...] = lands[2 * j][...]

        @pl.when(me == 0)
        def _():
            outs[2 * j][...] = jnp.zeros_like(outs[2 * j])

        @pl.when(me < n - 1)
        def _():
            row_copy(j, 1).wait_recv()
            outs[2 * j + 1][...] = lands[2 * j + 1][...]
            row_copy(j, 0).wait_send()

        @pl.when(me == n - 1)
        def _():
            outs[2 * j + 1][...] = jnp.zeros_like(outs[2 * j + 1])

        @pl.when(me > 0)
        def _():
            row_copy(j, 1).wait_send()

    for j in range(gathers):

        def finish_given(k, carry):
            share(1 + j, k).wait()
            return carry

        lax.fori_loop(1, n, finish_given, 0)
        pltpu.make_async_copy(given[j], gathered[j].at[me], own.at[j]).wait()


def exchange(stats, rows, identity, given=()):
    n = lax.axis_size("rows")
    edge = []
    for array in rows:
        edge += [jax.ShapeDtypeStruct(array.shape[:1] + (1,) + array.shape[2:], array.dtype)] * 2
    whole = [jax.ShapeDtypeStruct((n,) + array.shape, array.dtype) for array in given]
    count, gathers = len(rows), len(given)
    nbytes = 4 * stats.size * n + sum(2 * e.size * e.dtype.itemsize for e in (*edge, *whole))
    return pl.pallas_call(
        functools.partial(exchange_kernel, n, count, gathers),
        out_shape=(jax.ShapeDtypeStruct(stats.shape, F32), *edge, *whole),
        in_specs=[WHOLE] + [ANYWHERE] * (count + gathers),
        out_specs=(WHOLE,) * (1 + 2 * count) + (ANYWHERE,) * gathers,
        scratch_shapes=[
            pltpu.VMEM((n,) + stats.shape, F32),
            *[pltpu.VMEM(e.shape, e.dtype) for e in edge],
            pltpu.SemaphoreType.DMA((1 + gathers, n)),
            pltpu.SemaphoreType.DMA((1 + gathers, n)),
            pltpu.SemaphoreType.DMA((max(1, 2 * count),)),
            pltpu.SemaphoreType.DMA((max(1, 2 * count),)),
            pltpu.SemaphoreType.DMA((max(1, gathers),)),
        ],
        compiler_params=pltpu.CompilerParams(collective_id=identity, has_side_effects=True),
        cost_estimate=pl.CostEstimate(
            flops=6_000_000_000, bytes_accessed=nbytes, transcendentals=0
        ),
        name=f"exchange{identity}",
    )(stats, *rows, *given)


def group_sums(rows):
    channels = rows.shape[1]
    size = channels // GROUPS
    one = lax.broadcasted_iota(jnp.int32, (channels, channels), 0) // size
    two = lax.broadcasted_iota(jnp.int32, (channels, channels), 1) // size
    same = jnp.where(one == two, 1.0, 0.0).astype(BF16)
    high = rows.astype(BF16)
    rest = rows - high.astype(F32)
    mid = rest.astype(BF16)
    tail = (rest - mid.astype(F32)).astype(BF16)
    return dot(high, same, 1, 0) + dot(mid, same, 1, 0) + dot(tail, same, 1, 0)


def image_count(info, i, channels):
    return (info[i, 0] * info[i, 1]).astype(F32) * (channels // GROUPS)


def norm_of(stats, count):
    sums = group_sums(stats)
    average = sums[0:1] / count
    square = sums[1:2] / count
    return average, lax.rsqrt(square - average * average + EPS)


def means_of(stats, weight, count):
    sums = group_sums(stats * weight)
    return sums[0:1] / count, sums[1:2] / count


def window(info, i, row, shape):
    ok = (row >= 0) & (row < info[i, 0])
    limit = jnp.where(ok, info[i, 1], 0)
    return jnp.where(lax.broadcasted_iota(jnp.int32, shape, 0) < limit, 1.0, 0.0)


def padded_row(center, above, below, i, r):
    if r == 0:
        return above[i, 0]
    if r == center.shape[1] + 1:
        return below[i, 0]
    return center[i, r - 1]


def put_shifted(out, i, r, value, plain=None):
    width, channels = value.shape
    column = lax.broadcasted_iota(jnp.int32, value.shape, 0)
    left = jnp.where(column == 0, 0.0, pltpu.roll(value, 1, 0))
    right = jnp.where(column == width - 1, 0.0, pltpu.roll(value, width - 1, 0))
    out[i, r, :, :channels] = left.astype(BF16)
    low = value.astype(BF16)
    out[i, r, :, channels : 2 * channels] = low
    if plain is not None:
        plain[i, r] = low
    out[i, r, :, 2 * channels :] = right.astype(BF16)


def sigmoid(v):
    return 1.0 / (1.0 + jnp.exp(-v))


def silu_slope(v):
    s = sigmoid(v)
    return s * (1.0 + v * (1.0 - s))


def put_stats(stats_ref, i, first, second):
    channels = first.shape[1]
    one = jnp.sum(first, axis=0, keepdims=True)
    two = jnp.sum(second, axis=0, keepdims=True)
    row = lax.broadcasted_iota(jnp.int32, (8, channels), 0)
    stats_ref[i] = jnp.where(row == 0, one, jnp.where(row == 1, two, 0.0))


def tap_rows(shifted, tap, images, rows_dev, width):
    block = shifted[:, pl.ds(tap, rows_dev)]
    return block.reshape(images * rows_dev * width, shifted.shape[3])


def conv1_kernel(info, image, above, below, stats, gain, weight, first, out_stats, hidden, acc, shifted):
    images, rows_dev, width, channels = image.shape
    tap = pl.program_id(0)
    base = info[0, 2]

    @pl.when(tap == 0)
    def _():
        for i in range(images):
            average, inverse = norm_of(stats[i], image_count(info, i, channels))
            for r in range(rows_dev + 2):
                inside = window(info, i, base + r - 1, (width, channels))
                start = padded_row(image, above, below, i, r).astype(F32) * inside
                value = (start - average) * inverse * inside * gain[...]
                put_shifted(shifted, i, r, value * sigmoid(value) * inside, hidden)

    part = dot(tap_rows(shifted, tap, images, rows_dev, width), weight[0], 1, 0)

    @pl.when(tap == 0)
    def _():
        acc[...] = part

    @pl.when(tap > 0)
    def _():
        acc[...] += part

    @pl.when(tap == 2)
    def _():
        for i in range(images):
            one = two = jnp.zeros((width, channels), F32)
            for r in range(rows_dev):
                inside = window(info, i, base + r, (width, channels))
                at = (i * rows_dev + r) * width
                value = acc[at : at + width] * inside
                first[i, r] = value
                one = one + value
                two = two + value * value
            put_stats(out_stats, i, one, two)


def moved_of(value, inside, average, inverse, gain, scale, shift):
    normal = (value - average) * inverse * inside
    return normal, normal * gain * (1.0 + scale) + shift


def conv2_kernel(
    info, first, above, below, stats, gain, shifts, image, weight, middle, out_stats, second, acc,
    shifted,
):
    images, rows_dev, width, channels = first.shape
    tap = pl.program_id(0)
    base = info[0, 2]

    @pl.when(tap == 0)
    def _():
        for i in range(images):
            average, inverse = norm_of(stats[i], image_count(info, i, channels))
            scale, shift = shifts[i : i + 1, :channels], shifts[i : i + 1, channels:]
            for r in range(rows_dev + 2):
                inside = window(info, i, base + r - 1, (width, channels))
                value = padded_row(first, above, below, i, r)
                _, moved = moved_of(value, inside, average, inverse, gain[...], scale, shift)
                put_shifted(shifted, i, r, moved * sigmoid(moved) * inside, second)

    part = dot(tap_rows(shifted, tap, images, rows_dev, width), weight[0], 1, 0)

    @pl.when(tap == 0)
    def _():
        acc[...] = part

    @pl.when(tap > 0)
    def _():
        acc[...] += part

    @pl.when(tap == 2)
    def _():
        for i in range(images):
            one = two = jnp.zeros((width, channels), F32)
            for r in range(rows_dev):
                inside = window(info, i, base + r, (width, channels))
                at = (i * rows_dev + r) * width
                value = (image[i, r].astype(F32) + acc[at : at + width]) * inside
                middle[i, r] = value
                one = one + value
                two = two + value * value
            put_stats(out_stats, i, one, two)


def dgrad(shifted, tap, weight, images, rows_dev, width):
    channels = weight.shape[2]
    lhs = tap_rows(shifted, tap, images, rows_dev, width)
    part = None
    for b in range(3):
        term = dot(
            lhs[:, b * channels : (b + 1) * channels],
            weight[0, (2 - b) * channels : (3 - b) * channels, :],
            1,
            1,
        )
        part = term if part is None else part + term
    return part


def back2_kernel(
    info, grad, grad_above, grad_below, middle, mid_above, mid_below, cot, cot_above, cot_below,
    mid_stats, grad_stats, attn_gain, first, first_stats, gain, shifts, weight,
    grad_middle, moved_grad, out_stats, plain, acc, shifted,
):
    images, rows_dev, width, channels = first.shape
    tap = pl.program_id(0)
    base = info[0, 2]

    @pl.when(tap == 0)
    def _():
        for i in range(images):
            count = image_count(info, i, channels)
            average, inverse = norm_of(mid_stats[i], count)
            mean, cross = means_of(grad_stats[i], attn_gain[...], count)
            for r in range(rows_dev + 2):
                inside = window(info, i, base + r - 1, (width, channels))
                normal = (padded_row(middle, mid_above, mid_below, i, r) - average) * inverse
                dx = padded_row(grad, grad_above, grad_below, i, r) * attn_gain[...]
                term = (dx - mean - normal * cross) * inverse * inside
                total = padded_row(cot, cot_above, cot_below, i, r).astype(F32) + term
                if 0 < r <= rows_dev:
                    grad_middle[i, r - 1] = total
                put_shifted(shifted, i, r, total * inside, plain)

    part = dgrad(shifted, tap, weight, images, rows_dev, width)

    @pl.when(tap == 0)
    def _():
        acc[...] = part

    @pl.when(tap > 0)
    def _():
        acc[...] += part

    @pl.when(tap == 2)
    def _():
        for i in range(images):
            average, inverse = norm_of(first_stats[i], image_count(info, i, channels))
            scale, shift = shifts[i : i + 1, :channels], shifts[i : i + 1, channels:]
            one = two = jnp.zeros((width, channels), F32)
            for r in range(rows_dev):
                inside = window(info, i, base + r, (width, channels))
                at = (i * rows_dev + r) * width
                normal, moved = moved_of(
                    first[i, r], inside, average, inverse, gain[...], scale, shift
                )
                value = acc[at : at + width] * inside * silu_slope(moved)
                moved_grad[i, r] = value
                one = one + value
                two = two + value * normal
            put_stats(out_stats, i, one, two)


def back1_kernel(
    info, grad, grad_above, grad_below, first, first_above, first_below, first_stats, grad_stats,
    gain, shifts, image, image_stats, first_gain, weight,
    pre_grad, out_stats, plain, acc, shifted,
):
    images, rows_dev, width, channels = first.shape
    tap = pl.program_id(0)
    base = info[0, 2]

    @pl.when(tap == 0)
    def _():
        for i in range(images):
            count = image_count(info, i, channels)
            average, inverse = norm_of(first_stats[i], count)
            factor = gain[...] * (1.0 + shifts[i : i + 1, :channels])
            mean, cross = means_of(grad_stats[i], factor, count)
            for r in range(rows_dev + 2):
                inside = window(info, i, base + r - 1, (width, channels))
                normal = (padded_row(first, first_above, first_below, i, r) - average) * inverse
                dx = padded_row(grad, grad_above, grad_below, i, r) * factor
                put_shifted(shifted, i, r, (dx - mean - normal * cross) * inverse * inside, plain)

    part = dgrad(shifted, tap, weight, images, rows_dev, width)

    @pl.when(tap == 0)
    def _():
        acc[...] = part

    @pl.when(tap > 0)
    def _():
        acc[...] += part

    @pl.when(tap == 2)
    def _():
        for i in range(images):
            average, inverse = norm_of(image_stats[i], image_count(info, i, channels))
            one = two = jnp.zeros((width, channels), F32)
            for r in range(rows_dev):
                inside = window(info, i, base + r, (width, channels))
                at = (i * rows_dev + r) * width
                normal = (image[i, r].astype(F32) - average) * inverse * inside
                slope = silu_slope(normal * first_gain[...])
                value = acc[at : at + width] * inside * slope
                pre_grad[i, r] = value
                one = one + value
                two = two + value * normal
            put_stats(out_stats, i, one, two)


def conv_call(kernel, info, inputs, weight, outs, flipped):
    images, rows_dev, width, channels = outs[0].shape

    def whole(shape):
        return pl.BlockSpec(shape, lambda tap: (0,) * len(shape))

    def tap_of(tap):
        return ((2 - tap) if flipped else tap, 0, 0)

    weight = weight.reshape(3, 3 * channels, channels)
    flops = 2 * 9 * images * rows_dev * width * channels * channels
    moved = sum(a.size * a.dtype.itemsize for a in (*inputs, weight, *outs))
    return pl.pallas_call(
        kernel,
        grid=(3,),
        out_shape=tuple(outs),
        in_specs=[SCALARS]
        + [whole(a.shape) for a in inputs]
        + [pl.BlockSpec((1, 3 * channels, channels), tap_of)],
        out_specs=tuple(whole(o.shape) for o in outs),
        scratch_shapes=[
            pltpu.VMEM((images * rows_dev * width, channels), F32),
            pltpu.VMEM((images, rows_dev + 2, width, 3 * channels), BF16),
        ],
        compiler_params=pltpu.CompilerParams(vmem_limit_bytes=48 << 20),
        cost_estimate=pl.CostEstimate(flops=flops, bytes_accessed=moved, transcendentals=0),
        name=kernel.__name__,
    )(info, *inputs, weight)


def weight_grad_kernel(grads, hidden, out, turned, shifted):
    images, padded, width, channels = hidden.shape
    rows_dev = padded - 2
    pixels = images * rows_dev * width
    tap = pl.program_id(0)

    @pl.when(tap == 0)
    def _():
        center = grads[:, 1 : rows_dev + 1]
        turned[...] = center.reshape(pixels, channels).astype(F32).T.astype(BF16)
        for i in range(images):
            for r in range(padded):
                put_shifted(shifted, i, r, hidden[i, r].astype(F32))

    column = pl.multiple_of((tap % 3) * channels, channels)
    rhs = shifted[:, pl.ds(tap // 3, rows_dev), :, pl.ds(column, channels)]
    out[...] = dot(turned[...], rhs.reshape(pixels, channels), 1, 0).astype(BF16)


def weight_grad(grads, hidden):
    images, padded, width, channels = hidden.shape
    pixels = images * (padded - 2) * width

    def whole(shape):
        return pl.BlockSpec(shape, lambda tap: (0,) * len(shape))

    return pl.pallas_call(
        weight_grad_kernel,
        grid=(9,),
        out_shape=jax.ShapeDtypeStruct((channels, 9 * channels), BF16),
        in_specs=[whole(grads.shape), whole(hidden.shape)],
        out_specs=pl.BlockSpec((channels, channels), lambda tap: (0, tap)),
        scratch_shapes=[
            pltpu.VMEM((channels, pixels), BF16),
            pltpu.VMEM(hidden.shape[:3] + (3 * channels,), BF16),
        ],
        compiler_params=pltpu.CompilerParams(vmem_limit_bytes=32 << 20),
        cost_estimate=pl.CostEstimate(
            flops=18 * pixels * channels * channels,
            bytes_accessed=18 * channels * channels,
            transcendentals=0,
        ),
        name="weight_grad",
    )(grads, hidden)


def project_kernel(info, middle, stats, gain, weight, attn, qkv):
    images, rows_dev, width, channels = middle.shape
    pixels = rows_dev * width
    heads, wide = HEADS, weight.shape[0] // HEADS
    base = info[0, 2]
    for i in range(images):
        average, inverse = norm_of(stats[i], image_count(info, i, channels))
        for r in range(rows_dev):
            inside = window(info, i, base + r, (width, channels))
            value = (middle[i, r] - average) * inverse * inside * gain[...]
            attn[i, r * width : (r + 1) * width] = value.astype(BF16)
        for h in range(heads):
            block = dot(weight[h * wide : (h + 1) * wide], attn[i], 1, 1)
            qkv[i * heads + h] = block.astype(BF16)


def project(info, middle, stats, gain, weight):
    images, rows_dev, width, channels = middle.shape
    pixels = rows_dev * width
    return pl.pallas_call(
        project_kernel,
        out_shape=(
            jax.ShapeDtypeStruct((images, pixels, channels), BF16),
            jax.ShapeDtypeStruct((images * HEADS, weight.shape[0] // HEADS, pixels), BF16),
        ),
        in_specs=[SCALARS, WHOLE, WHOLE, WHOLE, WHOLE],
        out_specs=(WHOLE, WHOLE),
        compiler_params=pltpu.CompilerParams(vmem_limit_bytes=32 << 20),
        name="project",
    )(info, middle, stats, gain, weight)


def unproject_kernel(info, middle, stats, grads, weight, out, out_stats):
    images, rows_dev, width, channels = middle.shape
    wide, pixels = grads.shape[1], grads.shape[2]
    base = info[0, 2]
    for i in range(images):
        average, inverse = norm_of(stats[i], image_count(info, i, channels))
        acc = None
        for h in range(HEADS):
            turned = grads[i * HEADS + h].astype(F32).T.astype(BF16)
            term = dot(turned, weight[h * wide : (h + 1) * wide], 1, 0)
            acc = term if acc is None else acc + term
        one = two = jnp.zeros((width, channels), F32)
        for r in range(rows_dev):
            inside = window(info, i, base + r, (width, channels))
            value = acc[r * width : (r + 1) * width] * inside
            out[i, r] = value
            one = one + value
            two = two + value * ((middle[i, r] - average) * inverse)
        put_stats(out_stats, i, one, two)


def unproject(info, middle, stats, grads, weight):
    images, rows_dev, width, channels = middle.shape
    return pl.pallas_call(
        unproject_kernel,
        out_shape=(
            jax.ShapeDtypeStruct(middle.shape, F32),
            jax.ShapeDtypeStruct(stats.shape, F32),
        ),
        in_specs=[SCALARS, WHOLE, WHOLE, WHOLE, WHOLE],
        out_specs=(WHOLE, WHOLE),
        compiler_params=pltpu.CompilerParams(vmem_limit_bytes=32 << 20),
        name="unproject",
    )(info, middle, stats, grads, weight)


def finish_kernel(info, pre_grad, grad_stats, image, stats, gain, grad_middle, out):
    images, rows_dev, width, channels = image.shape
    base = info[0, 2]
    for i in range(images):
        count = image_count(info, i, channels)
        average, inverse = norm_of(stats[i], count)
        mean, cross = means_of(grad_stats[i], gain[...], count)
        for r in range(rows_dev):
            inside = window(info, i, base + r, (width, channels))
            normal = (image[i, r].astype(F32) - average) * inverse
            term = (pre_grad[i, r] * gain[...] - mean - normal * cross) * inverse
            out[i, r] = (grad_middle[i, r] + term) * inside


def finish(info, pre_grad, grad_stats, image, stats, gain, grad_middle):
    return pl.pallas_call(
        finish_kernel,
        out_shape=jax.ShapeDtypeStruct(image.shape, F32),
        in_specs=[SCALARS] + [WHOLE] * 6,
        out_specs=WHOLE,
        compiler_params=pltpu.CompilerParams(vmem_limit_bytes=32 << 20),
        name="finish",
    )(info, pre_grad, grad_stats, image, stats, gain, grad_middle)


DMA = pltpu.SemaphoreType.DMA


def remote(src, dst, send, recv, device):
    return pltpu.make_async_remote_copy(
        src_ref=src,
        dst_ref=dst,
        send_sem=send,
        recv_sem=recv,
        device_id=device,
        device_id_type=MESH,
    )


class Grid:
    def __init__(self, items, n):
        self.items, self.n = items, n
        self.item, self.me = lax.axis_index("items"), lax.axis_index("rows")

    def row(self, k):
        return {"items": self.item, "rows": lax.rem(self.me + k, self.n)}

    def peer(self, k):
        return {"items": lax.rem(self.item + k, self.items), "rows": self.me}

    def greet(self):
        barrier = pltpu.get_barrier_semaphore()

        def rows(k, carry):
            pl.semaphore_signal(barrier, inc=1, device_id=self.row(k), device_id_type=MESH)
            return carry

        def items(k, carry):
            pl.semaphore_signal(barrier, inc=1, device_id=self.peer(k), device_id_type=MESH)
            return carry

        lax.fori_loop(1, self.n, rows, 0)
        lax.fori_loop(1, self.items, items, 0)

    def met(self):
        pl.semaphore_wait(pltpu.get_barrier_semaphore(), self.n + self.items - 2)

    def loop(self, count, body):
        def step(k, carry):
            body(k)
            return carry

        lax.fori_loop(1, count, step, 0)


class Sums:
    def __init__(self, grid, own, slots, send, recv):
        self.grid, self.own, self.slots, self.send, self.recv = grid, own, slots, send, recv

    def copy(self, k):
        return remote(
            self.own, self.slots.at[self.grid.me], self.send.at[k], self.recv.at[k], self.grid.row(k)
        )

    def start(self):
        self.grid.loop(self.grid.n, lambda k: self.copy(k).start())
        self.slots[self.grid.me] = self.own[...]

    def result(self):
        self.grid.loop(self.grid.n, lambda k: self.copy(k).wait())
        slots = self.slots
        return lax.fori_loop(1, self.grid.n, lambda k, s: s + slots[k], slots[0])


class Edges:
    def __init__(self, grid, field, send, recv):
        self.grid, self.field, self.send, self.recv = grid, field, send, recv

    def copy(self, side):
        last = self.field.shape[0] - 1
        at, to = (last - 1, 0) if side == 0 else (1, last)
        grid = self.grid
        return remote(
            self.field.at[at : at + 1],
            self.field.at[to : to + 1],
            self.send.at[side],
            self.recv.at[side],
            {"items": grid.item, "rows": grid.me + 1 if side == 0 else grid.me - 1},
        )

    def both(self, down, up):
        @pl.when(self.grid.me < self.grid.n - 1)
        def _():
            down()

        @pl.when(self.grid.me > 0)
        def _():
            up()

    def clear(self):
        last = self.field.shape[0] - 1

        @pl.when(self.grid.me == 0)
        def _():
            self.field[0] = jnp.zeros(self.field.shape[1:], self.field.dtype)

        @pl.when(self.grid.me == self.grid.n - 1)
        def _():
            self.field[last] = jnp.zeros(self.field.shape[1:], self.field.dtype)

    def start(self):
        self.both(lambda: self.copy(0).start(), lambda: self.copy(1).start())

    def wait(self):
        self.both(lambda: self.copy(1).wait_recv(), lambda: self.copy(0).wait_recv())
        self.both(lambda: self.copy(0).wait_send(), lambda: self.copy(1).wait_send())


def shift_into(out, r, value):
    width, channels = value.shape
    column = lax.broadcasted_iota(jnp.int32, value.shape, 0)
    left = jnp.where(column == 0, 0.0, pltpu.roll(value, 1, 0))
    right = jnp.where(column == width - 1, 0.0, pltpu.roll(value, width - 1, 0))
    out[r, :, :channels] = left.astype(BF16)
    out[r, :, channels : 2 * channels] = value.astype(BF16)
    out[r, :, 2 * channels :] = right.astype(BF16)


def row_stats(rows, width, channels, row):
    def step(r, carry):
        one, two = row(r)
        return carry[0] + one, carry[1] + two

    zero = jnp.zeros((width, channels), F32)
    one, two = lax.fori_loop(0, rows, step, (zero, zero))
    one = jnp.sum(one, axis=0, keepdims=True)
    two = jnp.sum(two, axis=0, keepdims=True)
    at = lax.broadcasted_iota(jnp.int32, (8, channels), 0)
    return jnp.where(at == 0, one, jnp.where(at == 1, two, 0.0))


def each_row(rows, body):
    def step(r, carry):
        body(r)
        return carry

    lax.fori_loop(0, rows, step, 0)


def conv_taps(shifted, weight, acc, rows_dev):
    pixels, wide = acc.shape[0], shifted.shape[2]
    acc[...] = jnp.zeros_like(acc)

    def step(tap, carry):
        acc[...] += dot(shifted[pl.ds(tap, rows_dev)].reshape(pixels, wide), weight[tap], 1, 0)
        return carry

    lax.fori_loop(0, 3, step, 0)


def forward_kernel(items, n, step, bq, *refs):
    (info, image, cot, text, embed, gain1, gain2, gain3, w1_in, w2_in, embed_in, text_in, qkv_in, proj_in,
     first_out, mid_out, cot_out, hidden_all, second_all, attn_out, turned_out, o_out, dq_out, dkv_out, dt_out,
     dt_all, text_cols, stats_out, shifts_out,
     image_v, cot_v, text_v, w1, w2, embed_w, text_w, qkv_w, proj_w, first_v, mid_v, hidden, second, attn,
     turned, keys, values, queries, go, text_kv, cols, shifted, acc, own, slots,
     key_land, value_land, query_land, go_land, text_pair, o, dq, dkv, dtext,
     load, sum_send, sum_recv, edge_send, edge_recv, row_send, row_recv, item_send, item_recv,
     *scratch) = refs
    grid = Grid(items, n)
    item, me = grid.item, grid.me
    rows_dev, width, channels = image.shape
    pixels = rows_dev * width
    heads, head_dim, wide = HEADS, channels // HEADS, 3 * channels // HEADS
    base = me * rows_dev
    count = (info[0, 0] * info[0, 1]).astype(F32) * (channels // GROUPS)
    att = Attention(n, pixels, head_dim, n * text.shape[0], step, bq, scratch)

    def inside(row):
        return window(info, 0, row, (width, channels))

    loads = []

    def fetch(src, dst):
        c = pltpu.make_async_copy(src, dst, load.at[len(loads)])
        c.start()
        loads.append(c)
        return c

    center = slice(1, rows_dev + 1)
    got_image = fetch(image, image_v.at[center])
    got_cot = fetch(cot, cot_v.at[center])
    got_proj = fetch(proj_in, proj_w)
    got_text = fetch(text, text_v)
    got_text_w = fetch(text_in, text_w)
    got_w1 = fetch(w1_in, w1)
    got_embed_w = fetch(embed_in, embed_w)
    got_w2 = fetch(w2_in, w2)
    got_qkv_w = fetch(qkv_in, qkv_w)
    edges = [
        Edges(grid, field, edge_send.at[j], edge_recv.at[j])
        for j, field in enumerate((image_v, cot_v, first_v, mid_v))
    ]
    sums = [Sums(grid, own.at[j], slots.at[j], sum_send.at[j], sum_recv.at[j]) for j in range(3)]
    grid.greet()
    for e in edges:
        e.clear()
    got_image.wait()

    def start_row(r):
        return image_v[1 + r].astype(F32) * inside(base + r)

    def start_stats(r):
        v = start_row(r)
        return v, v * v

    own[0] = row_stats(rows_dev, width, channels, start_stats)
    grid.met()
    sums[0].start()
    edges[0].start()
    got_cot.wait()
    edges[1].start()

    got_text.wait()
    got_text_w.wait()
    text_all = dot(text_v[...], text_w[...], 1, 0).astype(BF16)
    share = text_v.shape[1] // n
    for h in range(heads):
        text_kv[h] = text_all[:, h * 2 * head_dim : (h + 1) * 2 * head_dim]
    for r in range(n):
        cols[r] = text_v[:, r * share : (r + 1) * share]

    def scatter(j, src, dst):
        def copy(k):
            to = lax.rem(me + k, n)
            return remote(src.at[to], dst.at[me], row_send.at[j, k], row_recv.at[j, k], grid.row(k))

        return copy

    kv_copy = scatter(0, text_kv, text_pair)
    col_copy = scatter(1, cols, text_cols.at[item])
    grid.loop(n, lambda k: kv_copy(k).start())
    grid.loop(n, lambda k: col_copy(k).start())
    own_kv = fetch(text_kv.at[me], text_pair.at[me])
    own_col = fetch(cols.at[me], text_cols.at[item, me])

    got_proj.wait()

    def to_grad(r):
        attn[pl.ds(r * width, width)] = (cot_v[1 + r].astype(F32) * inside(base + r)).astype(BF16)

    each_row(rows_dev, to_grad)
    for h in range(heads):
        go[h] = dot(proj_w[h * head_dim : (h + 1) * head_dim], attn[...], 1, 1).astype(BF16)
    go_copy = scatter(2, go, go_land)
    own_go = fetch(go.at[me], go_land.at[me])

    stats = sums[0].result()
    stats_out[0] = stats
    average, inverse = norm_of(stats, count)
    edges[0].wait()

    def to_hidden(r):
        ok = inside(base + r - 1)
        value = (image_v[r].astype(F32) * ok - average) * inverse * ok * gain1[...]
        value = value * sigmoid(value) * ok
        shift_into(shifted, r, value)
        hidden[r] = value.astype(BF16)

    each_row(rows_dev + 2, to_hidden)

    def spread(j, src, dst):
        def copy(k):
            return remote(src, dst.at[item], item_send.at[j, k], item_recv.at[j, k], grid.peer(k))

        return copy

    hidden_copy = spread(0, hidden, hidden_all)
    grid.loop(items, lambda k: hidden_copy(k).start())
    own_hidden = fetch(hidden, hidden_all.at[item])
    got_w1.wait()
    conv_taps(shifted, w1, acc, rows_dev)

    def first_row(r):
        value = acc[pl.ds(r * width, width)] * inside(base + r)
        first_v[1 + r] = value
        return value, value * value

    own[1] = row_stats(rows_dev, width, channels, first_row)
    sums[1].start()
    edges[2].start()

    e = embed[...].astype(F32)
    low = (e * sigmoid(e)).astype(BF16)
    got_embed_w.wait()
    shifts_out[...] = dot(low, embed_w[...], 1, 0)
    scale, shift = shifts_out[:, :channels], shifts_out[:, channels:]

    stats = sums[1].result()
    stats_out[1] = stats
    average, inverse = norm_of(stats, count)
    edges[2].wait()
    own_first = fetch(first_v, first_out)

    def to_second(r):
        ok = inside(base + r - 1)
        _, moved = moved_of(first_v[r], ok, average, inverse, gain2[...], scale, shift)
        value = moved * sigmoid(moved) * ok
        shift_into(shifted, r, value)
        second[r] = value.astype(BF16)

    each_row(rows_dev + 2, to_second)
    second_copy = spread(1, second, second_all)
    grid.loop(items, lambda k: second_copy(k).start())
    own_second = fetch(second, second_all.at[item])
    got_w2.wait()
    conv_taps(shifted, w2, acc, rows_dev)

    def middle_row(r):
        value = (image_v[1 + r].astype(F32) + acc[pl.ds(r * width, width)]) * inside(base + r)
        mid_v[1 + r] = value
        return value, value * value

    own[2] = row_stats(rows_dev, width, channels, middle_row)
    sums[2].start()
    edges[3].start()
    edges[1].wait()
    own_cot = fetch(cot_v, cot_out)
    got_qkv_w.wait()
    for j in range(3):
        block = qkv_w[:, j * channels : (j + 1) * channels].astype(F32).T
        turned[j * channels : (j + 1) * channels] = block.astype(BF16)
    own_turned = fetch(turned, turned_out)

    stats = sums[2].result()
    stats_out[2] = stats
    average, inverse = norm_of(stats, count)

    def to_attn(r):
        value = (mid_v[1 + r] - average) * inverse * inside(base + r) * gain3[...]
        attn[pl.ds(r * width, width)] = value.astype(BF16)

    each_row(rows_dev, to_attn)
    own_attn = fetch(attn, attn_out)
    key_copy = scatter(3, keys, key_land)
    value_copy = scatter(4, values, value_land)
    query_copy = scatter(5, queries, query_land)

    def head(k):
        to = lax.rem(me + k, n)
        rows = pl.ds(pl.multiple_of(to * wide, wide), wide)
        block = dot(turned[rows], attn[...], 1, 1).astype(BF16)
        queries[to] = block[:head_dim]
        keys[to] = block[head_dim : 2 * head_dim]
        values[to] = block[2 * head_dim :]

    def send_head(k):
        head(k)
        key_copy(k).start()

    grid.loop(n, send_head)
    head(0)
    query_land[me] = queries[me]
    att.stage_key(me, keys[me], width, info[0, 0], info[0, 1])
    att.stage_value(me, values[me])
    grid.loop(n, lambda k: kv_copy(k).wait())
    own_kv.wait()
    att.stage_text(text_pair[...].reshape(n * text.shape[0], 2 * head_dim))
    edges[3].wait()
    own_mid = fetch(mid_v, mid_out)

    def source(k):
        return lax.rem(me + n - k, n)

    def stage_key(k):
        key_copy(k).wait()
        att.stage_key(source(k), key_land[source(k)], width, info[0, 0], info[0, 1])

    grid.loop(n, stage_key)
    grid.loop(n, lambda k: value_copy(k).start())

    def scored():
        def stage_value(k):
            value_copy(k).wait()
            att.stage_value(source(k), value_land[source(k)])

        grid.loop(n, stage_value)

        def rest(k):
            query_copy(k).start()
            go_copy(k).start()

        grid.loop(n, rest)
        own_go.wait()

    def before(k):
        query_copy(k).wait()
        go_copy(k).wait()

    def give(j, src, dst):
        def copy(h):
            to = source(h)
            return remote(
                src.at[to],
                dst.at[me],
                row_send.at[j, h],
                row_recv.at[j, h],
                {"items": item, "rows": to},
            )

        return copy

    o_copy = give(6, o, o_out)
    dq_copy = give(7, dq, dq_out)
    dkv_copy = give(8, dkv, dkv_out)
    dt_copy = give(9, dtext, dt_out)

    def done(h):
        @pl.when(h > 0)
        def _():
            o_copy(h).start()
            dq_copy(h).start()

    att.attend(query_land, go_land, o, dq, source, scored, before, done)

    def send_keys(h):
        at = pl.ds(pl.multiple_of(source(h) * pixels, pixels), pixels)
        dkv[source(h), :head_dim] = att.key_grad(at)
        dkv[source(h), head_dim:] = att.value_grad(at)

    def send_next(h):
        send_keys(h)
        dkv_copy(h).start()

    grid.loop(n, send_next)
    send_keys(0)
    flat = jnp.concatenate(
        [
            (att.dkt[:, n * pixels :] * (head_dim**-0.5)).T,
            att.dvt[:, n * pixels :].T,
        ],
        axis=1,
    )
    for r in range(n):
        tokens = text.shape[0]
        dtext[r] = flat[r * tokens : (r + 1) * tokens].astype(BF16)
    grid.loop(n, lambda h: dt_copy(h).start())

    def gather_copy(k):
        return remote(
            dtext, dt_all.at[item, me], row_send.at[10, k], row_recv.at[10, k], grid.row(k)
        )

    grid.loop(n, lambda k: gather_copy(k).start())
    own_o = fetch(o.at[me], o_out.at[me])
    own_dq = fetch(dq.at[me], dq_out.at[me])
    own_dkv = fetch(dkv.at[me], dkv_out.at[me])
    own_dt = fetch(dtext.at[me], dt_out.at[me])
    own_all = fetch(dtext, dt_all.at[item, me])
    grid.loop(n, lambda k: col_copy(k).wait())
    own_col.wait()
    cols_copy = spread(2, text_cols.at[item], text_cols)
    grid.loop(items, lambda k: cols_copy(k).start())
    grid.loop(items, lambda k: hidden_copy(k).wait())
    grid.loop(items, lambda k: second_copy(k).wait())
    grid.loop(items, lambda k: cols_copy(k).wait())
    for copy in (o_copy, dq_copy, dkv_copy, dt_copy, gather_copy):
        grid.loop(n, lambda h: copy(h).wait())
    for c in (own_hidden, own_first, own_second, own_cot, own_turned, own_attn, own_mid, own_o, own_dq, own_dkv,
              own_dt, own_all):
        c.wait()


def forward_call(info, image, cot, text, embed, gains, weights, identity):
    items, n = lax.axis_size("items"), lax.axis_size("rows")
    rows_dev, width, channels = image.shape
    pixels = rows_dev * width
    padded = (rows_dev + 2, width, channels)
    tokens, text_width = text.shape
    head_dim = channels // HEADS
    w1, w2, embed_w, text_w, qkv_w, proj_w = weights
    sds = jax.ShapeDtypeStruct
    outs = (
        sds(padded, F32),
        sds(padded, F32),
        sds(padded, BF16),
        sds((items,) + padded, BF16),
        sds((items,) + padded, BF16),
        sds((pixels, channels), BF16),
        sds((3 * channels, channels), BF16),
        sds((n, head_dim, pixels), BF16),
        sds((n, head_dim, pixels), BF16),
        sds((n, 2 * head_dim, pixels), BF16),
        sds((n, tokens, 2 * head_dim), BF16),
        sds((items, n, n, tokens, 2 * head_dim), BF16),
        sds((items, n, tokens, text_width // n), BF16),
        sds((3, 8, channels), F32),
        sds((1, 2 * channels), F32),
    )
    v = pltpu.VMEM
    scratch = [
        v(padded, BF16),
        v(padded, BF16),
        v(text.shape, BF16),
        v(w1.shape, BF16),
        v(w2.shape, BF16),
        v(embed_w.shape, BF16),
        v(text_w.shape, BF16),
        v(qkv_w.shape, BF16),
        v(proj_w.shape, BF16),
        v(padded, F32),
        v(padded, F32),
        v(padded, BF16),
        v(padded, BF16),
        v((pixels, channels), BF16),
        v((3 * channels, channels), BF16),
        v((n, head_dim, pixels), BF16),
        v((n, head_dim, pixels), BF16),
        v((n, head_dim, pixels), BF16),
        v((n, head_dim, pixels), BF16),
        v((n, tokens, 2 * head_dim), BF16),
        v((n, tokens, text_width // n), BF16),
        v((rows_dev + 2, width, 3 * channels), BF16),
        v((pixels, channels), F32),
        v((3, 8, channels), F32),
        v((3, n, 8, channels), F32),
        v((n, head_dim, pixels), BF16),
        v((n, head_dim, pixels), BF16),
        v((n, head_dim, pixels), BF16),
        v((n, head_dim, pixels), BF16),
        v((n, tokens, 2 * head_dim), BF16),
        v((n, head_dim, pixels), BF16),
        v((n, head_dim, pixels), BF16),
        v((n, 2 * head_dim, pixels), BF16),
        v((n, tokens, 2 * head_dim), BF16),
        DMA((28,)),
        DMA((3, n)),
        DMA((3, n)),
        DMA((4, 2)),
        DMA((4, 2)),
        DMA((11, n)),
        DMA((11, n)),
        DMA((3, items)),
        DMA((3, items)),
    ]
    step, bq, extra = attention_scratch(n, pixels, head_dim, n * tokens)
    scratch += extra
    return pl.pallas_call(
        functools.partial(forward_kernel, items, n, step, bq),
        out_shape=outs,
        in_specs=[SCALARS] + [ANYWHERE] * 3 + [WHOLE] * 4 + [ANYWHERE] * 6,
        out_specs=(ANYWHERE,) * 13 + (WHOLE,) * 2,
        scratch_shapes=scratch,
        compiler_params=pltpu.CompilerParams(
            collective_id=identity, has_side_effects=True, vmem_limit_bytes=62 << 20
        ),
        cost_estimate=pl.CostEstimate(
            flops=40 * pixels * channels * channels, bytes_accessed=60 << 20, transcendentals=0
        ),
        name="forward",
    )(info, image, cot, text, embed, *gains, *weights)


class KernelSum:
    def __init__(self, grid, turned, quarter, part, from_core, chip_sum, from_chip, final, item_sems, core_sems,
                 chip_sems, final_sems):
        self.grid = grid
        self.turned, self.quarter, self.part, self.from_core = turned, quarter, part, from_core
        self.chip_sum, self.from_chip, self.final = chip_sum, from_chip, final
        self.item_sems, self.core_sems = item_sems, core_sems
        self.chip_sems, self.final_sems = chip_sems, final_sems
        self.chips = grid.n // 2
        self.chip, self.core = grid.me // 2, lax.rem(grid.me, 2)

    def grads_copy(self, k):
        grid = self.grid
        send, recv = self.item_sems
        to = lax.rem(grid.item + k, grid.items)
        return remote(
            self.turned.at[to], self.quarter.at[grid.item], send.at[k], recv.at[k], grid.peer(k)
        )

    def send_grads(self, shifted):
        grid, chips = self.grid, self.chips
        rows_dev, width, channels = shifted.shape[0] - 2, shifted.shape[1], shifted.shape[2] // 3
        center = shifted[1 : rows_dev + 1, :, channels : 2 * channels]
        block = center.reshape(rows_dev * width, channels).astype(F32).T.astype(BF16)
        share = channels // grid.n
        rows = share // grid.items
        for z in range(chips):
            for c in range(2):
                for q in range(grid.items):
                    at = (z * 2 + c) * share + q * rows
                    to = (c * chips + z) * rows
                    self.turned[q, to : to + rows] = block[at : at + rows]
        grid.loop(grid.items, lambda k: self.grads_copy(k).start())
        self.quarter[grid.item] = self.turned[grid.item]

    def wait_grads(self):
        self.grid.loop(self.grid.items, lambda k: self.grads_copy(k).wait())

    def core_copy(self, a):
        send, recv = self.core_sems
        grid = self.grid
        return remote(
            self.part.at[a, 1 - self.core],
            self.from_core.at[a],
            send.at[a],
            recv.at[a],
            {"items": grid.item, "rows": grid.me + 1 - 2 * self.core},
        )

    def compute(self, a, shifted):
        items, padded, width, wide = shifted.shape
        rows_dev, channels = padded - 2, wide // 3
        half = self.turned.shape[1] // 2
        for b in range(3):
            acc = None
            for g in range(items):
                rhs = shifted[g, a : a + rows_dev, :, b * channels : (b + 1) * channels]
                term = dot(self.quarter[g], rhs.reshape(rows_dev * width, channels), 1, 0)
                acc = term if acc is None else acc + term
            self.part[a, 0, b] = acc[:half].astype(BF16)
            self.part[a, 1, b] = acc[half:].astype(BF16)
        self.core_copy(a).start()

    def chip_copy(self, a, k):
        send, recv = self.chip_sems
        grid = self.grid
        to = lax.rem(self.chip + k, self.chips)
        return remote(
            self.chip_sum.at[a, to],
            self.from_chip.at[a, k],
            send.at[a, k],
            recv.at[a, k],
            {"items": grid.item, "rows": to * 2 + self.core},
        )

    def over_chips(self, a):
        self.core_copy(a).wait()
        rows = self.chip_sum.shape[3]
        for b in range(3):
            both = self.part[a, self.core, b].astype(F32) + self.from_core[a, b].astype(F32)
            for z in range(self.chips):
                self.chip_sum[a, z, b] = both[z * rows : (z + 1) * rows].astype(BF16)
        for k in range(1, self.chips):
            self.chip_copy(a, k).start()

    def final_copy(self, a, k):
        send, recv = self.final_sems
        mine = self.final.at[a, self.grid.item]
        return remote(mine, mine, send.at[a, k], recv.at[a, k], self.grid.peer(k))

    def over_items(self, a):
        for k in range(1, self.chips):
            self.chip_copy(a, k).wait()
        total = self.chip_sum[a, self.chip].astype(F32)
        for k in range(1, self.chips):
            total = total + self.from_chip[a, k].astype(F32)
        self.final[a, self.grid.item] = total.astype(BF16)
        for k in range(1, self.grid.items):
            self.final_copy(a, k).start()

    def put(self, a, out):
        for k in range(1, self.grid.items):
            self.final_copy(a, k).wait()
        channels = self.final.shape[4]
        for b in range(3):
            rows = [self.final[a, q, b].astype(F32) for q in range(self.grid.items)]
            at = (a * 3 + b) * channels
            out[at : at + channels] = jnp.concatenate(rows, axis=0).T


class SideSum:
    def __init__(self, grid, values, from_core, core_sum, from_item, item_sum, from_chip, final, core_sems,
                 item_sems, chip_sems, final_sems):
        self.grid = grid
        self.values, self.from_core, self.core_sum = values, from_core, core_sum
        self.from_item, self.item_sum, self.from_chip, self.final = (
            from_item,
            item_sum,
            from_chip,
            final,
        )
        self.core_sems, self.item_sems = core_sems, item_sems
        self.chip_sems, self.final_sems = chip_sems, final_sems
        self.chips = grid.n // 2
        self.chip, self.core = grid.me // 2, lax.rem(grid.me, 2)

    def core_copy(self):
        send, recv = self.core_sems
        grid = self.grid
        return remote(
            self.values.at[1 - self.core],
            self.from_core,
            send.at[0],
            recv.at[0],
            {"items": grid.item, "rows": grid.me + 1 - 2 * self.core},
        )

    def item_copy(self, k):
        send, recv = self.item_sems
        grid = self.grid
        to = lax.rem(grid.item + k, grid.items)
        return remote(
            self.core_sum.at[to], self.from_item.at[k], send.at[k], recv.at[k], grid.peer(k)
        )

    def over_items(self):
        self.core_copy().wait()
        for z in range(self.chips):
            both = self.values[self.core, z].astype(F32) + self.from_core[z].astype(F32)
            for q in range(self.grid.items):
                self.core_sum[q, z] = both[q].astype(BF16)
        for k in range(1, self.grid.items):
            self.item_copy(k).start()

    def chip_copy(self, k):
        send, recv = self.chip_sems
        grid = self.grid
        to = lax.rem(self.chip + k, self.chips)
        return remote(
            self.item_sum.at[to],
            self.from_chip.at[k],
            send.at[k],
            recv.at[k],
            {"items": grid.item, "rows": to * 2 + self.core},
        )

    def over_chips(self):
        for k in range(1, self.grid.items):
            self.item_copy(k).wait()
        total = self.core_sum[self.grid.item].astype(F32)
        for k in range(1, self.grid.items):
            total = total + self.from_item[k].astype(F32)
        self.item_sum[...] = total.astype(BF16)
        for k in range(1, self.chips):
            self.chip_copy(k).start()

    def final_copy(self, k):
        send, recv = self.final_sems
        mine = self.final.at[self.grid.item]
        return remote(mine, mine, send.at[k], recv.at[k], self.grid.peer(k))

    def spread(self):
        for k in range(1, self.chips):
            self.chip_copy(k).wait()
        total = self.item_sum[self.chip].astype(F32)
        for k in range(1, self.chips):
            total = total + self.from_chip[k].astype(F32)
        self.final[self.grid.item] = total.astype(BF16)
        for k in range(1, self.grid.items):
            self.final_copy(k).start()

    def put(self, qkv_out, proj_out):
        for k in range(1, self.grid.items):
            self.final_copy(k).wait()
        rows = jnp.concatenate(
            [self.final[q].astype(F32) for q in range(self.grid.items)], axis=0
        )
        share, channels = rows.shape[0], rows.shape[1] // 4
        for w in range(3):
            qkv_out[:, w * share : (w + 1) * share] = rows[:, w * channels : (w + 1) * channels].T
        proj_out[...] = rows[:, 3 * channels :].T


def conv_taps_back(shifted, weight, acc, rows_dev):
    pixels, channels = acc.shape
    acc[...] = jnp.zeros_like(acc)

    def step(tap, carry):
        lhs = shifted[pl.ds(tap, rows_dev)].reshape(pixels, 3 * channels)
        total = None
        for b in range(3):
            at = pl.multiple_of(((2 - tap) * 3 + 2 - b) * channels, channels)
            term = dot(
                lhs[:, b * channels : (b + 1) * channels], weight[pl.ds(at, channels)], 1, 1
            )
            total = term if total is None else total + term
        acc[...] += total
        return carry

    lax.fori_loop(0, 3, step, 0)


def backward_kernel(items, n, *refs):
    (info, embed, gain1, gain2, gain3, stats_in, shifts,
     o_in, dq_in, dkv_in, dt_in, dt_all, first, middle, cot, image, hidden_all, second_all, attn_in, turned_in, text_cols,
     proj_in, w1_in, w2_in, text_in, embed_in,
     output, image_grad, conv1_out, conv2_out, qkv_out, proj_out, vectors, text_grad, text_w_grad, embed_grad,
     weight, proj_w, qkv_turned, first_v, mid_v, cot_v, image_v, attn, cols, rows_v, dq, o, dt, own_dt,
     grad_v, grad_mid, moved_v, pre, acc, shifted, shifted_all, masked, out_v, image_out,
     turned, quarter, part, from_core, chip_sum, from_chip, final,
     side_v, side_core, side_sum, side_item, side_total, side_chip, side_final,
     vector, vector_land, own, slots,
     load, sum_send, sum_recv, edge_send, edge_recv, dt_send, dt_recv, vec_send, vec_recv,
     k_item_send, k_item_recv, k_core_send, k_core_recv, k_chip_send, k_chip_recv, k_final_send, k_final_recv,
     s_core_send, s_core_recv, s_item_send, s_item_recv, s_chip_send, s_chip_recv, s_final_send,
     s_final_recv) = refs
    grid = Grid(items, n)
    item, me = grid.item, grid.me
    rows_dev, width, channels = image.shape
    pixels = rows_dev * width
    heads, head_dim, wide = HEADS, channels // HEADS, 3 * channels // HEADS
    share = channels // n
    base = me * rows_dev
    count = (info[0, 0] * info[0, 1]).astype(F32) * (channels // GROUPS)
    scale, shift = shifts[:, :channels], shifts[:, channels:]

    def inside(row):
        return window(info, 0, row, (width, channels))

    fetched = []

    def fetch(src, dst):
        c = pltpu.make_async_copy(src, dst, load.at[len(fetched)])
        c.start()
        fetched.append(c)
        return c

    got_dq = fetch(dq_in, dq.at[:, :head_dim])
    got_dkv = fetch(dkv_in, dq.at[:, head_dim:])
    got_turned = fetch(turned_in, qkv_turned)
    got_mid = fetch(middle, mid_v)
    got_cot = fetch(cot, cot_v)
    got_w2 = fetch(w2_in, weight)
    got_first = fetch(first, first_v)
    got_attn = fetch(attn_in, attn)
    got_o = fetch(o_in, o)
    got_proj = fetch(proj_in, proj_w)
    got_dt = fetch(dt_in, own_dt)
    got_all = fetch(dt_all.at[item], dt.at[item])
    got_second = fetch(second_all, rows_v)
    got_image = fetch(image, image_v)
    got_cols = fetch(text_cols, cols)
    grid.greet()
    edges = [
        Edges(grid, field, edge_send.at[j], edge_recv.at[j])
        for j, field in enumerate((grad_v, moved_v))
    ]
    for e in edges:
        e.clear()
    sums = [Sums(grid, own.at[j], slots.at[j], sum_send.at[j], sum_recv.at[j]) for j in range(3)]
    kernel_sums = [
        KernelSum(grid, turned.at[j], quarter.at[j], part.at[j], from_core.at[j], chip_sum.at[j], from_chip.at[j],
                  final.at[j], (k_item_send.at[j], k_item_recv.at[j]), (k_core_send.at[j], k_core_recv.at[j]),
                  (k_chip_send.at[j], k_chip_recv.at[j]), (k_final_send.at[j], k_final_recv.at[j]))
        for j in range(2)
    ]
    sum2, sum1 = kernel_sums
    side = SideSum(grid, side_v, side_core, side_sum, side_item, side_total, side_chip, side_final,
                   (s_core_send, s_core_recv), (s_item_send, s_item_recv), (s_chip_send, s_chip_recv),
                   (s_final_send, s_final_recv))

    def dt_copy(k):
        mine = dt.at[item]
        return remote(mine, mine, dt_send.at[k], dt_recv.at[k], grid.peer(k))

    got_turned.wait()
    got_dq.wait()
    got_dkv.wait()

    def unproject_head(h):
        rows = pl.ds(pl.multiple_of(h * wide, wide), wide)
        return dot(dq[h].astype(F32).T.astype(BF16), qkv_turned[rows], 1, 0)

    acc[...] = unproject_head(0)

    def next_head(h):
        acc[...] += unproject_head(h)

    grid.loop(n, next_head)
    got_mid.wait()
    average, inverse = norm_of(stats_in[2], count)

    def grad_row(r):
        value = acc[pl.ds(r * width, width)] * inside(base + r)
        grad_v[1 + r] = value
        return value, value * ((mid_v[1 + r] - average) * inverse)

    own[0] = row_stats(rows_dev, width, channels, grad_row)
    grid.met()
    sums[0].start()
    edges[0].start()
    got_all.wait()
    grid.loop(items, lambda k: dt_copy(k).start())

    got_attn.wait()

    def qkv_head(h):
        block = dot(dq[h], attn[...], 1, 0).astype(BF16)
        for w in range(3):
            rows = block[w * head_dim : (w + 1) * head_dim]
            side_v[lax.rem(h, 2), h // 2, :, :, w * channels : (w + 1) * channels] = rows.reshape(
                items, share // items, channels
            )

    each_row(heads, qkv_head)
    got_cot.wait()

    def mask_row(r):
        masked[pl.ds(r * width, width)] = (cot_v[1 + r].astype(F32) * inside(base + r)).astype(BF16)

    each_row(rows_dev, mask_row)

    got_o.wait()
    flat_o = o[...].reshape(channels, pixels)
    block = dot(masked[...].astype(F32).T.astype(BF16), flat_o, 1, 1).astype(BF16)
    for r in range(n):
        rows = block[r * share : (r + 1) * share]
        side_v[r % 2, r // 2, :, :, 3 * channels :] = rows.reshape(items, share // items, channels)
    side.core_copy().start()

    stats4 = sums[0].result()
    mean, cross = means_of(stats4, gain3[...], count)
    edges[0].wait()

    def to_grad2(r):
        normal = (mid_v[r] - average) * inverse
        ok = inside(base + r - 1)
        term = (grad_v[r] * gain3[...] - mean - normal * cross) * inverse * ok
        total = cot_v[r].astype(F32) + term
        grad_mid[r] = total
        shift_into(shifted, r, total * ok)

    each_row(rows_dev + 2, to_grad2)
    sum2.send_grads(shifted)
    side.over_items()
    got_w2.wait()
    conv_taps_back(shifted, weight, acc, rows_dev)
    got_first.wait()
    average2, inverse2 = norm_of(stats_in[1], count)

    def moved_row(r):
        ok = inside(base + r)
        normal, moved = moved_of(first_v[1 + r], ok, average2, inverse2, gain2[...], scale, shift)
        value = acc[pl.ds(r * width, width)] * ok * silu_slope(moved)
        moved_v[1 + r] = value
        return value, value * normal

    own[1] = row_stats(rows_dev, width, channels, moved_row)
    sums[1].start()
    edges[1].start()
    got_w1 = fetch(w1_in, weight)
    got_second.wait()

    def shift_rows():
        for g in range(items):
            each_row(rows_dev + 2, lambda r: shift_into(shifted_all.at[g], r, rows_v[g, r].astype(F32)))

    shift_rows()
    got_hidden = fetch(hidden_all, rows_v)
    sum2.wait_grads()
    for a in range(3):
        sum2.compute(a, shifted_all)

    stats5 = sums[1].result()
    factor = gain2[...] * (1.0 + scale)
    mean, cross = means_of(stats5, factor, count)
    edges[1].wait()

    def to_grad1(r):
        normal = (first_v[r] - average2) * inverse2
        value = (moved_v[r] * factor - mean - normal * cross) * inverse2
        shift_into(shifted, r, value * inside(base + r - 1))

    each_row(rows_dev + 2, to_grad1)
    sum1.send_grads(shifted)
    side.over_chips()
    for a in range(3):
        sum2.over_chips(a)
    got_w1.wait()
    conv_taps_back(shifted, weight, acc, rows_dev)
    got_image.wait()
    average1, inverse1 = norm_of(stats_in[0], count)

    def pre_row(r):
        ok = inside(base + r)
        normal = (image_v[r].astype(F32) - average1) * inverse1 * ok
        value = acc[pl.ds(r * width, width)] * ok * silu_slope(normal * gain1[...])
        pre[r] = value
        return value, value * normal

    own[2] = row_stats(rows_dev, width, channels, pre_row)
    sums[2].start()
    tall = text_in.shape[0]
    got_text_w = [
        fetch(text_in.at[:, j * channels : (j + 1) * channels], weight.at[j * tall : (j + 1) * tall])
        for j in range(2)
    ]
    got_hidden.wait()
    shift_rows()
    sum1.wait_grads()
    sum1.compute(0, shifted_all)
    sum1.compute(1, shifted_all)
    sum1.over_chips(0)
    sum1.compute(2, shifted_all)
    sum1.over_chips(1)
    sum1.over_chips(2)
    for a in range(3):
        sum2.over_items(a)
    side.spread()

    stats6 = sums[2].result()
    e = embed[...].astype(F32)
    low = (e * sigmoid(e)).astype(BF16).astype(F32)
    vector[...] = jnp.zeros_like(vector)
    vector[0:1] = stats6[1:2]
    vector[1:2] = stats5[1:2] * (1.0 + scale)
    vector[2:3] = stats4[1:2]
    vector[3:4] = (stats5[1:2] * gain2[...]).astype(BF16).astype(F32)
    vector[4:5] = stats5[0:1].astype(BF16).astype(F32)
    for j in range(embed.shape[1] // channels):
        vector[5 + j : 6 + j] = low[:, j * channels : (j + 1) * channels]

    def vector_copy(k):
        return remote(
            vector, vector_land.at[item], vec_send.at[k], vec_recv.at[k], grid.peer(k)
        )

    grid.loop(items, lambda k: vector_copy(k).start())
    vector_land[item] = vector[...]

    mean, cross = means_of(stats6, gain1[...], count)

    def finish_row(r):
        normal = (image_v[r].astype(F32) - average1) * inverse1
        term = (pre[r] * gain1[...] - mean - normal * cross) * inverse1
        image_out[r] = (grad_mid[1 + r] + term) * inside(base + r)

    each_row(rows_dev, finish_row)
    put_image = fetch(image_out, image_grad)

    got_proj.wait()
    acc[...] = dot(flat_o.astype(F32).T.astype(BF16), proj_w[...], 1, 0)

    def output_row(r):
        value = mid_v[1 + r] + acc[pl.ds(r * width, width)] * inside(base + r)
        out_v[r] = value.astype(BF16)

    each_row(rows_dev, output_row)
    put_output = fetch(out_v, output)

    got_dt.wait()
    for c in got_text_w:
        c.wait()
    half = heads // 2
    total = None
    for j in range(2):
        lhs = jnp.concatenate([own_dt[j * half + h] for h in range(half)], axis=1)
        term = dot(lhs, weight[j * tall : (j + 1) * tall], 1, 1)
        total = term if total is None else total + term
    text_grad[...] = total
    got_embed_w = [
        fetch(embed_in.at[:, j * channels : (j + 1) * channels], weight.at[j * tall : (j + 1) * tall])
        for j in range(2)
    ]
    for a in range(3):
        sum1.over_items(a)
    for a in range(3):
        sum2.put(a, conv2_out)

    grid.loop(items, lambda k: dt_copy(k).wait())
    got_cols.wait()
    tokens = cols.shape[0] * cols.shape[1]
    flat_cols = cols[...].reshape(tokens, cols.shape[2]).astype(F32).T.astype(BF16)
    for h in range(heads):
        rhs = jnp.concatenate([dt[g, h].reshape(tokens // items, 2 * head_dim) for g in range(items)], axis=0)
        text_w_grad[:, h * 2 * head_dim : (h + 1) * 2 * head_dim] = dot(flat_cols, rhs, 1, 0)

    for c in got_embed_w:
        c.wait()
    total = None
    for j in range(2):
        lhs = vector[3 + j : 4 + j] if j else vector[3:4]
        lhs = jnp.broadcast_to(lhs, (8, channels)).astype(BF16)
        term = dot(lhs, weight[j * tall : (j + 1) * tall], 1, 1)
        total = term if total is None else total + term
    embed_grad[...] = total[0:1] * silu_slope(e)
    side.put(qkv_out, proj_out)
    for a in range(3):
        sum1.put(a, conv1_out)
    grid.loop(items, lambda k: vector_copy(k).wait())
    vectors[...] = vector_land[...]
    put_image.wait()
    put_output.wait()


def backward_call(info, embed, gains, stats, shifts, arrays, identity):
    items, n = lax.axis_size("items"), lax.axis_size("rows")
    o_pair, _, _, dtext = arrays[:4]
    image, text_cols, text_w = arrays[8], arrays[13], arrays[17]
    rows_dev, width, channels = image.shape
    pixels = rows_dev * width
    head_dim = channels // HEADS
    share = channels // n
    rows = share // items
    chips = n // 2
    padded = (rows_dev + 2, width, channels)
    tokens = dtext.shape[1]
    sds = jax.ShapeDtypeStruct
    outs = (
        sds(image.shape, BF16),
        sds(image.shape, F32),
        sds((9 * channels, share), F32),
        sds((9 * channels, share), F32),
        sds((channels, 3 * share), F32),
        sds((channels, share), F32),
        sds((items, 16, channels), F32),
        sds((tokens, text_w.shape[0]), F32),
        sds((text_w.shape[0] // n, 2 * channels), F32),
        sds(embed.shape, F32),
    )
    v = pltpu.VMEM
    scratch = [
        v((9 * channels, channels), BF16),
        v((channels, channels), BF16),
        v((3 * channels, channels), BF16),
        v(padded, F32),
        v(padded, F32),
        v(padded, BF16),
        v(image.shape, BF16),
        v((pixels, channels), BF16),
        v(text_cols.shape, BF16),
        v((items,) + padded, BF16),
        v((n, 3 * head_dim, pixels), BF16),
        v(o_pair.shape, BF16),
        v((items, n) + dtext.shape, BF16),
        v(dtext.shape, BF16),
        v(padded, F32),
        v(padded, F32),
        v(padded, F32),
        v(image.shape, F32),
        v((pixels, channels), F32),
        v((rows_dev + 2, width, 3 * channels), BF16),
        v((items, rows_dev + 2, width, 3 * channels), BF16),
        v((pixels, channels), BF16),
        v(image.shape, BF16),
        v(image.shape, F32),
        v((2, items, channels // items, pixels), BF16),
        v((2, items, channels // items, pixels), BF16),
        v((2, 3, 2, 3, chips * rows, channels), BF16),
        v((2, 3, 3, chips * rows, channels), BF16),
        v((2, 3, chips, 3, rows, channels), BF16),
        v((2, 3, chips, 3, rows, channels), BF16),
        v((2, 3, items, 3, rows, channels), BF16),
        v((2, chips, items, rows, 4 * channels), BF16),
        v((chips, items, rows, 4 * channels), BF16),
        v((items, chips, rows, 4 * channels), BF16),
        v((items, chips, rows, 4 * channels), BF16),
        v((chips, rows, 4 * channels), BF16),
        v((chips, rows, 4 * channels), BF16),
        v((items, rows, 4 * channels), BF16),
        v((16, channels), F32),
        v((items, 16, channels), F32),
        v((3, 8, channels), F32),
        v((3, n, 8, channels), F32),
        DMA((32,)),
        DMA((3, n)),
        DMA((3, n)),
        DMA((2, 2)),
        DMA((2, 2)),
        DMA((items,)),
        DMA((items,)),
        DMA((items,)),
        DMA((items,)),
        DMA((2, items)),
        DMA((2, items)),
        DMA((2, 3)),
        DMA((2, 3)),
        DMA((2, 3, chips)),
        DMA((2, 3, chips)),
        DMA((2, 3, items)),
        DMA((2, 3, items)),
        DMA((1,)),
        DMA((1,)),
        DMA((items,)),
        DMA((items,)),
        DMA((chips,)),
        DMA((chips,)),
        DMA((items,)),
        DMA((items,)),
    ]
    return pl.pallas_call(
        functools.partial(backward_kernel, items, n),
        out_shape=outs,
        in_specs=[SCALARS] + [WHOLE] * 6 + [ANYWHERE] * len(arrays),
        out_specs=(ANYWHERE,) * 2 + (WHOLE,) * 8,
        scratch_shapes=scratch,
        compiler_params=pltpu.CompilerParams(
            collective_id=identity, has_side_effects=True, vmem_limit_bytes=62 << 20
        ),
        cost_estimate=pl.CostEstimate(
            flops=80 * pixels * channels * channels, bytes_accessed=60 << 20, transcendentals=0
        ),
        name="backward",
    )(info, embed, *gains, stats, shifts, *arrays)


def own_shards(
    info, image, embed, text, gain1, conv1_w, embed_w, gain2, conv2_w, gain3, qkv_w, text_w, proj_w,
    cotangent,
):
    _, rows_dev, width, channels = image.shape
    items, parts = lax.axis_size("items"), lax.axis_size("rows")
    me = lax.axis_index("rows")
    head_dim = channels // HEADS
    tokens = text.shape[1]
    share = channels // parts
    (first, middle, cot, hidden_all, second_all, attn_flat, qkv_turned, attended, dq, dkv, own_dt, all_dt,
     text_cols, stats, shifts) = forward_call(
        info,
        image[0],
        cotangent[0],
        text[0],
        embed,
        (gain1, gain2, gain3),
        (
            conv1_w.reshape(3, 3 * channels, channels),
            conv2_w.reshape(3, 3 * channels, channels),
            embed_w,
            text_w,
            qkv_w,
            proj_w,
        ),
        0,
    )
    text_w_rows = text_cols.shape[3]
    (output, image_grad, conv1_total, conv2_total, qkv_total, proj_total, vectors, text_grad, text_w_grad,
     embed_grad) = backward_call(
        info,
        embed,
        (gain1, gain2, gain3),
        stats,
        shifts,
        (
            attended,
            dq,
            dkv,
            own_dt,
            all_dt,
            first,
            middle,
            cot,
            image[0],
            hidden_all,
            second_all,
            attn_flat,
            qkv_turned,
            text_cols.reshape(items * parts, tokens, text_w_rows),
            proj_w,
            conv1_w.reshape(9 * channels, channels),
            conv2_w.reshape(9 * channels, channels),
            text_w,
            embed_w,
        ),
        1,
    )
    embed_rows = embed.shape[1] // channels
    all_shifts = vectors[:, 3:5].reshape(items, 2 * channels).astype(BF16)
    all_embed = vectors[:, 5 : 5 + embed_rows].reshape(items, embed.shape[1]).astype(BF16)
    embed_share = embed_w.shape[0] // parts
    own_embed = lax.dynamic_slice_in_dim(all_embed, me * embed_share, embed_share, 1)
    embed_w_grad = jnp.einsum("ic,ik->ck", own_embed, all_shifts, preferred_element_type=F32)
    gains = jnp.sum(vectors[:, :3], axis=0)
    gains = lax.dynamic_slice_in_dim(gains, me * share, share, 1)
    return (
        output[None],
        image_grad[None],
        embed_grad,
        text_grad[None],
        gains[0],
        conv1_total.reshape(3, 3, channels, share),
        embed_w_grad,
        gains[1],
        conv2_total.reshape(3, 3, channels, share),
        gains[2],
        qkv_total,
        text_w_grad,
        proj_total,
    )


def shards(
    image, embed, text, extent, first_norm_gain1, conv1_w, embed_w, second_norm_gain2, conv2_w,
    attention_norm_gain, qkv_w, text_w, proj_w, cotangent,
):
    images, rows_dev, width, channels = image.shape
    parts = lax.axis_size("rows")
    me = lax.axis_index("rows")
    pairs = images * HEADS // parts
    head_dim = channels // HEADS
    pixels = rows_dev * width
    group = max(1, 512 // pixels)
    span = group * pixels
    chunks = parts // group
    tokens = text.shape[1]
    first_row = jnp.full((images, 1), me * rows_dev, jnp.int32)
    info = jnp.concatenate([extent, first_row], axis=1)
    gain1 = first_norm_gain1.reshape(1, channels)
    gain2 = second_norm_gain2.reshape(1, channels)
    gain3 = attention_norm_gain.reshape(1, channels)
    rowpos = me * rows_dev + jnp.arange(rows_dev, dtype=jnp.int32)
    colpos = jnp.arange(width, dtype=jnp.int32)
    inside = (rowpos[None, :, None] < extent[:, 0, None, None]) & (
        colpos[None, None, :] < extent[:, 1, None, None]
    )
    image_window = inside.astype(F32)[..., None]

    items = lax.axis_size("items")
    own_path = (
        images == 1
        and parts == HEADS
        and channels % (16 * items * parts) == 0
        and pixels % 512 == 0
        and tokens % 16 == 0
        and text.shape[2] % (128 * parts) == 0
        and text.shape[2] == embed.shape[1] <= 4 * channels
    )
    if own_path:
        return own_shards(
            info, image, embed, text, gain1, conv1_w, embed_w, gain2, conv2_w, gain3, qkv_w, text_w,
            proj_w, cotangent,
        )

    embed_float = embed.astype(F32)
    embed_low = jax.nn.silu(embed_float).astype(BF16)
    shifts = jnp.dot(embed_low, embed_w, preferred_element_type=F32)
    qkv_turned = qkv_w.T
    proj_shaped = proj_w.reshape(HEADS, head_dim, channels)

    start = image.astype(F32) * image_window
    zeros = jnp.zeros((images, 6, channels), F32)
    stats0 = jnp.concatenate(
        [
            jnp.sum(start, axis=(1, 2))[:, None],
            jnp.sum(start * start, axis=(1, 2))[:, None],
            zeros,
        ],
        axis=1,
    )
    stats1, image_above, image_below, cot_above, cot_below = exchange(
        stats0, (image, cotangent), 0
    )
    full = jax.ShapeDtypeStruct(image.shape, F32)
    sums = jax.ShapeDtypeStruct((images, 8, channels), F32)
    padded = jax.ShapeDtypeStruct((images, rows_dev + 2, width, channels), BF16)
    first, stats, hidden = conv_call(
        conv1_kernel,
        info,
        (image, image_above, image_below, stats1, gain1),
        conv1_w,
        (full, sums, padded),
        False,
    )
    stats2, first_above, first_below, all_text = exchange(stats, (first,), 1, (text,))
    gathered_text = jnp.moveaxis(all_text, 0, 1).reshape(images, parts * tokens, text.shape[2])
    text_share = text.shape[2] // parts
    text_cols = lax.dynamic_slice_in_dim(gathered_text, me * text_share, text_share, 2)
    text_cols = lax.all_gather(text_cols, "items", axis=0, tiled=True)
    middle, stats, second = conv_call(
        conv2_kernel,
        info,
        (first, first_above, first_below, stats2, gain2, shifts, image),
        conv2_w,
        (full, sums, padded),
        False,
    )
    stats3, mid_above, mid_below = exchange(stats, (middle,), 2)
    attn_flat, qkv_pix = project(info, middle, stats3, gain3, qkv_turned)

    def to_pairs(values):
        wide = values.shape[1]
        moved = lax.all_to_all(values, "rows", split_axis=0, concat_axis=0, tiled=True)
        moved = moved.reshape(chunks, group, pairs, wide, pixels)
        return jnp.transpose(moved, (2, 0, 3, 1, 4)).reshape(pairs, chunks, wide, span)

    def from_pairs(values):
        wide = values.shape[2]
        moved = values.reshape(pairs, chunks, wide, group, pixels)
        moved = jnp.transpose(moved, (1, 3, 0, 2, 4)).reshape(parts * pairs, wide, pixels)
        return lax.all_to_all(moved, "rows", split_axis=0, concat_axis=0, tiled=True)

    qkv_pair = to_pairs(qkv_pix)
    grad_proj = (cotangent.astype(F32) * image_window).astype(BF16).reshape(images, pixels, channels)
    grad_heads = jnp.einsum(
        "ipc,hdc->ihdp", grad_proj, proj_shaped, preferred_element_type=F32
    ).astype(BF16)
    grad_pair = to_pairs(grad_heads.reshape(images * HEADS, head_dim, pixels))
    pair_results = []
    for p in range(pairs):
        pair = me * pairs + p
        item, head = pair // HEADS, pair % HEADS
        weight = lax.dynamic_slice_in_dim(text_w, head * 2 * head_dim, 2 * head_dim, 1)
        own = lax.dynamic_index_in_dim(gathered_text, item, 0, False)
        text_pair = jnp.dot(own, weight, preferred_element_type=F32).astype(BF16)
        pair_extent = lax.dynamic_slice_in_dim(extent, item, 1, 0)
        pair_results.append(attention(pair_extent, qkv_pair[p], text_pair, grad_pair[p], width))
    attended, qkv_grad_pair, text_grad_pair = (jnp.stack(r) for r in zip(*pair_results))
    qkv_back = from_pairs(qkv_grad_pair)
    heads_out = from_pairs(attended).reshape(images, HEADS, head_dim, pixels)

    attn_grad, stats = unproject(info, middle, stats3, qkv_back, qkv_turned)
    stats4, grad_above, grad_below, text_back = exchange(stats, (attn_grad,), 3, (text_grad_pair,))
    text_back = text_back.reshape(images, HEADS, parts * tokens, 2 * head_dim)
    text_all = lax.all_gather(text_back, "items", axis=0, tiled=True)
    proj_grad = jnp.einsum("ipc,ihdp->chd", grad_proj, heads_out, preferred_element_type=F32)
    qkv_grad = jnp.einsum(
        "ihwdp,ipc->hdwc",
        qkv_back.reshape(images, HEADS, 3, head_dim, pixels),
        attn_flat,
        preferred_element_type=F32,
    )
    grad_middle, moved_grad, stats, conv2_grad = conv_call(
        back2_kernel,
        info,
        (attn_grad, grad_above, grad_below, middle, mid_above, mid_below, cotangent, cot_above,
         cot_below, stats3, stats4, gain3, first, stats2, gain2, shifts),
        conv2_w,
        (full, full, sums, padded),
        True,
    )
    stats5, moved_above, moved_below = exchange(stats, (moved_grad,), 4)
    pre_grad, stats, conv1_grad = conv_call(
        back1_kernel,
        info,
        (moved_grad, moved_above, moved_below, first, first_above, first_below, stats2, stats5,
         gain2, shifts, image, stats1, gain1),
        conv1_w,
        (full, sums, padded),
        True,
    )
    (stats6,) = exchange(stats, (), 5)
    image_grad = finish(info, pre_grad, stats6, image, stats1, gain1, grad_middle)

    projected = jnp.einsum(
        "ihdp,hdc->ipc", heads_out, proj_shaped, preferred_element_type=F32
    ).reshape(image.shape)
    output = (middle + projected * image_window).astype(BF16)
    own_text = lax.dynamic_slice_in_dim(text_back, me * tokens, tokens, 2)
    text_shaped = text_w.reshape(text_w.shape[0], HEADS, 2 * head_dim)
    text_grad = jnp.einsum("ihtk,chk->itc", own_text, text_shaped, preferred_element_type=F32)
    text_w_grad = jnp.einsum(
        "gtc,ghtk->chk", text_cols, text_all, preferred_element_type=F32
    ).reshape(text_share, 2 * channels)
    scale_sum = stats5[:, 1] * gain2
    grad_shifts = jnp.concatenate([scale_sum, stats5[:, 0]], axis=1).astype(BF16)
    embed_grad = jnp.einsum(
        "ik,ck->ic", grad_shifts, embed_w, preferred_element_type=F32
    ) * silu_slope(embed_float)
    embed_share = embed_w.shape[0] // parts
    gains = jnp.stack(
        [
            jnp.sum(stats6[:, 1], axis=0),
            jnp.sum(stats5[:, 1] * (1.0 + shifts[:, :channels]), axis=0),
            jnp.sum(stats4[:, 1], axis=0),
        ]
    )
    share = channels // parts
    def total(values):
        return lax.psum(
            lax.psum_scatter(values.astype(BF16), "rows", scatter_dimension=0, tiled=True),
            "items",
        ).astype(F32)

    def kernel_total(values):
        return total(values).T.reshape(3, 3, channels, share)

    conv1_total = kernel_total(weight_grad(conv1_grad, hidden))
    conv2_total = kernel_total(weight_grad(conv2_grad, second))
    by_head = jnp.swapaxes(qkv_grad, 1, 2).reshape(3 * channels, channels)
    qkv_total = total(by_head).T
    proj_total = total(proj_grad.reshape(channels, channels)).T
    gains = lax.psum(gains, "items")
    all_shifts = lax.all_gather(grad_shifts, "items", axis=0, tiled=True)
    embed_rows = lax.dynamic_slice_in_dim(embed_low, me * embed_share, embed_share, 1)
    embed_rows = lax.all_gather(embed_rows, "items", axis=0, tiled=True)
    embed_w_grad = jnp.einsum("ic,ik->ck", embed_rows, all_shifts, preferred_element_type=F32)
    gains = lax.dynamic_slice_in_dim(gains, me * share, share, 1)
    return (
        output,
        image_grad,
        embed_grad,
        text_grad,
        gains[0],
        conv1_total,
        embed_w_grad,
        gains[1],
        conv2_total,
        gains[2],
        qkv_total,
        text_w_grad,
        proj_total,
    )


def solution(mesh):
    in_specs = (
        P("items", "rows", None, None),
        P("items", None),
        P("items", "rows", None),
        P("items", None),
        P(),
        P(),
        P(),
        P(),
        P(),
        P(),
        P(),
        P(),
        P(),
        P("items", "rows", None, None),
    )
    out_specs = (
        P("items", "rows", None, None),
        P("items", "rows", None, None),
        P("items", None),
        P("items", "rows", None),
        P("rows"),
        P(None, None, None, "rows"),
        P("rows", None),
        P("rows"),
        P(None, None, None, "rows"),
        P("rows"),
        P(None, "rows"),
        P("rows", None),
        P(None, "rows"),
    )
    return jax.shard_map(shards, mesh=mesh, in_specs=in_specs, out_specs=out_specs, check_vma=False)
```

```python
import functools

import jax
import jax.numpy as jnp
from jax import lax
from jax.experimental import pallas as pl
from jax.experimental.pallas import tpu as pltpu
from jax.sharding import PartitionSpec as P

GROUPS = 32
HEADS = 8
F32, BF16 = jnp.float32, jnp.bfloat16
NEG = -1e30


def dot(a, b, ca, cb):
    return lax.dot_general(a, b, (((ca,), (cb,)), ((), ())), preferred_element_type=F32)

def nothing(*_):
    return None


class Attention:
    def __init__(self, chunks, span, d, tlen, step, bq, scratch):
        self.chunks, self.span, self.d, self.tlen, self.step, self.bq = chunks, span, d, tlen, step, bq
        self.kn, self.vn, self.kt, self.vt, s0, s1, e0, e1, self.dkt, self.dvt = scratch
        self.scores, self.raised = (s0, s1), (e0, e1)
        self.pix = chunks * span

    def stage_key(self, c, k, width, rows_ok, cols_ok):
        d, span = self.d, self.span
        base = pl.multiple_of(c * span, span)
        pos = base + lax.broadcasted_iota(jnp.int32, (16, span), 1)
        row = lax.broadcasted_iota(jnp.int32, (16, span), 0)
        ok = (pos // width < rows_ok) & (pos % width < cols_ok)
        extra = jnp.where((row == 0) & jnp.logical_not(ok), NEG, 0.0)
        rest = jnp.zeros((128 - d - 16, span), F32)
        self.kt[:, pl.ds(base, span)] = k
        ka = jnp.concatenate([k.astype(F32), extra, rest], axis=0)
        self.kn[pl.ds(base, span), :] = ka.T.astype(BF16)

    def stage_value(self, c, v):
        d, span = self.d, self.span
        base = pl.multiple_of(c * span, span)
        row = lax.broadcasted_iota(jnp.int32, (16, span), 0)
        rest = jnp.zeros((128 - d - 16, span), F32)
        self.vt[:, pl.ds(base, span)] = v
        va = jnp.concatenate([v.astype(F32), jnp.where(row < 3, 1.0, 0.0), rest], axis=0)
        self.vn[pl.ds(base, span), :] = va.T.astype(BF16)

    def stage_text(self, text):
        d, tlen, pix = self.d, self.tlen, self.pix
        tk = text[:, :d].astype(F32)
        tv = text[:, d:].astype(F32)
        self.kt[:, pix:] = tk.T.astype(BF16)
        self.vt[:, pix:] = tv.T.astype(BF16)
        lanes = lax.broadcasted_iota(jnp.int32, (tlen, 128 - d), 1)
        rest = jnp.zeros((tlen, 128 - d), F32)
        self.kn[pix:, :] = jnp.concatenate([tk, rest], axis=1).astype(BF16)
        ones = jnp.where(lanes < 3, 1.0, 0.0)
        self.vn[pix:, :] = jnp.concatenate([tv, ones], axis=1).astype(BF16)

    def query(self, q):
        d, bq = self.d, self.bq
        r = lax.broadcasted_iota(jnp.int32, (128 - d, bq), 0)
        rest = jnp.where(r == 0, 1.0, 0.0)
        return jnp.concatenate([q.astype(F32) * (d**-0.5), rest], axis=0).astype(BF16)

    def run(self, score, exp, back):
        d, bq, step = self.d, self.bq, self.step
        kn, vn, kt, vt, dkt, dvt = self.kn, self.vn, self.kt, self.vt, self.dkt, self.dvt
        scores, raised = self.scores, self.raised

        def body(j, carry):
            pk, total, acc, dq = carry
            at = pl.ds(pl.multiple_of(j * step, step), step)
            if score:
                slot, qa = score
                s = dot(kn[at, :], qa, 1, 0)
                scores[slot][at, :] = s
                pk = jnp.maximum(pk, jnp.max(s.reshape(step // 8, 8, bq), axis=0))
            if exp:
                slot, peak = exp
                e = jnp.exp(scores[slot][at, :] - peak)
                total = total + jnp.sum(e.reshape(step // 8, 8, bq), axis=0)
                low = e.astype(BF16)
                raised[slot][at, :] = low
                acc = acc + dot(vt[:, at], low, 1, 0)
            if back:
                slot, goa, q = back
                dp = dot(vn[at, :], goa, 1, 0)
                e = raised[slot][at, :]
                ds = (e.astype(F32) * dp).astype(BF16)
                dvt[:, at] += dot(goa[:d], e, 1, 1)
                dkt[:, at] += dot(q, ds, 1, 1)
                dq = dq + dot(kt[:, at], ds, 1, 0)
            return pk, total, acc, dq

        init = (
            jnp.full((8, bq), -3e38, F32),
            jnp.zeros((8, bq), F32),
            jnp.zeros((d, bq), F32),
            jnp.zeros((d, bq), F32),
        )
        return lax.fori_loop(0, (self.pix + self.tlen) // step, body, init)

    def attended(self, go, total, acc):
        d, bq = self.d, self.bq
        inv = 1.0 / jnp.sum(total, axis=0, keepdims=True)
        o = acc * inv
        go = go.astype(F32)
        nd = -jnp.sum(go * o, axis=0, keepdims=True) * inv
        hi = nd.astype(BF16).astype(F32)
        mid = (nd - hi).astype(BF16).astype(F32)
        lo = nd - hi - mid
        r = lax.broadcasted_iota(jnp.int32, (16, bq), 0)
        extra = jnp.where(r == 0, hi, jnp.where(r == 1, mid, jnp.where(r == 2, lo, 0.0)))
        rest = jnp.zeros((128 - d - 16, bq), F32)
        return o.astype(BF16), jnp.concatenate([go * inv, extra, rest], axis=0).astype(BF16)

    def attend(self, q_ref, go_ref, o_ref, dq_ref, order, scored=nothing, before=nothing, done=nothing):
        d, bq, chunks = self.d, self.bq, self.chunks
        self.dkt[...] = jnp.zeros_like(self.dkt)
        self.dvt[...] = jnp.zeros_like(self.dvt)

        def columns(half):
            return slice(half * bq, (half + 1) * bq)

        def q_of(h, half):
            return q_ref[order(h), :d, columns(half)]

        def finish_exp(h, half, total, acc):
            c = order(h)
            o, goa = self.attended(go_ref[c, :, columns(half)], total, acc)
            o_ref[c, :, columns(half)] = o
            return goa

        def put_dq(h, half, dq):
            dq_ref[order(h), :d, columns(half)] = (dq * (d**-0.5)).astype(BF16)

        def top(pk):
            return jnp.max(pk, axis=0, keepdims=True)

        run = self.run
        pk, _, _, _ = run((0, self.query(q_of(0, 0))), None, None)
        scored()
        pk, total, acc, _ = run((1, self.query(q_of(0, 1))), (0, top(pk)), None)
        goa = finish_exp(0, 0, total, acc)

        def two(h, carry):
            pk, goa = carry
            before(h + 1)
            qa = self.query(q_of(h + 1, 0))
            pk2, total, acc, dq = run((0, qa), (1, top(pk)), (0, goa, q_of(h, 0)))
            put_dq(h, 0, dq)
            goa = finish_exp(h, 1, total, acc)
            qa = self.query(q_of(h + 1, 1))
            pk3, total, acc, dq = run((1, qa), (0, top(pk2)), (1, goa, q_of(h, 1)))
            put_dq(h, 1, dq)
            done(h)
            return pk3, finish_exp(h + 1, 0, total, acc)

        pk, goa = lax.fori_loop(0, chunks - 1, two, (pk, goa))
        last = chunks - 1
        _, total, acc, dq = run(None, (1, top(pk)), (0, goa, q_of(last, 0)))
        put_dq(last, 0, dq)
        goa = finish_exp(last, 1, total, acc)
        _, _, _, dq = run(None, None, (1, goa, q_of(last, 1)))
        put_dq(last, 1, dq)
        done(last)

    def key_grad(self, at):
        return (self.dkt[:, at] * (self.d**-0.5)).astype(BF16)

    def value_grad(self, at):
        return self.dvt[:, at].astype(BF16)

    def text_grad(self, out):
        d, pix = self.d, self.pix
        out[:, :d] = (self.dkt[:, pix:] * (d**-0.5)).T.astype(BF16)
        out[:, d:] = self.dvt[:, pix:].T.astype(BF16)


def attention_scratch(chunks, span, d, tlen):
    keys = chunks * span + tlen
    bq = span // 2
    lanes = keys // 128
    step = 128 * max(n for n in range(1, 12) if lanes % n == 0)
    shapes = [((keys, 128), BF16)] * 2 + [((d, keys), BF16)] * 2
    shapes += [((keys, bq), F32)] * 2 + [((keys, bq), BF16)] * 2 + [((d, keys), F32)] * 2
    return step, bq, [pltpu.VMEM(*shape) for shape in shapes]


def attention_kernel(width, step, bq, ext_ref, qkv_ref, text_ref, go_ref, out_ref, dqkv_ref, dtext_ref, *scratch):
    chunks, _, span = qkv_ref.shape
    d = go_ref.shape[1]
    att = Attention(chunks, span, d, text_ref.shape[0], step, bq, scratch)

    def stage(c, carry):
        att.stage_key(c, qkv_ref[c, d : 2 * d, :], width, ext_ref[0, 0], ext_ref[0, 1])
        att.stage_value(c, qkv_ref[c, 2 * d :, :])
        return carry

    lax.fori_loop(0, chunks, stage, 0)
    att.stage_text(text_ref)
    att.attend(qkv_ref, go_ref, out_ref, dqkv_ref, lambda h: h)

    def finish(c, carry):
        at = pl.ds(pl.multiple_of(c * span, span), span)
        dqkv_ref[c, d : 2 * d, :] = att.key_grad(at)
        dqkv_ref[c, 2 * d :, :] = att.value_grad(at)
        return carry

    lax.fori_loop(0, chunks, finish, 0)
    att.text_grad(dtext_ref)


def attention(ext, qkv, text, go, width):
    chunks, wide, span = qkv.shape
    d = wide // 3
    tlen = text.shape[0]
    keys = chunks * span + tlen
    step, bq, scratch = attention_scratch(chunks, span, d, tlen)
    vm = pl.BlockSpec(memory_space=pltpu.VMEM)
    flops = 2 * 6 * chunks * span * keys * d
    return pl.pallas_call(
        functools.partial(attention_kernel, width, step, bq),
        out_shape=(
            jax.ShapeDtypeStruct(go.shape, BF16),
            jax.ShapeDtypeStruct(qkv.shape, BF16),
            jax.ShapeDtypeStruct((tlen, 2 * d), BF16),
        ),
        in_specs=[pl.BlockSpec(memory_space=pltpu.SMEM), vm, vm, vm],
        out_specs=(vm, vm, vm),
        scratch_shapes=scratch,
        compiler_params=pltpu.CompilerParams(vmem_limit_bytes=56 << 20),
        cost_estimate=pl.CostEstimate(
            flops=4 * flops, bytes_accessed=16 * chunks * span * d, transcendentals=chunks * span * keys
        ),
    )(ext, qkv, text, go)


MESH = pl.DeviceIdType.MESH
EPS = 1e-05
WHOLE = pl.BlockSpec(memory_space=pltpu.VMEM)
SCALARS = pl.BlockSpec(memory_space=pltpu.SMEM)
ANYWHERE = pl.BlockSpec(memory_space=pl.ANY)


def exchange_kernel(n, count, gathers, *refs):
    inputs, refs = refs[: 1 + count + gathers], refs[1 + count + gathers :]
    outputs, refs = refs[: 1 + 2 * count + gathers], refs[1 + 2 * count + gathers :]
    stats_ref, rows, given = inputs[0], inputs[1 : 1 + count], inputs[1 + count :]
    total_ref, outs, gathered = outputs[0], outputs[1 : 1 + 2 * count], outputs[1 + 2 * count :]
    slots, lands = refs[0], refs[1 : 1 + 2 * count]
    send, recv, row_send, row_recv, own = refs[1 + 2 * count :]
    me = lax.axis_index("rows")
    barrier = pltpu.get_barrier_semaphore()

    def greet(k, carry):
        pl.semaphore_signal(
            barrier, inc=1, device_id={"rows": lax.rem(me + k, n)}, device_id_type=MESH
        )
        return carry

    lax.fori_loop(1, n, greet, 0)
    slots[me] = stats_ref[...]
    pl.semaphore_wait(barrier, n - 1)
    shared = [(stats_ref, slots)] + list(zip(given, gathered))

    def share(j, k):
        return pltpu.make_async_remote_copy(
            src_ref=shared[j][0],
            dst_ref=shared[j][1].at[me],
            send_sem=send.at[j, k],
            recv_sem=recv.at[j, k],
            device_id={"rows": lax.rem(me + k, n)},
            device_id_type=MESH,
        )

    def start(k, carry):
        share(0, k).start()
        return carry

    lax.fori_loop(1, n, start, 0)

    def row_copy(j, side):
        last = rows[j].shape[1] - 1
        at = last if side == 0 else 0
        return pltpu.make_async_remote_copy(
            src_ref=rows[j].at[:, at : at + 1],
            dst_ref=lands[2 * j + side],
            send_sem=row_send.at[2 * j + side],
            recv_sem=row_recv.at[2 * j + side],
            device_id={"rows": me + 1 if side == 0 else me - 1},
            device_id_type=MESH,
        )

    for j in range(count):

        @pl.when(me < n - 1)
        def _():
            row_copy(j, 0).start()

        @pl.when(me > 0)
        def _():
            row_copy(j, 1).start()

    for j in range(gathers):

        def start_given(k, carry):
            share(1 + j, k).start()
            return carry

        lax.fori_loop(1, n, start_given, 0)
        pltpu.make_async_copy(given[j], gathered[j].at[me], own.at[j]).start()

    def finish(k, carry):
        share(0, k).wait()
        return carry

    lax.fori_loop(1, n, finish, 0)
    total_ref[...] = lax.fori_loop(1, n, lambda k, s: s + slots[k], slots[0])
    for j in range(count):

        @pl.when(me > 0)
        def _():
            row_copy(j, 0).wait_recv()
            outs[2 * j][...] = lands[2 * j][...]

        @pl.when(me == 0)
        def _():
            outs[2 * j][...] = jnp.zeros_like(outs[2 * j])

        @pl.when(me < n - 1)
        def _():
            row_copy(j, 1).wait_recv()
            outs[2 * j + 1][...] = lands[2 * j + 1][...]
            row_copy(j, 0).wait_send()

        @pl.when(me == n - 1)
        def _():
            outs[2 * j + 1][...] = jnp.zeros_like(outs[2 * j + 1])

        @pl.when(me > 0)
        def _():
            row_copy(j, 1).wait_send()

    for j in range(gathers):

        def finish_given(k, carry):
            share(1 + j, k).wait()
            return carry

        lax.fori_loop(1, n, finish_given, 0)
        pltpu.make_async_copy(given[j], gathered[j].at[me], own.at[j]).wait()


def exchange(stats, rows, identity, given=()):
    n = lax.axis_size("rows")
    edge = []
    for array in rows:
        edge += [jax.ShapeDtypeStruct(array.shape[:1] + (1,) + array.shape[2:], array.dtype)] * 2
    whole = [jax.ShapeDtypeStruct((n,) + array.shape, array.dtype) for array in given]
    count, gathers = len(rows), len(given)
    nbytes = 4 * stats.size * n + sum(2 * e.size * e.dtype.itemsize for e in (*edge, *whole))
    return pl.pallas_call(
        functools.partial(exchange_kernel, n, count, gathers),
        out_shape=(jax.ShapeDtypeStruct(stats.shape, F32), *edge, *whole),
        in_specs=[WHOLE] + [ANYWHERE] * (count + gathers),
        out_specs=(WHOLE,) * (1 + 2 * count) + (ANYWHERE,) * gathers,
        scratch_shapes=[
            pltpu.VMEM((n,) + stats.shape, F32),
            *[pltpu.VMEM(e.shape, e.dtype) for e in edge],
            pltpu.SemaphoreType.DMA((1 + gathers, n)),
            pltpu.SemaphoreType.DMA((1 + gathers, n)),
            pltpu.SemaphoreType.DMA((max(1, 2 * count),)),
            pltpu.SemaphoreType.DMA((max(1, 2 * count),)),
            pltpu.SemaphoreType.DMA((max(1, gathers),)),
        ],
        compiler_params=pltpu.CompilerParams(collective_id=identity, has_side_effects=True),
        cost_estimate=pl.CostEstimate(
            flops=6_000_000_000, bytes_accessed=nbytes, transcendentals=0
        ),
        name=f"exchange{identity}",
    )(stats, *rows, *given)


def group_matrix(channels):
    size = channels // GROUPS
    one = lax.broadcasted_iota(jnp.int32, (channels, channels), 0) // size
    two = lax.broadcasted_iota(jnp.int32, (channels, channels), 1) // size
    return jnp.where(one == two, 1.0, 0.0).astype(BF16)


def group_sums(rows, same=None):
    if same is None:
        same = group_matrix(rows.shape[1])
    high = rows.astype(BF16).astype(F32)
    mid = (rows - high).astype(BF16).astype(F32)
    tail = rows - high - mid
    sums = dot(jnp.concatenate([high, mid, tail], axis=0).astype(BF16), same, 1, 0)
    n = rows.shape[0]
    return sums[:n] + sums[n : 2 * n] + sums[2 * n :]


def image_count(info, i, channels):
    return (info[i, 0] * info[i, 1]).astype(F32) * (channels // GROUPS)


def norm_of(stats, count, same=None):
    sums = group_sums(stats, same)
    average = sums[0:1] / count
    square = sums[1:2] / count
    return average, lax.rsqrt(square - average * average + EPS)


def means_of(stats, weight, count, same=None):
    sums = group_sums(stats * weight, same)
    return sums[0:1] / count, sums[1:2] / count


def window(info, i, row, shape):
    ok = (row >= 0) & (row < info[i, 0])
    limit = jnp.where(ok, info[i, 1], 0)
    return jnp.where(lax.broadcasted_iota(jnp.int32, shape, 0) < limit, 1.0, 0.0)


def padded_row(center, above, below, i, r):
    if r == 0:
        return above[i, 0]
    if r == center.shape[1] + 1:
        return below[i, 0]
    return center[i, r - 1]


def put_shifted(out, i, r, value, plain=None):
    width, channels = value.shape
    column = lax.broadcasted_iota(jnp.int32, value.shape, 0)
    left = jnp.where(column == 0, 0.0, pltpu.roll(value, 1, 0))
    right = jnp.where(column == width - 1, 0.0, pltpu.roll(value, width - 1, 0))
    out[i, r, :, :channels] = left.astype(BF16)
    low = value.astype(BF16)
    out[i, r, :, channels : 2 * channels] = low
    if plain is not None:
        plain[i, r] = low
    out[i, r, :, 2 * channels :] = right.astype(BF16)


def sigmoid(v):
    return 1.0 / (1.0 + jnp.exp(-v))


def silu_slope(v):
    s = sigmoid(v)
    return s * (1.0 + v * (1.0 - s))


def put_stats(stats_ref, i, first, second):
    channels = first.shape[1]
    one = jnp.sum(first, axis=0, keepdims=True)
    two = jnp.sum(second, axis=0, keepdims=True)
    row = lax.broadcasted_iota(jnp.int32, (8, channels), 0)
    stats_ref[i] = jnp.where(row == 0, one, jnp.where(row == 1, two, 0.0))


def tap_rows(shifted, tap, images, rows_dev, width):
    block = shifted[:, pl.ds(tap, rows_dev)]
    return block.reshape(images * rows_dev * width, shifted.shape[3])


def conv1_kernel(info, image, above, below, stats, gain, weight, first, out_stats, hidden, acc, shifted):
    images, rows_dev, width, channels = image.shape
    tap = pl.program_id(0)
    base = info[0, 2]

    @pl.when(tap == 0)
    def _():
        for i in range(images):
            average, inverse = norm_of(stats[i], image_count(info, i, channels))
            for r in range(rows_dev + 2):
                inside = window(info, i, base + r - 1, (width, channels))
                start = padded_row(image, above, below, i, r).astype(F32) * inside
                value = (start - average) * inverse * inside * gain[...]
                put_shifted(shifted, i, r, value * sigmoid(value) * inside, hidden)

    part = dot(tap_rows(shifted, tap, images, rows_dev, width), weight[0], 1, 0)

    @pl.when(tap == 0)
    def _():
        acc[...] = part

    @pl.when(tap > 0)
    def _():
        acc[...] += part

    @pl.when(tap == 2)
    def _():
        for i in range(images):
            one = two = jnp.zeros((width, channels), F32)
            for r in range(rows_dev):
                inside = window(info, i, base + r, (width, channels))
                at = (i * rows_dev + r) * width
                value = acc[at : at + width] * inside
                first[i, r] = value
                one = one + value
                two = two + value * value
            put_stats(out_stats, i, one, two)


def moved_of(value, inside, average, inverse, gain, scale, shift):
    normal = (value - average) * inverse * inside
    return normal, normal * gain * (1.0 + scale) + shift


def conv2_kernel(
    info, first, above, below, stats, gain, shifts, image, weight, middle, out_stats, second, acc,
    shifted,
):
    images, rows_dev, width, channels = first.shape
    tap = pl.program_id(0)
    base = info[0, 2]

    @pl.when(tap == 0)
    def _():
        for i in range(images):
            average, inverse = norm_of(stats[i], image_count(info, i, channels))
            scale, shift = shifts[i : i + 1, :channels], shifts[i : i + 1, channels:]
            for r in range(rows_dev + 2):
                inside = window(info, i, base + r - 1, (width, channels))
                value = padded_row(first, above, below, i, r)
                _, moved = moved_of(value, inside, average, inverse, gain[...], scale, shift)
                put_shifted(shifted, i, r, moved * sigmoid(moved) * inside, second)

    part = dot(tap_rows(shifted, tap, images, rows_dev, width), weight[0], 1, 0)

    @pl.when(tap == 0)
    def _():
        acc[...] = part

    @pl.when(tap > 0)
    def _():
        acc[...] += part

    @pl.when(tap == 2)
    def _():
        for i in range(images):
            one = two = jnp.zeros((width, channels), F32)
            for r in range(rows_dev):
                inside = window(info, i, base + r, (width, channels))
                at = (i * rows_dev + r) * width
                value = (image[i, r].astype(F32) + acc[at : at + width]) * inside
                middle[i, r] = value
                one = one + value
                two = two + value * value
            put_stats(out_stats, i, one, two)


def dgrad(shifted, tap, weight, images, rows_dev, width):
    channels = weight.shape[2]
    lhs = tap_rows(shifted, tap, images, rows_dev, width)
    part = None
    for b in range(3):
        term = dot(
            lhs[:, b * channels : (b + 1) * channels],
            weight[0, (2 - b) * channels : (3 - b) * channels, :],
            1,
            1,
        )
        part = term if part is None else part + term
    return part


def back2_kernel(
    info, grad, grad_above, grad_below, middle, mid_above, mid_below, cot, cot_above, cot_below,
    mid_stats, grad_stats, attn_gain, first, first_stats, gain, shifts, weight,
    grad_middle, moved_grad, out_stats, plain, acc, shifted,
):
    images, rows_dev, width, channels = first.shape
    tap = pl.program_id(0)
    base = info[0, 2]

    @pl.when(tap == 0)
    def _():
        for i in range(images):
            count = image_count(info, i, channels)
            average, inverse = norm_of(mid_stats[i], count)
            mean, cross = means_of(grad_stats[i], attn_gain[...], count)
            for r in range(rows_dev + 2):
                inside = window(info, i, base + r - 1, (width, channels))
                normal = (padded_row(middle, mid_above, mid_below, i, r) - average) * inverse
                dx = padded_row(grad, grad_above, grad_below, i, r) * attn_gain[...]
                term = (dx - mean - normal * cross) * inverse * inside
                total = padded_row(cot, cot_above, cot_below, i, r).astype(F32) + term
                if 0 < r <= rows_dev:
                    grad_middle[i, r - 1] = total
                put_shifted(shifted, i, r, total * inside, plain)

    part = dgrad(shifted, tap, weight, images, rows_dev, width)

    @pl.when(tap == 0)
    def _():
        acc[...] = part

    @pl.when(tap > 0)
    def _():
        acc[...] += part

    @pl.when(tap == 2)
    def _():
        for i in range(images):
            average, inverse = norm_of(first_stats[i], image_count(info, i, channels))
            scale, shift = shifts[i : i + 1, :channels], shifts[i : i + 1, channels:]
            one = two = jnp.zeros((width, channels), F32)
            for r in range(rows_dev):
                inside = window(info, i, base + r, (width, channels))
                at = (i * rows_dev + r) * width
                normal, moved = moved_of(
                    first[i, r], inside, average, inverse, gain[...], scale, shift
                )
                value = acc[at : at + width] * inside * silu_slope(moved)
                moved_grad[i, r] = value
                one = one + value
                two = two + value * normal
            put_stats(out_stats, i, one, two)


def back1_kernel(
    info, grad, grad_above, grad_below, first, first_above, first_below, first_stats, grad_stats,
    gain, shifts, image, image_stats, first_gain, weight,
    pre_grad, out_stats, plain, acc, shifted,
):
    images, rows_dev, width, channels = first.shape
    tap = pl.program_id(0)
    base = info[0, 2]

    @pl.when(tap == 0)
    def _():
        for i in range(images):
            count = image_count(info, i, channels)
            average, inverse = norm_of(first_stats[i], count)
            factor = gain[...] * (1.0 + shifts[i : i + 1, :channels])
            mean, cross = means_of(grad_stats[i], factor, count)
            for r in range(rows_dev + 2):
                inside = window(info, i, base + r - 1, (width, channels))
                normal = (padded_row(first, first_above, first_below, i, r) - average) * inverse
                dx = padded_row(grad, grad_above, grad_below, i, r) * factor
                put_shifted(shifted, i, r, (dx - mean - normal * cross) * inverse * inside, plain)

    part = dgrad(shifted, tap, weight, images, rows_dev, width)

    @pl.when(tap == 0)
    def _():
        acc[...] = part

    @pl.when(tap > 0)
    def _():
        acc[...] += part

    @pl.when(tap == 2)
    def _():
        for i in range(images):
            average, inverse = norm_of(image_stats[i], image_count(info, i, channels))
            one = two = jnp.zeros((width, channels), F32)
            for r in range(rows_dev):
                inside = window(info, i, base + r, (width, channels))
                at = (i * rows_dev + r) * width
                normal = (image[i, r].astype(F32) - average) * inverse * inside
                slope = silu_slope(normal * first_gain[...])
                value = acc[at : at + width] * inside * slope
                pre_grad[i, r] = value
                one = one + value
                two = two + value * normal
            put_stats(out_stats, i, one, two)


def conv_call(kernel, info, inputs, weight, outs, flipped):
    images, rows_dev, width, channels = outs[0].shape

    def whole(shape):
        return pl.BlockSpec(shape, lambda tap: (0,) * len(shape))

    def tap_of(tap):
        return ((2 - tap) if flipped else tap, 0, 0)

    weight = weight.reshape(3, 3 * channels, channels)
    flops = 2 * 9 * images * rows_dev * width * channels * channels
    moved = sum(a.size * a.dtype.itemsize for a in (*inputs, weight, *outs))
    return pl.pallas_call(
        kernel,
        grid=(3,),
        out_shape=tuple(outs),
        in_specs=[SCALARS]
        + [whole(a.shape) for a in inputs]
        + [pl.BlockSpec((1, 3 * channels, channels), tap_of)],
        out_specs=tuple(whole(o.shape) for o in outs),
        scratch_shapes=[
            pltpu.VMEM((images * rows_dev * width, channels), F32),
            pltpu.VMEM((images, rows_dev + 2, width, 3 * channels), BF16),
        ],
        compiler_params=pltpu.CompilerParams(vmem_limit_bytes=48 << 20),
        cost_estimate=pl.CostEstimate(flops=flops, bytes_accessed=moved, transcendentals=0),
        name=kernel.__name__,
    )(info, *inputs, weight)


def weight_grad_kernel(grads, hidden, out, turned, shifted):
    images, padded, width, channels = hidden.shape
    rows_dev = padded - 2
    pixels = images * rows_dev * width
    tap = pl.program_id(0)

    @pl.when(tap == 0)
    def _():
        center = grads[:, 1 : rows_dev + 1]
        turned[...] = center.reshape(pixels, channels).astype(F32).T.astype(BF16)
        for i in range(images):
            for r in range(padded):
                put_shifted(shifted, i, r, hidden[i, r].astype(F32))

    column = pl.multiple_of((tap % 3) * channels, channels)
    rhs = shifted[:, pl.ds(tap // 3, rows_dev), :, pl.ds(column, channels)]
    out[...] = dot(turned[...], rhs.reshape(pixels, channels), 1, 0).astype(BF16)


def weight_grad(grads, hidden):
    images, padded, width, channels = hidden.shape
    pixels = images * (padded - 2) * width

    def whole(shape):
        return pl.BlockSpec(shape, lambda tap: (0,) * len(shape))

    return pl.pallas_call(
        weight_grad_kernel,
        grid=(9,),
        out_shape=jax.ShapeDtypeStruct((channels, 9 * channels), BF16),
        in_specs=[whole(grads.shape), whole(hidden.shape)],
        out_specs=pl.BlockSpec((channels, channels), lambda tap: (0, tap)),
        scratch_shapes=[
            pltpu.VMEM((channels, pixels), BF16),
            pltpu.VMEM(hidden.shape[:3] + (3 * channels,), BF16),
        ],
        compiler_params=pltpu.CompilerParams(vmem_limit_bytes=32 << 20),
        cost_estimate=pl.CostEstimate(
            flops=18 * pixels * channels * channels,
            bytes_accessed=18 * channels * channels,
            transcendentals=0,
        ),
        name="weight_grad",
    )(grads, hidden)


def project_kernel(info, middle, stats, gain, weight, attn, qkv):
    images, rows_dev, width, channels = middle.shape
    pixels = rows_dev * width
    heads, wide = HEADS, weight.shape[0] // HEADS
    base = info[0, 2]
    for i in range(images):
        average, inverse = norm_of(stats[i], image_count(info, i, channels))
        for r in range(rows_dev):
            inside = window(info, i, base + r, (width, channels))
            value = (middle[i, r] - average) * inverse * inside * gain[...]
            attn[i, r * width : (r + 1) * width] = value.astype(BF16)
        for h in range(heads):
            block = dot(weight[h * wide : (h + 1) * wide], attn[i], 1, 1)
            qkv[i * heads + h] = block.astype(BF16)


def project(info, middle, stats, gain, weight):
    images, rows_dev, width, channels = middle.shape
    pixels = rows_dev * width
    return pl.pallas_call(
        project_kernel,
        out_shape=(
            jax.ShapeDtypeStruct((images, pixels, channels), BF16),
            jax.ShapeDtypeStruct((images * HEADS, weight.shape[0] // HEADS, pixels), BF16),
        ),
        in_specs=[SCALARS, WHOLE, WHOLE, WHOLE, WHOLE],
        out_specs=(WHOLE, WHOLE),
        compiler_params=pltpu.CompilerParams(vmem_limit_bytes=32 << 20),
        name="project",
    )(info, middle, stats, gain, weight)


def unproject_kernel(info, middle, stats, grads, weight, out, out_stats):
    images, rows_dev, width, channels = middle.shape
    wide, pixels = grads.shape[1], grads.shape[2]
    base = info[0, 2]
    for i in range(images):
        average, inverse = norm_of(stats[i], image_count(info, i, channels))
        acc = None
        for h in range(HEADS):
            turned = grads[i * HEADS + h].astype(F32).T.astype(BF16)
            term = dot(turned, weight[h * wide : (h + 1) * wide], 1, 0)
            acc = term if acc is None else acc + term
        one = two = jnp.zeros((width, channels), F32)
        for r in range(rows_dev):
            inside = window(info, i, base + r, (width, channels))
            value = acc[r * width : (r + 1) * width] * inside
            out[i, r] = value
            one = one + value
            two = two + value * ((middle[i, r] - average) * inverse)
        put_stats(out_stats, i, one, two)


def unproject(info, middle, stats, grads, weight):
    images, rows_dev, width, channels = middle.shape
    return pl.pallas_call(
        unproject_kernel,
        out_shape=(
            jax.ShapeDtypeStruct(middle.shape, F32),
            jax.ShapeDtypeStruct(stats.shape, F32),
        ),
        in_specs=[SCALARS, WHOLE, WHOLE, WHOLE, WHOLE],
        out_specs=(WHOLE, WHOLE),
        compiler_params=pltpu.CompilerParams(vmem_limit_bytes=32 << 20),
        name="unproject",
    )(info, middle, stats, grads, weight)


def finish_kernel(info, pre_grad, grad_stats, image, stats, gain, grad_middle, out):
    images, rows_dev, width, channels = image.shape
    base = info[0, 2]
    for i in range(images):
        count = image_count(info, i, channels)
        average, inverse = norm_of(stats[i], count)
        mean, cross = means_of(grad_stats[i], gain[...], count)
        for r in range(rows_dev):
            inside = window(info, i, base + r, (width, channels))
            normal = (image[i, r].astype(F32) - average) * inverse
            term = (pre_grad[i, r] * gain[...] - mean - normal * cross) * inverse
            out[i, r] = (grad_middle[i, r] + term) * inside


def finish(info, pre_grad, grad_stats, image, stats, gain, grad_middle):
    return pl.pallas_call(
        finish_kernel,
        out_shape=jax.ShapeDtypeStruct(image.shape, F32),
        in_specs=[SCALARS] + [WHOLE] * 6,
        out_specs=WHOLE,
        compiler_params=pltpu.CompilerParams(vmem_limit_bytes=32 << 20),
        name="finish",
    )(info, pre_grad, grad_stats, image, stats, gain, grad_middle)


DMA = pltpu.SemaphoreType.DMA


def remote(src, dst, send, recv, device):
    return pltpu.make_async_remote_copy(
        src_ref=src,
        dst_ref=dst,
        send_sem=send,
        recv_sem=recv,
        device_id=device,
        device_id_type=MESH,
    )


class Grid:
    def __init__(self, items, n):
        self.items, self.n = items, n
        self.item, self.me = lax.axis_index("items"), lax.axis_index("rows")

    def row(self, k):
        return {"items": self.item, "rows": lax.rem(self.me + k, self.n)}

    def peer(self, k):
        return {"items": lax.rem(self.item + k, self.items), "rows": self.me}

    def greet(self):
        barrier = pltpu.get_barrier_semaphore()

        def rows(k, carry):
            pl.semaphore_signal(barrier, inc=1, device_id=self.row(k), device_id_type=MESH)
            return carry

        def items(k, carry):
            pl.semaphore_signal(barrier, inc=1, device_id=self.peer(k), device_id_type=MESH)
            return carry

        lax.fori_loop(1, self.n, rows, 0)
        lax.fori_loop(1, self.items, items, 0)

    def met(self):
        pl.semaphore_wait(pltpu.get_barrier_semaphore(), self.n + self.items - 2)

    def loop(self, count, body):
        def step(k, carry):
            body(k)
            return carry

        lax.fori_loop(1, count, step, 0)


class Sums:
    def __init__(self, grid, own, slots, send, recv):
        self.grid, self.own, self.slots, self.send, self.recv = grid, own, slots, send, recv

    def copy(self, k):
        return remote(
            self.own, self.slots.at[self.grid.me], self.send.at[k], self.recv.at[k], self.grid.row(k)
        )

    def start(self):
        self.grid.loop(self.grid.n, lambda k: self.copy(k).start())
        self.slots[self.grid.me] = self.own[...]

    def result(self):
        self.grid.loop(self.grid.n, lambda k: self.copy(k).wait())
        slots = self.slots
        return lax.fori_loop(1, self.grid.n, lambda k, s: s + slots[k], slots[0])


class Edges:
    def __init__(self, grid, field, send, recv):
        self.grid, self.field, self.send, self.recv = grid, field, send, recv

    def copy(self, side):
        last = self.field.shape[0] - 1
        at, to = (last - 1, 0) if side == 0 else (1, last)
        grid = self.grid
        return remote(
            self.field.at[at : at + 1],
            self.field.at[to : to + 1],
            self.send.at[side],
            self.recv.at[side],
            {"items": grid.item, "rows": grid.me + 1 if side == 0 else grid.me - 1},
        )

    def both(self, down, up):
        @pl.when(self.grid.me < self.grid.n - 1)
        def _():
            down()

        @pl.when(self.grid.me > 0)
        def _():
            up()

    def clear(self):
        last = self.field.shape[0] - 1

        @pl.when(self.grid.me == 0)
        def _():
            self.field[0] = jnp.zeros(self.field.shape[1:], self.field.dtype)

        @pl.when(self.grid.me == self.grid.n - 1)
        def _():
            self.field[last] = jnp.zeros(self.field.shape[1:], self.field.dtype)

    def start(self):
        self.both(lambda: self.copy(0).start(), lambda: self.copy(1).start())

    def wait(self):
        self.both(lambda: self.copy(1).wait_recv(), lambda: self.copy(0).wait_recv())
        self.both(lambda: self.copy(0).wait_send(), lambda: self.copy(1).wait_send())


def shift_into(out, r, value):
    width, channels = value.shape
    column = lax.broadcasted_iota(jnp.int32, value.shape, 0)
    left = jnp.where(column == 0, 0.0, pltpu.roll(value, 1, 0))
    right = jnp.where(column == width - 1, 0.0, pltpu.roll(value, width - 1, 0))
    out[r, :, :channels] = left.astype(BF16)
    out[r, :, channels : 2 * channels] = value.astype(BF16)
    out[r, :, 2 * channels :] = right.astype(BF16)


def row_stats(rows, width, channels, row):
    def step(r, carry):
        one, two = row(r)
        return carry[0] + one, carry[1] + two

    zero = jnp.zeros((width, channels), F32)
    one, two = lax.fori_loop(0, rows, step, (zero, zero))
    one = jnp.sum(one, axis=0, keepdims=True)
    two = jnp.sum(two, axis=0, keepdims=True)
    at = lax.broadcasted_iota(jnp.int32, (8, channels), 0)
    return jnp.where(at == 0, one, jnp.where(at == 1, two, 0.0))


def each_row(rows, body):
    def step(r, carry):
        body(r)
        return carry

    lax.fori_loop(0, rows, step, 0)


def conv_taps(shifted, weight, acc, rows_dev):
    pixels, wide = acc.shape[0], shifted.shape[2]
    acc[...] = jnp.zeros_like(acc)

    def step(tap, carry):
        acc[...] += dot(shifted[pl.ds(tap, rows_dev)].reshape(pixels, wide), weight[tap], 1, 0)
        return carry

    lax.fori_loop(0, 3, step, 0)


def forward_kernel(items, n, step, bq, *refs):
    (info, image, cot, text, embed, gain1, gain2, gain3, w1_in, w2_in, embed_in, text_in, qkv_in, proj_in,
     first_out, mid_out, cot_out, hidden_all, second_all, attn_out, turned_out, o_out, dq_out, dkv_out, dt_out,
     dt_all, text_cols, stats_out, shifts_out,
     image_v, cot_v, text_v, w1, w2, embed_w, text_w, qkv_w, proj_w, first_v, mid_v, hidden, second, attn,
     turned, keys, values, queries, go, text_kv, cols, shifted, acc, own, slots,
     key_land, value_land, query_land, go_land, text_pair, o, dq, dkv, dtext, same,
     load, sum_send, sum_recv, edge_send, edge_recv, row_send, row_recv, item_send, item_recv,
     *scratch) = refs
    grid = Grid(items, n)
    item, me = grid.item, grid.me
    rows_dev, width, channels = image.shape
    pixels = rows_dev * width
    heads, head_dim, wide = HEADS, channels // HEADS, 3 * channels // HEADS
    base = me * rows_dev
    count = (info[0, 0] * info[0, 1]).astype(F32) * (channels // GROUPS)
    att = Attention(n, pixels, head_dim, n * text.shape[0], step, bq, scratch)

    def inside(row):
        return window(info, 0, row, (width, channels))

    loads = []

    def fetch(src, dst):
        c = pltpu.make_async_copy(src, dst, load.at[len(loads)])
        c.start()
        loads.append(c)
        return c

    center = slice(1, rows_dev + 1)
    got_image = fetch(image, image_v.at[center])
    got_cot = fetch(cot, cot_v.at[center])
    got_proj = fetch(proj_in, proj_w)
    got_text = fetch(text, text_v)
    got_text_w = fetch(text_in, text_w)
    got_w1 = fetch(w1_in, w1)
    got_embed_w = fetch(embed_in, embed_w)
    got_w2 = fetch(w2_in, w2)
    got_qkv_w = fetch(qkv_in, qkv_w)
    edges = [
        Edges(grid, field, edge_send.at[j], edge_recv.at[j])
        for j, field in enumerate((image_v, cot_v, first_v, mid_v))
    ]
    sums = [Sums(grid, own.at[j], slots.at[j], sum_send.at[j], sum_recv.at[j]) for j in range(3)]
    grid.greet()
    for e in edges:
        e.clear()
    same[...] = group_matrix(channels)
    got_image.wait()

    def start_row(r):
        return image_v[1 + r].astype(F32) * inside(base + r)

    def start_stats(r):
        v = start_row(r)
        return v, v * v

    own[0] = row_stats(rows_dev, width, channels, start_stats)
    grid.met()
    sums[0].start()
    edges[0].start()
    got_cot.wait()
    edges[1].start()

    got_text.wait()
    got_text_w.wait()
    text_all = dot(text_v[...], text_w[...], 1, 0).astype(BF16)
    share = text_v.shape[1] // n
    for h in range(heads):
        text_kv[h] = text_all[:, h * 2 * head_dim : (h + 1) * 2 * head_dim]
    for r in range(n):
        cols[r] = text_v[:, r * share : (r + 1) * share]

    def scatter(j, src, dst):
        def copy(k):
            to = lax.rem(me + k, n)
            return remote(src.at[to], dst.at[me], row_send.at[j, k], row_recv.at[j, k], grid.row(k))

        return copy

    kv_copy = scatter(0, text_kv, text_pair)
    col_copy = scatter(1, cols, text_cols.at[item])
    grid.loop(n, lambda k: kv_copy(k).start())
    grid.loop(n, lambda k: col_copy(k).start())
    own_kv = fetch(text_kv.at[me], text_pair.at[me])
    own_col = fetch(cols.at[me], text_cols.at[item, me])

    got_proj.wait()

    def to_grad(r):
        attn[pl.ds(r * width, width)] = (cot_v[1 + r].astype(F32) * inside(base + r)).astype(BF16)

    each_row(rows_dev, to_grad)
    for h in range(heads):
        go[h] = dot(proj_w[h * head_dim : (h + 1) * head_dim], attn[...], 1, 1).astype(BF16)
    go_copy = scatter(2, go, go_land)
    own_go = fetch(go.at[me], go_land.at[me])

    stats = sums[0].result()
    stats_out[0] = stats
    average, inverse = norm_of(stats, count, same[...])
    edges[0].wait()

    def to_hidden(r):
        ok = inside(base + r - 1)
        value = (image_v[r].astype(F32) * ok - average) * inverse * ok * gain1[...]
        value = value * sigmoid(value) * ok
        shift_into(shifted, r, value)
        hidden[r] = value.astype(BF16)

    each_row(rows_dev + 2, to_hidden)

    def spread(j, src, dst):
        def copy(k):
            return remote(src, dst.at[item], item_send.at[j, k], item_recv.at[j, k], grid.peer(k))

        return copy

    hidden_copy = spread(0, hidden, hidden_all)
    grid.loop(items, lambda k: hidden_copy(k).start())
    own_hidden = fetch(hidden, hidden_all.at[item])
    got_w1.wait()
    conv_taps(shifted, w1, acc, rows_dev)

    def first_row(r):
        value = acc[pl.ds(r * width, width)] * inside(base + r)
        first_v[1 + r] = value
        return value, value * value

    own[1] = row_stats(rows_dev, width, channels, first_row)
    sums[1].start()
    edges[2].start()

    e = embed[...].astype(F32)
    low = (e * sigmoid(e)).astype(BF16)
    got_embed_w.wait()
    shifts_out[...] = dot(low, embed_w[...], 1, 0)
    scale, shift = shifts_out[:, :channels], shifts_out[:, channels:]

    stats = sums[1].result()
    stats_out[1] = stats
    average, inverse = norm_of(stats, count, same[...])
    edges[2].wait()
    own_first = fetch(first_v, first_out)

    def to_second(r):
        ok = inside(base + r - 1)
        _, moved = moved_of(first_v[r], ok, average, inverse, gain2[...], scale, shift)
        value = moved * sigmoid(moved) * ok
        shift_into(shifted, r, value)
        second[r] = value.astype(BF16)

    each_row(rows_dev + 2, to_second)
    second_copy = spread(1, second, second_all)
    grid.loop(items, lambda k: second_copy(k).start())
    own_second = fetch(second, second_all.at[item])
    got_w2.wait()
    conv_taps(shifted, w2, acc, rows_dev)

    def middle_row(r):
        value = (image_v[1 + r].astype(F32) + acc[pl.ds(r * width, width)]) * inside(base + r)
        mid_v[1 + r] = value
        return value, value * value

    own[2] = row_stats(rows_dev, width, channels, middle_row)
    sums[2].start()
    edges[3].start()
    edges[1].wait()
    own_cot = fetch(cot_v, cot_out)
    got_qkv_w.wait()
    for j in range(3):
        block = qkv_w[:, j * channels : (j + 1) * channels].astype(F32).T
        turned[j * channels : (j + 1) * channels] = block.astype(BF16)
    own_turned = fetch(turned, turned_out)

    stats = sums[2].result()
    stats_out[2] = stats
    average, inverse = norm_of(stats, count, same[...])

    def to_attn(r):
        value = (mid_v[1 + r] - average) * inverse * inside(base + r) * gain3[...]
        attn[pl.ds(r * width, width)] = value.astype(BF16)

    each_row(rows_dev, to_attn)
    own_attn = fetch(attn, attn_out)
    key_copy = scatter(3, keys, key_land)
    value_copy = scatter(4, values, value_land)
    query_copy = scatter(5, queries, query_land)

    def head(k):
        to = lax.rem(me + k, n)
        rows = pl.ds(pl.multiple_of(to * wide, wide), wide)
        block = dot(turned[rows], attn[...], 1, 1).astype(BF16)
        queries[to] = block[:head_dim]
        keys[to] = block[head_dim : 2 * head_dim]
        values[to] = block[2 * head_dim :]

    def send_head(k):
        head(k)
        key_copy(k).start()

    grid.loop(n, send_head)
    head(0)
    query_land[me] = queries[me]
    att.stage_key(me, keys[me], width, info[0, 0], info[0, 1])
    att.stage_value(me, values[me])
    grid.loop(n, lambda k: kv_copy(k).wait())
    own_kv.wait()
    att.stage_text(text_pair[...].reshape(n * text.shape[0], 2 * head_dim))
    edges[3].wait()
    own_mid = fetch(mid_v, mid_out)

    def source(k):
        return lax.rem(me + n - k, n)

    def stage_key(k):
        key_copy(k).wait()
        att.stage_key(source(k), key_land[source(k)], width, info[0, 0], info[0, 1])

    grid.loop(n, stage_key)
    grid.loop(n, lambda k: value_copy(k).start())

    def scored():
        def stage_value(k):
            value_copy(k).wait()
            att.stage_value(source(k), value_land[source(k)])

        grid.loop(n, stage_value)

        def rest(k):
            query_copy(k).start()
            go_copy(k).start()

        grid.loop(n, rest)
        own_go.wait()

    def before(k):
        query_copy(k).wait()
        go_copy(k).wait()

    def give(j, src, dst):
        def copy(h):
            to = source(h)
            return remote(
                src.at[to],
                dst.at[me],
                row_send.at[j, h],
                row_recv.at[j, h],
                {"items": item, "rows": to},
            )

        return copy

    o_copy = give(6, o, o_out)
    dq_copy = give(7, dq, dq_out)
    dkv_copy = give(8, dkv, dkv_out)
    dt_copy = give(9, dtext, dt_out)

    def done(h):
        @pl.when(h > 0)
        def _():
            o_copy(h).start()
            dq_copy(h).start()

    att.attend(query_land, go_land, o, dq, source, scored, before, done)

    def send_keys(h):
        at = pl.ds(pl.multiple_of(source(h) * pixels, pixels), pixels)
        dkv[source(h), :head_dim] = att.key_grad(at)
        dkv[source(h), head_dim:] = att.value_grad(at)

    def send_next(h):
        send_keys(h)
        dkv_copy(h).start()

    grid.loop(n, send_next)
    send_keys(0)
    flat = jnp.concatenate(
        [
            (att.dkt[:, n * pixels :] * (head_dim**-0.5)).T,
            att.dvt[:, n * pixels :].T,
        ],
        axis=1,
    )
    for r in range(n):
        tokens = text.shape[0]
        dtext[r] = flat[r * tokens : (r + 1) * tokens].astype(BF16)
    grid.loop(n, lambda h: dt_copy(h).start())

    def gather_copy(k):
        return remote(
            dtext, dt_all.at[item, me], row_send.at[10, k], row_recv.at[10, k], grid.row(k)
        )

    grid.loop(n, lambda k: gather_copy(k).start())
    own_o = fetch(o.at[me], o_out.at[me])
    own_dq = fetch(dq.at[me], dq_out.at[me])
    own_dkv = fetch(dkv.at[me], dkv_out.at[me])
    own_dt = fetch(dtext.at[me], dt_out.at[me])
    own_all = fetch(dtext, dt_all.at[item, me])
    grid.loop(n, lambda k: col_copy(k).wait())
    own_col.wait()
    cols_copy = spread(2, text_cols.at[item], text_cols)
    grid.loop(items, lambda k: cols_copy(k).start())
    grid.loop(items, lambda k: hidden_copy(k).wait())
    grid.loop(items, lambda k: second_copy(k).wait())
    grid.loop(items, lambda k: cols_copy(k).wait())
    for copy in (o_copy, dq_copy, dkv_copy, dt_copy, gather_copy):
        grid.loop(n, lambda h: copy(h).wait())
    for c in (own_hidden, own_first, own_second, own_cot, own_turned, own_attn, own_mid, own_o, own_dq, own_dkv,
              own_dt, own_all):
        c.wait()


def forward_call(info, image, cot, text, embed, gains, weights, identity):
    items, n = lax.axis_size("items"), lax.axis_size("rows")
    rows_dev, width, channels = image.shape
    pixels = rows_dev * width
    padded = (rows_dev + 2, width, channels)
    tokens, text_width = text.shape
    head_dim = channels // HEADS
    w1, w2, embed_w, text_w, qkv_w, proj_w = weights
    sds = jax.ShapeDtypeStruct
    outs = (
        sds(padded, F32),
        sds(padded, F32),
        sds(padded, BF16),
        sds((items,) + padded, BF16),
        sds((items,) + padded, BF16),
        sds((pixels, channels), BF16),
        sds((3 * channels, channels), BF16),
        sds((n, head_dim, pixels), BF16),
        sds((n, head_dim, pixels), BF16),
        sds((n, 2 * head_dim, pixels), BF16),
        sds((n, tokens, 2 * head_dim), BF16),
        sds((items, n, n, tokens, 2 * head_dim), BF16),
        sds((items, n, tokens, text_width // n), BF16),
        sds((3, 8, channels), F32),
        sds((1, 2 * channels), F32),
    )
    v = pltpu.VMEM
    scratch = [
        v(padded, BF16),
        v(padded, BF16),
        v(text.shape, BF16),
        v(w1.shape, BF16),
        v(w2.shape, BF16),
        v(embed_w.shape, BF16),
        v(text_w.shape, BF16),
        v(qkv_w.shape, BF16),
        v(proj_w.shape, BF16),
        v(padded, F32),
        v(padded, F32),
        v(padded, BF16),
        v(padded, BF16),
        v((pixels, channels), BF16),
        v((3 * channels, channels), BF16),
        v((n, head_dim, pixels), BF16),
        v((n, head_dim, pixels), BF16),
        v((n, head_dim, pixels), BF16),
        v((n, head_dim, pixels), BF16),
        v((n, tokens, 2 * head_dim), BF16),
        v((n, tokens, text_width // n), BF16),
        v((rows_dev + 2, width, 3 * channels), BF16),
        v((pixels, channels), F32),
        v((3, 8, channels), F32),
        v((3, n, 8, channels), F32),
        v((n, head_dim, pixels), BF16),
        v((n, head_dim, pixels), BF16),
        v((n, head_dim, pixels), BF16),
        v((n, head_dim, pixels), BF16),
        v((n, tokens, 2 * head_dim), BF16),
        v((n, head_dim, pixels), BF16),
        v((n, head_dim, pixels), BF16),
        v((n, 2 * head_dim, pixels), BF16),
        v((n, tokens, 2 * head_dim), BF16),
        v((channels, channels), BF16),
        DMA((28,)),
        DMA((3, n)),
        DMA((3, n)),
        DMA((4, 2)),
        DMA((4, 2)),
        DMA((11, n)),
        DMA((11, n)),
        DMA((3, items)),
        DMA((3, items)),
    ]
    step, bq, extra = attention_scratch(n, pixels, head_dim, n * tokens)
    scratch += extra
    return pl.pallas_call(
        functools.partial(forward_kernel, items, n, step, bq),
        out_shape=outs,
        in_specs=[SCALARS] + [ANYWHERE] * 3 + [WHOLE] * 4 + [ANYWHERE] * 6,
        out_specs=(ANYWHERE,) * 13 + (WHOLE,) * 2,
        scratch_shapes=scratch,
        compiler_params=pltpu.CompilerParams(
            collective_id=identity, has_side_effects=True, vmem_limit_bytes=62 << 20
        ),
        cost_estimate=pl.CostEstimate(
            flops=40 * pixels * channels * channels, bytes_accessed=60 << 20, transcendentals=0
        ),
        name="forward",
    )(info, image, cot, text, embed, *gains, *weights)


class KernelSum:
    def __init__(self, grid, turned, quarter, part, from_core, chip_sum, from_chip, final, item_sems, core_sems,
                 chip_sems, final_sems):
        self.grid = grid
        self.turned, self.quarter, self.part, self.from_core = turned, quarter, part, from_core
        self.chip_sum, self.from_chip, self.final = chip_sum, from_chip, final
        self.item_sems, self.core_sems = item_sems, core_sems
        self.chip_sems, self.final_sems = chip_sems, final_sems
        self.chips = grid.n // 2
        self.chip, self.core = grid.me // 2, lax.rem(grid.me, 2)

    def grads_copy(self, k):
        grid = self.grid
        send, recv = self.item_sems
        to = lax.rem(grid.item + k, grid.items)
        return remote(
            self.turned.at[to], self.quarter.at[grid.item], send.at[k], recv.at[k], grid.peer(k)
        )

    def send_grads(self, shifted):
        grid, chips = self.grid, self.chips
        rows_dev, width, channels = shifted.shape[0] - 2, shifted.shape[1], shifted.shape[2] // 3
        center = shifted[1 : rows_dev + 1, :, channels : 2 * channels]
        block = center.reshape(rows_dev * width, channels).astype(F32).T.astype(BF16)
        share = channels // grid.n
        rows = share // grid.items
        for z in range(chips):
            for c in range(2):
                for q in range(grid.items):
                    at = (z * 2 + c) * share + q * rows
                    to = (c * chips + z) * rows
                    self.turned[q, to : to + rows] = block[at : at + rows]
        grid.loop(grid.items, lambda k: self.grads_copy(k).start())
        self.quarter[grid.item] = self.turned[grid.item]

    def wait_grads(self):
        self.grid.loop(self.grid.items, lambda k: self.grads_copy(k).wait())

    def core_copy(self, a):
        send, recv = self.core_sems
        grid = self.grid
        return remote(
            self.part.at[a, 1 - self.core],
            self.from_core.at[a],
            send.at[a],
            recv.at[a],
            {"items": grid.item, "rows": grid.me + 1 - 2 * self.core},
        )

    def compute(self, a, shifted):
        items, padded, width, wide = shifted.shape
        rows_dev, channels = padded - 2, wide // 3
        half = self.turned.shape[1] // 2
        for b in range(3):
            acc = None
            for g in range(items):
                rhs = shifted[g, a : a + rows_dev, :, b * channels : (b + 1) * channels]
                term = dot(self.quarter[g], rhs.reshape(rows_dev * width, channels), 1, 0)
                acc = term if acc is None else acc + term
            self.part[a, 0, b] = acc[:half].astype(BF16)
            self.part[a, 1, b] = acc[half:].astype(BF16)
        self.core_copy(a).start()

    def chip_copy(self, a, k):
        send, recv = self.chip_sems
        grid = self.grid
        to = lax.rem(self.chip + k, self.chips)
        return remote(
            self.chip_sum.at[a, to],
            self.from_chip.at[a, k],
            send.at[a, k],
            recv.at[a, k],
            {"items": grid.item, "rows": to * 2 + self.core},
        )

    def over_chips(self, a):
        self.core_copy(a).wait()
        rows = self.chip_sum.shape[3]
        for b in range(3):
            both = self.part[a, self.core, b].astype(F32) + self.from_core[a, b].astype(F32)
            for z in range(self.chips):
                self.chip_sum[a, z, b] = both[z * rows : (z + 1) * rows].astype(BF16)
        for k in range(1, self.chips):
            self.chip_copy(a, k).start()

    def final_copy(self, a, k):
        send, recv = self.final_sems
        mine = self.final.at[a, self.grid.item]
        return remote(mine, mine, send.at[a, k], recv.at[a, k], self.grid.peer(k))

    def over_items(self, a):
        for k in range(1, self.chips):
            self.chip_copy(a, k).wait()
        total = self.chip_sum[a, self.chip].astype(F32)
        for k in range(1, self.chips):
            total = total + self.from_chip[a, k].astype(F32)
        self.final[a, self.grid.item] = total.astype(BF16)
        for k in range(1, self.grid.items):
            self.final_copy(a, k).start()

    def wait_final(self, a):
        for k in range(1, self.grid.items):
            self.final_copy(a, k).wait()


class SideSum:
    def __init__(self, grid, values, from_core, core_sum, from_item, item_sum, from_chip, final, core_sems,
                 item_sems, chip_sems, final_sems):
        self.grid = grid
        self.values, self.from_core, self.core_sum = values, from_core, core_sum
        self.from_item, self.item_sum, self.from_chip, self.final = (
            from_item,
            item_sum,
            from_chip,
            final,
        )
        self.core_sems, self.item_sems = core_sems, item_sems
        self.chip_sems, self.final_sems = chip_sems, final_sems
        self.chips = grid.n // 2
        self.chip, self.core = grid.me // 2, lax.rem(grid.me, 2)

    def core_copy(self):
        send, recv = self.core_sems
        grid = self.grid
        return remote(
            self.values.at[1 - self.core],
            self.from_core,
            send.at[0],
            recv.at[0],
            {"items": grid.item, "rows": grid.me + 1 - 2 * self.core},
        )

    def item_copy(self, k):
        send, recv = self.item_sems
        grid = self.grid
        to = lax.rem(grid.item + k, grid.items)
        return remote(
            self.core_sum.at[to], self.from_item.at[k], send.at[k], recv.at[k], grid.peer(k)
        )

    def over_items(self):
        self.core_copy().wait()
        for z in range(self.chips):
            both = self.values[self.core, z].astype(F32) + self.from_core[z].astype(F32)
            for q in range(self.grid.items):
                self.core_sum[q, z] = both[q].astype(BF16)
        for k in range(1, self.grid.items):
            self.item_copy(k).start()

    def chip_copy(self, k):
        send, recv = self.chip_sems
        grid = self.grid
        to = lax.rem(self.chip + k, self.chips)
        return remote(
            self.item_sum.at[to],
            self.from_chip.at[k],
            send.at[k],
            recv.at[k],
            {"items": grid.item, "rows": to * 2 + self.core},
        )

    def over_chips(self):
        for k in range(1, self.grid.items):
            self.item_copy(k).wait()
        total = self.core_sum[self.grid.item].astype(F32)
        for k in range(1, self.grid.items):
            total = total + self.from_item[k].astype(F32)
        self.item_sum[...] = total.astype(BF16)
        for k in range(1, self.chips):
            self.chip_copy(k).start()

    def final_copy(self, k):
        send, recv = self.final_sems
        mine = self.final.at[self.grid.item]
        return remote(mine, mine, send.at[k], recv.at[k], self.grid.peer(k))

    def spread(self):
        for k in range(1, self.chips):
            self.chip_copy(k).wait()
        total = self.item_sum[self.chip].astype(F32)
        for k in range(1, self.chips):
            total = total + self.from_chip[k].astype(F32)
        self.final[self.grid.item] = total.astype(BF16)
        for k in range(1, self.grid.items):
            self.final_copy(k).start()

    def wait_final(self):
        for k in range(1, self.grid.items):
            self.final_copy(k).wait()


def conv_taps_back(shifted, weight, acc, rows_dev):
    pixels, channels = acc.shape
    acc[...] = jnp.zeros_like(acc)

    def step(tap, carry):
        lhs = shifted[pl.ds(tap, rows_dev)].reshape(pixels, 3 * channels)
        total = None
        for b in range(3):
            at = pl.multiple_of(((2 - tap) * 3 + 2 - b) * channels, channels)
            term = dot(
                lhs[:, b * channels : (b + 1) * channels], weight[pl.ds(at, channels)], 1, 1
            )
            total = term if total is None else total + term
        acc[...] += total
        return carry

    lax.fori_loop(0, 3, step, 0)


def backward_kernel(items, n, *refs):
    (info, embed, gain1, gain2, gain3, stats_in, shifts,
     o_in, dq_in, dkv_in, dt_in, dt_all, first, middle, cot, image, hidden_all, second_all, attn_in, turned_in, text_cols,
     proj_in, w1_in, w2_in, text_in, embed_in,
     output, image_grad, text_grad, text_w_grad, embed_grad, final_out, side_out, vectors,
     weight, proj_w, qkv_turned, first_v, mid_v, cot_v, image_v, attn, cols, rows_v, dq, o, dt, own_dt,
     grad_v, grad_mid, moved_v, pre, acc, shifted, shifted_all, masked, out_v, image_out, text_v, text_w_v, embed_v, same,
     turned, quarter, part, from_core, chip_sum, from_chip, final,
     side_v, side_core, side_sum, side_item, side_total, side_chip, side_final,
     vector, vector_land, own, slots,
     load, sum_send, sum_recv, edge_send, edge_recv, dt_send, dt_recv, vec_send, vec_recv,
     k_item_send, k_item_recv, k_core_send, k_core_recv, k_chip_send, k_chip_recv, k_final_send, k_final_recv,
     s_core_send, s_core_recv, s_item_send, s_item_recv, s_chip_send, s_chip_recv, s_final_send,
     s_final_recv) = refs
    grid = Grid(items, n)
    item, me = grid.item, grid.me
    rows_dev, width, channels = image.shape
    pixels = rows_dev * width
    heads, head_dim, wide = HEADS, channels // HEADS, 3 * channels // HEADS
    share = channels // n
    base = me * rows_dev
    count = (info[0, 0] * info[0, 1]).astype(F32) * (channels // GROUPS)
    scale, shift = shifts[:, :channels], shifts[:, channels:]

    def inside(row):
        return window(info, 0, row, (width, channels))

    fetched = []

    def fetch(src, dst):
        c = pltpu.make_async_copy(src, dst, load.at[len(fetched)])
        c.start()
        fetched.append(c)
        return c

    got_dq = fetch(dq_in, dq.at[:, :head_dim])
    got_dkv = fetch(dkv_in, dq.at[:, head_dim:])
    got_turned = fetch(turned_in, qkv_turned)
    got_mid = fetch(middle, mid_v)
    got_cot = fetch(cot, cot_v)
    got_w2 = fetch(w2_in, weight)
    got_first = fetch(first, first_v)
    got_attn = fetch(attn_in, attn)
    got_o = fetch(o_in, o)
    got_proj = fetch(proj_in, proj_w)
    got_dt = fetch(dt_in, own_dt)
    got_all = fetch(dt_all.at[item], dt.at[item])
    got_second = fetch(second_all, rows_v)
    got_image = fetch(image, image_v)
    got_cols = fetch(text_cols, cols)
    grid.greet()
    edges = [
        Edges(grid, field, edge_send.at[j], edge_recv.at[j])
        for j, field in enumerate((grad_v, moved_v))
    ]
    for e in edges:
        e.clear()
    same[...] = group_matrix(channels)
    sums = [Sums(grid, own.at[j], slots.at[j], sum_send.at[j], sum_recv.at[j]) for j in range(3)]
    kernel_sums = [
        KernelSum(grid, turned.at[j], quarter.at[j], part.at[j], from_core.at[j], chip_sum.at[j], from_chip.at[j],
                  final.at[j], (k_item_send.at[j], k_item_recv.at[j]), (k_core_send.at[j], k_core_recv.at[j]),
                  (k_chip_send.at[j], k_chip_recv.at[j]), (k_final_send.at[j], k_final_recv.at[j]))
        for j in range(2)
    ]
    sum2, sum1 = kernel_sums
    side = SideSum(grid, side_v, side_core, side_sum, side_item, side_total, side_chip, side_final,
                   (s_core_send, s_core_recv), (s_item_send, s_item_recv), (s_chip_send, s_chip_recv),
                   (s_final_send, s_final_recv))

    def dt_copy(k):
        mine = dt.at[item]
        return remote(mine, mine, dt_send.at[k], dt_recv.at[k], grid.peer(k))

    got_turned.wait()
    got_dq.wait()
    got_dkv.wait()

    def unproject_head(h):
        rows = pl.ds(pl.multiple_of(h * wide, wide), wide)
        return dot(dq[h].astype(F32).T.astype(BF16), qkv_turned[rows], 1, 0)

    acc[...] = unproject_head(0)

    def next_head(h):
        acc[...] += unproject_head(h)

    grid.loop(n, next_head)
    got_mid.wait()
    average, inverse = norm_of(stats_in[2], count, same[...])

    def grad_row(r):
        value = acc[pl.ds(r * width, width)] * inside(base + r)
        grad_v[1 + r] = value
        return value, value * ((mid_v[1 + r] - average) * inverse)

    own[0] = row_stats(rows_dev, width, channels, grad_row)
    grid.met()
    sums[0].start()
    edges[0].start()
    got_all.wait()
    grid.loop(items, lambda k: dt_copy(k).start())

    got_attn.wait()

    def qkv_head(h):
        block = dot(dq[h], attn[...], 1, 0).astype(BF16)
        for w in range(3):
            rows = block[w * head_dim : (w + 1) * head_dim]
            side_v[lax.rem(h, 2), h // 2, :, :, w * channels : (w + 1) * channels] = rows.reshape(
                items, share // items, channels
            )

    each_row(heads, qkv_head)
    got_cot.wait()

    def mask_row(r):
        masked[pl.ds(r * width, width)] = (cot_v[1 + r].astype(F32) * inside(base + r)).astype(BF16)

    each_row(rows_dev, mask_row)

    got_o.wait()
    flat_o = o[...].reshape(channels, pixels)
    block = dot(masked[...].astype(F32).T.astype(BF16), flat_o, 1, 1).astype(BF16)
    for r in range(n):
        rows = block[r * share : (r + 1) * share]
        side_v[r % 2, r // 2, :, :, 3 * channels :] = rows.reshape(items, share // items, channels)
    side.core_copy().start()

    stats4 = sums[0].result()
    mean, cross = means_of(stats4, gain3[...], count, same[...])
    edges[0].wait()

    def to_grad2(r):
        normal = (mid_v[r] - average) * inverse
        ok = inside(base + r - 1)
        term = (grad_v[r] * gain3[...] - mean - normal * cross) * inverse * ok
        total = cot_v[r].astype(F32) + term
        grad_mid[r] = total
        shift_into(shifted, r, total * ok)

    each_row(rows_dev + 2, to_grad2)
    sum2.send_grads(shifted)
    side.over_items()
    got_w2.wait()
    conv_taps_back(shifted, weight, acc, rows_dev)
    got_first.wait()
    average2, inverse2 = norm_of(stats_in[1], count, same[...])

    def moved_row(r):
        ok = inside(base + r)
        normal, moved = moved_of(first_v[1 + r], ok, average2, inverse2, gain2[...], scale, shift)
        value = acc[pl.ds(r * width, width)] * ok * silu_slope(moved)
        moved_v[1 + r] = value
        return value, value * normal

    own[1] = row_stats(rows_dev, width, channels, moved_row)
    sums[1].start()
    edges[1].start()
    got_w1 = fetch(w1_in, weight)
    got_second.wait()

    def shift_rows():
        for g in range(items):
            each_row(rows_dev + 2, lambda r: shift_into(shifted_all.at[g], r, rows_v[g, r].astype(F32)))

    shift_rows()
    got_hidden = fetch(hidden_all, rows_v)
    sum2.wait_grads()
    for a in range(3):
        sum2.compute(a, shifted_all)

    stats5 = sums[1].result()
    factor = gain2[...] * (1.0 + scale)
    mean, cross = means_of(stats5, factor, count, same[...])
    edges[1].wait()

    def to_grad1(r):
        normal = (first_v[r] - average2) * inverse2
        value = (moved_v[r] * factor - mean - normal * cross) * inverse2
        shift_into(shifted, r, value * inside(base + r - 1))

    each_row(rows_dev + 2, to_grad1)
    sum1.send_grads(shifted)
    side.over_chips()
    for a in range(3):
        sum2.over_chips(a)
    got_w1.wait()
    conv_taps_back(shifted, weight, acc, rows_dev)
    got_image.wait()
    average1, inverse1 = norm_of(stats_in[0], count, same[...])

    def pre_row(r):
        ok = inside(base + r)
        normal = (image_v[r].astype(F32) - average1) * inverse1 * ok
        value = acc[pl.ds(r * width, width)] * ok * silu_slope(normal * gain1[...])
        pre[r] = value
        return value, value * normal

    own[2] = row_stats(rows_dev, width, channels, pre_row)
    sums[2].start()
    tall = text_in.shape[0]
    got_text_w = [
        fetch(text_in.at[:, j * channels : (j + 1) * channels], weight.at[j * tall : (j + 1) * tall])
        for j in range(2)
    ]
    got_hidden.wait()
    shift_rows()
    sum1.wait_grads()
    sum1.compute(0, shifted_all)
    sum1.compute(1, shifted_all)
    sum1.over_chips(0)
    sum1.compute(2, shifted_all)
    sum1.over_chips(1)
    sum1.over_chips(2)
    for a in range(3):
        sum2.over_items(a)
    side.spread()

    stats6 = sums[2].result()
    e = embed[...].astype(F32)
    low = (e * sigmoid(e)).astype(BF16).astype(F32)
    vector[...] = jnp.zeros_like(vector)
    vector[0:1] = stats6[1:2]
    vector[1:2] = stats5[1:2] * (1.0 + scale)
    vector[2:3] = stats4[1:2]
    vector[3:4] = (stats5[1:2] * gain2[...]).astype(BF16).astype(F32)
    vector[4:5] = stats5[0:1].astype(BF16).astype(F32)
    for j in range(embed.shape[1] // channels):
        vector[5 + j : 6 + j] = low[:, j * channels : (j + 1) * channels]

    def vector_copy(k):
        return remote(
            vector, vector_land.at[item], vec_send.at[k], vec_recv.at[k], grid.peer(k)
        )

    grid.loop(items, lambda k: vector_copy(k).start())
    vector_land[item] = vector[...]

    mean, cross = means_of(stats6, gain1[...], count, same[...])

    def finish_row(r):
        normal = (image_v[r].astype(F32) - average1) * inverse1
        term = (pre[r] * gain1[...] - mean - normal * cross) * inverse1
        image_out[r] = (grad_mid[1 + r] + term) * inside(base + r)

    each_row(rows_dev, finish_row)
    put_image = fetch(image_out, image_grad)

    got_proj.wait()
    acc[...] = dot(flat_o.astype(F32).T.astype(BF16), proj_w[...], 1, 0)

    def output_row(r):
        value = mid_v[1 + r] + acc[pl.ds(r * width, width)] * inside(base + r)
        out_v[r] = value.astype(BF16)

    each_row(rows_dev, output_row)
    put_output = fetch(out_v, output)

    got_dt.wait()
    for c in got_text_w:
        c.wait()
    half = heads // 2
    total = None
    for j in range(2):
        lhs = jnp.concatenate([own_dt[j * half + h] for h in range(half)], axis=1)
        term = dot(lhs, weight[j * tall : (j + 1) * tall], 1, 1)
        total = term if total is None else total + term
    text_v[...] = total
    put_text = fetch(text_v, text_grad)
    got_embed_w = [
        fetch(embed_in.at[:, j * channels : (j + 1) * channels], weight.at[j * tall : (j + 1) * tall])
        for j in range(2)
    ]
    for a in range(3):
        sum1.over_items(a)
    for a in range(3):
        sum2.wait_final(a)
    put_final2 = fetch(final.at[0], final_out.at[0])

    grid.loop(items, lambda k: dt_copy(k).wait())
    got_cols.wait()
    tokens = cols.shape[0] * cols.shape[1]
    flat_cols = cols[...].reshape(tokens, cols.shape[2]).astype(F32).T.astype(BF16)
    for h in range(heads):
        rhs = jnp.concatenate([dt[g, h].reshape(tokens // items, 2 * head_dim) for g in range(items)], axis=0)
        text_w_v[:, h * 2 * head_dim : (h + 1) * 2 * head_dim] = dot(flat_cols, rhs, 1, 0)
    put_text_w = fetch(text_w_v, text_w_grad)

    for c in got_embed_w:
        c.wait()
    total = None
    for j in range(2):
        lhs = vector[3 + j : 4 + j] if j else vector[3:4]
        lhs = jnp.broadcast_to(lhs, (8, channels)).astype(BF16)
        term = dot(lhs, weight[j * tall : (j + 1) * tall], 1, 1)
        total = term if total is None else total + term
    embed_v[...] = total[0:1] * silu_slope(e)
    put_embed = fetch(embed_v, embed_grad)
    grid.loop(items, lambda k: vector_copy(k).wait())
    put_vectors = fetch(vector_land, vectors)
    side.wait_final()
    put_side = fetch(side_final, side_out)
    for a in range(3):
        sum1.wait_final(a)
    put_final1 = fetch(final.at[1], final_out.at[1])
    for c in (put_image, put_output, put_text, put_final2, put_text_w, put_embed, put_vectors, put_side, put_final1):
        c.wait()


def finalize_kernel(final, side, vectors, output_in, image_in, text_in, text_w_in, embed_in,
                    output, image_grad, text_grad, text_w_grad, embed_grad, conv2, conv1, qkv, proj, embed_w,
                    gain1, gain2, gain3,
                    final_v, side_v, vector_v, conv_v, qkv_v, proj_v, embed_w_v, output_v, image_v, text_v, text_w_v,
                    embed_v, load):
    started = []

    def fetch(src, dst):
        c = pltpu.make_async_copy(src, dst, load.at[len(started)])
        c.start()
        started.append(c)
        return c

    got = [fetch(final.at[j], final_v.at[j]) for j in range(2)]
    got_vectors = fetch(vectors, vector_v)
    got_side = fetch(side, side_v)
    through = ((image_in, image_v, image_grad), (text_w_in, text_w_v, text_w_grad), (output_in, output_v, output),
               (text_in, text_v, text_grad), (embed_in, embed_v, embed_grad))
    got_through = [fetch(src, held) for src, held, _ in through]
    me = lax.axis_index("rows")
    items, rows, channels = side_v.shape[0], side_v.shape[1], side_v.shape[2] // 4
    share = items * rows
    for j, out in enumerate((conv2, conv1)):
        got[j].wait()
        for a in range(3):
            for b in range(3):
                for q in range(items):
                    conv_v[j, a * 3 + b, q * rows : (q + 1) * rows] = final_v[j, a, q, b].astype(F32)
        fetch(conv_v.at[j], out)
    for c, (_, held, dst) in zip(got_through, through):
        c.wait()
        fetch(held, dst)
    got_vectors.wait()
    total = vector_v[0]
    for g in range(1, items):
        total = total + vector_v[g]
    own = me * share
    block = channels // 4
    part = total[:, :block]
    for j in range(1, 4):
        part = jnp.where(own // block == j, total[:, j * block : (j + 1) * block], part)
    mine = part[:, :share]
    for j in range(1, block // share):
        mine = jnp.where(lax.rem(own, block) == j * share, part[:, j * share : (j + 1) * share], mine)
    for j, out in enumerate((gain1, gain2, gain3)):
        out[...] = mine[j : j + 1]
    wide = embed_w_v.shape[0]
    start = me * wide
    line = lax.broadcasted_iota(jnp.int32, (16, 1), 0)
    lhs = jnp.zeros((16, wide), F32)
    rhs = jnp.zeros((16, 2 * channels), F32)
    for g in range(items):
        row = vector_v[g, pl.ds(5 + start // channels, 1)]
        piece = row[:, :wide]
        for j in range(1, channels // wide):
            piece = jnp.where(lax.rem(start, channels) == j * wide, row[:, j * wide : (j + 1) * wide], piece)
        lhs = jnp.where(line == g, piece, lhs)
        both = jnp.concatenate([vector_v[g, 3:4], vector_v[g, 4:5]], axis=1)
        rhs = jnp.where(line == g, both, rhs)
    embed_w_v[...] = dot(lhs.astype(BF16), rhs.astype(BF16), 0, 0)
    fetch(embed_w_v, embed_w)
    got_side.wait()
    for q in range(items):
        for w in range(3):
            at = w * share + q * rows
            qkv_v[at : at + rows] = side_v[q, :, w * channels : (w + 1) * channels].astype(F32)
        proj_v[q * rows : (q + 1) * rows] = side_v[q, :, 3 * channels :].astype(F32)
    fetch(qkv_v, qkv)
    fetch(proj_v, proj)
    for j, c in enumerate(started):
        if j > 8:
            c.wait()


def finalize_call(arrays, share):
    final, side, vectors, output, image_grad, text_grad, text_w_grad, embed_grad = arrays
    channels = output.shape[-1]
    n = channels // share
    sds = jax.ShapeDtypeStruct
    kernels = (9, share, channels)
    embed_w = (embed_grad.shape[1] // n, 2 * channels)
    outs = [sds(a.shape, a.dtype) for a in arrays[3:]]
    outs += [sds(kernels, F32)] * 2
    outs += [sds((3 * share, channels), F32), sds((share, channels), F32), sds(embed_w, F32)]
    outs += [sds((1, share), F32)] * 3
    v = pltpu.VMEM
    return pl.pallas_call(
        finalize_kernel,
        out_shape=tuple(outs),
        in_specs=[ANYWHERE] * len(arrays),
        out_specs=(ANYWHERE,) * 10 + (WHOLE,) * 3,
        scratch_shapes=[
            v(final.shape, BF16),
            v(side.shape, BF16),
            v(vectors.shape, F32),
            v((2,) + kernels, F32),
            v((3 * share, channels), F32),
            v((share, channels), F32),
            v(embed_w, F32),
            *[v(a.shape, a.dtype) for a in arrays[3:]],
            DMA((24,)),
        ],
        compiler_params=pltpu.CompilerParams(vmem_limit_bytes=62 << 20),
        name="finalize",
    )(*arrays)


def backward_call(info, embed, gains, stats, shifts, arrays, identity):
    items, n = lax.axis_size("items"), lax.axis_size("rows")
    o_pair, _, _, dtext = arrays[:4]
    image, text_cols, text_w = arrays[8], arrays[13], arrays[17]
    rows_dev, width, channels = image.shape
    pixels = rows_dev * width
    head_dim = channels // HEADS
    share = channels // n
    rows = share // items
    chips = n // 2
    padded = (rows_dev + 2, width, channels)
    tokens = dtext.shape[1]
    sds = jax.ShapeDtypeStruct
    outs = (
        sds(image.shape, BF16),
        sds(image.shape, F32),
        sds((tokens, text_w.shape[0]), F32),
        sds((text_w.shape[0] // n, 2 * channels), F32),
        sds(embed.shape, F32),
        sds((2, 3, items, 3, rows, channels), BF16),
        sds((items, rows, 4 * channels), BF16),
        sds((items, 16, channels), F32),
    )
    v = pltpu.VMEM
    scratch = [
        v((9 * channels, channels), BF16),
        v((channels, channels), BF16),
        v((3 * channels, channels), BF16),
        v(padded, F32),
        v(padded, F32),
        v(padded, BF16),
        v(image.shape, BF16),
        v((pixels, channels), BF16),
        v(text_cols.shape, BF16),
        v((items,) + padded, BF16),
        v((n, 3 * head_dim, pixels), BF16),
        v(o_pair.shape, BF16),
        v((items, n) + dtext.shape, BF16),
        v(dtext.shape, BF16),
        v(padded, F32),
        v(padded, F32),
        v(padded, F32),
        v(image.shape, F32),
        v((pixels, channels), F32),
        v((rows_dev + 2, width, 3 * channels), BF16),
        v((items, rows_dev + 2, width, 3 * channels), BF16),
        v((pixels, channels), BF16),
        v(image.shape, BF16),
        v(image.shape, F32),
        v((tokens, text_w.shape[0]), F32),
        v((text_w.shape[0] // n, 2 * channels), F32),
        v(embed.shape, F32),
        v((channels, channels), BF16),
        v((2, items, channels // items, pixels), BF16),
        v((2, items, channels // items, pixels), BF16),
        v((2, 3, 2, 3, chips * rows, channels), BF16),
        v((2, 3, 3, chips * rows, channels), BF16),
        v((2, 3, chips, 3, rows, channels), BF16),
        v((2, 3, chips, 3, rows, channels), BF16),
        v((2, 3, items, 3, rows, channels), BF16),
        v((2, chips, items, rows, 4 * channels), BF16),
        v((chips, items, rows, 4 * channels), BF16),
        v((items, chips, rows, 4 * channels), BF16),
        v((items, chips, rows, 4 * channels), BF16),
        v((chips, rows, 4 * channels), BF16),
        v((chips, rows, 4 * channels), BF16),
        v((items, rows, 4 * channels), BF16),
        v((16, channels), F32),
        v((items, 16, channels), F32),
        v((3, 8, channels), F32),
        v((3, n, 8, channels), F32),
        DMA((32,)),
        DMA((3, n)),
        DMA((3, n)),
        DMA((2, 2)),
        DMA((2, 2)),
        DMA((items,)),
        DMA((items,)),
        DMA((items,)),
        DMA((items,)),
        DMA((2, items)),
        DMA((2, items)),
        DMA((2, 3)),
        DMA((2, 3)),
        DMA((2, 3, chips)),
        DMA((2, 3, chips)),
        DMA((2, 3, items)),
        DMA((2, 3, items)),
        DMA((1,)),
        DMA((1,)),
        DMA((items,)),
        DMA((items,)),
        DMA((chips,)),
        DMA((chips,)),
        DMA((items,)),
        DMA((items,)),
    ]
    return pl.pallas_call(
        functools.partial(backward_kernel, items, n),
        out_shape=outs,
        in_specs=[SCALARS] + [WHOLE] * 6 + [ANYWHERE] * len(arrays),
        out_specs=(ANYWHERE,) * 8,
        scratch_shapes=scratch,
        compiler_params=pltpu.CompilerParams(
            collective_id=identity, has_side_effects=True, vmem_limit_bytes=62 << 20
        ),
        cost_estimate=pl.CostEstimate(
            flops=80 * pixels * channels * channels, bytes_accessed=60 << 20, transcendentals=0
        ),
        name="backward",
    )(info, embed, *gains, stats, shifts, *arrays)


def own_shards(
    extent, image, embed, text, gain1, conv1_w, embed_w, gain2, conv2_w, gain3, qkv_w, text_w, proj_w,
    cotangent,
):
    _, rows_dev, width, channels = image.shape
    items, parts = lax.axis_size("items"), lax.axis_size("rows")
    me = lax.axis_index("rows")
    head_dim = channels // HEADS
    tokens = text.shape[1]
    share = channels // parts
    (first, middle, cot, hidden_all, second_all, attn_flat, qkv_turned, attended, dq, dkv, own_dt, all_dt,
     text_cols, stats, shifts) = forward_call(
        extent,
        image[0],
        cotangent[0],
        text[0],
        embed,
        (gain1, gain2, gain3),
        (
            conv1_w.reshape(3, 3 * channels, channels),
            conv2_w.reshape(3, 3 * channels, channels),
            embed_w,
            text_w,
            qkv_w,
            proj_w,
        ),
        0,
    )
    text_w_rows = text_cols.shape[3]
    output, image_grad, text_grad, text_w_grad, embed_grad, final, side, vectors = backward_call(
        extent,
        embed,
        (gain1, gain2, gain3),
        stats,
        shifts,
        (
            attended,
            dq,
            dkv,
            own_dt,
            all_dt,
            first,
            middle,
            cot,
            image[0],
            hidden_all,
            second_all,
            attn_flat,
            qkv_turned,
            text_cols.reshape(items * parts, tokens, text_w_rows),
            proj_w,
            conv1_w.reshape(9 * channels, channels),
            conv2_w.reshape(9 * channels, channels),
            text_w,
            embed_w,
        ),
        1,
    )
    (output, image_grad, text_grad, text_w_grad, embed_grad, conv2, conv1, qkv, proj, embed_w_grad, norm1, norm2,
     norm3) = finalize_call(
        (final, side, vectors, output, image_grad, text_grad, text_w_grad, embed_grad), share
    )

    def kernel(values):
        return jnp.swapaxes(values.reshape(3, 3, share, channels), 2, 3)

    return (
        output[None],
        image_grad[None],
        embed_grad,
        text_grad[None],
        norm1[0],
        kernel(conv1),
        embed_w_grad,
        norm2[0],
        kernel(conv2),
        norm3[0],
        qkv.T,
        text_w_grad,
        proj.T,
    )


def shards(
    image, embed, text, extent, first_norm_gain1, conv1_w, embed_w, second_norm_gain2, conv2_w,
    attention_norm_gain, qkv_w, text_w, proj_w, cotangent,
):
    images, rows_dev, width, channels = image.shape
    parts = lax.axis_size("rows")
    me = lax.axis_index("rows")
    pairs = images * HEADS // parts
    head_dim = channels // HEADS
    pixels = rows_dev * width
    group = max(1, 512 // pixels)
    span = group * pixels
    chunks = parts // group
    tokens = text.shape[1]
    first_row = jnp.full((images, 1), me * rows_dev, jnp.int32)
    info = jnp.concatenate([extent, first_row], axis=1)
    gain1 = first_norm_gain1.reshape(1, channels)
    gain2 = second_norm_gain2.reshape(1, channels)
    gain3 = attention_norm_gain.reshape(1, channels)
    rowpos = me * rows_dev + jnp.arange(rows_dev, dtype=jnp.int32)
    colpos = jnp.arange(width, dtype=jnp.int32)
    inside = (rowpos[None, :, None] < extent[:, 0, None, None]) & (
        colpos[None, None, :] < extent[:, 1, None, None]
    )
    image_window = inside.astype(F32)[..., None]

    items = lax.axis_size("items")
    own_path = (
        images == 1
        and parts == HEADS
        and channels % (16 * items * parts) == 0
        and pixels % 512 == 0
        and tokens % 16 == 0
        and text.shape[2] % (128 * parts) == 0
        and text.shape[2] == embed.shape[1] <= 4 * channels
    )
    if own_path:
        return own_shards(
            extent, image, embed, text, gain1, conv1_w, embed_w, gain2, conv2_w, gain3, qkv_w, text_w,
            proj_w, cotangent,
        )

    embed_float = embed.astype(F32)
    embed_low = jax.nn.silu(embed_float).astype(BF16)
    shifts = jnp.dot(embed_low, embed_w, preferred_element_type=F32)
    qkv_turned = qkv_w.T
    proj_shaped = proj_w.reshape(HEADS, head_dim, channels)

    start = image.astype(F32) * image_window
    zeros = jnp.zeros((images, 6, channels), F32)
    stats0 = jnp.concatenate(
        [
            jnp.sum(start, axis=(1, 2))[:, None],
            jnp.sum(start * start, axis=(1, 2))[:, None],
            zeros,
        ],
        axis=1,
    )
    stats1, image_above, image_below, cot_above, cot_below = exchange(
        stats0, (image, cotangent), 0
    )
    full = jax.ShapeDtypeStruct(image.shape, F32)
    sums = jax.ShapeDtypeStruct((images, 8, channels), F32)
    padded = jax.ShapeDtypeStruct((images, rows_dev + 2, width, channels), BF16)
    first, stats, hidden = conv_call(
        conv1_kernel,
        info,
        (image, image_above, image_below, stats1, gain1),
        conv1_w,
        (full, sums, padded),
        False,
    )
    stats2, first_above, first_below, all_text = exchange(stats, (first,), 1, (text,))
    gathered_text = jnp.moveaxis(all_text, 0, 1).reshape(images, parts * tokens, text.shape[2])
    text_share = text.shape[2] // parts
    text_cols = lax.dynamic_slice_in_dim(gathered_text, me * text_share, text_share, 2)
    text_cols = lax.all_gather(text_cols, "items", axis=0, tiled=True)
    middle, stats, second = conv_call(
        conv2_kernel,
        info,
        (first, first_above, first_below, stats2, gain2, shifts, image),
        conv2_w,
        (full, sums, padded),
        False,
    )
    stats3, mid_above, mid_below = exchange(stats, (middle,), 2)
    attn_flat, qkv_pix = project(info, middle, stats3, gain3, qkv_turned)

    def to_pairs(values):
        wide = values.shape[1]
        moved = lax.all_to_all(values, "rows", split_axis=0, concat_axis=0, tiled=True)
        moved = moved.reshape(chunks, group, pairs, wide, pixels)
        return jnp.transpose(moved, (2, 0, 3, 1, 4)).reshape(pairs, chunks, wide, span)

    def from_pairs(values):
        wide = values.shape[2]
        moved = values.reshape(pairs, chunks, wide, group, pixels)
        moved = jnp.transpose(moved, (1, 3, 0, 2, 4)).reshape(parts * pairs, wide, pixels)
        return lax.all_to_all(moved, "rows", split_axis=0, concat_axis=0, tiled=True)

    qkv_pair = to_pairs(qkv_pix)
    grad_proj = (cotangent.astype(F32) * image_window).astype(BF16).reshape(images, pixels, channels)
    grad_heads = jnp.einsum(
        "ipc,hdc->ihdp", grad_proj, proj_shaped, preferred_element_type=F32
    ).astype(BF16)
    grad_pair = to_pairs(grad_heads.reshape(images * HEADS, head_dim, pixels))
    pair_results = []
    for p in range(pairs):
        pair = me * pairs + p
        item, head = pair // HEADS, pair % HEADS
        weight = lax.dynamic_slice_in_dim(text_w, head * 2 * head_dim, 2 * head_dim, 1)
        own = lax.dynamic_index_in_dim(gathered_text, item, 0, False)
        text_pair = jnp.dot(own, weight, preferred_element_type=F32).astype(BF16)
        pair_extent = lax.dynamic_slice_in_dim(extent, item, 1, 0)
        pair_results.append(attention(pair_extent, qkv_pair[p], text_pair, grad_pair[p], width))
    attended, qkv_grad_pair, text_grad_pair = (jnp.stack(r) for r in zip(*pair_results))
    qkv_back = from_pairs(qkv_grad_pair)
    heads_out = from_pairs(attended).reshape(images, HEADS, head_dim, pixels)

    attn_grad, stats = unproject(info, middle, stats3, qkv_back, qkv_turned)
    stats4, grad_above, grad_below, text_back = exchange(stats, (attn_grad,), 3, (text_grad_pair,))
    text_back = text_back.reshape(images, HEADS, parts * tokens, 2 * head_dim)
    text_all = lax.all_gather(text_back, "items", axis=0, tiled=True)
    proj_grad = jnp.einsum("ipc,ihdp->chd", grad_proj, heads_out, preferred_element_type=F32)
    qkv_grad = jnp.einsum(
        "ihwdp,ipc->hdwc",
        qkv_back.reshape(images, HEADS, 3, head_dim, pixels),
        attn_flat,
        preferred_element_type=F32,
    )
    grad_middle, moved_grad, stats, conv2_grad = conv_call(
        back2_kernel,
        info,
        (attn_grad, grad_above, grad_below, middle, mid_above, mid_below, cotangent, cot_above,
         cot_below, stats3, stats4, gain3, first, stats2, gain2, shifts),
        conv2_w,
        (full, full, sums, padded),
        True,
    )
    stats5, moved_above, moved_below = exchange(stats, (moved_grad,), 4)
    pre_grad, stats, conv1_grad = conv_call(
        back1_kernel,
        info,
        (moved_grad, moved_above, moved_below, first, first_above, first_below, stats2, stats5,
         gain2, shifts, image, stats1, gain1),
        conv1_w,
        (full, sums, padded),
        True,
    )
    (stats6,) = exchange(stats, (), 5)
    image_grad = finish(info, pre_grad, stats6, image, stats1, gain1, grad_middle)

    projected = jnp.einsum(
        "ihdp,hdc->ipc", heads_out, proj_shaped, preferred_element_type=F32
    ).reshape(image.shape)
    output = (middle + projected * image_window).astype(BF16)
    own_text = lax.dynamic_slice_in_dim(text_back, me * tokens, tokens, 2)
    text_shaped = text_w.reshape(text_w.shape[0], HEADS, 2 * head_dim)
    text_grad = jnp.einsum("ihtk,chk->itc", own_text, text_shaped, preferred_element_type=F32)
    text_w_grad = jnp.einsum(
        "gtc,ghtk->chk", text_cols, text_all, preferred_element_type=F32
    ).reshape(text_share, 2 * channels)
    scale_sum = stats5[:, 1] * gain2
    grad_shifts = jnp.concatenate([scale_sum, stats5[:, 0]], axis=1).astype(BF16)
    embed_grad = jnp.einsum(
        "ik,ck->ic", grad_shifts, embed_w, preferred_element_type=F32
    ) * silu_slope(embed_float)
    embed_share = embed_w.shape[0] // parts
    gains = jnp.stack(
        [
            jnp.sum(stats6[:, 1], axis=0),
            jnp.sum(stats5[:, 1] * (1.0 + shifts[:, :channels]), axis=0),
            jnp.sum(stats4[:, 1], axis=0),
        ]
    )
    share = channels // parts
    def total(values):
        return lax.psum(
            lax.psum_scatter(values.astype(BF16), "rows", scatter_dimension=0, tiled=True),
            "items",
        ).astype(F32)

    def kernel_total(values):
        return total(values).T.reshape(3, 3, channels, share)

    conv1_total = kernel_total(weight_grad(conv1_grad, hidden))
    conv2_total = kernel_total(weight_grad(conv2_grad, second))
    by_head = jnp.swapaxes(qkv_grad, 1, 2).reshape(3 * channels, channels)
    qkv_total = total(by_head).T
    proj_total = total(proj_grad.reshape(channels, channels)).T
    gains = lax.psum(gains, "items")
    all_shifts = lax.all_gather(grad_shifts, "items", axis=0, tiled=True)
    embed_rows = lax.dynamic_slice_in_dim(embed_low, me * embed_share, embed_share, 1)
    embed_rows = lax.all_gather(embed_rows, "items", axis=0, tiled=True)
    embed_w_grad = jnp.einsum("ic,ik->ck", embed_rows, all_shifts, preferred_element_type=F32)
    gains = lax.dynamic_slice_in_dim(gains, me * share, share, 1)
    return (
        output,
        image_grad,
        embed_grad,
        text_grad,
        gains[0],
        conv1_total,
        embed_w_grad,
        gains[1],
        conv2_total,
        gains[2],
        qkv_total,
        text_w_grad,
        proj_total,
    )


def solution(mesh):
    in_specs = (
        P("items", "rows", None, None),
        P("items", None),
        P("items", "rows", None),
        P("items", None),
        P(),
        P(),
        P(),
        P(),
        P(),
        P(),
        P(),
        P(),
        P(),
        P("items", "rows", None, None),
    )
    out_specs = (
        P("items", "rows", None, None),
        P("items", "rows", None, None),
        P("items", None),
        P("items", "rows", None),
        P("rows"),
        P(None, None, None, "rows"),
        P("rows", None),
        P("rows"),
        P(None, None, None, "rows"),
        P("rows"),
        P(None, "rows"),
        P("rows", None),
        P(None, "rows"),
    )
    return jax.shard_map(shards, mesh=mesh, in_specs=in_specs, out_specs=out_specs, check_vma=False)
```

```python
import functools

import jax
import jax.numpy as jnp
from jax import lax
from jax.experimental import pallas as pl
from jax.experimental.pallas import tpu as pltpu
from jax.sharding import PartitionSpec as P

GROUPS = 32
HEADS = 8
F32, BF16 = jnp.float32, jnp.bfloat16
NEG = -1e30


def dot(a, b, ca, cb):
    return lax.dot_general(a, b, (((ca,), (cb,)), ((), ())), preferred_element_type=F32)

def nothing(*_):
    return None


class Attention:
    def __init__(self, chunks, span, d, tlen, step, bq, scratch):
        self.chunks, self.span, self.d, self.tlen, self.step, self.bq = chunks, span, d, tlen, step, bq
        self.kn, self.vn, self.kt, self.vt, s0, s1, e0, e1, self.dkt, self.dvt = scratch
        self.scores, self.raised = (s0, s1), (e0, e1)
        self.pix = chunks * span

    def stage_key(self, c, k, width, rows_ok, cols_ok):
        d, span = self.d, self.span
        base = pl.multiple_of(c * span, span)
        pos = base + lax.broadcasted_iota(jnp.int32, (16, span), 1)
        row = lax.broadcasted_iota(jnp.int32, (16, span), 0)
        ok = (pos // width < rows_ok) & (pos % width < cols_ok)
        extra = jnp.where((row == 0) & jnp.logical_not(ok), NEG, 0.0)
        rest = jnp.zeros((128 - d - 16, span), F32)
        self.kt[:, pl.ds(base, span)] = k
        ka = jnp.concatenate([k.astype(F32), extra, rest], axis=0)
        self.kn[pl.ds(base, span), :] = ka.T.astype(BF16)

    def stage_value(self, c, v):
        d, span = self.d, self.span
        base = pl.multiple_of(c * span, span)
        row = lax.broadcasted_iota(jnp.int32, (16, span), 0)
        rest = jnp.zeros((128 - d - 16, span), F32)
        self.vt[:, pl.ds(base, span)] = v
        va = jnp.concatenate([v.astype(F32), jnp.where(row < 3, 1.0, 0.0), rest], axis=0)
        self.vn[pl.ds(base, span), :] = va.T.astype(BF16)

    def stage_text(self, text):
        d, tlen, pix = self.d, self.tlen, self.pix
        tk = text[:, :d].astype(F32)
        tv = text[:, d:].astype(F32)
        self.kt[:, pix:] = tk.T.astype(BF16)
        self.vt[:, pix:] = tv.T.astype(BF16)
        lanes = lax.broadcasted_iota(jnp.int32, (tlen, 128 - d), 1)
        rest = jnp.zeros((tlen, 128 - d), F32)
        self.kn[pix:, :] = jnp.concatenate([tk, rest], axis=1).astype(BF16)
        ones = jnp.where(lanes < 3, 1.0, 0.0)
        self.vn[pix:, :] = jnp.concatenate([tv, ones], axis=1).astype(BF16)

    def query(self, q):
        d, bq = self.d, self.bq
        r = lax.broadcasted_iota(jnp.int32, (128 - d, bq), 0)
        rest = jnp.where(r == 0, 1.0, 0.0)
        return jnp.concatenate([q.astype(F32) * (d**-0.5), rest], axis=0).astype(BF16)

    def run(self, score, exp, back):
        d, bq, step = self.d, self.bq, self.step
        kn, vn, kt, vt, dkt, dvt = self.kn, self.vn, self.kt, self.vt, self.dkt, self.dvt
        scores, raised = self.scores, self.raised

        def body(j, carry):
            pk, total, acc, dq = carry
            at = pl.ds(pl.multiple_of(j * step, step), step)
            if score:
                slot, qa = score
                s = dot(kn[at, :], qa, 1, 0)
                scores[slot][at, :] = s
                pk = jnp.maximum(pk, jnp.max(s.reshape(step // 8, 8, bq), axis=0))
            if exp:
                slot, peak = exp
                e = jnp.exp(scores[slot][at, :] - peak)
                total = total + jnp.sum(e.reshape(step // 8, 8, bq), axis=0)
                low = e.astype(BF16)
                raised[slot][at, :] = low
                acc = acc + dot(vt[:, at], low, 1, 0)
            if back:
                slot, goa, q = back
                dp = dot(vn[at, :], goa, 1, 0)
                e = raised[slot][at, :]
                ds = (e.astype(F32) * dp).astype(BF16)
                dvt[:, at] += dot(goa[:d], e, 1, 1)
                dkt[:, at] += dot(q, ds, 1, 1)
                dq = dq + dot(kt[:, at], ds, 1, 0)
            return pk, total, acc, dq

        init = (
            jnp.full((8, bq), -3e38, F32),
            jnp.zeros((8, bq), F32),
            jnp.zeros((d, bq), F32),
            jnp.zeros((d, bq), F32),
        )
        return lax.fori_loop(0, (self.pix + self.tlen) // step, body, init)

    def attended(self, go, total, acc):
        d, bq = self.d, self.bq
        inv = 1.0 / jnp.sum(total, axis=0, keepdims=True)
        o = acc * inv
        go = go.astype(F32)
        nd = -jnp.sum(go * o, axis=0, keepdims=True) * inv
        hi = nd.astype(BF16).astype(F32)
        mid = (nd - hi).astype(BF16).astype(F32)
        lo = nd - hi - mid
        r = lax.broadcasted_iota(jnp.int32, (16, bq), 0)
        extra = jnp.where(r == 0, hi, jnp.where(r == 1, mid, jnp.where(r == 2, lo, 0.0)))
        rest = jnp.zeros((128 - d - 16, bq), F32)
        return o.astype(BF16), jnp.concatenate([go * inv, extra, rest], axis=0).astype(BF16)

    def attend(self, q_ref, go_ref, o_ref, dq_ref, order, before=nothing, done=nothing):
        d, bq, chunks = self.d, self.bq, self.chunks
        self.dkt[...] = jnp.zeros_like(self.dkt)
        self.dvt[...] = jnp.zeros_like(self.dvt)

        def columns(half):
            return slice(half * bq, (half + 1) * bq)

        def q_of(h, half):
            return q_ref[order(h), :d, columns(half)]

        def finish_exp(h, half, total, acc):
            c = order(h)
            o, goa = self.attended(go_ref[c, :, columns(half)], total, acc)
            o_ref[c, :, columns(half)] = o
            return goa

        def put_dq(h, half, dq):
            dq_ref[order(h), :d, columns(half)] = (dq * (d**-0.5)).astype(BF16)

        def top(pk):
            return jnp.max(pk, axis=0, keepdims=True)

        run = self.run
        pk, _, _, _ = run((0, self.query(q_of(0, 0))), None, None)
        pk, total, acc, _ = run((1, self.query(q_of(0, 1))), (0, top(pk)), None)
        goa = finish_exp(0, 0, total, acc)

        def two(h, carry):
            pk, goa = carry
            before(h + 1)
            qa = self.query(q_of(h + 1, 0))
            pk2, total, acc, dq = run((0, qa), (1, top(pk)), (0, goa, q_of(h, 0)))
            put_dq(h, 0, dq)
            goa = finish_exp(h, 1, total, acc)
            qa = self.query(q_of(h + 1, 1))
            pk3, total, acc, dq = run((1, qa), (0, top(pk2)), (1, goa, q_of(h, 1)))
            put_dq(h, 1, dq)
            done(h)
            return pk3, finish_exp(h + 1, 0, total, acc)

        pk, goa = lax.fori_loop(0, chunks - 1, two, (pk, goa))
        last = chunks - 1
        _, total, acc, dq = run(None, (1, top(pk)), (0, goa, q_of(last, 0)))
        put_dq(last, 0, dq)
        goa = finish_exp(last, 1, total, acc)
        _, _, _, dq = run(None, None, (1, goa, q_of(last, 1)))
        put_dq(last, 1, dq)
        done(last)

    def key_grad(self, at):
        return (self.dkt[:, at] * (self.d**-0.5)).astype(BF16)

    def value_grad(self, at):
        return self.dvt[:, at].astype(BF16)

    def text_grad(self, out):
        d, pix = self.d, self.pix
        out[:, :d] = (self.dkt[:, pix:] * (d**-0.5)).T.astype(BF16)
        out[:, d:] = self.dvt[:, pix:].T.astype(BF16)


def attention_scratch(chunks, span, d, tlen):
    keys = chunks * span + tlen
    bq = span // 2
    lanes = keys // 128
    step = 128 * max(n for n in range(1, 12) if lanes % n == 0)
    shapes = [((keys, 128), BF16)] * 2 + [((d, keys), BF16)] * 2
    shapes += [((keys, bq), F32)] * 2 + [((keys, bq), BF16)] * 2 + [((d, keys), F32)] * 2
    return step, bq, [pltpu.VMEM(*shape) for shape in shapes]


def attention_kernel(width, step, bq, ext_ref, qkv_ref, text_ref, go_ref, out_ref, dqkv_ref, dtext_ref, *scratch):
    chunks, _, span = qkv_ref.shape
    d = go_ref.shape[1]
    att = Attention(chunks, span, d, text_ref.shape[0], step, bq, scratch)

    def stage(c, carry):
        att.stage_key(c, qkv_ref[c, d : 2 * d, :], width, ext_ref[0, 0], ext_ref[0, 1])
        att.stage_value(c, qkv_ref[c, 2 * d :, :])
        return carry

    lax.fori_loop(0, chunks, stage, 0)
    att.stage_text(text_ref)
    att.attend(qkv_ref, go_ref, out_ref, dqkv_ref, lambda h: h)

    def finish(c, carry):
        at = pl.ds(pl.multiple_of(c * span, span), span)
        dqkv_ref[c, d : 2 * d, :] = att.key_grad(at)
        dqkv_ref[c, 2 * d :, :] = att.value_grad(at)
        return carry

    lax.fori_loop(0, chunks, finish, 0)
    att.text_grad(dtext_ref)


def attention(ext, qkv, text, go, width):
    chunks, wide, span = qkv.shape
    d = wide // 3
    tlen = text.shape[0]
    keys = chunks * span + tlen
    step, bq, scratch = attention_scratch(chunks, span, d, tlen)
    vm = pl.BlockSpec(memory_space=pltpu.VMEM)
    flops = 2 * 6 * chunks * span * keys * d
    return pl.pallas_call(
        functools.partial(attention_kernel, width, step, bq),
        out_shape=(
            jax.ShapeDtypeStruct(go.shape, BF16),
            jax.ShapeDtypeStruct(qkv.shape, BF16),
            jax.ShapeDtypeStruct((tlen, 2 * d), BF16),
        ),
        in_specs=[pl.BlockSpec(memory_space=pltpu.SMEM), vm, vm, vm],
        out_specs=(vm, vm, vm),
        scratch_shapes=scratch,
        compiler_params=pltpu.CompilerParams(vmem_limit_bytes=56 << 20),
        cost_estimate=pl.CostEstimate(
            flops=4 * flops, bytes_accessed=16 * chunks * span * d, transcendentals=chunks * span * keys
        ),
    )(ext, qkv, text, go)


MESH = pl.DeviceIdType.MESH
EPS = 1e-05
WHOLE = pl.BlockSpec(memory_space=pltpu.VMEM)
SCALARS = pl.BlockSpec(memory_space=pltpu.SMEM)
ANYWHERE = pl.BlockSpec(memory_space=pl.ANY)


def exchange_kernel(n, count, gathers, *refs):
    inputs, refs = refs[: 1 + count + gathers], refs[1 + count + gathers :]
    outputs, refs = refs[: 1 + 2 * count + gathers], refs[1 + 2 * count + gathers :]
    stats_ref, rows, given = inputs[0], inputs[1 : 1 + count], inputs[1 + count :]
    total_ref, outs, gathered = outputs[0], outputs[1 : 1 + 2 * count], outputs[1 + 2 * count :]
    slots, lands = refs[0], refs[1 : 1 + 2 * count]
    send, recv, row_send, row_recv, own = refs[1 + 2 * count :]
    me = lax.axis_index("rows")
    barrier = pltpu.get_barrier_semaphore()

    def greet(k, carry):
        pl.semaphore_signal(
            barrier, inc=1, device_id={"rows": lax.rem(me + k, n)}, device_id_type=MESH
        )
        return carry

    lax.fori_loop(1, n, greet, 0)
    slots[me] = stats_ref[...]
    pl.semaphore_wait(barrier, n - 1)
    shared = [(stats_ref, slots)] + list(zip(given, gathered))

    def share(j, k):
        return pltpu.make_async_remote_copy(
            src_ref=shared[j][0],
            dst_ref=shared[j][1].at[me],
            send_sem=send.at[j, k],
            recv_sem=recv.at[j, k],
            device_id={"rows": lax.rem(me + k, n)},
            device_id_type=MESH,
        )

    def start(k, carry):
        share(0, k).start()
        return carry

    lax.fori_loop(1, n, start, 0)

    def row_copy(j, side):
        last = rows[j].shape[1] - 1
        at = last if side == 0 else 0
        return pltpu.make_async_remote_copy(
            src_ref=rows[j].at[:, at : at + 1],
            dst_ref=lands[2 * j + side],
            send_sem=row_send.at[2 * j + side],
            recv_sem=row_recv.at[2 * j + side],
            device_id={"rows": me + 1 if side == 0 else me - 1},
            device_id_type=MESH,
        )

    for j in range(count):

        @pl.when(me < n - 1)
        def _():
            row_copy(j, 0).start()

        @pl.when(me > 0)
        def _():
            row_copy(j, 1).start()

    for j in range(gathers):

        def start_given(k, carry):
            share(1 + j, k).start()
            return carry

        lax.fori_loop(1, n, start_given, 0)
        pltpu.make_async_copy(given[j], gathered[j].at[me], own.at[j]).start()

    def finish(k, carry):
        share(0, k).wait()
        return carry

    lax.fori_loop(1, n, finish, 0)
    total_ref[...] = lax.fori_loop(1, n, lambda k, s: s + slots[k], slots[0])
    for j in range(count):

        @pl.when(me > 0)
        def _():
            row_copy(j, 0).wait_recv()
            outs[2 * j][...] = lands[2 * j][...]

        @pl.when(me == 0)
        def _():
            outs[2 * j][...] = jnp.zeros_like(outs[2 * j])

        @pl.when(me < n - 1)
        def _():
            row_copy(j, 1).wait_recv()
            outs[2 * j + 1][...] = lands[2 * j + 1][...]
            row_copy(j, 0).wait_send()

        @pl.when(me == n - 1)
        def _():
            outs[2 * j + 1][...] = jnp.zeros_like(outs[2 * j + 1])

        @pl.when(me > 0)
        def _():
            row_copy(j, 1).wait_send()

    for j in range(gathers):

        def finish_given(k, carry):
            share(1 + j, k).wait()
            return carry

        lax.fori_loop(1, n, finish_given, 0)
        pltpu.make_async_copy(given[j], gathered[j].at[me], own.at[j]).wait()


def exchange(stats, rows, identity, given=()):
    n = lax.axis_size("rows")
    edge = []
    for array in rows:
        edge += [jax.ShapeDtypeStruct(array.shape[:1] + (1,) + array.shape[2:], array.dtype)] * 2
    whole = [jax.ShapeDtypeStruct((n,) + array.shape, array.dtype) for array in given]
    count, gathers = len(rows), len(given)
    nbytes = 4 * stats.size * n + sum(2 * e.size * e.dtype.itemsize for e in (*edge, *whole))
    return pl.pallas_call(
        functools.partial(exchange_kernel, n, count, gathers),
        out_shape=(jax.ShapeDtypeStruct(stats.shape, F32), *edge, *whole),
        in_specs=[WHOLE] + [ANYWHERE] * (count + gathers),
        out_specs=(WHOLE,) * (1 + 2 * count) + (ANYWHERE,) * gathers,
        scratch_shapes=[
            pltpu.VMEM((n,) + stats.shape, F32),
            *[pltpu.VMEM(e.shape, e.dtype) for e in edge],
            pltpu.SemaphoreType.DMA((1 + gathers, n)),
            pltpu.SemaphoreType.DMA((1 + gathers, n)),
            pltpu.SemaphoreType.DMA((max(1, 2 * count),)),
            pltpu.SemaphoreType.DMA((max(1, 2 * count),)),
            pltpu.SemaphoreType.DMA((max(1, gathers),)),
        ],
        compiler_params=pltpu.CompilerParams(collective_id=identity, has_side_effects=True),
        cost_estimate=pl.CostEstimate(
            flops=6_000_000_000, bytes_accessed=nbytes, transcendentals=0
        ),
        name=f"exchange{identity}",
    )(stats, *rows, *given)


def group_matrix(channels):
    size = channels // GROUPS
    one = lax.broadcasted_iota(jnp.int32, (channels, channels), 0) // size
    two = lax.broadcasted_iota(jnp.int32, (channels, channels), 1) // size
    return jnp.where(one == two, 1.0, 0.0).astype(BF16)


def group_sums(rows, same=None):
    if same is None:
        same = group_matrix(rows.shape[1])
    high = rows.astype(BF16).astype(F32)
    mid = (rows - high).astype(BF16).astype(F32)
    tail = rows - high - mid
    sums = dot(jnp.concatenate([high, mid, tail], axis=0).astype(BF16), same, 1, 0)
    n = rows.shape[0]
    return sums[:n] + sums[n : 2 * n] + sums[2 * n :]


def image_count(info, i, channels):
    return (info[i, 0] * info[i, 1]).astype(F32) * (channels // GROUPS)


def norm_of(stats, count, same=None):
    sums = group_sums(stats, same)
    average = sums[0:1] / count
    square = sums[1:2] / count
    return average, lax.rsqrt(square - average * average + EPS)


def means_of(stats, weight, count, same=None):
    sums = group_sums(stats * weight, same)
    return sums[0:1] / count, sums[1:2] / count


def window(info, i, row, shape):
    ok = (row >= 0) & (row < info[i, 0])
    limit = jnp.where(ok, info[i, 1], 0)
    return jnp.where(lax.broadcasted_iota(jnp.int32, shape, 0) < limit, 1.0, 0.0)


def padded_row(center, above, below, i, r):
    if r == 0:
        return above[i, 0]
    if r == center.shape[1] + 1:
        return below[i, 0]
    return center[i, r - 1]


def put_shifted(out, i, r, value, plain=None):
    width, channels = value.shape
    column = lax.broadcasted_iota(jnp.int32, value.shape, 0)
    left = jnp.where(column == 0, 0.0, pltpu.roll(value, 1, 0))
    right = jnp.where(column == width - 1, 0.0, pltpu.roll(value, width - 1, 0))
    out[i, r, :, :channels] = left.astype(BF16)
    low = value.astype(BF16)
    out[i, r, :, channels : 2 * channels] = low
    if plain is not None:
        plain[i, r] = low
    out[i, r, :, 2 * channels :] = right.astype(BF16)


def sigmoid(v):
    return 1.0 / (1.0 + jnp.exp(-v))


def silu_slope(v):
    s = sigmoid(v)
    return s * (1.0 + v * (1.0 - s))


def put_stats(stats_ref, i, first, second):
    channels = first.shape[1]
    one = jnp.sum(first, axis=0, keepdims=True)
    two = jnp.sum(second, axis=0, keepdims=True)
    row = lax.broadcasted_iota(jnp.int32, (8, channels), 0)
    stats_ref[i] = jnp.where(row == 0, one, jnp.where(row == 1, two, 0.0))


def tap_rows(shifted, tap, images, rows_dev, width):
    block = shifted[:, pl.ds(tap, rows_dev)]
    return block.reshape(images * rows_dev * width, shifted.shape[3])


def conv1_kernel(info, image, above, below, stats, gain, weight, first, out_stats, hidden, acc, shifted):
    images, rows_dev, width, channels = image.shape
    tap = pl.program_id(0)
    base = info[0, 2]

    @pl.when(tap == 0)
    def _():
        for i in range(images):
            average, inverse = norm_of(stats[i], image_count(info, i, channels))
            for r in range(rows_dev + 2):
                inside = window(info, i, base + r - 1, (width, channels))
                start = padded_row(image, above, below, i, r).astype(F32) * inside
                value = (start - average) * inverse * inside * gain[...]
                put_shifted(shifted, i, r, value * sigmoid(value) * inside, hidden)

    part = dot(tap_rows(shifted, tap, images, rows_dev, width), weight[0], 1, 0)

    @pl.when(tap == 0)
    def _():
        acc[...] = part

    @pl.when(tap > 0)
    def _():
        acc[...] += part

    @pl.when(tap == 2)
    def _():
        for i in range(images):
            one = two = jnp.zeros((width, channels), F32)
            for r in range(rows_dev):
                inside = window(info, i, base + r, (width, channels))
                at = (i * rows_dev + r) * width
                value = acc[at : at + width] * inside
                first[i, r] = value
                one = one + value
                two = two + value * value
            put_stats(out_stats, i, one, two)


def moved_of(value, inside, average, inverse, gain, scale, shift):
    normal = (value - average) * inverse * inside
    return normal, normal * gain * (1.0 + scale) + shift


def conv2_kernel(
    info, first, above, below, stats, gain, shifts, image, weight, middle, out_stats, second, acc,
    shifted,
):
    images, rows_dev, width, channels = first.shape
    tap = pl.program_id(0)
    base = info[0, 2]

    @pl.when(tap == 0)
    def _():
        for i in range(images):
            average, inverse = norm_of(stats[i], image_count(info, i, channels))
            scale, shift = shifts[i : i + 1, :channels], shifts[i : i + 1, channels:]
            for r in range(rows_dev + 2):
                inside = window(info, i, base + r - 1, (width, channels))
                value = padded_row(first, above, below, i, r)
                _, moved = moved_of(value, inside, average, inverse, gain[...], scale, shift)
                put_shifted(shifted, i, r, moved * sigmoid(moved) * inside, second)

    part = dot(tap_rows(shifted, tap, images, rows_dev, width), weight[0], 1, 0)

    @pl.when(tap == 0)
    def _():
        acc[...] = part

    @pl.when(tap > 0)
    def _():
        acc[...] += part

    @pl.when(tap == 2)
    def _():
        for i in range(images):
            one = two = jnp.zeros((width, channels), F32)
            for r in range(rows_dev):
                inside = window(info, i, base + r, (width, channels))
                at = (i * rows_dev + r) * width
                value = (image[i, r].astype(F32) + acc[at : at + width]) * inside
                middle[i, r] = value
                one = one + value
                two = two + value * value
            put_stats(out_stats, i, one, two)


def dgrad(shifted, tap, weight, images, rows_dev, width):
    channels = weight.shape[2]
    lhs = tap_rows(shifted, tap, images, rows_dev, width)
    part = None
    for b in range(3):
        term = dot(
            lhs[:, b * channels : (b + 1) * channels],
            weight[0, (2 - b) * channels : (3 - b) * channels, :],
            1,
            1,
        )
        part = term if part is None else part + term
    return part


def back2_kernel(
    info, grad, grad_above, grad_below, middle, mid_above, mid_below, cot, cot_above, cot_below,
    mid_stats, grad_stats, attn_gain, first, first_stats, gain, shifts, weight,
    grad_middle, moved_grad, out_stats, plain, acc, shifted,
):
    images, rows_dev, width, channels = first.shape
    tap = pl.program_id(0)
    base = info[0, 2]

    @pl.when(tap == 0)
    def _():
        for i in range(images):
            count = image_count(info, i, channels)
            average, inverse = norm_of(mid_stats[i], count)
            mean, cross = means_of(grad_stats[i], attn_gain[...], count)
            for r in range(rows_dev + 2):
                inside = window(info, i, base + r - 1, (width, channels))
                normal = (padded_row(middle, mid_above, mid_below, i, r) - average) * inverse
                dx = padded_row(grad, grad_above, grad_below, i, r) * attn_gain[...]
                term = (dx - mean - normal * cross) * inverse * inside
                total = padded_row(cot, cot_above, cot_below, i, r).astype(F32) + term
                if 0 < r <= rows_dev:
                    grad_middle[i, r - 1] = total
                put_shifted(shifted, i, r, total * inside, plain)

    part = dgrad(shifted, tap, weight, images, rows_dev, width)

    @pl.when(tap == 0)
    def _():
        acc[...] = part

    @pl.when(tap > 0)
    def _():
        acc[...] += part

    @pl.when(tap == 2)
    def _():
        for i in range(images):
            average, inverse = norm_of(first_stats[i], image_count(info, i, channels))
            scale, shift = shifts[i : i + 1, :channels], shifts[i : i + 1, channels:]
            one = two = jnp.zeros((width, channels), F32)
            for r in range(rows_dev):
                inside = window(info, i, base + r, (width, channels))
                at = (i * rows_dev + r) * width
                normal, moved = moved_of(
                    first[i, r], inside, average, inverse, gain[...], scale, shift
                )
                value = acc[at : at + width] * inside * silu_slope(moved)
                moved_grad[i, r] = value
                one = one + value
                two = two + value * normal
            put_stats(out_stats, i, one, two)


def back1_kernel(
    info, grad, grad_above, grad_below, first, first_above, first_below, first_stats, grad_stats,
    gain, shifts, image, image_stats, first_gain, weight,
    pre_grad, out_stats, plain, acc, shifted,
):
    images, rows_dev, width, channels = first.shape
    tap = pl.program_id(0)
    base = info[0, 2]

    @pl.when(tap == 0)
    def _():
        for i in range(images):
            count = image_count(info, i, channels)
            average, inverse = norm_of(first_stats[i], count)
            factor = gain[...] * (1.0 + shifts[i : i + 1, :channels])
            mean, cross = means_of(grad_stats[i], factor, count)
            for r in range(rows_dev + 2):
                inside = window(info, i, base + r - 1, (width, channels))
                normal = (padded_row(first, first_above, first_below, i, r) - average) * inverse
                dx = padded_row(grad, grad_above, grad_below, i, r) * factor
                put_shifted(shifted, i, r, (dx - mean - normal * cross) * inverse * inside, plain)

    part = dgrad(shifted, tap, weight, images, rows_dev, width)

    @pl.when(tap == 0)
    def _():
        acc[...] = part

    @pl.when(tap > 0)
    def _():
        acc[...] += part

    @pl.when(tap == 2)
    def _():
        for i in range(images):
            average, inverse = norm_of(image_stats[i], image_count(info, i, channels))
            one = two = jnp.zeros((width, channels), F32)
            for r in range(rows_dev):
                inside = window(info, i, base + r, (width, channels))
                at = (i * rows_dev + r) * width
                normal = (image[i, r].astype(F32) - average) * inverse * inside
                slope = silu_slope(normal * first_gain[...])
                value = acc[at : at + width] * inside * slope
                pre_grad[i, r] = value
                one = one + value
                two = two + value * normal
            put_stats(out_stats, i, one, two)


def conv_call(kernel, info, inputs, weight, outs, flipped):
    images, rows_dev, width, channels = outs[0].shape

    def whole(shape):
        return pl.BlockSpec(shape, lambda tap: (0,) * len(shape))

    def tap_of(tap):
        return ((2 - tap) if flipped else tap, 0, 0)

    weight = weight.reshape(3, 3 * channels, channels)
    flops = 2 * 9 * images * rows_dev * width * channels * channels
    moved = sum(a.size * a.dtype.itemsize for a in (*inputs, weight, *outs))
    return pl.pallas_call(
        kernel,
        grid=(3,),
        out_shape=tuple(outs),
        in_specs=[SCALARS]
        + [whole(a.shape) for a in inputs]
        + [pl.BlockSpec((1, 3 * channels, channels), tap_of)],
        out_specs=tuple(whole(o.shape) for o in outs),
        scratch_shapes=[
            pltpu.VMEM((images * rows_dev * width, channels), F32),
            pltpu.VMEM((images, rows_dev + 2, width, 3 * channels), BF16),
        ],
        compiler_params=pltpu.CompilerParams(vmem_limit_bytes=48 << 20),
        cost_estimate=pl.CostEstimate(flops=flops, bytes_accessed=moved, transcendentals=0),
        name=kernel.__name__,
    )(info, *inputs, weight)


def weight_grad_kernel(grads, hidden, out, turned, shifted):
    images, padded, width, channels = hidden.shape
    rows_dev = padded - 2
    pixels = images * rows_dev * width
    tap = pl.program_id(0)

    @pl.when(tap == 0)
    def _():
        center = grads[:, 1 : rows_dev + 1]
        turned[...] = center.reshape(pixels, channels).astype(F32).T.astype(BF16)
        for i in range(images):
            for r in range(padded):
                put_shifted(shifted, i, r, hidden[i, r].astype(F32))

    column = pl.multiple_of((tap % 3) * channels, channels)
    rhs = shifted[:, pl.ds(tap // 3, rows_dev), :, pl.ds(column, channels)]
    out[...] = dot(turned[...], rhs.reshape(pixels, channels), 1, 0).astype(BF16)


def weight_grad(grads, hidden):
    images, padded, width, channels = hidden.shape
    pixels = images * (padded - 2) * width

    def whole(shape):
        return pl.BlockSpec(shape, lambda tap: (0,) * len(shape))

    return pl.pallas_call(
        weight_grad_kernel,
        grid=(9,),
        out_shape=jax.ShapeDtypeStruct((channels, 9 * channels), BF16),
        in_specs=[whole(grads.shape), whole(hidden.shape)],
        out_specs=pl.BlockSpec((channels, channels), lambda tap: (0, tap)),
        scratch_shapes=[
            pltpu.VMEM((channels, pixels), BF16),
            pltpu.VMEM(hidden.shape[:3] + (3 * channels,), BF16),
        ],
        compiler_params=pltpu.CompilerParams(vmem_limit_bytes=32 << 20),
        cost_estimate=pl.CostEstimate(
            flops=18 * pixels * channels * channels,
            bytes_accessed=18 * channels * channels,
            transcendentals=0,
        ),
        name="weight_grad",
    )(grads, hidden)


def project_kernel(info, middle, stats, gain, weight, attn, qkv):
    images, rows_dev, width, channels = middle.shape
    pixels = rows_dev * width
    heads, wide = HEADS, weight.shape[0] // HEADS
    base = info[0, 2]
    for i in range(images):
        average, inverse = norm_of(stats[i], image_count(info, i, channels))
        for r in range(rows_dev):
            inside = window(info, i, base + r, (width, channels))
            value = (middle[i, r] - average) * inverse * inside * gain[...]
            attn[i, r * width : (r + 1) * width] = value.astype(BF16)
        for h in range(heads):
            block = dot(weight[h * wide : (h + 1) * wide], attn[i], 1, 1)
            qkv[i * heads + h] = block.astype(BF16)


def project(info, middle, stats, gain, weight):
    images, rows_dev, width, channels = middle.shape
    pixels = rows_dev * width
    return pl.pallas_call(
        project_kernel,
        out_shape=(
            jax.ShapeDtypeStruct((images, pixels, channels), BF16),
            jax.ShapeDtypeStruct((images * HEADS, weight.shape[0] // HEADS, pixels), BF16),
        ),
        in_specs=[SCALARS, WHOLE, WHOLE, WHOLE, WHOLE],
        out_specs=(WHOLE, WHOLE),
        compiler_params=pltpu.CompilerParams(vmem_limit_bytes=32 << 20),
        name="project",
    )(info, middle, stats, gain, weight)


def unproject_kernel(info, middle, stats, grads, weight, out, out_stats):
    images, rows_dev, width, channels = middle.shape
    wide, pixels = grads.shape[1], grads.shape[2]
    base = info[0, 2]
    for i in range(images):
        average, inverse = norm_of(stats[i], image_count(info, i, channels))
        acc = None
        for h in range(HEADS):
            turned = grads[i * HEADS + h].astype(F32).T.astype(BF16)
            term = dot(turned, weight[h * wide : (h + 1) * wide], 1, 0)
            acc = term if acc is None else acc + term
        one = two = jnp.zeros((width, channels), F32)
        for r in range(rows_dev):
            inside = window(info, i, base + r, (width, channels))
            value = acc[r * width : (r + 1) * width] * inside
            out[i, r] = value
            one = one + value
            two = two + value * ((middle[i, r] - average) * inverse)
        put_stats(out_stats, i, one, two)


def unproject(info, middle, stats, grads, weight):
    images, rows_dev, width, channels = middle.shape
    return pl.pallas_call(
        unproject_kernel,
        out_shape=(
            jax.ShapeDtypeStruct(middle.shape, F32),
            jax.ShapeDtypeStruct(stats.shape, F32),
        ),
        in_specs=[SCALARS, WHOLE, WHOLE, WHOLE, WHOLE],
        out_specs=(WHOLE, WHOLE),
        compiler_params=pltpu.CompilerParams(vmem_limit_bytes=32 << 20),
        name="unproject",
    )(info, middle, stats, grads, weight)


def finish_kernel(info, pre_grad, grad_stats, image, stats, gain, grad_middle, out):
    images, rows_dev, width, channels = image.shape
    base = info[0, 2]
    for i in range(images):
        count = image_count(info, i, channels)
        average, inverse = norm_of(stats[i], count)
        mean, cross = means_of(grad_stats[i], gain[...], count)
        for r in range(rows_dev):
            inside = window(info, i, base + r, (width, channels))
            normal = (image[i, r].astype(F32) - average) * inverse
            term = (pre_grad[i, r] * gain[...] - mean - normal * cross) * inverse
            out[i, r] = (grad_middle[i, r] + term) * inside


def finish(info, pre_grad, grad_stats, image, stats, gain, grad_middle):
    return pl.pallas_call(
        finish_kernel,
        out_shape=jax.ShapeDtypeStruct(image.shape, F32),
        in_specs=[SCALARS] + [WHOLE] * 6,
        out_specs=WHOLE,
        compiler_params=pltpu.CompilerParams(vmem_limit_bytes=32 << 20),
        name="finish",
    )(info, pre_grad, grad_stats, image, stats, gain, grad_middle)


DMA = pltpu.SemaphoreType.DMA


def remote(src, dst, send, recv, device):
    return pltpu.make_async_remote_copy(
        src_ref=src,
        dst_ref=dst,
        send_sem=send,
        recv_sem=recv,
        device_id=device,
        device_id_type=MESH,
    )


class Grid:
    def __init__(self, items, n):
        self.items, self.n = items, n
        self.item, self.me = lax.axis_index("items"), lax.axis_index("rows")

    def row(self, k):
        return {"items": self.item, "rows": lax.rem(self.me + k, self.n)}

    def peer(self, k):
        return {"items": lax.rem(self.item + k, self.items), "rows": self.me}

    def greet(self):
        barrier = pltpu.get_barrier_semaphore()

        def rows(k, carry):
            pl.semaphore_signal(barrier, inc=1, device_id=self.row(k), device_id_type=MESH)
            return carry

        def items(k, carry):
            pl.semaphore_signal(barrier, inc=1, device_id=self.peer(k), device_id_type=MESH)
            return carry

        lax.fori_loop(1, self.n, rows, 0)
        lax.fori_loop(1, self.items, items, 0)

    def met(self):
        pl.semaphore_wait(pltpu.get_barrier_semaphore(), self.n + self.items - 2)

    def loop(self, count, body):
        def step(k, carry):
            body(k)
            return carry

        lax.fori_loop(1, count, step, 0)


class Sums:
    def __init__(self, grid, own, slots, send, recv):
        self.grid, self.own, self.slots, self.send, self.recv = grid, own, slots, send, recv

    def copy(self, k):
        return remote(
            self.own, self.slots.at[self.grid.me], self.send.at[k], self.recv.at[k], self.grid.row(k)
        )

    def start(self, stats):
        lines, lanes = self.own.shape
        half = lines // 2
        at = lax.broadcasted_iota(jnp.int32, (lines, lanes), 0)
        packed = jnp.zeros((lines, lanes), F32)
        for j in range(lines):
            piece = stats[j // half : j // half + 1, (j % half) * lanes : (j % half + 1) * lanes]
            packed = jnp.where(at == j, piece, packed)
        self.own[...] = packed
        self.grid.loop(self.grid.n, lambda k: self.copy(k).start())
        self.slots[self.grid.me] = packed

    def result(self):
        self.grid.loop(self.grid.n, lambda k: self.copy(k).wait())
        slots = self.slots
        total = lax.fori_loop(1, self.grid.n, lambda k, s: s + slots[k], slots[0])
        half = total.shape[0] // 2
        rows = [
            jnp.concatenate([total[r * half + j : r * half + j + 1] for j in range(half)], axis=1)
            for r in range(2)
        ]
        at = lax.broadcasted_iota(jnp.int32, (8, rows[0].shape[1]), 0)
        return jnp.where(at == 0, rows[0], jnp.where(at == 1, rows[1], 0.0))


class Edges:
    def __init__(self, grid, field, send, recv):
        self.grid, self.field, self.send, self.recv = grid, field, send, recv

    def copy(self, side):
        last = self.field.shape[0] - 1
        at, to = (last - 1, 0) if side == 0 else (1, last)
        grid = self.grid
        return remote(
            self.field.at[at : at + 1],
            self.field.at[to : to + 1],
            self.send.at[side],
            self.recv.at[side],
            {"items": grid.item, "rows": grid.me + 1 if side == 0 else grid.me - 1},
        )

    def both(self, down, up):
        @pl.when(self.grid.me < self.grid.n - 1)
        def _():
            down()

        @pl.when(self.grid.me > 0)
        def _():
            up()

    def clear(self):
        last = self.field.shape[0] - 1

        @pl.when(self.grid.me == 0)
        def _():
            self.field[0] = jnp.zeros(self.field.shape[1:], self.field.dtype)

        @pl.when(self.grid.me == self.grid.n - 1)
        def _():
            self.field[last] = jnp.zeros(self.field.shape[1:], self.field.dtype)

    def start(self):
        self.both(lambda: self.copy(0).start(), lambda: self.copy(1).start())

    def wait(self):
        self.both(lambda: self.copy(1).wait_recv(), lambda: self.copy(0).wait_recv())
        self.both(lambda: self.copy(0).wait_send(), lambda: self.copy(1).wait_send())


def shift_into(out, r, value):
    width, channels = value.shape
    column = lax.broadcasted_iota(jnp.int32, value.shape, 0)
    left = jnp.where(column == 0, 0.0, pltpu.roll(value, 1, 0))
    right = jnp.where(column == width - 1, 0.0, pltpu.roll(value, width - 1, 0))
    out[r, :, :channels] = left.astype(BF16)
    out[r, :, channels : 2 * channels] = value.astype(BF16)
    out[r, :, 2 * channels :] = right.astype(BF16)


def row_stats(rows, width, channels, row):
    def step(r, carry):
        one, two = row(r)
        return carry[0] + one, carry[1] + two

    zero = jnp.zeros((width, channels), F32)
    one, two = lax.fori_loop(0, rows, step, (zero, zero))
    one = jnp.sum(one, axis=0, keepdims=True)
    two = jnp.sum(two, axis=0, keepdims=True)
    at = lax.broadcasted_iota(jnp.int32, (8, channels), 0)
    return jnp.where(at == 0, one, jnp.where(at == 1, two, 0.0))


def each_row(rows, body):
    def step(r, carry):
        body(r)
        return carry

    lax.fori_loop(0, rows, step, 0)


def conv_taps(shifted, weight, acc, rows_dev):
    pixels, wide = acc.shape[0], shifted.shape[2]
    acc[...] = jnp.zeros_like(acc)

    def step(tap, carry):
        acc[...] += dot(shifted[pl.ds(tap, rows_dev)].reshape(pixels, wide), weight[tap], 1, 0)
        return carry

    lax.fori_loop(0, 3, step, 0)


def forward_kernel(items, n, step, bq, *refs):
    (info, image, cot, text, embed, gain1, gain2, gain3, w1_in, w2_in, embed_in, text_in, qkv_in, proj_in,
     first_out, mid_out, cot_out, hidden_all, second_all, attn_out, turned_out, output, query_part, side_out, dkv_out,
     dt_out, dt_all, text_cols, stats_out, shifts_out,
     image_v, cot_v, text_v, w1, w2, wide_w, qkv_w, proj_w, first_v, mid_v, hidden, second, attn,
     turned, pairs, queries, go, text_kv, cols, shifted, acc, own, slots,
     pair_land, query_land, go_land, text_pair, o, dq, dkv, dtext, same, o_land, dq_land, masked, out_v, query_acc,
     side_v, side_core, side_sum, side_item, side_total, cols_land,
     load, sum_send, sum_recv, edge_send, edge_recv, row_send, row_recv, item_send, item_recv,
     s_core_send, s_core_recv, s_item_send, s_item_recv, *scratch) = refs
    grid = Grid(items, n)
    item, me = grid.item, grid.me
    rows_dev, width, channels = image.shape
    pixels = rows_dev * width
    heads, head_dim, wide = HEADS, channels // HEADS, 3 * channels // HEADS
    base = me * rows_dev
    share_rows = channels // n
    count = (info[0, 0] * info[0, 1]).astype(F32) * (channels // GROUPS)
    att = Attention(n, pixels, head_dim, n * text.shape[0], step, bq, scratch)

    def inside(row):
        return window(info, 0, row, (width, channels))

    loads = []

    def fetch(src, dst):
        c = pltpu.make_async_copy(src, dst, load.at[len(loads)])
        c.start()
        loads.append(c)
        return c

    center = slice(1, rows_dev + 1)
    got_image = fetch(image, image_v.at[center])
    got_cot = fetch(cot, cot_v.at[center])
    got_proj = fetch(proj_in, proj_w)
    got_text = fetch(text, text_v)
    got_text_w = fetch(text_in, wide_w)
    got_w1 = fetch(w1_in, w1)
    got_w2 = fetch(w2_in, w2)
    got_qkv_w = fetch(qkv_in, qkv_w)
    edges = [
        Edges(grid, field, edge_send.at[j], edge_recv.at[j])
        for j, field in enumerate((image_v, cot_v, first_v, mid_v))
    ]
    sums = [Sums(grid, own.at[j], slots.at[j], sum_send.at[j], sum_recv.at[j]) for j in range(3)]
    grid.greet()
    for e in edges:
        e.clear()
    same[...] = group_matrix(channels)
    got_image.wait()

    def start_row(r):
        return image_v[1 + r].astype(F32) * inside(base + r)

    def start_stats(r):
        v = start_row(r)
        return v, v * v

    stats = row_stats(rows_dev, width, channels, start_stats)
    grid.met()
    sums[0].start(stats)
    edges[0].start()
    got_cot.wait()
    edges[1].start()

    got_text.wait()
    got_text_w.wait()
    text_all = dot(text_v[...], wide_w[...], 1, 0).astype(BF16)
    got_embed_w = fetch(embed_in, wide_w)
    share = text_v.shape[1] // n
    for h in range(heads):
        text_kv[h] = text_all[:, h * 2 * head_dim : (h + 1) * 2 * head_dim]
    for r in range(n):
        cols[r] = text_v[:, r * share : (r + 1) * share]

    def scatter(j, src, dst):
        def copy(k):
            to = lax.rem(me + k, n)
            return remote(src.at[to], dst.at[me], row_send.at[j, k], row_recv.at[j, k], grid.row(k))

        return copy

    kv_copy = scatter(0, text_kv, text_pair)
    col_copy = scatter(1, cols, cols_land)
    grid.loop(n, lambda k: kv_copy(k).start())
    grid.loop(n, lambda k: col_copy(k).start())
    own_kv = fetch(text_kv.at[me], text_pair.at[me])
    cols_land[me] = cols[me]

    got_proj.wait()

    def to_grad(r):
        masked[pl.ds(r * width, width)] = (cot_v[1 + r].astype(F32) * inside(base + r)).astype(BF16)

    each_row(rows_dev, to_grad)
    for h in range(heads):
        go[h] = dot(proj_w[h * head_dim : (h + 1) * head_dim], masked[...], 1, 1).astype(BF16)
    go_copy = scatter(2, go, go_land)
    own_go = fetch(go.at[me], go_land.at[me])

    stats = sums[0].result()
    stats_out[0] = stats
    average, inverse = norm_of(stats, count, same[...])
    edges[0].wait()

    def to_hidden(r):
        ok = inside(base + r - 1)
        value = (image_v[r].astype(F32) * ok - average) * inverse * ok * gain1[...]
        value = value * sigmoid(value) * ok
        shift_into(shifted, r, value)
        hidden[r] = value.astype(BF16)

    each_row(rows_dev + 2, to_hidden)

    def spread(j, src, dst):
        def copy(k):
            return remote(src, dst.at[item], item_send.at[j, k], item_recv.at[j, k], grid.peer(k))

        return copy

    hidden_copy = spread(0, hidden, hidden_all)
    grid.loop(items, lambda k: hidden_copy(k).start())
    own_hidden = fetch(hidden, hidden_all.at[item])
    got_w1.wait()
    conv_taps(shifted, w1, acc, rows_dev)

    def first_row(r):
        value = acc[pl.ds(r * width, width)] * inside(base + r)
        first_v[1 + r] = value
        return value, value * value

    stats = row_stats(rows_dev, width, channels, first_row)
    sums[1].start(stats)
    edges[2].start()

    e = embed[...].astype(F32)
    low = (e * sigmoid(e)).astype(BF16)
    got_embed_w.wait()
    shifts_out[...] = dot(low, wide_w[...], 1, 0)
    scale, shift = shifts_out[:, :channels], shifts_out[:, channels:]

    stats = sums[1].result()
    stats_out[1] = stats
    average, inverse = norm_of(stats, count, same[...])
    edges[2].wait()
    own_first = fetch(first_v, first_out)

    def to_second(r):
        ok = inside(base + r - 1)
        _, moved = moved_of(first_v[r], ok, average, inverse, gain2[...], scale, shift)
        value = moved * sigmoid(moved) * ok
        shift_into(shifted, r, value)
        second[r] = value.astype(BF16)

    each_row(rows_dev + 2, to_second)
    second_copy = spread(1, second, second_all)
    grid.loop(items, lambda k: second_copy(k).start())
    own_second = fetch(second, second_all.at[item])
    got_w2.wait()
    conv_taps(shifted, w2, acc, rows_dev)

    def middle_row(r):
        value = (image_v[1 + r].astype(F32) + acc[pl.ds(r * width, width)]) * inside(base + r)
        mid_v[1 + r] = value
        return value, value * value

    stats = row_stats(rows_dev, width, channels, middle_row)
    sums[2].start(stats)
    edges[3].start()
    edges[1].wait()
    own_cot = fetch(cot_v, cot_out)
    got_qkv_w.wait()
    for j in range(3):
        block = qkv_w[:, j * channels : (j + 1) * channels].astype(F32).T
        turned[j * channels : (j + 1) * channels] = block.astype(BF16)
    own_turned = fetch(turned, turned_out)

    stats = sums[2].result()
    stats_out[2] = stats
    average, inverse = norm_of(stats, count, same[...])

    def to_attn(r):
        value = (mid_v[1 + r] - average) * inverse * inside(base + r) * gain3[...]
        attn[pl.ds(r * width, width)] = value.astype(BF16)

    each_row(rows_dev, to_attn)
    own_attn = fetch(attn, attn_out)
    pair_copy = scatter(3, pairs, pair_land)
    query_copy = scatter(4, queries, query_land)

    def head(k):
        to = lax.rem(me + k, n)
        rows = pl.ds(pl.multiple_of(to * wide, wide), wide)
        block = dot(turned[rows], attn[...], 1, 1).astype(BF16)
        queries[to] = block[:head_dim]
        pairs[to] = block[head_dim:]

    def send_head(k):
        head(k)
        pair_copy(k).start()

    grid.loop(n, send_head)
    head(0)
    query_land[me] = queries[me]
    att.stage_key(me, pairs[me, :head_dim], width, info[0, 0], info[0, 1])
    att.stage_value(me, pairs[me, head_dim:])
    grid.loop(n, lambda k: kv_copy(k).wait())
    own_kv.wait()
    att.stage_text(text_pair[...].reshape(n * text.shape[0], 2 * head_dim))
    edges[3].wait()
    own_mid = fetch(mid_v, mid_out)

    def source(k):
        return lax.rem(me + n - k, n)

    def stage_pair(k):
        pair_copy(k).wait()
        c = source(k)
        att.stage_key(c, pair_land[c, :head_dim], width, info[0, 0], info[0, 1])
        att.stage_value(c, pair_land[c, head_dim:])

    grid.loop(n, stage_pair)

    def send_rest(k):
        query_copy(k).start()
        go_copy(k).start()

    grid.loop(n, send_rest)
    own_go.wait()

    def before(k):
        query_copy(k).wait()
        go_copy(k).wait()

    def give(j, src, dst):
        def copy(h):
            to = source(h)
            return remote(
                src.at[to],
                dst.at[me],
                row_send.at[j, h],
                row_recv.at[j, h],
                {"items": item, "rows": to},
            )

        return copy

    o_copy = give(5, o, o_land)
    dq_copy = give(6, dq, dq_land)
    dkv_copy = give(7, dkv, dkv_out)
    dt_copy = give(8, dtext, dt_out)

    def done(h):
        @pl.when(h > 0)
        def _():
            o_copy(h).start()
            dq_copy(h).start()

    grid.loop(n, lambda k: col_copy(k).wait())
    cols_copy = spread(2, cols_land, text_cols)
    grid.loop(items, lambda k: cols_copy(k).start())
    own_cols = fetch(cols_land, text_cols.at[item])
    att.attend(query_land, go_land, o, dq, source, before, done)

    def send_keys(h):
        at = pl.ds(pl.multiple_of(source(h) * pixels, pixels), pixels)
        dkv[source(h), :head_dim] = att.key_grad(at)
        dkv[source(h), head_dim:] = att.value_grad(at)

    def send_next(h):
        send_keys(h)
        dkv_copy(h).start()

    grid.loop(n, send_next)
    send_keys(0)
    flat = jnp.concatenate(
        [
            (att.dkt[:, n * pixels :] * (head_dim**-0.5)).T,
            att.dvt[:, n * pixels :].T,
        ],
        axis=1,
    )
    for r in range(n):
        tokens = text.shape[0]
        dtext[r] = flat[r * tokens : (r + 1) * tokens].astype(BF16)
    grid.loop(n, lambda h: dt_copy(h).start())

    def gather_copy(k):
        return remote(
            dtext, dt_all.at[item, me], row_send.at[9, k], row_recv.at[9, k], grid.row(k)
        )

    grid.loop(n, lambda k: gather_copy(k).start())
    own_dkv = fetch(dkv.at[me], dkv_out.at[me])
    own_dt = fetch(dtext.at[me], dt_out.at[me])
    own_all = fetch(dtext, dt_all.at[item, me])

    o_land[me] = o[me]
    dq_land[me] = dq[me]
    grid.loop(n, lambda h: o_copy(h).wait())
    grid.loop(n, lambda h: dq_copy(h).wait())
    side = SideSum(grid, side_v, side_core, side_sum, side_item, side_total, None, None,
                   (s_core_send, s_core_recv), (s_item_send, s_item_recv), None, None)

    def query_head(h):
        block = dot(dq_land[h], attn[...], 1, 0).astype(BF16)
        side.put_head(h, block, 0)

    each_row(heads, query_head)
    flat_o = o_land[...].reshape(channels, pixels)
    block = dot(masked[...].astype(F32).T.astype(BF16), flat_o, 1, 1).astype(BF16)
    for r in range(n):
        side.put_head(r, block[r * share_rows : (r + 1) * share_rows], 1)
    side.core_copy().start()
    query_acc[...] = jnp.zeros_like(query_acc)

    def unproject_query(h):
        rows = pl.ds(pl.multiple_of(h * wide, wide), head_dim)
        query_acc[...] += dot(dq_land[h].astype(F32).T.astype(BF16), turned[rows], 1, 0)

    each_row(heads, unproject_query)
    put_query = fetch(query_acc, query_part)
    side.over_items()
    acc[...] = dot(flat_o.astype(F32).T.astype(BF16), proj_w[...], 1, 0)

    def output_row(r):
        value = mid_v[1 + r] + acc[pl.ds(r * width, width)] * inside(base + r)
        out_v[r] = value.astype(BF16)

    each_row(rows_dev, output_row)
    put_output = fetch(out_v, output)
    side.sum_items()
    put_side = fetch(side_total, side_out)
    grid.loop(items, lambda k: hidden_copy(k).wait())
    grid.loop(items, lambda k: second_copy(k).wait())
    grid.loop(items, lambda k: cols_copy(k).wait())
    for copy in (dkv_copy, dt_copy, gather_copy):
        grid.loop(n, lambda h: copy(h).wait())
    for c in (own_hidden, own_first, own_second, own_cot, own_turned, own_attn, own_mid, own_dkv, own_dt, own_all,
              own_cols, put_query, put_output, put_side):
        c.wait()


def forward_call(info, image, cot, text, embed, gains, weights, identity):
    items, n = lax.axis_size("items"), lax.axis_size("rows")
    rows_dev, width, channels = image.shape
    pixels = rows_dev * width
    padded = (rows_dev + 2, width, channels)
    tokens, text_width = text.shape
    head_dim = channels // HEADS
    w1, w2, _, text_w, qkv_w, proj_w = weights
    chips = n // 2
    rows = channels // n // items
    sds = jax.ShapeDtypeStruct
    outs = (
        sds(padded, F32),
        sds(padded, F32),
        sds(padded, BF16),
        sds((items,) + padded, BF16),
        sds((items,) + padded, BF16),
        sds((pixels, channels), BF16),
        sds((3 * channels, channels), BF16),
        sds(image.shape, BF16),
        sds((pixels, channels), F32),
        sds((chips, rows, 2 * channels), BF16),
        sds((n, 2 * head_dim, pixels), BF16),
        sds((n, tokens, 2 * head_dim), BF16),
        sds((items, n, n, tokens, 2 * head_dim), BF16),
        sds((items, n, tokens, text_width // n), BF16),
        sds((3, 8, channels), F32),
        sds((1, 2 * channels), F32),
    )
    v = pltpu.VMEM
    scratch = [
        v(padded, BF16),
        v(padded, BF16),
        v(text.shape, BF16),
        v(w1.shape, BF16),
        v(w2.shape, BF16),
        v(text_w.shape, BF16),
        v(qkv_w.shape, BF16),
        v(proj_w.shape, BF16),
        v(padded, F32),
        v(padded, F32),
        v(padded, BF16),
        v(padded, BF16),
        v((pixels, channels), BF16),
        v((3 * channels, channels), BF16),
        v((n, 2 * head_dim, pixels), BF16),
        v((n, head_dim, pixels), BF16),
        v((n, head_dim, pixels), BF16),
        v((n, tokens, 2 * head_dim), BF16),
        v((n, tokens, text_width // n), BF16),
        v((rows_dev + 2, width, 3 * channels), BF16),
        v((pixels, channels), F32),
        v((3, channels // 64, 128), F32),
        v((3, n, channels // 64, 128), F32),
        v((n, 2 * head_dim, pixels), BF16),
        v((n, head_dim, pixels), BF16),
        v((n, head_dim, pixels), BF16),
        v((n, tokens, 2 * head_dim), BF16),
        v((n, head_dim, pixels), BF16),
        v((n, head_dim, pixels), BF16),
        v((n, 2 * head_dim, pixels), BF16),
        v((n, tokens, 2 * head_dim), BF16),
        v((channels, channels), BF16),
        v((n, head_dim, pixels), BF16),
        v((n, head_dim, pixels), BF16),
        v((pixels, channels), BF16),
        v(image.shape, BF16),
        v((pixels, channels), F32),
        v((2, chips, items, rows, 2 * channels), BF16),
        v((chips, items, rows, 2 * channels), BF16),
        v((items, chips, rows, 2 * channels), BF16),
        v((items, chips, rows, 2 * channels), BF16),
        v((chips, rows, 2 * channels), BF16),
        v((n, tokens, text_width // n), BF16),
        DMA((28,)),
        DMA((3, n)),
        DMA((3, n)),
        DMA((4, 2)),
        DMA((4, 2)),
        DMA((10, n)),
        DMA((10, n)),
        DMA((3, items)),
        DMA((3, items)),
        DMA((1,)),
        DMA((1,)),
        DMA((items,)),
        DMA((items,)),
    ]
    step, bq, extra = attention_scratch(n, pixels, head_dim, n * tokens)
    scratch += extra
    return pl.pallas_call(
        functools.partial(forward_kernel, items, n, step, bq),
        out_shape=outs,
        in_specs=[SCALARS] + [ANYWHERE] * 3 + [WHOLE] * 4 + [ANYWHERE] * 6,
        out_specs=(ANYWHERE,) * 14 + (WHOLE,) * 2,
        scratch_shapes=scratch,
        compiler_params=pltpu.CompilerParams(
            collective_id=identity, has_side_effects=True, vmem_limit_bytes=62 << 20
        ),
        cost_estimate=pl.CostEstimate(
            flops=40 * pixels * channels * channels, bytes_accessed=60 << 20, transcendentals=0
        ),
        name="forward",
    )(info, image, cot, text, embed, *gains, *weights)


class KernelSum:
    def __init__(self, grid, turned, quarter, part, from_core, chip_sum, from_chip, final, item_sems, core_sems,
                 chip_sems, final_sems):
        self.grid = grid
        self.turned, self.quarter, self.part, self.from_core = turned, quarter, part, from_core
        self.chip_sum, self.from_chip, self.final = chip_sum, from_chip, final
        self.item_sems, self.core_sems = item_sems, core_sems
        self.chip_sems, self.final_sems = chip_sems, final_sems
        self.chips = grid.n // 2
        self.chip, self.core = grid.me // 2, lax.rem(grid.me, 2)

    def grads_copy(self, k):
        grid = self.grid
        send, recv = self.item_sems
        to = lax.rem(grid.item + k, grid.items)
        return remote(
            self.turned.at[to], self.quarter.at[grid.item], send.at[k], recv.at[k], grid.peer(k)
        )

    def send_grads(self, shifted):
        grid, chips = self.grid, self.chips
        rows_dev, width, channels = shifted.shape[0] - 2, shifted.shape[1], shifted.shape[2] // 3
        center = shifted[1 : rows_dev + 1, :, channels : 2 * channels]
        block = center.reshape(rows_dev * width, channels).astype(F32).T.astype(BF16)
        share = channels // grid.n
        rows = share // grid.items
        for z in range(chips):
            for c in range(2):
                for q in range(grid.items):
                    at = (z * 2 + c) * share + q * rows
                    to = (c * chips + z) * rows
                    self.turned[q, to : to + rows] = block[at : at + rows]
        grid.loop(grid.items, lambda k: self.grads_copy(k).start())
        self.quarter[grid.item] = self.turned[grid.item]

    def wait_grads(self):
        self.grid.loop(self.grid.items, lambda k: self.grads_copy(k).wait())

    def core_copy(self, a):
        send, recv = self.core_sems
        grid = self.grid
        return remote(
            self.part.at[a, 1 - self.core],
            self.from_core.at[a],
            send.at[a],
            recv.at[a],
            {"items": grid.item, "rows": grid.me + 1 - 2 * self.core},
        )

    def compute(self, a, shifted):
        items, padded, width, wide = shifted.shape
        rows_dev, channels = padded - 2, wide // 3
        half = self.turned.shape[1] // 2
        for b in range(3):
            acc = None
            for g in range(items):
                rhs = shifted[g, a : a + rows_dev, :, b * channels : (b + 1) * channels]
                term = dot(self.quarter[g], rhs.reshape(rows_dev * width, channels), 1, 0)
                acc = term if acc is None else acc + term
            self.part[a, 0, b] = acc[:half].astype(BF16)
            self.part[a, 1, b] = acc[half:].astype(BF16)
        self.core_copy(a).start()

    def chip_copy(self, a, k):
        send, recv = self.chip_sems
        grid = self.grid
        to = lax.rem(self.chip + k, self.chips)
        return remote(
            self.chip_sum.at[a, to],
            self.from_chip.at[a, k],
            send.at[a, k],
            recv.at[a, k],
            {"items": grid.item, "rows": to * 2 + self.core},
        )

    def over_chips(self, a):
        self.core_copy(a).wait()
        rows = self.chip_sum.shape[3]
        for b in range(3):
            both = self.part[a, self.core, b].astype(F32) + self.from_core[a, b].astype(F32)
            for z in range(self.chips):
                self.chip_sum[a, z, b] = both[z * rows : (z + 1) * rows].astype(BF16)
        for k in range(1, self.chips):
            self.chip_copy(a, k).start()

    def final_copy(self, a, k):
        send, recv = self.final_sems
        mine = self.final.at[a, self.grid.item]
        return remote(mine, mine, send.at[a, k], recv.at[a, k], self.grid.peer(k))

    def over_items(self, a):
        for k in range(1, self.chips):
            self.chip_copy(a, k).wait()
        total = self.chip_sum[a, self.chip].astype(F32)
        for k in range(1, self.chips):
            total = total + self.from_chip[a, k].astype(F32)
        self.final[a, self.grid.item] = total.astype(BF16)
        for k in range(1, self.grid.items):
            self.final_copy(a, k).start()

    def wait_final(self, a):
        for k in range(1, self.grid.items):
            self.final_copy(a, k).wait()


class SideSum:
    def __init__(self, grid, values, from_core, core_sum, from_item, item_sum, from_chip, final, core_sems,
                 item_sems, chip_sems, final_sems):
        self.grid = grid
        self.values, self.from_core, self.core_sum = values, from_core, core_sum
        self.from_item, self.item_sum, self.from_chip, self.final = (
            from_item,
            item_sum,
            from_chip,
            final,
        )
        self.core_sems, self.item_sems = core_sems, item_sems
        self.chip_sems, self.final_sems = chip_sems, final_sems
        self.chips = grid.n // 2
        self.chip, self.core = grid.me // 2, lax.rem(grid.me, 2)

    def core_copy(self):
        send, recv = self.core_sems
        grid = self.grid
        return remote(
            self.values.at[1 - self.core],
            self.from_core,
            send.at[0],
            recv.at[0],
            {"items": grid.item, "rows": grid.me + 1 - 2 * self.core},
        )

    def item_copy(self, k):
        send, recv = self.item_sems
        grid = self.grid
        to = lax.rem(grid.item + k, grid.items)
        return remote(
            self.core_sum.at[to], self.from_item.at[k], send.at[k], recv.at[k], grid.peer(k)
        )

    def over_items(self):
        self.core_copy().wait()
        for z in range(self.chips):
            both = self.values[self.core, z].astype(F32) + self.from_core[z].astype(F32)
            for q in range(self.grid.items):
                self.core_sum[q, z] = both[q].astype(BF16)
        for k in range(1, self.grid.items):
            self.item_copy(k).start()

    def chip_copy(self, k):
        send, recv = self.chip_sems
        grid = self.grid
        to = lax.rem(self.chip + k, self.chips)
        return remote(
            self.item_sum.at[to],
            self.from_chip.at[k],
            send.at[k],
            recv.at[k],
            {"items": grid.item, "rows": to * 2 + self.core},
        )

    def put_head(self, h, block, j):
        items, rows = self.values.shape[2], self.values.shape[3]
        channels = block.shape[1]
        at = slice(j * channels, (j + 1) * channels)
        core, chip = (h % 2, h // 2) if isinstance(h, int) else (lax.rem(h, 2), h // 2)
        self.values[core, chip, :, :, at] = block.reshape(items, rows, channels)

    def sum_items(self):
        for k in range(1, self.grid.items):
            self.item_copy(k).wait()
        total = self.core_sum[self.grid.item].astype(F32)
        for k in range(1, self.grid.items):
            total = total + self.from_item[k].astype(F32)
        self.item_sum[:, :, : total.shape[2]] = total.astype(BF16)

    def over_chips(self):
        self.sum_items()
        for k in range(1, self.chips):
            self.chip_copy(k).start()

    def final_copy(self, k):
        send, recv = self.final_sems
        mine = self.final.at[self.grid.item]
        return remote(mine, mine, send.at[k], recv.at[k], self.grid.peer(k))

    def spread(self):
        for k in range(1, self.chips):
            self.chip_copy(k).wait()
        total = self.item_sum[self.chip].astype(F32)
        for k in range(1, self.chips):
            total = total + self.from_chip[k].astype(F32)
        self.final[self.grid.item] = total.astype(BF16)
        for k in range(1, self.grid.items):
            self.final_copy(k).start()

    def wait_final(self):
        for k in range(1, self.grid.items):
            self.final_copy(k).wait()


def conv_taps_back(shifted, weight, acc, rows_dev):
    pixels, channels = acc.shape
    acc[...] = jnp.zeros_like(acc)

    def step(tap, carry):
        lhs = shifted[pl.ds(tap, rows_dev)].reshape(pixels, 3 * channels)
        total = None
        for b in range(3):
            at = pl.multiple_of(((2 - tap) * 3 + 2 - b) * channels, channels)
            term = dot(
                lhs[:, b * channels : (b + 1) * channels], weight[pl.ds(at, channels)], 1, 1
            )
            total = term if total is None else total + term
        acc[...] += total
        return carry

    lax.fori_loop(0, 3, step, 0)


def backward_kernel(items, n, *refs):
    (info, embed, gain1, gain2, gain3, stats_in, shifts,
     query_part, side_in, dkv_in, dt_in, dt_all, first, middle, cot, image, hidden_all, second_all, attn_in,
     turned_in, text_cols, w1_in, w2_in, text_in, embed_in,
     image_grad, text_grad, text_w_grad, embed_grad, final_out, side_out, vectors,
     weight, qkv_turned, first_v, mid_v, cot_v, image_v, attn, cols, rows_v, dkv, dt, own_dt,
     grad_v, grad_mid, moved_v, pre, acc, shifted, shifted_all, image_out, text_v, text_w_v, embed_v, same,
     turned, quarter, part, from_core, chip_sum, from_chip, final,
     side_v, side_core, side_sum, side_item, side_total, side_chip, side_final,
     vector, vector_land, own, slots,
     load, sum_send, sum_recv, edge_send, edge_recv, dt_send, dt_recv, dt_core_send, dt_core_recv, vec_send, vec_recv,
     k_item_send, k_item_recv, k_core_send, k_core_recv, k_chip_send, k_chip_recv, k_final_send, k_final_recv,
     s_core_send, s_core_recv, s_item_send, s_item_recv, s_chip_send, s_chip_recv, s_final_send,
     s_final_recv) = refs
    grid = Grid(items, n)
    item, me = grid.item, grid.me
    rows_dev, width, channels = image.shape
    pixels = rows_dev * width
    heads, head_dim, wide = HEADS, channels // HEADS, 3 * channels // HEADS
    share = channels // n
    base = me * rows_dev
    count = (info[0, 0] * info[0, 1]).astype(F32) * (channels // GROUPS)
    scale, shift = shifts[:, :channels], shifts[:, channels:]

    def inside(row):
        return window(info, 0, row, (width, channels))

    fetched = []

    def fetch(src, dst):
        c = pltpu.make_async_copy(src, dst, load.at[len(fetched)])
        c.start()
        fetched.append(c)
        return c

    got_query = fetch(query_part, acc)
    got_dkv = fetch(dkv_in, dkv)
    got_turned = fetch(turned_in, qkv_turned)
    got_mid = fetch(middle, mid_v)
    got_cot = fetch(cot, cot_v)
    got_w2 = fetch(w2_in, weight)
    got_first = fetch(first, first_v)
    got_attn = fetch(attn_in, attn)
    got_side = fetch(side_in, side_total.at[:, :, 2 * channels :])
    got_dt = fetch(dt_in, own_dt)
    got_all = fetch(dt_all.at[item], dt.at[item])
    got_second = fetch(second_all, rows_v)
    got_image = fetch(image, image_v)
    got_cols = fetch(text_cols, cols)
    grid.greet()
    edges = [
        Edges(grid, field, edge_send.at[j], edge_recv.at[j])
        for j, field in enumerate((grad_v, moved_v))
    ]
    for e in edges:
        e.clear()
    same[...] = group_matrix(channels)
    sums = [Sums(grid, own.at[j], slots.at[j], sum_send.at[j], sum_recv.at[j]) for j in range(3)]
    kernel_sums = [
        KernelSum(grid, turned.at[j], quarter.at[j], part.at[j], from_core.at[j], chip_sum.at[j], from_chip.at[j],
                  final.at[j], (k_item_send.at[j], k_item_recv.at[j]), (k_core_send.at[j], k_core_recv.at[j]),
                  (k_chip_send.at[j], k_chip_recv.at[j]), (k_final_send.at[j], k_final_recv.at[j]))
        for j in range(2)
    ]
    sum2, sum1 = kernel_sums
    side = SideSum(grid, side_v, side_core, side_sum, side_item, side_total, side_chip, side_final,
                   (s_core_send, s_core_recv), (s_item_send, s_item_recv), (s_chip_send, s_chip_recv),
                   (s_final_send, s_final_recv))

    core = lax.rem(me, 2)
    half = heads // 2
    core_heads = pl.ds(core * half, half)

    def dt_copy(k):
        mine = dt.at[item, core_heads]
        return remote(mine, mine, dt_send.at[k], dt_recv.at[k], grid.peer(k))

    def dt_core_copy(k):
        mine = dt.at[lax.rem(item + k, items), core_heads]
        sibling = {"items": item, "rows": me + 1 - 2 * core}
        return remote(mine, mine, dt_core_send.at[k], dt_core_recv.at[k], sibling)

    got_turned.wait()
    got_dkv.wait()
    got_query.wait()

    def unproject_head(h):
        rows = pl.ds(pl.multiple_of(h * wide + head_dim, head_dim), 2 * head_dim)
        acc[...] += dot(dkv[h].astype(F32).T.astype(BF16), qkv_turned[rows], 1, 0)

    each_row(heads, unproject_head)
    got_mid.wait()
    average, inverse = norm_of(stats_in[2], count, same[...])

    def grad_row(r):
        value = acc[pl.ds(r * width, width)] * inside(base + r)
        grad_v[1 + r] = value
        return value, value * ((mid_v[1 + r] - average) * inverse)

    stats = row_stats(rows_dev, width, channels, grad_row)
    grid.met()
    sums[0].start(stats)
    edges[0].start()

    got_attn.wait()

    def qkv_head(h):
        block = dot(dkv[h], attn[...], 1, 0).astype(BF16)
        for w in range(2):
            side.put_head(h, block[w * head_dim : (w + 1) * head_dim], w)

    each_row(heads, qkv_head)
    side.core_copy().start()
    got_cot.wait()

    stats4 = sums[0].result()
    mean, cross = means_of(stats4, gain3[...], count, same[...])
    edges[0].wait()

    def to_grad2(r):
        normal = (mid_v[r] - average) * inverse
        ok = inside(base + r - 1)
        term = (grad_v[r] * gain3[...] - mean - normal * cross) * inverse * ok
        total = cot_v[r].astype(F32) + term
        grad_mid[r] = total
        shift_into(shifted, r, total * ok)

    each_row(rows_dev + 2, to_grad2)
    sum2.send_grads(shifted)
    got_w2.wait()
    conv_taps_back(shifted, weight, acc, rows_dev)
    got_first.wait()
    average2, inverse2 = norm_of(stats_in[1], count, same[...])

    def moved_row(r):
        ok = inside(base + r)
        normal, moved = moved_of(first_v[1 + r], ok, average2, inverse2, gain2[...], scale, shift)
        value = acc[pl.ds(r * width, width)] * ok * silu_slope(moved)
        moved_v[1 + r] = value
        return value, value * normal

    stats = row_stats(rows_dev, width, channels, moved_row)
    sums[1].start(stats)
    edges[1].start()
    got_w1 = fetch(w1_in, weight)
    got_second.wait()

    def shift_rows():
        for g in range(items):
            each_row(rows_dev + 2, lambda r: shift_into(shifted_all.at[g], r, rows_v[g, r].astype(F32)))

    shift_rows()
    got_hidden = fetch(hidden_all, rows_v)
    sum2.wait_grads()
    side.over_items()
    sum2.compute(0, shifted_all)
    sum2.compute(1, shifted_all)
    sum2.over_chips(0)
    sum2.compute(2, shifted_all)
    sum2.over_chips(1)
    sum2.over_chips(2)

    stats5 = sums[1].result()
    factor = gain2[...] * (1.0 + scale)
    mean, cross = means_of(stats5, factor, count, same[...])
    edges[1].wait()

    def to_grad1(r):
        normal = (first_v[r] - average2) * inverse2
        value = (moved_v[r] * factor - mean - normal * cross) * inverse2
        shift_into(shifted, r, value * inside(base + r - 1))

    each_row(rows_dev + 2, to_grad1)
    sum1.send_grads(shifted)
    got_w1.wait()
    conv_taps_back(shifted, weight, acc, rows_dev)
    got_image.wait()
    average1, inverse1 = norm_of(stats_in[0], count, same[...])

    def pre_row(r):
        ok = inside(base + r)
        normal = (image_v[r].astype(F32) - average1) * inverse1 * ok
        value = acc[pl.ds(r * width, width)] * ok * silu_slope(normal * gain1[...])
        pre[r] = value
        return value, value * normal

    stats = row_stats(rows_dev, width, channels, pre_row)
    sums[2].start(stats)
    tall = text_in.shape[0]
    got_text_w = [
        fetch(text_in.at[:, j * channels : (j + 1) * channels], weight.at[j * tall : (j + 1) * tall])
        for j in range(2)
    ]
    got_side.wait()
    side.over_chips()
    got_hidden.wait()
    shift_rows()
    sum1.wait_grads()
    got_all.wait()
    grid.loop(items, lambda k: dt_copy(k).start())
    sum1.compute(0, shifted_all)
    sum1.compute(1, shifted_all)
    sum1.over_chips(0)
    sum1.compute(2, shifted_all)
    sum1.over_chips(1)
    sum1.over_chips(2)
    for a in range(3):
        sum2.over_items(a)
    side.spread()
    grid.loop(items, lambda k: dt_copy(k).wait())
    grid.loop(items, lambda k: dt_core_copy(k).start())

    stats6 = sums[2].result()
    e = embed[...].astype(F32)
    low = (e * sigmoid(e)).astype(BF16).astype(F32)
    vector[...] = jnp.zeros_like(vector)
    vector[0:1] = stats6[1:2]
    vector[1:2] = stats5[1:2] * (1.0 + scale)
    vector[2:3] = stats4[1:2]
    vector[3:4] = (stats5[1:2] * gain2[...]).astype(BF16).astype(F32)
    vector[4:5] = stats5[0:1].astype(BF16).astype(F32)
    for j in range(embed.shape[1] // channels):
        vector[5 + j : 6 + j] = low[:, j * channels : (j + 1) * channels]

    def vector_copy(k):
        return remote(
            vector, vector_land.at[item], vec_send.at[k], vec_recv.at[k], grid.peer(k)
        )

    grid.loop(items, lambda k: vector_copy(k).start())
    vector_land[item] = vector[...]

    mean, cross = means_of(stats6, gain1[...], count, same[...])

    def finish_row(r):
        normal = (image_v[r].astype(F32) - average1) * inverse1
        term = (pre[r] * gain1[...] - mean - normal * cross) * inverse1
        image_out[r] = (grad_mid[1 + r] + term) * inside(base + r)

    each_row(rows_dev, finish_row)
    put_image = fetch(image_out, image_grad)

    got_dt.wait()
    for c in got_text_w:
        c.wait()
    total = None
    for j in range(2):
        lhs = jnp.concatenate([own_dt[j * half + h] for h in range(half)], axis=1)
        term = dot(lhs, weight[j * tall : (j + 1) * tall], 1, 1)
        total = term if total is None else total + term
    text_v[...] = total
    put_text = fetch(text_v, text_grad)
    got_embed_w = [
        fetch(embed_in.at[:, j * channels : (j + 1) * channels], weight.at[j * tall : (j + 1) * tall])
        for j in range(2)
    ]
    for a in range(3):
        sum1.over_items(a)
    for a in range(3):
        sum2.wait_final(a)
    put_final2 = fetch(final.at[0], final_out.at[0])

    grid.loop(items, lambda k: dt_core_copy(k).wait())
    got_cols.wait()
    tokens = cols.shape[0] * cols.shape[1]
    flat_cols = cols[...].reshape(tokens, cols.shape[2]).astype(F32).T.astype(BF16)
    for h in range(heads):
        rhs = jnp.concatenate([dt[g, h].reshape(tokens // items, 2 * head_dim) for g in range(items)], axis=0)
        text_w_v[:, h * 2 * head_dim : (h + 1) * 2 * head_dim] = dot(flat_cols, rhs, 1, 0)
    put_text_w = fetch(text_w_v, text_w_grad)

    for c in got_embed_w:
        c.wait()
    total = None
    for j in range(2):
        lhs = vector[3 + j : 4 + j] if j else vector[3:4]
        lhs = jnp.broadcast_to(lhs, (8, channels)).astype(BF16)
        term = dot(lhs, weight[j * tall : (j + 1) * tall], 1, 1)
        total = term if total is None else total + term
    embed_v[...] = total[0:1] * silu_slope(e)
    put_embed = fetch(embed_v, embed_grad)
    grid.loop(items, lambda k: vector_copy(k).wait())
    put_vectors = fetch(vector_land, vectors)
    side.wait_final()
    put_side = fetch(side_final, side_out)
    for a in range(3):
        sum1.wait_final(a)
    put_final1 = fetch(final.at[1], final_out.at[1])
    for c in (put_image, put_text, put_final2, put_text_w, put_embed, put_vectors, put_side, put_final1):
        c.wait()


def finalize_kernel(final, side, vectors, output_in, image_in, text_in, text_w_in, embed_in,
                    output, image_grad, text_grad, text_w_grad, embed_grad, conv2, conv1, qkv, proj, embed_w,
                    gain1, gain2, gain3,
                    final_v, side_v, vector_v, conv_v, qkv_v, proj_v, embed_w_v, output_v, image_v, text_v, text_w_v,
                    embed_v, load):
    started = []

    def fetch(src, dst):
        c = pltpu.make_async_copy(src, dst, load.at[len(started)])
        c.start()
        started.append(c)
        return c

    got = [fetch(final.at[j], final_v.at[j]) for j in range(2)]
    got_vectors = fetch(vectors, vector_v)
    got_side = fetch(side, side_v)
    through = ((image_in, image_v, image_grad), (text_w_in, text_w_v, text_w_grad), (output_in, output_v, output),
               (text_in, text_v, text_grad), (embed_in, embed_v, embed_grad))
    got_through = [fetch(src, held) for src, held, _ in through]
    me = lax.axis_index("rows")
    items, rows, channels = side_v.shape[0], side_v.shape[1], side_v.shape[2] // 4
    share = items * rows
    for j, out in enumerate((conv2, conv1)):
        got[j].wait()
        for a in range(3):
            for b in range(3):
                for q in range(items):
                    conv_v[j, a * 3 + b, q * rows : (q + 1) * rows] = final_v[j, a, q, b].astype(F32)
        fetch(conv_v.at[j], out)
    for c, (_, held, dst) in zip(got_through, through):
        c.wait()
        fetch(held, dst)
    got_vectors.wait()
    total = vector_v[0]
    for g in range(1, items):
        total = total + vector_v[g]
    own = me * share
    block = channels // 4
    part = total[:, :block]
    for j in range(1, 4):
        part = jnp.where(own // block == j, total[:, j * block : (j + 1) * block], part)
    mine = part[:, :share]
    for j in range(1, block // share):
        mine = jnp.where(lax.rem(own, block) == j * share, part[:, j * share : (j + 1) * share], mine)
    for j, out in enumerate((gain1, gain2, gain3)):
        out[...] = mine[j : j + 1]
    wide = embed_w_v.shape[0]
    start = me * wide
    line = lax.broadcasted_iota(jnp.int32, (16, 1), 0)
    lhs = jnp.zeros((16, wide), F32)
    rhs = jnp.zeros((16, 2 * channels), F32)
    for g in range(items):
        row = vector_v[g, pl.ds(5 + start // channels, 1)]
        piece = row[:, :wide]
        for j in range(1, channels // wide):
            piece = jnp.where(lax.rem(start, channels) == j * wide, row[:, j * wide : (j + 1) * wide], piece)
        lhs = jnp.where(line == g, piece, lhs)
        both = jnp.concatenate([vector_v[g, 3:4], vector_v[g, 4:5]], axis=1)
        rhs = jnp.where(line == g, both, rhs)
    embed_w_v[...] = dot(lhs.astype(BF16), rhs.astype(BF16), 0, 0)
    fetch(embed_w_v, embed_w)
    got_side.wait()
    for q in range(items):
        for w in range(3):
            at = (w + 1) % 3 * share + q * rows
            qkv_v[at : at + rows] = side_v[q, :, w * channels : (w + 1) * channels].astype(F32)
        proj_v[q * rows : (q + 1) * rows] = side_v[q, :, 3 * channels :].astype(F32)
    fetch(qkv_v, qkv)
    fetch(proj_v, proj)
    for j, c in enumerate(started):
        if j > 8:
            c.wait()


def finalize_call(arrays, share):
    final, side, vectors, output, image_grad, text_grad, text_w_grad, embed_grad = arrays
    channels = output.shape[-1]
    n = channels // share
    sds = jax.ShapeDtypeStruct
    kernels = (9, share, channels)
    embed_w = (embed_grad.shape[1] // n, 2 * channels)
    outs = [sds(a.shape, a.dtype) for a in arrays[3:]]
    outs += [sds(kernels, F32)] * 2
    outs += [sds((3 * share, channels), F32), sds((share, channels), F32), sds(embed_w, F32)]
    outs += [sds((1, share), F32)] * 3
    v = pltpu.VMEM
    return pl.pallas_call(
        finalize_kernel,
        out_shape=tuple(outs),
        in_specs=[ANYWHERE] * len(arrays),
        out_specs=(ANYWHERE,) * 10 + (WHOLE,) * 3,
        scratch_shapes=[
            v(final.shape, BF16),
            v(side.shape, BF16),
            v(vectors.shape, F32),
            v((2,) + kernels, F32),
            v((3 * share, channels), F32),
            v((share, channels), F32),
            v(embed_w, F32),
            *[v(a.shape, a.dtype) for a in arrays[3:]],
            DMA((24,)),
        ],
        compiler_params=pltpu.CompilerParams(vmem_limit_bytes=62 << 20),
        name="finalize",
    )(*arrays)


def backward_call(info, embed, gains, stats, shifts, arrays, identity):
    items, n = lax.axis_size("items"), lax.axis_size("rows")
    dtext = arrays[3]
    image, text_cols, text_w = arrays[8], arrays[13], arrays[16]
    rows_dev, width, channels = image.shape
    pixels = rows_dev * width
    head_dim = channels // HEADS
    share = channels // n
    rows = share // items
    chips = n // 2
    padded = (rows_dev + 2, width, channels)
    tokens = dtext.shape[1]
    sds = jax.ShapeDtypeStruct
    outs = (
        sds(image.shape, F32),
        sds((tokens, text_w.shape[0]), F32),
        sds((text_w.shape[0] // n, 2 * channels), F32),
        sds(embed.shape, F32),
        sds((2, 3, items, 3, rows, channels), BF16),
        sds((items, rows, 4 * channels), BF16),
        sds((items, 16, channels), F32),
    )
    v = pltpu.VMEM
    scratch = [
        v((9 * channels, channels), BF16),
        v((3 * channels, channels), BF16),
        v(padded, F32),
        v(padded, F32),
        v(padded, BF16),
        v(image.shape, BF16),
        v((pixels, channels), BF16),
        v(text_cols.shape, BF16),
        v((items,) + padded, BF16),
        v((n, 2 * head_dim, pixels), BF16),
        v((items, n) + dtext.shape, BF16),
        v(dtext.shape, BF16),
        v(padded, F32),
        v(padded, F32),
        v(padded, F32),
        v(image.shape, F32),
        v((pixels, channels), F32),
        v((rows_dev + 2, width, 3 * channels), BF16),
        v((items, rows_dev + 2, width, 3 * channels), BF16),
        v(image.shape, F32),
        v((tokens, text_w.shape[0]), F32),
        v((text_w.shape[0] // n, 2 * channels), F32),
        v(embed.shape, F32),
        v((channels, channels), BF16),
        v((2, items, channels // items, pixels), BF16),
        v((2, items, channels // items, pixels), BF16),
        v((2, 3, 2, 3, chips * rows, channels), BF16),
        v((2, 3, 3, chips * rows, channels), BF16),
        v((2, 3, chips, 3, rows, channels), BF16),
        v((2, 3, chips, 3, rows, channels), BF16),
        v((2, 3, items, 3, rows, channels), BF16),
        v((2, chips, items, rows, 2 * channels), BF16),
        v((chips, items, rows, 2 * channels), BF16),
        v((items, chips, rows, 2 * channels), BF16),
        v((items, chips, rows, 2 * channels), BF16),
        v((chips, rows, 4 * channels), BF16),
        v((chips, rows, 4 * channels), BF16),
        v((items, rows, 4 * channels), BF16),
        v((16, channels), F32),
        v((items, 16, channels), F32),
        v((3, channels // 64, 128), F32),
        v((3, n, channels // 64, 128), F32),
        DMA((32,)),
        DMA((3, n)),
        DMA((3, n)),
        DMA((2, 2)),
        DMA((2, 2)),
        DMA((items,)),
        DMA((items,)),
        DMA((items,)),
        DMA((items,)),
        DMA((items,)),
        DMA((items,)),
        DMA((2, items)),
        DMA((2, items)),
        DMA((2, 3)),
        DMA((2, 3)),
        DMA((2, 3, chips)),
        DMA((2, 3, chips)),
        DMA((2, 3, items)),
        DMA((2, 3, items)),
        DMA((1,)),
        DMA((1,)),
        DMA((items,)),
        DMA((items,)),
        DMA((chips,)),
        DMA((chips,)),
        DMA((items,)),
        DMA((items,)),
    ]
    return pl.pallas_call(
        functools.partial(backward_kernel, items, n),
        out_shape=outs,
        in_specs=[SCALARS] + [WHOLE] * 6 + [ANYWHERE] * len(arrays),
        out_specs=(ANYWHERE,) * 7,
        scratch_shapes=scratch,
        compiler_params=pltpu.CompilerParams(
            collective_id=identity, has_side_effects=True, vmem_limit_bytes=62 << 20
        ),
        cost_estimate=pl.CostEstimate(
            flops=80 * pixels * channels * channels, bytes_accessed=60 << 20, transcendentals=0
        ),
        name="backward",
    )(info, embed, *gains, stats, shifts, *arrays)


def own_shards(
    extent, image, embed, text, gain1, conv1_w, embed_w, gain2, conv2_w, gain3, qkv_w, text_w, proj_w,
    cotangent,
):
    _, rows_dev, width, channels = image.shape
    items, parts = lax.axis_size("items"), lax.axis_size("rows")
    me = lax.axis_index("rows")
    head_dim = channels // HEADS
    tokens = text.shape[1]
    share = channels // parts
    (first, middle, cot, hidden_all, second_all, attn_flat, qkv_turned, output, query_part, side_part, dkv, own_dt,
     all_dt, text_cols, stats, shifts) = forward_call(
        extent,
        image[0],
        cotangent[0],
        text[0],
        embed,
        (gain1, gain2, gain3),
        (
            conv1_w.reshape(3, 3 * channels, channels),
            conv2_w.reshape(3, 3 * channels, channels),
            embed_w,
            text_w,
            qkv_w,
            proj_w,
        ),
        0,
    )
    text_w_rows = text_cols.shape[3]
    image_grad, text_grad, text_w_grad, embed_grad, final, side, vectors = backward_call(
        extent,
        embed,
        (gain1, gain2, gain3),
        stats,
        shifts,
        (
            query_part,
            side_part,
            dkv,
            own_dt,
            all_dt,
            first,
            middle,
            cot,
            image[0],
            hidden_all,
            second_all,
            attn_flat,
            qkv_turned,
            text_cols.reshape(items * parts, tokens, text_w_rows),
            conv1_w.reshape(9 * channels, channels),
            conv2_w.reshape(9 * channels, channels),
            text_w,
            embed_w,
        ),
        1,
    )
    (output, image_grad, text_grad, text_w_grad, embed_grad, conv2, conv1, qkv, proj, embed_w_grad, norm1, norm2,
     norm3) = finalize_call(
        (final, side, vectors, output, image_grad, text_grad, text_w_grad, embed_grad), share
    )

    def kernel(values):
        return jnp.swapaxes(values.reshape(3, 3, share, channels), 2, 3)

    return (
        output[None],
        image_grad[None],
        embed_grad,
        text_grad[None],
        norm1[0],
        kernel(conv1),
        embed_w_grad,
        norm2[0],
        kernel(conv2),
        norm3[0],
        qkv.T,
        text_w_grad,
        proj.T,
    )


def shards(
    image, embed, text, extent, first_norm_gain1, conv1_w, embed_w, second_norm_gain2, conv2_w,
    attention_norm_gain, qkv_w, text_w, proj_w, cotangent,
):
    images, rows_dev, width, channels = image.shape
    parts = lax.axis_size("rows")
    me = lax.axis_index("rows")
    pairs = images * HEADS // parts
    head_dim = channels // HEADS
    pixels = rows_dev * width
    group = max(1, 512 // pixels)
    span = group * pixels
    chunks = parts // group
    tokens = text.shape[1]
    first_row = jnp.full((images, 1), me * rows_dev, jnp.int32)
    info = jnp.concatenate([extent, first_row], axis=1)
    gain1 = first_norm_gain1.reshape(1, channels)
    gain2 = second_norm_gain2.reshape(1, channels)
    gain3 = attention_norm_gain.reshape(1, channels)
    rowpos = me * rows_dev + jnp.arange(rows_dev, dtype=jnp.int32)
    colpos = jnp.arange(width, dtype=jnp.int32)
    inside = (rowpos[None, :, None] < extent[:, 0, None, None]) & (
        colpos[None, None, :] < extent[:, 1, None, None]
    )
    image_window = inside.astype(F32)[..., None]

    items = lax.axis_size("items")
    own_path = (
        images == 1
        and parts == HEADS
        and channels % (16 * items * parts) == 0
        and pixels % 512 == 0
        and channels % 512 == 0
        and tokens % 16 == 0
        and text.shape[2] % (128 * parts) == 0
        and text.shape[2] == embed.shape[1] <= 4 * channels
    )
    if own_path:
        return own_shards(
            extent, image, embed, text, gain1, conv1_w, embed_w, gain2, conv2_w, gain3, qkv_w, text_w,
            proj_w, cotangent,
        )

    embed_float = embed.astype(F32)
    embed_low = jax.nn.silu(embed_float).astype(BF16)
    shifts = jnp.dot(embed_low, embed_w, preferred_element_type=F32)
    qkv_turned = qkv_w.T
    proj_shaped = proj_w.reshape(HEADS, head_dim, channels)

    start = image.astype(F32) * image_window
    zeros = jnp.zeros((images, 6, channels), F32)
    stats0 = jnp.concatenate(
        [
            jnp.sum(start, axis=(1, 2))[:, None],
            jnp.sum(start * start, axis=(1, 2))[:, None],
            zeros,
        ],
        axis=1,
    )
    stats1, image_above, image_below, cot_above, cot_below = exchange(
        stats0, (image, cotangent), 0
    )
    full = jax.ShapeDtypeStruct(image.shape, F32)
    sums = jax.ShapeDtypeStruct((images, 8, channels), F32)
    padded = jax.ShapeDtypeStruct((images, rows_dev + 2, width, channels), BF16)
    first, stats, hidden = conv_call(
        conv1_kernel,
        info,
        (image, image_above, image_below, stats1, gain1),
        conv1_w,
        (full, sums, padded),
        False,
    )
    stats2, first_above, first_below, all_text = exchange(stats, (first,), 1, (text,))
    gathered_text = jnp.moveaxis(all_text, 0, 1).reshape(images, parts * tokens, text.shape[2])
    text_share = text.shape[2] // parts
    text_cols = lax.dynamic_slice_in_dim(gathered_text, me * text_share, text_share, 2)
    text_cols = lax.all_gather(text_cols, "items", axis=0, tiled=True)
    middle, stats, second = conv_call(
        conv2_kernel,
        info,
        (first, first_above, first_below, stats2, gain2, shifts, image),
        conv2_w,
        (full, sums, padded),
        False,
    )
    stats3, mid_above, mid_below = exchange(stats, (middle,), 2)
    attn_flat, qkv_pix = project(info, middle, stats3, gain3, qkv_turned)

    def to_pairs(values):
        wide = values.shape[1]
        moved = lax.all_to_all(values, "rows", split_axis=0, concat_axis=0, tiled=True)
        moved = moved.reshape(chunks, group, pairs, wide, pixels)
        return jnp.transpose(moved, (2, 0, 3, 1, 4)).reshape(pairs, chunks, wide, span)

    def from_pairs(values):
        wide = values.shape[2]
        moved = values.reshape(pairs, chunks, wide, group, pixels)
        moved = jnp.transpose(moved, (1, 3, 0, 2, 4)).reshape(parts * pairs, wide, pixels)
        return lax.all_to_all(moved, "rows", split_axis=0, concat_axis=0, tiled=True)

    qkv_pair = to_pairs(qkv_pix)
    grad_proj = (cotangent.astype(F32) * image_window).astype(BF16).reshape(images, pixels, channels)
    grad_heads = jnp.einsum(
        "ipc,hdc->ihdp", grad_proj, proj_shaped, preferred_element_type=F32
    ).astype(BF16)
    grad_pair = to_pairs(grad_heads.reshape(images * HEADS, head_dim, pixels))
    pair_results = []
    for p in range(pairs):
        pair = me * pairs + p
        item, head = pair // HEADS, pair % HEADS
        weight = lax.dynamic_slice_in_dim(text_w, head * 2 * head_dim, 2 * head_dim, 1)
        own = lax.dynamic_index_in_dim(gathered_text, item, 0, False)
        text_pair = jnp.dot(own, weight, preferred_element_type=F32).astype(BF16)
        pair_extent = lax.dynamic_slice_in_dim(extent, item, 1, 0)
        pair_results.append(attention(pair_extent, qkv_pair[p], text_pair, grad_pair[p], width))
    attended, qkv_grad_pair, text_grad_pair = (jnp.stack(r) for r in zip(*pair_results))
    qkv_back = from_pairs(qkv_grad_pair)
    heads_out = from_pairs(attended).reshape(images, HEADS, head_dim, pixels)

    attn_grad, stats = unproject(info, middle, stats3, qkv_back, qkv_turned)
    stats4, grad_above, grad_below, text_back = exchange(stats, (attn_grad,), 3, (text_grad_pair,))
    text_back = text_back.reshape(images, HEADS, parts * tokens, 2 * head_dim)
    text_all = lax.all_gather(text_back, "items", axis=0, tiled=True)
    proj_grad = jnp.einsum("ipc,ihdp->chd", grad_proj, heads_out, preferred_element_type=F32)
    qkv_grad = jnp.einsum(
        "ihwdp,ipc->hdwc",
        qkv_back.reshape(images, HEADS, 3, head_dim, pixels),
        attn_flat,
        preferred_element_type=F32,
    )
    grad_middle, moved_grad, stats, conv2_grad = conv_call(
        back2_kernel,
        info,
        (attn_grad, grad_above, grad_below, middle, mid_above, mid_below, cotangent, cot_above,
         cot_below, stats3, stats4, gain3, first, stats2, gain2, shifts),
        conv2_w,
        (full, full, sums, padded),
        True,
    )
    stats5, moved_above, moved_below = exchange(stats, (moved_grad,), 4)
    pre_grad, stats, conv1_grad = conv_call(
        back1_kernel,
        info,
        (moved_grad, moved_above, moved_below, first, first_above, first_below, stats2, stats5,
         gain2, shifts, image, stats1, gain1),
        conv1_w,
        (full, sums, padded),
        True,
    )
    (stats6,) = exchange(stats, (), 5)
    image_grad = finish(info, pre_grad, stats6, image, stats1, gain1, grad_middle)

    projected = jnp.einsum(
        "ihdp,hdc->ipc", heads_out, proj_shaped, preferred_element_type=F32
    ).reshape(image.shape)
    output = (middle + projected * image_window).astype(BF16)
    own_text = lax.dynamic_slice_in_dim(text_back, me * tokens, tokens, 2)
    text_shaped = text_w.reshape(text_w.shape[0], HEADS, 2 * head_dim)
    text_grad = jnp.einsum("ihtk,chk->itc", own_text, text_shaped, preferred_element_type=F32)
    text_w_grad = jnp.einsum(
        "gtc,ghtk->chk", text_cols, text_all, preferred_element_type=F32
    ).reshape(text_share, 2 * channels)
    scale_sum = stats5[:, 1] * gain2
    grad_shifts = jnp.concatenate([scale_sum, stats5[:, 0]], axis=1).astype(BF16)
    embed_grad = jnp.einsum(
        "ik,ck->ic", grad_shifts, embed_w, preferred_element_type=F32
    ) * silu_slope(embed_float)
    embed_share = embed_w.shape[0] // parts
    gains = jnp.stack(
        [
            jnp.sum(stats6[:, 1], axis=0),
            jnp.sum(stats5[:, 1] * (1.0 + shifts[:, :channels]), axis=0),
            jnp.sum(stats4[:, 1], axis=0),
        ]
    )
    share = channels // parts
    def total(values):
        return lax.psum(
            lax.psum_scatter(values.astype(BF16), "rows", scatter_dimension=0, tiled=True),
            "items",
        ).astype(F32)

    def kernel_total(values):
        return total(values).T.reshape(3, 3, channels, share)

    conv1_total = kernel_total(weight_grad(conv1_grad, hidden))
    conv2_total = kernel_total(weight_grad(conv2_grad, second))
    by_head = jnp.swapaxes(qkv_grad, 1, 2).reshape(3 * channels, channels)
    qkv_total = total(by_head).T
    proj_total = total(proj_grad.reshape(channels, channels)).T
    gains = lax.psum(gains, "items")
    all_shifts = lax.all_gather(grad_shifts, "items", axis=0, tiled=True)
    embed_rows = lax.dynamic_slice_in_dim(embed_low, me * embed_share, embed_share, 1)
    embed_rows = lax.all_gather(embed_rows, "items", axis=0, tiled=True)
    embed_w_grad = jnp.einsum("ic,ik->ck", embed_rows, all_shifts, preferred_element_type=F32)
    gains = lax.dynamic_slice_in_dim(gains, me * share, share, 1)
    return (
        output,
        image_grad,
        embed_grad,
        text_grad,
        gains[0],
        conv1_total,
        embed_w_grad,
        gains[1],
        conv2_total,
        gains[2],
        qkv_total,
        text_w_grad,
        proj_total,
    )


def solution(mesh):
    in_specs = (
        P("items", "rows", None, None),
        P("items", None),
        P("items", "rows", None),
        P("items", None),
        P(),
        P(),
        P(),
        P(),
        P(),
        P(),
        P(),
        P(),
        P(),
        P("items", "rows", None, None),
    )
    out_specs = (
        P("items", "rows", None, None),
        P("items", "rows", None, None),
        P("items", None),
        P("items", "rows", None),
        P("rows"),
        P(None, None, None, "rows"),
        P("rows", None),
        P("rows"),
        P(None, None, None, "rows"),
        P("rows"),
        P(None, "rows"),
        P("rows", None),
        P(None, "rows"),
    )
    return jax.shard_map(shards, mesh=mesh, in_specs=in_specs, out_specs=out_specs, check_vma=False)
```

```python
import functools

import jax
import jax.numpy as jnp
from jax import lax
from jax.experimental import pallas as pl
from jax.experimental.pallas import tpu as pltpu
from jax.sharding import PartitionSpec as P

GROUPS = 32
HEADS = 8
F32, BF16 = jnp.float32, jnp.bfloat16
NEG = -1e30


def dot(a, b, ca, cb):
    return lax.dot_general(a, b, (((ca,), (cb,)), ((), ())), preferred_element_type=F32)

def nothing(*_):
    return None


class Attention:
    def __init__(self, chunks, span, d, tlen, step, bq, scratch):
        self.chunks, self.span, self.d, self.tlen, self.step, self.bq = chunks, span, d, tlen, step, bq
        self.kn, self.vn, self.kt, self.vt, s0, s1, e0, e1, self.dkt, self.dvt = scratch
        self.scores, self.raised = (s0, s1), (e0, e1)
        self.pix = chunks * span

    def stage_key(self, c, k, width, rows_ok, cols_ok):
        d, span = self.d, self.span
        base = pl.multiple_of(c * span, span)
        pos = base + lax.broadcasted_iota(jnp.int32, (16, span), 1)
        row = lax.broadcasted_iota(jnp.int32, (16, span), 0)
        ok = (pos // width < rows_ok) & (pos % width < cols_ok)
        extra = jnp.where((row == 0) & jnp.logical_not(ok), NEG, 0.0)
        rest = jnp.zeros((128 - d - 16, span), F32)
        self.kt[:, pl.ds(base, span)] = k
        ka = jnp.concatenate([k.astype(F32), extra, rest], axis=0)
        self.kn[pl.ds(base, span), :] = ka.T.astype(BF16)

    def stage_value(self, c, v):
        d, span = self.d, self.span
        base = pl.multiple_of(c * span, span)
        row = lax.broadcasted_iota(jnp.int32, (16, span), 0)
        rest = jnp.zeros((128 - d - 16, span), F32)
        self.vt[:, pl.ds(base, span)] = v
        va = jnp.concatenate([v.astype(F32), jnp.where(row < 3, 1.0, 0.0), rest], axis=0)
        self.vn[pl.ds(base, span), :] = va.T.astype(BF16)

    def stage_text(self, text):
        d, tlen, pix = self.d, self.tlen, self.pix
        tk = text[:, :d].astype(F32)
        tv = text[:, d:].astype(F32)
        self.kt[:, pix:] = tk.T.astype(BF16)
        self.vt[:, pix:] = tv.T.astype(BF16)
        lanes = lax.broadcasted_iota(jnp.int32, (tlen, 128 - d), 1)
        rest = jnp.zeros((tlen, 128 - d), F32)
        self.kn[pix:, :] = jnp.concatenate([tk, rest], axis=1).astype(BF16)
        ones = jnp.where(lanes < 3, 1.0, 0.0)
        self.vn[pix:, :] = jnp.concatenate([tv, ones], axis=1).astype(BF16)

    def query(self, q):
        d, bq = self.d, self.bq
        r = lax.broadcasted_iota(jnp.int32, (128 - d, bq), 0)
        rest = jnp.where(r == 0, 1.0, 0.0)
        return jnp.concatenate([q.astype(F32) * (d**-0.5), rest], axis=0).astype(BF16)

    def run(self, score, exp, back):
        d, bq, step = self.d, self.bq, self.step
        kn, vn, kt, vt, dkt, dvt = self.kn, self.vn, self.kt, self.vt, self.dkt, self.dvt
        scores, raised = self.scores, self.raised

        def body(j, carry):
            pk, total, acc, dq = carry
            at = pl.ds(pl.multiple_of(j * step, step), step)
            if score:
                slot, qa = score
                s = dot(kn[at, :], qa, 1, 0)
                scores[slot][at, :] = s
                pk = jnp.maximum(pk, jnp.max(s.reshape(step // 8, 8, bq), axis=0))
            if exp:
                slot, peak = exp
                e = jnp.exp(scores[slot][at, :] - peak)
                total = total + jnp.sum(e.reshape(step // 8, 8, bq), axis=0)
                low = e.astype(BF16)
                raised[slot][at, :] = low
                acc = acc + dot(vt[:, at], low, 1, 0)
            if back:
                slot, goa, q = back
                dp = dot(vn[at, :], goa, 1, 0)
                e = raised[slot][at, :]
                ds = (e.astype(F32) * dp).astype(BF16)
                dvt[:, at] += dot(goa[:d], e, 1, 1)
                dkt[:, at] += dot(q, ds, 1, 1)
                dq = dq + dot(kt[:, at], ds, 1, 0)
            return pk, total, acc, dq

        init = (
            jnp.full((8, bq), -3e38, F32),
            jnp.zeros((8, bq), F32),
            jnp.zeros((d, bq), F32),
            jnp.zeros((d, bq), F32),
        )
        return lax.fori_loop(0, (self.pix + self.tlen) // step, body, init)

    def attended(self, go, total, acc):
        d, bq = self.d, self.bq
        inv = 1.0 / jnp.sum(total, axis=0, keepdims=True)
        o = acc * inv
        go = go.astype(F32)
        nd = -jnp.sum(go * o, axis=0, keepdims=True) * inv
        hi = nd.astype(BF16).astype(F32)
        mid = (nd - hi).astype(BF16).astype(F32)
        lo = nd - hi - mid
        r = lax.broadcasted_iota(jnp.int32, (16, bq), 0)
        extra = jnp.where(r == 0, hi, jnp.where(r == 1, mid, jnp.where(r == 2, lo, 0.0)))
        rest = jnp.zeros((128 - d - 16, bq), F32)
        return o.astype(BF16), jnp.concatenate([go * inv, extra, rest], axis=0).astype(BF16)

    def attend(self, q_ref, go_ref, o_ref, dq_ref, order, before=nothing, done=nothing):
        d, bq, chunks = self.d, self.bq, self.chunks
        self.dkt[...] = jnp.zeros_like(self.dkt)
        self.dvt[...] = jnp.zeros_like(self.dvt)

        def columns(half):
            return slice(half * bq, (half + 1) * bq)

        def q_of(h, half):
            return q_ref[order(h), :d, columns(half)]

        def finish_exp(h, half, total, acc):
            c = order(h)
            o, goa = self.attended(go_ref[c, :, columns(half)], total, acc)
            o_ref[c, :, columns(half)] = o
            return goa

        def put_dq(h, half, dq):
            dq_ref[order(h), :d, columns(half)] = (dq * (d**-0.5)).astype(BF16)

        def top(pk):
            return jnp.max(pk, axis=0, keepdims=True)

        run = self.run
        pk, _, _, _ = run((0, self.query(q_of(0, 0))), None, None)
        pk, total, acc, _ = run((1, self.query(q_of(0, 1))), (0, top(pk)), None)
        goa = finish_exp(0, 0, total, acc)

        def two(h, carry):
            pk, goa = carry
            before(h + 1)
            qa = self.query(q_of(h + 1, 0))
            pk2, total, acc, dq = run((0, qa), (1, top(pk)), (0, goa, q_of(h, 0)))
            put_dq(h, 0, dq)
            goa = finish_exp(h, 1, total, acc)
            qa = self.query(q_of(h + 1, 1))
            pk3, total, acc, dq = run((1, qa), (0, top(pk2)), (1, goa, q_of(h, 1)))
            put_dq(h, 1, dq)
            done(h)
            return pk3, finish_exp(h + 1, 0, total, acc)

        pk, goa = lax.fori_loop(0, chunks - 1, two, (pk, goa))
        last = chunks - 1
        _, total, acc, dq = run(None, (1, top(pk)), (0, goa, q_of(last, 0)))
        put_dq(last, 0, dq)
        goa = finish_exp(last, 1, total, acc)
        _, _, _, dq = run(None, None, (1, goa, q_of(last, 1)))
        put_dq(last, 1, dq)
        done(last)

    def key_grad(self, at):
        return (self.dkt[:, at] * (self.d**-0.5)).astype(BF16)

    def value_grad(self, at):
        return self.dvt[:, at].astype(BF16)

    def text_grad(self, out):
        d, pix = self.d, self.pix
        out[:, :d] = (self.dkt[:, pix:] * (d**-0.5)).T.astype(BF16)
        out[:, d:] = self.dvt[:, pix:].T.astype(BF16)


def attention_scratch(chunks, span, d, tlen):
    keys = chunks * span + tlen
    bq = span // 2
    lanes = keys // 128
    step = 128 * max(n for n in range(1, 12) if lanes % n == 0)
    shapes = [((keys, 128), BF16)] * 2 + [((d, keys), BF16)] * 2
    shapes += [((keys, bq), F32)] * 2 + [((keys, bq), BF16)] * 2 + [((d, keys), F32)] * 2
    return step, bq, [pltpu.VMEM(*shape) for shape in shapes]


def attention_kernel(width, step, bq, ext_ref, qkv_ref, text_ref, go_ref, out_ref, dqkv_ref, dtext_ref, *scratch):
    chunks, _, span = qkv_ref.shape
    d = go_ref.shape[1]
    att = Attention(chunks, span, d, text_ref.shape[0], step, bq, scratch)

    def stage(c, carry):
        att.stage_key(c, qkv_ref[c, d : 2 * d, :], width, ext_ref[0, 0], ext_ref[0, 1])
        att.stage_value(c, qkv_ref[c, 2 * d :, :])
        return carry

    lax.fori_loop(0, chunks, stage, 0)
    att.stage_text(text_ref)
    att.attend(qkv_ref, go_ref, out_ref, dqkv_ref, lambda h: h)

    def finish(c, carry):
        at = pl.ds(pl.multiple_of(c * span, span), span)
        dqkv_ref[c, d : 2 * d, :] = att.key_grad(at)
        dqkv_ref[c, 2 * d :, :] = att.value_grad(at)
        return carry

    lax.fori_loop(0, chunks, finish, 0)
    att.text_grad(dtext_ref)


def attention(ext, qkv, text, go, width):
    chunks, wide, span = qkv.shape
    d = wide // 3
    tlen = text.shape[0]
    keys = chunks * span + tlen
    step, bq, scratch = attention_scratch(chunks, span, d, tlen)
    vm = pl.BlockSpec(memory_space=pltpu.VMEM)
    flops = 2 * 6 * chunks * span * keys * d
    return pl.pallas_call(
        functools.partial(attention_kernel, width, step, bq),
        out_shape=(
            jax.ShapeDtypeStruct(go.shape, BF16),
            jax.ShapeDtypeStruct(qkv.shape, BF16),
            jax.ShapeDtypeStruct((tlen, 2 * d), BF16),
        ),
        in_specs=[pl.BlockSpec(memory_space=pltpu.SMEM), vm, vm, vm],
        out_specs=(vm, vm, vm),
        scratch_shapes=scratch,
        compiler_params=pltpu.CompilerParams(vmem_limit_bytes=56 << 20),
        cost_estimate=pl.CostEstimate(
            flops=4 * flops, bytes_accessed=16 * chunks * span * d, transcendentals=chunks * span * keys
        ),
    )(ext, qkv, text, go)


MESH = pl.DeviceIdType.MESH
EPS = 1e-05
WHOLE = pl.BlockSpec(memory_space=pltpu.VMEM)
SCALARS = pl.BlockSpec(memory_space=pltpu.SMEM)
ANYWHERE = pl.BlockSpec(memory_space=pl.ANY)


def exchange_kernel(n, count, gathers, *refs):
    inputs, refs = refs[: 1 + count + gathers], refs[1 + count + gathers :]
    outputs, refs = refs[: 1 + 2 * count + gathers], refs[1 + 2 * count + gathers :]
    stats_ref, rows, given = inputs[0], inputs[1 : 1 + count], inputs[1 + count :]
    total_ref, outs, gathered = outputs[0], outputs[1 : 1 + 2 * count], outputs[1 + 2 * count :]
    slots, lands = refs[0], refs[1 : 1 + 2 * count]
    send, recv, row_send, row_recv, own = refs[1 + 2 * count :]
    me = lax.axis_index("rows")
    barrier = pltpu.get_barrier_semaphore()

    def greet(k, carry):
        pl.semaphore_signal(
            barrier, inc=1, device_id={"rows": lax.rem(me + k, n)}, device_id_type=MESH
        )
        return carry

    lax.fori_loop(1, n, greet, 0)
    slots[me] = stats_ref[...]
    pl.semaphore_wait(barrier, n - 1)
    shared = [(stats_ref, slots)] + list(zip(given, gathered))

    def share(j, k):
        return pltpu.make_async_remote_copy(
            src_ref=shared[j][0],
            dst_ref=shared[j][1].at[me],
            send_sem=send.at[j, k],
            recv_sem=recv.at[j, k],
            device_id={"rows": lax.rem(me + k, n)},
            device_id_type=MESH,
        )

    def start(k, carry):
        share(0, k).start()
        return carry

    lax.fori_loop(1, n, start, 0)

    def row_copy(j, side):
        last = rows[j].shape[1] - 1
        at = last if side == 0 else 0
        return pltpu.make_async_remote_copy(
            src_ref=rows[j].at[:, at : at + 1],
            dst_ref=lands[2 * j + side],
            send_sem=row_send.at[2 * j + side],
            recv_sem=row_recv.at[2 * j + side],
            device_id={"rows": me + 1 if side == 0 else me - 1},
            device_id_type=MESH,
        )

    for j in range(count):

        @pl.when(me < n - 1)
        def _():
            row_copy(j, 0).start()

        @pl.when(me > 0)
        def _():
            row_copy(j, 1).start()

    for j in range(gathers):

        def start_given(k, carry):
            share(1 + j, k).start()
            return carry

        lax.fori_loop(1, n, start_given, 0)
        pltpu.make_async_copy(given[j], gathered[j].at[me], own.at[j]).start()

    def finish(k, carry):
        share(0, k).wait()
        return carry

    lax.fori_loop(1, n, finish, 0)
    total_ref[...] = lax.fori_loop(1, n, lambda k, s: s + slots[k], slots[0])
    for j in range(count):

        @pl.when(me > 0)
        def _():
            row_copy(j, 0).wait_recv()
            outs[2 * j][...] = lands[2 * j][...]

        @pl.when(me == 0)
        def _():
            outs[2 * j][...] = jnp.zeros_like(outs[2 * j])

        @pl.when(me < n - 1)
        def _():
            row_copy(j, 1).wait_recv()
            outs[2 * j + 1][...] = lands[2 * j + 1][...]
            row_copy(j, 0).wait_send()

        @pl.when(me == n - 1)
        def _():
            outs[2 * j + 1][...] = jnp.zeros_like(outs[2 * j + 1])

        @pl.when(me > 0)
        def _():
            row_copy(j, 1).wait_send()

    for j in range(gathers):

        def finish_given(k, carry):
            share(1 + j, k).wait()
            return carry

        lax.fori_loop(1, n, finish_given, 0)
        pltpu.make_async_copy(given[j], gathered[j].at[me], own.at[j]).wait()


def exchange(stats, rows, identity, given=()):
    n = lax.axis_size("rows")
    edge = []
    for array in rows:
        edge += [jax.ShapeDtypeStruct(array.shape[:1] + (1,) + array.shape[2:], array.dtype)] * 2
    whole = [jax.ShapeDtypeStruct((n,) + array.shape, array.dtype) for array in given]
    count, gathers = len(rows), len(given)
    nbytes = 4 * stats.size * n + sum(2 * e.size * e.dtype.itemsize for e in (*edge, *whole))
    return pl.pallas_call(
        functools.partial(exchange_kernel, n, count, gathers),
        out_shape=(jax.ShapeDtypeStruct(stats.shape, F32), *edge, *whole),
        in_specs=[WHOLE] + [ANYWHERE] * (count + gathers),
        out_specs=(WHOLE,) * (1 + 2 * count) + (ANYWHERE,) * gathers,
        scratch_shapes=[
            pltpu.VMEM((n,) + stats.shape, F32),
            *[pltpu.VMEM(e.shape, e.dtype) for e in edge],
            pltpu.SemaphoreType.DMA((1 + gathers, n)),
            pltpu.SemaphoreType.DMA((1 + gathers, n)),
            pltpu.SemaphoreType.DMA((max(1, 2 * count),)),
            pltpu.SemaphoreType.DMA((max(1, 2 * count),)),
            pltpu.SemaphoreType.DMA((max(1, gathers),)),
        ],
        compiler_params=pltpu.CompilerParams(collective_id=identity, has_side_effects=True),
        cost_estimate=pl.CostEstimate(
            flops=6_000_000_000, bytes_accessed=nbytes, transcendentals=0
        ),
        name=f"exchange{identity}",
    )(stats, *rows, *given)


def group_matrix(channels):
    size = channels // GROUPS
    one = lax.broadcasted_iota(jnp.int32, (channels, channels), 0) // size
    two = lax.broadcasted_iota(jnp.int32, (channels, channels), 1) // size
    return jnp.where(one == two, 1.0, 0.0).astype(BF16)


def group_sums(rows, same=None):
    if same is None:
        same = group_matrix(rows.shape[1])
    high = rows.astype(BF16).astype(F32)
    mid = (rows - high).astype(BF16).astype(F32)
    tail = rows - high - mid
    sums = dot(jnp.concatenate([high, mid, tail], axis=0).astype(BF16), same, 1, 0)
    n = rows.shape[0]
    return sums[:n] + sums[n : 2 * n] + sums[2 * n :]


def image_count(info, i, channels):
    return (info[i, 0] * info[i, 1]).astype(F32) * (channels // GROUPS)


def norm_of(stats, count, same=None):
    sums = group_sums(stats, same)
    average = sums[0:1] / count
    square = sums[1:2] / count
    return average, lax.rsqrt(square - average * average + EPS)


def means_of(stats, weight, count, same=None):
    sums = group_sums(stats * weight, same)
    return sums[0:1] / count, sums[1:2] / count


def window(info, i, row, shape):
    ok = (row >= 0) & (row < info[i, 0])
    limit = jnp.where(ok, info[i, 1], 0)
    return jnp.where(lax.broadcasted_iota(jnp.int32, shape, 0) < limit, 1.0, 0.0)


def padded_row(center, above, below, i, r):
    if r == 0:
        return above[i, 0]
    if r == center.shape[1] + 1:
        return below[i, 0]
    return center[i, r - 1]


def put_shifted(out, i, r, value, plain=None):
    width, channels = value.shape
    column = lax.broadcasted_iota(jnp.int32, value.shape, 0)
    left = jnp.where(column == 0, 0.0, pltpu.roll(value, 1, 0))
    right = jnp.where(column == width - 1, 0.0, pltpu.roll(value, width - 1, 0))
    out[i, r, :, :channels] = left.astype(BF16)
    low = value.astype(BF16)
    out[i, r, :, channels : 2 * channels] = low
    if plain is not None:
        plain[i, r] = low
    out[i, r, :, 2 * channels :] = right.astype(BF16)


def sigmoid(v):
    return 1.0 / (1.0 + jnp.exp(-v))


def silu_slope(v):
    s = sigmoid(v)
    return s * (1.0 + v * (1.0 - s))


def put_stats(stats_ref, i, first, second):
    channels = first.shape[1]
    one = jnp.sum(first, axis=0, keepdims=True)
    two = jnp.sum(second, axis=0, keepdims=True)
    row = lax.broadcasted_iota(jnp.int32, (8, channels), 0)
    stats_ref[i] = jnp.where(row == 0, one, jnp.where(row == 1, two, 0.0))


def tap_rows(shifted, tap, images, rows_dev, width):
    block = shifted[:, pl.ds(tap, rows_dev)]
    return block.reshape(images * rows_dev * width, shifted.shape[3])


def conv1_kernel(info, image, above, below, stats, gain, weight, first, out_stats, hidden, acc, shifted):
    images, rows_dev, width, channels = image.shape
    tap = pl.program_id(0)
    base = info[0, 2]

    @pl.when(tap == 0)
    def _():
        for i in range(images):
            average, inverse = norm_of(stats[i], image_count(info, i, channels))
            for r in range(rows_dev + 2):
                inside = window(info, i, base + r - 1, (width, channels))
                start = padded_row(image, above, below, i, r).astype(F32) * inside
                value = (start - average) * inverse * inside * gain[...]
                put_shifted(shifted, i, r, value * sigmoid(value) * inside, hidden)

    part = dot(tap_rows(shifted, tap, images, rows_dev, width), weight[0], 1, 0)

    @pl.when(tap == 0)
    def _():
        acc[...] = part

    @pl.when(tap > 0)
    def _():
        acc[...] += part

    @pl.when(tap == 2)
    def _():
        for i in range(images):
            one = two = jnp.zeros((width, channels), F32)
            for r in range(rows_dev):
                inside = window(info, i, base + r, (width, channels))
                at = (i * rows_dev + r) * width
                value = acc[at : at + width] * inside
                first[i, r] = value
                one = one + value
                two = two + value * value
            put_stats(out_stats, i, one, two)


def moved_of(value, inside, average, inverse, gain, scale, shift):
    normal = (value - average) * inverse * inside
    return normal, normal * gain * (1.0 + scale) + shift


def conv2_kernel(
    info, first, above, below, stats, gain, shifts, image, weight, middle, out_stats, second, acc,
    shifted,
):
    images, rows_dev, width, channels = first.shape
    tap = pl.program_id(0)
    base = info[0, 2]

    @pl.when(tap == 0)
    def _():
        for i in range(images):
            average, inverse = norm_of(stats[i], image_count(info, i, channels))
            scale, shift = shifts[i : i + 1, :channels], shifts[i : i + 1, channels:]
            for r in range(rows_dev + 2):
                inside = window(info, i, base + r - 1, (width, channels))
                value = padded_row(first, above, below, i, r)
                _, moved = moved_of(value, inside, average, inverse, gain[...], scale, shift)
                put_shifted(shifted, i, r, moved * sigmoid(moved) * inside, second)

    part = dot(tap_rows(shifted, tap, images, rows_dev, width), weight[0], 1, 0)

    @pl.when(tap == 0)
    def _():
        acc[...] = part

    @pl.when(tap > 0)
    def _():
        acc[...] += part

    @pl.when(tap == 2)
    def _():
        for i in range(images):
            one = two = jnp.zeros((width, channels), F32)
            for r in range(rows_dev):
                inside = window(info, i, base + r, (width, channels))
                at = (i * rows_dev + r) * width
                value = (image[i, r].astype(F32) + acc[at : at + width]) * inside
                middle[i, r] = value
                one = one + value
                two = two + value * value
            put_stats(out_stats, i, one, two)


def dgrad(shifted, tap, weight, images, rows_dev, width):
    channels = weight.shape[2]
    lhs = tap_rows(shifted, tap, images, rows_dev, width)
    part = None
    for b in range(3):
        term = dot(
            lhs[:, b * channels : (b + 1) * channels],
            weight[0, (2 - b) * channels : (3 - b) * channels, :],
            1,
            1,
        )
        part = term if part is None else part + term
    return part


def back2_kernel(
    info, grad, grad_above, grad_below, middle, mid_above, mid_below, cot, cot_above, cot_below,
    mid_stats, grad_stats, attn_gain, first, first_stats, gain, shifts, weight,
    grad_middle, moved_grad, out_stats, plain, acc, shifted,
):
    images, rows_dev, width, channels = first.shape
    tap = pl.program_id(0)
    base = info[0, 2]

    @pl.when(tap == 0)
    def _():
        for i in range(images):
            count = image_count(info, i, channels)
            average, inverse = norm_of(mid_stats[i], count)
            mean, cross = means_of(grad_stats[i], attn_gain[...], count)
            for r in range(rows_dev + 2):
                inside = window(info, i, base + r - 1, (width, channels))
                normal = (padded_row(middle, mid_above, mid_below, i, r) - average) * inverse
                dx = padded_row(grad, grad_above, grad_below, i, r) * attn_gain[...]
                term = (dx - mean - normal * cross) * inverse * inside
                total = padded_row(cot, cot_above, cot_below, i, r).astype(F32) + term
                if 0 < r <= rows_dev:
                    grad_middle[i, r - 1] = total
                put_shifted(shifted, i, r, total * inside, plain)

    part = dgrad(shifted, tap, weight, images, rows_dev, width)

    @pl.when(tap == 0)
    def _():
        acc[...] = part

    @pl.when(tap > 0)
    def _():
        acc[...] += part

    @pl.when(tap == 2)
    def _():
        for i in range(images):
            average, inverse = norm_of(first_stats[i], image_count(info, i, channels))
            scale, shift = shifts[i : i + 1, :channels], shifts[i : i + 1, channels:]
            one = two = jnp.zeros((width, channels), F32)
            for r in range(rows_dev):
                inside = window(info, i, base + r, (width, channels))
                at = (i * rows_dev + r) * width
                normal, moved = moved_of(
                    first[i, r], inside, average, inverse, gain[...], scale, shift
                )
                value = acc[at : at + width] * inside * silu_slope(moved)
                moved_grad[i, r] = value
                one = one + value
                two = two + value * normal
            put_stats(out_stats, i, one, two)


def back1_kernel(
    info, grad, grad_above, grad_below, first, first_above, first_below, first_stats, grad_stats,
    gain, shifts, image, image_stats, first_gain, weight,
    pre_grad, out_stats, plain, acc, shifted,
):
    images, rows_dev, width, channels = first.shape
    tap = pl.program_id(0)
    base = info[0, 2]

    @pl.when(tap == 0)
    def _():
        for i in range(images):
            count = image_count(info, i, channels)
            average, inverse = norm_of(first_stats[i], count)
            factor = gain[...] * (1.0 + shifts[i : i + 1, :channels])
            mean, cross = means_of(grad_stats[i], factor, count)
            for r in range(rows_dev + 2):
                inside = window(info, i, base + r - 1, (width, channels))
                normal = (padded_row(first, first_above, first_below, i, r) - average) * inverse
                dx = padded_row(grad, grad_above, grad_below, i, r) * factor
                put_shifted(shifted, i, r, (dx - mean - normal * cross) * inverse * inside, plain)

    part = dgrad(shifted, tap, weight, images, rows_dev, width)

    @pl.when(tap == 0)
    def _():
        acc[...] = part

    @pl.when(tap > 0)
    def _():
        acc[...] += part

    @pl.when(tap == 2)
    def _():
        for i in range(images):
            average, inverse = norm_of(image_stats[i], image_count(info, i, channels))
            one = two = jnp.zeros((width, channels), F32)
            for r in range(rows_dev):
                inside = window(info, i, base + r, (width, channels))
                at = (i * rows_dev + r) * width
                normal = (image[i, r].astype(F32) - average) * inverse * inside
                slope = silu_slope(normal * first_gain[...])
                value = acc[at : at + width] * inside * slope
                pre_grad[i, r] = value
                one = one + value
                two = two + value * normal
            put_stats(out_stats, i, one, two)


def conv_call(kernel, info, inputs, weight, outs, flipped):
    images, rows_dev, width, channels = outs[0].shape

    def whole(shape):
        return pl.BlockSpec(shape, lambda tap: (0,) * len(shape))

    def tap_of(tap):
        return ((2 - tap) if flipped else tap, 0, 0)

    weight = weight.reshape(3, 3 * channels, channels)
    flops = 2 * 9 * images * rows_dev * width * channels * channels
    moved = sum(a.size * a.dtype.itemsize for a in (*inputs, weight, *outs))
    return pl.pallas_call(
        kernel,
        grid=(3,),
        out_shape=tuple(outs),
        in_specs=[SCALARS]
        + [whole(a.shape) for a in inputs]
        + [pl.BlockSpec((1, 3 * channels, channels), tap_of)],
        out_specs=tuple(whole(o.shape) for o in outs),
        scratch_shapes=[
            pltpu.VMEM((images * rows_dev * width, channels), F32),
            pltpu.VMEM((images, rows_dev + 2, width, 3 * channels), BF16),
        ],
        compiler_params=pltpu.CompilerParams(vmem_limit_bytes=48 << 20),
        cost_estimate=pl.CostEstimate(flops=flops, bytes_accessed=moved, transcendentals=0),
        name=kernel.__name__,
    )(info, *inputs, weight)


def weight_grad_kernel(grads, hidden, out, turned, shifted):
    images, padded, width, channels = hidden.shape
    rows_dev = padded - 2
    pixels = images * rows_dev * width
    tap = pl.program_id(0)

    @pl.when(tap == 0)
    def _():
        center = grads[:, 1 : rows_dev + 1]
        turned[...] = center.reshape(pixels, channels).astype(F32).T.astype(BF16)
        for i in range(images):
            for r in range(padded):
                put_shifted(shifted, i, r, hidden[i, r].astype(F32))

    column = pl.multiple_of((tap % 3) * channels, channels)
    rhs = shifted[:, pl.ds(tap // 3, rows_dev), :, pl.ds(column, channels)]
    out[...] = dot(turned[...], rhs.reshape(pixels, channels), 1, 0).astype(BF16)


def weight_grad(grads, hidden):
    images, padded, width, channels = hidden.shape
    pixels = images * (padded - 2) * width

    def whole(shape):
        return pl.BlockSpec(shape, lambda tap: (0,) * len(shape))

    return pl.pallas_call(
        weight_grad_kernel,
        grid=(9,),
        out_shape=jax.ShapeDtypeStruct((channels, 9 * channels), BF16),
        in_specs=[whole(grads.shape), whole(hidden.shape)],
        out_specs=pl.BlockSpec((channels, channels), lambda tap: (0, tap)),
        scratch_shapes=[
            pltpu.VMEM((channels, pixels), BF16),
            pltpu.VMEM(hidden.shape[:3] + (3 * channels,), BF16),
        ],
        compiler_params=pltpu.CompilerParams(vmem_limit_bytes=32 << 20),
        cost_estimate=pl.CostEstimate(
            flops=18 * pixels * channels * channels,
            bytes_accessed=18 * channels * channels,
            transcendentals=0,
        ),
        name="weight_grad",
    )(grads, hidden)


def project_kernel(info, middle, stats, gain, weight, attn, qkv):
    images, rows_dev, width, channels = middle.shape
    pixels = rows_dev * width
    heads, wide = HEADS, weight.shape[0] // HEADS
    base = info[0, 2]
    for i in range(images):
        average, inverse = norm_of(stats[i], image_count(info, i, channels))
        for r in range(rows_dev):
            inside = window(info, i, base + r, (width, channels))
            value = (middle[i, r] - average) * inverse * inside * gain[...]
            attn[i, r * width : (r + 1) * width] = value.astype(BF16)
        for h in range(heads):
            block = dot(weight[h * wide : (h + 1) * wide], attn[i], 1, 1)
            qkv[i * heads + h] = block.astype(BF16)


def project(info, middle, stats, gain, weight):
    images, rows_dev, width, channels = middle.shape
    pixels = rows_dev * width
    return pl.pallas_call(
        project_kernel,
        out_shape=(
            jax.ShapeDtypeStruct((images, pixels, channels), BF16),
            jax.ShapeDtypeStruct((images * HEADS, weight.shape[0] // HEADS, pixels), BF16),
        ),
        in_specs=[SCALARS, WHOLE, WHOLE, WHOLE, WHOLE],
        out_specs=(WHOLE, WHOLE),
        compiler_params=pltpu.CompilerParams(vmem_limit_bytes=32 << 20),
        name="project",
    )(info, middle, stats, gain, weight)


def unproject_kernel(info, middle, stats, grads, weight, out, out_stats):
    images, rows_dev, width, channels = middle.shape
    wide, pixels = grads.shape[1], grads.shape[2]
    base = info[0, 2]
    for i in range(images):
        average, inverse = norm_of(stats[i], image_count(info, i, channels))
        acc = None
        for h in range(HEADS):
            turned = grads[i * HEADS + h].astype(F32).T.astype(BF16)
            term = dot(turned, weight[h * wide : (h + 1) * wide], 1, 0)
            acc = term if acc is None else acc + term
        one = two = jnp.zeros((width, channels), F32)
        for r in range(rows_dev):
            inside = window(info, i, base + r, (width, channels))
            value = acc[r * width : (r + 1) * width] * inside
            out[i, r] = value
            one = one + value
            two = two + value * ((middle[i, r] - average) * inverse)
        put_stats(out_stats, i, one, two)


def unproject(info, middle, stats, grads, weight):
    images, rows_dev, width, channels = middle.shape
    return pl.pallas_call(
        unproject_kernel,
        out_shape=(
            jax.ShapeDtypeStruct(middle.shape, F32),
            jax.ShapeDtypeStruct(stats.shape, F32),
        ),
        in_specs=[SCALARS, WHOLE, WHOLE, WHOLE, WHOLE],
        out_specs=(WHOLE, WHOLE),
        compiler_params=pltpu.CompilerParams(vmem_limit_bytes=32 << 20),
        name="unproject",
    )(info, middle, stats, grads, weight)


def finish_kernel(info, pre_grad, grad_stats, image, stats, gain, grad_middle, out):
    images, rows_dev, width, channels = image.shape
    base = info[0, 2]
    for i in range(images):
        count = image_count(info, i, channels)
        average, inverse = norm_of(stats[i], count)
        mean, cross = means_of(grad_stats[i], gain[...], count)
        for r in range(rows_dev):
            inside = window(info, i, base + r, (width, channels))
            normal = (image[i, r].astype(F32) - average) * inverse
            term = (pre_grad[i, r] * gain[...] - mean - normal * cross) * inverse
            out[i, r] = (grad_middle[i, r] + term) * inside


def finish(info, pre_grad, grad_stats, image, stats, gain, grad_middle):
    return pl.pallas_call(
        finish_kernel,
        out_shape=jax.ShapeDtypeStruct(image.shape, F32),
        in_specs=[SCALARS] + [WHOLE] * 6,
        out_specs=WHOLE,
        compiler_params=pltpu.CompilerParams(vmem_limit_bytes=32 << 20),
        name="finish",
    )(info, pre_grad, grad_stats, image, stats, gain, grad_middle)


DMA = pltpu.SemaphoreType.DMA


def remote(src, dst, send, recv, device):
    return pltpu.make_async_remote_copy(
        src_ref=src,
        dst_ref=dst,
        send_sem=send,
        recv_sem=recv,
        device_id=device,
        device_id_type=MESH,
    )


class Grid:
    def __init__(self, items, n):
        self.items, self.n = items, n
        self.item, self.me = lax.axis_index("items"), lax.axis_index("rows")

    def row(self, k):
        return {"items": self.item, "rows": lax.rem(self.me + k, self.n)}

    def peer(self, k):
        return {"items": lax.rem(self.item + k, self.items), "rows": self.me}

    def greet(self):
        barrier = pltpu.get_barrier_semaphore()

        def rows(k, carry):
            pl.semaphore_signal(barrier, inc=1, device_id=self.row(k), device_id_type=MESH)
            return carry

        def items(k, carry):
            pl.semaphore_signal(barrier, inc=1, device_id=self.peer(k), device_id_type=MESH)
            return carry

        lax.fori_loop(1, self.n, rows, 0)
        lax.fori_loop(1, self.items, items, 0)

    def met(self):
        pl.semaphore_wait(pltpu.get_barrier_semaphore(), self.n + self.items - 2)

    def loop(self, count, body):
        def step(k, carry):
            body(k)
            return carry

        lax.fori_loop(1, count, step, 0)


class Sums:
    def __init__(self, grid, own, slots, send, recv):
        self.grid, self.own, self.slots, self.send, self.recv = grid, own, slots, send, recv

    def copy(self, k):
        return remote(
            self.own, self.slots.at[self.grid.me], self.send.at[k], self.recv.at[k], self.grid.row(k)
        )

    def start(self, stats):
        lines, lanes = self.own.shape
        half = lines // 2
        at = lax.broadcasted_iota(jnp.int32, (lines, lanes), 0)
        packed = jnp.zeros((lines, lanes), F32)
        for j in range(lines):
            piece = stats[j // half : j // half + 1, (j % half) * lanes : (j % half + 1) * lanes]
            packed = jnp.where(at == j, piece, packed)
        self.own[...] = packed
        self.grid.loop(self.grid.n, lambda k: self.copy(k).start())
        self.slots[self.grid.me] = packed

    def result(self):
        self.grid.loop(self.grid.n, lambda k: self.copy(k).wait())
        slots = self.slots
        total = lax.fori_loop(1, self.grid.n, lambda k, s: s + slots[k], slots[0])
        half = total.shape[0] // 2
        rows = [
            jnp.concatenate([total[r * half + j : r * half + j + 1] for j in range(half)], axis=1)
            for r in range(2)
        ]
        at = lax.broadcasted_iota(jnp.int32, (8, rows[0].shape[1]), 0)
        return jnp.where(at == 0, rows[0], jnp.where(at == 1, rows[1], 0.0))


class Edges:
    def __init__(self, grid, field, send, recv):
        self.grid, self.field, self.send, self.recv = grid, field, send, recv

    def copy(self, side):
        last = self.field.shape[0] - 1
        at, to = (last - 1, 0) if side == 0 else (1, last)
        grid = self.grid
        return remote(
            self.field.at[at : at + 1],
            self.field.at[to : to + 1],
            self.send.at[side],
            self.recv.at[side],
            {"items": grid.item, "rows": grid.me + 1 if side == 0 else grid.me - 1},
        )

    def both(self, down, up):
        @pl.when(self.grid.me < self.grid.n - 1)
        def _():
            down()

        @pl.when(self.grid.me > 0)
        def _():
            up()

    def clear(self):
        last = self.field.shape[0] - 1

        @pl.when(self.grid.me == 0)
        def _():
            self.field[0] = jnp.zeros(self.field.shape[1:], self.field.dtype)

        @pl.when(self.grid.me == self.grid.n - 1)
        def _():
            self.field[last] = jnp.zeros(self.field.shape[1:], self.field.dtype)

    def start(self):
        self.both(lambda: self.copy(0).start(), lambda: self.copy(1).start())

    def wait(self):
        self.both(lambda: self.copy(1).wait_recv(), lambda: self.copy(0).wait_recv())
        self.both(lambda: self.copy(0).wait_send(), lambda: self.copy(1).wait_send())


def shift_into(out, r, value):
    width, channels = value.shape
    column = lax.broadcasted_iota(jnp.int32, value.shape, 0)
    left = jnp.where(column == 0, 0.0, pltpu.roll(value, 1, 0))
    right = jnp.where(column == width - 1, 0.0, pltpu.roll(value, width - 1, 0))
    out[r, :, :channels] = left.astype(BF16)
    out[r, :, channels : 2 * channels] = value.astype(BF16)
    out[r, :, 2 * channels :] = right.astype(BF16)


def row_stats(rows, width, channels, row):
    def step(r, carry):
        one, two = row(r)
        return carry[0] + one, carry[1] + two

    zero = jnp.zeros((width, channels), F32)
    one, two = lax.fori_loop(0, rows, step, (zero, zero))
    one = jnp.sum(one, axis=0, keepdims=True)
    two = jnp.sum(two, axis=0, keepdims=True)
    at = lax.broadcasted_iota(jnp.int32, (8, channels), 0)
    return jnp.where(at == 0, one, jnp.where(at == 1, two, 0.0))


def each_row(rows, body):
    def step(r, carry):
        body(r)
        return carry

    lax.fori_loop(0, rows, step, 0)


def conv_taps(shifted, weight, acc, rows_dev):
    pixels, wide = acc.shape[0], shifted.shape[2]
    acc[...] = jnp.zeros_like(acc)

    def step(tap, carry):
        acc[...] += dot(shifted[pl.ds(tap, rows_dev)].reshape(pixels, wide), weight[tap], 1, 0)
        return carry

    lax.fori_loop(0, 3, step, 0)


def forward_kernel(items, n, step, bq, *refs):
    (info, image, cot, text, embed, gain1, gain2, gain3, w1_in, w2_in, embed_in, text_in, qkv_in, proj_in,
     first_out, mid_out, cot_out, hidden_all, second_all, attn_out, turned_out, output, query_part, side_out, dkv_out,
     dt_out, text_cols, stats_out, shifts_out,
     image_v, cot_v, text_v, w1, w2, wide_w, qkv_w, proj_w, first_v, mid_v, hidden, second, attn,
     turned, pairs, queries, go, text_kv, cols, shifted, acc, own, slots,
     pair_land, query_land, go_land, text_pair, o, dq, dkv, dtext, same, o_land, dq_land, masked, out_v, query_acc,
     side_v, side_core, side_sum, side_item, side_total, cols_land,
     load, sum_send, sum_recv, edge_send, edge_recv, row_send, row_recv, item_send, item_recv,
     s_core_send, s_core_recv, s_item_send, s_item_recv, *scratch) = refs
    grid = Grid(items, n)
    item, me = grid.item, grid.me
    rows_dev, width, channels = image.shape
    pixels = rows_dev * width
    heads, head_dim, wide = HEADS, channels // HEADS, 3 * channels // HEADS
    base = me * rows_dev
    share_rows = channels // n
    count = (info[0, 0] * info[0, 1]).astype(F32) * (channels // GROUPS)
    att = Attention(n, pixels, head_dim, n * text.shape[0], step, bq, scratch)

    def inside(row):
        return window(info, 0, row, (width, channels))

    loads = []

    def fetch(src, dst):
        c = pltpu.make_async_copy(src, dst, load.at[len(loads)])
        c.start()
        loads.append(c)
        return c

    center = slice(1, rows_dev + 1)
    got_image = fetch(image, image_v.at[center])
    got_cot = fetch(cot, cot_v.at[center])
    got_proj = fetch(proj_in, proj_w)
    got_text = fetch(text, text_v)
    got_text_w = fetch(text_in, wide_w)
    got_w1 = fetch(w1_in, w1)
    got_w2 = fetch(w2_in, w2)
    got_qkv_w = fetch(qkv_in, qkv_w)
    edges = [
        Edges(grid, field, edge_send.at[j], edge_recv.at[j])
        for j, field in enumerate((image_v, cot_v, first_v, mid_v))
    ]
    sums = [Sums(grid, own.at[j], slots.at[j], sum_send.at[j], sum_recv.at[j]) for j in range(3)]
    grid.greet()
    for e in edges:
        e.clear()
    same[...] = group_matrix(channels)
    got_image.wait()

    def start_row(r):
        return image_v[1 + r].astype(F32) * inside(base + r)

    def start_stats(r):
        v = start_row(r)
        return v, v * v

    stats = row_stats(rows_dev, width, channels, start_stats)
    grid.met()
    sums[0].start(stats)
    edges[0].start()
    got_cot.wait()
    edges[1].start()

    got_text.wait()
    got_text_w.wait()
    text_all = dot(text_v[...], wide_w[...], 1, 0).astype(BF16)
    got_embed_w = fetch(embed_in, wide_w)
    share = text_v.shape[1] // n
    for h in range(heads):
        text_kv[h] = text_all[:, h * 2 * head_dim : (h + 1) * 2 * head_dim]
    for r in range(n):
        cols[r] = text_v[:, r * share : (r + 1) * share]

    def scatter(j, src, dst):
        def copy(k):
            to = lax.rem(me + k, n)
            return remote(src.at[to], dst.at[me], row_send.at[j, k], row_recv.at[j, k], grid.row(k))

        return copy

    kv_copy = scatter(0, text_kv, text_pair)
    col_copy = scatter(1, cols, cols_land)
    grid.loop(n, lambda k: kv_copy(k).start())
    grid.loop(n, lambda k: col_copy(k).start())
    own_kv = fetch(text_kv.at[me], text_pair.at[me])
    cols_land[me] = cols[me]

    got_proj.wait()

    def to_grad(r):
        masked[pl.ds(r * width, width)] = (cot_v[1 + r].astype(F32) * inside(base + r)).astype(BF16)

    each_row(rows_dev, to_grad)
    for h in range(heads):
        go[h] = dot(proj_w[h * head_dim : (h + 1) * head_dim], masked[...], 1, 1).astype(BF16)
    go_copy = scatter(2, go, go_land)
    own_go = fetch(go.at[me], go_land.at[me])

    stats = sums[0].result()
    stats_out[0] = stats
    average, inverse = norm_of(stats, count, same[...])
    edges[0].wait()

    def to_hidden(r):
        ok = inside(base + r - 1)
        value = (image_v[r].astype(F32) * ok - average) * inverse * ok * gain1[...]
        value = value * sigmoid(value) * ok
        shift_into(shifted, r, value)
        hidden[r] = value.astype(BF16)

    each_row(rows_dev + 2, to_hidden)

    def spread(j, src, dst):
        def copy(k):
            return remote(src, dst.at[item], item_send.at[j, k], item_recv.at[j, k], grid.peer(k))

        return copy

    hidden_copy = spread(0, hidden, hidden_all)
    grid.loop(items, lambda k: hidden_copy(k).start())
    own_hidden = fetch(hidden, hidden_all.at[item])
    got_w1.wait()
    conv_taps(shifted, w1, acc, rows_dev)

    def first_row(r):
        value = acc[pl.ds(r * width, width)] * inside(base + r)
        first_v[1 + r] = value
        return value, value * value

    stats = row_stats(rows_dev, width, channels, first_row)
    sums[1].start(stats)
    edges[2].start()

    e = embed[...].astype(F32)
    low = (e * sigmoid(e)).astype(BF16)
    got_embed_w.wait()
    shifts_out[...] = dot(low, wide_w[...], 1, 0)
    scale, shift = shifts_out[:, :channels], shifts_out[:, channels:]

    stats = sums[1].result()
    stats_out[1] = stats
    average, inverse = norm_of(stats, count, same[...])
    edges[2].wait()
    own_first = fetch(first_v, first_out)

    def to_second(r):
        ok = inside(base + r - 1)
        _, moved = moved_of(first_v[r], ok, average, inverse, gain2[...], scale, shift)
        value = moved * sigmoid(moved) * ok
        shift_into(shifted, r, value)
        second[r] = value.astype(BF16)

    each_row(rows_dev + 2, to_second)
    second_copy = spread(1, second, second_all)
    grid.loop(items, lambda k: second_copy(k).start())
    own_second = fetch(second, second_all.at[item])
    got_w2.wait()
    conv_taps(shifted, w2, acc, rows_dev)

    def middle_row(r):
        value = (image_v[1 + r].astype(F32) + acc[pl.ds(r * width, width)]) * inside(base + r)
        mid_v[1 + r] = value
        return value, value * value

    stats = row_stats(rows_dev, width, channels, middle_row)
    sums[2].start(stats)
    edges[3].start()
    edges[1].wait()
    own_cot = fetch(cot_v, cot_out)
    got_qkv_w.wait()
    for j in range(3):
        block = qkv_w[:, j * channels : (j + 1) * channels].astype(F32).T
        turned[j * channels : (j + 1) * channels] = block.astype(BF16)
    own_turned = fetch(turned, turned_out)

    stats = sums[2].result()
    stats_out[2] = stats
    average, inverse = norm_of(stats, count, same[...])

    def to_attn(r):
        value = (mid_v[1 + r] - average) * inverse * inside(base + r) * gain3[...]
        attn[pl.ds(r * width, width)] = value.astype(BF16)

    each_row(rows_dev, to_attn)
    own_attn = fetch(attn, attn_out)
    pair_copy = scatter(3, pairs, pair_land)
    query_copy = scatter(4, queries, query_land)

    def head(k):
        to = lax.rem(me + k, n)
        rows = pl.ds(pl.multiple_of(to * wide, wide), wide)
        block = dot(turned[rows], attn[...], 1, 1).astype(BF16)
        queries[to] = block[:head_dim]
        pairs[to] = block[head_dim:]

    def send_head(k):
        head(k)
        pair_copy(k).start()

    grid.loop(n, send_head)
    head(0)
    query_land[me] = queries[me]
    att.stage_key(me, pairs[me, :head_dim], width, info[0, 0], info[0, 1])
    att.stage_value(me, pairs[me, head_dim:])
    grid.loop(n, lambda k: kv_copy(k).wait())
    own_kv.wait()
    att.stage_text(text_pair[...].reshape(n * text.shape[0], 2 * head_dim))
    edges[3].wait()
    own_mid = fetch(mid_v, mid_out)

    def source(k):
        return lax.rem(me + n - k, n)

    def stage_pair(k):
        pair_copy(k).wait()
        c = source(k)
        att.stage_key(c, pair_land[c, :head_dim], width, info[0, 0], info[0, 1])
        att.stage_value(c, pair_land[c, head_dim:])

    grid.loop(n, stage_pair)

    def send_rest(k):
        query_copy(k).start()
        go_copy(k).start()

    grid.loop(n, send_rest)
    own_go.wait()

    def before(k):
        query_copy(k).wait()
        go_copy(k).wait()

    def give(j, src, dst):
        def copy(h):
            to = source(h)
            return remote(
                src.at[to],
                dst.at[me],
                row_send.at[j, h],
                row_recv.at[j, h],
                {"items": item, "rows": to},
            )

        return copy

    o_copy = give(5, o, o_land)
    dq_copy = give(6, dq, dq_land)
    dkv_copy = give(7, dkv, dkv_out)

    def done(h):
        @pl.when(h > 0)
        def _():
            o_copy(h).start()
            dq_copy(h).start()

    grid.loop(n, lambda k: col_copy(k).wait())
    cols_copy = spread(2, cols_land, text_cols)
    grid.loop(items, lambda k: cols_copy(k).start())
    own_cols = fetch(cols_land, text_cols.at[item])
    att.attend(query_land, go_land, o, dq, source, before, done)

    def send_keys(h):
        at = pl.ds(pl.multiple_of(source(h) * pixels, pixels), pixels)
        dkv[source(h), :head_dim] = att.key_grad(at)
        dkv[source(h), head_dim:] = att.value_grad(at)

    def send_next(h):
        send_keys(h)
        dkv_copy(h).start()

    grid.loop(n, send_next)
    send_keys(0)
    flat = jnp.concatenate(
        [
            (att.dkt[:, n * pixels :] * (head_dim**-0.5)).T,
            att.dvt[:, n * pixels :].T,
        ],
        axis=1,
    )
    for r in range(n):
        tokens = text.shape[0]
        dtext[r] = flat[r * tokens : (r + 1) * tokens].astype(BF16)

    own_dkv = fetch(dkv.at[me], dkv_out.at[me])
    own_dt = fetch(dtext, dt_out)

    o_land[me] = o[me]
    dq_land[me] = dq[me]
    grid.loop(n, lambda h: o_copy(h).wait())
    grid.loop(n, lambda h: dq_copy(h).wait())
    side = SideSum(grid, side_v, side_core, side_sum, side_item, side_total, None, None,
                   (s_core_send, s_core_recv), (s_item_send, s_item_recv), None, None)

    def query_head(h):
        block = dot(dq_land[h], attn[...], 1, 0).astype(BF16)
        side.put_head(h, block, 0)

    each_row(heads, query_head)
    flat_o = o_land[...].reshape(channels, pixels)
    block = dot(masked[...].astype(F32).T.astype(BF16), flat_o, 1, 1).astype(BF16)
    for r in range(n):
        side.put_head(r, block[r * share_rows : (r + 1) * share_rows], 1)
    side.core_copy().start()
    query_acc[...] = jnp.zeros_like(query_acc)

    def unproject_query(h):
        rows = pl.ds(pl.multiple_of(h * wide, wide), head_dim)
        query_acc[...] += dot(dq_land[h].astype(F32).T.astype(BF16), turned[rows], 1, 0)

    each_row(heads, unproject_query)
    put_query = fetch(query_acc, query_part)
    side.over_items()
    acc[...] = dot(flat_o.astype(F32).T.astype(BF16), proj_w[...], 1, 0)

    def output_row(r):
        value = mid_v[1 + r] + acc[pl.ds(r * width, width)] * inside(base + r)
        out_v[r] = value.astype(BF16)

    each_row(rows_dev, output_row)
    put_output = fetch(out_v, output)
    side.sum_items()
    put_side = fetch(side_total, side_out)
    grid.loop(items, lambda k: hidden_copy(k).wait())
    grid.loop(items, lambda k: second_copy(k).wait())
    grid.loop(items, lambda k: cols_copy(k).wait())
    grid.loop(n, lambda h: dkv_copy(h).wait())
    for c in (own_hidden, own_first, own_second, own_cot, own_turned, own_attn, own_mid, own_dkv, own_dt,
              own_cols, put_query, put_output, put_side):
        c.wait()


def forward_call(info, image, cot, text, embed, gains, weights, identity):
    items, n = lax.axis_size("items"), lax.axis_size("rows")
    rows_dev, width, channels = image.shape
    pixels = rows_dev * width
    padded = (rows_dev + 2, width, channels)
    tokens, text_width = text.shape
    head_dim = channels // HEADS
    w1, w2, _, text_w, qkv_w, proj_w = weights
    chips = n // 2
    rows = channels // n // items
    sds = jax.ShapeDtypeStruct
    outs = (
        sds(padded, F32),
        sds(padded, F32),
        sds(padded, BF16),
        sds((items,) + padded, BF16),
        sds((items,) + padded, BF16),
        sds((pixels, channels), BF16),
        sds((3 * channels, channels), BF16),
        sds(image.shape, BF16),
        sds((pixels, channels), F32),
        sds((chips, rows, 2 * channels), BF16),
        sds((n, 2 * head_dim, pixels), BF16),
        sds((n, tokens, 2 * head_dim), BF16),
        sds((items, n, tokens, text_width // n), BF16),
        sds((3, 8, channels), F32),
        sds((1, 2 * channels), F32),
    )
    v = pltpu.VMEM
    scratch = [
        v(padded, BF16),
        v(padded, BF16),
        v(text.shape, BF16),
        v(w1.shape, BF16),
        v(w2.shape, BF16),
        v(text_w.shape, BF16),
        v(qkv_w.shape, BF16),
        v(proj_w.shape, BF16),
        v(padded, F32),
        v(padded, F32),
        v(padded, BF16),
        v(padded, BF16),
        v((pixels, channels), BF16),
        v((3 * channels, channels), BF16),
        v((n, 2 * head_dim, pixels), BF16),
        v((n, head_dim, pixels), BF16),
        v((n, head_dim, pixels), BF16),
        v((n, tokens, 2 * head_dim), BF16),
        v((n, tokens, text_width // n), BF16),
        v((rows_dev + 2, width, 3 * channels), BF16),
        v((pixels, channels), F32),
        v((3, channels // 64, 128), F32),
        v((3, n, channels // 64, 128), F32),
        v((n, 2 * head_dim, pixels), BF16),
        v((n, head_dim, pixels), BF16),
        v((n, head_dim, pixels), BF16),
        v((n, tokens, 2 * head_dim), BF16),
        v((n, head_dim, pixels), BF16),
        v((n, head_dim, pixels), BF16),
        v((n, 2 * head_dim, pixels), BF16),
        v((n, tokens, 2 * head_dim), BF16),
        v((channels, channels), BF16),
        v((n, head_dim, pixels), BF16),
        v((n, head_dim, pixels), BF16),
        v((pixels, channels), BF16),
        v(image.shape, BF16),
        v((pixels, channels), F32),
        v((2, chips, items, rows, 2 * channels), BF16),
        v((chips, items, rows, 2 * channels), BF16),
        v((items, chips, rows, 2 * channels), BF16),
        v((items, chips, rows, 2 * channels), BF16),
        v((chips, rows, 2 * channels), BF16),
        v((n, tokens, text_width // n), BF16),
        DMA((28,)),
        DMA((3, n)),
        DMA((3, n)),
        DMA((4, 2)),
        DMA((4, 2)),
        DMA((8, n)),
        DMA((8, n)),
        DMA((3, items)),
        DMA((3, items)),
        DMA((1,)),
        DMA((1,)),
        DMA((items,)),
        DMA((items,)),
    ]
    step, bq, extra = attention_scratch(n, pixels, head_dim, n * tokens)
    scratch += extra
    return pl.pallas_call(
        functools.partial(forward_kernel, items, n, step, bq),
        out_shape=outs,
        in_specs=[SCALARS] + [ANYWHERE] * 3 + [WHOLE] * 4 + [ANYWHERE] * 6,
        out_specs=(ANYWHERE,) * 13 + (WHOLE,) * 2,
        scratch_shapes=scratch,
        compiler_params=pltpu.CompilerParams(
            collective_id=identity, has_side_effects=True, vmem_limit_bytes=62 << 20
        ),
        cost_estimate=pl.CostEstimate(
            flops=40 * pixels * channels * channels, bytes_accessed=60 << 20, transcendentals=0
        ),
        name="forward",
    )(info, image, cot, text, embed, *gains, *weights)


class KernelSum:
    def __init__(self, grid, turned, quarter, part, from_core, chip_sum, from_chip, final, item_sems, core_sems,
                 chip_sems, final_sems):
        self.grid = grid
        self.turned, self.quarter, self.part, self.from_core = turned, quarter, part, from_core
        self.chip_sum, self.from_chip, self.final = chip_sum, from_chip, final
        self.item_sems, self.core_sems = item_sems, core_sems
        self.chip_sems, self.final_sems = chip_sems, final_sems
        self.chips = grid.n // 2
        self.chip, self.core = grid.me // 2, lax.rem(grid.me, 2)

    def grads_copy(self, k):
        grid = self.grid
        send, recv = self.item_sems
        to = lax.rem(grid.item + k, grid.items)
        return remote(
            self.turned.at[to], self.quarter.at[grid.item], send.at[k], recv.at[k], grid.peer(k)
        )

    def send_grads(self, shifted):
        grid, chips = self.grid, self.chips
        rows_dev, width, channels = shifted.shape[0] - 2, shifted.shape[1], shifted.shape[2] // 3
        center = shifted[1 : rows_dev + 1, :, channels : 2 * channels]
        block = center.reshape(rows_dev * width, channels).astype(F32).T.astype(BF16)
        share = channels // grid.n
        rows = share // grid.items
        for z in range(chips):
            for c in range(2):
                for q in range(grid.items):
                    at = (z * 2 + c) * share + q * rows
                    to = (c * chips + z) * rows
                    self.turned[q, to : to + rows] = block[at : at + rows]
        grid.loop(grid.items, lambda k: self.grads_copy(k).start())
        self.quarter[grid.item] = self.turned[grid.item]

    def wait_grads(self):
        self.grid.loop(self.grid.items, lambda k: self.grads_copy(k).wait())

    def core_copy(self, a):
        send, recv = self.core_sems
        grid = self.grid
        return remote(
            self.part.at[a, 1 - self.core],
            self.from_core.at[a],
            send.at[a],
            recv.at[a],
            {"items": grid.item, "rows": grid.me + 1 - 2 * self.core},
        )

    def compute(self, a, shifted):
        items, padded, width, wide = shifted.shape
        rows_dev, channels = padded - 2, wide // 3
        half = self.turned.shape[1] // 2
        for b in range(3):
            acc = None
            for g in range(items):
                rhs = shifted[g, a : a + rows_dev, :, b * channels : (b + 1) * channels]
                term = dot(self.quarter[g], rhs.reshape(rows_dev * width, channels), 1, 0)
                acc = term if acc is None else acc + term
            self.part[a, 0, b] = acc[:half].astype(BF16)
            self.part[a, 1, b] = acc[half:].astype(BF16)
        self.core_copy(a).start()

    def chip_copy(self, a, k):
        send, recv = self.chip_sems
        grid = self.grid
        to = lax.rem(self.chip + k, self.chips)
        return remote(
            self.chip_sum.at[a, to],
            self.from_chip.at[a, k],
            send.at[a, k],
            recv.at[a, k],
            {"items": grid.item, "rows": to * 2 + self.core},
        )

    def over_chips(self, a):
        self.core_copy(a).wait()
        rows = self.chip_sum.shape[3]
        for b in range(3):
            both = self.part[a, self.core, b].astype(F32) + self.from_core[a, b].astype(F32)
            for z in range(self.chips):
                self.chip_sum[a, z, b] = both[z * rows : (z + 1) * rows].astype(BF16)
        for k in range(1, self.chips):
            self.chip_copy(a, k).start()

    def final_copy(self, a, k):
        send, recv = self.final_sems
        mine = self.final.at[a, self.grid.item]
        return remote(mine, mine, send.at[a, k], recv.at[a, k], self.grid.peer(k))

    def over_items(self, a):
        for k in range(1, self.chips):
            self.chip_copy(a, k).wait()
        total = self.chip_sum[a, self.chip].astype(F32)
        for k in range(1, self.chips):
            total = total + self.from_chip[a, k].astype(F32)
        self.final[a, self.grid.item] = total.astype(BF16)
        for k in range(1, self.grid.items):
            self.final_copy(a, k).start()

    def wait_final(self, a):
        for k in range(1, self.grid.items):
            self.final_copy(a, k).wait()


class SideSum:
    def __init__(self, grid, values, from_core, core_sum, from_item, item_sum, from_chip, final, core_sems,
                 item_sems, chip_sems, final_sems):
        self.grid = grid
        self.values, self.from_core, self.core_sum = values, from_core, core_sum
        self.from_item, self.item_sum, self.from_chip, self.final = (
            from_item,
            item_sum,
            from_chip,
            final,
        )
        self.core_sems, self.item_sems = core_sems, item_sems
        self.chip_sems, self.final_sems = chip_sems, final_sems
        self.chips = grid.n // 2
        self.chip, self.core = grid.me // 2, lax.rem(grid.me, 2)

    def core_copy(self):
        send, recv = self.core_sems
        grid = self.grid
        return remote(
            self.values.at[1 - self.core],
            self.from_core,
            send.at[0],
            recv.at[0],
            {"items": grid.item, "rows": grid.me + 1 - 2 * self.core},
        )

    def item_copy(self, k):
        send, recv = self.item_sems
        grid = self.grid
        to = lax.rem(grid.item + k, grid.items)
        return remote(
            self.core_sum.at[to], self.from_item.at[k], send.at[k], recv.at[k], grid.peer(k)
        )

    def over_items(self):
        self.core_copy().wait()
        for z in range(self.chips):
            both = self.values[self.core, z].astype(F32) + self.from_core[z].astype(F32)
            for q in range(self.grid.items):
                self.core_sum[q, z] = both[q].astype(BF16)
        for k in range(1, self.grid.items):
            self.item_copy(k).start()

    def chip_copy(self, k):
        send, recv = self.chip_sems
        grid = self.grid
        to = lax.rem(self.chip + k, self.chips)
        return remote(
            self.item_sum.at[to],
            self.from_chip.at[k],
            send.at[k],
            recv.at[k],
            {"items": grid.item, "rows": to * 2 + self.core},
        )

    def put_head(self, h, block, j):
        items, rows = self.values.shape[2], self.values.shape[3]
        channels = block.shape[1]
        at = slice(j * channels, (j + 1) * channels)
        core, chip = (h % 2, h // 2) if isinstance(h, int) else (lax.rem(h, 2), h // 2)
        self.values[core, chip, :, :, at] = block.reshape(items, rows, channels)

    def sum_items(self):
        for k in range(1, self.grid.items):
            self.item_copy(k).wait()
        total = self.core_sum[self.grid.item].astype(F32)
        for k in range(1, self.grid.items):
            total = total + self.from_item[k].astype(F32)
        self.item_sum[:, :, : total.shape[2]] = total.astype(BF16)

    def over_chips(self):
        self.sum_items()
        for k in range(1, self.chips):
            self.chip_copy(k).start()

    def final_copy(self, k):
        send, recv = self.final_sems
        mine = self.final.at[self.grid.item]
        return remote(mine, mine, send.at[k], recv.at[k], self.grid.peer(k))

    def spread(self):
        for k in range(1, self.chips):
            self.chip_copy(k).wait()
        total = self.item_sum[self.chip].astype(F32)
        for k in range(1, self.chips):
            total = total + self.from_chip[k].astype(F32)
        self.final[self.grid.item] = total.astype(BF16)
        for k in range(1, self.grid.items):
            self.final_copy(k).start()

    def wait_final(self):
        for k in range(1, self.grid.items):
            self.final_copy(k).wait()


def conv_taps_back(shifted, weight, acc, rows_dev):
    pixels, channels = acc.shape
    acc[...] = jnp.zeros_like(acc)

    def step(tap, carry):
        lhs = shifted[pl.ds(tap, rows_dev)].reshape(pixels, 3 * channels)
        total = None
        for b in range(3):
            at = pl.multiple_of(((2 - tap) * 3 + 2 - b) * channels, channels)
            term = dot(
                lhs[:, b * channels : (b + 1) * channels], weight[pl.ds(at, channels)], 1, 1
            )
            total = term if total is None else total + term
        acc[...] += total
        return carry

    lax.fori_loop(0, 3, step, 0)


def backward_kernel(items, n, *refs):
    (info, embed, gain1, gain2, gain3, stats_in, shifts,
     query_part, side_in, dkv_in, dt_in, first, middle, cot, image, hidden_all, second_all, attn_in,
     turned_in, text_cols, w1_in, w2_in, text_in, embed_in,
     image_grad, text_grad, text_w_grad, embed_grad, final_out, side_out, vectors,
     weight, qkv_turned, first_v, mid_v, cot_v, image_v, attn, cols, rows_v, dkv, dtext, dt, own_dt,
     grad_v, grad_mid, moved_v, pre, acc, shifted, shifted_all, image_out, text_v, text_w_v, embed_v, same,
     turned, quarter, part, from_core, chip_sum, from_chip, final,
     side_v, side_core, side_sum, side_item, side_total, side_chip, side_final,
     vector, vector_land, own, slots,
     load, sum_send, sum_recv, edge_send, edge_recv, text_send, text_recv, dt_send, dt_recv, dt_core_send, dt_core_recv, vec_send, vec_recv,
     k_item_send, k_item_recv, k_core_send, k_core_recv, k_chip_send, k_chip_recv, k_final_send, k_final_recv,
     s_core_send, s_core_recv, s_item_send, s_item_recv, s_chip_send, s_chip_recv, s_final_send,
     s_final_recv) = refs
    grid = Grid(items, n)
    item, me = grid.item, grid.me
    rows_dev, width, channels = image.shape
    pixels = rows_dev * width
    heads, head_dim, wide = HEADS, channels // HEADS, 3 * channels // HEADS
    share = channels // n
    base = me * rows_dev
    count = (info[0, 0] * info[0, 1]).astype(F32) * (channels // GROUPS)
    scale, shift = shifts[:, :channels], shifts[:, channels:]

    def inside(row):
        return window(info, 0, row, (width, channels))

    fetched = []

    def fetch(src, dst):
        c = pltpu.make_async_copy(src, dst, load.at[len(fetched)])
        c.start()
        fetched.append(c)
        return c

    got_query = fetch(query_part, acc)
    got_dkv = fetch(dkv_in, dkv)
    got_turned = fetch(turned_in, qkv_turned)
    got_mid = fetch(middle, mid_v)
    got_cot = fetch(cot, cot_v)
    got_w2 = fetch(w2_in, weight)
    got_first = fetch(first, first_v)
    got_attn = fetch(attn_in, attn)
    got_side = fetch(side_in, side_total.at[:, :, 2 * channels :])
    got_dt = fetch(dt_in, dtext)
    got_second = fetch(second_all, rows_v)
    got_image = fetch(image, image_v)
    got_cols = fetch(text_cols, cols)
    grid.greet()
    edges = [
        Edges(grid, field, edge_send.at[j], edge_recv.at[j])
        for j, field in enumerate((grad_v, moved_v))
    ]
    for e in edges:
        e.clear()
    same[...] = group_matrix(channels)
    sums = [Sums(grid, own.at[j], slots.at[j], sum_send.at[j], sum_recv.at[j]) for j in range(3)]
    kernel_sums = [
        KernelSum(grid, turned.at[j], quarter.at[j], part.at[j], from_core.at[j], chip_sum.at[j], from_chip.at[j],
                  final.at[j], (k_item_send.at[j], k_item_recv.at[j]), (k_core_send.at[j], k_core_recv.at[j]),
                  (k_chip_send.at[j], k_chip_recv.at[j]), (k_final_send.at[j], k_final_recv.at[j]))
        for j in range(2)
    ]
    sum2, sum1 = kernel_sums
    side = SideSum(grid, side_v, side_core, side_sum, side_item, side_total, side_chip, side_final,
                   (s_core_send, s_core_recv), (s_item_send, s_item_recv), (s_chip_send, s_chip_recv),
                   (s_final_send, s_final_recv))

    core, chip, chips = lax.rem(me, 2), me // 2, n // 2
    half = heads // 2

    def text_copy(k):
        to = lax.rem(me + k, n)
        return remote(dtext.at[to], own_dt.at[me], text_send.at[0, k], text_recv.at[0, k], grid.row(k))

    def gather_copy(k):
        to = {"items": item, "rows": lax.rem(chip + k, chips) * 2 + core}
        return remote(dtext, dt.at[item, core, chip], text_send.at[1, k], text_recv.at[1, k], to)

    def dt_copy(k):
        mine = dt.at[item, core]
        return remote(mine, mine, dt_send.at[k], dt_recv.at[k], grid.peer(k))

    def dt_core_copy(k):
        mine = dt.at[lax.rem(item + k, items), core]
        sibling = {"items": item, "rows": me + 1 - 2 * core}
        return remote(mine, mine, dt_core_send.at[k], dt_core_recv.at[k], sibling)

    got_turned.wait()
    got_dkv.wait()
    got_query.wait()

    def unproject_head(h):
        rows = pl.ds(pl.multiple_of(h * wide + head_dim, head_dim), 2 * head_dim)
        acc[...] += dot(dkv[h].astype(F32).T.astype(BF16), qkv_turned[rows], 1, 0)

    each_row(heads, unproject_head)
    got_mid.wait()
    average, inverse = norm_of(stats_in[2], count, same[...])

    def grad_row(r):
        value = acc[pl.ds(r * width, width)] * inside(base + r)
        grad_v[1 + r] = value
        return value, value * ((mid_v[1 + r] - average) * inverse)

    stats = row_stats(rows_dev, width, channels, grad_row)
    grid.met()
    sums[0].start(stats)
    edges[0].start()


    got_attn.wait()

    def qkv_head(h):
        block = dot(dkv[h], attn[...], 1, 0).astype(BF16)
        for w in range(2):
            side.put_head(h, block[w * head_dim : (w + 1) * head_dim], w)

    each_row(heads, qkv_head)
    side.core_copy().start()
    got_cot.wait()

    stats4 = sums[0].result()
    got_dt.wait()
    grid.loop(n, lambda k: text_copy(k).start())
    grid.loop(chips, lambda k: gather_copy(k).start())
    own_dt[me] = dtext[me]
    dt[item, core, chip] = dtext[...]
    mean, cross = means_of(stats4, gain3[...], count, same[...])
    edges[0].wait()

    def to_grad2(r):
        normal = (mid_v[r] - average) * inverse
        ok = inside(base + r - 1)
        term = (grad_v[r] * gain3[...] - mean - normal * cross) * inverse * ok
        total = cot_v[r].astype(F32) + term
        grad_mid[r] = total
        shift_into(shifted, r, total * ok)

    each_row(rows_dev + 2, to_grad2)
    sum2.send_grads(shifted)
    got_w2.wait()
    conv_taps_back(shifted, weight, acc, rows_dev)
    got_first.wait()
    average2, inverse2 = norm_of(stats_in[1], count, same[...])

    def moved_row(r):
        ok = inside(base + r)
        normal, moved = moved_of(first_v[1 + r], ok, average2, inverse2, gain2[...], scale, shift)
        value = acc[pl.ds(r * width, width)] * ok * silu_slope(moved)
        moved_v[1 + r] = value
        return value, value * normal

    stats = row_stats(rows_dev, width, channels, moved_row)
    sums[1].start(stats)
    edges[1].start()
    got_w1 = fetch(w1_in, weight)
    got_second.wait()

    def shift_rows():
        for g in range(items):
            each_row(rows_dev + 2, lambda r: shift_into(shifted_all.at[g], r, rows_v[g, r].astype(F32)))

    shift_rows()
    got_hidden = fetch(hidden_all, rows_v)
    sum2.wait_grads()
    side.over_items()
    sum2.compute(0, shifted_all)
    sum2.compute(1, shifted_all)
    sum2.over_chips(0)
    sum2.compute(2, shifted_all)
    sum2.over_chips(1)
    sum2.over_chips(2)

    stats5 = sums[1].result()
    factor = gain2[...] * (1.0 + scale)
    mean, cross = means_of(stats5, factor, count, same[...])
    edges[1].wait()

    def to_grad1(r):
        normal = (first_v[r] - average2) * inverse2
        value = (moved_v[r] * factor - mean - normal * cross) * inverse2
        shift_into(shifted, r, value * inside(base + r - 1))

    each_row(rows_dev + 2, to_grad1)
    sum1.send_grads(shifted)
    got_w1.wait()
    conv_taps_back(shifted, weight, acc, rows_dev)
    got_image.wait()
    average1, inverse1 = norm_of(stats_in[0], count, same[...])

    def pre_row(r):
        ok = inside(base + r)
        normal = (image_v[r].astype(F32) - average1) * inverse1 * ok
        value = acc[pl.ds(r * width, width)] * ok * silu_slope(normal * gain1[...])
        pre[r] = value
        return value, value * normal

    stats = row_stats(rows_dev, width, channels, pre_row)
    sums[2].start(stats)
    tall = text_in.shape[0]
    got_text_w = [
        fetch(text_in.at[:, j * channels : (j + 1) * channels], weight.at[j * tall : (j + 1) * tall])
        for j in range(2)
    ]
    got_side.wait()
    side.over_chips()
    got_hidden.wait()
    shift_rows()
    sum1.wait_grads()
    grid.loop(chips, lambda k: gather_copy(k).wait())
    grid.loop(items, lambda k: dt_copy(k).start())
    dt_core_copy(0).start()
    sum1.compute(0, shifted_all)
    sum2.over_items(0)
    sum1.over_chips(0)
    sum1.compute(1, shifted_all)
    sum2.over_items(1)
    sum1.over_chips(1)
    sum1.compute(2, shifted_all)
    sum1.over_chips(2)
    sum2.over_items(2)
    side.spread()
    grid.loop(items, lambda k: dt_copy(k).wait())
    grid.loop(items, lambda k: dt_core_copy(k).start())

    stats6 = sums[2].result()
    e = embed[...].astype(F32)
    low = (e * sigmoid(e)).astype(BF16).astype(F32)
    vector[...] = jnp.zeros_like(vector)
    vector[0:1] = stats6[1:2]
    vector[1:2] = stats5[1:2] * (1.0 + scale)
    vector[2:3] = stats4[1:2]
    vector[3:4] = (stats5[1:2] * gain2[...]).astype(BF16).astype(F32)
    vector[4:5] = stats5[0:1].astype(BF16).astype(F32)
    for j in range(embed.shape[1] // channels):
        vector[5 + j : 6 + j] = low[:, j * channels : (j + 1) * channels]

    def vector_copy(k):
        return remote(
            vector, vector_land.at[item], vec_send.at[k], vec_recv.at[k], grid.peer(k)
        )

    grid.loop(items, lambda k: vector_copy(k).start())
    vector_land[item] = vector[...]

    mean, cross = means_of(stats6, gain1[...], count, same[...])

    def finish_row(r):
        normal = (image_v[r].astype(F32) - average1) * inverse1
        term = (pre[r] * gain1[...] - mean - normal * cross) * inverse1
        image_out[r] = (grad_mid[1 + r] + term) * inside(base + r)

    each_row(rows_dev, finish_row)
    put_image = fetch(image_out, image_grad)

    grid.loop(n, lambda k: text_copy(k).wait())
    for c in got_text_w:
        c.wait()
    total = None
    for j in range(2):
        lhs = jnp.concatenate([own_dt[j * half + h] for h in range(half)], axis=1)
        term = dot(lhs, weight[j * tall : (j + 1) * tall], 1, 1)
        total = term if total is None else total + term
    text_v[...] = total
    put_text = fetch(text_v, text_grad)
    got_embed_w = [
        fetch(embed_in.at[:, j * channels : (j + 1) * channels], weight.at[j * tall : (j + 1) * tall])
        for j in range(2)
    ]
    for a in range(3):
        sum1.over_items(a)
    for a in range(3):
        sum2.wait_final(a)
    put_final2 = fetch(final.at[0], final_out.at[0])

    dt_core_copy(0).wait()
    grid.loop(items, lambda k: dt_core_copy(k).wait())
    got_cols.wait()
    tokens = cols.shape[0] * cols.shape[1]
    flat_cols = cols[...].reshape(tokens, cols.shape[2]).astype(F32).T.astype(BF16)
    for h in range(heads):
        rhs = jnp.concatenate([dt[g, h % 2, h // 2].reshape(tokens // items, 2 * head_dim) for g in range(items)], axis=0)
        text_w_v[:, h * 2 * head_dim : (h + 1) * 2 * head_dim] = dot(flat_cols, rhs, 1, 0)
    put_text_w = fetch(text_w_v, text_w_grad)

    for c in got_embed_w:
        c.wait()
    total = None
    for j in range(2):
        lhs = vector[3 + j : 4 + j] if j else vector[3:4]
        lhs = jnp.broadcast_to(lhs, (8, channels)).astype(BF16)
        term = dot(lhs, weight[j * tall : (j + 1) * tall], 1, 1)
        total = term if total is None else total + term
    embed_v[...] = total[0:1] * silu_slope(e)
    put_embed = fetch(embed_v, embed_grad)
    grid.loop(items, lambda k: vector_copy(k).wait())
    put_vectors = fetch(vector_land, vectors)
    side.wait_final()
    put_side = fetch(side_final, side_out)
    for a in range(3):
        sum1.wait_final(a)
    put_final1 = fetch(final.at[1], final_out.at[1])
    for c in (put_image, put_text, put_final2, put_text_w, put_embed, put_vectors, put_side, put_final1):
        c.wait()


def finalize_kernel(final, side, vectors, output_in, image_in, text_in, text_w_in, embed_in,
                    output, image_grad, text_grad, text_w_grad, embed_grad, conv2, conv1, qkv, proj, embed_w,
                    gain1, gain2, gain3,
                    final_v, side_v, vector_v, conv_v, qkv_v, proj_v, embed_w_v, output_v, image_v, text_v, text_w_v,
                    embed_v, load):
    started = []

    def fetch(src, dst):
        c = pltpu.make_async_copy(src, dst, load.at[len(started)])
        c.start()
        started.append(c)
        return c

    got = [fetch(final.at[j], final_v.at[j]) for j in range(2)]
    got_vectors = fetch(vectors, vector_v)
    got_side = fetch(side, side_v)
    through = ((image_in, image_v, image_grad), (text_w_in, text_w_v, text_w_grad), (output_in, output_v, output),
               (text_in, text_v, text_grad), (embed_in, embed_v, embed_grad))
    got_through = [fetch(src, held) for src, held, _ in through]
    me = lax.axis_index("rows")
    items, rows, channels = side_v.shape[0], side_v.shape[1], side_v.shape[2] // 4
    share = items * rows
    for j, out in enumerate((conv2, conv1)):
        got[j].wait()
        for a in range(3):
            for b in range(3):
                for q in range(items):
                    conv_v[j, a * 3 + b, q * rows : (q + 1) * rows] = final_v[j, a, q, b].astype(F32)
        fetch(conv_v.at[j], out)
    for c, (_, held, dst) in zip(got_through, through):
        c.wait()
        fetch(held, dst)
    got_vectors.wait()
    total = vector_v[0]
    for g in range(1, items):
        total = total + vector_v[g]
    own = me * share
    block = channels // 4
    part = total[:, :block]
    for j in range(1, 4):
        part = jnp.where(own // block == j, total[:, j * block : (j + 1) * block], part)
    mine = part[:, :share]
    for j in range(1, block // share):
        mine = jnp.where(lax.rem(own, block) == j * share, part[:, j * share : (j + 1) * share], mine)
    for j, out in enumerate((gain1, gain2, gain3)):
        out[...] = mine[j : j + 1]
    wide = embed_w_v.shape[0]
    start = me * wide
    line = lax.broadcasted_iota(jnp.int32, (16, 1), 0)
    lhs = jnp.zeros((16, wide), F32)
    rhs = jnp.zeros((16, 2 * channels), F32)
    for g in range(items):
        row = vector_v[g, pl.ds(5 + start // channels, 1)]
        piece = row[:, :wide]
        for j in range(1, channels // wide):
            piece = jnp.where(lax.rem(start, channels) == j * wide, row[:, j * wide : (j + 1) * wide], piece)
        lhs = jnp.where(line == g, piece, lhs)
        both = jnp.concatenate([vector_v[g, 3:4], vector_v[g, 4:5]], axis=1)
        rhs = jnp.where(line == g, both, rhs)
    embed_w_v[...] = dot(lhs.astype(BF16), rhs.astype(BF16), 0, 0)
    fetch(embed_w_v, embed_w)
    got_side.wait()
    for q in range(items):
        for w in range(3):
            at = (w + 1) % 3 * share + q * rows
            qkv_v[at : at + rows] = side_v[q, :, w * channels : (w + 1) * channels].astype(F32)
        proj_v[q * rows : (q + 1) * rows] = side_v[q, :, 3 * channels :].astype(F32)
    fetch(qkv_v, qkv)
    fetch(proj_v, proj)
    for j, c in enumerate(started):
        if j > 8:
            c.wait()


def finalize_call(arrays, share):
    final, side, vectors, output, image_grad, text_grad, text_w_grad, embed_grad = arrays
    channels = output.shape[-1]
    n = channels // share
    sds = jax.ShapeDtypeStruct
    kernels = (9, share, channels)
    embed_w = (embed_grad.shape[1] // n, 2 * channels)
    outs = [sds(a.shape, a.dtype) for a in arrays[3:]]
    outs += [sds(kernels, F32)] * 2
    outs += [sds((3 * share, channels), F32), sds((share, channels), F32), sds(embed_w, F32)]
    outs += [sds((1, share), F32)] * 3
    v = pltpu.VMEM
    return pl.pallas_call(
        finalize_kernel,
        out_shape=tuple(outs),
        in_specs=[ANYWHERE] * len(arrays),
        out_specs=(ANYWHERE,) * 10 + (WHOLE,) * 3,
        scratch_shapes=[
            v(final.shape, BF16),
            v(side.shape, BF16),
            v(vectors.shape, F32),
            v((2,) + kernels, F32),
            v((3 * share, channels), F32),
            v((share, channels), F32),
            v(embed_w, F32),
            *[v(a.shape, a.dtype) for a in arrays[3:]],
            DMA((24,)),
        ],
        compiler_params=pltpu.CompilerParams(vmem_limit_bytes=62 << 20),
        name="finalize",
    )(*arrays)


def backward_call(info, embed, gains, stats, shifts, arrays, identity):
    items, n = lax.axis_size("items"), lax.axis_size("rows")
    dtext = arrays[3]
    image, text_cols, text_w = arrays[7], arrays[12], arrays[15]
    rows_dev, width, channels = image.shape
    pixels = rows_dev * width
    head_dim = channels // HEADS
    share = channels // n
    rows = share // items
    chips = n // 2
    padded = (rows_dev + 2, width, channels)
    tokens = dtext.shape[1]
    sds = jax.ShapeDtypeStruct
    outs = (
        sds(image.shape, F32),
        sds((tokens, text_w.shape[0]), F32),
        sds((text_w.shape[0] // n, 2 * channels), F32),
        sds(embed.shape, F32),
        sds((2, 3, items, 3, rows, channels), BF16),
        sds((items, rows, 4 * channels), BF16),
        sds((items, 16, channels), F32),
    )
    v = pltpu.VMEM
    scratch = [
        v((9 * channels, channels), BF16),
        v((3 * channels, channels), BF16),
        v(padded, F32),
        v(padded, F32),
        v(padded, BF16),
        v(image.shape, BF16),
        v((pixels, channels), BF16),
        v(text_cols.shape, BF16),
        v((items,) + padded, BF16),
        v((n, 2 * head_dim, pixels), BF16),
        v(dtext.shape, BF16),
        v((items, 2, chips) + dtext.shape, BF16),
        v(dtext.shape, BF16),
        v(padded, F32),
        v(padded, F32),
        v(padded, F32),
        v(image.shape, F32),
        v((pixels, channels), F32),
        v((rows_dev + 2, width, 3 * channels), BF16),
        v((items, rows_dev + 2, width, 3 * channels), BF16),
        v(image.shape, F32),
        v((tokens, text_w.shape[0]), F32),
        v((text_w.shape[0] // n, 2 * channels), F32),
        v(embed.shape, F32),
        v((channels, channels), BF16),
        v((2, items, channels // items, pixels), BF16),
        v((2, items, channels // items, pixels), BF16),
        v((2, 3, 2, 3, chips * rows, channels), BF16),
        v((2, 3, 3, chips * rows, channels), BF16),
        v((2, 3, chips, 3, rows, channels), BF16),
        v((2, 3, chips, 3, rows, channels), BF16),
        v((2, 3, items, 3, rows, channels), BF16),
        v((2, chips, items, rows, 2 * channels), BF16),
        v((chips, items, rows, 2 * channels), BF16),
        v((items, chips, rows, 2 * channels), BF16),
        v((items, chips, rows, 2 * channels), BF16),
        v((chips, rows, 4 * channels), BF16),
        v((chips, rows, 4 * channels), BF16),
        v((items, rows, 4 * channels), BF16),
        v((16, channels), F32),
        v((items, 16, channels), F32),
        v((3, channels // 64, 128), F32),
        v((3, n, channels // 64, 128), F32),
        DMA((32,)),
        DMA((3, n)),
        DMA((3, n)),
        DMA((2, 2)),
        DMA((2, 2)),
        DMA((2, n)),
        DMA((2, n)),
        DMA((items,)),
        DMA((items,)),
        DMA((items,)),
        DMA((items,)),
        DMA((items,)),
        DMA((items,)),
        DMA((2, items)),
        DMA((2, items)),
        DMA((2, 3)),
        DMA((2, 3)),
        DMA((2, 3, chips)),
        DMA((2, 3, chips)),
        DMA((2, 3, items)),
        DMA((2, 3, items)),
        DMA((1,)),
        DMA((1,)),
        DMA((items,)),
        DMA((items,)),
        DMA((chips,)),
        DMA((chips,)),
        DMA((items,)),
        DMA((items,)),
    ]
    return pl.pallas_call(
        functools.partial(backward_kernel, items, n),
        out_shape=outs,
        in_specs=[SCALARS] + [WHOLE] * 6 + [ANYWHERE] * len(arrays),
        out_specs=(ANYWHERE,) * 7,
        scratch_shapes=scratch,
        compiler_params=pltpu.CompilerParams(
            collective_id=identity, has_side_effects=True, vmem_limit_bytes=62 << 20
        ),
        cost_estimate=pl.CostEstimate(
            flops=80 * pixels * channels * channels, bytes_accessed=60 << 20, transcendentals=0
        ),
        name="backward",
    )(info, embed, *gains, stats, shifts, *arrays)


def own_shards(
    extent, image, embed, text, gain1, conv1_w, embed_w, gain2, conv2_w, gain3, qkv_w, text_w, proj_w,
    cotangent,
):
    _, rows_dev, width, channels = image.shape
    items, parts = lax.axis_size("items"), lax.axis_size("rows")
    me = lax.axis_index("rows")
    head_dim = channels // HEADS
    tokens = text.shape[1]
    share = channels // parts
    (first, middle, cot, hidden_all, second_all, attn_flat, qkv_turned, output, query_part, side_part, dkv, dtext,
     text_cols, stats, shifts) = forward_call(
        extent,
        image[0],
        cotangent[0],
        text[0],
        embed,
        (gain1, gain2, gain3),
        (
            conv1_w.reshape(3, 3 * channels, channels),
            conv2_w.reshape(3, 3 * channels, channels),
            embed_w,
            text_w,
            qkv_w,
            proj_w,
        ),
        0,
    )
    text_w_rows = text_cols.shape[3]
    image_grad, text_grad, text_w_grad, embed_grad, final, side, vectors = backward_call(
        extent,
        embed,
        (gain1, gain2, gain3),
        stats,
        shifts,
        (
            query_part,
            side_part,
            dkv,
            dtext,
            first,
            middle,
            cot,
            image[0],
            hidden_all,
            second_all,
            attn_flat,
            qkv_turned,
            text_cols.reshape(items * parts, tokens, text_w_rows),
            conv1_w.reshape(9 * channels, channels),
            conv2_w.reshape(9 * channels, channels),
            text_w,
            embed_w,
        ),
        1,
    )
    (output, image_grad, text_grad, text_w_grad, embed_grad, conv2, conv1, qkv, proj, embed_w_grad, norm1, norm2,
     norm3) = finalize_call(
        (final, side, vectors, output, image_grad, text_grad, text_w_grad, embed_grad), share
    )

    def kernel(values):
        return jnp.swapaxes(values.reshape(3, 3, share, channels), 2, 3)

    return (
        output[None],
        image_grad[None],
        embed_grad,
        text_grad[None],
        norm1[0],
        kernel(conv1),
        embed_w_grad,
        norm2[0],
        kernel(conv2),
        norm3[0],
        qkv.T,
        text_w_grad,
        proj.T,
    )


def shards(
    image, embed, text, extent, first_norm_gain1, conv1_w, embed_w, second_norm_gain2, conv2_w,
    attention_norm_gain, qkv_w, text_w, proj_w, cotangent,
):
    images, rows_dev, width, channels = image.shape
    parts = lax.axis_size("rows")
    me = lax.axis_index("rows")
    pairs = images * HEADS // parts
    head_dim = channels // HEADS
    pixels = rows_dev * width
    group = max(1, 512 // pixels)
    span = group * pixels
    chunks = parts // group
    tokens = text.shape[1]
    first_row = jnp.full((images, 1), me * rows_dev, jnp.int32)
    info = jnp.concatenate([extent, first_row], axis=1)
    gain1 = first_norm_gain1.reshape(1, channels)
    gain2 = second_norm_gain2.reshape(1, channels)
    gain3 = attention_norm_gain.reshape(1, channels)
    rowpos = me * rows_dev + jnp.arange(rows_dev, dtype=jnp.int32)
    colpos = jnp.arange(width, dtype=jnp.int32)
    inside = (rowpos[None, :, None] < extent[:, 0, None, None]) & (
        colpos[None, None, :] < extent[:, 1, None, None]
    )
    image_window = inside.astype(F32)[..., None]

    items = lax.axis_size("items")
    own_path = (
        images == 1
        and parts == HEADS
        and channels % (16 * items * parts) == 0
        and parts == 8
        and pixels % 512 == 0
        and channels % 512 == 0
        and tokens % 16 == 0
        and text.shape[2] % (128 * parts) == 0
        and text.shape[2] == embed.shape[1] <= 4 * channels
    )
    if own_path:
        return own_shards(
            extent, image, embed, text, gain1, conv1_w, embed_w, gain2, conv2_w, gain3, qkv_w, text_w,
            proj_w, cotangent,
        )

    embed_float = embed.astype(F32)
    embed_low = jax.nn.silu(embed_float).astype(BF16)
    shifts = jnp.dot(embed_low, embed_w, preferred_element_type=F32)
    qkv_turned = qkv_w.T
    proj_shaped = proj_w.reshape(HEADS, head_dim, channels)

    start = image.astype(F32) * image_window
    zeros = jnp.zeros((images, 6, channels), F32)
    stats0 = jnp.concatenate(
        [
            jnp.sum(start, axis=(1, 2))[:, None],
            jnp.sum(start * start, axis=(1, 2))[:, None],
            zeros,
        ],
        axis=1,
    )
    stats1, image_above, image_below, cot_above, cot_below = exchange(
        stats0, (image, cotangent), 0
    )
    full = jax.ShapeDtypeStruct(image.shape, F32)
    sums = jax.ShapeDtypeStruct((images, 8, channels), F32)
    padded = jax.ShapeDtypeStruct((images, rows_dev + 2, width, channels), BF16)
    first, stats, hidden = conv_call(
        conv1_kernel,
        info,
        (image, image_above, image_below, stats1, gain1),
        conv1_w,
        (full, sums, padded),
        False,
    )
    stats2, first_above, first_below, all_text = exchange(stats, (first,), 1, (text,))
    gathered_text = jnp.moveaxis(all_text, 0, 1).reshape(images, parts * tokens, text.shape[2])
    text_share = text.shape[2] // parts
    text_cols = lax.dynamic_slice_in_dim(gathered_text, me * text_share, text_share, 2)
    text_cols = lax.all_gather(text_cols, "items", axis=0, tiled=True)
    middle, stats, second = conv_call(
        conv2_kernel,
        info,
        (first, first_above, first_below, stats2, gain2, shifts, image),
        conv2_w,
        (full, sums, padded),
        False,
    )
    stats3, mid_above, mid_below = exchange(stats, (middle,), 2)
    attn_flat, qkv_pix = project(info, middle, stats3, gain3, qkv_turned)

    def to_pairs(values):
        wide = values.shape[1]
        moved = lax.all_to_all(values, "rows", split_axis=0, concat_axis=0, tiled=True)
        moved = moved.reshape(chunks, group, pairs, wide, pixels)
        return jnp.transpose(moved, (2, 0, 3, 1, 4)).reshape(pairs, chunks, wide, span)

    def from_pairs(values):
        wide = values.shape[2]
        moved = values.reshape(pairs, chunks, wide, group, pixels)
        moved = jnp.transpose(moved, (1, 3, 0, 2, 4)).reshape(parts * pairs, wide, pixels)
        return lax.all_to_all(moved, "rows", split_axis=0, concat_axis=0, tiled=True)

    qkv_pair = to_pairs(qkv_pix)
    grad_proj = (cotangent.astype(F32) * image_window).astype(BF16).reshape(images, pixels, channels)
    grad_heads = jnp.einsum(
        "ipc,hdc->ihdp", grad_proj, proj_shaped, preferred_element_type=F32
    ).astype(BF16)
    grad_pair = to_pairs(grad_heads.reshape(images * HEADS, head_dim, pixels))
    pair_results = []
    for p in range(pairs):
        pair = me * pairs + p
        item, head = pair // HEADS, pair % HEADS
        weight = lax.dynamic_slice_in_dim(text_w, head * 2 * head_dim, 2 * head_dim, 1)
        own = lax.dynamic_index_in_dim(gathered_text, item, 0, False)
        text_pair = jnp.dot(own, weight, preferred_element_type=F32).astype(BF16)
        pair_extent = lax.dynamic_slice_in_dim(extent, item, 1, 0)
        pair_results.append(attention(pair_extent, qkv_pair[p], text_pair, grad_pair[p], width))
    attended, qkv_grad_pair, text_grad_pair = (jnp.stack(r) for r in zip(*pair_results))
    qkv_back = from_pairs(qkv_grad_pair)
    heads_out = from_pairs(attended).reshape(images, HEADS, head_dim, pixels)

    attn_grad, stats = unproject(info, middle, stats3, qkv_back, qkv_turned)
    stats4, grad_above, grad_below, text_back = exchange(stats, (attn_grad,), 3, (text_grad_pair,))
    text_back = text_back.reshape(images, HEADS, parts * tokens, 2 * head_dim)
    text_all = lax.all_gather(text_back, "items", axis=0, tiled=True)
    proj_grad = jnp.einsum("ipc,ihdp->chd", grad_proj, heads_out, preferred_element_type=F32)
    qkv_grad = jnp.einsum(
        "ihwdp,ipc->hdwc",
        qkv_back.reshape(images, HEADS, 3, head_dim, pixels),
        attn_flat,
        preferred_element_type=F32,
    )
    grad_middle, moved_grad, stats, conv2_grad = conv_call(
        back2_kernel,
        info,
        (attn_grad, grad_above, grad_below, middle, mid_above, mid_below, cotangent, cot_above,
         cot_below, stats3, stats4, gain3, first, stats2, gain2, shifts),
        conv2_w,
        (full, full, sums, padded),
        True,
    )
    stats5, moved_above, moved_below = exchange(stats, (moved_grad,), 4)
    pre_grad, stats, conv1_grad = conv_call(
        back1_kernel,
        info,
        (moved_grad, moved_above, moved_below, first, first_above, first_below, stats2, stats5,
         gain2, shifts, image, stats1, gain1),
        conv1_w,
        (full, sums, padded),
        True,
    )
    (stats6,) = exchange(stats, (), 5)
    image_grad = finish(info, pre_grad, stats6, image, stats1, gain1, grad_middle)

    projected = jnp.einsum(
        "ihdp,hdc->ipc", heads_out, proj_shaped, preferred_element_type=F32
    ).reshape(image.shape)
    output = (middle + projected * image_window).astype(BF16)
    own_text = lax.dynamic_slice_in_dim(text_back, me * tokens, tokens, 2)
    text_shaped = text_w.reshape(text_w.shape[0], HEADS, 2 * head_dim)
    text_grad = jnp.einsum("ihtk,chk->itc", own_text, text_shaped, preferred_element_type=F32)
    text_w_grad = jnp.einsum(
        "gtc,ghtk->chk", text_cols, text_all, preferred_element_type=F32
    ).reshape(text_share, 2 * channels)
    scale_sum = stats5[:, 1] * gain2
    grad_shifts = jnp.concatenate([scale_sum, stats5[:, 0]], axis=1).astype(BF16)
    embed_grad = jnp.einsum(
        "ik,ck->ic", grad_shifts, embed_w, preferred_element_type=F32
    ) * silu_slope(embed_float)
    embed_share = embed_w.shape[0] // parts
    gains = jnp.stack(
        [
            jnp.sum(stats6[:, 1], axis=0),
            jnp.sum(stats5[:, 1] * (1.0 + shifts[:, :channels]), axis=0),
            jnp.sum(stats4[:, 1], axis=0),
        ]
    )
    share = channels // parts
    def total(values):
        return lax.psum(
            lax.psum_scatter(values.astype(BF16), "rows", scatter_dimension=0, tiled=True),
            "items",
        ).astype(F32)

    def kernel_total(values):
        return total(values).T.reshape(3, 3, channels, share)

    conv1_total = kernel_total(weight_grad(conv1_grad, hidden))
    conv2_total = kernel_total(weight_grad(conv2_grad, second))
    by_head = jnp.swapaxes(qkv_grad, 1, 2).reshape(3 * channels, channels)
    qkv_total = total(by_head).T
    proj_total = total(proj_grad.reshape(channels, channels)).T
    gains = lax.psum(gains, "items")
    all_shifts = lax.all_gather(grad_shifts, "items", axis=0, tiled=True)
    embed_rows = lax.dynamic_slice_in_dim(embed_low, me * embed_share, embed_share, 1)
    embed_rows = lax.all_gather(embed_rows, "items", axis=0, tiled=True)
    embed_w_grad = jnp.einsum("ic,ik->ck", embed_rows, all_shifts, preferred_element_type=F32)
    gains = lax.dynamic_slice_in_dim(gains, me * share, share, 1)
    return (
        output,
        image_grad,
        embed_grad,
        text_grad,
        gains[0],
        conv1_total,
        embed_w_grad,
        gains[1],
        conv2_total,
        gains[2],
        qkv_total,
        text_w_grad,
        proj_total,
    )


def solution(mesh):
    in_specs = (
        P("items", "rows", None, None),
        P("items", None),
        P("items", "rows", None),
        P("items", None),
        P(),
        P(),
        P(),
        P(),
        P(),
        P(),
        P(),
        P(),
        P(),
        P("items", "rows", None, None),
    )
    out_specs = (
        P("items", "rows", None, None),
        P("items", "rows", None, None),
        P("items", None),
        P("items", "rows", None),
        P("rows"),
        P(None, None, None, "rows"),
        P("rows", None),
        P("rows"),
        P(None, None, None, "rows"),
        P("rows"),
        P(None, "rows"),
        P("rows", None),
        P(None, "rows"),
    )
    return jax.shard_map(shards, mesh=mesh, in_specs=in_specs, out_specs=out_specs, check_vma=False)
```

```python
import functools

import jax
import jax.numpy as jnp
from jax import lax
from jax.experimental import pallas as pl
from jax.experimental.pallas import tpu as pltpu
from jax.sharding import PartitionSpec as P

GROUPS = 32
HEADS = 8
F32, BF16 = jnp.float32, jnp.bfloat16
NEG = -1e30


def dot(a, b, ca, cb):
    return lax.dot_general(a, b, (((ca,), (cb,)), ((), ())), preferred_element_type=F32)

def nothing(*_):
    return None


class Attention:
    def __init__(self, chunks, span, d, tlen, step, bq, scratch):
        self.chunks, self.span, self.d, self.tlen, self.step, self.bq = chunks, span, d, tlen, step, bq
        self.kn, self.vn, self.kt, self.vt, s0, s1, e0, e1, self.dkt, self.dvt = scratch
        self.scores, self.raised = (s0, s1), (e0, e1)
        self.pix = chunks * span

    def stage_key(self, c, k, width, rows_ok, cols_ok):
        d, span = self.d, self.span
        base = pl.multiple_of(c * span, span)
        pos = base + lax.broadcasted_iota(jnp.int32, (16, span), 1)
        row = lax.broadcasted_iota(jnp.int32, (16, span), 0)
        ok = (pos // width < rows_ok) & (pos % width < cols_ok)
        extra = jnp.where((row == 0) & jnp.logical_not(ok), NEG, 0.0)
        rest = jnp.zeros((128 - d - 16, span), F32)
        self.kt[:, pl.ds(base, span)] = k
        ka = jnp.concatenate([k.astype(F32), extra, rest], axis=0)
        self.kn[pl.ds(base, span), :] = ka.T.astype(BF16)

    def stage_value(self, c, v):
        d, span = self.d, self.span
        base = pl.multiple_of(c * span, span)
        row = lax.broadcasted_iota(jnp.int32, (16, span), 0)
        rest = jnp.zeros((128 - d - 16, span), F32)
        self.vt[:, pl.ds(base, span)] = v
        va = jnp.concatenate([v.astype(F32), jnp.where(row < 3, 1.0, 0.0), rest], axis=0)
        self.vn[pl.ds(base, span), :] = va.T.astype(BF16)

    def stage_text(self, text):
        d, tlen, pix = self.d, self.tlen, self.pix
        tk = text[:, :d].astype(F32)
        tv = text[:, d:].astype(F32)
        self.kt[:, pix:] = tk.T.astype(BF16)
        self.vt[:, pix:] = tv.T.astype(BF16)
        lanes = lax.broadcasted_iota(jnp.int32, (tlen, 128 - d), 1)
        rest = jnp.zeros((tlen, 128 - d), F32)
        self.kn[pix:, :] = jnp.concatenate([tk, rest], axis=1).astype(BF16)
        ones = jnp.where(lanes < 3, 1.0, 0.0)
        self.vn[pix:, :] = jnp.concatenate([tv, ones], axis=1).astype(BF16)

    def query(self, q):
        d, bq = self.d, self.bq
        r = lax.broadcasted_iota(jnp.int32, (128 - d, bq), 0)
        rest = jnp.where(r == 0, 1.0, 0.0)
        return jnp.concatenate([q.astype(F32) * (d**-0.5), rest], axis=0).astype(BF16)

    def run(self, score, exp, back):
        d, bq, step = self.d, self.bq, self.step
        kn, vn, kt, vt, dkt, dvt = self.kn, self.vn, self.kt, self.vt, self.dkt, self.dvt
        scores, raised = self.scores, self.raised

        def body(j, carry):
            pk, total, acc, dq = carry
            at = pl.ds(pl.multiple_of(j * step, step), step)
            if score:
                slot, qa = score
                s = dot(kn[at, :], qa, 1, 0)
                scores[slot][at, :] = s
                pk = jnp.maximum(pk, jnp.max(s.reshape(step // 8, 8, bq), axis=0))
            if exp:
                slot, peak = exp
                e = jnp.exp(scores[slot][at, :] - peak)
                total = total + jnp.sum(e.reshape(step // 8, 8, bq), axis=0)
                low = e.astype(BF16)
                raised[slot][at, :] = low
                acc = acc + dot(vt[:, at], low, 1, 0)
            if back:
                slot, goa, q = back
                dp = dot(vn[at, :], goa, 1, 0)
                e = raised[slot][at, :]
                ds = (e.astype(F32) * dp).astype(BF16)
                dvt[:, at] += dot(goa[:d], e, 1, 1)
                dkt[:, at] += dot(q, ds, 1, 1)
                dq = dq + dot(kt[:, at], ds, 1, 0)
            return pk, total, acc, dq

        init = (
            jnp.full((8, bq), -3e38, F32),
            jnp.zeros((8, bq), F32),
            jnp.zeros((d, bq), F32),
            jnp.zeros((d, bq), F32),
        )
        return lax.fori_loop(0, (self.pix + self.tlen) // step, body, init)

    def attended(self, go, total, acc):
        d, bq = self.d, self.bq
        inv = 1.0 / jnp.sum(total, axis=0, keepdims=True)
        o = acc * inv
        go = go.astype(F32)
        nd = -jnp.sum(go * o, axis=0, keepdims=True) * inv
        hi = nd.astype(BF16).astype(F32)
        mid = (nd - hi).astype(BF16).astype(F32)
        lo = nd - hi - mid
        r = lax.broadcasted_iota(jnp.int32, (16, bq), 0)
        extra = jnp.where(r == 0, hi, jnp.where(r == 1, mid, jnp.where(r == 2, lo, 0.0)))
        rest = jnp.zeros((128 - d - 16, bq), F32)
        return o.astype(BF16), jnp.concatenate([go * inv, extra, rest], axis=0).astype(BF16)

    def attend(self, q_ref, go_ref, o_ref, dq_ref, order, before=nothing, done=nothing):
        d, bq, chunks = self.d, self.bq, self.chunks
        self.dkt[...] = jnp.zeros_like(self.dkt)
        self.dvt[...] = jnp.zeros_like(self.dvt)

        def columns(half):
            return slice(half * bq, (half + 1) * bq)

        def q_of(h, half):
            return q_ref[order(h), :d, columns(half)]

        def finish_exp(h, half, total, acc):
            c = order(h)
            o, goa = self.attended(go_ref[c, :, columns(half)], total, acc)
            o_ref[c, :, columns(half)] = o
            return goa

        def put_dq(h, half, dq):
            dq_ref[order(h), :d, columns(half)] = (dq * (d**-0.5)).astype(BF16)

        def top(pk):
            return jnp.max(pk, axis=0, keepdims=True)

        run = self.run
        pk, _, _, _ = run((0, self.query(q_of(0, 0))), None, None)
        pk, total, acc, _ = run((1, self.query(q_of(0, 1))), (0, top(pk)), None)
        goa = finish_exp(0, 0, total, acc)

        def two(h, carry):
            pk, goa = carry
            before(h + 1)
            qa = self.query(q_of(h + 1, 0))
            pk2, total, acc, dq = run((0, qa), (1, top(pk)), (0, goa, q_of(h, 0)))
            put_dq(h, 0, dq)
            goa = finish_exp(h, 1, total, acc)
            qa = self.query(q_of(h + 1, 1))
            pk3, total, acc, dq = run((1, qa), (0, top(pk2)), (1, goa, q_of(h, 1)))
            put_dq(h, 1, dq)
            done(h)
            return pk3, finish_exp(h + 1, 0, total, acc)

        pk, goa = lax.fori_loop(0, chunks - 1, two, (pk, goa))
        last = chunks - 1
        _, total, acc, dq = run(None, (1, top(pk)), (0, goa, q_of(last, 0)))
        put_dq(last, 0, dq)
        goa = finish_exp(last, 1, total, acc)
        _, _, _, dq = run(None, None, (1, goa, q_of(last, 1)))
        put_dq(last, 1, dq)
        done(last)

    def key_grad(self, at):
        return (self.dkt[:, at] * (self.d**-0.5)).astype(BF16)

    def value_grad(self, at):
        return self.dvt[:, at].astype(BF16)

    def text_grad(self, out):
        d, pix = self.d, self.pix
        out[:, :d] = (self.dkt[:, pix:] * (d**-0.5)).T.astype(BF16)
        out[:, d:] = self.dvt[:, pix:].T.astype(BF16)


def attention_scratch(chunks, span, d, tlen):
    keys = chunks * span + tlen
    bq = span // 2
    lanes = keys // 128
    step = 128 * max(n for n in range(1, 12) if lanes % n == 0)
    shapes = [((keys, 128), BF16)] * 2 + [((d, keys), BF16)] * 2
    shapes += [((keys, bq), F32)] * 2 + [((keys, bq), BF16)] * 2 + [((d, keys), F32)] * 2
    return step, bq, [pltpu.VMEM(*shape) for shape in shapes]


def attention_kernel(width, step, bq, ext_ref, qkv_ref, text_ref, go_ref, out_ref, dqkv_ref, dtext_ref, *scratch):
    chunks, _, span = qkv_ref.shape
    d = go_ref.shape[1]
    att = Attention(chunks, span, d, text_ref.shape[0], step, bq, scratch)

    def stage(c, carry):
        att.stage_key(c, qkv_ref[c, d : 2 * d, :], width, ext_ref[0, 0], ext_ref[0, 1])
        att.stage_value(c, qkv_ref[c, 2 * d :, :])
        return carry

    lax.fori_loop(0, chunks, stage, 0)
    att.stage_text(text_ref)
    att.attend(qkv_ref, go_ref, out_ref, dqkv_ref, lambda h: h)

    def finish(c, carry):
        at = pl.ds(pl.multiple_of(c * span, span), span)
        dqkv_ref[c, d : 2 * d, :] = att.key_grad(at)
        dqkv_ref[c, 2 * d :, :] = att.value_grad(at)
        return carry

    lax.fori_loop(0, chunks, finish, 0)
    att.text_grad(dtext_ref)


def attention(ext, qkv, text, go, width):
    chunks, wide, span = qkv.shape
    d = wide // 3
    tlen = text.shape[0]
    keys = chunks * span + tlen
    step, bq, scratch = attention_scratch(chunks, span, d, tlen)
    vm = pl.BlockSpec(memory_space=pltpu.VMEM)
    flops = 2 * 6 * chunks * span * keys * d
    return pl.pallas_call(
        functools.partial(attention_kernel, width, step, bq),
        out_shape=(
            jax.ShapeDtypeStruct(go.shape, BF16),
            jax.ShapeDtypeStruct(qkv.shape, BF16),
            jax.ShapeDtypeStruct((tlen, 2 * d), BF16),
        ),
        in_specs=[pl.BlockSpec(memory_space=pltpu.SMEM), vm, vm, vm],
        out_specs=(vm, vm, vm),
        scratch_shapes=scratch,
        compiler_params=pltpu.CompilerParams(vmem_limit_bytes=56 << 20),
        cost_estimate=pl.CostEstimate(
            flops=4 * flops, bytes_accessed=16 * chunks * span * d, transcendentals=chunks * span * keys
        ),
    )(ext, qkv, text, go)


MESH = pl.DeviceIdType.MESH
EPS = 1e-05
WHOLE = pl.BlockSpec(memory_space=pltpu.VMEM)
SCALARS = pl.BlockSpec(memory_space=pltpu.SMEM)
ANYWHERE = pl.BlockSpec(memory_space=pl.ANY)


def exchange_kernel(n, count, gathers, *refs):
    inputs, refs = refs[: 1 + count + gathers], refs[1 + count + gathers :]
    outputs, refs = refs[: 1 + 2 * count + gathers], refs[1 + 2 * count + gathers :]
    stats_ref, rows, given = inputs[0], inputs[1 : 1 + count], inputs[1 + count :]
    total_ref, outs, gathered = outputs[0], outputs[1 : 1 + 2 * count], outputs[1 + 2 * count :]
    slots, lands = refs[0], refs[1 : 1 + 2 * count]
    send, recv, row_send, row_recv, own = refs[1 + 2 * count :]
    me = lax.axis_index("rows")
    barrier = pltpu.get_barrier_semaphore()

    def greet(k, carry):
        pl.semaphore_signal(
            barrier, inc=1, device_id={"rows": lax.rem(me + k, n)}, device_id_type=MESH
        )
        return carry

    lax.fori_loop(1, n, greet, 0)
    slots[me] = stats_ref[...]
    pl.semaphore_wait(barrier, n - 1)
    shared = [(stats_ref, slots)] + list(zip(given, gathered))

    def share(j, k):
        return pltpu.make_async_remote_copy(
            src_ref=shared[j][0],
            dst_ref=shared[j][1].at[me],
            send_sem=send.at[j, k],
            recv_sem=recv.at[j, k],
            device_id={"rows": lax.rem(me + k, n)},
            device_id_type=MESH,
        )

    def start(k, carry):
        share(0, k).start()
        return carry

    lax.fori_loop(1, n, start, 0)

    def row_copy(j, side):
        last = rows[j].shape[1] - 1
        at = last if side == 0 else 0
        return pltpu.make_async_remote_copy(
            src_ref=rows[j].at[:, at : at + 1],
            dst_ref=lands[2 * j + side],
            send_sem=row_send.at[2 * j + side],
            recv_sem=row_recv.at[2 * j + side],
            device_id={"rows": me + 1 if side == 0 else me - 1},
            device_id_type=MESH,
        )

    for j in range(count):

        @pl.when(me < n - 1)
        def _():
            row_copy(j, 0).start()

        @pl.when(me > 0)
        def _():
            row_copy(j, 1).start()

    for j in range(gathers):

        def start_given(k, carry):
            share(1 + j, k).start()
            return carry

        lax.fori_loop(1, n, start_given, 0)
        pltpu.make_async_copy(given[j], gathered[j].at[me], own.at[j]).start()

    def finish(k, carry):
        share(0, k).wait()
        return carry

    lax.fori_loop(1, n, finish, 0)
    total_ref[...] = lax.fori_loop(1, n, lambda k, s: s + slots[k], slots[0])
    for j in range(count):

        @pl.when(me > 0)
        def _():
            row_copy(j, 0).wait_recv()
            outs[2 * j][...] = lands[2 * j][...]

        @pl.when(me == 0)
        def _():
            outs[2 * j][...] = jnp.zeros_like(outs[2 * j])

        @pl.when(me < n - 1)
        def _():
            row_copy(j, 1).wait_recv()
            outs[2 * j + 1][...] = lands[2 * j + 1][...]
            row_copy(j, 0).wait_send()

        @pl.when(me == n - 1)
        def _():
            outs[2 * j + 1][...] = jnp.zeros_like(outs[2 * j + 1])

        @pl.when(me > 0)
        def _():
            row_copy(j, 1).wait_send()

    for j in range(gathers):

        def finish_given(k, carry):
            share(1 + j, k).wait()
            return carry

        lax.fori_loop(1, n, finish_given, 0)
        pltpu.make_async_copy(given[j], gathered[j].at[me], own.at[j]).wait()


def exchange(stats, rows, identity, given=()):
    n = lax.axis_size("rows")
    edge = []
    for array in rows:
        edge += [jax.ShapeDtypeStruct(array.shape[:1] + (1,) + array.shape[2:], array.dtype)] * 2
    whole = [jax.ShapeDtypeStruct((n,) + array.shape, array.dtype) for array in given]
    count, gathers = len(rows), len(given)
    nbytes = 4 * stats.size * n + sum(2 * e.size * e.dtype.itemsize for e in (*edge, *whole))
    return pl.pallas_call(
        functools.partial(exchange_kernel, n, count, gathers),
        out_shape=(jax.ShapeDtypeStruct(stats.shape, F32), *edge, *whole),
        in_specs=[WHOLE] + [ANYWHERE] * (count + gathers),
        out_specs=(WHOLE,) * (1 + 2 * count) + (ANYWHERE,) * gathers,
        scratch_shapes=[
            pltpu.VMEM((n,) + stats.shape, F32),
            *[pltpu.VMEM(e.shape, e.dtype) for e in edge],
            pltpu.SemaphoreType.DMA((1 + gathers, n)),
            pltpu.SemaphoreType.DMA((1 + gathers, n)),
            pltpu.SemaphoreType.DMA((max(1, 2 * count),)),
            pltpu.SemaphoreType.DMA((max(1, 2 * count),)),
            pltpu.SemaphoreType.DMA((max(1, gathers),)),
        ],
        compiler_params=pltpu.CompilerParams(collective_id=identity, has_side_effects=True),
        cost_estimate=pl.CostEstimate(
            flops=6_000_000_000, bytes_accessed=nbytes, transcendentals=0
        ),
        name=f"exchange{identity}",
    )(stats, *rows, *given)


def group_matrix(channels):
    size = channels // GROUPS
    one = lax.broadcasted_iota(jnp.int32, (channels, channels), 0) // size
    two = lax.broadcasted_iota(jnp.int32, (channels, channels), 1) // size
    return jnp.where(one == two, 1.0, 0.0).astype(BF16)


def group_sums(rows, same=None):
    if same is None:
        same = group_matrix(rows.shape[1])
    high = rows.astype(BF16).astype(F32)
    mid = (rows - high).astype(BF16).astype(F32)
    tail = rows - high - mid
    sums = dot(jnp.concatenate([high, mid, tail], axis=0).astype(BF16), same, 1, 0)
    n = rows.shape[0]
    return sums[:n] + sums[n : 2 * n] + sums[2 * n :]


def image_count(info, i, channels):
    return (info[i, 0] * info[i, 1]).astype(F32) * (channels // GROUPS)


def norm_of(stats, count, same=None):
    sums = group_sums(stats, same)
    average = sums[0:1] / count
    square = sums[1:2] / count
    return average, lax.rsqrt(square - average * average + EPS)


def means_of(stats, weight, count, same=None):
    sums = group_sums(stats * weight, same)
    return sums[0:1] / count, sums[1:2] / count


def window(info, i, row, shape):
    ok = (row >= 0) & (row < info[i, 0])
    limit = jnp.where(ok, info[i, 1], 0)
    return jnp.where(lax.broadcasted_iota(jnp.int32, shape, 0) < limit, 1.0, 0.0)


def padded_row(center, above, below, i, r):
    if r == 0:
        return above[i, 0]
    if r == center.shape[1] + 1:
        return below[i, 0]
    return center[i, r - 1]


def put_shifted(out, i, r, value, plain=None):
    width, channels = value.shape
    column = lax.broadcasted_iota(jnp.int32, value.shape, 0)
    left = jnp.where(column == 0, 0.0, pltpu.roll(value, 1, 0))
    right = jnp.where(column == width - 1, 0.0, pltpu.roll(value, width - 1, 0))
    out[i, r, :, :channels] = left.astype(BF16)
    low = value.astype(BF16)
    out[i, r, :, channels : 2 * channels] = low
    if plain is not None:
        plain[i, r] = low
    out[i, r, :, 2 * channels :] = right.astype(BF16)


def sigmoid(v):
    return 1.0 / (1.0 + jnp.exp(-v))


def silu_slope(v):
    s = sigmoid(v)
    return s * (1.0 + v * (1.0 - s))


def put_stats(stats_ref, i, first, second):
    channels = first.shape[1]
    one = jnp.sum(first, axis=0, keepdims=True)
    two = jnp.sum(second, axis=0, keepdims=True)
    row = lax.broadcasted_iota(jnp.int32, (8, channels), 0)
    stats_ref[i] = jnp.where(row == 0, one, jnp.where(row == 1, two, 0.0))


def tap_rows(shifted, tap, images, rows_dev, width):
    block = shifted[:, pl.ds(tap, rows_dev)]
    return block.reshape(images * rows_dev * width, shifted.shape[3])


def conv1_kernel(info, image, above, below, stats, gain, weight, first, out_stats, hidden, acc, shifted):
    images, rows_dev, width, channels = image.shape
    tap = pl.program_id(0)
    base = info[0, 2]

    @pl.when(tap == 0)
    def _():
        for i in range(images):
            average, inverse = norm_of(stats[i], image_count(info, i, channels))
            for r in range(rows_dev + 2):
                inside = window(info, i, base + r - 1, (width, channels))
                start = padded_row(image, above, below, i, r).astype(F32) * inside
                value = (start - average) * inverse * inside * gain[...]
                put_shifted(shifted, i, r, value * sigmoid(value) * inside, hidden)

    part = dot(tap_rows(shifted, tap, images, rows_dev, width), weight[0], 1, 0)

    @pl.when(tap == 0)
    def _():
        acc[...] = part

    @pl.when(tap > 0)
    def _():
        acc[...] += part

    @pl.when(tap == 2)
    def _():
        for i in range(images):
            one = two = jnp.zeros((width, channels), F32)
            for r in range(rows_dev):
                inside = window(info, i, base + r, (width, channels))
                at = (i * rows_dev + r) * width
                value = acc[at : at + width] * inside
                first[i, r] = value
                one = one + value
                two = two + value * value
            put_stats(out_stats, i, one, two)


def moved_of(value, inside, average, inverse, gain, scale, shift):
    normal = (value - average) * inverse * inside
    return normal, normal * gain * (1.0 + scale) + shift


def conv2_kernel(
    info, first, above, below, stats, gain, shifts, image, weight, middle, out_stats, second, acc,
    shifted,
):
    images, rows_dev, width, channels = first.shape
    tap = pl.program_id(0)
    base = info[0, 2]

    @pl.when(tap == 0)
    def _():
        for i in range(images):
            average, inverse = norm_of(stats[i], image_count(info, i, channels))
            scale, shift = shifts[i : i + 1, :channels], shifts[i : i + 1, channels:]
            for r in range(rows_dev + 2):
                inside = window(info, i, base + r - 1, (width, channels))
                value = padded_row(first, above, below, i, r)
                _, moved = moved_of(value, inside, average, inverse, gain[...], scale, shift)
                put_shifted(shifted, i, r, moved * sigmoid(moved) * inside, second)

    part = dot(tap_rows(shifted, tap, images, rows_dev, width), weight[0], 1, 0)

    @pl.when(tap == 0)
    def _():
        acc[...] = part

    @pl.when(tap > 0)
    def _():
        acc[...] += part

    @pl.when(tap == 2)
    def _():
        for i in range(images):
            one = two = jnp.zeros((width, channels), F32)
            for r in range(rows_dev):
                inside = window(info, i, base + r, (width, channels))
                at = (i * rows_dev + r) * width
                value = (image[i, r].astype(F32) + acc[at : at + width]) * inside
                middle[i, r] = value
                one = one + value
                two = two + value * value
            put_stats(out_stats, i, one, two)


def dgrad(shifted, tap, weight, images, rows_dev, width):
    channels = weight.shape[2]
    lhs = tap_rows(shifted, tap, images, rows_dev, width)
    part = None
    for b in range(3):
        term = dot(
            lhs[:, b * channels : (b + 1) * channels],
            weight[0, (2 - b) * channels : (3 - b) * channels, :],
            1,
            1,
        )
        part = term if part is None else part + term
    return part


def back2_kernel(
    info, grad, grad_above, grad_below, middle, mid_above, mid_below, cot, cot_above, cot_below,
    mid_stats, grad_stats, attn_gain, first, first_stats, gain, shifts, weight,
    grad_middle, moved_grad, out_stats, plain, acc, shifted,
):
    images, rows_dev, width, channels = first.shape
    tap = pl.program_id(0)
    base = info[0, 2]

    @pl.when(tap == 0)
    def _():
        for i in range(images):
            count = image_count(info, i, channels)
            average, inverse = norm_of(mid_stats[i], count)
            mean, cross = means_of(grad_stats[i], attn_gain[...], count)
            for r in range(rows_dev + 2):
                inside = window(info, i, base + r - 1, (width, channels))
                normal = (padded_row(middle, mid_above, mid_below, i, r) - average) * inverse
                dx = padded_row(grad, grad_above, grad_below, i, r) * attn_gain[...]
                term = (dx - mean - normal * cross) * inverse * inside
                total = padded_row(cot, cot_above, cot_below, i, r).astype(F32) + term
                if 0 < r <= rows_dev:
                    grad_middle[i, r - 1] = total
                put_shifted(shifted, i, r, total * inside, plain)

    part = dgrad(shifted, tap, weight, images, rows_dev, width)

    @pl.when(tap == 0)
    def _():
        acc[...] = part

    @pl.when(tap > 0)
    def _():
        acc[...] += part

    @pl.when(tap == 2)
    def _():
        for i in range(images):
            average, inverse = norm_of(first_stats[i], image_count(info, i, channels))
            scale, shift = shifts[i : i + 1, :channels], shifts[i : i + 1, channels:]
            one = two = jnp.zeros((width, channels), F32)
            for r in range(rows_dev):
                inside = window(info, i, base + r, (width, channels))
                at = (i * rows_dev + r) * width
                normal, moved = moved_of(
                    first[i, r], inside, average, inverse, gain[...], scale, shift
                )
                value = acc[at : at + width] * inside * silu_slope(moved)
                moved_grad[i, r] = value
                one = one + value
                two = two + value * normal
            put_stats(out_stats, i, one, two)


def back1_kernel(
    info, grad, grad_above, grad_below, first, first_above, first_below, first_stats, grad_stats,
    gain, shifts, image, image_stats, first_gain, weight,
    pre_grad, out_stats, plain, acc, shifted,
):
    images, rows_dev, width, channels = first.shape
    tap = pl.program_id(0)
    base = info[0, 2]

    @pl.when(tap == 0)
    def _():
        for i in range(images):
            count = image_count(info, i, channels)
            average, inverse = norm_of(first_stats[i], count)
            factor = gain[...] * (1.0 + shifts[i : i + 1, :channels])
            mean, cross = means_of(grad_stats[i], factor, count)
            for r in range(rows_dev + 2):
                inside = window(info, i, base + r - 1, (width, channels))
                normal = (padded_row(first, first_above, first_below, i, r) - average) * inverse
                dx = padded_row(grad, grad_above, grad_below, i, r) * factor
                put_shifted(shifted, i, r, (dx - mean - normal * cross) * inverse * inside, plain)

    part = dgrad(shifted, tap, weight, images, rows_dev, width)

    @pl.when(tap == 0)
    def _():
        acc[...] = part

    @pl.when(tap > 0)
    def _():
        acc[...] += part

    @pl.when(tap == 2)
    def _():
        for i in range(images):
            average, inverse = norm_of(image_stats[i], image_count(info, i, channels))
            one = two = jnp.zeros((width, channels), F32)
            for r in range(rows_dev):
                inside = window(info, i, base + r, (width, channels))
                at = (i * rows_dev + r) * width
                normal = (image[i, r].astype(F32) - average) * inverse * inside
                slope = silu_slope(normal * first_gain[...])
                value = acc[at : at + width] * inside * slope
                pre_grad[i, r] = value
                one = one + value
                two = two + value * normal
            put_stats(out_stats, i, one, two)


def conv_call(kernel, info, inputs, weight, outs, flipped):
    images, rows_dev, width, channels = outs[0].shape

    def whole(shape):
        return pl.BlockSpec(shape, lambda tap: (0,) * len(shape))

    def tap_of(tap):
        return ((2 - tap) if flipped else tap, 0, 0)

    weight = weight.reshape(3, 3 * channels, channels)
    flops = 2 * 9 * images * rows_dev * width * channels * channels
    moved = sum(a.size * a.dtype.itemsize for a in (*inputs, weight, *outs))
    return pl.pallas_call(
        kernel,
        grid=(3,),
        out_shape=tuple(outs),
        in_specs=[SCALARS]
        + [whole(a.shape) for a in inputs]
        + [pl.BlockSpec((1, 3 * channels, channels), tap_of)],
        out_specs=tuple(whole(o.shape) for o in outs),
        scratch_shapes=[
            pltpu.VMEM((images * rows_dev * width, channels), F32),
            pltpu.VMEM((images, rows_dev + 2, width, 3 * channels), BF16),
        ],
        compiler_params=pltpu.CompilerParams(vmem_limit_bytes=48 << 20),
        cost_estimate=pl.CostEstimate(flops=flops, bytes_accessed=moved, transcendentals=0),
        name=kernel.__name__,
    )(info, *inputs, weight)


def weight_grad_kernel(grads, hidden, out, turned, shifted):
    images, padded, width, channels = hidden.shape
    rows_dev = padded - 2
    pixels = images * rows_dev * width
    tap = pl.program_id(0)

    @pl.when(tap == 0)
    def _():
        center = grads[:, 1 : rows_dev + 1]
        turned[...] = center.reshape(pixels, channels).astype(F32).T.astype(BF16)
        for i in range(images):
            for r in range(padded):
                put_shifted(shifted, i, r, hidden[i, r].astype(F32))

    column = pl.multiple_of((tap % 3) * channels, channels)
    rhs = shifted[:, pl.ds(tap // 3, rows_dev), :, pl.ds(column, channels)]
    out[...] = dot(turned[...], rhs.reshape(pixels, channels), 1, 0).astype(BF16)


def weight_grad(grads, hidden):
    images, padded, width, channels = hidden.shape
    pixels = images * (padded - 2) * width

    def whole(shape):
        return pl.BlockSpec(shape, lambda tap: (0,) * len(shape))

    return pl.pallas_call(
        weight_grad_kernel,
        grid=(9,),
        out_shape=jax.ShapeDtypeStruct((channels, 9 * channels), BF16),
        in_specs=[whole(grads.shape), whole(hidden.shape)],
        out_specs=pl.BlockSpec((channels, channels), lambda tap: (0, tap)),
        scratch_shapes=[
            pltpu.VMEM((channels, pixels), BF16),
            pltpu.VMEM(hidden.shape[:3] + (3 * channels,), BF16),
        ],
        compiler_params=pltpu.CompilerParams(vmem_limit_bytes=32 << 20),
        cost_estimate=pl.CostEstimate(
            flops=18 * pixels * channels * channels,
            bytes_accessed=18 * channels * channels,
            transcendentals=0,
        ),
        name="weight_grad",
    )(grads, hidden)


def project_kernel(info, middle, stats, gain, weight, attn, qkv):
    images, rows_dev, width, channels = middle.shape
    pixels = rows_dev * width
    heads, wide = HEADS, weight.shape[0] // HEADS
    base = info[0, 2]
    for i in range(images):
        average, inverse = norm_of(stats[i], image_count(info, i, channels))
        for r in range(rows_dev):
            inside = window(info, i, base + r, (width, channels))
            value = (middle[i, r] - average) * inverse * inside * gain[...]
            attn[i, r * width : (r + 1) * width] = value.astype(BF16)
        for h in range(heads):
            block = dot(weight[h * wide : (h + 1) * wide], attn[i], 1, 1)
            qkv[i * heads + h] = block.astype(BF16)


def project(info, middle, stats, gain, weight):
    images, rows_dev, width, channels = middle.shape
    pixels = rows_dev * width
    return pl.pallas_call(
        project_kernel,
        out_shape=(
            jax.ShapeDtypeStruct((images, pixels, channels), BF16),
            jax.ShapeDtypeStruct((images * HEADS, weight.shape[0] // HEADS, pixels), BF16),
        ),
        in_specs=[SCALARS, WHOLE, WHOLE, WHOLE, WHOLE],
        out_specs=(WHOLE, WHOLE),
        compiler_params=pltpu.CompilerParams(vmem_limit_bytes=32 << 20),
        name="project",
    )(info, middle, stats, gain, weight)


def unproject_kernel(info, middle, stats, grads, weight, out, out_stats):
    images, rows_dev, width, channels = middle.shape
    wide, pixels = grads.shape[1], grads.shape[2]
    base = info[0, 2]
    for i in range(images):
        average, inverse = norm_of(stats[i], image_count(info, i, channels))
        acc = None
        for h in range(HEADS):
            turned = grads[i * HEADS + h].astype(F32).T.astype(BF16)
            term = dot(turned, weight[h * wide : (h + 1) * wide], 1, 0)
            acc = term if acc is None else acc + term
        one = two = jnp.zeros((width, channels), F32)
        for r in range(rows_dev):
            inside = window(info, i, base + r, (width, channels))
            value = acc[r * width : (r + 1) * width] * inside
            out[i, r] = value
            one = one + value
            two = two + value * ((middle[i, r] - average) * inverse)
        put_stats(out_stats, i, one, two)


def unproject(info, middle, stats, grads, weight):
    images, rows_dev, width, channels = middle.shape
    return pl.pallas_call(
        unproject_kernel,
        out_shape=(
            jax.ShapeDtypeStruct(middle.shape, F32),
            jax.ShapeDtypeStruct(stats.shape, F32),
        ),
        in_specs=[SCALARS, WHOLE, WHOLE, WHOLE, WHOLE],
        out_specs=(WHOLE, WHOLE),
        compiler_params=pltpu.CompilerParams(vmem_limit_bytes=32 << 20),
        name="unproject",
    )(info, middle, stats, grads, weight)


def finish_kernel(info, pre_grad, grad_stats, image, stats, gain, grad_middle, out):
    images, rows_dev, width, channels = image.shape
    base = info[0, 2]
    for i in range(images):
        count = image_count(info, i, channels)
        average, inverse = norm_of(stats[i], count)
        mean, cross = means_of(grad_stats[i], gain[...], count)
        for r in range(rows_dev):
            inside = window(info, i, base + r, (width, channels))
            normal = (image[i, r].astype(F32) - average) * inverse
            term = (pre_grad[i, r] * gain[...] - mean - normal * cross) * inverse
            out[i, r] = (grad_middle[i, r] + term) * inside


def finish(info, pre_grad, grad_stats, image, stats, gain, grad_middle):
    return pl.pallas_call(
        finish_kernel,
        out_shape=jax.ShapeDtypeStruct(image.shape, F32),
        in_specs=[SCALARS] + [WHOLE] * 6,
        out_specs=WHOLE,
        compiler_params=pltpu.CompilerParams(vmem_limit_bytes=32 << 20),
        name="finish",
    )(info, pre_grad, grad_stats, image, stats, gain, grad_middle)


DMA = pltpu.SemaphoreType.DMA


def remote(src, dst, send, recv, device):
    return pltpu.make_async_remote_copy(
        src_ref=src,
        dst_ref=dst,
        send_sem=send,
        recv_sem=recv,
        device_id=device,
        device_id_type=MESH,
    )


class Grid:
    def __init__(self, items, n):
        self.items, self.n = items, n
        self.item, self.me = lax.axis_index("items"), lax.axis_index("rows")

    def row(self, k):
        return {"items": self.item, "rows": lax.rem(self.me + k, self.n)}

    def peer(self, k):
        return {"items": lax.rem(self.item + k, self.items), "rows": self.me}

    def greet(self):
        barrier = pltpu.get_barrier_semaphore()

        def rows(k, carry):
            pl.semaphore_signal(barrier, inc=1, device_id=self.row(k), device_id_type=MESH)
            return carry

        def items(k, carry):
            pl.semaphore_signal(barrier, inc=1, device_id=self.peer(k), device_id_type=MESH)
            return carry

        lax.fori_loop(1, self.n, rows, 0)
        lax.fori_loop(1, self.items, items, 0)

    def met(self):
        pl.semaphore_wait(pltpu.get_barrier_semaphore(), self.n + self.items - 2)

    def loop(self, count, body):
        def step(k, carry):
            body(k)
            return carry

        lax.fori_loop(1, count, step, 0)


class Sums:
    def __init__(self, grid, own, slots, send, recv):
        self.grid, self.own, self.slots, self.send, self.recv = grid, own, slots, send, recv

    def copy(self, k):
        return remote(
            self.own, self.slots.at[self.grid.me], self.send.at[k], self.recv.at[k], self.grid.row(k)
        )

    def start(self, stats):
        lines, lanes = self.own.shape
        half = lines // 2
        at = lax.broadcasted_iota(jnp.int32, (lines, lanes), 0)
        packed = jnp.zeros((lines, lanes), F32)
        for j in range(lines):
            piece = stats[j // half : j // half + 1, (j % half) * lanes : (j % half + 1) * lanes]
            packed = jnp.where(at == j, piece, packed)
        self.own[...] = packed
        self.grid.loop(self.grid.n, lambda k: self.copy(k).start())
        self.slots[self.grid.me] = packed

    def result(self):
        self.grid.loop(self.grid.n, lambda k: self.copy(k).wait())
        slots = self.slots
        total = lax.fori_loop(1, self.grid.n, lambda k, s: s + slots[k], slots[0])
        half = total.shape[0] // 2
        rows = [
            jnp.concatenate([total[r * half + j : r * half + j + 1] for j in range(half)], axis=1)
            for r in range(2)
        ]
        at = lax.broadcasted_iota(jnp.int32, (8, rows[0].shape[1]), 0)
        return jnp.where(at == 0, rows[0], jnp.where(at == 1, rows[1], 0.0))


class Edges:
    def __init__(self, grid, field, send, recv):
        self.grid, self.field, self.send, self.recv = grid, field, send, recv

    def copy(self, side):
        last = self.field.shape[0] - 1
        at, to = (last - 1, 0) if side == 0 else (1, last)
        grid = self.grid
        return remote(
            self.field.at[at : at + 1],
            self.field.at[to : to + 1],
            self.send.at[side],
            self.recv.at[side],
            {"items": grid.item, "rows": grid.me + 1 if side == 0 else grid.me - 1},
        )

    def both(self, down, up):
        @pl.when(self.grid.me < self.grid.n - 1)
        def _():
            down()

        @pl.when(self.grid.me > 0)
        def _():
            up()

    def clear(self):
        last = self.field.shape[0] - 1

        @pl.when(self.grid.me == 0)
        def _():
            self.field[0] = jnp.zeros(self.field.shape[1:], self.field.dtype)

        @pl.when(self.grid.me == self.grid.n - 1)
        def _():
            self.field[last] = jnp.zeros(self.field.shape[1:], self.field.dtype)

    def start(self):
        self.both(lambda: self.copy(0).start(), lambda: self.copy(1).start())

    def wait(self):
        self.both(lambda: self.copy(1).wait_recv(), lambda: self.copy(0).wait_recv())
        self.both(lambda: self.copy(0).wait_send(), lambda: self.copy(1).wait_send())


def shift_into(out, r, value):
    width, channels = value.shape
    column = lax.broadcasted_iota(jnp.int32, value.shape, 0)
    left = jnp.where(column == 0, 0.0, pltpu.roll(value, 1, 0))
    right = jnp.where(column == width - 1, 0.0, pltpu.roll(value, width - 1, 0))
    out[r, :, :channels] = left.astype(BF16)
    out[r, :, channels : 2 * channels] = value.astype(BF16)
    out[r, :, 2 * channels :] = right.astype(BF16)


def row_stats(rows, width, channels, row):
    def step(r, carry):
        one, two = row(r)
        return carry[0] + one, carry[1] + two

    zero = jnp.zeros((width, channels), F32)
    one, two = lax.fori_loop(0, rows, step, (zero, zero))
    one = jnp.sum(one, axis=0, keepdims=True)
    two = jnp.sum(two, axis=0, keepdims=True)
    at = lax.broadcasted_iota(jnp.int32, (8, channels), 0)
    return jnp.where(at == 0, one, jnp.where(at == 1, two, 0.0))


def each_row(rows, body):
    def step(r, carry):
        body(r)
        return carry

    lax.fori_loop(0, rows, step, 0)


def conv_taps(shifted, weight, acc, rows_dev):
    pixels, wide = acc.shape[0], shifted.shape[2]
    acc[...] = jnp.zeros_like(acc)

    def step(tap, carry):
        acc[...] += dot(shifted[pl.ds(tap, rows_dev)].reshape(pixels, wide), weight[tap], 1, 0)
        return carry

    lax.fori_loop(0, 3, step, 0)


def forward_kernel(items, n, step, bq, *refs):
    (info, image, cot, text, embed, gain1, gain2, gain3, w1_in, w2_in, embed_in, text_in, qkv_in, proj_in,
     first_out, mid_out, cot_out, hidden_all, second_all, attn_out, turned_out, output, query_part, side_out, dkv_out,
     dt_out, text_cols, stats_out, shifts_out,
     image_v, cot_v, text_v, w1, w2, wide_w, qkv_w, proj_w, first_v, mid_v, hidden, second, attn,
     turned, pairs, queries, go, text_kv, cols, shifted, acc, own, slots,
     pair_land, query_land, go_land, text_pair, o, dq, dkv, dtext, same, o_land, dq_land, masked, out_v, query_acc,
     side_v, side_core, side_sum, side_item, side_total, cols_land,
     load, sum_send, sum_recv, edge_send, edge_recv, row_send, row_recv, item_send, item_recv,
     s_core_send, s_core_recv, s_item_send, s_item_recv, *scratch) = refs
    grid = Grid(items, n)
    grid.greet()
    item, me = grid.item, grid.me
    rows_dev, width, channels = image.shape
    pixels = rows_dev * width
    heads, head_dim, wide = HEADS, channels // HEADS, 3 * channels // HEADS
    base = me * rows_dev
    share_rows = channels // n
    count = (info[0, 0] * info[0, 1]).astype(F32) * (channels // GROUPS)
    att = Attention(n, pixels, head_dim, n * text.shape[0], step, bq, scratch)

    def inside(row):
        return window(info, 0, row, (width, channels))

    loads = []

    def fetch(src, dst):
        c = pltpu.make_async_copy(src, dst, load.at[len(loads)])
        c.start()
        loads.append(c)
        return c

    center = slice(1, rows_dev + 1)
    got_image = fetch(image, image_v.at[center])
    got_cot = fetch(cot, cot_v.at[center])
    got_proj = fetch(proj_in, proj_w)
    got_text = fetch(text, text_v)
    got_text_w = fetch(text_in, wide_w)
    got_w1 = fetch(w1_in, w1)
    got_w2 = fetch(w2_in, w2)
    got_qkv_w = fetch(qkv_in, qkv_w)
    edges = [
        Edges(grid, field, edge_send.at[j], edge_recv.at[j])
        for j, field in enumerate((image_v, cot_v, first_v, mid_v))
    ]
    sums = [Sums(grid, own.at[j], slots.at[j], sum_send.at[j], sum_recv.at[j]) for j in range(3)]
    for e in edges:
        e.clear()
    same[...] = group_matrix(channels)
    got_image.wait()

    def start_row(r):
        return image_v[1 + r].astype(F32) * inside(base + r)

    def start_stats(r):
        v = start_row(r)
        return v, v * v

    stats = row_stats(rows_dev, width, channels, start_stats)
    grid.met()
    sums[0].start(stats)
    edges[0].start()
    got_cot.wait()
    edges[1].start()

    got_text.wait()
    got_text_w.wait()
    text_all = dot(text_v[...], wide_w[...], 1, 0).astype(BF16)
    got_embed_w = fetch(embed_in, wide_w)
    share = text_v.shape[1] // n
    for h in range(heads):
        text_kv[h] = text_all[:, h * 2 * head_dim : (h + 1) * 2 * head_dim]
    for r in range(n):
        cols[r] = text_v[:, r * share : (r + 1) * share]

    def scatter(j, src, dst):
        def copy(k):
            to = lax.rem(me + k, n)
            return remote(src.at[to], dst.at[me], row_send.at[j, k], row_recv.at[j, k], grid.row(k))

        return copy

    kv_copy = scatter(0, text_kv, text_pair)
    col_copy = scatter(1, cols, cols_land)
    grid.loop(n, lambda k: kv_copy(k).start())
    grid.loop(n, lambda k: col_copy(k).start())
    own_kv = fetch(text_kv.at[me], text_pair.at[me])
    cols_land[me] = cols[me]

    got_proj.wait()

    def to_grad(r):
        masked[pl.ds(r * width, width)] = (cot_v[1 + r].astype(F32) * inside(base + r)).astype(BF16)

    each_row(rows_dev, to_grad)
    for h in range(heads):
        go[h] = dot(proj_w[h * head_dim : (h + 1) * head_dim], masked[...], 1, 1).astype(BF16)
    go_copy = scatter(2, go, go_land)
    own_go = fetch(go.at[me], go_land.at[me])

    stats = sums[0].result()
    stats_out[0] = stats
    average, inverse = norm_of(stats, count, same[...])
    edges[0].wait()
    grid.loop(n // 2, lambda k: go_copy(k).start())

    def to_hidden(r):
        ok = inside(base + r - 1)
        value = (image_v[r].astype(F32) * ok - average) * inverse * ok * gain1[...]
        value = value * sigmoid(value) * ok
        shift_into(shifted, r, value)
        hidden[r] = value.astype(BF16)

    each_row(rows_dev + 2, to_hidden)

    def spread(j, src, dst):
        def copy(k):
            return remote(src, dst.at[item], item_send.at[j, k], item_recv.at[j, k], grid.peer(k))

        return copy

    hidden_copy = spread(0, hidden, hidden_all)
    grid.loop(items, lambda k: hidden_copy(k).start())
    own_hidden = fetch(hidden, hidden_all.at[item])
    got_w1.wait()
    conv_taps(shifted, w1, acc, rows_dev)

    def first_row(r):
        value = acc[pl.ds(r * width, width)] * inside(base + r)
        first_v[1 + r] = value
        return value, value * value

    stats = row_stats(rows_dev, width, channels, first_row)
    sums[1].start(stats)
    edges[2].start()

    e = embed[...].astype(F32)
    low = (e * sigmoid(e)).astype(BF16)
    got_embed_w.wait()
    shifts_out[...] = dot(low, wide_w[...], 1, 0)
    scale, shift = shifts_out[:, :channels], shifts_out[:, channels:]

    stats = sums[1].result()
    stats_out[1] = stats
    average, inverse = norm_of(stats, count, same[...])
    edges[2].wait()
    own_first = fetch(first_v, first_out)

    def to_second(r):
        ok = inside(base + r - 1)
        _, moved = moved_of(first_v[r], ok, average, inverse, gain2[...], scale, shift)
        value = moved * sigmoid(moved) * ok
        shift_into(shifted, r, value)
        second[r] = value.astype(BF16)

    each_row(rows_dev + 2, to_second)
    second_copy = spread(1, second, second_all)
    grid.loop(items, lambda k: second_copy(k).start())
    own_second = fetch(second, second_all.at[item])
    got_w2.wait()
    conv_taps(shifted, w2, acc, rows_dev)

    def middle_row(r):
        value = (image_v[1 + r].astype(F32) + acc[pl.ds(r * width, width)]) * inside(base + r)
        mid_v[1 + r] = value
        return value, value * value

    stats = row_stats(rows_dev, width, channels, middle_row)
    sums[2].start(stats)
    edges[3].start()
    edges[1].wait()
    own_cot = fetch(cot_v, cot_out)
    got_qkv_w.wait()
    for j in range(3):
        block = qkv_w[:, j * channels : (j + 1) * channels].astype(F32).T
        turned[j * channels : (j + 1) * channels] = block.astype(BF16)
    own_turned = fetch(turned, turned_out)

    stats = sums[2].result()
    stats_out[2] = stats
    average, inverse = norm_of(stats, count, same[...])

    def to_attn(r):
        value = (mid_v[1 + r] - average) * inverse * inside(base + r) * gain3[...]
        attn[pl.ds(r * width, width)] = value.astype(BF16)

    each_row(rows_dev, to_attn)
    own_attn = fetch(attn, attn_out)
    pair_copy = scatter(3, pairs, pair_land)
    query_copy = scatter(4, queries, query_land)

    def head(k):
        to = lax.rem(me + k, n)
        rows = pl.ds(pl.multiple_of(to * wide, wide), wide)
        block = dot(turned[rows], attn[...], 1, 1).astype(BF16)
        queries[to] = block[:head_dim]
        pairs[to] = block[head_dim:]

    def send_head(k):
        head(k)
        pair_copy(k).start()

    grid.loop(n, send_head)
    head(0)
    query_land[me] = queries[me]
    att.stage_key(me, pairs[me, :head_dim], width, info[0, 0], info[0, 1])
    att.stage_value(me, pairs[me, head_dim:])
    grid.loop(n, lambda k: kv_copy(k).wait())
    own_kv.wait()
    att.stage_text(text_pair[...].reshape(n * text.shape[0], 2 * head_dim))
    edges[3].wait()
    own_mid = fetch(mid_v, mid_out)

    def source(k):
        return lax.rem(me + n - k, n)

    def stage_pair(k):
        pair_copy(k).wait()
        c = source(k)
        att.stage_key(c, pair_land[c, :head_dim], width, info[0, 0], info[0, 1])
        att.stage_value(c, pair_land[c, head_dim:])

    grid.loop(n, stage_pair)

    def send_rest(k):
        query_copy(k).start()

        @pl.when(k >= n // 2)
        def _():
            go_copy(k).start()

    grid.loop(n, send_rest)
    own_go.wait()

    def before(k):
        query_copy(k).wait()
        go_copy(k).wait()

    def give(j, src, dst):
        def copy(h):
            to = source(h)
            return remote(
                src.at[to],
                dst.at[me],
                row_send.at[j, h],
                row_recv.at[j, h],
                {"items": item, "rows": to},
            )

        return copy

    o_copy = give(5, o, o_land)
    dq_copy = give(6, dq, dq_land)
    dkv_copy = give(7, dkv, dkv_out)

    def done(h):
        @pl.when(h > 0)
        def _():
            o_copy(h).start()
            dq_copy(h).start()

    grid.loop(n, lambda k: col_copy(k).wait())
    cols_copy = spread(2, cols_land, text_cols)
    grid.loop(items, lambda k: cols_copy(k).start())
    own_cols = fetch(cols_land, text_cols.at[item])
    att.attend(query_land, go_land, o, dq, source, before, done)

    def send_keys(h):
        at = pl.ds(pl.multiple_of(source(h) * pixels, pixels), pixels)
        dkv[source(h), :head_dim] = att.key_grad(at)
        dkv[source(h), head_dim:] = att.value_grad(at)

    def send_next(h):
        send_keys(h)
        dkv_copy(h).start()

    grid.loop(n, send_next)
    send_keys(0)
    flat = jnp.concatenate(
        [
            (att.dkt[:, n * pixels :] * (head_dim**-0.5)).T,
            att.dvt[:, n * pixels :].T,
        ],
        axis=1,
    )
    for r in range(n):
        tokens = text.shape[0]
        dtext[r] = flat[r * tokens : (r + 1) * tokens].astype(BF16)

    own_dkv = fetch(dkv.at[me], dkv_out.at[me])
    own_dt = fetch(dtext, dt_out)

    o_land[me] = o[me]
    dq_land[me] = dq[me]
    grid.loop(n, lambda h: o_copy(h).wait())
    grid.loop(n, lambda h: dq_copy(h).wait())
    side = SideSum(grid, side_v, side_core, side_sum, side_item, side_total, None, None,
                   (s_core_send, s_core_recv), (s_item_send, s_item_recv), None, None)

    def query_head(h):
        block = dot(dq_land[h], attn[...], 1, 0).astype(BF16)
        side.put_head(h, block, 0)

    each_row(heads, query_head)
    flat_o = o_land[...].reshape(channels, pixels)
    block = dot(masked[...].astype(F32).T.astype(BF16), flat_o, 1, 1).astype(BF16)
    for r in range(n):
        side.put_head(r, block[r * share_rows : (r + 1) * share_rows], 1)
    side.core_copy().start()
    query_acc[...] = jnp.zeros_like(query_acc)

    def unproject_query(h):
        rows = pl.ds(pl.multiple_of(h * wide, wide), head_dim)
        query_acc[...] += dot(dq_land[h].astype(F32).T.astype(BF16), turned[rows], 1, 0)

    each_row(heads, unproject_query)
    put_query = fetch(query_acc, query_part)
    side.over_items()
    acc[...] = dot(flat_o.astype(F32).T.astype(BF16), proj_w[...], 1, 0)

    def output_row(r):
        value = mid_v[1 + r] + acc[pl.ds(r * width, width)] * inside(base + r)
        out_v[r] = value.astype(BF16)

    each_row(rows_dev, output_row)
    put_output = fetch(out_v, output)
    side.sum_items()
    put_side = fetch(side_total, side_out)
    grid.loop(items, lambda k: hidden_copy(k).wait())
    grid.loop(items, lambda k: second_copy(k).wait())
    grid.loop(items, lambda k: cols_copy(k).wait())
    grid.loop(n, lambda h: dkv_copy(h).wait())
    for c in (own_hidden, own_first, own_second, own_cot, own_turned, own_attn, own_mid, own_dkv, own_dt,
              own_cols, put_query, put_output, put_side):
        c.wait()


def forward_call(info, image, cot, text, embed, gains, weights, identity):
    items, n = lax.axis_size("items"), lax.axis_size("rows")
    rows_dev, width, channels = image.shape
    pixels = rows_dev * width
    padded = (rows_dev + 2, width, channels)
    tokens, text_width = text.shape
    head_dim = channels // HEADS
    w1, w2, _, text_w, qkv_w, proj_w = weights
    chips = n // 2
    rows = channels // n // items
    sds = jax.ShapeDtypeStruct
    outs = (
        sds(padded, F32),
        sds(padded, F32),
        sds(padded, BF16),
        sds((items,) + padded, BF16),
        sds((items,) + padded, BF16),
        sds((pixels, channels), BF16),
        sds((3 * channels, channels), BF16),
        sds(image.shape, BF16),
        sds((pixels, channels), F32),
        sds((chips, rows, 2 * channels), BF16),
        sds((n, 2 * head_dim, pixels), BF16),
        sds((n, tokens, 2 * head_dim), BF16),
        sds((items, n, tokens, text_width // n), BF16),
        sds((3, 8, channels), F32),
        sds((1, 2 * channels), F32),
    )
    v = pltpu.VMEM
    scratch = [
        v(padded, BF16),
        v(padded, BF16),
        v(text.shape, BF16),
        v(w1.shape, BF16),
        v(w2.shape, BF16),
        v(text_w.shape, BF16),
        v(qkv_w.shape, BF16),
        v(proj_w.shape, BF16),
        v(padded, F32),
        v(padded, F32),
        v(padded, BF16),
        v(padded, BF16),
        v((pixels, channels), BF16),
        v((3 * channels, channels), BF16),
        v((n, 2 * head_dim, pixels), BF16),
        v((n, head_dim, pixels), BF16),
        v((n, head_dim, pixels), BF16),
        v((n, tokens, 2 * head_dim), BF16),
        v((n, tokens, text_width // n), BF16),
        v((rows_dev + 2, width, 3 * channels), BF16),
        v((pixels, channels), F32),
        v((3, channels // 64, 128), F32),
        v((3, n, channels // 64, 128), F32),
        v((n, 2 * head_dim, pixels), BF16),
        v((n, head_dim, pixels), BF16),
        v((n, head_dim, pixels), BF16),
        v((n, tokens, 2 * head_dim), BF16),
        v((n, head_dim, pixels), BF16),
        v((n, head_dim, pixels), BF16),
        v((n, 2 * head_dim, pixels), BF16),
        v((n, tokens, 2 * head_dim), BF16),
        v((channels, channels), BF16),
        v((n, head_dim, pixels), BF16),
        v((n, head_dim, pixels), BF16),
        v((pixels, channels), BF16),
        v(image.shape, BF16),
        v((pixels, channels), F32),
        v((2, chips, items, rows, 2 * channels), BF16),
        v((chips, items, rows, 2 * channels), BF16),
        v((items, chips, rows, 2 * channels), BF16),
        v((items, chips, rows, 2 * channels), BF16),
        v((chips, rows, 2 * channels), BF16),
        v((n, tokens, text_width // n), BF16),
        DMA((28,)),
        DMA((3, n)),
        DMA((3, n)),
        DMA((4, 2)),
        DMA((4, 2)),
        DMA((8, n)),
        DMA((8, n)),
        DMA((3, items)),
        DMA((3, items)),
        DMA((1,)),
        DMA((1,)),
        DMA((items,)),
        DMA((items,)),
    ]
    step, bq, extra = attention_scratch(n, pixels, head_dim, n * tokens)
    scratch += extra
    return pl.pallas_call(
        functools.partial(forward_kernel, items, n, step, bq),
        out_shape=outs,
        in_specs=[SCALARS] + [ANYWHERE] * 3 + [WHOLE] * 4 + [ANYWHERE] * 6,
        out_specs=(ANYWHERE,) * 13 + (WHOLE,) * 2,
        scratch_shapes=scratch,
        compiler_params=pltpu.CompilerParams(
            collective_id=identity, has_side_effects=True, vmem_limit_bytes=62 << 20
        ),
        cost_estimate=pl.CostEstimate(
            flops=40 * pixels * channels * channels, bytes_accessed=60 << 20, transcendentals=0
        ),
        name="forward",
    )(info, image, cot, text, embed, *gains, *weights)


class KernelSum:
    def __init__(self, grid, turned, quarter, part, from_core, chip_sum, from_chip, final, item_sems, core_sems,
                 chip_sems, final_sems):
        self.grid = grid
        self.turned, self.quarter, self.part, self.from_core = turned, quarter, part, from_core
        self.chip_sum, self.from_chip, self.final = chip_sum, from_chip, final
        self.item_sems, self.core_sems = item_sems, core_sems
        self.chip_sems, self.final_sems = chip_sems, final_sems
        self.chips = grid.n // 2
        self.chip, self.core = grid.me // 2, lax.rem(grid.me, 2)

    def grads_copy(self, k):
        grid = self.grid
        send, recv = self.item_sems
        to = lax.rem(grid.item + k, grid.items)
        return remote(
            self.turned.at[to], self.quarter.at[grid.item], send.at[k], recv.at[k], grid.peer(k)
        )

    def send_grads(self, shifted):
        grid, chips = self.grid, self.chips
        rows_dev, width, channels = shifted.shape[0] - 2, shifted.shape[1], shifted.shape[2] // 3
        center = shifted[1 : rows_dev + 1, :, channels : 2 * channels]
        block = center.reshape(rows_dev * width, channels).astype(F32).T.astype(BF16)
        share = channels // grid.n
        rows = share // grid.items
        for z in range(chips):
            for c in range(2):
                for q in range(grid.items):
                    at = (z * 2 + c) * share + q * rows
                    to = (c * chips + z) * rows
                    self.turned[q, to : to + rows] = block[at : at + rows]
        grid.loop(grid.items, lambda k: self.grads_copy(k).start())
        self.quarter[grid.item] = self.turned[grid.item]

    def wait_grads(self):
        self.grid.loop(self.grid.items, lambda k: self.grads_copy(k).wait())

    def core_copy(self, a):
        send, recv = self.core_sems
        grid = self.grid
        return remote(
            self.part.at[a, 1 - self.core],
            self.from_core.at[a],
            send.at[a],
            recv.at[a],
            {"items": grid.item, "rows": grid.me + 1 - 2 * self.core},
        )

    def compute(self, a, shifted):
        items, padded, width, wide = shifted.shape
        rows_dev, channels = padded - 2, wide // 3
        half = self.turned.shape[1] // 2
        for b in range(3):
            acc = None
            for g in range(items):
                rhs = shifted[g, a : a + rows_dev, :, b * channels : (b + 1) * channels]
                term = dot(self.quarter[g], rhs.reshape(rows_dev * width, channels), 1, 0)
                acc = term if acc is None else acc + term
            self.part[a, 0, b] = acc[:half].astype(BF16)
            self.part[a, 1, b] = acc[half:].astype(BF16)
        self.core_copy(a).start()

    def chip_copy(self, a, k):
        send, recv = self.chip_sems
        grid = self.grid
        to = lax.rem(self.chip + k, self.chips)
        return remote(
            self.chip_sum.at[a, to],
            self.from_chip.at[a, k],
            send.at[a, k],
            recv.at[a, k],
            {"items": grid.item, "rows": to * 2 + self.core},
        )

    def over_chips(self, a):
        self.core_copy(a).wait()
        rows = self.chip_sum.shape[3]
        for b in range(3):
            both = self.part[a, self.core, b].astype(F32) + self.from_core[a, b].astype(F32)
            for z in range(self.chips):
                self.chip_sum[a, z, b] = both[z * rows : (z + 1) * rows].astype(BF16)
        for k in range(1, self.chips):
            self.chip_copy(a, k).start()

    def final_copy(self, a, k):
        send, recv = self.final_sems
        mine = self.final.at[a, self.grid.item]
        return remote(mine, mine, send.at[a, k], recv.at[a, k], self.grid.peer(k))

    def over_items(self, a):
        for k in range(1, self.chips):
            self.chip_copy(a, k).wait()
        total = self.chip_sum[a, self.chip].astype(F32)
        for k in range(1, self.chips):
            total = total + self.from_chip[a, k].astype(F32)
        self.final[a, self.grid.item] = total.astype(BF16)
        for k in range(1, self.grid.items):
            self.final_copy(a, k).start()

    def wait_final(self, a):
        for k in range(1, self.grid.items):
            self.final_copy(a, k).wait()


class SideSum:
    def __init__(self, grid, values, from_core, core_sum, from_item, item_sum, from_chip, final, core_sems,
                 item_sems, chip_sems, final_sems):
        self.grid = grid
        self.values, self.from_core, self.core_sum = values, from_core, core_sum
        self.from_item, self.item_sum, self.from_chip, self.final = (
            from_item,
            item_sum,
            from_chip,
            final,
        )
        self.core_sems, self.item_sems = core_sems, item_sems
        self.chip_sems, self.final_sems = chip_sems, final_sems
        self.chips = grid.n // 2
        self.chip, self.core = grid.me // 2, lax.rem(grid.me, 2)

    def core_copy(self):
        send, recv = self.core_sems
        grid = self.grid
        return remote(
            self.values.at[1 - self.core],
            self.from_core,
            send.at[0],
            recv.at[0],
            {"items": grid.item, "rows": grid.me + 1 - 2 * self.core},
        )

    def item_copy(self, k):
        send, recv = self.item_sems
        grid = self.grid
        to = lax.rem(grid.item + k, grid.items)
        return remote(
            self.core_sum.at[to], self.from_item.at[k], send.at[k], recv.at[k], grid.peer(k)
        )

    def over_items(self):
        self.core_copy().wait()
        for z in range(self.chips):
            both = self.values[self.core, z].astype(F32) + self.from_core[z].astype(F32)
            for q in range(self.grid.items):
                self.core_sum[q, z] = both[q].astype(BF16)
        for k in range(1, self.grid.items):
            self.item_copy(k).start()

    def chip_copy(self, k):
        send, recv = self.chip_sems
        grid = self.grid
        to = lax.rem(self.chip + k, self.chips)
        return remote(
            self.item_sum.at[to],
            self.from_chip.at[k],
            send.at[k],
            recv.at[k],
            {"items": grid.item, "rows": to * 2 + self.core},
        )

    def put_head(self, h, block, j):
        items, rows = self.values.shape[2], self.values.shape[3]
        channels = block.shape[1]
        at = slice(j * channels, (j + 1) * channels)
        core, chip = (h % 2, h // 2) if isinstance(h, int) else (lax.rem(h, 2), h // 2)
        self.values[core, chip, :, :, at] = block.reshape(items, rows, channels)

    def sum_items(self):
        for k in range(1, self.grid.items):
            self.item_copy(k).wait()
        total = self.core_sum[self.grid.item].astype(F32)
        for k in range(1, self.grid.items):
            total = total + self.from_item[k].astype(F32)
        self.item_sum[:, :, : total.shape[2]] = total.astype(BF16)

    def over_chips(self):
        self.sum_items()
        for k in range(1, self.chips):
            self.chip_copy(k).start()

    def final_copy(self, k):
        send, recv = self.final_sems
        mine = self.final.at[self.grid.item]
        return remote(mine, mine, send.at[k], recv.at[k], self.grid.peer(k))

    def spread(self):
        for k in range(1, self.chips):
            self.chip_copy(k).wait()
        total = self.item_sum[self.chip].astype(F32)
        for k in range(1, self.chips):
            total = total + self.from_chip[k].astype(F32)
        self.final[self.grid.item] = total.astype(BF16)
        for k in range(1, self.grid.items):
            self.final_copy(k).start()

    def wait_final(self):
        for k in range(1, self.grid.items):
            self.final_copy(k).wait()


def conv_taps_back(shifted, weight, acc, rows_dev):
    pixels, channels = acc.shape
    acc[...] = jnp.zeros_like(acc)

    def step(tap, carry):
        lhs = shifted[pl.ds(tap, rows_dev)].reshape(pixels, 3 * channels)
        total = None
        for b in range(3):
            at = pl.multiple_of(((2 - tap) * 3 + 2 - b) * channels, channels)
            term = dot(
                lhs[:, b * channels : (b + 1) * channels], weight[pl.ds(at, channels)], 1, 1
            )
            total = term if total is None else total + term
        acc[...] += total
        return carry

    lax.fori_loop(0, 3, step, 0)


def backward_kernel(items, n, *refs):
    (info, embed, gain1, gain2, gain3, stats_in, shifts,
     query_part, side_in, dkv_in, dt_in, first, middle, cot, image, hidden_all, second_all, attn_in,
     turned_in, text_cols, w1_in, w2_in, text_in, embed_in,
     image_grad, text_grad, text_w_grad, embed_grad, final_out, side_out, vectors,
     weight, qkv_turned, first_v, mid_v, cot_v, image_v, attn, cols, rows_v, dkv, dtext, dt, own_dt,
     grad_v, grad_mid, moved_v, pre, acc, shifted, shifted_all, image_out, text_v, text_w_v, embed_v, same,
     turned, quarter, part, from_core, chip_sum, from_chip, final,
     side_v, side_core, side_sum, side_item, side_total, side_chip, side_final,
     vector, vector_land, own, slots,
     load, sum_send, sum_recv, edge_send, edge_recv, text_send, text_recv, dt_send, dt_recv, dt_core_send, dt_core_recv, vec_send, vec_recv,
     k_item_send, k_item_recv, k_core_send, k_core_recv, k_chip_send, k_chip_recv, k_final_send, k_final_recv,
     s_core_send, s_core_recv, s_item_send, s_item_recv, s_chip_send, s_chip_recv, s_final_send,
     s_final_recv) = refs
    grid = Grid(items, n)
    item, me = grid.item, grid.me
    rows_dev, width, channels = image.shape
    pixels = rows_dev * width
    heads, head_dim, wide = HEADS, channels // HEADS, 3 * channels // HEADS
    share = channels // n
    base = me * rows_dev
    count = (info[0, 0] * info[0, 1]).astype(F32) * (channels // GROUPS)
    scale, shift = shifts[:, :channels], shifts[:, channels:]

    def inside(row):
        return window(info, 0, row, (width, channels))

    fetched = []

    def fetch(src, dst):
        c = pltpu.make_async_copy(src, dst, load.at[len(fetched)])
        c.start()
        fetched.append(c)
        return c

    got_query = fetch(query_part, acc)
    got_dkv = fetch(dkv_in, dkv)
    got_turned = fetch(turned_in, qkv_turned)
    got_mid = fetch(middle, mid_v)
    got_cot = fetch(cot, cot_v)
    got_w2 = fetch(w2_in, weight)
    got_first = fetch(first, first_v)
    got_attn = fetch(attn_in, attn)
    got_side = fetch(side_in, side_total.at[:, :, 2 * channels :])
    got_dt = fetch(dt_in, dtext)
    got_second = fetch(second_all, rows_v)
    got_image = fetch(image, image_v)
    got_cols = fetch(text_cols, cols)
    grid.greet()
    edges = [
        Edges(grid, field, edge_send.at[j], edge_recv.at[j])
        for j, field in enumerate((grad_v, moved_v))
    ]
    for e in edges:
        e.clear()
    same[...] = group_matrix(channels)
    sums = [Sums(grid, own.at[j], slots.at[j], sum_send.at[j], sum_recv.at[j]) for j in range(3)]
    kernel_sums = [
        KernelSum(grid, turned.at[j], quarter.at[j], part.at[j], from_core.at[j], chip_sum.at[j], from_chip.at[j],
                  final.at[j], (k_item_send.at[j], k_item_recv.at[j]), (k_core_send.at[j], k_core_recv.at[j]),
                  (k_chip_send.at[j], k_chip_recv.at[j]), (k_final_send.at[j], k_final_recv.at[j]))
        for j in range(2)
    ]
    sum2, sum1 = kernel_sums
    side = SideSum(grid, side_v, side_core, side_sum, side_item, side_total, side_chip, side_final,
                   (s_core_send, s_core_recv), (s_item_send, s_item_recv), (s_chip_send, s_chip_recv),
                   (s_final_send, s_final_recv))

    core, chip, chips = lax.rem(me, 2), me // 2, n // 2
    half = heads // 2

    def text_copy(k):
        to = lax.rem(me + k, n)
        return remote(dtext.at[to], own_dt.at[me], text_send.at[0, k], text_recv.at[0, k], grid.row(k))

    def gather_copy(k):
        to = {"items": item, "rows": lax.rem(chip + k, chips) * 2 + core}
        return remote(dtext, dt.at[item, core, chip], text_send.at[1, k], text_recv.at[1, k], to)

    def dt_copy(k):
        mine = dt.at[item, core]
        return remote(mine, mine, dt_send.at[k], dt_recv.at[k], grid.peer(k))

    def dt_core_copy(k):
        mine = dt.at[lax.rem(item + k, items), core]
        sibling = {"items": item, "rows": me + 1 - 2 * core}
        return remote(mine, mine, dt_core_send.at[k], dt_core_recv.at[k], sibling)

    got_turned.wait()
    got_dkv.wait()
    got_query.wait()

    def unproject_head(h):
        rows = pl.ds(pl.multiple_of(h * wide + head_dim, head_dim), 2 * head_dim)
        acc[...] += dot(dkv[h].astype(F32).T.astype(BF16), qkv_turned[rows], 1, 0)

    each_row(heads, unproject_head)
    got_mid.wait()
    average, inverse = norm_of(stats_in[2], count, same[...])

    def grad_row(r):
        value = acc[pl.ds(r * width, width)] * inside(base + r)
        grad_v[1 + r] = value
        return value, value * ((mid_v[1 + r] - average) * inverse)

    stats = row_stats(rows_dev, width, channels, grad_row)
    grid.met()
    sums[0].start(stats)
    edges[0].start()


    got_attn.wait()

    def qkv_head(h):
        block = dot(dkv[h], attn[...], 1, 0).astype(BF16)
        for w in range(2):
            side.put_head(h, block[w * head_dim : (w + 1) * head_dim], w)

    each_row(heads, qkv_head)
    side.core_copy().start()
    got_cot.wait()

    stats4 = sums[0].result()
    got_dt.wait()
    grid.loop(n, lambda k: text_copy(k).start())
    grid.loop(chips, lambda k: gather_copy(k).start())
    own_dt[me] = dtext[me]
    dt[item, core, chip] = dtext[...]
    mean, cross = means_of(stats4, gain3[...], count, same[...])
    edges[0].wait()

    def to_grad2(r):
        normal = (mid_v[r] - average) * inverse
        ok = inside(base + r - 1)
        term = (grad_v[r] * gain3[...] - mean - normal * cross) * inverse * ok
        total = cot_v[r].astype(F32) + term
        grad_mid[r] = total
        shift_into(shifted, r, total * ok)

    each_row(rows_dev + 2, to_grad2)
    sum2.send_grads(shifted)
    got_w2.wait()
    conv_taps_back(shifted, weight, acc, rows_dev)
    got_first.wait()
    average2, inverse2 = norm_of(stats_in[1], count, same[...])

    def moved_row(r):
        ok = inside(base + r)
        normal, moved = moved_of(first_v[1 + r], ok, average2, inverse2, gain2[...], scale, shift)
        value = acc[pl.ds(r * width, width)] * ok * silu_slope(moved)
        moved_v[1 + r] = value
        return value, value * normal

    stats = row_stats(rows_dev, width, channels, moved_row)
    sums[1].start(stats)
    edges[1].start()
    got_w1 = fetch(w1_in, weight)
    got_second.wait()

    def shift_rows():
        for g in range(items):
            each_row(rows_dev + 2, lambda r: shift_into(shifted_all.at[g], r, rows_v[g, r].astype(F32)))

    shift_rows()
    got_hidden = fetch(hidden_all, rows_v)
    sum2.wait_grads()
    side.over_items()
    sum2.compute(0, shifted_all)
    sum2.compute(1, shifted_all)
    sum2.over_chips(0)
    sum2.compute(2, shifted_all)
    sum2.over_chips(1)
    sum2.over_chips(2)

    stats5 = sums[1].result()
    factor = gain2[...] * (1.0 + scale)
    mean, cross = means_of(stats5, factor, count, same[...])
    edges[1].wait()

    def to_grad1(r):
        normal = (first_v[r] - average2) * inverse2
        value = (moved_v[r] * factor - mean - normal * cross) * inverse2
        shift_into(shifted, r, value * inside(base + r - 1))

    each_row(rows_dev + 2, to_grad1)
    sum1.send_grads(shifted)
    got_w1.wait()
    conv_taps_back(shifted, weight, acc, rows_dev)
    got_image.wait()
    average1, inverse1 = norm_of(stats_in[0], count, same[...])

    def pre_row(r):
        ok = inside(base + r)
        normal = (image_v[r].astype(F32) - average1) * inverse1 * ok
        value = acc[pl.ds(r * width, width)] * ok * silu_slope(normal * gain1[...])
        pre[r] = value
        return value, value * normal

    stats = row_stats(rows_dev, width, channels, pre_row)
    sums[2].start(stats)
    tall = text_in.shape[0]
    got_text_w = [
        fetch(text_in.at[:, j * channels : (j + 1) * channels], weight.at[j * tall : (j + 1) * tall])
        for j in range(2)
    ]
    got_side.wait()
    side.over_chips()
    got_hidden.wait()
    shift_rows()
    sum1.wait_grads()
    grid.loop(chips, lambda k: gather_copy(k).wait())
    grid.loop(items, lambda k: dt_copy(k).start())
    dt_core_copy(0).start()
    sum1.compute(0, shifted_all)
    sum2.over_items(0)
    sum1.over_chips(0)
    sum1.compute(1, shifted_all)
    sum2.over_items(1)
    sum1.over_chips(1)
    sum1.compute(2, shifted_all)
    sum1.over_chips(2)
    sum2.over_items(2)
    side.spread()
    grid.loop(items, lambda k: dt_copy(k).wait())
    grid.loop(items, lambda k: dt_core_copy(k).start())

    stats6 = sums[2].result()
    e = embed[...].astype(F32)
    low = (e * sigmoid(e)).astype(BF16).astype(F32)
    vector[...] = jnp.zeros_like(vector)
    vector[0:1] = stats6[1:2]
    vector[1:2] = stats5[1:2] * (1.0 + scale)
    vector[2:3] = stats4[1:2]
    vector[3:4] = (stats5[1:2] * gain2[...]).astype(BF16).astype(F32)
    vector[4:5] = stats5[0:1].astype(BF16).astype(F32)
    for j in range(embed.shape[1] // channels):
        vector[5 + j : 6 + j] = low[:, j * channels : (j + 1) * channels]

    def vector_copy(k):
        return remote(
            vector, vector_land.at[item], vec_send.at[k], vec_recv.at[k], grid.peer(k)
        )

    grid.loop(items, lambda k: vector_copy(k).start())
    vector_land[item] = vector[...]

    mean, cross = means_of(stats6, gain1[...], count, same[...])

    def finish_row(r):
        normal = (image_v[r].astype(F32) - average1) * inverse1
        term = (pre[r] * gain1[...] - mean - normal * cross) * inverse1
        image_out[r] = (grad_mid[1 + r] + term) * inside(base + r)

    each_row(rows_dev, finish_row)
    put_image = fetch(image_out, image_grad)

    grid.loop(n, lambda k: text_copy(k).wait())
    for c in got_text_w:
        c.wait()
    total = None
    for j in range(2):
        lhs = jnp.concatenate([own_dt[j * half + h] for h in range(half)], axis=1)
        term = dot(lhs, weight[j * tall : (j + 1) * tall], 1, 1)
        total = term if total is None else total + term
    text_v[...] = total
    put_text = fetch(text_v, text_grad)
    got_embed_w = [
        fetch(embed_in.at[:, j * channels : (j + 1) * channels], weight.at[j * tall : (j + 1) * tall])
        for j in range(2)
    ]
    for a in range(3):
        sum1.over_items(a)
    for a in range(3):
        sum2.wait_final(a)
    put_final2 = fetch(final.at[0], final_out.at[0])

    dt_core_copy(0).wait()
    grid.loop(items, lambda k: dt_core_copy(k).wait())
    got_cols.wait()
    tokens = cols.shape[0] * cols.shape[1]
    flat_cols = cols[...].reshape(tokens, cols.shape[2]).astype(F32).T.astype(BF16)
    for h in range(heads):
        rhs = jnp.concatenate([dt[g, h % 2, h // 2].reshape(tokens // items, 2 * head_dim) for g in range(items)], axis=0)
        text_w_v[:, h * 2 * head_dim : (h + 1) * 2 * head_dim] = dot(flat_cols, rhs, 1, 0)
    put_text_w = fetch(text_w_v, text_w_grad)

    for c in got_embed_w:
        c.wait()
    total = None
    for j in range(2):
        lhs = vector[3 + j : 4 + j] if j else vector[3:4]
        lhs = jnp.broadcast_to(lhs, (8, channels)).astype(BF16)
        term = dot(lhs, weight[j * tall : (j + 1) * tall], 1, 1)
        total = term if total is None else total + term
    embed_v[...] = total[0:1] * silu_slope(e)
    put_embed = fetch(embed_v, embed_grad)
    grid.loop(items, lambda k: vector_copy(k).wait())
    put_vectors = fetch(vector_land, vectors)
    side.wait_final()
    put_side = fetch(side_final, side_out)
    for a in range(3):
        sum1.wait_final(a)
    put_final1 = fetch(final.at[1], final_out.at[1])
    for c in (put_image, put_text, put_final2, put_text_w, put_embed, put_vectors, put_side, put_final1):
        c.wait()


def finalize_kernel(final, side, vectors, output_in, image_in, text_in, text_w_in, embed_in,
                    output, image_grad, text_grad, text_w_grad, embed_grad, conv2, conv1, qkv, proj, embed_w,
                    gain1, gain2, gain3,
                    final_v, side_v, vector_v, conv_v, qkv_v, proj_v, embed_w_v, output_v, image_v, text_v, text_w_v,
                    embed_v, load):
    started = []

    def fetch(src, dst):
        c = pltpu.make_async_copy(src, dst, load.at[len(started)])
        c.start()
        started.append(c)
        return c

    got = [fetch(final.at[j], final_v.at[j]) for j in range(2)]
    got_vectors = fetch(vectors, vector_v)
    got_side = fetch(side, side_v)
    through = ((image_in, image_v, image_grad), (text_w_in, text_w_v, text_w_grad), (output_in, output_v, output),
               (text_in, text_v, text_grad), (embed_in, embed_v, embed_grad))
    got_through = [fetch(src, held) for src, held, _ in through]
    me = lax.axis_index("rows")
    items, rows, channels = side_v.shape[0], side_v.shape[1], side_v.shape[2] // 4
    share = items * rows
    for j, out in enumerate((conv2, conv1)):
        got[j].wait()
        for a in range(3):
            for b in range(3):
                for q in range(items):
                    conv_v[j, a * 3 + b, q * rows : (q + 1) * rows] = final_v[j, a, q, b].astype(F32)
        fetch(conv_v.at[j], out)
    for c, (_, held, dst) in zip(got_through, through):
        c.wait()
        fetch(held, dst)
    got_vectors.wait()
    total = vector_v[0]
    for g in range(1, items):
        total = total + vector_v[g]
    own = me * share
    block = channels // 4
    part = total[:, :block]
    for j in range(1, 4):
        part = jnp.where(own // block == j, total[:, j * block : (j + 1) * block], part)
    mine = part[:, :share]
    for j in range(1, block // share):
        mine = jnp.where(lax.rem(own, block) == j * share, part[:, j * share : (j + 1) * share], mine)
    for j, out in enumerate((gain1, gain2, gain3)):
        out[...] = mine[j : j + 1]
    wide = embed_w_v.shape[0]
    start = me * wide
    line = lax.broadcasted_iota(jnp.int32, (16, 1), 0)
    lhs = jnp.zeros((16, wide), F32)
    rhs = jnp.zeros((16, 2 * channels), F32)
    for g in range(items):
        row = vector_v[g, pl.ds(5 + start // channels, 1)]
        piece = row[:, :wide]
        for j in range(1, channels // wide):
            piece = jnp.where(lax.rem(start, channels) == j * wide, row[:, j * wide : (j + 1) * wide], piece)
        lhs = jnp.where(line == g, piece, lhs)
        both = jnp.concatenate([vector_v[g, 3:4], vector_v[g, 4:5]], axis=1)
        rhs = jnp.where(line == g, both, rhs)
    embed_w_v[...] = dot(lhs.astype(BF16), rhs.astype(BF16), 0, 0)
    fetch(embed_w_v, embed_w)
    got_side.wait()
    for q in range(items):
        for w in range(3):
            at = (w + 1) % 3 * share + q * rows
            qkv_v[at : at + rows] = side_v[q, :, w * channels : (w + 1) * channels].astype(F32)
        proj_v[q * rows : (q + 1) * rows] = side_v[q, :, 3 * channels :].astype(F32)
    fetch(qkv_v, qkv)
    fetch(proj_v, proj)
    for j, c in enumerate(started):
        if j > 8:
            c.wait()


def finalize_call(arrays, share):
    final, side, vectors, output, image_grad, text_grad, text_w_grad, embed_grad = arrays
    channels = output.shape[-1]
    n = channels // share
    sds = jax.ShapeDtypeStruct
    kernels = (9, share, channels)
    embed_w = (embed_grad.shape[1] // n, 2 * channels)
    outs = [sds(a.shape, a.dtype) for a in arrays[3:]]
    outs += [sds(kernels, F32)] * 2
    outs += [sds((3 * share, channels), F32), sds((share, channels), F32), sds(embed_w, F32)]
    outs += [sds((1, share), F32)] * 3
    v = pltpu.VMEM
    return pl.pallas_call(
        finalize_kernel,
        out_shape=tuple(outs),
        in_specs=[ANYWHERE] * len(arrays),
        out_specs=(ANYWHERE,) * 10 + (WHOLE,) * 3,
        scratch_shapes=[
            v(final.shape, BF16),
            v(side.shape, BF16),
            v(vectors.shape, F32),
            v((2,) + kernels, F32),
            v((3 * share, channels), F32),
            v((share, channels), F32),
            v(embed_w, F32),
            *[v(a.shape, a.dtype) for a in arrays[3:]],
            DMA((24,)),
        ],
        compiler_params=pltpu.CompilerParams(vmem_limit_bytes=62 << 20),
        name="finalize",
    )(*arrays)


def backward_call(info, embed, gains, stats, shifts, arrays, identity):
    items, n = lax.axis_size("items"), lax.axis_size("rows")
    dtext = arrays[3]
    image, text_cols, text_w = arrays[7], arrays[12], arrays[15]
    rows_dev, width, channels = image.shape
    pixels = rows_dev * width
    head_dim = channels // HEADS
    share = channels // n
    rows = share // items
    chips = n // 2
    padded = (rows_dev + 2, width, channels)
    tokens = dtext.shape[1]
    sds = jax.ShapeDtypeStruct
    outs = (
        sds(image.shape, F32),
        sds((tokens, text_w.shape[0]), F32),
        sds((text_w.shape[0] // n, 2 * channels), F32),
        sds(embed.shape, F32),
        sds((2, 3, items, 3, rows, channels), BF16),
        sds((items, rows, 4 * channels), BF16),
        sds((items, 16, channels), F32),
    )
    v = pltpu.VMEM
    scratch = [
        v((9 * channels, channels), BF16),
        v((3 * channels, channels), BF16),
        v(padded, F32),
        v(padded, F32),
        v(padded, BF16),
        v(image.shape, BF16),
        v((pixels, channels), BF16),
        v(text_cols.shape, BF16),
        v((items,) + padded, BF16),
        v((n, 2 * head_dim, pixels), BF16),
        v(dtext.shape, BF16),
        v((items, 2, chips) + dtext.shape, BF16),
        v(dtext.shape, BF16),
        v(padded, F32),
        v(padded, F32),
        v(padded, F32),
        v(image.shape, F32),
        v((pixels, channels), F32),
        v((rows_dev + 2, width, 3 * channels), BF16),
        v((items, rows_dev + 2, width, 3 * channels), BF16),
        v(image.shape, F32),
        v((tokens, text_w.shape[0]), F32),
        v((text_w.shape[0] // n, 2 * channels), F32),
        v(embed.shape, F32),
        v((channels, channels), BF16),
        v((2, items, channels // items, pixels), BF16),
        v((2, items, channels // items, pixels), BF16),
        v((2, 3, 2, 3, chips * rows, channels), BF16),
        v((2, 3, 3, chips * rows, channels), BF16),
        v((2, 3, chips, 3, rows, channels), BF16),
        v((2, 3, chips, 3, rows, channels), BF16),
        v((2, 3, items, 3, rows, channels), BF16),
        v((2, chips, items, rows, 2 * channels), BF16),
        v((chips, items, rows, 2 * channels), BF16),
        v((items, chips, rows, 2 * channels), BF16),
        v((items, chips, rows, 2 * channels), BF16),
        v((chips, rows, 4 * channels), BF16),
        v((chips, rows, 4 * channels), BF16),
        v((items, rows, 4 * channels), BF16),
        v((16, channels), F32),
        v((items, 16, channels), F32),
        v((3, channels // 64, 128), F32),
        v((3, n, channels // 64, 128), F32),
        DMA((32,)),
        DMA((3, n)),
        DMA((3, n)),
        DMA((2, 2)),
        DMA((2, 2)),
        DMA((2, n)),
        DMA((2, n)),
        DMA((items,)),
        DMA((items,)),
        DMA((items,)),
        DMA((items,)),
        DMA((items,)),
        DMA((items,)),
        DMA((2, items)),
        DMA((2, items)),
        DMA((2, 3)),
        DMA((2, 3)),
        DMA((2, 3, chips)),
        DMA((2, 3, chips)),
        DMA((2, 3, items)),
        DMA((2, 3, items)),
        DMA((1,)),
        DMA((1,)),
        DMA((items,)),
        DMA((items,)),
        DMA((chips,)),
        DMA((chips,)),
        DMA((items,)),
        DMA((items,)),
    ]
    return pl.pallas_call(
        functools.partial(backward_kernel, items, n),
        out_shape=outs,
        in_specs=[SCALARS] + [WHOLE] * 6 + [ANYWHERE] * len(arrays),
        out_specs=(ANYWHERE,) * 7,
        scratch_shapes=scratch,
        compiler_params=pltpu.CompilerParams(
            collective_id=identity, has_side_effects=True, vmem_limit_bytes=62 << 20
        ),
        cost_estimate=pl.CostEstimate(
            flops=80 * pixels * channels * channels, bytes_accessed=60 << 20, transcendentals=0
        ),
        name="backward",
    )(info, embed, *gains, stats, shifts, *arrays)


def own_shards(
    extent, image, embed, text, gain1, conv1_w, embed_w, gain2, conv2_w, gain3, qkv_w, text_w, proj_w,
    cotangent,
):
    _, rows_dev, width, channels = image.shape
    items, parts = lax.axis_size("items"), lax.axis_size("rows")
    me = lax.axis_index("rows")
    head_dim = channels // HEADS
    tokens = text.shape[1]
    share = channels // parts
    (first, middle, cot, hidden_all, second_all, attn_flat, qkv_turned, output, query_part, side_part, dkv, dtext,
     text_cols, stats, shifts) = forward_call(
        extent,
        image[0],
        cotangent[0],
        text[0],
        embed,
        (gain1, gain2, gain3),
        (
            conv1_w.reshape(3, 3 * channels, channels),
            conv2_w.reshape(3, 3 * channels, channels),
            embed_w,
            text_w,
            qkv_w,
            proj_w,
        ),
        0,
    )
    text_w_rows = text_cols.shape[3]
    image_grad, text_grad, text_w_grad, embed_grad, final, side, vectors = backward_call(
        extent,
        embed,
        (gain1, gain2, gain3),
        stats,
        shifts,
        (
            query_part,
            side_part,
            dkv,
            dtext,
            first,
            middle,
            cot,
            image[0],
            hidden_all,
            second_all,
            attn_flat,
            qkv_turned,
            text_cols.reshape(items * parts, tokens, text_w_rows),
            conv1_w.reshape(9 * channels, channels),
            conv2_w.reshape(9 * channels, channels),
            text_w,
            embed_w,
        ),
        1,
    )
    (output, image_grad, text_grad, text_w_grad, embed_grad, conv2, conv1, qkv, proj, embed_w_grad, norm1, norm2,
     norm3) = finalize_call(
        (final, side, vectors, output, image_grad, text_grad, text_w_grad, embed_grad), share
    )

    def kernel(values):
        return jnp.swapaxes(values.reshape(3, 3, share, channels), 2, 3)

    return (
        output[None],
        image_grad[None],
        embed_grad,
        text_grad[None],
        norm1[0],
        kernel(conv1),
        embed_w_grad,
        norm2[0],
        kernel(conv2),
        norm3[0],
        qkv.T,
        text_w_grad,
        proj.T,
    )


def shards(
    image, embed, text, extent, first_norm_gain1, conv1_w, embed_w, second_norm_gain2, conv2_w,
    attention_norm_gain, qkv_w, text_w, proj_w, cotangent,
):
    images, rows_dev, width, channels = image.shape
    parts = lax.axis_size("rows")
    me = lax.axis_index("rows")
    pairs = images * HEADS // parts
    head_dim = channels // HEADS
    pixels = rows_dev * width
    group = max(1, 512 // pixels)
    span = group * pixels
    chunks = parts // group
    tokens = text.shape[1]
    first_row = jnp.full((images, 1), me * rows_dev, jnp.int32)
    info = jnp.concatenate([extent, first_row], axis=1)
    gain1 = first_norm_gain1.reshape(1, channels)
    gain2 = second_norm_gain2.reshape(1, channels)
    gain3 = attention_norm_gain.reshape(1, channels)
    rowpos = me * rows_dev + jnp.arange(rows_dev, dtype=jnp.int32)
    colpos = jnp.arange(width, dtype=jnp.int32)
    inside = (rowpos[None, :, None] < extent[:, 0, None, None]) & (
        colpos[None, None, :] < extent[:, 1, None, None]
    )
    image_window = inside.astype(F32)[..., None]

    items = lax.axis_size("items")
    own_path = (
        images == 1
        and parts == HEADS
        and channels % (16 * items * parts) == 0
        and parts == 8
        and pixels % 512 == 0
        and channels % 512 == 0
        and tokens % 16 == 0
        and text.shape[2] % (128 * parts) == 0
        and text.shape[2] == embed.shape[1] <= 4 * channels
    )
    if own_path:
        return own_shards(
            extent, image, embed, text, gain1, conv1_w, embed_w, gain2, conv2_w, gain3, qkv_w, text_w,
            proj_w, cotangent,
        )

    embed_float = embed.astype(F32)
    embed_low = jax.nn.silu(embed_float).astype(BF16)
    shifts = jnp.dot(embed_low, embed_w, preferred_element_type=F32)
    qkv_turned = qkv_w.T
    proj_shaped = proj_w.reshape(HEADS, head_dim, channels)

    start = image.astype(F32) * image_window
    zeros = jnp.zeros((images, 6, channels), F32)
    stats0 = jnp.concatenate(
        [
            jnp.sum(start, axis=(1, 2))[:, None],
            jnp.sum(start * start, axis=(1, 2))[:, None],
            zeros,
        ],
        axis=1,
    )
    stats1, image_above, image_below, cot_above, cot_below = exchange(
        stats0, (image, cotangent), 0
    )
    full = jax.ShapeDtypeStruct(image.shape, F32)
    sums = jax.ShapeDtypeStruct((images, 8, channels), F32)
    padded = jax.ShapeDtypeStruct((images, rows_dev + 2, width, channels), BF16)
    first, stats, hidden = conv_call(
        conv1_kernel,
        info,
        (image, image_above, image_below, stats1, gain1),
        conv1_w,
        (full, sums, padded),
        False,
    )
    stats2, first_above, first_below, all_text = exchange(stats, (first,), 1, (text,))
    gathered_text = jnp.moveaxis(all_text, 0, 1).reshape(images, parts * tokens, text.shape[2])
    text_share = text.shape[2] // parts
    text_cols = lax.dynamic_slice_in_dim(gathered_text, me * text_share, text_share, 2)
    text_cols = lax.all_gather(text_cols, "items", axis=0, tiled=True)
    middle, stats, second = conv_call(
        conv2_kernel,
        info,
        (first, first_above, first_below, stats2, gain2, shifts, image),
        conv2_w,
        (full, sums, padded),
        False,
    )
    stats3, mid_above, mid_below = exchange(stats, (middle,), 2)
    attn_flat, qkv_pix = project(info, middle, stats3, gain3, qkv_turned)

    def to_pairs(values):
        wide = values.shape[1]
        moved = lax.all_to_all(values, "rows", split_axis=0, concat_axis=0, tiled=True)
        moved = moved.reshape(chunks, group, pairs, wide, pixels)
        return jnp.transpose(moved, (2, 0, 3, 1, 4)).reshape(pairs, chunks, wide, span)

    def from_pairs(values):
        wide = values.shape[2]
        moved = values.reshape(pairs, chunks, wide, group, pixels)
        moved = jnp.transpose(moved, (1, 3, 0, 2, 4)).reshape(parts * pairs, wide, pixels)
        return lax.all_to_all(moved, "rows", split_axis=0, concat_axis=0, tiled=True)

    qkv_pair = to_pairs(qkv_pix)
    grad_proj = (cotangent.astype(F32) * image_window).astype(BF16).reshape(images, pixels, channels)
    grad_heads = jnp.einsum(
        "ipc,hdc->ihdp", grad_proj, proj_shaped, preferred_element_type=F32
    ).astype(BF16)
    grad_pair = to_pairs(grad_heads.reshape(images * HEADS, head_dim, pixels))
    pair_results = []
    for p in range(pairs):
        pair = me * pairs + p
        item, head = pair // HEADS, pair % HEADS
        weight = lax.dynamic_slice_in_dim(text_w, head * 2 * head_dim, 2 * head_dim, 1)
        own = lax.dynamic_index_in_dim(gathered_text, item, 0, False)
        text_pair = jnp.dot(own, weight, preferred_element_type=F32).astype(BF16)
        pair_extent = lax.dynamic_slice_in_dim(extent, item, 1, 0)
        pair_results.append(attention(pair_extent, qkv_pair[p], text_pair, grad_pair[p], width))
    attended, qkv_grad_pair, text_grad_pair = (jnp.stack(r) for r in zip(*pair_results))
    qkv_back = from_pairs(qkv_grad_pair)
    heads_out = from_pairs(attended).reshape(images, HEADS, head_dim, pixels)

    attn_grad, stats = unproject(info, middle, stats3, qkv_back, qkv_turned)
    stats4, grad_above, grad_below, text_back = exchange(stats, (attn_grad,), 3, (text_grad_pair,))
    text_back = text_back.reshape(images, HEADS, parts * tokens, 2 * head_dim)
    text_all = lax.all_gather(text_back, "items", axis=0, tiled=True)
    proj_grad = jnp.einsum("ipc,ihdp->chd", grad_proj, heads_out, preferred_element_type=F32)
    qkv_grad = jnp.einsum(
        "ihwdp,ipc->hdwc",
        qkv_back.reshape(images, HEADS, 3, head_dim, pixels),
        attn_flat,
        preferred_element_type=F32,
    )
    grad_middle, moved_grad, stats, conv2_grad = conv_call(
        back2_kernel,
        info,
        (attn_grad, grad_above, grad_below, middle, mid_above, mid_below, cotangent, cot_above,
         cot_below, stats3, stats4, gain3, first, stats2, gain2, shifts),
        conv2_w,
        (full, full, sums, padded),
        True,
    )
    stats5, moved_above, moved_below = exchange(stats, (moved_grad,), 4)
    pre_grad, stats, conv1_grad = conv_call(
        back1_kernel,
        info,
        (moved_grad, moved_above, moved_below, first, first_above, first_below, stats2, stats5,
         gain2, shifts, image, stats1, gain1),
        conv1_w,
        (full, sums, padded),
        True,
    )
    (stats6,) = exchange(stats, (), 5)
    image_grad = finish(info, pre_grad, stats6, image, stats1, gain1, grad_middle)

    projected = jnp.einsum(
        "ihdp,hdc->ipc", heads_out, proj_shaped, preferred_element_type=F32
    ).reshape(image.shape)
    output = (middle + projected * image_window).astype(BF16)
    own_text = lax.dynamic_slice_in_dim(text_back, me * tokens, tokens, 2)
    text_shaped = text_w.reshape(text_w.shape[0], HEADS, 2 * head_dim)
    text_grad = jnp.einsum("ihtk,chk->itc", own_text, text_shaped, preferred_element_type=F32)
    text_w_grad = jnp.einsum(
        "gtc,ghtk->chk", text_cols, text_all, preferred_element_type=F32
    ).reshape(text_share, 2 * channels)
    scale_sum = stats5[:, 1] * gain2
    grad_shifts = jnp.concatenate([scale_sum, stats5[:, 0]], axis=1).astype(BF16)
    embed_grad = jnp.einsum(
        "ik,ck->ic", grad_shifts, embed_w, preferred_element_type=F32
    ) * silu_slope(embed_float)
    embed_share = embed_w.shape[0] // parts
    gains = jnp.stack(
        [
            jnp.sum(stats6[:, 1], axis=0),
            jnp.sum(stats5[:, 1] * (1.0 + shifts[:, :channels]), axis=0),
            jnp.sum(stats4[:, 1], axis=0),
        ]
    )
    share = channels // parts
    def total(values):
        return lax.psum(
            lax.psum_scatter(values.astype(BF16), "rows", scatter_dimension=0, tiled=True),
            "items",
        ).astype(F32)

    def kernel_total(values):
        return total(values).T.reshape(3, 3, channels, share)

    conv1_total = kernel_total(weight_grad(conv1_grad, hidden))
    conv2_total = kernel_total(weight_grad(conv2_grad, second))
    by_head = jnp.swapaxes(qkv_grad, 1, 2).reshape(3 * channels, channels)
    qkv_total = total(by_head).T
    proj_total = total(proj_grad.reshape(channels, channels)).T
    gains = lax.psum(gains, "items")
    all_shifts = lax.all_gather(grad_shifts, "items", axis=0, tiled=True)
    embed_rows = lax.dynamic_slice_in_dim(embed_low, me * embed_share, embed_share, 1)
    embed_rows = lax.all_gather(embed_rows, "items", axis=0, tiled=True)
    embed_w_grad = jnp.einsum("ic,ik->ck", embed_rows, all_shifts, preferred_element_type=F32)
    gains = lax.dynamic_slice_in_dim(gains, me * share, share, 1)
    return (
        output,
        image_grad,
        embed_grad,
        text_grad,
        gains[0],
        conv1_total,
        embed_w_grad,
        gains[1],
        conv2_total,
        gains[2],
        qkv_total,
        text_w_grad,
        proj_total,
    )


def solution(mesh):
    in_specs = (
        P("items", "rows", None, None),
        P("items", None),
        P("items", "rows", None),
        P("items", None),
        P(),
        P(),
        P(),
        P(),
        P(),
        P(),
        P(),
        P(),
        P(),
        P("items", "rows", None, None),
    )
    out_specs = (
        P("items", "rows", None, None),
        P("items", "rows", None, None),
        P("items", None),
        P("items", "rows", None),
        P("rows"),
        P(None, None, None, "rows"),
        P("rows", None),
        P("rows"),
        P(None, None, None, "rows"),
        P("rows"),
        P(None, "rows"),
        P("rows", None),
        P(None, "rows"),
    )
    return jax.shard_map(shards, mesh=mesh, in_specs=in_specs, out_specs=out_specs, check_vma=False)
```

```python
import functools

import jax
import jax.numpy as jnp
from jax import lax
from jax.experimental import pallas as pl
from jax.experimental.pallas import tpu as pltpu
from jax.sharding import PartitionSpec as P

GROUPS = 32
HEADS = 8
F32, BF16 = jnp.float32, jnp.bfloat16
NEG = -1e30


def dot(a, b, ca, cb):
    return lax.dot_general(a, b, (((ca,), (cb,)), ((), ())), preferred_element_type=F32)

def nothing(*_):
    return None


class Attention:
    def __init__(self, chunks, span, d, tlen, step, bq, scratch):
        self.chunks, self.span, self.d, self.tlen, self.step, self.bq = chunks, span, d, tlen, step, bq
        self.kn, self.vn, self.kt, self.vt, s0, s1, e0, e1, self.dkt, self.dvt = scratch
        self.scores, self.raised = (s0, s1), (e0, e1)
        self.pix = chunks * span

    def stage_key(self, c, k, width, rows_ok, cols_ok):
        d, span = self.d, self.span
        base = pl.multiple_of(c * span, span)
        pos = base + lax.broadcasted_iota(jnp.int32, (16, span), 1)
        row = lax.broadcasted_iota(jnp.int32, (16, span), 0)
        ok = (pos // width < rows_ok) & (pos % width < cols_ok)
        extra = jnp.where((row == 0) & jnp.logical_not(ok), NEG, 0.0)
        rest = jnp.zeros((128 - d - 16, span), F32)
        self.kt[:, pl.ds(base, span)] = k
        ka = jnp.concatenate([k.astype(F32), extra, rest], axis=0)
        self.kn[pl.ds(base, span), :] = ka.T.astype(BF16)

    def stage_value(self, c, v):
        d, span = self.d, self.span
        base = pl.multiple_of(c * span, span)
        row = lax.broadcasted_iota(jnp.int32, (16, span), 0)
        rest = jnp.zeros((128 - d - 16, span), F32)
        self.vt[:, pl.ds(base, span)] = v
        va = jnp.concatenate([v.astype(F32), jnp.where(row < 3, 1.0, 0.0), rest], axis=0)
        self.vn[pl.ds(base, span), :] = va.T.astype(BF16)

    def stage_text(self, text):
        d, tlen, pix = self.d, self.tlen, self.pix
        tk = text[:, :d].astype(F32)
        tv = text[:, d:].astype(F32)
        self.kt[:, pix:] = tk.T.astype(BF16)
        self.vt[:, pix:] = tv.T.astype(BF16)
        lanes = lax.broadcasted_iota(jnp.int32, (tlen, 128 - d), 1)
        rest = jnp.zeros((tlen, 128 - d), F32)
        self.kn[pix:, :] = jnp.concatenate([tk, rest], axis=1).astype(BF16)
        ones = jnp.where(lanes < 3, 1.0, 0.0)
        self.vn[pix:, :] = jnp.concatenate([tv, ones], axis=1).astype(BF16)

    def query(self, q):
        d, bq = self.d, self.bq
        r = lax.broadcasted_iota(jnp.int32, (128 - d, bq), 0)
        rest = jnp.where(r == 0, 1.0, 0.0)
        return jnp.concatenate([q.astype(F32) * (d**-0.5), rest], axis=0).astype(BF16)

    def run(self, score, exp, back):
        d, bq, step = self.d, self.bq, self.step
        kn, vn, kt, vt, dkt, dvt = self.kn, self.vn, self.kt, self.vt, self.dkt, self.dvt
        scores, raised = self.scores, self.raised

        def body(j, carry):
            pk, total, acc, dq = carry
            at = pl.ds(pl.multiple_of(j * step, step), step)
            if score:
                slot, qa = score
                s = dot(kn[at, :], qa, 1, 0)
                scores[slot][at, :] = s
                pk = jnp.maximum(pk, jnp.max(s.reshape(step // 8, 8, bq), axis=0))
            if exp:
                slot, peak = exp
                e = jnp.exp(scores[slot][at, :] - peak)
                total = total + jnp.sum(e.reshape(step // 8, 8, bq), axis=0)
                low = e.astype(BF16)
                raised[slot][at, :] = low
                acc = acc + dot(vt[:, at], low, 1, 0)
            if back:
                slot, goa, q = back
                dp = dot(vn[at, :], goa, 1, 0)
                e = raised[slot][at, :]
                ds = e * dp.astype(BF16)
                dvt[:, at] += dot(goa[:d], e, 1, 1)
                dkt[:, at] += dot(q, ds, 1, 1)
                dq = dq + dot(kt[:, at], ds, 1, 0)
            return pk, total, acc, dq

        init = (
            jnp.full((8, bq), -3e38, F32),
            jnp.zeros((8, bq), F32),
            jnp.zeros((d, bq), F32),
            jnp.zeros((d, bq), F32),
        )
        return lax.fori_loop(0, (self.pix + self.tlen) // step, body, init)

    def attended(self, go, total, acc):
        d, bq = self.d, self.bq
        inv = 1.0 / jnp.sum(total, axis=0, keepdims=True)
        o = acc * inv
        go = go.astype(F32)
        nd = -jnp.sum(go * o, axis=0, keepdims=True) * inv
        hi = nd.astype(BF16).astype(F32)
        mid = (nd - hi).astype(BF16).astype(F32)
        lo = nd - hi - mid
        r = lax.broadcasted_iota(jnp.int32, (16, bq), 0)
        extra = jnp.where(r == 0, hi, jnp.where(r == 1, mid, jnp.where(r == 2, lo, 0.0)))
        rest = jnp.zeros((128 - d - 16, bq), F32)
        return o.astype(BF16), jnp.concatenate([go * inv, extra, rest], axis=0).astype(BF16)

    def attend(self, q_ref, go_ref, o_ref, dq_ref, order, before=nothing, done=nothing):
        d, bq, chunks = self.d, self.bq, self.chunks
        self.dkt[...] = jnp.zeros_like(self.dkt)
        self.dvt[...] = jnp.zeros_like(self.dvt)

        def columns(half):
            return slice(half * bq, (half + 1) * bq)

        def q_of(h, half):
            return q_ref[order(h), :d, columns(half)]

        def finish_exp(h, half, total, acc):
            c = order(h)
            o, goa = self.attended(go_ref[c, :, columns(half)], total, acc)
            o_ref[c, :, columns(half)] = o
            return goa

        def put_dq(h, half, dq):
            dq_ref[order(h), :d, columns(half)] = (dq * (d**-0.5)).astype(BF16)

        def top(pk):
            return jnp.max(pk, axis=0, keepdims=True)

        run = self.run
        pk, _, _, _ = run((0, self.query(q_of(0, 0))), None, None)
        pk, total, acc, _ = run((1, self.query(q_of(0, 1))), (0, top(pk)), None)
        goa = finish_exp(0, 0, total, acc)

        def two(h, carry):
            pk, goa = carry
            before(h + 1)
            qa = self.query(q_of(h + 1, 0))
            pk2, total, acc, dq = run((0, qa), (1, top(pk)), (0, goa, q_of(h, 0)))
            put_dq(h, 0, dq)
            goa = finish_exp(h, 1, total, acc)
            qa = self.query(q_of(h + 1, 1))
            pk3, total, acc, dq = run((1, qa), (0, top(pk2)), (1, goa, q_of(h, 1)))
            put_dq(h, 1, dq)
            done(h)
            return pk3, finish_exp(h + 1, 0, total, acc)

        pk, goa = lax.fori_loop(0, chunks - 1, two, (pk, goa))
        last = chunks - 1
        _, total, acc, dq = run(None, (1, top(pk)), (0, goa, q_of(last, 0)))
        put_dq(last, 0, dq)
        goa = finish_exp(last, 1, total, acc)
        _, _, _, dq = run(None, None, (1, goa, q_of(last, 1)))
        put_dq(last, 1, dq)
        done(last)

    def key_grad(self, at):
        return (self.dkt[:, at] * (self.d**-0.5)).astype(BF16)

    def value_grad(self, at):
        return self.dvt[:, at].astype(BF16)

    def text_grad(self, out):
        d, pix = self.d, self.pix
        out[:, :d] = (self.dkt[:, pix:] * (d**-0.5)).T.astype(BF16)
        out[:, d:] = self.dvt[:, pix:].T.astype(BF16)


def attention_scratch(chunks, span, d, tlen):
    keys = chunks * span + tlen
    bq = span // 2
    lanes = keys // 128
    step = 128 * max(n for n in range(1, 12) if lanes % n == 0)
    shapes = [((keys, 128), BF16)] * 2 + [((d, keys), BF16)] * 2
    shapes += [((keys, bq), F32)] * 2 + [((keys, bq), BF16)] * 2 + [((d, keys), F32)] * 2
    return step, bq, [pltpu.VMEM(*shape) for shape in shapes]


def attention_kernel(width, step, bq, ext_ref, qkv_ref, text_ref, go_ref, out_ref, dqkv_ref, dtext_ref, *scratch):
    chunks, _, span = qkv_ref.shape
    d = go_ref.shape[1]
    att = Attention(chunks, span, d, text_ref.shape[0], step, bq, scratch)

    def stage(c, carry):
        att.stage_key(c, qkv_ref[c, d : 2 * d, :], width, ext_ref[0, 0], ext_ref[0, 1])
        att.stage_value(c, qkv_ref[c, 2 * d :, :])
        return carry

    lax.fori_loop(0, chunks, stage, 0)
    att.stage_text(text_ref)
    att.attend(qkv_ref, go_ref, out_ref, dqkv_ref, lambda h: h)

    def finish(c, carry):
        at = pl.ds(pl.multiple_of(c * span, span), span)
        dqkv_ref[c, d : 2 * d, :] = att.key_grad(at)
        dqkv_ref[c, 2 * d :, :] = att.value_grad(at)
        return carry

    lax.fori_loop(0, chunks, finish, 0)
    att.text_grad(dtext_ref)


def attention(ext, qkv, text, go, width):
    chunks, wide, span = qkv.shape
    d = wide // 3
    tlen = text.shape[0]
    keys = chunks * span + tlen
    step, bq, scratch = attention_scratch(chunks, span, d, tlen)
    vm = pl.BlockSpec(memory_space=pltpu.VMEM)
    flops = 2 * 6 * chunks * span * keys * d
    return pl.pallas_call(
        functools.partial(attention_kernel, width, step, bq),
        out_shape=(
            jax.ShapeDtypeStruct(go.shape, BF16),
            jax.ShapeDtypeStruct(qkv.shape, BF16),
            jax.ShapeDtypeStruct((tlen, 2 * d), BF16),
        ),
        in_specs=[pl.BlockSpec(memory_space=pltpu.SMEM), vm, vm, vm],
        out_specs=(vm, vm, vm),
        scratch_shapes=scratch,
        compiler_params=pltpu.CompilerParams(vmem_limit_bytes=56 << 20),
        cost_estimate=pl.CostEstimate(
            flops=4 * flops, bytes_accessed=16 * chunks * span * d, transcendentals=chunks * span * keys
        ),
    )(ext, qkv, text, go)


MESH = pl.DeviceIdType.MESH
EPS = 1e-05
WHOLE = pl.BlockSpec(memory_space=pltpu.VMEM)
SCALARS = pl.BlockSpec(memory_space=pltpu.SMEM)
ANYWHERE = pl.BlockSpec(memory_space=pl.ANY)


def exchange_kernel(n, count, gathers, *refs):
    inputs, refs = refs[: 1 + count + gathers], refs[1 + count + gathers :]
    outputs, refs = refs[: 1 + 2 * count + gathers], refs[1 + 2 * count + gathers :]
    stats_ref, rows, given = inputs[0], inputs[1 : 1 + count], inputs[1 + count :]
    total_ref, outs, gathered = outputs[0], outputs[1 : 1 + 2 * count], outputs[1 + 2 * count :]
    slots, lands = refs[0], refs[1 : 1 + 2 * count]
    send, recv, row_send, row_recv, own = refs[1 + 2 * count :]
    me = lax.axis_index("rows")
    barrier = pltpu.get_barrier_semaphore()

    def greet(k, carry):
        pl.semaphore_signal(
            barrier, inc=1, device_id={"rows": lax.rem(me + k, n)}, device_id_type=MESH
        )
        return carry

    lax.fori_loop(1, n, greet, 0)
    slots[me] = stats_ref[...]
    pl.semaphore_wait(barrier, n - 1)
    shared = [(stats_ref, slots)] + list(zip(given, gathered))

    def share(j, k):
        return pltpu.make_async_remote_copy(
            src_ref=shared[j][0],
            dst_ref=shared[j][1].at[me],
            send_sem=send.at[j, k],
            recv_sem=recv.at[j, k],
            device_id={"rows": lax.rem(me + k, n)},
            device_id_type=MESH,
        )

    def start(k, carry):
        share(0, k).start()
        return carry

    lax.fori_loop(1, n, start, 0)

    def row_copy(j, side):
        last = rows[j].shape[1] - 1
        at = last if side == 0 else 0
        return pltpu.make_async_remote_copy(
            src_ref=rows[j].at[:, at : at + 1],
            dst_ref=lands[2 * j + side],
            send_sem=row_send.at[2 * j + side],
            recv_sem=row_recv.at[2 * j + side],
            device_id={"rows": me + 1 if side == 0 else me - 1},
            device_id_type=MESH,
        )

    for j in range(count):

        @pl.when(me < n - 1)
        def _():
            row_copy(j, 0).start()

        @pl.when(me > 0)
        def _():
            row_copy(j, 1).start()

    for j in range(gathers):

        def start_given(k, carry):
            share(1 + j, k).start()
            return carry

        lax.fori_loop(1, n, start_given, 0)
        pltpu.make_async_copy(given[j], gathered[j].at[me], own.at[j]).start()

    def finish(k, carry):
        share(0, k).wait()
        return carry

    lax.fori_loop(1, n, finish, 0)
    total_ref[...] = lax.fori_loop(1, n, lambda k, s: s + slots[k], slots[0])
    for j in range(count):

        @pl.when(me > 0)
        def _():
            row_copy(j, 0).wait_recv()
            outs[2 * j][...] = lands[2 * j][...]

        @pl.when(me == 0)
        def _():
            outs[2 * j][...] = jnp.zeros_like(outs[2 * j])

        @pl.when(me < n - 1)
        def _():
            row_copy(j, 1).wait_recv()
            outs[2 * j + 1][...] = lands[2 * j + 1][...]
            row_copy(j, 0).wait_send()

        @pl.when(me == n - 1)
        def _():
            outs[2 * j + 1][...] = jnp.zeros_like(outs[2 * j + 1])

        @pl.when(me > 0)
        def _():
            row_copy(j, 1).wait_send()

    for j in range(gathers):

        def finish_given(k, carry):
            share(1 + j, k).wait()
            return carry

        lax.fori_loop(1, n, finish_given, 0)
        pltpu.make_async_copy(given[j], gathered[j].at[me], own.at[j]).wait()


def exchange(stats, rows, identity, given=()):
    n = lax.axis_size("rows")
    edge = []
    for array in rows:
        edge += [jax.ShapeDtypeStruct(array.shape[:1] + (1,) + array.shape[2:], array.dtype)] * 2
    whole = [jax.ShapeDtypeStruct((n,) + array.shape, array.dtype) for array in given]
    count, gathers = len(rows), len(given)
    nbytes = 4 * stats.size * n + sum(2 * e.size * e.dtype.itemsize for e in (*edge, *whole))
    return pl.pallas_call(
        functools.partial(exchange_kernel, n, count, gathers),
        out_shape=(jax.ShapeDtypeStruct(stats.shape, F32), *edge, *whole),
        in_specs=[WHOLE] + [ANYWHERE] * (count + gathers),
        out_specs=(WHOLE,) * (1 + 2 * count) + (ANYWHERE,) * gathers,
        scratch_shapes=[
            pltpu.VMEM((n,) + stats.shape, F32),
            *[pltpu.VMEM(e.shape, e.dtype) for e in edge],
            pltpu.SemaphoreType.DMA((1 + gathers, n)),
            pltpu.SemaphoreType.DMA((1 + gathers, n)),
            pltpu.SemaphoreType.DMA((max(1, 2 * count),)),
            pltpu.SemaphoreType.DMA((max(1, 2 * count),)),
            pltpu.SemaphoreType.DMA((max(1, gathers),)),
        ],
        compiler_params=pltpu.CompilerParams(collective_id=identity, has_side_effects=True),
        cost_estimate=pl.CostEstimate(
            flops=6_000_000_000, bytes_accessed=nbytes, transcendentals=0
        ),
        name=f"exchange{identity}",
    )(stats, *rows, *given)


def group_matrix(channels):
    size = channels // GROUPS
    one = lax.broadcasted_iota(jnp.int32, (channels, channels), 0) // size
    two = lax.broadcasted_iota(jnp.int32, (channels, channels), 1) // size
    return jnp.where(one == two, 1.0, 0.0).astype(BF16)


def group_sums(rows, same=None):
    if same is None:
        same = group_matrix(rows.shape[1])
    high = rows.astype(BF16).astype(F32)
    mid = (rows - high).astype(BF16).astype(F32)
    tail = rows - high - mid
    sums = dot(jnp.concatenate([high, mid, tail], axis=0).astype(BF16), same, 1, 0)
    n = rows.shape[0]
    return sums[:n] + sums[n : 2 * n] + sums[2 * n :]


def image_count(info, i, channels):
    return (info[i, 0] * info[i, 1]).astype(F32) * (channels // GROUPS)


def norm_of(stats, count, same=None):
    sums = group_sums(stats, same)
    average = sums[0:1] / count
    square = sums[1:2] / count
    return average, lax.rsqrt(square - average * average + EPS)


def means_of(stats, weight, count, same=None):
    sums = group_sums(stats * weight, same)
    return sums[0:1] / count, sums[1:2] / count


def window(info, i, row, shape):
    ok = (row >= 0) & (row < info[i, 0])
    limit = jnp.where(ok, info[i, 1], 0)
    return jnp.where(lax.broadcasted_iota(jnp.int32, shape, 0) < limit, 1.0, 0.0)


def padded_row(center, above, below, i, r):
    if r == 0:
        return above[i, 0]
    if r == center.shape[1] + 1:
        return below[i, 0]
    return center[i, r - 1]


def put_shifted(out, i, r, value, plain=None):
    width, channels = value.shape
    column = lax.broadcasted_iota(jnp.int32, value.shape, 0)
    left = jnp.where(column == 0, 0.0, pltpu.roll(value, 1, 0))
    right = jnp.where(column == width - 1, 0.0, pltpu.roll(value, width - 1, 0))
    out[i, r, :, :channels] = left.astype(BF16)
    low = value.astype(BF16)
    out[i, r, :, channels : 2 * channels] = low
    if plain is not None:
        plain[i, r] = low
    out[i, r, :, 2 * channels :] = right.astype(BF16)


def sigmoid(v):
    return 1.0 / (1.0 + jnp.exp(-v))


def silu_slope(v):
    s = sigmoid(v)
    return s * (1.0 + v * (1.0 - s))


def put_stats(stats_ref, i, first, second):
    channels = first.shape[1]
    one = jnp.sum(first, axis=0, keepdims=True)
    two = jnp.sum(second, axis=0, keepdims=True)
    row = lax.broadcasted_iota(jnp.int32, (8, channels), 0)
    stats_ref[i] = jnp.where(row == 0, one, jnp.where(row == 1, two, 0.0))


def tap_rows(shifted, tap, images, rows_dev, width):
    block = shifted[:, pl.ds(tap, rows_dev)]
    return block.reshape(images * rows_dev * width, shifted.shape[3])


def conv1_kernel(info, image, above, below, stats, gain, weight, first, out_stats, hidden, acc, shifted):
    images, rows_dev, width, channels = image.shape
    tap = pl.program_id(0)
    base = info[0, 2]

    @pl.when(tap == 0)
    def _():
        for i in range(images):
            average, inverse = norm_of(stats[i], image_count(info, i, channels))
            for r in range(rows_dev + 2):
                inside = window(info, i, base + r - 1, (width, channels))
                start = padded_row(image, above, below, i, r).astype(F32) * inside
                value = (start - average) * inverse * inside * gain[...]
                put_shifted(shifted, i, r, value * sigmoid(value) * inside, hidden)

    part = dot(tap_rows(shifted, tap, images, rows_dev, width), weight[0], 1, 0)

    @pl.when(tap == 0)
    def _():
        acc[...] = part

    @pl.when(tap > 0)
    def _():
        acc[...] += part

    @pl.when(tap == 2)
    def _():
        for i in range(images):
            one = two = jnp.zeros((width, channels), F32)
            for r in range(rows_dev):
                inside = window(info, i, base + r, (width, channels))
                at = (i * rows_dev + r) * width
                value = acc[at : at + width] * inside
                first[i, r] = value
                one = one + value
                two = two + value * value
            put_stats(out_stats, i, one, two)


def moved_of(value, inside, average, inverse, gain, scale, shift):
    normal = (value - average) * inverse * inside
    return normal, normal * gain * (1.0 + scale) + shift


def conv2_kernel(
    info, first, above, below, stats, gain, shifts, image, weight, middle, out_stats, second, acc,
    shifted,
):
    images, rows_dev, width, channels = first.shape
    tap = pl.program_id(0)
    base = info[0, 2]

    @pl.when(tap == 0)
    def _():
        for i in range(images):
            average, inverse = norm_of(stats[i], image_count(info, i, channels))
            scale, shift = shifts[i : i + 1, :channels], shifts[i : i + 1, channels:]
            for r in range(rows_dev + 2):
                inside = window(info, i, base + r - 1, (width, channels))
                value = padded_row(first, above, below, i, r)
                _, moved = moved_of(value, inside, average, inverse, gain[...], scale, shift)
                put_shifted(shifted, i, r, moved * sigmoid(moved) * inside, second)

    part = dot(tap_rows(shifted, tap, images, rows_dev, width), weight[0], 1, 0)

    @pl.when(tap == 0)
    def _():
        acc[...] = part

    @pl.when(tap > 0)
    def _():
        acc[...] += part

    @pl.when(tap == 2)
    def _():
        for i in range(images):
            one = two = jnp.zeros((width, channels), F32)
            for r in range(rows_dev):
                inside = window(info, i, base + r, (width, channels))
                at = (i * rows_dev + r) * width
                value = (image[i, r].astype(F32) + acc[at : at + width]) * inside
                middle[i, r] = value
                one = one + value
                two = two + value * value
            put_stats(out_stats, i, one, two)


def dgrad(shifted, tap, weight, images, rows_dev, width):
    channels = weight.shape[2]
    lhs = tap_rows(shifted, tap, images, rows_dev, width)
    part = None
    for b in range(3):
        term = dot(
            lhs[:, b * channels : (b + 1) * channels],
            weight[0, (2 - b) * channels : (3 - b) * channels, :],
            1,
            1,
        )
        part = term if part is None else part + term
    return part


def back2_kernel(
    info, grad, grad_above, grad_below, middle, mid_above, mid_below, cot, cot_above, cot_below,
    mid_stats, grad_stats, attn_gain, first, first_stats, gain, shifts, weight,
    grad_middle, moved_grad, out_stats, plain, acc, shifted,
):
    images, rows_dev, width, channels = first.shape
    tap = pl.program_id(0)
    base = info[0, 2]

    @pl.when(tap == 0)
    def _():
        for i in range(images):
            count = image_count(info, i, channels)
            average, inverse = norm_of(mid_stats[i], count)
            mean, cross = means_of(grad_stats[i], attn_gain[...], count)
            for r in range(rows_dev + 2):
                inside = window(info, i, base + r - 1, (width, channels))
                normal = (padded_row(middle, mid_above, mid_below, i, r) - average) * inverse
                dx = padded_row(grad, grad_above, grad_below, i, r) * attn_gain[...]
                term = (dx - mean - normal * cross) * inverse * inside
                total = padded_row(cot, cot_above, cot_below, i, r).astype(F32) + term
                if 0 < r <= rows_dev:
                    grad_middle[i, r - 1] = total
                put_shifted(shifted, i, r, total * inside, plain)

    part = dgrad(shifted, tap, weight, images, rows_dev, width)

    @pl.when(tap == 0)
    def _():
        acc[...] = part

    @pl.when(tap > 0)
    def _():
        acc[...] += part

    @pl.when(tap == 2)
    def _():
        for i in range(images):
            average, inverse = norm_of(first_stats[i], image_count(info, i, channels))
            scale, shift = shifts[i : i + 1, :channels], shifts[i : i + 1, channels:]
            one = two = jnp.zeros((width, channels), F32)
            for r in range(rows_dev):
                inside = window(info, i, base + r, (width, channels))
                at = (i * rows_dev + r) * width
                normal, moved = moved_of(
                    first[i, r], inside, average, inverse, gain[...], scale, shift
                )
                value = acc[at : at + width] * inside * silu_slope(moved)
                moved_grad[i, r] = value
                one = one + value
                two = two + value * normal
            put_stats(out_stats, i, one, two)


def back1_kernel(
    info, grad, grad_above, grad_below, first, first_above, first_below, first_stats, grad_stats,
    gain, shifts, image, image_stats, first_gain, weight,
    pre_grad, out_stats, plain, acc, shifted,
):
    images, rows_dev, width, channels = first.shape
    tap = pl.program_id(0)
    base = info[0, 2]

    @pl.when(tap == 0)
    def _():
        for i in range(images):
            count = image_count(info, i, channels)
            average, inverse = norm_of(first_stats[i], count)
            factor = gain[...] * (1.0 + shifts[i : i + 1, :channels])
            mean, cross = means_of(grad_stats[i], factor, count)
            for r in range(rows_dev + 2):
                inside = window(info, i, base + r - 1, (width, channels))
                normal = (padded_row(first, first_above, first_below, i, r) - average) * inverse
                dx = padded_row(grad, grad_above, grad_below, i, r) * factor
                put_shifted(shifted, i, r, (dx - mean - normal * cross) * inverse * inside, plain)

    part = dgrad(shifted, tap, weight, images, rows_dev, width)

    @pl.when(tap == 0)
    def _():
        acc[...] = part

    @pl.when(tap > 0)
    def _():
        acc[...] += part

    @pl.when(tap == 2)
    def _():
        for i in range(images):
            average, inverse = norm_of(image_stats[i], image_count(info, i, channels))
            one = two = jnp.zeros((width, channels), F32)
            for r in range(rows_dev):
                inside = window(info, i, base + r, (width, channels))
                at = (i * rows_dev + r) * width
                normal = (image[i, r].astype(F32) - average) * inverse * inside
                slope = silu_slope(normal * first_gain[...])
                value = acc[at : at + width] * inside * slope
                pre_grad[i, r] = value
                one = one + value
                two = two + value * normal
            put_stats(out_stats, i, one, two)


def conv_call(kernel, info, inputs, weight, outs, flipped):
    images, rows_dev, width, channels = outs[0].shape

    def whole(shape):
        return pl.BlockSpec(shape, lambda tap: (0,) * len(shape))

    def tap_of(tap):
        return ((2 - tap) if flipped else tap, 0, 0)

    weight = weight.reshape(3, 3 * channels, channels)
    flops = 2 * 9 * images * rows_dev * width * channels * channels
    moved = sum(a.size * a.dtype.itemsize for a in (*inputs, weight, *outs))
    return pl.pallas_call(
        kernel,
        grid=(3,),
        out_shape=tuple(outs),
        in_specs=[SCALARS]
        + [whole(a.shape) for a in inputs]
        + [pl.BlockSpec((1, 3 * channels, channels), tap_of)],
        out_specs=tuple(whole(o.shape) for o in outs),
        scratch_shapes=[
            pltpu.VMEM((images * rows_dev * width, channels), F32),
            pltpu.VMEM((images, rows_dev + 2, width, 3 * channels), BF16),
        ],
        compiler_params=pltpu.CompilerParams(vmem_limit_bytes=48 << 20),
        cost_estimate=pl.CostEstimate(flops=flops, bytes_accessed=moved, transcendentals=0),
        name=kernel.__name__,
    )(info, *inputs, weight)


def weight_grad_kernel(grads, hidden, out, turned, shifted):
    images, padded, width, channels = hidden.shape
    rows_dev = padded - 2
    pixels = images * rows_dev * width
    tap = pl.program_id(0)

    @pl.when(tap == 0)
    def _():
        center = grads[:, 1 : rows_dev + 1]
        turned[...] = center.reshape(pixels, channels).astype(F32).T.astype(BF16)
        for i in range(images):
            for r in range(padded):
                put_shifted(shifted, i, r, hidden[i, r].astype(F32))

    column = pl.multiple_of((tap % 3) * channels, channels)
    rhs = shifted[:, pl.ds(tap // 3, rows_dev), :, pl.ds(column, channels)]
    out[...] = dot(turned[...], rhs.reshape(pixels, channels), 1, 0).astype(BF16)


def weight_grad(grads, hidden):
    images, padded, width, channels = hidden.shape
    pixels = images * (padded - 2) * width

    def whole(shape):
        return pl.BlockSpec(shape, lambda tap: (0,) * len(shape))

    return pl.pallas_call(
        weight_grad_kernel,
        grid=(9,),
        out_shape=jax.ShapeDtypeStruct((channels, 9 * channels), BF16),
        in_specs=[whole(grads.shape), whole(hidden.shape)],
        out_specs=pl.BlockSpec((channels, channels), lambda tap: (0, tap)),
        scratch_shapes=[
            pltpu.VMEM((channels, pixels), BF16),
            pltpu.VMEM(hidden.shape[:3] + (3 * channels,), BF16),
        ],
        compiler_params=pltpu.CompilerParams(vmem_limit_bytes=32 << 20),
        cost_estimate=pl.CostEstimate(
            flops=18 * pixels * channels * channels,
            bytes_accessed=18 * channels * channels,
            transcendentals=0,
        ),
        name="weight_grad",
    )(grads, hidden)


def project_kernel(info, middle, stats, gain, weight, attn, qkv):
    images, rows_dev, width, channels = middle.shape
    pixels = rows_dev * width
    heads, wide = HEADS, weight.shape[0] // HEADS
    base = info[0, 2]
    for i in range(images):
        average, inverse = norm_of(stats[i], image_count(info, i, channels))
        for r in range(rows_dev):
            inside = window(info, i, base + r, (width, channels))
            value = (middle[i, r] - average) * inverse * inside * gain[...]
            attn[i, r * width : (r + 1) * width] = value.astype(BF16)
        for h in range(heads):
            block = dot(weight[h * wide : (h + 1) * wide], attn[i], 1, 1)
            qkv[i * heads + h] = block.astype(BF16)


def project(info, middle, stats, gain, weight):
    images, rows_dev, width, channels = middle.shape
    pixels = rows_dev * width
    return pl.pallas_call(
        project_kernel,
        out_shape=(
            jax.ShapeDtypeStruct((images, pixels, channels), BF16),
            jax.ShapeDtypeStruct((images * HEADS, weight.shape[0] // HEADS, pixels), BF16),
        ),
        in_specs=[SCALARS, WHOLE, WHOLE, WHOLE, WHOLE],
        out_specs=(WHOLE, WHOLE),
        compiler_params=pltpu.CompilerParams(vmem_limit_bytes=32 << 20),
        name="project",
    )(info, middle, stats, gain, weight)


def unproject_kernel(info, middle, stats, grads, weight, out, out_stats):
    images, rows_dev, width, channels = middle.shape
    wide, pixels = grads.shape[1], grads.shape[2]
    base = info[0, 2]
    for i in range(images):
        average, inverse = norm_of(stats[i], image_count(info, i, channels))
        acc = None
        for h in range(HEADS):
            turned = grads[i * HEADS + h].astype(F32).T.astype(BF16)
            term = dot(turned, weight[h * wide : (h + 1) * wide], 1, 0)
            acc = term if acc is None else acc + term
        one = two = jnp.zeros((width, channels), F32)
        for r in range(rows_dev):
            inside = window(info, i, base + r, (width, channels))
            value = acc[r * width : (r + 1) * width] * inside
            out[i, r] = value
            one = one + value
            two = two + value * ((middle[i, r] - average) * inverse)
        put_stats(out_stats, i, one, two)


def unproject(info, middle, stats, grads, weight):
    images, rows_dev, width, channels = middle.shape
    return pl.pallas_call(
        unproject_kernel,
        out_shape=(
            jax.ShapeDtypeStruct(middle.shape, F32),
            jax.ShapeDtypeStruct(stats.shape, F32),
        ),
        in_specs=[SCALARS, WHOLE, WHOLE, WHOLE, WHOLE],
        out_specs=(WHOLE, WHOLE),
        compiler_params=pltpu.CompilerParams(vmem_limit_bytes=32 << 20),
        name="unproject",
    )(info, middle, stats, grads, weight)


def finish_kernel(info, pre_grad, grad_stats, image, stats, gain, grad_middle, out):
    images, rows_dev, width, channels = image.shape
    base = info[0, 2]
    for i in range(images):
        count = image_count(info, i, channels)
        average, inverse = norm_of(stats[i], count)
        mean, cross = means_of(grad_stats[i], gain[...], count)
        for r in range(rows_dev):
            inside = window(info, i, base + r, (width, channels))
            normal = (image[i, r].astype(F32) - average) * inverse
            term = (pre_grad[i, r] * gain[...] - mean - normal * cross) * inverse
            out[i, r] = (grad_middle[i, r] + term) * inside


def finish(info, pre_grad, grad_stats, image, stats, gain, grad_middle):
    return pl.pallas_call(
        finish_kernel,
        out_shape=jax.ShapeDtypeStruct(image.shape, F32),
        in_specs=[SCALARS] + [WHOLE] * 6,
        out_specs=WHOLE,
        compiler_params=pltpu.CompilerParams(vmem_limit_bytes=32 << 20),
        name="finish",
    )(info, pre_grad, grad_stats, image, stats, gain, grad_middle)


DMA = pltpu.SemaphoreType.DMA


def remote(src, dst, send, recv, device):
    return pltpu.make_async_remote_copy(
        src_ref=src,
        dst_ref=dst,
        send_sem=send,
        recv_sem=recv,
        device_id=device,
        device_id_type=MESH,
    )


class Grid:
    def __init__(self, items, n):
        self.items, self.n = items, n
        self.item, self.me = lax.axis_index("items"), lax.axis_index("rows")

    def row(self, k):
        return {"items": self.item, "rows": lax.rem(self.me + k, self.n)}

    def peer(self, k):
        return {"items": lax.rem(self.item + k, self.items), "rows": self.me}

    def greet(self):
        barrier = pltpu.get_barrier_semaphore()

        def rows(k, carry):
            pl.semaphore_signal(barrier, inc=1, device_id=self.row(k), device_id_type=MESH)
            return carry

        def items(k, carry):
            pl.semaphore_signal(barrier, inc=1, device_id=self.peer(k), device_id_type=MESH)
            return carry

        lax.fori_loop(1, self.n, rows, 0)
        lax.fori_loop(1, self.items, items, 0)

    def met(self):
        pl.semaphore_wait(pltpu.get_barrier_semaphore(), self.n + self.items - 2)

    def loop(self, count, body):
        def step(k, carry):
            body(k)
            return carry

        lax.fori_loop(1, count, step, 0)


class Sums:
    def __init__(self, grid, own, slots, send, recv):
        self.grid, self.own, self.slots, self.send, self.recv = grid, own, slots, send, recv

    def copy(self, k):
        return remote(
            self.own, self.slots.at[self.grid.me], self.send.at[k], self.recv.at[k], self.grid.row(k)
        )

    def start(self, stats):
        lines, lanes = self.own.shape
        half = lines // 2
        at = lax.broadcasted_iota(jnp.int32, (lines, lanes), 0)
        packed = jnp.zeros((lines, lanes), F32)
        for j in range(lines):
            piece = stats[j // half : j // half + 1, (j % half) * lanes : (j % half + 1) * lanes]
            packed = jnp.where(at == j, piece, packed)
        self.own[...] = packed
        self.grid.loop(self.grid.n, lambda k: self.copy(k).start())
        self.slots[self.grid.me] = packed

    def result(self):
        self.grid.loop(self.grid.n, lambda k: self.copy(k).wait())
        slots = self.slots
        total = lax.fori_loop(1, self.grid.n, lambda k, s: s + slots[k], slots[0])
        half = total.shape[0] // 2
        rows = [
            jnp.concatenate([total[r * half + j : r * half + j + 1] for j in range(half)], axis=1)
            for r in range(2)
        ]
        at = lax.broadcasted_iota(jnp.int32, (8, rows[0].shape[1]), 0)
        return jnp.where(at == 0, rows[0], jnp.where(at == 1, rows[1], 0.0))


class Edges:
    def __init__(self, grid, field, send, recv):
        self.grid, self.field, self.send, self.recv = grid, field, send, recv

    def copy(self, side):
        last = self.field.shape[0] - 1
        at, to = (last - 1, 0) if side == 0 else (1, last)
        grid = self.grid
        return remote(
            self.field.at[at : at + 1],
            self.field.at[to : to + 1],
            self.send.at[side],
            self.recv.at[side],
            {"items": grid.item, "rows": grid.me + 1 if side == 0 else grid.me - 1},
        )

    def both(self, down, up):
        @pl.when(self.grid.me < self.grid.n - 1)
        def _():
            down()

        @pl.when(self.grid.me > 0)
        def _():
            up()

    def clear(self):
        last = self.field.shape[0] - 1

        @pl.when(self.grid.me == 0)
        def _():
            self.field[0] = jnp.zeros(self.field.shape[1:], self.field.dtype)

        @pl.when(self.grid.me == self.grid.n - 1)
        def _():
            self.field[last] = jnp.zeros(self.field.shape[1:], self.field.dtype)

    def start(self):
        self.both(lambda: self.copy(0).start(), lambda: self.copy(1).start())

    def wait(self):
        self.both(lambda: self.copy(1).wait_recv(), lambda: self.copy(0).wait_recv())
        self.both(lambda: self.copy(0).wait_send(), lambda: self.copy(1).wait_send())


def shift_into(out, r, value):
    width, channels = value.shape
    column = lax.broadcasted_iota(jnp.int32, value.shape, 0)
    left = jnp.where(column == 0, 0.0, pltpu.roll(value, 1, 0))
    right = jnp.where(column == width - 1, 0.0, pltpu.roll(value, width - 1, 0))
    out[r, :, :channels] = left.astype(BF16)
    out[r, :, channels : 2 * channels] = value.astype(BF16)
    out[r, :, 2 * channels :] = right.astype(BF16)


def row_stats(rows, width, channels, row):
    def step(r, carry):
        one, two = row(r)
        return carry[0] + one, carry[1] + two

    zero = jnp.zeros((width, channels), F32)
    one, two = lax.fori_loop(0, rows, step, (zero, zero))
    one = jnp.sum(one, axis=0, keepdims=True)
    two = jnp.sum(two, axis=0, keepdims=True)
    at = lax.broadcasted_iota(jnp.int32, (8, channels), 0)
    return jnp.where(at == 0, one, jnp.where(at == 1, two, 0.0))


def each_row(rows, body):
    def step(r, carry):
        body(r)
        return carry

    lax.fori_loop(0, rows, step, 0)


def conv_taps(shifted, weight, acc, rows_dev):
    pixels, wide = acc.shape[0], shifted.shape[2]
    acc[...] = jnp.zeros_like(acc)

    def step(tap, carry):
        acc[...] += dot(shifted[pl.ds(tap, rows_dev)].reshape(pixels, wide), weight[tap], 1, 0)
        return carry

    lax.fori_loop(0, 3, step, 0)


def forward_kernel(items, n, step, bq, *refs):
    (info, image, cot, text, embed, gain1, gain2, gain3, w1_in, w2_in, embed_in, text_in, qkv_in, proj_in,
     first_out, mid_out, cot_out, hidden_all, second_all, attn_out, turned_out, output, query_part, side_out, dkv_out,
     dt_out, text_cols, stats_out, shifts_out,
     image_v, cot_v, text_v, w1, w2, wide_w, qkv_w, proj_w, first_v, mid_v, hidden, second, attn,
     turned, pairs, queries, go, text_kv, cols, shifted, acc, own, slots,
     pair_land, query_land, go_land, text_pair, o, dq, dkv, dtext, same, o_land, dq_land, masked, out_v, query_acc,
     side_v, side_core, side_sum, side_item, side_total, cols_land,
     load, sum_send, sum_recv, edge_send, edge_recv, row_send, row_recv, item_send, item_recv,
     s_core_send, s_core_recv, s_item_send, s_item_recv, *scratch) = refs
    grid = Grid(items, n)
    grid.greet()
    item, me = grid.item, grid.me
    rows_dev, width, channels = image.shape
    pixels = rows_dev * width
    heads, head_dim, wide = HEADS, channels // HEADS, 3 * channels // HEADS
    base = me * rows_dev
    share_rows = channels // n
    count = (info[0, 0] * info[0, 1]).astype(F32) * (channels // GROUPS)
    att = Attention(n, pixels, head_dim, n * text.shape[0], step, bq, scratch)

    def inside(row):
        return window(info, 0, row, (width, channels))

    loads = []

    def fetch(src, dst):
        c = pltpu.make_async_copy(src, dst, load.at[len(loads)])
        c.start()
        loads.append(c)
        return c

    center = slice(1, rows_dev + 1)
    got_image = fetch(image, image_v.at[center])
    got_cot = fetch(cot, cot_v.at[center])
    got_proj = fetch(proj_in, proj_w)
    got_text = fetch(text, text_v)
    got_text_w = fetch(text_in, wide_w)
    got_w1 = fetch(w1_in, w1)
    got_w2 = fetch(w2_in, w2)
    got_qkv_w = fetch(qkv_in, qkv_w)
    edges = [
        Edges(grid, field, edge_send.at[j], edge_recv.at[j])
        for j, field in enumerate((image_v, cot_v, first_v, mid_v))
    ]
    sums = [Sums(grid, own.at[j], slots.at[j], sum_send.at[j], sum_recv.at[j]) for j in range(3)]
    for e in edges:
        e.clear()
    same[...] = group_matrix(channels)
    got_image.wait()

    def start_row(r):
        return image_v[1 + r].astype(F32) * inside(base + r)

    def start_stats(r):
        v = start_row(r)
        return v, v * v

    stats = row_stats(rows_dev, width, channels, start_stats)
    grid.met()
    sums[0].start(stats)
    edges[0].start()
    got_cot.wait()
    edges[1].start()

    got_text.wait()
    got_text_w.wait()
    text_all = dot(text_v[...], wide_w[...], 1, 0).astype(BF16)
    got_embed_w = fetch(embed_in, wide_w)
    share = text_v.shape[1] // n
    for h in range(heads):
        text_kv[h] = text_all[:, h * 2 * head_dim : (h + 1) * 2 * head_dim]
    for r in range(n):
        cols[r] = text_v[:, r * share : (r + 1) * share]

    def scatter(j, src, dst):
        def copy(k):
            to = lax.rem(me + k, n)
            return remote(src.at[to], dst.at[me], row_send.at[j, k], row_recv.at[j, k], grid.row(k))

        return copy

    kv_copy = scatter(0, text_kv, text_pair)
    col_copy = scatter(1, cols, cols_land)
    grid.loop(n, lambda k: kv_copy(k).start())
    grid.loop(n, lambda k: col_copy(k).start())
    own_kv = fetch(text_kv.at[me], text_pair.at[me])
    cols_land[me] = cols[me]

    got_proj.wait()

    def to_grad(r):
        masked[pl.ds(r * width, width)] = (cot_v[1 + r].astype(F32) * inside(base + r)).astype(BF16)

    each_row(rows_dev, to_grad)
    for h in range(heads):
        go[h] = dot(proj_w[h * head_dim : (h + 1) * head_dim], masked[...], 1, 1).astype(BF16)
    go_copy = scatter(2, go, go_land)
    own_go = fetch(go.at[me], go_land.at[me])

    stats = sums[0].result()
    stats_out[0] = stats
    average, inverse = norm_of(stats, count, same[...])
    edges[0].wait()
    grid.loop(n // 2, lambda k: go_copy(k).start())

    def to_hidden(r):
        ok = inside(base + r - 1)
        value = (image_v[r].astype(F32) * ok - average) * inverse * ok * gain1[...]
        value = value * sigmoid(value) * ok
        shift_into(shifted, r, value)
        hidden[r] = value.astype(BF16)

    each_row(rows_dev + 2, to_hidden)

    def spread(j, src, dst):
        def copy(k):
            return remote(src, dst.at[item], item_send.at[j, k], item_recv.at[j, k], grid.peer(k))

        return copy

    hidden_copy = spread(0, hidden, hidden_all)
    grid.loop(items, lambda k: hidden_copy(k).start())
    own_hidden = fetch(hidden, hidden_all.at[item])
    got_w1.wait()
    conv_taps(shifted, w1, acc, rows_dev)

    def first_row(r):
        value = acc[pl.ds(r * width, width)] * inside(base + r)
        first_v[1 + r] = value
        return value, value * value

    stats = row_stats(rows_dev, width, channels, first_row)
    sums[1].start(stats)
    edges[2].start()

    e = embed[...].astype(F32)
    low = (e * sigmoid(e)).astype(BF16)
    got_embed_w.wait()
    shifts_out[...] = dot(low, wide_w[...], 1, 0)
    scale, shift = shifts_out[:, :channels], shifts_out[:, channels:]

    stats = sums[1].result()
    stats_out[1] = stats
    average, inverse = norm_of(stats, count, same[...])
    edges[2].wait()
    own_first = fetch(first_v, first_out)

    def to_second(r):
        ok = inside(base + r - 1)
        _, moved = moved_of(first_v[r], ok, average, inverse, gain2[...], scale, shift)
        value = moved * sigmoid(moved) * ok
        shift_into(shifted, r, value)
        second[r] = value.astype(BF16)

    each_row(rows_dev + 2, to_second)
    second_copy = spread(1, second, second_all)
    grid.loop(items, lambda k: second_copy(k).start())
    own_second = fetch(second, second_all.at[item])
    got_w2.wait()
    conv_taps(shifted, w2, acc, rows_dev)

    def middle_row(r):
        value = (image_v[1 + r].astype(F32) + acc[pl.ds(r * width, width)]) * inside(base + r)
        mid_v[1 + r] = value
        return value, value * value

    stats = row_stats(rows_dev, width, channels, middle_row)
    sums[2].start(stats)
    edges[3].start()
    edges[1].wait()
    own_cot = fetch(cot_v, cot_out)
    got_qkv_w.wait()
    for j in range(3):
        block = qkv_w[:, j * channels : (j + 1) * channels].astype(F32).T
        turned[j * channels : (j + 1) * channels] = block.astype(BF16)
    own_turned = fetch(turned, turned_out)

    stats = sums[2].result()
    stats_out[2] = stats
    average, inverse = norm_of(stats, count, same[...])

    def to_attn(r):
        value = (mid_v[1 + r] - average) * inverse * inside(base + r) * gain3[...]
        attn[pl.ds(r * width, width)] = value.astype(BF16)

    each_row(rows_dev, to_attn)
    own_attn = fetch(attn, attn_out)
    pair_copy = scatter(3, pairs, pair_land)
    query_copy = scatter(4, queries, query_land)

    def head(k):
        to = lax.rem(me + k, n)
        rows = pl.ds(pl.multiple_of(to * wide, wide), wide)
        block = dot(turned[rows], attn[...], 1, 1).astype(BF16)
        queries[to] = block[:head_dim]
        pairs[to] = block[head_dim:]

    def send_head(k):
        head(k)
        pair_copy(k).start()

    grid.loop(n, send_head)
    head(0)
    query_land[me] = queries[me]
    att.stage_key(me, pairs[me, :head_dim], width, info[0, 0], info[0, 1])
    att.stage_value(me, pairs[me, head_dim:])
    grid.loop(n, lambda k: kv_copy(k).wait())
    own_kv.wait()
    att.stage_text(text_pair[...].reshape(n * text.shape[0], 2 * head_dim))
    edges[3].wait()
    own_mid = fetch(mid_v, mid_out)

    def source(k):
        return lax.rem(me + n - k, n)

    def stage_pair(k):
        pair_copy(k).wait()
        c = source(k)
        att.stage_key(c, pair_land[c, :head_dim], width, info[0, 0], info[0, 1])
        att.stage_value(c, pair_land[c, head_dim:])

    grid.loop(n, stage_pair)

    def send_rest(k):
        query_copy(k).start()

        @pl.when(k >= n // 2)
        def _():
            go_copy(k).start()

    grid.loop(n, send_rest)
    own_go.wait()

    def before(k):
        query_copy(k).wait()
        go_copy(k).wait()

    def give(j, src, dst):
        def copy(h):
            to = source(h)
            return remote(
                src.at[to],
                dst.at[me],
                row_send.at[j, h],
                row_recv.at[j, h],
                {"items": item, "rows": to},
            )

        return copy

    o_copy = give(5, o, o_land)
    dq_copy = give(6, dq, dq_land)
    dkv_copy = give(7, dkv, dkv_out)

    def done(h):
        @pl.when(h > 0)
        def _():
            o_copy(h).start()
            dq_copy(h).start()

    grid.loop(n, lambda k: col_copy(k).wait())
    cols_copy = spread(2, cols_land, text_cols)
    grid.loop(items, lambda k: cols_copy(k).start())
    own_cols = fetch(cols_land, text_cols.at[item])
    att.attend(query_land, go_land, o, dq, source, before, done)

    def send_keys(h):
        at = pl.ds(pl.multiple_of(source(h) * pixels, pixels), pixels)
        dkv[source(h), :head_dim] = att.key_grad(at)
        dkv[source(h), head_dim:] = att.value_grad(at)

    def send_next(h):
        send_keys(h)
        dkv_copy(h).start()

    grid.loop(n, send_next)
    send_keys(0)
    flat = jnp.concatenate(
        [
            (att.dkt[:, n * pixels :] * (head_dim**-0.5)).T,
            att.dvt[:, n * pixels :].T,
        ],
        axis=1,
    )
    for r in range(n):
        tokens = text.shape[0]
        dtext[r] = flat[r * tokens : (r + 1) * tokens].astype(BF16)

    own_dkv = fetch(dkv.at[me], dkv_out.at[me])
    own_dt = fetch(dtext, dt_out)

    o_land[me] = o[me]
    dq_land[me] = dq[me]
    grid.loop(n, lambda h: o_copy(h).wait())
    grid.loop(n, lambda h: dq_copy(h).wait())
    side = SideSum(grid, side_v, side_core, side_sum, side_item, side_total, None, None,
                   (s_core_send, s_core_recv), (s_item_send, s_item_recv), None, None)

    def query_head(h):
        block = dot(dq_land[h], attn[...], 1, 0).astype(BF16)
        side.put_head(h, block, 0)

    each_row(heads, query_head)
    flat_o = o_land[...].reshape(channels, pixels)
    block = dot(masked[...].astype(F32).T.astype(BF16), flat_o, 1, 1).astype(BF16)
    for r in range(n):
        side.put_head(r, block[r * share_rows : (r + 1) * share_rows], 1)
    side.core_copy().start()
    query_acc[...] = jnp.zeros_like(query_acc)

    def unproject_query(h):
        rows = pl.ds(pl.multiple_of(h * wide, wide), head_dim)
        query_acc[...] += dot(dq_land[h].astype(F32).T.astype(BF16), turned[rows], 1, 0)

    each_row(heads, unproject_query)
    put_query = fetch(query_acc, query_part)
    side.over_items()
    acc[...] = dot(flat_o.astype(F32).T.astype(BF16), proj_w[...], 1, 0)

    def output_row(r):
        value = mid_v[1 + r] + acc[pl.ds(r * width, width)] * inside(base + r)
        out_v[r] = value.astype(BF16)

    each_row(rows_dev, output_row)
    put_output = fetch(out_v, output)
    side.sum_items()
    put_side = fetch(side_total, side_out)
    grid.loop(items, lambda k: hidden_copy(k).wait())
    grid.loop(items, lambda k: second_copy(k).wait())
    grid.loop(items, lambda k: cols_copy(k).wait())
    grid.loop(n, lambda h: dkv_copy(h).wait())
    for c in (own_hidden, own_first, own_second, own_cot, own_turned, own_attn, own_mid, own_dkv, own_dt,
              own_cols, put_query, put_output, put_side):
        c.wait()


def forward_call(info, image, cot, text, embed, gains, weights, identity):
    items, n = lax.axis_size("items"), lax.axis_size("rows")
    rows_dev, width, channels = image.shape
    pixels = rows_dev * width
    padded = (rows_dev + 2, width, channels)
    tokens, text_width = text.shape
    head_dim = channels // HEADS
    w1, w2, _, text_w, qkv_w, proj_w = weights
    chips = n // 2
    rows = channels // n // items
    sds = jax.ShapeDtypeStruct
    outs = (
        sds(padded, F32),
        sds(padded, F32),
        sds(padded, BF16),
        sds((items,) + padded, BF16),
        sds((items,) + padded, BF16),
        sds((pixels, channels), BF16),
        sds((3 * channels, channels), BF16),
        sds(image.shape, BF16),
        sds((pixels, channels), F32),
        sds((chips, rows, 2 * channels), BF16),
        sds((n, 2 * head_dim, pixels), BF16),
        sds((n, tokens, 2 * head_dim), BF16),
        sds((items, n, tokens, text_width // n), BF16),
        sds((3, 8, channels), F32),
        sds((1, 2 * channels), F32),
    )
    v = pltpu.VMEM
    scratch = [
        v(padded, BF16),
        v(padded, BF16),
        v(text.shape, BF16),
        v(w1.shape, BF16),
        v(w2.shape, BF16),
        v(text_w.shape, BF16),
        v(qkv_w.shape, BF16),
        v(proj_w.shape, BF16),
        v(padded, F32),
        v(padded, F32),
        v(padded, BF16),
        v(padded, BF16),
        v((pixels, channels), BF16),
        v((3 * channels, channels), BF16),
        v((n, 2 * head_dim, pixels), BF16),
        v((n, head_dim, pixels), BF16),
        v((n, head_dim, pixels), BF16),
        v((n, tokens, 2 * head_dim), BF16),
        v((n, tokens, text_width // n), BF16),
        v((rows_dev + 2, width, 3 * channels), BF16),
        v((pixels, channels), F32),
        v((3, channels // 64, 128), F32),
        v((3, n, channels // 64, 128), F32),
        v((n, 2 * head_dim, pixels), BF16),
        v((n, head_dim, pixels), BF16),
        v((n, head_dim, pixels), BF16),
        v((n, tokens, 2 * head_dim), BF16),
        v((n, head_dim, pixels), BF16),
        v((n, head_dim, pixels), BF16),
        v((n, 2 * head_dim, pixels), BF16),
        v((n, tokens, 2 * head_dim), BF16),
        v((channels, channels), BF16),
        v((n, head_dim, pixels), BF16),
        v((n, head_dim, pixels), BF16),
        v((pixels, channels), BF16),
        v(image.shape, BF16),
        v((pixels, channels), F32),
        v((2, chips, items, rows, 2 * channels), BF16),
        v((chips, items, rows, 2 * channels), BF16),
        v((items, chips, rows, 2 * channels), BF16),
        v((items, chips, rows, 2 * channels), BF16),
        v((chips, rows, 2 * channels), BF16),
        v((n, tokens, text_width // n), BF16),
        DMA((28,)),
        DMA((3, n)),
        DMA((3, n)),
        DMA((4, 2)),
        DMA((4, 2)),
        DMA((8, n)),
        DMA((8, n)),
        DMA((3, items)),
        DMA((3, items)),
        DMA((1,)),
        DMA((1,)),
        DMA((items,)),
        DMA((items,)),
    ]
    step, bq, extra = attention_scratch(n, pixels, head_dim, n * tokens)
    scratch += extra
    return pl.pallas_call(
        functools.partial(forward_kernel, items, n, step, bq),
        out_shape=outs,
        in_specs=[SCALARS] + [ANYWHERE] * 3 + [WHOLE] * 4 + [ANYWHERE] * 6,
        out_specs=(ANYWHERE,) * 13 + (WHOLE,) * 2,
        scratch_shapes=scratch,
        compiler_params=pltpu.CompilerParams(
            collective_id=identity, has_side_effects=True, vmem_limit_bytes=62 << 20
        ),
        cost_estimate=pl.CostEstimate(
            flops=40 * pixels * channels * channels, bytes_accessed=60 << 20, transcendentals=0
        ),
        name="forward",
    )(info, image, cot, text, embed, *gains, *weights)


class KernelSum:
    def __init__(self, grid, turned, quarter, part, from_core, chip_sum, from_chip, final, item_sems, core_sems,
                 chip_sems, final_sems):
        self.grid = grid
        self.turned, self.quarter, self.part, self.from_core = turned, quarter, part, from_core
        self.chip_sum, self.from_chip, self.final = chip_sum, from_chip, final
        self.item_sems, self.core_sems = item_sems, core_sems
        self.chip_sems, self.final_sems = chip_sems, final_sems
        self.chips = grid.n // 2
        self.chip, self.core = grid.me // 2, lax.rem(grid.me, 2)

    def grads_copy(self, k):
        grid = self.grid
        send, recv = self.item_sems
        to = lax.rem(grid.item + k, grid.items)
        return remote(
            self.turned.at[to], self.quarter.at[grid.item], send.at[k], recv.at[k], grid.peer(k)
        )

    def send_grads(self, shifted):
        grid, chips = self.grid, self.chips
        rows_dev, width, channels = shifted.shape[0] - 2, shifted.shape[1], shifted.shape[2] // 3
        center = shifted[1 : rows_dev + 1, :, channels : 2 * channels]
        block = center.reshape(rows_dev * width, channels).astype(F32).T.astype(BF16)
        share = channels // grid.n
        rows = share // grid.items
        for z in range(chips):
            for c in range(2):
                for q in range(grid.items):
                    at = (z * 2 + c) * share + q * rows
                    to = (c * chips + z) * rows
                    self.turned[q, to : to + rows] = block[at : at + rows]
        grid.loop(grid.items, lambda k: self.grads_copy(k).start())
        self.quarter[grid.item] = self.turned[grid.item]

    def wait_grads(self):
        self.grid.loop(self.grid.items, lambda k: self.grads_copy(k).wait())

    def core_copy(self, a):
        send, recv = self.core_sems
        grid = self.grid
        return remote(
            self.part.at[a, 1 - self.core],
            self.from_core.at[a],
            send.at[a],
            recv.at[a],
            {"items": grid.item, "rows": grid.me + 1 - 2 * self.core},
        )

    def compute(self, a, shifted):
        items, padded, width, wide = shifted.shape
        rows_dev, channels = padded - 2, wide // 3
        half = self.turned.shape[1] // 2
        for b in range(3):
            acc = None
            for g in range(items):
                rhs = shifted[g, a : a + rows_dev, :, b * channels : (b + 1) * channels]
                term = dot(self.quarter[g], rhs.reshape(rows_dev * width, channels), 1, 0)
                acc = term if acc is None else acc + term
            self.part[a, 0, b] = acc[:half].astype(BF16)
            self.part[a, 1, b] = acc[half:].astype(BF16)
        self.core_copy(a).start()

    def chip_copy(self, a, k):
        send, recv = self.chip_sems
        grid = self.grid
        to = lax.rem(self.chip + k, self.chips)
        return remote(
            self.chip_sum.at[a, to],
            self.from_chip.at[a, k],
            send.at[a, k],
            recv.at[a, k],
            {"items": grid.item, "rows": to * 2 + self.core},
        )

    def over_chips(self, a):
        self.core_copy(a).wait()
        rows = self.chip_sum.shape[3]
        for b in range(3):
            both = self.part[a, self.core, b].astype(F32) + self.from_core[a, b].astype(F32)
            for z in range(self.chips):
                self.chip_sum[a, z, b] = both[z * rows : (z + 1) * rows].astype(BF16)
        for k in range(1, self.chips):
            self.chip_copy(a, k).start()

    def final_copy(self, a, k):
        send, recv = self.final_sems
        mine = self.final.at[a, self.grid.item]
        return remote(mine, mine, send.at[a, k], recv.at[a, k], self.grid.peer(k))

    def over_items(self, a):
        for k in range(1, self.chips):
            self.chip_copy(a, k).wait()
        total = self.chip_sum[a, self.chip].astype(F32)
        for k in range(1, self.chips):
            total = total + self.from_chip[a, k].astype(F32)
        self.final[a, self.grid.item] = total.astype(BF16)
        for k in range(1, self.grid.items):
            self.final_copy(a, k).start()

    def wait_final(self, a):
        for k in range(1, self.grid.items):
            self.final_copy(a, k).wait()


class SideSum:
    def __init__(self, grid, values, from_core, core_sum, from_item, item_sum, from_chip, final, core_sems,
                 item_sems, chip_sems, final_sems):
        self.grid = grid
        self.values, self.from_core, self.core_sum = values, from_core, core_sum
        self.from_item, self.item_sum, self.from_chip, self.final = (
            from_item,
            item_sum,
            from_chip,
            final,
        )
        self.core_sems, self.item_sems = core_sems, item_sems
        self.chip_sems, self.final_sems = chip_sems, final_sems
        self.chips = grid.n // 2
        self.chip, self.core = grid.me // 2, lax.rem(grid.me, 2)

    def core_copy(self):
        send, recv = self.core_sems
        grid = self.grid
        return remote(
            self.values.at[1 - self.core],
            self.from_core,
            send.at[0],
            recv.at[0],
            {"items": grid.item, "rows": grid.me + 1 - 2 * self.core},
        )

    def item_copy(self, k):
        send, recv = self.item_sems
        grid = self.grid
        to = lax.rem(grid.item + k, grid.items)
        return remote(
            self.core_sum.at[to], self.from_item.at[k], send.at[k], recv.at[k], grid.peer(k)
        )

    def over_items(self):
        self.core_copy().wait()
        for z in range(self.chips):
            both = self.values[self.core, z].astype(F32) + self.from_core[z].astype(F32)
            for q in range(self.grid.items):
                self.core_sum[q, z] = both[q].astype(BF16)
        for k in range(1, self.grid.items):
            self.item_copy(k).start()

    def chip_copy(self, k):
        send, recv = self.chip_sems
        grid = self.grid
        to = lax.rem(self.chip + k, self.chips)
        return remote(
            self.item_sum.at[to],
            self.from_chip.at[k],
            send.at[k],
            recv.at[k],
            {"items": grid.item, "rows": to * 2 + self.core},
        )

    def put_head(self, h, block, j):
        items, rows = self.values.shape[2], self.values.shape[3]
        channels = block.shape[1]
        at = slice(j * channels, (j + 1) * channels)
        core, chip = (h % 2, h // 2) if isinstance(h, int) else (lax.rem(h, 2), h // 2)
        self.values[core, chip, :, :, at] = block.reshape(items, rows, channels)

    def sum_items(self):
        for k in range(1, self.grid.items):
            self.item_copy(k).wait()
        total = self.core_sum[self.grid.item].astype(F32)
        for k in range(1, self.grid.items):
            total = total + self.from_item[k].astype(F32)
        self.item_sum[:, :, : total.shape[2]] = total.astype(BF16)

    def over_chips(self):
        self.sum_items()
        for k in range(1, self.chips):
            self.chip_copy(k).start()

    def final_copy(self, k):
        send, recv = self.final_sems
        mine = self.final.at[self.grid.item]
        return remote(mine, mine, send.at[k], recv.at[k], self.grid.peer(k))

    def spread(self):
        for k in range(1, self.chips):
            self.chip_copy(k).wait()
        total = self.item_sum[self.chip].astype(F32)
        for k in range(1, self.chips):
            total = total + self.from_chip[k].astype(F32)
        self.final[self.grid.item] = total.astype(BF16)
        for k in range(1, self.grid.items):
            self.final_copy(k).start()

    def wait_final(self):
        for k in range(1, self.grid.items):
            self.final_copy(k).wait()


def conv_taps_back(shifted, weight, acc, rows_dev):
    pixels, channels = acc.shape
    acc[...] = jnp.zeros_like(acc)

    def step(tap, carry):
        lhs = shifted[pl.ds(tap, rows_dev)].reshape(pixels, 3 * channels)
        total = None
        for b in range(3):
            at = pl.multiple_of(((2 - tap) * 3 + 2 - b) * channels, channels)
            term = dot(
                lhs[:, b * channels : (b + 1) * channels], weight[pl.ds(at, channels)], 1, 1
            )
            total = term if total is None else total + term
        acc[...] += total
        return carry

    lax.fori_loop(0, 3, step, 0)


def backward_kernel(items, n, *refs):
    (info, embed, gain1, gain2, gain3, stats_in, shifts,
     query_part, side_in, dkv_in, dt_in, first, middle, cot, image, hidden_all, second_all, attn_in,
     turned_in, text_cols, w1_in, w2_in, text_in, embed_in,
     image_grad, text_grad, text_w_grad, embed_grad, final_out, side_out, vectors,
     weight, qkv_turned, first_v, mid_v, cot_v, image_v, attn, cols, rows_v, dkv, dtext, dt, own_dt,
     grad_v, grad_mid, moved_v, pre, acc, shifted, shifted_all, image_out, text_v, text_w_v, embed_v, same,
     turned, quarter, part, from_core, chip_sum, from_chip, final,
     side_v, side_core, side_sum, side_item, side_total, side_chip, side_final,
     vector, vector_land, own, slots,
     load, sum_send, sum_recv, edge_send, edge_recv, text_send, text_recv, dt_send, dt_recv, dt_core_send, dt_core_recv, vec_send, vec_recv,
     k_item_send, k_item_recv, k_core_send, k_core_recv, k_chip_send, k_chip_recv, k_final_send, k_final_recv,
     s_core_send, s_core_recv, s_item_send, s_item_recv, s_chip_send, s_chip_recv, s_final_send,
     s_final_recv) = refs
    grid = Grid(items, n)
    item, me = grid.item, grid.me
    rows_dev, width, channels = image.shape
    pixels = rows_dev * width
    heads, head_dim, wide = HEADS, channels // HEADS, 3 * channels // HEADS
    share = channels // n
    base = me * rows_dev
    count = (info[0, 0] * info[0, 1]).astype(F32) * (channels // GROUPS)
    scale, shift = shifts[:, :channels], shifts[:, channels:]

    def inside(row):
        return window(info, 0, row, (width, channels))

    fetched = []

    def fetch(src, dst):
        c = pltpu.make_async_copy(src, dst, load.at[len(fetched)])
        c.start()
        fetched.append(c)
        return c

    got_query = fetch(query_part, acc)
    got_dkv = fetch(dkv_in, dkv)
    got_turned = fetch(turned_in, qkv_turned)
    got_mid = fetch(middle, mid_v)
    got_cot = fetch(cot, cot_v)
    got_w2 = fetch(w2_in, weight)
    got_first = fetch(first, first_v)
    got_attn = fetch(attn_in, attn)
    got_side = fetch(side_in, side_total.at[:, :, 2 * channels :])
    got_dt = fetch(dt_in, dtext)
    got_second = fetch(second_all, rows_v)
    got_image = fetch(image, image_v)
    got_cols = fetch(text_cols, cols)
    grid.greet()
    edges = [
        Edges(grid, field, edge_send.at[j], edge_recv.at[j])
        for j, field in enumerate((grad_v, moved_v))
    ]
    for e in edges:
        e.clear()
    same[...] = group_matrix(channels)
    sums = [Sums(grid, own.at[j], slots.at[j], sum_send.at[j], sum_recv.at[j]) for j in range(3)]
    kernel_sums = [
        KernelSum(grid, turned.at[j], quarter.at[j], part.at[j], from_core.at[j], chip_sum.at[j], from_chip.at[j],
                  final.at[j], (k_item_send.at[j], k_item_recv.at[j]), (k_core_send.at[j], k_core_recv.at[j]),
                  (k_chip_send.at[j], k_chip_recv.at[j]), (k_final_send.at[j], k_final_recv.at[j]))
        for j in range(2)
    ]
    sum2, sum1 = kernel_sums
    side = SideSum(grid, side_v, side_core, side_sum, side_item, side_total, side_chip, side_final,
                   (s_core_send, s_core_recv), (s_item_send, s_item_recv), (s_chip_send, s_chip_recv),
                   (s_final_send, s_final_recv))

    core, chip, chips = lax.rem(me, 2), me // 2, n // 2
    half = heads // 2

    def text_copy(k):
        to = lax.rem(me + k, n)
        return remote(dtext.at[to], own_dt.at[me], text_send.at[0, k], text_recv.at[0, k], grid.row(k))

    def gather_copy(k):
        to = {"items": item, "rows": lax.rem(chip + k, chips) * 2 + core}
        return remote(dtext, dt.at[item, core, chip], text_send.at[1, k], text_recv.at[1, k], to)

    def dt_copy(k):
        mine = dt.at[item, core]
        return remote(mine, mine, dt_send.at[k], dt_recv.at[k], grid.peer(k))

    def dt_core_copy(k):
        mine = dt.at[lax.rem(item + k, items), core]
        sibling = {"items": item, "rows": me + 1 - 2 * core}
        return remote(mine, mine, dt_core_send.at[k], dt_core_recv.at[k], sibling)

    got_turned.wait()
    got_dkv.wait()
    got_query.wait()

    def unproject_head(h):
        rows = pl.ds(pl.multiple_of(h * wide + head_dim, head_dim), 2 * head_dim)
        acc[...] += dot(dkv[h].astype(F32).T.astype(BF16), qkv_turned[rows], 1, 0)

    each_row(heads, unproject_head)
    got_mid.wait()
    average, inverse = norm_of(stats_in[2], count, same[...])

    def grad_row(r):
        value = acc[pl.ds(r * width, width)] * inside(base + r)
        grad_v[1 + r] = value
        return value, value * ((mid_v[1 + r] - average) * inverse)

    stats = row_stats(rows_dev, width, channels, grad_row)
    grid.met()
    sums[0].start(stats)
    edges[0].start()


    got_attn.wait()

    def qkv_head(h):
        block = dot(dkv[h], attn[...], 1, 0).astype(BF16)
        for w in range(2):
            side.put_head(h, block[w * head_dim : (w + 1) * head_dim], w)

    each_row(heads, qkv_head)
    side.core_copy().start()
    got_cot.wait()

    stats4 = sums[0].result()
    got_dt.wait()
    grid.loop(n, lambda k: text_copy(k).start())
    grid.loop(chips, lambda k: gather_copy(k).start())
    own_dt[me] = dtext[me]
    dt[item, core, chip] = dtext[...]
    mean, cross = means_of(stats4, gain3[...], count, same[...])
    edges[0].wait()

    def to_grad2(r):
        normal = (mid_v[r] - average) * inverse
        ok = inside(base + r - 1)
        term = (grad_v[r] * gain3[...] - mean - normal * cross) * inverse * ok
        total = cot_v[r].astype(F32) + term
        grad_mid[r] = total
        shift_into(shifted, r, total * ok)

    each_row(rows_dev + 2, to_grad2)
    sum2.send_grads(shifted)
    got_w2.wait()
    conv_taps_back(shifted, weight, acc, rows_dev)
    got_first.wait()
    average2, inverse2 = norm_of(stats_in[1], count, same[...])

    def moved_row(r):
        ok = inside(base + r)
        normal, moved = moved_of(first_v[1 + r], ok, average2, inverse2, gain2[...], scale, shift)
        value = acc[pl.ds(r * width, width)] * ok * silu_slope(moved)
        moved_v[1 + r] = value
        return value, value * normal

    stats = row_stats(rows_dev, width, channels, moved_row)
    sums[1].start(stats)
    edges[1].start()
    got_w1 = fetch(w1_in, weight)
    got_second.wait()

    def shift_rows():
        for g in range(items):
            each_row(rows_dev + 2, lambda r: shift_into(shifted_all.at[g], r, rows_v[g, r].astype(F32)))

    shift_rows()
    got_hidden = fetch(hidden_all, rows_v)
    sum2.wait_grads()
    side.over_items()
    sum2.compute(0, shifted_all)
    sum2.compute(1, shifted_all)
    sum2.over_chips(0)
    sum2.compute(2, shifted_all)
    sum2.over_chips(1)
    sum2.over_chips(2)

    stats5 = sums[1].result()
    factor = gain2[...] * (1.0 + scale)
    mean, cross = means_of(stats5, factor, count, same[...])
    edges[1].wait()

    def to_grad1(r):
        normal = (first_v[r] - average2) * inverse2
        value = (moved_v[r] * factor - mean - normal * cross) * inverse2
        shift_into(shifted, r, value * inside(base + r - 1))

    each_row(rows_dev + 2, to_grad1)
    sum1.send_grads(shifted)
    got_w1.wait()
    conv_taps_back(shifted, weight, acc, rows_dev)
    got_image.wait()
    average1, inverse1 = norm_of(stats_in[0], count, same[...])

    def pre_row(r):
        ok = inside(base + r)
        normal = (image_v[r].astype(F32) - average1) * inverse1 * ok
        value = acc[pl.ds(r * width, width)] * ok * silu_slope(normal * gain1[...])
        pre[r] = value
        return value, value * normal

    stats = row_stats(rows_dev, width, channels, pre_row)
    sums[2].start(stats)
    tall = text_in.shape[0]
    got_text_w = [
        fetch(text_in.at[:, j * channels : (j + 1) * channels], weight.at[j * tall : (j + 1) * tall])
        for j in range(2)
    ]
    got_side.wait()
    side.over_chips()
    got_hidden.wait()
    shift_rows()
    sum1.wait_grads()
    grid.loop(chips, lambda k: gather_copy(k).wait())
    grid.loop(items, lambda k: dt_copy(k).start())
    dt_core_copy(0).start()
    sum1.compute(0, shifted_all)
    sum2.over_items(0)
    sum1.over_chips(0)
    sum1.compute(1, shifted_all)
    sum2.over_items(1)
    sum1.over_chips(1)
    sum1.compute(2, shifted_all)
    sum1.over_chips(2)
    sum2.over_items(2)
    side.spread()
    grid.loop(items, lambda k: dt_copy(k).wait())
    grid.loop(items, lambda k: dt_core_copy(k).start())

    stats6 = sums[2].result()
    e = embed[...].astype(F32)
    low = (e * sigmoid(e)).astype(BF16).astype(F32)
    vector[...] = jnp.zeros_like(vector)
    vector[0:1] = stats6[1:2]
    vector[1:2] = stats5[1:2] * (1.0 + scale)
    vector[2:3] = stats4[1:2]
    vector[3:4] = (stats5[1:2] * gain2[...]).astype(BF16).astype(F32)
    vector[4:5] = stats5[0:1].astype(BF16).astype(F32)
    for j in range(embed.shape[1] // channels):
        vector[5 + j : 6 + j] = low[:, j * channels : (j + 1) * channels]

    def vector_copy(k):
        return remote(
            vector, vector_land.at[item], vec_send.at[k], vec_recv.at[k], grid.peer(k)
        )

    grid.loop(items, lambda k: vector_copy(k).start())
    vector_land[item] = vector[...]

    mean, cross = means_of(stats6, gain1[...], count, same[...])

    def finish_row(r):
        normal = (image_v[r].astype(F32) - average1) * inverse1
        term = (pre[r] * gain1[...] - mean - normal * cross) * inverse1
        image_out[r] = (grad_mid[1 + r] + term) * inside(base + r)

    each_row(rows_dev, finish_row)
    put_image = fetch(image_out, image_grad)

    grid.loop(n, lambda k: text_copy(k).wait())
    for c in got_text_w:
        c.wait()
    total = None
    for j in range(2):
        lhs = jnp.concatenate([own_dt[j * half + h] for h in range(half)], axis=1)
        term = dot(lhs, weight[j * tall : (j + 1) * tall], 1, 1)
        total = term if total is None else total + term
    text_v[...] = total
    put_text = fetch(text_v, text_grad)
    got_embed_w = [
        fetch(embed_in.at[:, j * channels : (j + 1) * channels], weight.at[j * tall : (j + 1) * tall])
        for j in range(2)
    ]
    for a in range(3):
        sum1.over_items(a)
    for a in range(3):
        sum2.wait_final(a)
    put_final2 = fetch(final.at[0], final_out.at[0])

    dt_core_copy(0).wait()
    grid.loop(items, lambda k: dt_core_copy(k).wait())
    got_cols.wait()
    tokens = cols.shape[0] * cols.shape[1]
    flat_cols = cols[...].reshape(tokens, cols.shape[2]).astype(F32).T.astype(BF16)
    for h in range(heads):
        rhs = jnp.concatenate([dt[g, h % 2, h // 2].reshape(tokens // items, 2 * head_dim) for g in range(items)], axis=0)
        text_w_v[:, h * 2 * head_dim : (h + 1) * 2 * head_dim] = dot(flat_cols, rhs, 1, 0)
    put_text_w = fetch(text_w_v, text_w_grad)

    for c in got_embed_w:
        c.wait()
    total = None
    for j in range(2):
        lhs = vector[3 + j : 4 + j] if j else vector[3:4]
        lhs = jnp.broadcast_to(lhs, (8, channels)).astype(BF16)
        term = dot(lhs, weight[j * tall : (j + 1) * tall], 1, 1)
        total = term if total is None else total + term
    embed_v[...] = total[0:1] * silu_slope(e)
    put_embed = fetch(embed_v, embed_grad)
    grid.loop(items, lambda k: vector_copy(k).wait())
    put_vectors = fetch(vector_land, vectors)
    side.wait_final()
    put_side = fetch(side_final, side_out)
    for a in range(3):
        sum1.wait_final(a)
    put_final1 = fetch(final.at[1], final_out.at[1])
    for c in (put_image, put_text, put_final2, put_text_w, put_embed, put_vectors, put_side, put_final1):
        c.wait()


def finalize_kernel(final, side, vectors, output_in, image_in, text_in, text_w_in, embed_in,
                    output, image_grad, text_grad, text_w_grad, embed_grad, conv2, conv1, qkv, proj, embed_w,
                    gain1, gain2, gain3,
                    final_v, side_v, vector_v, conv_v, qkv_v, proj_v, embed_w_v, output_v, image_v, text_v, text_w_v,
                    embed_v, load):
    started = []

    def fetch(src, dst):
        c = pltpu.make_async_copy(src, dst, load.at[len(started)])
        c.start()
        started.append(c)
        return c

    got = [fetch(final.at[j], final_v.at[j]) for j in range(2)]
    got_vectors = fetch(vectors, vector_v)
    got_side = fetch(side, side_v)
    through = ((image_in, image_v, image_grad), (text_w_in, text_w_v, text_w_grad), (output_in, output_v, output),
               (text_in, text_v, text_grad), (embed_in, embed_v, embed_grad))
    got_through = [fetch(src, held) for src, held, _ in through]
    me = lax.axis_index("rows")
    items, rows, channels = side_v.shape[0], side_v.shape[1], side_v.shape[2] // 4
    share = items * rows
    for j, out in enumerate((conv2, conv1)):
        got[j].wait()
        for a in range(3):
            for b in range(3):
                for q in range(items):
                    conv_v[j, a * 3 + b, q * rows : (q + 1) * rows] = final_v[j, a, q, b].astype(F32)
        fetch(conv_v.at[j], out)
    for c, (_, held, dst) in zip(got_through, through):
        c.wait()
        fetch(held, dst)
    got_vectors.wait()
    total = vector_v[0]
    for g in range(1, items):
        total = total + vector_v[g]
    own = me * share
    block = channels // 4
    part = total[:, :block]
    for j in range(1, 4):
        part = jnp.where(own // block == j, total[:, j * block : (j + 1) * block], part)
    mine = part[:, :share]
    for j in range(1, block // share):
        mine = jnp.where(lax.rem(own, block) == j * share, part[:, j * share : (j + 1) * share], mine)
    for j, out in enumerate((gain1, gain2, gain3)):
        out[...] = mine[j : j + 1]
    wide = embed_w_v.shape[0]
    start = me * wide
    line = lax.broadcasted_iota(jnp.int32, (16, 1), 0)
    lhs = jnp.zeros((16, wide), F32)
    rhs = jnp.zeros((16, 2 * channels), F32)
    for g in range(items):
        row = vector_v[g, pl.ds(5 + start // channels, 1)]
        piece = row[:, :wide]
        for j in range(1, channels // wide):
            piece = jnp.where(lax.rem(start, channels) == j * wide, row[:, j * wide : (j + 1) * wide], piece)
        lhs = jnp.where(line == g, piece, lhs)
        both = jnp.concatenate([vector_v[g, 3:4], vector_v[g, 4:5]], axis=1)
        rhs = jnp.where(line == g, both, rhs)
    embed_w_v[...] = dot(lhs.astype(BF16), rhs.astype(BF16), 0, 0)
    fetch(embed_w_v, embed_w)
    got_side.wait()
    for q in range(items):
        for w in range(3):
            at = (w + 1) % 3 * share + q * rows
            qkv_v[at : at + rows] = side_v[q, :, w * channels : (w + 1) * channels].astype(F32)
        proj_v[q * rows : (q + 1) * rows] = side_v[q, :, 3 * channels :].astype(F32)
    fetch(qkv_v, qkv)
    fetch(proj_v, proj)
    for j, c in enumerate(started):
        if j > 8:
            c.wait()


def finalize_call(arrays, share):
    final, side, vectors, output, image_grad, text_grad, text_w_grad, embed_grad = arrays
    channels = output.shape[-1]
    n = channels // share
    sds = jax.ShapeDtypeStruct
    kernels = (9, share, channels)
    embed_w = (embed_grad.shape[1] // n, 2 * channels)
    outs = [sds(a.shape, a.dtype) for a in arrays[3:]]
    outs += [sds(kernels, F32)] * 2
    outs += [sds((3 * share, channels), F32), sds((share, channels), F32), sds(embed_w, F32)]
    outs += [sds((1, share), F32)] * 3
    v = pltpu.VMEM
    return pl.pallas_call(
        finalize_kernel,
        out_shape=tuple(outs),
        in_specs=[ANYWHERE] * len(arrays),
        out_specs=(ANYWHERE,) * 10 + (WHOLE,) * 3,
        scratch_shapes=[
            v(final.shape, BF16),
            v(side.shape, BF16),
            v(vectors.shape, F32),
            v((2,) + kernels, F32),
            v((3 * share, channels), F32),
            v((share, channels), F32),
            v(embed_w, F32),
            *[v(a.shape, a.dtype) for a in arrays[3:]],
            DMA((24,)),
        ],
        compiler_params=pltpu.CompilerParams(vmem_limit_bytes=62 << 20),
        name="finalize",
    )(*arrays)


def backward_call(info, embed, gains, stats, shifts, arrays, identity):
    items, n = lax.axis_size("items"), lax.axis_size("rows")
    dtext = arrays[3]
    image, text_cols, text_w = arrays[7], arrays[12], arrays[15]
    rows_dev, width, channels = image.shape
    pixels = rows_dev * width
    head_dim = channels // HEADS
    share = channels // n
    rows = share // items
    chips = n // 2
    padded = (rows_dev + 2, width, channels)
    tokens = dtext.shape[1]
    sds = jax.ShapeDtypeStruct
    outs = (
        sds(image.shape, F32),
        sds((tokens, text_w.shape[0]), F32),
        sds((text_w.shape[0] // n, 2 * channels), F32),
        sds(embed.shape, F32),
        sds((2, 3, items, 3, rows, channels), BF16),
        sds((items, rows, 4 * channels), BF16),
        sds((items, 16, channels), F32),
    )
    v = pltpu.VMEM
    scratch = [
        v((9 * channels, channels), BF16),
        v((3 * channels, channels), BF16),
        v(padded, F32),
        v(padded, F32),
        v(padded, BF16),
        v(image.shape, BF16),
        v((pixels, channels), BF16),
        v(text_cols.shape, BF16),
        v((items,) + padded, BF16),
        v((n, 2 * head_dim, pixels), BF16),
        v(dtext.shape, BF16),
        v((items, 2, chips) + dtext.shape, BF16),
        v(dtext.shape, BF16),
        v(padded, F32),
        v(padded, F32),
        v(padded, F32),
        v(image.shape, F32),
        v((pixels, channels), F32),
        v((rows_dev + 2, width, 3 * channels), BF16),
        v((items, rows_dev + 2, width, 3 * channels), BF16),
        v(image.shape, F32),
        v((tokens, text_w.shape[0]), F32),
        v((text_w.shape[0] // n, 2 * channels), F32),
        v(embed.shape, F32),
        v((channels, channels), BF16),
        v((2, items, channels // items, pixels), BF16),
        v((2, items, channels // items, pixels), BF16),
        v((2, 3, 2, 3, chips * rows, channels), BF16),
        v((2, 3, 3, chips * rows, channels), BF16),
        v((2, 3, chips, 3, rows, channels), BF16),
        v((2, 3, chips, 3, rows, channels), BF16),
        v((2, 3, items, 3, rows, channels), BF16),
        v((2, chips, items, rows, 2 * channels), BF16),
        v((chips, items, rows, 2 * channels), BF16),
        v((items, chips, rows, 2 * channels), BF16),
        v((items, chips, rows, 2 * channels), BF16),
        v((chips, rows, 4 * channels), BF16),
        v((chips, rows, 4 * channels), BF16),
        v((items, rows, 4 * channels), BF16),
        v((16, channels), F32),
        v((items, 16, channels), F32),
        v((3, channels // 64, 128), F32),
        v((3, n, channels // 64, 128), F32),
        DMA((32,)),
        DMA((3, n)),
        DMA((3, n)),
        DMA((2, 2)),
        DMA((2, 2)),
        DMA((2, n)),
        DMA((2, n)),
        DMA((items,)),
        DMA((items,)),
        DMA((items,)),
        DMA((items,)),
        DMA((items,)),
        DMA((items,)),
        DMA((2, items)),
        DMA((2, items)),
        DMA((2, 3)),
        DMA((2, 3)),
        DMA((2, 3, chips)),
        DMA((2, 3, chips)),
        DMA((2, 3, items)),
        DMA((2, 3, items)),
        DMA((1,)),
        DMA((1,)),
        DMA((items,)),
        DMA((items,)),
        DMA((chips,)),
        DMA((chips,)),
        DMA((items,)),
        DMA((items,)),
    ]
    return pl.pallas_call(
        functools.partial(backward_kernel, items, n),
        out_shape=outs,
        in_specs=[SCALARS] + [WHOLE] * 6 + [ANYWHERE] * len(arrays),
        out_specs=(ANYWHERE,) * 7,
        scratch_shapes=scratch,
        compiler_params=pltpu.CompilerParams(
            collective_id=identity, has_side_effects=True, vmem_limit_bytes=62 << 20
        ),
        cost_estimate=pl.CostEstimate(
            flops=80 * pixels * channels * channels, bytes_accessed=60 << 20, transcendentals=0
        ),
        name="backward",
    )(info, embed, *gains, stats, shifts, *arrays)


def own_shards(
    extent, image, embed, text, gain1, conv1_w, embed_w, gain2, conv2_w, gain3, qkv_w, text_w, proj_w,
    cotangent,
):
    _, rows_dev, width, channels = image.shape
    items, parts = lax.axis_size("items"), lax.axis_size("rows")
    me = lax.axis_index("rows")
    head_dim = channels // HEADS
    tokens = text.shape[1]
    share = channels // parts
    (first, middle, cot, hidden_all, second_all, attn_flat, qkv_turned, output, query_part, side_part, dkv, dtext,
     text_cols, stats, shifts) = forward_call(
        extent,
        image[0],
        cotangent[0],
        text[0],
        embed,
        (gain1, gain2, gain3),
        (
            conv1_w.reshape(3, 3 * channels, channels),
            conv2_w.reshape(3, 3 * channels, channels),
            embed_w,
            text_w,
            qkv_w,
            proj_w,
        ),
        0,
    )
    text_w_rows = text_cols.shape[3]
    image_grad, text_grad, text_w_grad, embed_grad, final, side, vectors = backward_call(
        extent,
        embed,
        (gain1, gain2, gain3),
        stats,
        shifts,
        (
            query_part,
            side_part,
            dkv,
            dtext,
            first,
            middle,
            cot,
            image[0],
            hidden_all,
            second_all,
            attn_flat,
            qkv_turned,
            text_cols.reshape(items * parts, tokens, text_w_rows),
            conv1_w.reshape(9 * channels, channels),
            conv2_w.reshape(9 * channels, channels),
            text_w,
            embed_w,
        ),
        1,
    )
    (output, image_grad, text_grad, text_w_grad, embed_grad, conv2, conv1, qkv, proj, embed_w_grad, norm1, norm2,
     norm3) = finalize_call(
        (final, side, vectors, output, image_grad, text_grad, text_w_grad, embed_grad), share
    )

    def kernel(values):
        return jnp.swapaxes(values.reshape(3, 3, share, channels), 2, 3)

    return (
        output[None],
        image_grad[None],
        embed_grad,
        text_grad[None],
        norm1[0],
        kernel(conv1),
        embed_w_grad,
        norm2[0],
        kernel(conv2),
        norm3[0],
        qkv.T,
        text_w_grad,
        proj.T,
    )


def shards(
    image, embed, text, extent, first_norm_gain1, conv1_w, embed_w, second_norm_gain2, conv2_w,
    attention_norm_gain, qkv_w, text_w, proj_w, cotangent,
):
    images, rows_dev, width, channels = image.shape
    parts = lax.axis_size("rows")
    me = lax.axis_index("rows")
    pairs = images * HEADS // parts
    head_dim = channels // HEADS
    pixels = rows_dev * width
    group = max(1, 512 // pixels)
    span = group * pixels
    chunks = parts // group
    tokens = text.shape[1]
    first_row = jnp.full((images, 1), me * rows_dev, jnp.int32)
    info = jnp.concatenate([extent, first_row], axis=1)
    gain1 = first_norm_gain1.reshape(1, channels)
    gain2 = second_norm_gain2.reshape(1, channels)
    gain3 = attention_norm_gain.reshape(1, channels)
    rowpos = me * rows_dev + jnp.arange(rows_dev, dtype=jnp.int32)
    colpos = jnp.arange(width, dtype=jnp.int32)
    inside = (rowpos[None, :, None] < extent[:, 0, None, None]) & (
        colpos[None, None, :] < extent[:, 1, None, None]
    )
    image_window = inside.astype(F32)[..., None]

    items = lax.axis_size("items")
    own_path = (
        images == 1
        and parts == HEADS
        and channels % (16 * items * parts) == 0
        and parts == 8
        and pixels % 512 == 0
        and channels % 512 == 0
        and tokens % 16 == 0
        and text.shape[2] % (128 * parts) == 0
        and text.shape[2] == embed.shape[1] <= 4 * channels
    )
    if own_path:
        return own_shards(
            extent, image, embed, text, gain1, conv1_w, embed_w, gain2, conv2_w, gain3, qkv_w, text_w,
            proj_w, cotangent,
        )

    embed_float = embed.astype(F32)
    embed_low = jax.nn.silu(embed_float).astype(BF16)
    shifts = jnp.dot(embed_low, embed_w, preferred_element_type=F32)
    qkv_turned = qkv_w.T
    proj_shaped = proj_w.reshape(HEADS, head_dim, channels)

    start = image.astype(F32) * image_window
    zeros = jnp.zeros((images, 6, channels), F32)
    stats0 = jnp.concatenate(
        [
            jnp.sum(start, axis=(1, 2))[:, None],
            jnp.sum(start * start, axis=(1, 2))[:, None],
            zeros,
        ],
        axis=1,
    )
    stats1, image_above, image_below, cot_above, cot_below = exchange(
        stats0, (image, cotangent), 0
    )
    full = jax.ShapeDtypeStruct(image.shape, F32)
    sums = jax.ShapeDtypeStruct((images, 8, channels), F32)
    padded = jax.ShapeDtypeStruct((images, rows_dev + 2, width, channels), BF16)
    first, stats, hidden = conv_call(
        conv1_kernel,
        info,
        (image, image_above, image_below, stats1, gain1),
        conv1_w,
        (full, sums, padded),
        False,
    )
    stats2, first_above, first_below, all_text = exchange(stats, (first,), 1, (text,))
    gathered_text = jnp.moveaxis(all_text, 0, 1).reshape(images, parts * tokens, text.shape[2])
    text_share = text.shape[2] // parts
    text_cols = lax.dynamic_slice_in_dim(gathered_text, me * text_share, text_share, 2)
    text_cols = lax.all_gather(text_cols, "items", axis=0, tiled=True)
    middle, stats, second = conv_call(
        conv2_kernel,
        info,
        (first, first_above, first_below, stats2, gain2, shifts, image),
        conv2_w,
        (full, sums, padded),
        False,
    )
    stats3, mid_above, mid_below = exchange(stats, (middle,), 2)
    attn_flat, qkv_pix = project(info, middle, stats3, gain3, qkv_turned)

    def to_pairs(values):
        wide = values.shape[1]
        moved = lax.all_to_all(values, "rows", split_axis=0, concat_axis=0, tiled=True)
        moved = moved.reshape(chunks, group, pairs, wide, pixels)
        return jnp.transpose(moved, (2, 0, 3, 1, 4)).reshape(pairs, chunks, wide, span)

    def from_pairs(values):
        wide = values.shape[2]
        moved = values.reshape(pairs, chunks, wide, group, pixels)
        moved = jnp.transpose(moved, (1, 3, 0, 2, 4)).reshape(parts * pairs, wide, pixels)
        return lax.all_to_all(moved, "rows", split_axis=0, concat_axis=0, tiled=True)

    qkv_pair = to_pairs(qkv_pix)
    grad_proj = (cotangent.astype(F32) * image_window).astype(BF16).reshape(images, pixels, channels)
    grad_heads = jnp.einsum(
        "ipc,hdc->ihdp", grad_proj, proj_shaped, preferred_element_type=F32
    ).astype(BF16)
    grad_pair = to_pairs(grad_heads.reshape(images * HEADS, head_dim, pixels))
    pair_results = []
    for p in range(pairs):
        pair = me * pairs + p
        item, head = pair // HEADS, pair % HEADS
        weight = lax.dynamic_slice_in_dim(text_w, head * 2 * head_dim, 2 * head_dim, 1)
        own = lax.dynamic_index_in_dim(gathered_text, item, 0, False)
        text_pair = jnp.dot(own, weight, preferred_element_type=F32).astype(BF16)
        pair_extent = lax.dynamic_slice_in_dim(extent, item, 1, 0)
        pair_results.append(attention(pair_extent, qkv_pair[p], text_pair, grad_pair[p], width))
    attended, qkv_grad_pair, text_grad_pair = (jnp.stack(r) for r in zip(*pair_results))
    qkv_back = from_pairs(qkv_grad_pair)
    heads_out = from_pairs(attended).reshape(images, HEADS, head_dim, pixels)

    attn_grad, stats = unproject(info, middle, stats3, qkv_back, qkv_turned)
    stats4, grad_above, grad_below, text_back = exchange(stats, (attn_grad,), 3, (text_grad_pair,))
    text_back = text_back.reshape(images, HEADS, parts * tokens, 2 * head_dim)
    text_all = lax.all_gather(text_back, "items", axis=0, tiled=True)
    proj_grad = jnp.einsum("ipc,ihdp->chd", grad_proj, heads_out, preferred_element_type=F32)
    qkv_grad = jnp.einsum(
        "ihwdp,ipc->hdwc",
        qkv_back.reshape(images, HEADS, 3, head_dim, pixels),
        attn_flat,
        preferred_element_type=F32,
    )
    grad_middle, moved_grad, stats, conv2_grad = conv_call(
        back2_kernel,
        info,
        (attn_grad, grad_above, grad_below, middle, mid_above, mid_below, cotangent, cot_above,
         cot_below, stats3, stats4, gain3, first, stats2, gain2, shifts),
        conv2_w,
        (full, full, sums, padded),
        True,
    )
    stats5, moved_above, moved_below = exchange(stats, (moved_grad,), 4)
    pre_grad, stats, conv1_grad = conv_call(
        back1_kernel,
        info,
        (moved_grad, moved_above, moved_below, first, first_above, first_below, stats2, stats5,
         gain2, shifts, image, stats1, gain1),
        conv1_w,
        (full, sums, padded),
        True,
    )
    (stats6,) = exchange(stats, (), 5)
    image_grad = finish(info, pre_grad, stats6, image, stats1, gain1, grad_middle)

    projected = jnp.einsum(
        "ihdp,hdc->ipc", heads_out, proj_shaped, preferred_element_type=F32
    ).reshape(image.shape)
    output = (middle + projected * image_window).astype(BF16)
    own_text = lax.dynamic_slice_in_dim(text_back, me * tokens, tokens, 2)
    text_shaped = text_w.reshape(text_w.shape[0], HEADS, 2 * head_dim)
    text_grad = jnp.einsum("ihtk,chk->itc", own_text, text_shaped, preferred_element_type=F32)
    text_w_grad = jnp.einsum(
        "gtc,ghtk->chk", text_cols, text_all, preferred_element_type=F32
    ).reshape(text_share, 2 * channels)
    scale_sum = stats5[:, 1] * gain2
    grad_shifts = jnp.concatenate([scale_sum, stats5[:, 0]], axis=1).astype(BF16)
    embed_grad = jnp.einsum(
        "ik,ck->ic", grad_shifts, embed_w, preferred_element_type=F32
    ) * silu_slope(embed_float)
    embed_share = embed_w.shape[0] // parts
    gains = jnp.stack(
        [
            jnp.sum(stats6[:, 1], axis=0),
            jnp.sum(stats5[:, 1] * (1.0 + shifts[:, :channels]), axis=0),
            jnp.sum(stats4[:, 1], axis=0),
        ]
    )
    share = channels // parts
    def total(values):
        return lax.psum(
            lax.psum_scatter(values.astype(BF16), "rows", scatter_dimension=0, tiled=True),
            "items",
        ).astype(F32)

    def kernel_total(values):
        return total(values).T.reshape(3, 3, channels, share)

    conv1_total = kernel_total(weight_grad(conv1_grad, hidden))
    conv2_total = kernel_total(weight_grad(conv2_grad, second))
    by_head = jnp.swapaxes(qkv_grad, 1, 2).reshape(3 * channels, channels)
    qkv_total = total(by_head).T
    proj_total = total(proj_grad.reshape(channels, channels)).T
    gains = lax.psum(gains, "items")
    all_shifts = lax.all_gather(grad_shifts, "items", axis=0, tiled=True)
    embed_rows = lax.dynamic_slice_in_dim(embed_low, me * embed_share, embed_share, 1)
    embed_rows = lax.all_gather(embed_rows, "items", axis=0, tiled=True)
    embed_w_grad = jnp.einsum("ic,ik->ck", embed_rows, all_shifts, preferred_element_type=F32)
    gains = lax.dynamic_slice_in_dim(gains, me * share, share, 1)
    return (
        output,
        image_grad,
        embed_grad,
        text_grad,
        gains[0],
        conv1_total,
        embed_w_grad,
        gains[1],
        conv2_total,
        gains[2],
        qkv_total,
        text_w_grad,
        proj_total,
    )


def solution(mesh):
    in_specs = (
        P("items", "rows", None, None),
        P("items", None),
        P("items", "rows", None),
        P("items", None),
        P(),
        P(),
        P(),
        P(),
        P(),
        P(),
        P(),
        P(),
        P(),
        P("items", "rows", None, None),
    )
    out_specs = (
        P("items", "rows", None, None),
        P("items", "rows", None, None),
        P("items", None),
        P("items", "rows", None),
        P("rows"),
        P(None, None, None, "rows"),
        P("rows", None),
        P("rows"),
        P(None, None, None, "rows"),
        P("rows"),
        P(None, "rows"),
        P("rows", None),
        P(None, "rows"),
    )
    return jax.shard_map(shards, mesh=mesh, in_specs=in_specs, out_specs=out_specs, check_vma=False)
```
